32 devices in a mesh: dp: 2 (over x), context: 8 (over z, core), tensor: 2 (over y).
Axes of the slice: x: 2, y: 2, z: 4, core: 2. Of those that a mesh axis runs over, the one named last changes fastest.
Arguments:
- tokens: bfloat16 [4, 4096, 768], P('dp', 'context'), may hold values from -6 to 6
- documents: int32 [4, 4096], P('dp', 'context'), may hold values from 0 to 15, never falling along the last dimension, each value on 1 to 1024 neighbouring positions
- norm_gain: float32 [768], P(('dp', 'context')), may hold values from 0.5 to 1.5
- entry_weight: float32 [768, 2, 1536], P(('dp', 'context'), None, 'tensor'), may hold values from -0.21875 to 0.21875
- state_weight: float32 [768, 256], P(('dp', 'context')), may hold values from -0.21875 to 0.21875
- step_weight: float32 [768, 24], P(('dp', 'context'), 'tensor'), may hold values from -0.109375 to 0.109375
- inner_kernel: float32 [5, 1536], P(None, 'tensor'), may hold values from -0.5 to 0.5
- state_filter: float32 [5, 256], replicated, may hold values from -0.5 to 0.5
- step_bias: float32 [24], P('tensor'), may hold values from -7 to -3
- decay_log: float32 [24], P('tensor'), may hold values from -1 to 1.5
- skip_gain: float32 [24], P('tensor'), may hold values from 0.25 to 1
- gate_gain: float32 [1536], P('tensor'), may hold values from 0.5 to 1.5
- exit_weight: float32 [768, 1536], P(('dp', 'context'), 'tensor'), may hold values from -0.15625 to 0.15625
- cotangent: bfloat16 [4, 4096, 768], P('dp', 'context'), may hold values from -6 to 6
Outputs:
- block_out: bfloat16 [4, 4096, 768], P('dp', 'context')
- token_grad: float32 [4, 4096, 768], P('dp', 'context')
- norm_grad: float32 [768], P(('dp', 'context'))
- entry_grad: float32 [768, 2, 1536], P(('dp', 'context'), None, 'tensor')
- state_weight_gradient: float32 [768, 256], P(('dp', 'context'))
- step_weight_gradient: float32 [768, 24], P(('dp', 'context'), 'tensor')
- kernel_grad: float32 [5, 1536], P(None, 'tensor')
- filter_grad: float32 [5, 256], replicated
- bias_grad: float32 [24], P('tensor')
- decay_grad: float32 [24], P('tensor')
- skip_grad: float32 [24], P('tensor')
- gate_grad: float32 [1536], P('tensor')
- exit_weight_gradient: float32 [768, 1536], P(('dp', 'context'), 'tensor')
The draws below stay inside these ranges and needn't reach their ends.
Inputs may be any that keep to these rules, and one draw needn't show every extreme that they name: `documents`: in each sequence the document numbers start at 0, never fall, every one of 0 to 15 occurs, each document has 1 to 1024 positions, and one has exactly 1024.
All inputs are finite; a program needn't handle non-finite values.
Results may differ from the reference program's by a relative error of at most 0.012.
The reference program's roundings to bfloat16 on the way count: a program that leaves them out, or rounds other values in their place, can miss the bound.
Values may be sent and summed in bfloat16 or wider, within the bound.
A program may use at most 256 MiB of HBM per device.

```python
import math
import jax
import jax.numpy as jnp
import numpy as np
from jax import lax

D = 768
HEADS = 24
HEAD = 64
NSTATE = 128
CONV = 4
SPAN = 256
BLOCK = 512
INNER = 1536
SEQS = 4
SEQLEN = 4096
DOCS = 16
MOST = 1024


def strengthened(drawn, stream_key, source, target, parts, factor):
    owner, partner = [(jnp.arange(drawn.shape[dim]) // (drawn.shape[dim] // parts)).reshape([-1 if axis == dim else 1 for axis in range(drawn.ndim)]) for dim in (source, target)]
    chosen = jax.random.permutation(stream_key, parts)[partner]
    strong = (owner == chosen) | (owner == (partner + parts // 2) % parts)
    return jnp.where(strong, factor * drawn, drawn)


def level_of(rng, dims, shards, smallest, largest):
    def one(axis_at, blocks):
        draws = jax.random.uniform(jax.random.fold_in(jax.random.fold_in(rng, 6), axis_at), (blocks,), jnp.float32, smallest / len(shards), largest / len(shards))
        return jnp.repeat(jnp.exp(draws), dims[axis_at] // blocks).reshape((-1,) + (1,) * (len(dims) - axis_at - 1))

    level = one(*shards[0])
    for cut in shards[1:]:
        level = level * one(*cut)
    return level


def profile(number_of, total, limit, lean):
    weights = [(1 << 20) // math.isqrt(grade ** lean) + 1 for grade in range(2, number_of + 1)]
    surplus, given = total - limit - (number_of - 1), [1] * (number_of - 1)
    while surplus > 0:
        free = [i for i in range(number_of - 1) if given[i] < limit]
        pool, left = sum([weights[i] for i in free]), surplus
        for i in free:
            extra = min(limit - given[i], max(1, left * weights[i] // pool), surplus)
            given[i] = given[i] + extra
            surplus = surplus - extra
    return np.array([limit] + given)


def ragged(rng, number_of, total, bound, skew):
    if number_of == 2:
        one = jax.random.randint(rng, (), max(1, total - bound), min(bound, total - 1) + 1)
        return jnp.stack([one, total - one])
    sizes = jnp.asarray(profile(number_of, total, bound, skew), jnp.int32)
    twos = (number_of - 1) // 2
    source_of, sink = sizes[1:1 + 2 * twos:2], sizes[2:2 + 2 * twos:2]
    slack = jnp.minimum(source_of - 1, bound - sink)
    shifted = jax.random.randint(jax.random.fold_in(rng, 1), (twos,), 0, 1 << 20) % (slack + 1)
    sizes = sizes.at[1:1 + 2 * twos:2].set(source_of - shifted).at[2:2 + 2 * twos:2].set(sink + shifted)
    return sizes[jax.random.permutation(jax.random.fold_in(rng, 2), number_of)]


def centred(stream_key, shape, width, most, cuts=(), dtype=jnp.bfloat16):
    values = jax.random.normal(stream_key, shape, jnp.float32) * width
    if len(cuts) > 0:
        values = level_of(stream_key, shape, cuts, -0.22, 0.18) * values
    return jnp.clip(values, min=-most, max=most).astype(dtype)


def noise_with(key, dims, scale, most, cuts, heavy, held_as=jnp.bfloat16):
    drawn = scale * jax.random.normal(key, dims, jnp.float32)
    if cuts:
        drawn = drawn * level_of(key, dims, cuts, -0.22, 0.18)
    return jnp.clip(strengthened(drawn, jax.random.fold_in(key, 3), *heavy), -most, most).astype(held_as)


def setup_inputs(seed: int = 0) -> dict:
    streams_of = jax.random.split(jax.random.key(seed), 15)
    return {
        "tokens": centred(streams_of[0], (SEQS, SEQLEN, D), 1.0, 6.0, ((0, 2), (1, 8))),
        "documents": jax.vmap(lambda own: jnp.searchsorted(jnp.cumsum(ragged(own, DOCS, SEQLEN, MOST, 3)), jnp.arange(SEQLEN), side="right"))(jax.random.split(streams_of[1], SEQS)).reshape((SEQS, SEQLEN)).astype(jnp.int32),
        "norm_gain": jnp.clip(1.0 + 0.1 * jax.random.normal(streams_of[2], (D,), jnp.float32), 0.5, 1.5),
        "entry_weight": centred(streams_of[3], (D, 2, INNER), D ** -0.5, 0.21875, ((0, 16), (2, 2)), jnp.float32),
        "state_weight": centred(streams_of[4], (D, 2 * NSTATE), D ** -0.5, 0.21875, ((0, 16),), jnp.float32),
        "step_weight": centred(streams_of[5], (D, HEADS), (4 * D) ** -0.5, 0.109375, ((0, 16), (1, 2)), jnp.float32),
        "inner_kernel": jnp.clip(jax.random.uniform(streams_of[6], (CONV + 1, INNER), jnp.float32, -0.5, 0.5) * level_of(streams_of[6], (CONV + 1, INNER), ((1, 2),), -0.4, 0.0), -0.5, 0.5),
        "state_filter": jnp.clip(jax.random.uniform(streams_of[7], (CONV + 1, 2 * NSTATE), jnp.float32, -0.5, 0.5), -0.5, 0.5),
        "step_bias": jnp.clip(-7.0 + 4.0 * jax.random.uniform(streams_of[8], (HEADS,), jnp.float32) ** level_of(streams_of[8], (HEADS,), ((0, 2),), -0.2, 0.2), -7.0, -3.0),
        "decay_log": jnp.clip(-1.0 + 2.5 * jax.random.uniform(streams_of[9], (HEADS,), jnp.float32) ** level_of(streams_of[9], (HEADS,), ((0, 2),), -0.2, 0.2), -1.0, 1.5),
        "skip_gain": jnp.clip(0.25 + 0.75 * jax.random.uniform(streams_of[10], (HEADS,), jnp.float32) ** level_of(streams_of[10], (HEADS,), ((0, 2),), -0.2, 0.2), 0.25, 1.0),
        "gate_gain": jnp.clip(1.0 + 0.1 * jax.random.normal(streams_of[11], (INNER,), jnp.float32), 0.5, 1.5),
        "exit_weight": centred(streams_of[12], (D, INNER), INNER ** -0.5, 0.15625, ((0, 16), (1, 2)), jnp.float32),
        "cotangent": noise_with(streams_of[13], (SEQS, SEQLEN, D), 1.0, 6.0, ((0, 2), (1, 8)), (1, 2, 8, 2.0)),
    }


EPSILON = 1e-05
PRECISION_HIGH = lax.Precision.HIGHEST

@jax.custom_vjp
def reduced_precision(v):
    return lax.optimization_barrier(v.astype(jnp.bfloat16)).astype(jnp.float32)

@jax.custom_vjp
def reduced_backward(v):
    return v

def low_keep(v):
    return (reduced_precision(v), None)

def low_pass(kept, grad):
    return (grad,)

def back_keep(v):
    return (v, None)

def back_low(kept, grad):
    return (reduced_precision(grad),)
reduced_precision.defvjp(low_keep, low_pass)
reduced_backward.defvjp(back_keep, back_low)

def block_step(state, pieces):
    values, writer, reader, log_decay, steps, segment, before = pieces
    length = segment.shape[0]
    cumulative = jnp.cumsum(log_decay, axis=0)
    places = jnp.arange(length)
    same = (places[:, None] >= places[None, :]) & (segment[:, None] == segment[None, :])
    spread = cumulative[:, None, :] - cumulative[None, :, :]
    decay = jnp.exp(jnp.where(same[:, :, None], spread, 0.0)) * same[:, :, None].astype(jnp.float32)
    scores = jnp.dot(reader, writer.T, precision=PRECISION_HIGH)
    weights = decay * scores[:, :, None] * steps[None, :, :]
    local = jnp.einsum('tuh,uhp->thp', weights, values, precision=PRECISION_HIGH)
    opened = (segment == before).astype(jnp.float32)
    carried = jnp.einsum('tn,hpn->thp', reader, state, precision=PRECISION_HIGH)
    result = local + (opened[:, None] * jnp.exp(cumulative))[:, :, None] * carried
    final = cumulative[-1]
    tail = (segment == segment[-1]).astype(jnp.float32)[:, None] * jnp.exp(final[None, :] - cumulative) * steps
    keep = (segment[-1] == before).astype(jnp.float32)
    state = keep * jnp.exp(final)[:, None, None] * state + jnp.einsum('uh,uhp,un->hpn', tail, values, writer, precision=PRECISION_HIGH)
    return (state, result)

def sequence_scan(pieces):
    values, writer, reader, log_decay, steps, segment = pieces
    length = min(SPAN, BLOCK)
    count = SEQLEN // length
    segment = segment.astype(jnp.int32)
    previous = jnp.concatenate([jnp.full((1,), -1, jnp.int32), segment[:-1]])
    before = previous.reshape(count, length)[:, 0]
    blocks = (values.reshape(count, length, HEADS, HEAD), writer.reshape(count, length, NSTATE), reader.reshape(count, length, NSTATE), log_decay.reshape(count, length, HEADS), steps.reshape(count, length, HEADS), segment.reshape(count, length), before)
    start = jnp.zeros((HEADS, HEAD, NSTATE), jnp.float32)
    final, outputs = lax.scan(jax.checkpoint(block_step), start, blocks)
    return outputs.reshape(SEQLEN, HEADS * HEAD)

def forward(inputs, documents, norm_gain, entry_weight, state_weight, step_weight, inner_kernel, state_filter, step_bias, decay_log, skip_gain, gate_gain, exit_weight):
    gain_low = reduced_precision(norm_gain)
    entry_reduced = reduced_precision(entry_weight)
    state_low = reduced_precision(state_weight)
    step_reduced = reduced_precision(step_weight)
    exit_reduced = reduced_precision(exit_weight)
    scale = lax.rsqrt(lax.optimization_barrier(jnp.mean(inputs * inputs, axis=-1, keepdims=True)) + EPSILON)
    hidden_activation = reduced_precision(inputs * scale * gain_low)
    gate_preactivation = reduced_backward(jnp.einsum('bqm,mj->bqj', hidden_activation, entry_reduced[:, 0, :], precision=PRECISION_HIGH))
    convolution_weight = jnp.concatenate([entry_reduced[:, 1, :], state_low], axis=1)
    convolution_input = reduced_backward(reduced_precision(jnp.einsum('bqm,mj->bqj', hidden_activation, convolution_weight, precision=PRECISION_HIGH)))
    step_unactivated = reduced_backward(jnp.einsum('wje,en->wjn', hidden_activation, step_reduced, precision=PRECISION_HIGH))
    kernel = jnp.concatenate([inner_kernel, state_filter], axis=1)
    padded = jnp.pad(convolution_input, ((0, 0), (CONV - 1, 0), (0, 0)))
    ids_padded = jnp.pad(documents, ((0, 0), (CONV - 1, 0)), constant_values=-1)
    preact = kernel[CONV]
    for offset in range(CONV):
        match = (ids_padded[:, offset:offset + SEQLEN] == documents).astype(jnp.float32)
        preact = preact + kernel[offset] * padded[:, offset:offset + SEQLEN] * match[:, :, None]
    mixed = jax.nn.silu(preact)
    inner = mixed[:, :, :INNER]
    writer = mixed[:, :, INNER:INNER + NSTATE]
    reader = mixed[:, :, INNER + NSTATE:]
    steps = jax.nn.softplus(step_unactivated + step_bias)
    log_decay = -steps * jnp.exp(decay_log)
    scanned = lax.map(sequence_scan, (inner, writer, reader, log_decay, steps, documents))
    output = scanned + jnp.repeat(skip_gain, HEAD) * inner
    gated = output * jax.nn.silu(gate_preactivation)
    normal = lax.rsqrt(lax.optimization_barrier(jnp.mean(gated * gated, axis=-1, keepdims=True)) + EPSILON)
    unit_activation = reduced_precision(gated * normal * gate_gain)
    branch_path = reduced_backward(jnp.einsum('yjr,pr->yjp', unit_activation, exit_reduced, precision=PRECISION_HIGH))
    return inputs + branch_path

def reference(tokens, documents, norm_gain, entry_weight, state_weight, step_weight, inner_kernel, state_filter, step_bias, decay_log, skip_gain, gate_gain, exit_weight, cotangent):
    inputs = tokens.astype(jnp.float32)

    def closed(inputs, norm_gain, entry_weight, state_weight, step_weight, inner_kernel, state_filter, step_bias, decay_log, skip_gain, gate_gain, exit_weight):
        return forward(inputs, documents, norm_gain, entry_weight, state_weight, step_weight, inner_kernel, state_filter, step_bias, decay_log, skip_gain, gate_gain, exit_weight)
    result, pullback = jax.vjp(closed, inputs, norm_gain, entry_weight, state_weight, step_weight, inner_kernel, state_filter, step_bias, decay_log, skip_gain, gate_gain, exit_weight)
    grads = pullback(cotangent.astype(jnp.float32))
    return (result.astype(jnp.bfloat16), grads[0], grads[1], grads[2], grads[3], grads[4], grads[5], grads[6], grads[7], grads[8], grads[9], grads[10], grads[11])
```

```python
import functools
import jax
import jax.numpy as jnp
from jax import lax
from jax.experimental import pallas as pl
from jax.experimental.pallas import tpu as pltpu
from jax.sharding import PartitionSpec as P

HEAD = 64
NSTATE = 128
CONV = 4
EPSILON = 1e-05
Q = 128
HALO = 16
LANES = 128
WIDE = 256
LOG2E = 1.4426950408889634
FAR = -1e30
LOW = jnp.bfloat16
F32 = jnp.float32
VMEM_LIMIT = 60 * 1024 * 1024


def mm(a, b):
    return lax.dot_general(a, b, (((1,), (0,)), ((), ())), preferred_element_type=F32)


def mm_nt(a, b):
    return lax.dot_general(a, b, (((1,), (1,)), ((), ())), preferred_element_type=F32)


def mm_tn(a, b):
    return lax.dot_general(a, b, (((0,), (0,)), ((), ())), preferred_element_type=F32)


def mm_exact(a, b):
    return lax.dot_general(
        a, b, (((1,), (0,)), ((), ())), precision=lax.Precision.HIGHEST, preferred_element_type=F32
    )


def split3(v):
    high = v.astype(LOW).astype(F32)
    rest = v - high
    mid = rest.astype(LOW).astype(F32)
    low = rest - mid
    return (high + pltpu.roll(mid, 32, 1) + pltpu.roll(low, 64, 1)).astype(LOW)


def iota(shape, dim):
    return lax.broadcasted_iota(jnp.int32, shape, dim)


def spreader(first_head, width, count):
    k = iota((LANES, width * count), 0)
    lane = iota((LANES, width * count), 1)
    hit = ((k & 31) == first_head + lane // width) & (k < 96)
    return hit.astype(F32).astype(LOW)


def gatherer(first_head, width, count):
    lane = iota((width * count, LANES), 0)
    k = iota((width * count, LANES), 1)
    return (k == first_head + lane // width).astype(F32).astype(LOW)


def head_sums(v, collect):
    high = v.astype(LOW)
    rest = (v - high.astype(F32)).astype(LOW)
    return mm(high, collect) + mm(rest, collect)


def sigmoid(v):
    return 1.0 / (1.0 + jnp.exp(-v))


def twice(v):
    return jnp.concatenate([v, v], axis=1)


def conv_forward(cin, taps, masks):
    rows = cin.shape[0] - HALO
    out = taps[CONV : CONV + 1] + taps[CONV - 1 : CONV] * cin[HALO:]
    for back in range(1, CONV):
        part = cin[HALO - back : HALO - back + rows]
        out = out + taps[CONV - 1 - back : CONV - back] * (part * twice(masks[back - 1]))
    return out


def conv_backward(pg, cin, taps, masks):
    rows, width = pg.shape
    sums = [None] * (CONV + 1)
    sums[CONV] = jnp.sum(pg, axis=0, keepdims=True)
    sums[CONV - 1] = jnp.sum(pg * cin[HALO:], axis=0, keepdims=True)
    pad = jnp.zeros((HALO, width), F32)
    grad = jnp.concatenate([pad, pg * taps[CONV - 1 : CONV]], axis=0)
    for back in range(1, CONV):
        masked = pg * twice(masks[back - 1])
        part = cin[HALO - back : HALO - back + rows]
        sums[CONV - 1 - back] = jnp.sum(masked * part, axis=0, keepdims=True)
        padded = jnp.concatenate([pad, masked * taps[CONV - 1 - back : CONV - back], pad], axis=0)
        grad = grad + padded[back : back + rows + HALO]
    return sums, grad


def front_body(
    which, tokens, halo, halo_docs, doc_col, doc_row, w_gate, w_inner, w_small, par, par_heads,
    state_filter, hidden_out, cin_out, gate_out, pre_out, loc_out, fold_out, gain_out,
    cin_state_out, pre_state_out, bc_out, bct_out, score_out, mask_out, zst_out, dt_out, sp_out,
    cumt_out, fac_out, match_out, hidden, sp_tail, facs
):
    step = pl.program_id(0)
    rows = tokens.shape[1]
    spans = rows // Q

    @pl.when(step == 0)
    def _():
        gain_t = jnp.transpose(w_small[0, :, LANES : 2 * LANES].astype(F32))
        gain = gain_t[24:25]
        for ref, first, count in ((halo, 0, HALO), (tokens, HALO, rows)):
            value = (ref[...] if ref is halo else ref[0]).astype(F32)
            scale = lax.rsqrt(jnp.mean(value * value, axis=1, keepdims=True) + EPSILON)
            hidden[first : first + count] = (value * scale * gain).astype(LOW)
        hidden_out[...] = hidden[HALO:]
        both = [mm(hidden[...], w_small[index]) for index in range(2)]
        cin = jnp.concatenate([both[0][:, :LANES], both[1][:, :LANES]], axis=1).astype(LOW)
        cin_state_out[...] = cin
        docs = jnp.concatenate([halo_docs[...], doc_col[...]], axis=0)
        masks = []
        for back in range(1, CONV):
            match = (docs[HALO - back : HALO - back + rows] == docs[HALO:]).astype(F32)
            match_out[back - 1] = match
            masks.append(match)
        pre = conv_forward(cin.astype(F32), state_filter[...], masks)
        pre_state_out[...] = pre
        mixed = (pre * sigmoid(pre)).astype(LOW)
        bc_out[...] = mixed
        turned = jnp.transpose(mixed.astype(F32)).astype(LOW)
        bct_out[...] = turned
        heads = par_heads[...]
        used = iota((rows, LANES), 1) < 24
        raw = both[0][HALO:, LANES:] + both[1][HALO:, LANES:]
        zst = jnp.where(used, raw, 0.0) + heads[0:1]
        zst_out[...] = zst
        dt = jnp.where(used, jnp.maximum(zst, 0.0) + jnp.log1p(jnp.exp(-jnp.abs(zst))), 0.0)
        dt_out[...] = dt
        decay = -dt * jnp.exp(heads[1:2])
        t_at, u_at = iota((Q, Q), 0), iota((Q, Q), 1)
        lower = (t_at >= u_at).astype(F32)
        fac_rows = []
        for index in range(spans):
            at = slice(index * Q, (index + 1) * Q)
            cum = mm_exact(lower, decay[at])
            final = cum[Q - 1 : Q]
            before = docs[HALO + index * Q - 1 : HALO + index * Q]
            here = doc_col[at]
            last = here[Q - 1 : Q]
            opened = (here == before).astype(F32)
            tail = (here == last).astype(F32) * jnp.exp(final - cum)
            fac_rows.append((last == before).astype(F32) * jnp.exp(final))
            cum2 = cum * LOG2E
            turned_cum = jnp.transpose(cum2)
            for group in range(6):
                cumt_out[group, 0:4, at] = turned_cum[4 * group : 4 * group + 4]
            sp_out[0, at] = split3(dt[at])
            sp_out[1, at] = split3(cum2)
            lanes_used = iota((Q, LANES), 1) < 24
            sp_out[2, at] = split3(jnp.where(lanes_used, opened * jnp.exp(cum), 0.0))
            sp_out[3, at] = split3(jnp.where(lanes_used, tail, 0.0))
            sp_tail[at] = split3(jnp.where(lanes_used, tail * dt[at], 0.0))
            same = (t_at >= u_at) & (here == doc_row[0:1, at])
            mask_out[at] = jnp.where(same, 0.0, FAR)
            score_out[at] = mm_nt(mixed[at, LANES:], mixed[at, :LANES])
        gain_total = fac_rows[0]
        for row in fac_rows[1:]:
            gain_total = gain_total * row
        rows8 = jnp.concatenate(
            fac_rows + [gain_total] + [jnp.zeros((1, LANES), F32)] * (7 - spans), axis=0
        )
        rows8 = jnp.where(iota((8, LANES), 1) < 24, rows8, 0.0)
        fac_out[...] = rows8
        facs[...] = split3(rows8)

    cin = mm(hidden[...], w_inner[0]).astype(LOW)
    cin_out[...] = cin
    gate_out[...] = mm(hidden[HALO:], w_gate[0])
    masks = [match_out[back] for back in range(CONV - 1)]
    pre = conv_forward(cin.astype(F32), par[0], masks)
    pre_out[...] = pre
    spread = spreader(4 * step, HEAD, 4)
    value = (pre * sigmoid(pre) * mm(sp_tail[...], spread)).astype(LOW)
    facx = mm(facs[...], spread)
    fold = jnp.zeros((NSTATE, WIDE), F32)
    for index in range(spans):
        at = slice(index * Q, (index + 1) * Q)
        loc = mm(bct_out[:NSTATE, at], value[at])
        loc_out[at] = loc
        fold = facx[index : index + 1] * fold + loc
    fold_out[...] = fold
    gain_out[...] = jnp.broadcast_to(facx[spans : spans + 1], (8, WIDE))


def const(shape):
    zeros = (0,) * len(shape)
    return pl.BlockSpec(shape, lambda *_: zeros)


def params(**extra):
    return pltpu.CompilerParams(vmem_limit_bytes=VMEM_LIMIT, **extra)


def front(which, tokens, halo, halo_docs, doc_col, doc_row, weights, par, par_heads, state_filter):
    rows, model = tokens.shape[1:]
    wide = 2 * 3 * WIDE
    ext = rows + HALO
    shape = jax.ShapeDtypeStruct
    outs = (
        (shape((rows, model), LOW), const((rows, model))),
        (shape((ext, wide), LOW), pl.BlockSpec((ext, WIDE), lambda s, w: (0, s))),
        (shape((rows, wide), F32), pl.BlockSpec((rows, WIDE), lambda s, w: (0, s))),
        (shape((rows, wide), F32), pl.BlockSpec((rows, WIDE), lambda s, w: (0, s))),
        (shape((rows, wide), F32), pl.BlockSpec((rows, WIDE), lambda s, w: (0, s))),
        (shape((NSTATE, wide), F32), pl.BlockSpec((NSTATE, WIDE), lambda s, w: (0, s))),
        (shape((8, wide), F32), pl.BlockSpec((8, WIDE), lambda s, w: (0, s))),
        (shape((ext, WIDE), LOW), const((ext, WIDE))),
        (shape((rows, WIDE), F32), const((rows, WIDE))),
        (shape((rows, WIDE), LOW), const((rows, WIDE))),
        (shape((WIDE, rows), LOW), const((WIDE, rows))),
        (shape((rows, Q), F32), const((rows, Q))),
        (shape((rows, Q), F32), const((rows, Q))),
        (shape((rows, LANES), F32), const((rows, LANES))),
        (shape((rows, LANES), F32), const((rows, LANES))),
        (shape((4, rows, LANES), LOW), const((4, rows, LANES))),
        (shape((6, 8, rows), F32), const((6, 8, rows))),
        (shape((8, LANES), F32), const((8, LANES))),
        (shape((CONV - 1, rows, LANES), F32), const((CONV - 1, rows, LANES))),
    )
    return pl.pallas_call(
        front_body,
        out_shape=[out[0] for out in outs],
        grid_spec=pltpu.PrefetchScalarGridSpec(
            num_scalar_prefetch=1,
            grid=(6,),
            in_specs=[
                pl.BlockSpec((1, rows, model), lambda s, w: (w[0], 0, 0)),
                const((HALO, model)),
                const((HALO, LANES)),
                const((rows, LANES)),
                const((8, rows)),
                pl.BlockSpec((1, model, WIDE), lambda s, w: (s // 3, 0, s % 3)),
                pl.BlockSpec((1, model, WIDE), lambda s, w: (s // 3, 0, 3 + s % 3)),
                pl.BlockSpec((2, model, WIDE), lambda s, w: (0, 0, 9)),
                pl.BlockSpec((1, 8, WIDE), lambda s, w: (s // 3, 0, s % 3)),
                const((8, LANES)),
                const((8, WIDE)),
            ],
            out_specs=[out[1] for out in outs],
            scratch_shapes=[
                pltpu.VMEM((ext, model), LOW),
                pltpu.VMEM((rows, LANES), LOW),
                pltpu.VMEM((8, LANES), LOW),
            ],
        ),
        compiler_params=params(),
        name="front",
    )(
        which, tokens, halo, halo_docs, doc_col, doc_row, weights, weights, weights, par, par_heads,
        state_filter,
    )


def middle_body(
    which, tokens, cot, cot_t, pre_ref, gate_ref, loc_ref, carry_ref, w_exit, par, par_heads, bc,
    bct, score, mask, sp, cumt, fac, block_out, exit_out, dy_out, gpg_out, enter_out, row_out,
    skip_out, outputs, gates, unit_grads, mixes, sums, total
):
    step = pl.program_id(0)
    rows = pre_ref.shape[0]
    spans = rows // Q
    wide = 6 * WIDE

    @pl.when(step == 0)
    def _():
        sums[...] = jnp.zeros_like(sums)
        total[...] = jnp.zeros_like(total)
        skip_out[...] = jnp.zeros_like(skip_out)

    @pl.when(step < 6)
    def _():
        group = step
        spread = spreader(4 * group, HEAD, 4)
        pre = pre_ref[...]
        mix = pre * sigmoid(pre)
        mixes[group] = mix
        value = mix * mm(sp[0], spread)
        growth = mm(sp[2], spread)
        facx = mm(split3(fac[...]), spread)
        cums = mm(sp[1], spreader(4 * group, LANES, 4))
        skipx = mm(split3(par_heads[...]), spread)[2:3]
        state = carry_ref[...].astype(F32)
        half = iota((Q, LANES), 1) < HEAD
        for index in range(spans):
            at = slice(index * Q, (index + 1) * Q)
            carried = mm(bc[at, LANES:], state.astype(LOW)) * growth[at]
            parts = []
            for pair in range(2):
                lanes = slice(pair * LANES, (pair + 1) * LANES)
                local = None
                for side in range(2):
                    head = 2 * pair + side
                    across = cumt[group, head : head + 1, at]
                    spread_at = cums[at, head * LANES : (head + 1) * LANES] - across + mask[at]
                    weight = (jnp.exp2(spread_at) * score[at]).astype(LOW)
                    keep = half if side == 0 else jnp.logical_not(half)
                    seen = jnp.where(keep, value[at, lanes], 0.0).astype(LOW)
                    part = mm(weight, seen)
                    local = part if local is None else local + part
                parts.append(local)
            out = jnp.concatenate(parts, axis=1) + carried + skipx * mix[at]
            outputs[group, at] = out
            state = facx[index : index + 1] * state + loc_ref[at]
        gate = gate_ref[...]
        gates[group] = gate
        gated = outputs[group] * (gate * sigmoid(gate))
        unit_grad = mm(cot[0], w_exit[0])
        unit_grads[group] = unit_grad
        square = gated * gated
        cross = unit_grad * par[0, 5:6] * gated
        sums[0] += square[:, :LANES] + square[:, LANES:]
        sums[1] += cross[:, :LANES] + cross[:, LANES:]

    @pl.when(step == 5)
    def _():
        square = jnp.sum(sums[0], axis=1, keepdims=True)
        cross = jnp.sum(sums[1], axis=1, keepdims=True)
        normal = lax.rsqrt(square / wide + EPSILON)
        sums[0] = jnp.broadcast_to(normal, (rows, LANES))
        sums[1] = jnp.broadcast_to(normal * normal * normal * cross / wide, (rows, LANES))

    @pl.when(step >= 6)
    def _():
        group = step - 6
        spread = spreader(4 * group, HEAD, 4)
        normal = twice(sums[0])
        pull = twice(sums[1])
        gain = par[0, 5:6]
        gate = gates[group]
        out = outputs[group]
        unit_grad = unit_grads[group]
        sigma = sigmoid(gate)
        act = gate * sigma
        gated = out * act
        scaled_in = gated * normal
        unit = (scaled_in * gain).astype(LOW)
        total[...] += mm_nt(unit, w_exit[0])
        exit_out[0] = mm(cot_t[...], unit).astype(LOW)
        gate_sum = jnp.sum(unit_grad * scaled_in, axis=0, keepdims=True)
        gated_grad = normal * (unit_grad * gain) - pull * gated
        dy = gated_grad * act
        dy_out[...] = dy
        gpg_out[...] = (gated_grad * out * sigma * (1.0 + gate * (1.0 - sigma))).astype(LOW)
        skip_sum = jnp.sum(dy * mixes[group], axis=0, keepdims=True)
        row_out[...] = jnp.broadcast_to(gate_sum, (8, WIDE))
        skip_out[...] += head_sums(
            jnp.broadcast_to(skip_sum, (8, WIDE)), gatherer(4 * group, HEAD, 4)
        )
        facx = mm(split3(fac[...]), spread)
        pushed = (dy * mm(sp[2], spread)).astype(LOW)
        enter = jnp.zeros((NSTATE, WIDE), F32)
        for index in reversed(range(spans)):
            at = slice(index * Q, (index + 1) * Q)
            enter = facx[index : index + 1] * enter + mm(bct[NSTATE:, at], pushed[at])
        enter_out[...] = enter

    @pl.when(step == 11)
    def _():
        block_out[...] = (tokens[0].astype(F32) + total[...]).astype(LOW)


def middle(
    which, tokens, cot, cot_t, pre, gate, loc, carry, weights, par, par_heads, bc, bct, score, mask,
    sp, cumt, fac
):
    rows, model = tokens.shape[1:]
    wide = 6 * WIDE
    shape = jax.ShapeDtypeStruct

    def early(s):
        return jnp.minimum(s, 5)

    def late(s):
        return jnp.maximum(s - 6, 0)

    def group(s):
        return s % 6

    outs = (
        (shape((rows, model), LOW), const((rows, model))),
        (
            shape((2, model, 3 * WIDE), LOW),
            pl.BlockSpec((1, model, WIDE), lambda s, w: (late(s) // 3, 0, late(s) % 3)),
        ),
        (shape((rows, wide), F32), pl.BlockSpec((rows, WIDE), lambda s, w: (0, late(s)))),
        (shape((rows, wide), LOW), pl.BlockSpec((rows, WIDE), lambda s, w: (0, late(s)))),
        (shape((NSTATE, wide), F32), pl.BlockSpec((NSTATE, WIDE), lambda s, w: (0, late(s)))),
        (shape((8, wide), F32), pl.BlockSpec((8, WIDE), lambda s, w: (0, late(s)))),
        (shape((8, LANES), F32), const((8, LANES))),
    )
    return pl.pallas_call(
        middle_body,
        out_shape=[out[0] for out in outs],
        grid_spec=pltpu.PrefetchScalarGridSpec(
            num_scalar_prefetch=1,
            grid=(12,),
            in_specs=[
                pl.BlockSpec((1, rows, model), lambda s, w: (w[0], 0, 0)),
                pl.BlockSpec((1, rows, model), lambda s, w: (w[0], 0, 0)),
                const((model, rows)),
                pl.BlockSpec((rows, WIDE), lambda s, w: (0, early(s))),
                pl.BlockSpec((rows, WIDE), lambda s, w: (0, early(s))),
                pl.BlockSpec((rows, WIDE), lambda s, w: (0, early(s))),
                pl.BlockSpec((NSTATE, WIDE), lambda s, w: (0, early(s))),
                pl.BlockSpec((1, model, WIDE), lambda s, w: (group(s) // 3, 0, 6 + group(s) % 3)),
                pl.BlockSpec((1, 8, WIDE), lambda s, w: (group(s) // 3, 0, group(s) % 3)),
                const((8, LANES)),
                const((rows, WIDE)),
                const((WIDE, rows)),
                const((rows, Q)),
                const((rows, Q)),
                const((4, rows, LANES)),
                const((6, 8, rows)),
                const((8, LANES)),
            ],
            out_specs=[out[1] for out in outs],
            scratch_shapes=[
                pltpu.VMEM((6, rows, WIDE), F32),
                pltpu.VMEM((6, rows, WIDE), F32),
                pltpu.VMEM((6, rows, WIDE), F32),
                pltpu.VMEM((6, rows, WIDE), F32),
                pltpu.VMEM((2, rows, LANES), F32),
                pltpu.VMEM((rows, model), F32),
            ],
        ),
        compiler_params=params(),
        name="middle",
    )(
        which, tokens, cot, cot_t, pre, gate, loc, carry, weights, par, par_heads, bc, bct, score,
        mask, sp, cumt, fac,
    )


def scan_back_body(
    pre_ref, dy_ref, loc_ref, carry_ref, adj_ref, cin_ref, par, par_heads, state_filter, cin_state,
    pre_state, bc, bct, score, mask, sp, cumt, fac, match, zst, dt_ref, cg_out, edge_out, tap_out,
    cg_state_out, edge_state_out, tap_state_out, srg_out, small_out, d_bc, d_score, d_cum, heads
):
    group = pl.program_id(0)
    rows = pre_ref.shape[0]
    spans = rows // Q

    @pl.when(group == 0)
    def _():
        d_bc[...] = jnp.zeros_like(d_bc)
        d_score[...] = jnp.zeros_like(d_score)
        d_cum[...] = jnp.zeros_like(d_cum)
        heads[...] = jnp.zeros_like(heads)

    spread = spreader(4 * group, HEAD, 4)
    collect = gatherer(4 * group, HEAD, 4)
    pre = pre_ref[...]
    sigma = sigmoid(pre)
    mix = pre * sigma
    dtx = mm(sp[0], spread)
    growth = mm(sp[2], spread)
    tails = mm(sp[3], spread)
    facx = mm(split3(fac[...]), spread)
    cums = mm(sp[1], spreader(4 * group, LANES, 4))
    skipx = mm(split3(par_heads[...]), spread)[2:3]
    states = [carry_ref[...].astype(F32)]
    for index in range(spans - 1):
        at = slice(index * Q, (index + 1) * Q)
        states.append(facx[index : index + 1] * states[-1] + loc_ref[at])
    adjoint = adj_ref[...].astype(F32)
    half = iota((Q, LANES), 1) < HEAD
    ones = jnp.ones((8, Q), F32).astype(LOW)
    masks = [match[back] for back in range(CONV - 1)]
    pgs = [None] * spans
    for index in reversed(range(spans)):
        at = slice(index * Q, (index + 1) * Q)
        dy = dy_ref[at]
        value = mix[at] * dtx[at]
        state_low, adj_low = states[index].astype(LOW), adjoint.astype(LOW)
        pushed = dy * growth[at]
        pushed_low = pushed.astype(LOW)
        reached = mm(bc[at, :LANES], adj_low) * tails[at]
        carried = mm(bc[at, LANES:], state_low)
        d_bc[at, :LANES] += mm_nt((value * tails[at]).astype(LOW), adj_low)
        d_bc[at, LANES:] += mm_nt(pushed_low, state_low)
        heads[0, at] += head_sums(value * reached, collect)
        heads[1, at] += head_sums(pushed * carried, collect)
        fac_part = jnp.sum(adjoint * states[index], axis=0, keepdims=True)
        heads[3, index * 8 : index * 8 + 8] += head_sums(
            jnp.broadcast_to(fac_part, (8, WIDE)), collect
        )
        adjoint = facx[index : index + 1] * adjoint + mm(bct[NSTATE:, at], pushed_low)
        parts = []
        sum_score = None
        for pair in range(2):
            lanes = slice(pair * LANES, (pair + 1) * LANES)
            value_low = value[:, lanes].astype(LOW)
            local = None
            for side in range(2):
                head = 2 * pair + side
                across = cumt[group, head : head + 1, at]
                spread_at = cums[at, head * LANES : (head + 1) * LANES] - across + mask[at]
                decay = jnp.exp2(spread_at)
                keep = half if side == 0 else jnp.logical_not(half)
                dy_low = jnp.where(keep, dy[:, lanes], 0.0).astype(LOW)
                inner = decay * mm_nt(dy_low, value_low)
                sum_score = inner if sum_score is None else sum_score + inner
                moved = (inner * score[at]).astype(LOW)
                turn = mm_nt(ones, moved) - mm(ones, moved)
                d_cum[group, head : head + 1, at] = turn[0:1]
                part = mm_tn((decay * score[at]).astype(LOW), dy_low)
                local = part if local is None else local + part
            parts.append(local)
        d_score[at] += sum_score
        d_value = jnp.concatenate(parts, axis=1) + reached
        heads[2, at] += head_sums(mix[at] * d_value, collect)
        d_mix = dtx[at] * d_value + skipx * dy
        s = sigma[at]
        pgs[index] = d_mix * s * (1.0 + pre[at] * (1.0 - s))
    pg = jnp.concatenate(pgs, axis=0)
    sums, grad = conv_backward(pg, cin_ref[...].astype(F32), par[0], masks)
    tap_out[...] = jnp.concatenate(sums + [jnp.zeros((3, WIDE), F32)], axis=0)
    cg_out[...] = grad[HALO:]
    edge_out[...] = grad[:HALO]

    @pl.when(group == 5)
    def _():
        t_at, u_at = iota((Q, Q), 0), iota((Q, Q), 1)
        onward = (t_at <= u_at).astype(F32)
        earlier = (t_at > u_at).astype(F32)
        rate = jnp.exp(par_heads[1:2])
        bias_sum = jnp.zeros((1, LANES), F32)
        decay_sum = jnp.zeros((1, LANES), F32)
        used = iota((Q, LANES), 1) < 24
        for index in range(spans):
            at = slice(index * Q, (index + 1) * Q)
            pieces = [d_cum[piece, 0:4, at] for piece in range(6)]
            pieces.append(jnp.zeros((LANES - 24, Q), F32))
            cum_col = jnp.transpose(jnp.concatenate(pieces, axis=0))
            fac_row = fac[index : index + 1] * heads[3, index * 8 : index * 8 + 1]
            d_decay = (
                mm_exact(onward, cum_col + heads[1, at]) + mm_exact(earlier, heads[0, at]) + fac_row
            )
            dt = dt_ref[at]
            raw = (heads[2, at] - d_decay * rate) * sigmoid(zst[at])
            raw = jnp.where(used, raw, 0.0)
            srg_out[at] = raw.astype(LOW)
            bias_sum += jnp.sum(raw, axis=0, keepdims=True)
            decay_sum -= jnp.sum(
                jnp.where(used, d_decay * dt * rate, 0.0), axis=0, keepdims=True
            )
            score_low = d_score[at].astype(LOW)
            d_bc[at, :LANES] += mm_tn(score_low, bc[at, LANES:])
            d_bc[at, LANES:] += mm(score_low, bc[at, :LANES])
        small_out[...] = jnp.concatenate(
            [bias_sum, decay_sum, jnp.zeros((6, LANES), F32)], axis=0
        )
        pre = pre_state[...]
        s = sigmoid(pre)
        pg = d_bc[...] * s * (1.0 + pre * (1.0 - s))
        sums, grad = conv_backward(pg, cin_state[...].astype(F32), state_filter[...], masks)
        tap_state_out[...] = jnp.concatenate(sums + [jnp.zeros((3, WIDE), F32)], axis=0)
        cg_state_out[...] = grad[HALO:]
        edge_state_out[...] = grad[:HALO]


def scan_back(
    pre, dy, loc, carry, adj, cin, par, par_heads, state_filter, cin_state, pre_state, bc, bct,
    score, mask, sp, cumt, fac, match, zst, dt
):
    rows, wide = pre.shape
    ext = rows + HALO
    shape = jax.ShapeDtypeStruct
    column = lambda count: pl.BlockSpec((count, WIDE), lambda s: (0, s))
    outs = (
        (shape((rows, wide), F32), column(rows)),
        (shape((HALO, wide), F32), column(HALO)),
        (shape((8, wide), F32), column(8)),
        (shape((rows, WIDE), F32), const((rows, WIDE))),
        (shape((HALO, WIDE), F32), const((HALO, WIDE))),
        (shape((8, WIDE), F32), const((8, WIDE))),
        (shape((rows, LANES), LOW), const((rows, LANES))),
        (shape((8, LANES), F32), const((8, LANES))),
    )
    return pl.pallas_call(
        scan_back_body,
        out_shape=[out[0] for out in outs],
        grid=(6,),
        in_specs=[
            column(rows),
            column(rows),
            column(rows),
            column(NSTATE),
            column(NSTATE),
            column(ext),
            pl.BlockSpec((1, 8, WIDE), lambda s: (s // 3, 0, s % 3)),
            const((8, LANES)),
            const((8, WIDE)),
            const((ext, WIDE)),
            const((rows, WIDE)),
            const((rows, WIDE)),
            const((WIDE, rows)),
            const((rows, Q)),
            const((rows, Q)),
            const((4, rows, LANES)),
            const((6, 8, rows)),
            const((8, LANES)),
            const((CONV - 1, rows, LANES)),
            const((rows, LANES)),
            const((rows, LANES)),
        ],
        out_specs=[out[1] for out in outs],
        scratch_shapes=[
            pltpu.VMEM((rows, WIDE), F32),
            pltpu.VMEM((rows, Q), F32),
            pltpu.VMEM((6, 8, rows), F32),
            pltpu.VMEM((4, rows, LANES), F32),
        ],
        compiler_params=params(),
        name="scan_back",
    )(
        pre, dy, loc, carry, adj, cin, par, par_heads, state_filter, cin_state, pre_state, bc, bct,
        score, mask, sp, cumt, fac, match, zst, dt,
    )


def tail_body(
    which, tokens, cot, hidden_t, gpg, cg, edge, cg_state, edge_state, srg, w_gate, w_inner, w_small,
    gate_out, inner_out, small_out, token_out, norm_out, total
):
    step = pl.program_id(0)
    rows = gpg.shape[0]

    def joined(grad, arrived):
        return jnp.concatenate(
            [grad[: rows - HALO], grad[rows - HALO :] + arrived[...]], axis=0
        ).astype(LOW)

    @pl.when(step == 0)
    def _():
        state = joined(cg_state, edge_state)
        steps = srg[...]
        turned = hidden_t[...]
        small_out[:, :WIDE] = mm(turned, state).astype(LOW)
        small_out[:, WIDE:] = mm(turned, steps).astype(LOW)
        acc = mm_nt(state[:, :LANES], w_small[0, :, :LANES])
        acc += mm_nt(state[:, LANES:], w_small[1, :, :LANES])
        acc += mm_nt(steps, w_small[0, :, LANES:])
        acc += mm_nt(steps, w_small[1, :, LANES:])
        total[...] = acc

    grad = joined(cg, edge)
    gate_grad = gpg[...]
    turned = hidden_t[...]
    gate_out[0] = mm(turned, gate_grad).astype(LOW)
    inner_out[0] = mm(turned, grad).astype(LOW)
    total[...] += mm_nt(gate_grad, w_gate[0]) + mm_nt(grad, w_inner[0])

    @pl.when(step == 5)
    def _():
        value = tokens[0].astype(F32)
        scale = lax.rsqrt(jnp.mean(value * value, axis=1, keepdims=True) + EPSILON)
        hidden_grad = total[...]
        norm_sum = jnp.sum(hidden_grad * (value * scale), axis=0, keepdims=True)
        norm_out[...] = jnp.broadcast_to(norm_sum, norm_out.shape)
        gain = jnp.transpose(w_small[0, :, LANES : 2 * LANES].astype(F32))[24:25]
        normed = hidden_grad * gain
        pull = jnp.sum(normed * value, axis=1, keepdims=True) / value.shape[1]
        token_out[...] = (
            cot[0].astype(F32) + scale * normed - (scale * scale * scale) * value * pull
        )


def tail(which, tokens, cot, hidden_t, gpg, cg, edge, cg_state, edge_state, srg, weights):
    rows, model = tokens.shape[1:]
    shape = jax.ShapeDtypeStruct
    column = lambda count: pl.BlockSpec((count, WIDE), lambda s, w: (0, s))
    parts = pl.BlockSpec((1, model, WIDE), lambda s, w: (s // 3, 0, s % 3))
    outs = (
        (shape((2, model, 3 * WIDE), LOW), parts),
        (shape((2, model, 3 * WIDE), LOW), parts),
        (shape((model, WIDE + LANES), LOW), const((model, WIDE + LANES))),
        (shape((rows, model), F32), const((rows, model))),
        (shape((8, model), F32), const((8, model))),
    )
    return pl.pallas_call(
        tail_body,
        out_shape=[out[0] for out in outs],
        grid_spec=pltpu.PrefetchScalarGridSpec(
            num_scalar_prefetch=1,
            grid=(6,),
            in_specs=[
                pl.BlockSpec((1, rows, model), lambda s, w: (w[0], 0, 0)),
                pl.BlockSpec((1, rows, model), lambda s, w: (w[0], 0, 0)),
                const((model, rows)),
                column(rows),
                column(rows),
                column(HALO),
                const((rows, WIDE)),
                const((HALO, WIDE)),
                const((rows, LANES)),
                pl.BlockSpec((1, model, WIDE), lambda s, w: (s // 3, 0, s % 3)),
                pl.BlockSpec((1, model, WIDE), lambda s, w: (s // 3, 0, 3 + s % 3)),
                pl.BlockSpec((2, model, WIDE), lambda s, w: (0, 0, 9)),
            ],
            out_specs=[out[1] for out in outs],
            scratch_shapes=[pltpu.VMEM((rows, model), F32)],
        ),
        compiler_params=params(),
        name="tail",
    )(
        which, tokens, cot, hidden_t, gpg, cg, edge, cg_state, edge_state, srg, weights, weights,
        weights,
    )


def chained(fold, gain, hops, backward):
    count = lax.axis_size("context")
    by = -1 if backward else 1
    pairs = [(i, i + by) for i in range(count) if 0 <= i + by < count]
    carry = jnp.zeros_like(fold)
    for _ in range(hops):
        carry = lax.ppermute(fold + gain[0:1] * carry, "context", pairs)
    return carry


def body(
    tokens, documents, norm_gain, entry_weight, state_weight, step_weight, inner_kernel,
    state_filter, step_bias, decay_log, skip_gain, gate_gain, exit_weight, cotangent,
):
    every = ("tensor", "dp", "context")
    seqs, rows, model = tokens.shape
    count = lax.axis_size("context")
    position, side = lax.axis_index("context"), lax.axis_index("tensor")
    group_count = lax.axis_size("dp") * count
    own_rows = norm_gain.shape[0]
    which = jnp.reshape(side, (1,)).astype(jnp.int32)
    longest = rows * count // 4
    hops = min(count - 1, -(-(longest - 1) // rows))

    first = (side == 0).astype(F32)
    state_half = jnp.where(side == 0, state_weight[:, :NSTATE], state_weight[:, NSTATE:])
    packed = jnp.concatenate(
        [
            entry_weight[:, 0],
            entry_weight[:, 1],
            exit_weight,
            state_half,
            step_weight * first,
            step_weight * (1.0 - first),
            norm_gain[:, None],
            jnp.zeros((own_rows, LANES - 25), F32),
        ],
        axis=1,
    ).astype(LOW)
    weights = lax.all_gather(packed, every, axis=0, tiled=True).reshape(2, model, -1)

    def placed(v):
        return jnp.concatenate([v * first, v * (1.0 - first), jnp.zeros((LANES - 24,), F32)])

    row6 = jnp.concatenate(
        [placed(step_bias), placed(decay_log), placed(skip_gain), jnp.zeros((model - 3 * LANES,))]
    )
    par_own = jnp.concatenate(
        [inner_kernel, gate_gain[None], row6[None], jnp.zeros((1, model), F32)], axis=0
    )
    par = lax.all_gather(par_own, "tensor", axis=0)
    par_heads = jnp.concatenate(
        [(par[0, 6] + par[1, 6])[: 3 * LANES].reshape(3, LANES), jnp.zeros((5, LANES), F32)], axis=0
    )
    filt = jnp.concatenate([state_filter, jnp.zeros((3, WIDE), F32)], axis=0)

    docs = lax.dynamic_index_in_dim(documents, side, 0, keepdims=False).astype(F32)
    doc_col = jnp.broadcast_to(docs[:, None], (rows, LANES))
    doc_row = jnp.broadcast_to(docs[None], (8, rows))
    forward = [(i, i + 1) for i in range(count - 1)]
    own_tokens = lax.dynamic_index_in_dim(tokens, side, 0, keepdims=False)
    halo = lax.ppermute(own_tokens[-HALO:], "context", forward)
    halo_docs = lax.ppermute(doc_col[-HALO:], "context", forward)
    halo_docs = jnp.where(position == 0, -1.0, halo_docs)

    (
        hidden, cin, gate, pre, loc, fold, gain, cin_state, pre_state, bc, bct, score, mask, zst, dt,
        sp, cumt, fac, match,
    ) = front(which, tokens, halo, halo_docs, doc_col, doc_row, weights, par, par_heads, filt)
    carry = chained(fold, gain, hops, False)
    cot_t = lax.dynamic_index_in_dim(cotangent, side, 0, keepdims=False).T
    block_own, exit_part, dy, gpg, enter, gate_row, skip_row = middle(
        which, tokens, cotangent, cot_t, pre, gate, loc, carry, weights, par, par_heads, bc, bct,
        score, mask, sp, cumt, fac,
    )
    adj = chained(enter, gain, hops, True)
    cg, edge, taps, cg_state, edge_state, taps_state, srg, head_rows = scan_back(
        pre, dy, loc, carry, adj, cin, par, par_heads, filt, cin_state, pre_state, bc, bct, score,
        mask, sp, cumt, fac, match, zst, dt,
    )
    back = [(i + 1, i) for i in range(count - 1)]
    edge, edge_state = lax.ppermute((edge, edge_state), "context", back)
    gate_part, inner_part, small_part, token_own, norm_row = tail(
        which, tokens, cotangent, hidden.T, gpg, cg, edge, cg_state, edge_state, srg, weights
    )

    small_both = jnp.stack([small_part, small_part])
    parts = jnp.concatenate([gate_part, inner_part, exit_part, small_both], axis=2)
    mine = lax.psum_scatter(
        parts.reshape(2 * model, -1).astype(F32), every, scatter_dimension=0, tiled=True
    )
    smalls = lax.psum((taps, taps_state, gate_row, skip_row, head_rows, norm_row), every)
    taps, taps_state, gate_row, skip_row, head_rows, norm_row = smalls
    block_out = lax.all_gather(block_own, "tensor", axis=0)
    token_grad = lax.all_gather(token_own, "tensor", axis=0)
    wide = 3 * WIDE
    at = lax.axis_index("dp") * count + position
    half = lambda v: lax.dynamic_slice_in_dim(v, side * wide, wide, axis=-1)
    twelve = lambda v: lax.dynamic_slice_in_dim(v[:24], side * 12, 12, axis=0)
    step_grad = lax.dynamic_slice_in_dim(mine[:, 9 * WIDE + WIDE : 9 * WIDE + WIDE + 24], side * 12, 12, axis=1)
    return (
        block_out,
        token_grad,
        lax.dynamic_slice_in_dim(norm_row[0], at * own_rows, own_rows, axis=0),
        jnp.stack([mine[:, :wide], mine[:, wide : 2 * wide]], axis=1),
        mine[:, 9 * WIDE : 10 * WIDE],
        step_grad,
        half(taps[: CONV + 1]),
        taps_state[: CONV + 1],
        twelve(head_rows[0]),
        twelve(head_rows[1]),
        twelve(skip_row[0]),
        half(gate_row[0]),
        mine[:, 2 * wide : 3 * wide],
    )


def solution(mesh):
    in_specs = (
        P("dp", "context", None),
        P("dp", "context"),
        P(("dp", "context")),
        P(("dp", "context"), None, "tensor"),
        P(("dp", "context"), None),
        P(("dp", "context"), "tensor"),
        P(None, "tensor"),
        P(),
        P("tensor"),
        P("tensor"),
        P("tensor"),
        P("tensor"),
        P(("dp", "context"), "tensor"),
        P("dp", "context", None),
    )
    out_specs = (
        P("dp", "context", None),
        P("dp", "context", None),
        P(("dp", "context")),
        P(("dp", "context"), None, "tensor"),
        P(("dp", "context"), None),
        P(("dp", "context"), "tensor"),
        P(None, "tensor"),
        P(),
        P("tensor"),
        P("tensor"),
        P("tensor"),
        P("tensor"),
        P(("dp", "context"), "tensor"),
    )
    return jax.shard_map(body, mesh=mesh, in_specs=in_specs, out_specs=out_specs, check_vma=False)
```

```python
import functools
import jax
import jax.numpy as jnp
from jax import lax
from jax.experimental import pallas as pl
from jax.experimental.pallas import tpu as pltpu
from jax.sharding import PartitionSpec as P

HEAD = 64
NSTATE = 128
CONV = 4
EPSILON = 1e-05
Q = 128
HALO = 16
LANES = 128
WIDE = 256
LOG2E = 1.4426950408889634
FAR = -1e30
LOW = jnp.bfloat16
F32 = jnp.float32
VMEM_LIMIT = 60 * 1024 * 1024


def mm(a, b):
    return lax.dot_general(a, b, (((1,), (0,)), ((), ())), preferred_element_type=F32)


def mm_nt(a, b):
    return lax.dot_general(a, b, (((1,), (1,)), ((), ())), preferred_element_type=F32)


def mm_tn(a, b):
    return lax.dot_general(a, b, (((0,), (0,)), ((), ())), preferred_element_type=F32)


def mm_exact(a, b):
    return lax.dot_general(
        a, b, (((1,), (0,)), ((), ())), precision=lax.Precision.HIGHEST, preferred_element_type=F32
    )


def split3(v):
    high = v.astype(LOW).astype(F32)
    rest = v - high
    mid = rest.astype(LOW).astype(F32)
    low = rest - mid
    return (high + pltpu.roll(mid, 32, 1) + pltpu.roll(low, 64, 1)).astype(LOW)


def iota(shape, dim):
    return lax.broadcasted_iota(jnp.int32, shape, dim)


def spreader(first_head, width, count):
    k = iota((LANES, width * count), 0)
    lane = iota((LANES, width * count), 1)
    hit = ((k & 31) == first_head + lane // width) & (k < 96)
    return hit.astype(F32).astype(LOW)


def gatherer(first_head, width, count):
    lane = iota((width * count, LANES), 0)
    k = iota((width * count, LANES), 1)
    return (k == first_head + lane // width).astype(F32).astype(LOW)


def head_sums(v, collect):
    high = v.astype(LOW)
    rest = (v - high.astype(F32)).astype(LOW)
    return mm(high, collect) + mm(rest, collect)


def sigmoid(v):
    return 1.0 / (1.0 + jnp.exp(-v))


def twice(v):
    return jnp.concatenate([v, v], axis=1)


def conv_forward(cin, taps, masks):
    rows = cin.shape[0] - HALO
    out = taps[CONV : CONV + 1] + taps[CONV - 1 : CONV] * cin[HALO:]
    for back in range(1, CONV):
        part = cin[HALO - back : HALO - back + rows]
        out = out + taps[CONV - 1 - back : CONV - back] * (part * twice(masks[back - 1]))
    return out


def conv_backward(pg, cin, taps, masks):
    rows, width = pg.shape
    sums = [None] * (CONV + 1)
    sums[CONV] = jnp.sum(pg, axis=0, keepdims=True)
    sums[CONV - 1] = jnp.sum(pg * cin[HALO:], axis=0, keepdims=True)
    pad = jnp.zeros((HALO, width), F32)
    grad = jnp.concatenate([pad, pg * taps[CONV - 1 : CONV]], axis=0)
    for back in range(1, CONV):
        masked = pg * twice(masks[back - 1])
        part = cin[HALO - back : HALO - back + rows]
        sums[CONV - 1 - back] = jnp.sum(masked * part, axis=0, keepdims=True)
        padded = jnp.concatenate([pad, masked * taps[CONV - 1 - back : CONV - back], pad], axis=0)
        grad = grad + padded[back : back + rows + HALO]
    return sums, grad


def front_body(
    which, tokens, halo, halo_docs, doc_col, doc_row, w_gate, w_inner, w_small, par, par_heads,
    state_filter, hidden_out, cin_out, gate_out, pre_out, loc_out, fold_out, gain_out,
    cin_state_out, pre_state_out, bc_out, bct_out, score_out, mask_out, zst_out, dt_out, sp_out,
    cumt_out, fac_out, match_out, hidden, sp_tail, facs
):
    step = pl.program_id(0)
    rows = tokens.shape[1]
    spans = rows // Q

    @pl.when(step == 0)
    def _():
        gain_t = jnp.transpose(w_small[0, :, LANES : 2 * LANES].astype(F32))
        gain = gain_t[24:25]
        for ref, first, count in ((halo, 0, HALO), (tokens, HALO, rows)):
            value = (ref[...] if ref is halo else ref[0]).astype(F32)
            scale = lax.rsqrt(jnp.mean(value * value, axis=1, keepdims=True) + EPSILON)
            hidden[first : first + count] = (value * scale * gain).astype(LOW)
        hidden_out[...] = hidden[HALO:]
        both = [mm(hidden[...], w_small[index]) for index in range(2)]
        cin = jnp.concatenate([both[0][:, :LANES], both[1][:, :LANES]], axis=1).astype(LOW)
        cin_state_out[...] = cin
        docs = jnp.concatenate([halo_docs[...], doc_col[...]], axis=0)
        masks = []
        for back in range(1, CONV):
            match = (docs[HALO - back : HALO - back + rows] == docs[HALO:]).astype(F32)
            match_out[back - 1] = match
            masks.append(match)
        pre = conv_forward(cin.astype(F32), state_filter[...], masks)
        pre_state_out[...] = pre
        mixed = (pre * sigmoid(pre)).astype(LOW)
        bc_out[...] = mixed
        turned = jnp.transpose(mixed.astype(F32)).astype(LOW)
        bct_out[...] = turned
        heads = par_heads[...]
        used = iota((rows, LANES), 1) < 24
        raw = both[0][HALO:, LANES:] + both[1][HALO:, LANES:]
        zst = jnp.where(used, raw, 0.0) + heads[0:1]
        zst_out[...] = zst
        dt = jnp.where(used, jnp.maximum(zst, 0.0) + jnp.log1p(jnp.exp(-jnp.abs(zst))), 0.0)
        dt_out[...] = dt
        decay = -dt * jnp.exp(heads[1:2])
        t_at, u_at = iota((Q, Q), 0), iota((Q, Q), 1)
        lower = (t_at >= u_at).astype(F32)
        fac_rows = []
        for index in range(spans):
            at = slice(index * Q, (index + 1) * Q)
            cum = mm_exact(lower, decay[at])
            final = cum[Q - 1 : Q]
            before = docs[HALO + index * Q - 1 : HALO + index * Q]
            here = doc_col[at]
            last = here[Q - 1 : Q]
            opened = (here == before).astype(F32)
            tail = (here == last).astype(F32) * jnp.exp(final - cum)
            fac_rows.append((last == before).astype(F32) * jnp.exp(final))
            cum2 = cum * LOG2E
            turned_cum = jnp.transpose(cum2)
            for group in range(6):
                cumt_out[group, 0:4, at] = turned_cum[4 * group : 4 * group + 4]
            sp_out[0, at] = split3(dt[at])
            sp_out[1, at] = split3(cum2)
            lanes_used = iota((Q, LANES), 1) < 24
            sp_out[2, at] = split3(jnp.where(lanes_used, opened * jnp.exp(cum), 0.0))
            sp_out[3, at] = split3(jnp.where(lanes_used, tail, 0.0))
            sp_tail[at] = split3(jnp.where(lanes_used, tail * dt[at], 0.0))
            same = (t_at >= u_at) & (here == doc_row[0:1, at])
            mask_out[at] = jnp.where(same, 0.0, FAR)
            score_out[at] = mm_nt(mixed[at, LANES:], mixed[at, :LANES])
        gain_total = fac_rows[0]
        for row in fac_rows[1:]:
            gain_total = gain_total * row
        rows8 = jnp.concatenate(
            fac_rows + [gain_total] + [jnp.zeros((1, LANES), F32)] * (7 - spans), axis=0
        )
        rows8 = jnp.where(iota((8, LANES), 1) < 24, rows8, 0.0)
        fac_out[...] = rows8
        facs[...] = split3(rows8)

    cin = mm(hidden[...], w_inner[0]).astype(LOW)
    cin_out[...] = cin
    gate_out[...] = mm(hidden[HALO:], w_gate[0])
    masks = [match_out[back] for back in range(CONV - 1)]
    pre = conv_forward(cin.astype(F32), par[0], masks)
    pre_out[...] = pre
    spread = spreader(4 * step, HEAD, 4)
    value = (pre * sigmoid(pre) * mm(sp_tail[...], spread)).astype(LOW)
    facx = mm(facs[...], spread)
    fold = jnp.zeros((NSTATE, WIDE), F32)
    for index in range(spans):
        at = slice(index * Q, (index + 1) * Q)
        loc = mm(bct_out[:NSTATE, at], value[at])
        loc_out[at] = loc
        fold = facx[index : index + 1] * fold + loc
    fold_out[...] = fold
    gain_out[...] = jnp.broadcast_to(facx[spans : spans + 1], (8, WIDE))


def const(shape):
    zeros = (0,) * len(shape)
    return pl.BlockSpec(shape, lambda *_: zeros)


def params(**extra):
    return pltpu.CompilerParams(vmem_limit_bytes=VMEM_LIMIT, **extra)


def front(which, tokens, halo, halo_docs, doc_col, doc_row, weights, par, par_heads, state_filter):
    rows, model = tokens.shape[1:]
    wide = 2 * 3 * WIDE
    ext = rows + HALO
    shape = jax.ShapeDtypeStruct
    outs = (
        (shape((rows, model), LOW), const((rows, model))),
        (shape((ext, wide), LOW), pl.BlockSpec((ext, WIDE), lambda s, w: (0, s))),
        (shape((rows, wide), F32), pl.BlockSpec((rows, WIDE), lambda s, w: (0, s))),
        (shape((rows, wide), F32), pl.BlockSpec((rows, WIDE), lambda s, w: (0, s))),
        (shape((rows, wide), F32), pl.BlockSpec((rows, WIDE), lambda s, w: (0, s))),
        (shape((NSTATE, wide), F32), pl.BlockSpec((NSTATE, WIDE), lambda s, w: (0, s))),
        (shape((8, wide), F32), pl.BlockSpec((8, WIDE), lambda s, w: (0, s))),
        (shape((ext, WIDE), LOW), const((ext, WIDE))),
        (shape((rows, WIDE), F32), const((rows, WIDE))),
        (shape((rows, WIDE), LOW), const((rows, WIDE))),
        (shape((WIDE, rows), LOW), const((WIDE, rows))),
        (shape((rows, Q), F32), const((rows, Q))),
        (shape((rows, Q), F32), const((rows, Q))),
        (shape((rows, LANES), F32), const((rows, LANES))),
        (shape((rows, LANES), F32), const((rows, LANES))),
        (shape((4, rows, LANES), LOW), const((4, rows, LANES))),
        (shape((6, 8, rows), F32), const((6, 8, rows))),
        (shape((8, LANES), F32), const((8, LANES))),
        (shape((CONV - 1, rows, LANES), F32), const((CONV - 1, rows, LANES))),
    )
    return pl.pallas_call(
        front_body,
        out_shape=[out[0] for out in outs],
        grid_spec=pltpu.PrefetchScalarGridSpec(
            num_scalar_prefetch=1,
            grid=(6,),
            in_specs=[
                pl.BlockSpec((1, rows, model), lambda s, w: (w[0], 0, 0)),
                const((HALO, model)),
                const((HALO, LANES)),
                const((rows, LANES)),
                const((8, rows)),
                pl.BlockSpec((1, model, WIDE), lambda s, w: (s // 3, 0, s % 3)),
                pl.BlockSpec((1, model, WIDE), lambda s, w: (s // 3, 0, 3 + s % 3)),
                pl.BlockSpec((2, model, WIDE), lambda s, w: (0, 0, 9)),
                pl.BlockSpec((1, 8, WIDE), lambda s, w: (s // 3, 0, s % 3)),
                const((8, LANES)),
                const((8, WIDE)),
            ],
            out_specs=[out[1] for out in outs],
            scratch_shapes=[
                pltpu.VMEM((ext, model), LOW),
                pltpu.VMEM((rows, LANES), LOW),
                pltpu.VMEM((8, LANES), LOW),
            ],
        ),
        compiler_params=params(),
        name="front",
    )(
        which, tokens, halo, halo_docs, doc_col, doc_row, weights, weights, weights, par, par_heads,
        state_filter,
    )


def middle_body(
    which, tokens, cot, cot_t, pre_ref, gate_ref, loc_ref, carry_ref, w_exit, par, par_heads, bc,
    bct, score, mask, sp, cumt, fac, block_out, exit_out, dy_out, gpg_out, enter_out, row_out,
    skip_out, outputs, gates, unit_grads, mixes, sums, total
):
    step = pl.program_id(0)
    rows = pre_ref.shape[0]
    spans = rows // Q
    wide = 6 * WIDE

    @pl.when(step == 0)
    def _():
        sums[...] = jnp.zeros_like(sums)
        total[...] = jnp.zeros_like(total)
        skip_out[...] = jnp.zeros_like(skip_out)

    @pl.when(step < 6)
    def _():
        group = step
        spread = spreader(4 * group, HEAD, 4)
        pre = pre_ref[...]
        mix = pre * sigmoid(pre)
        mixes[group] = mix
        value = mix * mm(sp[0], spread)
        growth = mm(sp[2], spread)
        facx = mm(split3(fac[...]), spread)
        cums = mm(sp[1], spreader(4 * group, LANES, 4))
        skipx = mm(split3(par_heads[...]), spread)[2:3]
        state = carry_ref[...].astype(F32)
        half = iota((Q, LANES), 1) < HEAD
        for index in range(spans):
            at = slice(index * Q, (index + 1) * Q)
            carried = mm(bc[at, LANES:], state.astype(LOW)) * growth[at]
            parts = []
            for pair in range(2):
                lanes = slice(pair * LANES, (pair + 1) * LANES)
                local = None
                for side in range(2):
                    head = 2 * pair + side
                    across = cumt[group, head : head + 1, at]
                    spread_at = cums[at, head * LANES : (head + 1) * LANES] - across + mask[at]
                    weight = (jnp.exp2(spread_at) * score[at]).astype(LOW)
                    keep = half if side == 0 else jnp.logical_not(half)
                    seen = jnp.where(keep, value[at, lanes], 0.0).astype(LOW)
                    part = mm(weight, seen)
                    local = part if local is None else local + part
                parts.append(local)
            out = jnp.concatenate(parts, axis=1) + carried + skipx * mix[at]
            outputs[group, at] = out
            state = facx[index : index + 1] * state + loc_ref[at]
        gate = gate_ref[...]
        gates[group] = gate
        gated = outputs[group] * (gate * sigmoid(gate))
        unit_grad = mm(cot[0], w_exit[0])
        unit_grads[group] = unit_grad
        square = gated * gated
        cross = unit_grad * par[0, 5:6] * gated
        sums[0] += square[:, :LANES] + square[:, LANES:]
        sums[1] += cross[:, :LANES] + cross[:, LANES:]

    @pl.when(step == 5)
    def _():
        square = jnp.sum(sums[0], axis=1, keepdims=True)
        cross = jnp.sum(sums[1], axis=1, keepdims=True)
        normal = lax.rsqrt(square / wide + EPSILON)
        sums[0] = jnp.broadcast_to(normal, (rows, LANES))
        sums[1] = jnp.broadcast_to(normal * normal * normal * cross / wide, (rows, LANES))

    @pl.when(step >= 6)
    def _():
        group = step - 6
        spread = spreader(4 * group, HEAD, 4)
        normal = twice(sums[0])
        pull = twice(sums[1])
        gain = par[0, 5:6]
        gate = gates[group]
        out = outputs[group]
        unit_grad = unit_grads[group]
        sigma = sigmoid(gate)
        act = gate * sigma
        gated = out * act
        scaled_in = gated * normal
        unit = (scaled_in * gain).astype(LOW)
        total[...] += mm_nt(unit, w_exit[0])
        exit_out[0] = mm(cot_t[...], unit).astype(LOW)
        gate_sum = jnp.sum(unit_grad * scaled_in, axis=0, keepdims=True)
        gated_grad = normal * (unit_grad * gain) - pull * gated
        dy = gated_grad * act
        dy_out[...] = dy
        gpg_out[...] = (gated_grad * out * sigma * (1.0 + gate * (1.0 - sigma))).astype(LOW)
        skip_sum = jnp.sum(dy * mixes[group], axis=0, keepdims=True)
        row_out[...] = jnp.broadcast_to(gate_sum, (8, WIDE))
        skip_out[...] += head_sums(
            jnp.broadcast_to(skip_sum, (8, WIDE)), gatherer(4 * group, HEAD, 4)
        )
        facx = mm(split3(fac[...]), spread)
        pushed = (dy * mm(sp[2], spread)).astype(LOW)
        enter = jnp.zeros((NSTATE, WIDE), F32)
        for index in reversed(range(spans)):
            at = slice(index * Q, (index + 1) * Q)
            enter = facx[index : index + 1] * enter + mm(bct[NSTATE:, at], pushed[at])
        enter_out[...] = enter

    @pl.when(step == 11)
    def _():
        block_out[...] = (tokens[0].astype(F32) + total[...]).astype(LOW)


def middle(
    which, tokens, cot, cot_t, pre, gate, loc, carry, weights, par, par_heads, bc, bct, score, mask,
    sp, cumt, fac
):
    rows, model = tokens.shape[1:]
    wide = 6 * WIDE
    shape = jax.ShapeDtypeStruct

    def early(s):
        return jnp.minimum(s, 5)

    def late(s):
        return jnp.maximum(s - 6, 0)

    def group(s):
        return s % 6

    outs = (
        (shape((rows, model), LOW), const((rows, model))),
        (
            shape((2, model, 3 * WIDE), LOW),
            pl.BlockSpec((1, model, WIDE), lambda s, w: (late(s) // 3, 0, late(s) % 3)),
        ),
        (shape((rows, wide), F32), pl.BlockSpec((rows, WIDE), lambda s, w: (0, late(s)))),
        (shape((rows, wide), LOW), pl.BlockSpec((rows, WIDE), lambda s, w: (0, late(s)))),
        (shape((NSTATE, wide), F32), pl.BlockSpec((NSTATE, WIDE), lambda s, w: (0, late(s)))),
        (shape((8, wide), F32), pl.BlockSpec((8, WIDE), lambda s, w: (0, late(s)))),
        (shape((8, LANES), F32), const((8, LANES))),
    )
    return pl.pallas_call(
        middle_body,
        out_shape=[out[0] for out in outs],
        grid_spec=pltpu.PrefetchScalarGridSpec(
            num_scalar_prefetch=1,
            grid=(12,),
            in_specs=[
                pl.BlockSpec((1, rows, model), lambda s, w: (w[0], 0, 0)),
                pl.BlockSpec((1, rows, model), lambda s, w: (w[0], 0, 0)),
                const((model, rows)),
                pl.BlockSpec((rows, WIDE), lambda s, w: (0, early(s))),
                pl.BlockSpec((rows, WIDE), lambda s, w: (0, early(s))),
                pl.BlockSpec((rows, WIDE), lambda s, w: (0, early(s))),
                pl.BlockSpec((NSTATE, WIDE), lambda s, w: (0, early(s))),
                pl.BlockSpec((1, model, WIDE), lambda s, w: (group(s) // 3, 0, 6 + group(s) % 3)),
                pl.BlockSpec((1, 8, WIDE), lambda s, w: (group(s) // 3, 0, group(s) % 3)),
                const((8, LANES)),
                const((rows, WIDE)),
                const((WIDE, rows)),
                const((rows, Q)),
                const((rows, Q)),
                const((4, rows, LANES)),
                const((6, 8, rows)),
                const((8, LANES)),
            ],
            out_specs=[out[1] for out in outs],
            scratch_shapes=[
                pltpu.VMEM((6, rows, WIDE), F32),
                pltpu.VMEM((6, rows, WIDE), F32),
                pltpu.VMEM((6, rows, WIDE), F32),
                pltpu.VMEM((6, rows, WIDE), F32),
                pltpu.VMEM((2, rows, LANES), F32),
                pltpu.VMEM((rows, model), F32),
            ],
        ),
        compiler_params=params(),
        name="middle",
    )(
        which, tokens, cot, cot_t, pre, gate, loc, carry, weights, par, par_heads, bc, bct, score,
        mask, sp, cumt, fac,
    )


def scan_back_body(
    pre_ref, dy_ref, loc_ref, carry_ref, adj_ref, cin_ref, par, par_heads, state_filter, cin_state,
    pre_state, bc, bct, score, mask, sp, cumt, fac, match, zst, dt_ref, cg_out, edge_out, tap_out,
    cg_state_out, edge_state_out, tap_state_out, srg_out, small_out, d_bc, d_score, d_cum, heads
):
    group = pl.program_id(0)
    rows = pre_ref.shape[0]
    spans = rows // Q

    @pl.when(group == 0)
    def _():
        d_bc[...] = jnp.zeros_like(d_bc)
        d_score[...] = jnp.zeros_like(d_score)
        d_cum[...] = jnp.zeros_like(d_cum)
        heads[...] = jnp.zeros_like(heads)

    spread = spreader(4 * group, HEAD, 4)
    collect = gatherer(4 * group, HEAD, 4)
    pre = pre_ref[...]
    sigma = sigmoid(pre)
    mix = pre * sigma
    dtx = mm(sp[0], spread)
    growth = mm(sp[2], spread)
    tails = mm(sp[3], spread)
    facx = mm(split3(fac[...]), spread)
    cums = mm(sp[1], spreader(4 * group, LANES, 4))
    skipx = mm(split3(par_heads[...]), spread)[2:3]
    states = [carry_ref[...].astype(F32)]
    for index in range(spans - 1):
        at = slice(index * Q, (index + 1) * Q)
        states.append(facx[index : index + 1] * states[-1] + loc_ref[at])
    adjoint = adj_ref[...].astype(F32)
    half = iota((Q, LANES), 1) < HEAD
    ones = jnp.ones((8, Q), F32).astype(LOW)
    masks = [match[back] for back in range(CONV - 1)]
    pgs = [None] * spans
    for index in reversed(range(spans)):
        at = slice(index * Q, (index + 1) * Q)
        dy = dy_ref[at]
        value = mix[at] * dtx[at]
        state_low, adj_low = states[index].astype(LOW), adjoint.astype(LOW)
        pushed = dy * growth[at]
        pushed_low = pushed.astype(LOW)
        reached = mm(bc[at, :LANES], adj_low) * tails[at]
        carried = mm(bc[at, LANES:], state_low)
        d_bc[at, :LANES] += mm_nt((value * tails[at]).astype(LOW), adj_low)
        d_bc[at, LANES:] += mm_nt(pushed_low, state_low)
        heads[0, at] += head_sums(value * reached, collect)
        heads[1, at] += head_sums(pushed * carried, collect)
        fac_part = jnp.sum(adjoint * states[index], axis=0, keepdims=True)
        heads[3, index * 8 : index * 8 + 8] += head_sums(
            jnp.broadcast_to(fac_part, (8, WIDE)), collect
        )
        adjoint = facx[index : index + 1] * adjoint + mm(bct[NSTATE:, at], pushed_low)
        parts = []
        sum_score = None
        for pair in range(2):
            lanes = slice(pair * LANES, (pair + 1) * LANES)
            value_low = value[:, lanes].astype(LOW)
            local = None
            for side in range(2):
                head = 2 * pair + side
                across = cumt[group, head : head + 1, at]
                spread_at = cums[at, head * LANES : (head + 1) * LANES] - across + mask[at]
                decay = jnp.exp2(spread_at)
                keep = half if side == 0 else jnp.logical_not(half)
                dy_low = jnp.where(keep, dy[:, lanes], 0.0).astype(LOW)
                inner = decay * mm_nt(dy_low, value_low)
                sum_score = inner if sum_score is None else sum_score + inner
                moved = (inner * score[at]).astype(LOW)
                turn = mm_nt(ones, moved) - mm(ones, moved)
                d_cum[group, head : head + 1, at] = turn[0:1]
                part = mm_tn((decay * score[at]).astype(LOW), dy_low)
                local = part if local is None else local + part
            parts.append(local)
        d_score[at] += sum_score
        d_value = jnp.concatenate(parts, axis=1) + reached
        heads[2, at] += head_sums(mix[at] * d_value, collect)
        d_mix = dtx[at] * d_value + skipx * dy
        s = sigma[at]
        pgs[index] = d_mix * s * (1.0 + pre[at] * (1.0 - s))
    pg = jnp.concatenate(pgs, axis=0)
    sums, grad = conv_backward(pg, cin_ref[...].astype(F32), par[0], masks)
    tap_out[...] = jnp.concatenate(sums + [jnp.zeros((3, WIDE), F32)], axis=0)
    cg_out[...] = grad[HALO:]
    edge_out[...] = grad[:HALO]

    @pl.when(group == 5)
    def _():
        t_at, u_at = iota((Q, Q), 0), iota((Q, Q), 1)
        onward = (t_at <= u_at).astype(F32)
        earlier = (t_at > u_at).astype(F32)
        rate = jnp.exp(par_heads[1:2])
        bias_sum = jnp.zeros((1, LANES), F32)
        decay_sum = jnp.zeros((1, LANES), F32)
        used = iota((Q, LANES), 1) < 24
        for index in range(spans):
            at = slice(index * Q, (index + 1) * Q)
            pieces = [d_cum[piece, 0:4, at] for piece in range(6)]
            pieces.append(jnp.zeros((LANES - 24, Q), F32))
            cum_col = jnp.transpose(jnp.concatenate(pieces, axis=0))
            fac_row = fac[index : index + 1] * heads[3, index * 8 : index * 8 + 1]
            d_decay = (
                mm_exact(onward, cum_col + heads[1, at]) + mm_exact(earlier, heads[0, at]) + fac_row
            )
            dt = dt_ref[at]
            raw = (heads[2, at] - d_decay * rate) * sigmoid(zst[at])
            raw = jnp.where(used, raw, 0.0)
            srg_out[at] = raw.astype(LOW)
            bias_sum += jnp.sum(raw, axis=0, keepdims=True)
            decay_sum -= jnp.sum(
                jnp.where(used, d_decay * dt * rate, 0.0), axis=0, keepdims=True
            )
            score_low = d_score[at].astype(LOW)
            d_bc[at, :LANES] += mm_tn(score_low, bc[at, LANES:])
            d_bc[at, LANES:] += mm(score_low, bc[at, :LANES])
        small_out[...] = jnp.concatenate(
            [bias_sum, decay_sum, jnp.zeros((6, LANES), F32)], axis=0
        )
        pre = pre_state[...]
        s = sigmoid(pre)
        pg = d_bc[...] * s * (1.0 + pre * (1.0 - s))
        sums, grad = conv_backward(pg, cin_state[...].astype(F32), state_filter[...], masks)
        tap_state_out[...] = jnp.concatenate(sums + [jnp.zeros((3, WIDE), F32)], axis=0)
        cg_state_out[...] = grad[HALO:]
        edge_state_out[...] = grad[:HALO]


def scan_back(
    pre, dy, loc, carry, adj, cin, par, par_heads, state_filter, cin_state, pre_state, bc, bct,
    score, mask, sp, cumt, fac, match, zst, dt
):
    rows, wide = pre.shape
    ext = rows + HALO
    shape = jax.ShapeDtypeStruct
    column = lambda count: pl.BlockSpec((count, WIDE), lambda s: (0, s))
    outs = (
        (shape((rows, wide), F32), column(rows)),
        (shape((HALO, wide), F32), column(HALO)),
        (shape((8, wide), F32), column(8)),
        (shape((rows, WIDE), F32), const((rows, WIDE))),
        (shape((HALO, WIDE), F32), const((HALO, WIDE))),
        (shape((8, WIDE), F32), const((8, WIDE))),
        (shape((rows, LANES), LOW), const((rows, LANES))),
        (shape((8, LANES), F32), const((8, LANES))),
    )
    return pl.pallas_call(
        scan_back_body,
        out_shape=[out[0] for out in outs],
        grid=(6,),
        in_specs=[
            column(rows),
            column(rows),
            column(rows),
            column(NSTATE),
            column(NSTATE),
            column(ext),
            pl.BlockSpec((1, 8, WIDE), lambda s: (s // 3, 0, s % 3)),
            const((8, LANES)),
            const((8, WIDE)),
            const((ext, WIDE)),
            const((rows, WIDE)),
            const((rows, WIDE)),
            const((WIDE, rows)),
            const((rows, Q)),
            const((rows, Q)),
            const((4, rows, LANES)),
            const((6, 8, rows)),
            const((8, LANES)),
            const((CONV - 1, rows, LANES)),
            const((rows, LANES)),
            const((rows, LANES)),
        ],
        out_specs=[out[1] for out in outs],
        scratch_shapes=[
            pltpu.VMEM((rows, WIDE), F32),
            pltpu.VMEM((rows, Q), F32),
            pltpu.VMEM((6, 8, rows), F32),
            pltpu.VMEM((4, rows, LANES), F32),
        ],
        compiler_params=params(),
        name="scan_back",
    )(
        pre, dy, loc, carry, adj, cin, par, par_heads, state_filter, cin_state, pre_state, bc, bct,
        score, mask, sp, cumt, fac, match, zst, dt,
    )


def tail_body(
    which, tokens, cot, hidden_t, gpg, cg, edge, cg_state, edge_state, srg, w_gate, w_inner, w_small,
    gate_out, inner_out, small_out, token_out, norm_out, total
):
    step = pl.program_id(0)
    rows = gpg.shape[0]

    def joined(grad, arrived):
        return jnp.concatenate(
            [grad[: rows - HALO], grad[rows - HALO :] + arrived[...]], axis=0
        ).astype(LOW)

    @pl.when(step == 0)
    def _():
        state = joined(cg_state, edge_state)
        steps = srg[...]
        turned = hidden_t[...]
        state_part = mm(turned, state).astype(LOW)
        step_part = mm(turned, steps).astype(LOW)
        for part in range(2):
            small_out[part, :, :LANES] = state_part[:, part * LANES : (part + 1) * LANES]
            small_out[part, :, LANES:] = step_part
        acc = mm_nt(state[:, :LANES], w_small[0, :, :LANES])
        acc += mm_nt(state[:, LANES:], w_small[1, :, :LANES])
        acc += mm_nt(steps, w_small[0, :, LANES:])
        acc += mm_nt(steps, w_small[1, :, LANES:])
        total[...] = acc

    grad = joined(cg, edge)
    gate_grad = gpg[...]
    turned = hidden_t[...]
    gate_out[0] = mm(turned, gate_grad).astype(LOW)
    inner_out[0] = mm(turned, grad).astype(LOW)
    total[...] += mm_nt(gate_grad, w_gate[0]) + mm_nt(grad, w_inner[0])

    @pl.when(step == 5)
    def _():
        value = tokens[0].astype(F32)
        scale = lax.rsqrt(jnp.mean(value * value, axis=1, keepdims=True) + EPSILON)
        hidden_grad = total[...]
        norm_sum = jnp.sum(hidden_grad * (value * scale), axis=0, keepdims=True)
        norm_out[...] = jnp.broadcast_to(norm_sum, norm_out.shape)
        gain = jnp.transpose(w_small[0, :, LANES : 2 * LANES].astype(F32))[24:25]
        normed = hidden_grad * gain
        pull = jnp.sum(normed * value, axis=1, keepdims=True) / value.shape[1]
        token_out[...] = (
            cot[0].astype(F32) + scale * normed - (scale * scale * scale) * value * pull
        ).astype(LOW)


def tail(which, tokens, cot, hidden_t, gpg, cg, edge, cg_state, edge_state, srg, weights):
    rows, model = tokens.shape[1:]
    shape = jax.ShapeDtypeStruct
    column = lambda count: pl.BlockSpec((count, WIDE), lambda s, w: (0, s))
    parts = pl.BlockSpec((1, model, WIDE), lambda s, w: (s // 3, 0, s % 3))
    outs = (
        (shape((2, model, 3 * WIDE), LOW), parts),
        (shape((2, model, 3 * WIDE), LOW), parts),
        (shape((2, model, WIDE), LOW), const((2, model, WIDE))),
        (shape((rows, model), LOW), const((rows, model))),
        (shape((8, model), F32), const((8, model))),
    )
    return pl.pallas_call(
        tail_body,
        out_shape=[out[0] for out in outs],
        grid_spec=pltpu.PrefetchScalarGridSpec(
            num_scalar_prefetch=1,
            grid=(6,),
            in_specs=[
                pl.BlockSpec((1, rows, model), lambda s, w: (w[0], 0, 0)),
                pl.BlockSpec((1, rows, model), lambda s, w: (w[0], 0, 0)),
                const((model, rows)),
                column(rows),
                column(rows),
                column(HALO),
                const((rows, WIDE)),
                const((HALO, WIDE)),
                const((rows, LANES)),
                pl.BlockSpec((1, model, WIDE), lambda s, w: (s // 3, 0, s % 3)),
                pl.BlockSpec((1, model, WIDE), lambda s, w: (s // 3, 0, 3 + s % 3)),
                pl.BlockSpec((2, model, WIDE), lambda s, w: (0, 0, 9)),
            ],
            out_specs=[out[1] for out in outs],
            scratch_shapes=[pltpu.VMEM((rows, model), F32)],
        ),
        compiler_params=params(),
        name="tail",
    )(
        which, tokens, cot, hidden_t, gpg, cg, edge, cg_state, edge_state, srg, weights, weights,
        weights,
    )


def ring_place():
    position = lax.axis_index("context")
    return {
        "x": lax.axis_index("dp"),
        "y": lax.axis_index("tensor"),
        "z": position // 2,
        "c": position % 2,
    }


def device(x, y, z, c):
    return {"dp": x, "context": z * 2 + c, "tensor": y}


def remote(src, dst, send_sem, recv_sem, target):
    return pltpu.make_async_remote_copy(
        src_ref=src,
        dst_ref=dst,
        send_sem=send_sem,
        recv_sem=recv_sem,
        device_id=target,
        device_id_type=pl.DeviceIdType.MESH,
    )


def greet(targets, depth):
    barrier = pltpu.get_barrier_semaphore()
    for target in targets:
        pl.semaphore_signal(barrier, inc=1, device_id=target, device_id_type=pl.DeviceIdType.MESH)
    if depth > 1:
        here = ring_place()

        def one(step, carry):
            away = lax.rem(here["z"] + step, depth)
            pl.semaphore_signal(
                barrier,
                inc=1,
                device_id=device(here["x"], here["y"], away, here["c"]),
                device_id_type=pl.DeviceIdType.MESH,
            )
            return carry

        lax.fori_loop(1, depth, one, 0)
    pl.semaphore_wait(barrier, len(targets) + max(depth - 1, 0))


def each(count, run, first=0):
    def one(step, carry):
        run(step)
        return carry

    lax.fori_loop(first, count, one, 0)


def gather_body(
    depth, packed, par_own, edge_own, docs_own, weights, par, edge, docs, docs_in, sends, lands,
    side_send, side_land, local
):
    here = ring_place()
    x, y, z, c = here["x"], here["y"], here["z"], here["c"]
    count = 2 * depth
    position = z * 2 + c
    onward, behind = lax.rem(position + 1, count), lax.rem(position + count - 1, count)
    other = 1 - c
    x1, y1 = x + (1 - c) * (1 - 2 * x), y + c * (1 - 2 * y)
    x2, y2 = x + c * (1 - 2 * x), y + (1 - c) * (1 - 2 * y)
    partner = device(x, y, z, other)
    first_peer, second_peer = device(x1, y1, z, c), device(x2, y2, z, c)
    y_peer = device(x, 1 - y, z, c)
    next_one = {"dp": x, "context": onward, "tensor": y}
    last_one = {"dp": x, "context": behind, "tensor": y}
    greet([partner, device(1 - x, y, z, c), y_peer, next_one, last_one], depth)

    def chunk(cx, cy, cz, cc):
        return weights.at[cy, cx, cz * 2 + cc]

    def landed(cx, cy, cz, cc):
        return lands.at[((cy * 2 + cx) * depth + cz) * 2 + cc]

    def moved(kind, index, cx, cy, cz, cc, target, own=False):
        return remote(
            packed if own else chunk(cx, cy, cz, cc),
            chunk(cx, cy, cz, cc),
            sends.at[kind, index],
            landed(cx, cy, cz, cc),
            target,
        )

    def arrive(cx, cy, cz, cc):
        moved(0, 0, cx, cy, cz, cc, partner).wait_recv()

    sides = [
        remote(edge_own, edge, side_send.at[0], side_land.at[0], next_one),
        remote(docs_own, docs_in, side_send.at[1], side_land.at[1], next_one),
        remote(par_own, par.at[y], side_send.at[2], side_land.at[2], y_peer),
    ]
    keep = pltpu.make_async_copy(packed, chunk(x, y, z, c), local.at[0])
    keep_par = pltpu.make_async_copy(par_own, par.at[y], local.at[1])
    keep.start()
    keep_par.start()

    def to_depth(step):
        away = lax.rem(z + step, depth)
        return moved(3, step, x, y, z, c, device(x, y, away, c), True)

    own_first = moved(1, 0, x, y, z, c, first_peer, True)
    own_second = moved(2, 0, x, y, z, c, second_peer, True)
    own_core = moved(0, 0, x, y, z, c, partner, True)
    own_first.start()
    own_second.start()
    each(depth, lambda step: to_depth(step).start(), 1)
    own_core.start()
    for copy in sides:
        copy.start()

    def near(step):
        away = lax.rem(z + depth - step, depth)
        arrive(x, y, away, c)
        moved(1, step, x, y, away, c, first_peer).start()
        moved(2, step, x, y, away, c, second_peer).start()
        moved(0, step, x, y, away, c, partner).start()

    each(depth, near, 1)

    def across(step):
        away = lax.rem(z + depth - step, depth)
        arrive(x1, y1, away, c)
        moved(2, depth + step, x1, y1, away, c, second_peer).start()
        moved(0, depth + step, x1, y1, away, c, partner).start()

    each(depth, across)

    def far(step):
        away = lax.rem(z + depth - step, depth)
        arrive(x2, y2, away, c)
        moved(0, 2 * depth + step, x2, y2, away, c, partner).start()
        arrive(1 - x, 1 - y, away, c)
        moved(0, 3 * depth + step, 1 - x, 1 - y, away, c, partner).start()

    each(depth, far)

    def from_core(step):
        arrive(x, y, step, other)
        arrive(1 - x, y, step, other)
        arrive(x, 1 - y, step, other)
        arrive(1 - x, 1 - y, step, other)

    each(depth, from_core)
    for copy in sides:
        copy.wait_recv()
    docs[...] = jnp.where(position == 0, -1.0, docs_in[...])
    each(4 * depth, lambda step: moved(0, step, x, y, z, c, partner).wait_send())
    each(depth, lambda step: moved(1, step, x, y, z, c, partner).wait_send())
    each(2 * depth, lambda step: moved(2, step, x, y, z, c, partner).wait_send())
    each(depth, lambda step: moved(3, step, x, y, z, c, partner).wait_send(), 1)
    for copy in sides:
        copy.wait_send()
    keep.wait()
    keep_par.wait()


def gather(packed, par_own, edge_own, docs_own):
    count = lax.axis_size("context")
    depth = count // 2
    shape = jax.ShapeDtypeStruct
    vmem = pl.BlockSpec(memory_space=pltpu.VMEM)
    return pl.pallas_call(
        functools.partial(gather_body, depth),
        out_shape=(
            shape((2, 2, count) + packed.shape, LOW),
            shape((2,) + par_own.shape, F32),
            shape(edge_own.shape, LOW),
            shape(docs_own.shape, F32),
        ),
        in_specs=[vmem] * 4,
        out_specs=[pl.BlockSpec(memory_space=pl.ANY), vmem, vmem, vmem],
        scratch_shapes=[
            pltpu.VMEM(docs_own.shape, F32),
            pltpu.SemaphoreType.DMA((4, 4 * depth)),
            pltpu.SemaphoreType.DMA((8 * depth,)),
            pltpu.SemaphoreType.DMA((3,)),
            pltpu.SemaphoreType.DMA((3,)),
            pltpu.SemaphoreType.DMA((2,)),
        ],
        compiler_params=params(collective_id=0, has_side_effects=True),
        name="gather",
    )(packed, par_own, edge_own, docs_own)


CUTS = 4


def chain_body(
    depth, rounds, backward, fold, gain, out, from_mate, from_chip, to_mate, to_chip, mate_send,
    mate_land, chip_send, chip_land
):
    here = ring_place()
    x, y, z, c = here["x"], here["y"], here["z"], here["c"]
    first = 1 if backward else 0
    order = depth - 1 - z if backward else z
    by = -1 if backward else 1
    width = fold.shape[1] // CUTS
    mate = device(x, y, z, 1 - c)
    after = device(x, y, z + by, first)
    before = device(x, y, z - by, 1 - first)
    leads = c == first
    barrier = pltpu.get_barrier_semaphore()

    def signal(target):
        pl.semaphore_signal(barrier, inc=1, device_id=target, device_id_type=pl.DeviceIdType.MESH)

    signal(mate)

    linked_before = leads & (order > 0)
    linked_after = jnp.logical_not(leads) & (order < depth - 1)

    @pl.when(linked_before)
    def _():
        signal(before)

    @pl.when(linked_after)
    def _():
        signal(after)

    pl.semaphore_wait(
        barrier, 1 + linked_before.astype(jnp.int32) + linked_after.astype(jnp.int32)
    )

    def mate_copy(turn, cut):
        return remote(
            to_mate.at[turn, cut], from_mate.at[turn, cut], mate_send.at[turn, cut],
            mate_land.at[turn, cut], mate,
        )

    def chip_copy(turn, cut):
        return remote(
            to_chip.at[turn, cut], from_chip.at[turn, cut], chip_send.at[turn, cut],
            chip_land.at[turn, cut], after,
        )

    def lanes(cut):
        return slice(cut * width, (cut + 1) * width)

    def joined(cut, arrived):
        at = lanes(cut)
        return (fold[:, at] + gain[0:1, at] * arrived.astype(F32)).astype(LOW)

    @pl.when(leads)
    def _():
        for cut in range(CUTS):
            to_mate[0, cut] = fold[:, lanes(cut)].astype(LOW)
            mate_copy(0, cut).start()

        @pl.when(order > 0)
        def _():
            for turn in range(rounds):
                for cut in range(CUTS):
                    chip_copy(turn, cut).wait_recv()
                    to_mate[turn + 1, cut] = joined(cut, from_chip[turn, cut])
                    mate_copy(turn + 1, cut).start()
            for cut in range(CUTS):
                out[:, lanes(cut)] = from_chip[rounds - 1, cut]

        @pl.when(order == 0)
        def _():
            for turn in range(rounds):
                for cut in range(CUTS):
                    to_mate[turn + 1, cut] = fold[:, lanes(cut)].astype(LOW)
                    mate_copy(turn + 1, cut).start()
            out[...] = jnp.zeros_like(out)

        for turn in range(rounds + 1):
            for cut in range(CUTS):
                mate_copy(turn, cut).wait_send()

    @pl.when(jnp.logical_not(leads))
    def _():
        for turn in range(rounds):
            for cut in range(CUTS):
                mate_copy(turn, cut).wait_recv()

                @pl.when(order < depth - 1)
                def _():
                    to_chip[turn, cut] = joined(cut, from_mate[turn, cut])
                    chip_copy(turn, cut).start()

        for cut in range(CUTS):
            mate_copy(rounds, cut).wait_recv()
            out[:, lanes(cut)] = from_mate[rounds, cut]

        @pl.when(order < depth - 1)
        def _():
            for turn in range(rounds):
                for cut in range(CUTS):
                    chip_copy(turn, cut).wait_send()


def chain(fold, gain, rounds, backward, number):
    depth = lax.axis_size("context") // 2
    states, wide = fold.shape
    vmem = pl.BlockSpec(memory_space=pltpu.VMEM)
    slots = lambda turns: pltpu.VMEM((turns, CUTS, states, wide // CUTS), LOW)
    marks = lambda turns: pltpu.SemaphoreType.DMA((turns, CUTS))
    return pl.pallas_call(
        functools.partial(chain_body, depth, rounds, backward),
        out_shape=jax.ShapeDtypeStruct(fold.shape, LOW),
        in_specs=[vmem] * 2,
        out_specs=vmem,
        scratch_shapes=[
            slots(rounds + 1),
            slots(rounds),
            slots(rounds + 1),
            slots(rounds),
            marks(rounds + 1),
            marks(rounds + 1),
            marks(rounds),
            marks(rounds),
        ],
        compiler_params=params(collective_id=number, has_side_effects=True),
        name="chain_back" if backward else "chain",
    )(fold, gain)


def edges_body(count, own, own_state, out, out_state, send, land):
    position = lax.axis_index("context")
    before, after = {"context": position - 1}, {"context": position + 1}
    barrier = pltpu.get_barrier_semaphore()

    def signal(target):
        pl.semaphore_signal(barrier, inc=1, device_id=target, device_id_type=pl.DeviceIdType.MESH)

    @pl.when(position > 0)
    def _():
        signal(before)

    @pl.when(position < count - 1)
    def _():
        signal(after)

    has_before = (position > 0).astype(jnp.int32)
    has_after = (position < count - 1).astype(jnp.int32)
    pl.semaphore_wait(barrier, has_before + has_after)

    copies = [
        remote(own, out, send.at[0], land.at[0], before),
        remote(own_state, out_state, send.at[1], land.at[1], before),
    ]

    @pl.when(position > 0)
    def _():
        for copy in copies:
            copy.start()

    @pl.when(position == count - 1)
    def _():
        out[...] = jnp.zeros_like(out)
        out_state[...] = jnp.zeros_like(out_state)

    @pl.when(position < count - 1)
    def _():
        for copy in copies:
            copy.wait_recv()

    @pl.when(position > 0)
    def _():
        for copy in copies:
            copy.wait_send()


def edges(own, own_state):
    vmem = pl.BlockSpec(memory_space=pltpu.VMEM)
    return pl.pallas_call(
        functools.partial(edges_body, lax.axis_size("context")),
        out_shape=(
            jax.ShapeDtypeStruct(own.shape, F32),
            jax.ShapeDtypeStruct(own_state.shape, F32),
        ),
        in_specs=[vmem] * 2,
        out_specs=[vmem] * 2,
        scratch_shapes=[pltpu.SemaphoreType.DMA((2,)), pltpu.SemaphoreType.DMA((2,))],
        compiler_params=params(collective_id=3, has_side_effects=True),
        name="edges",
    )(own, own_state)


def reduce_body(
    depth, gate, inner, exits, small, token, vector, out, state_out, vector_out, token_out, own, core,
    send1, land1, send2, land2, send3, land3, state_own, vec_send, vec_land, own_sem, core_send,
    core_land, s1, l1, s2, l2, s3, l3, vs, vl, ts, tl, keep_sem
):
    here = ring_place()
    x, y, z, c = here["x"], here["y"], here["z"], here["c"]
    other = 1 - c
    x1, y1 = x + (1 - c) * (1 - 2 * x), y + c * (1 - 2 * y)
    x2, y2 = x + c * (1 - 2 * x), y + (1 - c) * (1 - 2 * y)
    partner = device(x, y, z, other)
    first_peer, second_peer = device(x1, y1, z, c), device(x2, y2, z, c)
    x_peer, y_peer = device(1 - x, y, z, c), device(x, 1 - y, z, c)
    wide = gate.shape[-1]
    tall = 3 * wide
    greet([partner, x_peer, y_peer], depth)
    pieces = [
        (gate, slice(0, wide)),
        (inner, slice(wide, 2 * wide)),
        (exits, slice(2 * wide, tall)),
        (small, slice(tall, tall + WIDE)),
    ]

    token_copy = remote(token, token_out.at[y], ts.at[0], tl.at[0], y_peer)
    token_keep = pltpu.make_async_copy(token, token_out.at[y], keep_sem.at[0])
    token_keep.start()

    def spot(step):
        return lax.rem(z + 1 + step, depth)

    def core_pieces(cx, cy, cz):
        for ref, cols in pieces:
            yield remote(
                ref.at[cy, cx, cz * 2 + other],
                core.at[cy, cx, cz, :, cols],
                core_send.at[cy, cx, cz],
                core_land.at[cy, cx, cz],
                partner,
            )

    def core_whole(cx, cy, cz):
        return remote(
            core.at[cy, cx, cz], core.at[cy, cx, cz], core_send.at[cy, cx, cz],
            core_land.at[cy, cx, cz], partner,
        )

    def own_pieces(cx, cy, cz):
        for ref, cols in pieces:
            yield pltpu.make_async_copy(
                ref.at[cy, cx, cz * 2 + c], own.at[cy, cx, cz, :, cols], own_sem.at[cy, cx, cz]
            )

    def own_whole(cx, cy, cz):
        return pltpu.make_async_copy(
            own.at[cy, cx, cz], own.at[cy, cx, cz], own_sem.at[cy, cx, cz]
        )

    def start(step):
        cz = spot(step)
        for cy in range(2):
            for cx in range(2):
                for copy in core_pieces(cx, cy, cz):
                    copy.start()
                for copy in own_pieces(cx, cy, cz):
                    copy.start()

    vec_send[0] = vector[...]
    vec_targets = [partner, x_peer, y_peer]

    def vec_copy(turn):
        return remote(vec_send.at[turn], vec_land.at[turn], vs.at[turn], vl.at[turn], vec_targets[turn])

    def vec_far(step):
        away = lax.rem(z + step, depth)
        return remote(
            vec_send.at[3], vec_land.at[3 + z], vs.at[2 + step], vl.at[3 + z],
            device(x, y, away, c),
        )

    vec_copy(0).start()
    each(depth, start)
    token_copy.start()
    for turn in range(3):
        vec_copy(turn).wait_recv()
        vec_send[turn + 1] = vec_send[turn] + vec_land[turn]
        if turn < 2:
            vec_copy(turn + 1).start()
    each(depth, lambda step: vec_far(step).start(), 1)
    vec_land[3 + z] = vec_send[3]

    def base(cx, cy, cz):
        return own[cy, cx, cz].astype(F32) + core[cy, cx, cz].astype(F32)

    def first_copy(cz):
        return remote(send1.at[cz], land1.at[cz], s1.at[cz], l1.at[cz], first_peer)

    def second_copy(cz):
        return remote(send2.at[cz], land2.at[cz], s2.at[cz], l2.at[cz], second_peer)

    def third_copy(cz):
        return remote(
            send3.at[cz], land3.at[z], s3.at[cz], l3.at[z], device(x, y, cz, c)
        )

    def third_arrival(cz):
        return remote(
            send3.at[cz], land3.at[cz], s3.at[cz], l3.at[cz], device(x, y, cz, c)
        )

    mine = y + c * (x - y)

    def other_axis(index):
        return x + c * (index - x), y + (1 - c) * (index - y)

    def stage1(step):
        cz = spot(step)
        for cy in range(2):
            for cx in range(2):
                core_whole(cx, cy, cz).wait_recv()
                own_whole(cx, cy, cz).wait()
        for index in range(2):
            kx, ky = other_axis(index)
            cx, cy = kx + (1 - c) * (1 - 2 * kx), ky + c * (1 - 2 * ky)
            send1[cz, index] = base(cx, cy, cz).astype(LOW)
        first_copy(cz).start()

    def stage2(step):
        cz = spot(step)
        first_copy(cz).wait_recv()
        kx, ky = other_axis(1 - mine)
        send2[cz] = (base(kx, ky, cz) + land1[cz, 1 - mine].astype(F32)).astype(LOW)
        second_copy(cz).start()

    def final(cz):
        second_copy(cz).wait_recv()
        return base(x, y, cz) + land1[cz, mine].astype(F32) + land2[cz].astype(F32)

    def stage3(step):
        cz = spot(step)
        send3[cz] = final(cz).astype(LOW)
        third_copy(cz).start()

    def turn(step):
        @pl.when(step < depth)
        def _():
            stage1(step)

        @pl.when((step >= 1) & (step <= depth))
        def _():
            stage2(step - 1)

        @pl.when((step >= 2) & (step <= depth))
        def _():
            stage3(step - 2)

    each(depth + 1, turn)
    out[...] = final(z)

    def add(step):
        cz = lax.rem(z + step, depth)
        third_arrival(cz).wait_recv()
        out[...] += land3[cz].astype(F32)

    each(depth, add, 1)
    state_own[...] = out[:, tall : tall + NSTATE]
    state_copy = remote(state_own, state_out.at[y], ts.at[1], tl.at[1], y_peer)
    state_copy.start()
    state_out[y] = state_own[...]

    def vec_sum(step):
        away = lax.rem(z + step, depth)
        remote(
            vec_send.at[3], vec_land.at[3 + away], vs.at[2 + step], vl.at[3 + away],
            device(x, y, away, c),
        ).wait_recv()

    each(depth, vec_sum, 1)
    vector_out[...] = vec_land[3]

    def vec_add(step):
        vector_out[...] += vec_land[3 + step]

    each(depth, vec_add, 1)

    for step in range(3):
        vec_copy(step).wait_send()
    each(depth, lambda step: vec_far(step).wait_send(), 1)

    def sent(cz):
        for cy in range(2):
            for cx in range(2):
                core_whole(cx, cy, cz).wait_send()
        first_copy(cz).wait_send()
        second_copy(cz).wait_send()

    each(depth, sent)
    each(depth, lambda step: third_copy(lax.rem(z + step, depth)).wait_send(), 1)
    token_copy.wait()
    state_copy.wait()
    token_keep.wait()


def reduce_all(gate, inner, exits, small, token, vector):
    count = lax.axis_size("context")
    depth = count // 2
    own_rows = gate.shape[3]
    tall = 3 * gate.shape[-1] + WIDE
    shape = jax.ShapeDtypeStruct
    vmem = pl.BlockSpec(memory_space=pltpu.VMEM)
    anywhere = pl.BlockSpec(memory_space=pl.ANY)
    buffer = lambda *lead: pltpu.VMEM(lead + (own_rows, tall), LOW)
    sem = lambda *lead: pltpu.SemaphoreType.DMA(lead)
    return pl.pallas_call(
        functools.partial(reduce_body, depth),
        out_shape=(
            shape((own_rows, tall), F32),
            shape((2, own_rows, NSTATE), F32),
            shape(vector.shape, F32),
            shape((2,) + token.shape, LOW),
        ),
        in_specs=[anywhere] * 4 + [vmem] * 2,
        out_specs=[vmem, vmem, vmem, anywhere],
        scratch_shapes=[
            buffer(2, 2, depth),
            buffer(2, 2, depth),
            buffer(depth, 2),
            buffer(depth, 2),
            buffer(depth),
            buffer(depth),
            buffer(depth),
            buffer(depth),
            pltpu.VMEM((own_rows, NSTATE), F32),
            pltpu.VMEM((4,) + vector.shape, F32),
            pltpu.VMEM((3 + depth,) + vector.shape, F32),
            sem(2, 2, depth),
            sem(2, 2, depth),
            sem(2, 2, depth),
            sem(depth),
            sem(depth),
            sem(depth),
            sem(depth),
            sem(depth),
            sem(depth),
            sem(2 + depth),
            sem(3 + depth),
            sem(2),
            sem(2),
            sem(1),
        ],
        compiler_params=params(collective_id=4, has_side_effects=True),
        name="reduce_all",
    )(gate, inner, exits, small, token, vector)


def body(
    tokens, documents, norm_gain, entry_weight, state_weight, step_weight, inner_kernel,
    state_filter, step_bias, decay_log, skip_gain, gate_gain, exit_weight, cotangent,
):
    seqs, rows, model = tokens.shape
    count = lax.axis_size("context")
    position, side = lax.axis_index("context"), lax.axis_index("tensor")
    own_rows = norm_gain.shape[0]
    wide = 3 * WIDE
    which = jnp.reshape(side, (1,)).astype(jnp.int32)
    longest = rows * count // 4
    rounds = min(count // 2 - 1, -(-(longest - 1) // (2 * rows)))

    first = (side == 0).astype(F32)
    state_half = jnp.where(side == 0, state_weight[:, :NSTATE], state_weight[:, NSTATE:])
    packed = jnp.concatenate(
        [
            entry_weight[:, 0],
            entry_weight[:, 1],
            exit_weight,
            state_half,
            step_weight * first,
            step_weight * (1.0 - first),
            norm_gain[:, None],
            jnp.zeros((own_rows, LANES - 25), F32),
        ],
        axis=1,
    ).astype(LOW)

    def placed(v):
        return jnp.concatenate([v * first, v * (1.0 - first), jnp.zeros((LANES - 24,), F32)])

    row6 = jnp.concatenate(
        [placed(step_bias), placed(decay_log), placed(skip_gain), jnp.zeros((model - 3 * LANES,))]
    )
    par_own = jnp.concatenate(
        [inner_kernel, gate_gain[None], row6[None], jnp.zeros((1, model), F32)], axis=0
    )
    docs = lax.dynamic_index_in_dim(documents, side, 0, keepdims=False).astype(F32)
    doc_col = jnp.broadcast_to(docs[:, None], (rows, LANES))
    doc_row = jnp.broadcast_to(docs[None], (8, rows))
    edge_own = lax.dynamic_index_in_dim(tokens[:, -HALO:], side, 0, keepdims=False)
    weights, par, halo, halo_docs = gather(packed, par_own, edge_own, doc_col[-HALO:])
    weights = weights.reshape(2, model, -1)
    par_heads = jnp.concatenate(
        [(par[0, 6] + par[1, 6])[: 3 * LANES].reshape(3, LANES), jnp.zeros((5, LANES), F32)], axis=0
    )
    filt = jnp.concatenate([state_filter, jnp.zeros((3, WIDE), F32)], axis=0)

    (
        hidden, cin, gate, pre, loc, fold, gain, cin_state, pre_state, bc, bct, score, mask, zst, dt,
        sp, cumt, fac, match,
    ) = front(which, tokens, halo, halo_docs, doc_col, doc_row, weights, par, par_heads, filt)
    carry = chain(fold, gain, rounds, False, 1)
    cot_t = lax.dynamic_index_in_dim(cotangent, side, 0, keepdims=False).T
    block_own, exit_part, dy, gpg, enter, gate_row, skip_row = middle(
        which, tokens, cotangent, cot_t, pre, gate, loc, carry, weights, par, par_heads, bc, bct,
        score, mask, sp, cumt, fac,
    )
    block_other = lax.ppermute(block_own, "tensor", [(0, 1), (1, 0)])
    adj = chain(enter, gain, rounds, True, 2)
    cg, edge, taps, cg_state, edge_state, taps_state, srg, head_rows = scan_back(
        pre, dy, loc, carry, adj, cin, par, par_heads, filt, cin_state, pre_state, bc, bct, score,
        mask, sp, cumt, fac, match, zst, dt,
    )
    edge, edge_state = edges(edge, edge_state)
    gate_part, inner_part, small_part, token_own, norm_row = tail(
        which, tokens, cotangent, hidden.T, gpg, cg, edge, cg_state, edge_state, srg, weights
    )
    row5 = jnp.concatenate([gate_row[0], head_rows[0], skip_row[0]])
    row6 = jnp.concatenate([norm_row[0], head_rows[1], jnp.zeros((2 * wide + WIDE - model - LANES,))])
    vector = jnp.concatenate(
        [
            jnp.concatenate([taps[: CONV + 1], taps_state[: CONV + 1]], axis=1),
            row5[None],
            row6[None],
            jnp.zeros((1, 2 * wide + WIDE), F32),
        ],
        axis=0,
    )
    cut = lambda v: v.reshape(2, 2, count, own_rows, v.shape[-1])
    mine, state_both, vector, token_both = reduce_all(
        cut(gate_part), cut(inner_part), cut(exit_part), cut(small_part), token_own, vector
    )
    block_out = jnp.where(
        (jnp.arange(2) == side)[:, None, None], block_own[None], block_other[None]
    )
    at = lax.axis_index("dp") * count + position
    half = lambda v: lax.dynamic_slice_in_dim(v, side * wide, wide, axis=-1)
    twelve = lambda v: lax.dynamic_slice_in_dim(v[..., :24], side * 12, 12, axis=-1)
    return (
        block_out,
        token_both.astype(F32),
        lax.dynamic_slice_in_dim(vector[6], at * own_rows, own_rows, axis=0),
        jnp.stack([mine[:, :wide], mine[:, wide : 2 * wide]], axis=1),
        jnp.concatenate([state_both[0], state_both[1]], axis=1),
        twelve(mine[:, 3 * wide + NSTATE :]),
        half(vector[: CONV + 1, : 2 * wide]),
        vector[: CONV + 1, 2 * wide :],
        twelve(vector[5, 2 * wide : 2 * wide + LANES]),
        twelve(vector[6, model : model + LANES]),
        twelve(vector[5, 2 * wide + LANES :]),
        half(vector[5, : 2 * wide]),
        mine[:, 2 * wide : 3 * wide],
    )


def solution(mesh):
    in_specs = (
        P("dp", "context", None),
        P("dp", "context"),
        P(("dp", "context")),
        P(("dp", "context"), None, "tensor"),
        P(("dp", "context"), None),
        P(("dp", "context"), "tensor"),
        P(None, "tensor"),
        P(),
        P("tensor"),
        P("tensor"),
        P("tensor"),
        P("tensor"),
        P(("dp", "context"), "tensor"),
        P("dp", "context", None),
    )
    out_specs = (
        P("dp", "context", None),
        P("dp", "context", None),
        P(("dp", "context")),
        P(("dp", "context"), None, "tensor"),
        P(("dp", "context"), None),
        P(("dp", "context"), "tensor"),
        P(None, "tensor"),
        P(),
        P("tensor"),
        P("tensor"),
        P("tensor"),
        P("tensor"),
        P(("dp", "context"), "tensor"),
    )
    return jax.shard_map(body, mesh=mesh, in_specs=in_specs, out_specs=out_specs, check_vma=False)
```

```python
import functools
import jax
import jax.numpy as jnp
from jax import lax
from jax.experimental import pallas as pl
from jax.experimental.pallas import tpu as pltpu
from jax.sharding import PartitionSpec as P

HEAD = 64
NSTATE = 128
CONV = 4
EPSILON = 1e-05
Q = 128
HALO = 16
EDGE = 8
LANES = 128
WIDE = 256
LOG2E = 1.4426950408889634
FAR = -1e30
LOW = jnp.bfloat16
F32 = jnp.float32
VMEM_LIMIT = 60 * 1024 * 1024


def mm(a, b):
    return lax.dot_general(a, b, (((1,), (0,)), ((), ())), preferred_element_type=F32)


def mm_nt(a, b):
    return lax.dot_general(a, b, (((1,), (1,)), ((), ())), preferred_element_type=F32)


def mm_tn(a, b):
    return lax.dot_general(a, b, (((0,), (0,)), ((), ())), preferred_element_type=F32)


def mm_exact(a, b):
    return lax.dot_general(
        a, b, (((1,), (0,)), ((), ())), precision=lax.Precision.HIGHEST, preferred_element_type=F32
    )


def split3(v):
    high = v.astype(LOW).astype(F32)
    rest = v - high
    mid = rest.astype(LOW).astype(F32)
    low = rest - mid
    return (high + pltpu.roll(mid, 32, 1) + pltpu.roll(low, 64, 1)).astype(LOW)


def iota(shape, dim):
    return lax.broadcasted_iota(jnp.int32, shape, dim)


def spreader(first_head, width, count):
    k = iota((LANES, width * count), 0)
    lane = iota((LANES, width * count), 1)
    hit = ((k & 31) == first_head + lane // width) & (k < 96)
    return hit.astype(F32).astype(LOW)


def gatherer(first_head, width, count):
    lane = iota((width * count, LANES), 0)
    k = iota((width * count, LANES), 1)
    return (k == first_head + lane // width).astype(F32).astype(LOW)


def head_sums(v, collect):
    high = v.astype(LOW)
    rest = (v - high.astype(F32)).astype(LOW)
    return mm(high, collect) + mm(rest, collect)


def sigmoid(v):
    return 1.0 / (1.0 + jnp.exp(-v))


def twice(v):
    return jnp.concatenate([v, v], axis=1)


def conv_forward(cin, taps, masks):
    rows = cin.shape[0] - HALO
    out = taps[CONV : CONV + 1] + taps[CONV - 1 : CONV] * cin[HALO:]
    for back in range(1, CONV):
        part = cin[HALO - back : HALO - back + rows]
        out = out + taps[CONV - 1 - back : CONV - back] * (part * twice(masks[back - 1]))
    return out


def conv_backward(pg, cin, taps, masks):
    rows, width = pg.shape
    sums = [None] * (CONV + 1)
    sums[CONV] = jnp.sum(pg, axis=0, keepdims=True)
    sums[CONV - 1] = jnp.sum(pg * cin[HALO:], axis=0, keepdims=True)
    pad = jnp.zeros((HALO, width), F32)
    grad = jnp.concatenate([pad, pg * taps[CONV - 1 : CONV]], axis=0)
    for back in range(1, CONV):
        masked = pg * twice(masks[back - 1])
        part = cin[HALO - back : HALO - back + rows]
        sums[CONV - 1 - back] = jnp.sum(masked * part, axis=0, keepdims=True)
        padded = jnp.concatenate([pad, masked * taps[CONV - 1 - back : CONV - back], pad], axis=0)
        grad = grad + padded[back : back + rows + HALO]
    return sums, grad


def front_body(
    which, tokens, halo, halo_docs, doc_col, doc_row, w_gate, w_inner, w_small, par, par_heads,
    state_filter, hidden_out, cin_out, gate_out, pre_out, loc_out, fold_out, gain_out,
    cin_state_out, pre_state_out, bc_out, bct_out, score_out, mask_out, zst_out, dt_out, sp_out,
    cumt_out, fac_out, match_out, hidden, sp_tail, facs
):
    step = pl.program_id(0)
    rows = tokens.shape[1]
    spans = rows // Q

    @pl.when(step == 0)
    def _():
        gain_t = jnp.transpose(w_small[0, :, LANES : 2 * LANES].astype(F32))
        gain = gain_t[24:25]
        for ref, first, count in ((halo, 0, HALO), (tokens, HALO, rows)):
            value = (ref[...] if ref is halo else ref[0]).astype(F32)
            scale = lax.rsqrt(jnp.mean(value * value, axis=1, keepdims=True) + EPSILON)
            hidden[first : first + count] = (value * scale * gain).astype(LOW)
        hidden_out[...] = jnp.transpose(hidden[HALO:])
        both = [mm(hidden[...], w_small[index]) for index in range(2)]
        cin = jnp.concatenate([both[0][:, :LANES], both[1][:, :LANES]], axis=1).astype(LOW)
        cin_state_out[...] = cin
        docs = jnp.concatenate([halo_docs[...], doc_col[...]], axis=0)
        masks = []
        for back in range(1, CONV):
            match = (docs[HALO - back : HALO - back + rows] == docs[HALO:]).astype(F32)
            match_out[back - 1] = match
            masks.append(match)
        pre = conv_forward(cin.astype(F32), state_filter[...], masks)
        pre_state_out[...] = pre
        mixed = (pre * sigmoid(pre)).astype(LOW)
        bc_out[...] = mixed
        turned = jnp.transpose(mixed.astype(F32)).astype(LOW)
        bct_out[...] = turned
        heads = par_heads[...]
        used = iota((rows, LANES), 1) < 24
        raw = both[0][HALO:, LANES:] + both[1][HALO:, LANES:]
        zst = jnp.where(used, raw, 0.0) + heads[0:1]
        zst_out[...] = zst
        dt = jnp.where(used, jnp.maximum(zst, 0.0) + jnp.log1p(jnp.exp(-jnp.abs(zst))), 0.0)
        dt_out[...] = dt
        decay = -dt * jnp.exp(heads[1:2])
        t_at, u_at = iota((Q, Q), 0), iota((Q, Q), 1)
        lower = (t_at >= u_at).astype(F32)
        fac_rows = []
        for index in range(spans):
            at = slice(index * Q, (index + 1) * Q)
            cum = mm_exact(lower, decay[at])
            final = cum[Q - 1 : Q]
            before = docs[HALO + index * Q - 1 : HALO + index * Q]
            here = doc_col[at]
            last = here[Q - 1 : Q]
            opened = (here == before).astype(F32)
            tail = (here == last).astype(F32) * jnp.exp(final - cum)
            fac_rows.append((last == before).astype(F32) * jnp.exp(final))
            cum2 = cum * LOG2E
            turned_cum = jnp.transpose(cum2)
            for group in range(6):
                cumt_out[group, 0:4, at] = turned_cum[4 * group : 4 * group + 4]
            sp_out[0, at] = split3(dt[at])
            sp_out[1, at] = split3(cum2)
            lanes_used = iota((Q, LANES), 1) < 24
            sp_out[2, at] = split3(jnp.where(lanes_used, opened * jnp.exp(cum), 0.0))
            sp_out[3, at] = split3(jnp.where(lanes_used, tail, 0.0))
            sp_tail[at] = split3(jnp.where(lanes_used, tail * dt[at], 0.0))
            same = (t_at >= u_at) & (here == doc_row[0:1, at])
            mask_out[at] = jnp.where(same, 0.0, FAR)
            score_out[at] = mm_nt(mixed[at, LANES:], mixed[at, :LANES])
        gain_total = fac_rows[0]
        for row in fac_rows[1:]:
            gain_total = gain_total * row
        rows8 = jnp.concatenate(
            fac_rows + [gain_total] + [jnp.zeros((1, LANES), F32)] * (7 - spans), axis=0
        )
        rows8 = jnp.where(iota((8, LANES), 1) < 24, rows8, 0.0)
        fac_out[...] = rows8
        facs[...] = split3(rows8)

    cin = mm(hidden[...], w_inner[0]).astype(LOW)
    cin_out[...] = cin
    gate_out[...] = mm(hidden[HALO:], w_gate[0])
    masks = [match_out[back] for back in range(CONV - 1)]
    pre = conv_forward(cin.astype(F32), par[0], masks)
    pre_out[...] = pre
    spread = spreader(4 * step, HEAD, 4)
    value = (pre * sigmoid(pre) * mm(sp_tail[...], spread)).astype(LOW)
    facx = mm(facs[...], spread)
    fold = jnp.zeros((NSTATE, WIDE), F32)
    for index in range(spans):
        at = slice(index * Q, (index + 1) * Q)
        loc = mm(bct_out[:NSTATE, at], value[at])
        loc_out[at] = loc
        fold = facx[index : index + 1] * fold + loc
    fold_out[...] = fold
    gain_out[...] = jnp.broadcast_to(facx[spans : spans + 1], (8, WIDE))


def const(shape):
    zeros = (0,) * len(shape)
    return pl.BlockSpec(shape, lambda *_: zeros)


def params(**extra):
    return pltpu.CompilerParams(vmem_limit_bytes=VMEM_LIMIT, **extra)


def front(which, tokens, halo, halo_docs, doc_col, doc_row, weights, par, par_heads, state_filter):
    rows, model = tokens.shape[1:]
    wide = 2 * 3 * WIDE
    ext = rows + HALO
    shape = jax.ShapeDtypeStruct
    outs = (
        (shape((model, rows), LOW), const((model, rows))),
        (shape((ext, wide), LOW), pl.BlockSpec((ext, WIDE), lambda s, w: (0, s))),
        (shape((rows, wide), F32), pl.BlockSpec((rows, WIDE), lambda s, w: (0, s))),
        (shape((rows, wide), F32), pl.BlockSpec((rows, WIDE), lambda s, w: (0, s))),
        (shape((rows, wide), F32), pl.BlockSpec((rows, WIDE), lambda s, w: (0, s))),
        (shape((NSTATE, wide), F32), pl.BlockSpec((NSTATE, WIDE), lambda s, w: (0, s))),
        (shape((8, wide), F32), pl.BlockSpec((8, WIDE), lambda s, w: (0, s))),
        (shape((ext, WIDE), LOW), const((ext, WIDE))),
        (shape((rows, WIDE), F32), const((rows, WIDE))),
        (shape((rows, WIDE), LOW), const((rows, WIDE))),
        (shape((WIDE, rows), LOW), const((WIDE, rows))),
        (shape((rows, Q), F32), const((rows, Q))),
        (shape((rows, Q), F32), const((rows, Q))),
        (shape((rows, LANES), F32), const((rows, LANES))),
        (shape((rows, LANES), F32), const((rows, LANES))),
        (shape((4, rows, LANES), LOW), const((4, rows, LANES))),
        (shape((6, 8, rows), F32), const((6, 8, rows))),
        (shape((8, LANES), F32), const((8, LANES))),
        (shape((CONV - 1, rows, LANES), F32), const((CONV - 1, rows, LANES))),
    )
    return pl.pallas_call(
        front_body,
        out_shape=[out[0] for out in outs],
        grid_spec=pltpu.PrefetchScalarGridSpec(
            num_scalar_prefetch=1,
            grid=(6,),
            in_specs=[
                pl.BlockSpec((1, rows, model), lambda s, w: (w[0], 0, 0)),
                const((HALO, model)),
                const((HALO, LANES)),
                const((rows, LANES)),
                const((8, rows)),
                pl.BlockSpec((1, model, WIDE), lambda s, w: (s // 3, 0, s % 3)),
                pl.BlockSpec((1, model, WIDE), lambda s, w: (s // 3, 0, 3 + s % 3)),
                pl.BlockSpec((2, model, WIDE), lambda s, w: (0, 0, 6)),
                pl.BlockSpec((1, 8, WIDE), lambda s, w: (s // 3, 0, s % 3)),
                const((8, LANES)),
                const((CONV + 1, WIDE)),
            ],
            out_specs=[out[1] for out in outs],
            scratch_shapes=[
                pltpu.VMEM((ext, model), LOW),
                pltpu.VMEM((rows, LANES), LOW),
                pltpu.VMEM((8, LANES), LOW),
            ],
        ),
        compiler_params=params(),
        name="front",
    )(
        which, tokens, halo, halo_docs, doc_col, doc_row, weights, weights, weights, par, par_heads,
        state_filter,
    )


def middle_body(
    which, tokens, cot, cot_t, pre_ref, gate_ref, loc_ref, carry_ref, w_exit, par, par_heads, bc,
    bct, score, mask, sp, cumt, fac, block_out, exit_out, dy_out, gpg_out, enter_out, row_out,
    skip_out, outputs, gates, unit_grads, mixes, sums, total
):
    step = pl.program_id(0)
    rows = pre_ref.shape[0]
    spans = rows // Q
    wide = 6 * WIDE

    @pl.when(step == 0)
    def _():
        sums[...] = jnp.zeros_like(sums)
        total[...] = jnp.zeros_like(total)
        skip_out[...] = jnp.zeros_like(skip_out)

    @pl.when(step < 6)
    def _():
        group = step
        spread = spreader(4 * group, HEAD, 4)
        pre = pre_ref[...]
        mix = pre * sigmoid(pre)
        mixes[group] = mix
        value = mix * mm(sp[0], spread)
        growth = mm(sp[2], spread)
        facx = mm(split3(fac[...]), spread)
        cums = mm(sp[1], spreader(4 * group, LANES, 4))
        skipx = mm(split3(par_heads[...]), spread)[2:3]
        state = carry_ref[...].astype(F32)
        half = iota((Q, LANES), 1) < HEAD
        for index in range(spans):
            at = slice(index * Q, (index + 1) * Q)
            carried = mm(bc[at, LANES:], state.astype(LOW)) * growth[at]
            parts = []
            for pair in range(2):
                lanes = slice(pair * LANES, (pair + 1) * LANES)
                local = None
                for side in range(2):
                    head = 2 * pair + side
                    across = cumt[group, head : head + 1, at]
                    spread_at = cums[at, head * LANES : (head + 1) * LANES] - across + mask[at]
                    weight = (jnp.exp2(spread_at) * score[at]).astype(LOW)
                    keep = half if side == 0 else jnp.logical_not(half)
                    seen = jnp.where(keep, value[at, lanes], 0.0).astype(LOW)
                    part = mm(weight, seen)
                    local = part if local is None else local + part
                parts.append(local)
            out = jnp.concatenate(parts, axis=1) + carried + skipx * mix[at]
            outputs[group, at] = out
            state = facx[index : index + 1] * state + loc_ref[at]
        gate = gate_ref[...]
        gates[group] = gate
        gated = outputs[group] * (gate * sigmoid(gate))
        unit_grad = mm(cot[0], w_exit[0])
        unit_grads[group] = unit_grad
        square = gated * gated
        cross = unit_grad * par[0, 5:6] * gated
        sums[0] += square[:, :LANES] + square[:, LANES:]
        sums[1] += cross[:, :LANES] + cross[:, LANES:]

    @pl.when(step == 5)
    def _():
        square = jnp.sum(sums[0], axis=1, keepdims=True)
        cross = jnp.sum(sums[1], axis=1, keepdims=True)
        normal = lax.rsqrt(square / wide + EPSILON)
        sums[0] = jnp.broadcast_to(normal, (rows, LANES))
        sums[1] = jnp.broadcast_to(normal * normal * normal * cross / wide, (rows, LANES))

    @pl.when(step >= 6)
    def _():
        group = step - 6
        spread = spreader(4 * group, HEAD, 4)
        normal = twice(sums[0])
        pull = twice(sums[1])
        gain = par[0, 5:6]
        gate = gates[group]
        out = outputs[group]
        unit_grad = unit_grads[group]
        sigma = sigmoid(gate)
        act = gate * sigma
        gated = out * act
        scaled_in = gated * normal
        unit = (scaled_in * gain).astype(LOW)
        total[...] += mm_nt(unit, w_exit[0])
        exit_out[0] = mm(cot_t[...], unit).astype(LOW)
        gate_sum = jnp.sum(unit_grad * scaled_in, axis=0, keepdims=True)
        gated_grad = normal * (unit_grad * gain) - pull * gated
        dy = gated_grad * act
        dy_out[...] = dy
        gpg_out[...] = (gated_grad * out * sigma * (1.0 + gate * (1.0 - sigma))).astype(LOW)
        skip_sum = jnp.sum(dy * mixes[group], axis=0, keepdims=True)
        row_out[...] = jnp.broadcast_to(gate_sum, (8, WIDE))
        skip_out[...] += head_sums(
            jnp.broadcast_to(skip_sum, (8, WIDE)), gatherer(4 * group, HEAD, 4)
        )
        facx = mm(split3(fac[...]), spread)
        pushed = (dy * mm(sp[2], spread)).astype(LOW)
        enter = jnp.zeros((NSTATE, WIDE), F32)
        for index in reversed(range(spans)):
            at = slice(index * Q, (index + 1) * Q)
            enter = facx[index : index + 1] * enter + mm(bct[NSTATE:, at], pushed[at])
        enter_out[...] = enter

    @pl.when(step == 11)
    def _():
        block_out[...] = (tokens[0].astype(F32) + total[...]).astype(LOW)


def middle(
    which, tokens, cot, cot_t, pre, gate, loc, carry, weights, par, par_heads, bc, bct, score, mask,
    sp, cumt, fac
):
    rows, model = tokens.shape[1:]
    wide = 6 * WIDE
    shape = jax.ShapeDtypeStruct

    def early(s):
        return jnp.minimum(s, 5)

    def late(s):
        return jnp.maximum(s - 6, 0)

    def group(s):
        return s % 6

    outs = (
        (shape((rows, model), LOW), const((rows, model))),
        (
            shape((2, model, 3 * WIDE), LOW),
            pl.BlockSpec((1, model, WIDE), lambda s, w: (late(s) // 3, 0, late(s) % 3)),
        ),
        (shape((rows, wide), F32), pl.BlockSpec((rows, WIDE), lambda s, w: (0, late(s)))),
        (shape((rows, wide), LOW), pl.BlockSpec((rows, WIDE), lambda s, w: (0, late(s)))),
        (shape((NSTATE, wide), F32), pl.BlockSpec((NSTATE, WIDE), lambda s, w: (0, late(s)))),
        (shape((8, wide), F32), pl.BlockSpec((8, WIDE), lambda s, w: (0, late(s)))),
        (shape((8, LANES), F32), const((8, LANES))),
    )
    return pl.pallas_call(
        middle_body,
        out_shape=[out[0] for out in outs],
        grid_spec=pltpu.PrefetchScalarGridSpec(
            num_scalar_prefetch=1,
            grid=(12,),
            in_specs=[
                pl.BlockSpec((1, rows, model), lambda s, w: (w[0], 0, 0)),
                pl.BlockSpec((1, rows, model), lambda s, w: (w[0], 0, 0)),
                const((model, rows)),
                pl.BlockSpec((rows, WIDE), lambda s, w: (0, early(s))),
                pl.BlockSpec((rows, WIDE), lambda s, w: (0, early(s))),
                pl.BlockSpec((rows, WIDE), lambda s, w: (0, early(s))),
                pl.BlockSpec((NSTATE, WIDE), lambda s, w: (0, early(s))),
                pl.BlockSpec((1, model, WIDE), lambda s, w: (group(s) // 3, 0, group(s) % 3)),
                pl.BlockSpec((1, 8, WIDE), lambda s, w: (group(s) // 3, 0, group(s) % 3)),
                const((8, LANES)),
                const((rows, WIDE)),
                const((WIDE, rows)),
                const((rows, Q)),
                const((rows, Q)),
                const((4, rows, LANES)),
                const((6, 8, rows)),
                const((8, LANES)),
            ],
            out_specs=[out[1] for out in outs],
            scratch_shapes=[
                pltpu.VMEM((6, rows, WIDE), F32),
                pltpu.VMEM((6, rows, WIDE), F32),
                pltpu.VMEM((6, rows, WIDE), F32),
                pltpu.VMEM((6, rows, WIDE), F32),
                pltpu.VMEM((2, rows, LANES), F32),
                pltpu.VMEM((rows, model), F32),
            ],
        ),
        compiler_params=params(),
        name="middle",
    )(
        which, tokens, cot, cot_t, pre, gate, loc, carry, weights, par, par_heads, bc, bct, score,
        mask, sp, cumt, fac,
    )


def scan_back_body(
    pre_ref, dy_ref, loc_ref, carry_ref, adj_ref, cin_ref, par, par_heads, state_filter, cin_state,
    pre_state, bc, bct, score, mask, sp, cumt, fac, match, zst, dt_ref, cg_out, edge_out, tap_out,
    cg_state_out, edge_state_out, tap_state_out, srg_out, small_out, d_bc, d_score, d_cum, heads
):
    group = pl.program_id(0)
    rows = pre_ref.shape[0]
    spans = rows // Q

    @pl.when(group == 0)
    def _():
        d_bc[...] = jnp.zeros_like(d_bc)
        d_score[...] = jnp.zeros_like(d_score)
        d_cum[...] = jnp.zeros_like(d_cum)
        heads[...] = jnp.zeros_like(heads)

    spread = spreader(4 * group, HEAD, 4)
    collect = gatherer(4 * group, HEAD, 4)
    pre = pre_ref[...]
    sigma = sigmoid(pre)
    mix = pre * sigma
    dtx = mm(sp[0], spread)
    growth = mm(sp[2], spread)
    tails = mm(sp[3], spread)
    facx = mm(split3(fac[...]), spread)
    cums = mm(sp[1], spreader(4 * group, LANES, 4))
    skipx = mm(split3(par_heads[...]), spread)[2:3]
    states = [carry_ref[...].astype(F32)]
    for index in range(spans - 1):
        at = slice(index * Q, (index + 1) * Q)
        states.append(facx[index : index + 1] * states[-1] + loc_ref[at])
    adjoint = adj_ref[...].astype(F32)
    half = iota((Q, LANES), 1) < HEAD
    ones = jnp.ones((8, Q), F32).astype(LOW)
    masks = [match[back] for back in range(CONV - 1)]
    pgs = [None] * spans
    for index in reversed(range(spans)):
        at = slice(index * Q, (index + 1) * Q)
        dy = dy_ref[at]
        value = mix[at] * dtx[at]
        state_low, adj_low = states[index].astype(LOW), adjoint.astype(LOW)
        pushed = dy * growth[at]
        pushed_low = pushed.astype(LOW)
        reached = mm(bc[at, :LANES], adj_low) * tails[at]
        carried = mm(bc[at, LANES:], state_low)
        d_bc[at, :LANES] += mm_nt((value * tails[at]).astype(LOW), adj_low)
        d_bc[at, LANES:] += mm_nt(pushed_low, state_low)
        heads[0, at] += head_sums(value * reached, collect)
        heads[1, at] += head_sums(pushed * carried, collect)
        fac_part = jnp.sum(adjoint * states[index], axis=0, keepdims=True)
        heads[3, index * 8 : index * 8 + 8] += head_sums(
            jnp.broadcast_to(fac_part, (8, WIDE)), collect
        )
        adjoint = facx[index : index + 1] * adjoint + mm(bct[NSTATE:, at], pushed_low)
        parts = []
        sum_score = None
        for pair in range(2):
            lanes = slice(pair * LANES, (pair + 1) * LANES)
            value_low = value[:, lanes].astype(LOW)
            local = None
            for side in range(2):
                head = 2 * pair + side
                across = cumt[group, head : head + 1, at]
                spread_at = cums[at, head * LANES : (head + 1) * LANES] - across + mask[at]
                decay = jnp.exp2(spread_at)
                keep = half if side == 0 else jnp.logical_not(half)
                dy_low = jnp.where(keep, dy[:, lanes], 0.0).astype(LOW)
                inner = decay * mm_nt(dy_low, value_low)
                sum_score = inner if sum_score is None else sum_score + inner
                moved = (inner * score[at]).astype(LOW)
                turn = mm_nt(ones, moved) - mm(ones, moved)
                d_cum[group, head : head + 1, at] = turn[0:1]
                part = mm_tn((decay * score[at]).astype(LOW), dy_low)
                local = part if local is None else local + part
            parts.append(local)
        d_score[at] += sum_score
        d_value = jnp.concatenate(parts, axis=1) + reached
        heads[2, at] += head_sums(mix[at] * d_value, collect)
        d_mix = dtx[at] * d_value + skipx * dy
        s = sigma[at]
        pgs[index] = d_mix * s * (1.0 + pre[at] * (1.0 - s))
    pg = jnp.concatenate(pgs, axis=0)
    sums, grad = conv_backward(pg, cin_ref[...].astype(F32), par[0], masks)
    tap_out[...] = jnp.concatenate(sums + [jnp.zeros((3, WIDE), F32)], axis=0)
    cg_out[...] = grad[HALO:]
    edge_out[...] = grad[HALO - EDGE : HALO]

    @pl.when(group == 5)
    def _():
        t_at, u_at = iota((Q, Q), 0), iota((Q, Q), 1)
        onward = (t_at <= u_at).astype(F32)
        earlier = (t_at > u_at).astype(F32)
        rate = jnp.exp(par_heads[1:2])
        bias_sum = jnp.zeros((1, LANES), F32)
        decay_sum = jnp.zeros((1, LANES), F32)
        used = iota((Q, LANES), 1) < 24
        for index in range(spans):
            at = slice(index * Q, (index + 1) * Q)
            pieces = [d_cum[piece, 0:4, at] for piece in range(6)]
            pieces.append(jnp.zeros((LANES - 24, Q), F32))
            cum_col = jnp.transpose(jnp.concatenate(pieces, axis=0))
            fac_row = fac[index : index + 1] * heads[3, index * 8 : index * 8 + 1]
            d_decay = (
                mm_exact(onward, cum_col + heads[1, at]) + mm_exact(earlier, heads[0, at]) + fac_row
            )
            dt = dt_ref[at]
            raw = (heads[2, at] - d_decay * rate) * sigmoid(zst[at])
            raw = jnp.where(used, raw, 0.0)
            srg_out[at] = raw.astype(LOW)
            bias_sum += jnp.sum(raw, axis=0, keepdims=True)
            decay_sum -= jnp.sum(
                jnp.where(used, d_decay * dt * rate, 0.0), axis=0, keepdims=True
            )
            score_low = d_score[at].astype(LOW)
            d_bc[at, :LANES] += mm_tn(score_low, bc[at, LANES:])
            d_bc[at, LANES:] += mm(score_low, bc[at, :LANES])
        small_out[...] = jnp.concatenate(
            [bias_sum, decay_sum, jnp.zeros((6, LANES), F32)], axis=0
        )
        pre = pre_state[...]
        s = sigmoid(pre)
        pg = d_bc[...] * s * (1.0 + pre * (1.0 - s))
        sums, grad = conv_backward(pg, cin_state[...].astype(F32), state_filter[...], masks)
        tap_state_out[...] = jnp.concatenate(sums + [jnp.zeros((3, WIDE), F32)], axis=0)
        cg_state_out[...] = grad[HALO:]
        edge_state_out[...] = grad[HALO - EDGE : HALO]


def scan_back(
    pre, dy, loc, carry, adj, cin, par, par_heads, state_filter, cin_state, pre_state, bc, bct,
    score, mask, sp, cumt, fac, match, zst, dt
):
    rows, wide = pre.shape
    ext = rows + HALO
    shape = jax.ShapeDtypeStruct
    column = lambda count: pl.BlockSpec((count, WIDE), lambda s: (0, s))
    outs = (
        (shape((rows, wide), F32), column(rows)),
        (shape((EDGE, wide), F32), column(EDGE)),
        (shape((8, wide), F32), column(8)),
        (shape((rows, WIDE), F32), const((rows, WIDE))),
        (shape((EDGE, WIDE), F32), const((EDGE, WIDE))),
        (shape((8, WIDE), F32), const((8, WIDE))),
        (shape((rows, LANES), LOW), const((rows, LANES))),
        (shape((8, LANES), F32), const((8, LANES))),
    )
    return pl.pallas_call(
        scan_back_body,
        out_shape=[out[0] for out in outs],
        grid=(6,),
        in_specs=[
            column(rows),
            column(rows),
            column(rows),
            column(NSTATE),
            column(NSTATE),
            column(ext),
            pl.BlockSpec((1, 8, WIDE), lambda s: (s // 3, 0, s % 3)),
            const((8, LANES)),
            const((CONV + 1, WIDE)),
            const((ext, WIDE)),
            const((rows, WIDE)),
            const((rows, WIDE)),
            const((WIDE, rows)),
            const((rows, Q)),
            const((rows, Q)),
            const((4, rows, LANES)),
            const((6, 8, rows)),
            const((8, LANES)),
            const((CONV - 1, rows, LANES)),
            const((rows, LANES)),
            const((rows, LANES)),
        ],
        out_specs=[out[1] for out in outs],
        scratch_shapes=[
            pltpu.VMEM((rows, WIDE), F32),
            pltpu.VMEM((rows, Q), F32),
            pltpu.VMEM((6, 8, rows), F32),
            pltpu.VMEM((4, rows, LANES), F32),
        ],
        compiler_params=params(),
        name="scan_back",
    )(
        pre, dy, loc, carry, adj, cin, par, par_heads, state_filter, cin_state, pre_state, bc, bct,
        score, mask, sp, cumt, fac, match, zst, dt,
    )


def tail_body(
    which, tokens, cot, hidden_t, gpg, cg, edge, cg_state, edge_state, srg, w_gate, w_inner, w_small,
    gate_out, inner_out, small_out, token_out, norm_out, total
):
    step = pl.program_id(0)
    rows = gpg.shape[0]

    def joined(grad, arrived):
        return jnp.concatenate(
            [grad[: rows - EDGE], grad[rows - EDGE :] + arrived[...]], axis=0
        ).astype(LOW)

    @pl.when(step == 0)
    def _():
        state = joined(cg_state, edge_state)
        steps = srg[...]
        turned = hidden_t[...]
        state_part = mm(turned, state).astype(LOW)
        step_part = mm(turned, steps).astype(LOW)
        for part in range(2):
            small_out[part, :, :LANES] = state_part[:, part * LANES : (part + 1) * LANES]
            small_out[part, :, LANES:] = step_part
        acc = mm_nt(state[:, :LANES], w_small[0, :, :LANES])
        acc += mm_nt(state[:, LANES:], w_small[1, :, :LANES])
        acc += mm_nt(steps, w_small[0, :, LANES:])
        acc += mm_nt(steps, w_small[1, :, LANES:])
        total[...] = acc

    grad = joined(cg, edge)
    gate_grad = gpg[...]
    turned = hidden_t[...]
    gate_out[0] = mm(turned, gate_grad).astype(LOW)
    inner_out[0] = mm(turned, grad).astype(LOW)
    total[...] += mm_nt(gate_grad, w_gate[0]) + mm_nt(grad, w_inner[0])

    @pl.when(step == 5)
    def _():
        value = tokens[0].astype(F32)
        scale = lax.rsqrt(jnp.mean(value * value, axis=1, keepdims=True) + EPSILON)
        hidden_grad = total[...]
        norm_sum = jnp.sum(hidden_grad * (value * scale), axis=0, keepdims=True)
        norm_out[...] = jnp.broadcast_to(norm_sum, norm_out.shape)
        gain = jnp.transpose(w_small[0, :, LANES : 2 * LANES].astype(F32))[24:25]
        normed = hidden_grad * gain
        pull = jnp.sum(normed * value, axis=1, keepdims=True) / value.shape[1]
        token_out[...] = (
            cot[0].astype(F32) + scale * normed - (scale * scale * scale) * value * pull
        ).astype(LOW)


def tail(which, tokens, cot, hidden_t, gpg, cg, edge, cg_state, edge_state, srg, weights):
    rows, model = tokens.shape[1:]
    shape = jax.ShapeDtypeStruct
    column = lambda count: pl.BlockSpec((count, WIDE), lambda s, w: (0, s))
    parts = pl.BlockSpec((1, model, WIDE), lambda s, w: (s // 3, 0, s % 3))
    outs = (
        (shape((2, model, 3 * WIDE), LOW), parts),
        (shape((2, model, 3 * WIDE), LOW), parts),
        (shape((2, model, WIDE), LOW), const((2, model, WIDE))),
        (shape((rows, model), LOW), const((rows, model))),
        (shape((8, model), F32), const((8, model))),
    )
    return pl.pallas_call(
        tail_body,
        out_shape=[out[0] for out in outs],
        grid_spec=pltpu.PrefetchScalarGridSpec(
            num_scalar_prefetch=1,
            grid=(6,),
            in_specs=[
                pl.BlockSpec((1, rows, model), lambda s, w: (w[0], 0, 0)),
                pl.BlockSpec((1, rows, model), lambda s, w: (w[0], 0, 0)),
                const((model, rows)),
                column(rows),
                column(rows),
                column(EDGE),
                const((rows, WIDE)),
                const((EDGE, WIDE)),
                const((rows, LANES)),
                pl.BlockSpec((1, model, WIDE), lambda s, w: (s // 3, 0, s % 3)),
                pl.BlockSpec((1, model, WIDE), lambda s, w: (s // 3, 0, 3 + s % 3)),
                pl.BlockSpec((2, model, WIDE), lambda s, w: (0, 0, 6)),
            ],
            out_specs=[out[1] for out in outs],
            scratch_shapes=[pltpu.VMEM((rows, model), F32)],
        ),
        compiler_params=params(),
        name="tail",
    )(
        which, tokens, cot, hidden_t, gpg, cg, edge, cg_state, edge_state, srg, weights, weights,
        weights,
    )


def remote(src, dst, send_sem, recv_sem, target):
    return pltpu.make_async_remote_copy(
        src_ref=src,
        dst_ref=dst,
        send_sem=send_sem,
        recv_sem=recv_sem,
        device_id=target,
        device_id_type=pl.DeviceIdType.MESH,
    )


def each(count, run, first=0):
    def one(step, carry):
        run(step)
        return carry

    lax.fori_loop(first, count, one, 0)


class Place:
    def __init__(self, depth):
        position = lax.axis_index("context")
        self.depth = depth
        self.position = position
        self.x, self.y = lax.axis_index("dp"), lax.axis_index("tensor")
        self.z, self.c = position // 2, position % 2
        self.mate = self.at(self.x, self.y, self.z, 1 - self.c)
        self.x_peer = self.at(1 - self.x, self.y, self.z, self.c)
        self.y_peer = self.at(self.x, 1 - self.y, self.z, self.c)

    def at(self, x, y, z, c):
        return {"dp": x, "context": z * 2 + c, "tensor": y}

    def up(self):
        return self.at(self.x, self.y, self.z + 1, self.c)

    def down(self):
        return self.at(self.x, self.y, self.z - 1, self.c)

    def away(self, z):
        return self.at(self.x, self.y, z, self.c)

    def axes(self, turned):
        x, y, z, c = self.x, self.y, self.z, self.c
        x1, y1 = x + (1 - turned) * (1 - 2 * x), y + turned * (1 - 2 * y)
        x2, y2 = x + turned * (1 - 2 * x), y + (1 - turned) * (1 - 2 * y)
        return (x1, y1), (x2, y2)

    def around(self, run, first=0):
        z, depth = self.z, self.depth
        if first == 0:
            run(z)

        def step(away):
            @pl.when(z - away >= 0)
            def _():
                run(z - away)

            @pl.when(z + away < depth)
            def _():
                run(z + away)

        each(depth, step, 1)

    def greet(self, always, sometimes=(), column=False):
        barrier = pltpu.get_barrier_semaphore()
        kind = pl.DeviceIdType.MESH
        total = len(always)
        for target in always:
            pl.semaphore_signal(barrier, inc=1, device_id=target, device_id_type=kind)
        for holds, target in sometimes:

            @pl.when(holds)
            def _():
                pl.semaphore_signal(barrier, inc=1, device_id=target, device_id_type=kind)

            total = total + holds.astype(jnp.int32)
        if column:
            for_all = lambda step: pl.semaphore_signal(
                barrier,
                inc=1,
                device_id=self.away(lax.rem(self.z + step, self.depth)),
                device_id_type=kind,
            )
            each(self.depth, for_all, 1)
            total = total + (self.depth - 1)
        pl.semaphore_wait(barrier, total)


class Gathering:
    def __init__(self, place, own, full, sends, lands, local):
        self.place, self.own_ref, self.full = place, own, full
        self.sends, self.lands, self.local = sends, lands, local
        (self.x1, self.y1), (self.x2, self.y2) = place.axes(place.c)
        self.first = place.at(self.x1, self.y1, place.z, place.c)
        self.second = place.at(self.x2, self.y2, place.z, place.c)

    @staticmethod
    def scratch(depth):
        sem = pltpu.SemaphoreType.DMA
        return [sem((5, 4 * depth)), sem((8 * depth,)), sem((1,))]

    def copy(self, kind, index, x, y, z, c, target, own=False):
        chunk = self.full.at[y, x, z * 2 + c]
        mark = ((y * 2 + x) * self.place.depth + z) * 2 + c
        return remote(
            self.own_ref if own else chunk, chunk, self.sends.at[kind, index], self.lands.at[mark],
            target,
        )

    def arrive(self, x, y, z, c):
        self.copy(0, 0, x, y, z, c, self.place.mate).wait_recv()

    def kept(self):
        p = self.place
        return pltpu.make_async_copy(
            self.own_ref, self.full.at[p.y, p.x, p.z * 2 + p.c], self.local.at[0]
        )

    def own(self):
        p = self.place
        mine = (p.x, p.y, p.z, p.c)

        @pl.when(p.z + 1 < p.depth)
        def _():
            self.copy(3, p.z, *mine, p.up(), True).start()

        @pl.when(p.z > 0)
        def _():
            self.copy(4, p.z, *mine, p.down(), True).start()

        self.copy(1, p.z, *mine, self.first, True).start()
        self.copy(2, p.z, *mine, self.second, True).start()
        self.copy(0, p.z, *mine, p.mate, True).start()
        self.kept().start()

    def near(self):
        p = self.place

        def run(z):
            chunk = (p.x, p.y, z, p.c)
            self.arrive(*chunk)

            @pl.when((z < p.z) & (p.z + 1 < p.depth))
            def _():
                self.copy(3, z, *chunk, p.up()).start()

            @pl.when((z > p.z) & (p.z > 0))
            def _():
                self.copy(4, z, *chunk, p.down()).start()

            self.copy(1, z, *chunk, self.first).start()
            self.copy(2, z, *chunk, self.second).start()
            self.copy(0, z, *chunk, p.mate).start()

        p.around(run, 1)

    def across(self):
        p = self.place

        def run(z):
            chunk = (self.x1, self.y1, z, p.c)
            self.arrive(*chunk)
            self.copy(2, p.depth + z, *chunk, self.second).start()
            self.copy(0, p.depth + z, *chunk, p.mate).start()

        p.around(run)

    def far(self):
        p = self.place

        def near_row(z):
            self.arrive(self.x2, self.y2, z, p.c)
            self.copy(0, 2 * p.depth + z, self.x2, self.y2, z, p.c, p.mate).start()

        def far_row(z):
            self.arrive(1 - p.x, 1 - p.y, z, p.c)
            self.copy(0, 3 * p.depth + z, 1 - p.x, 1 - p.y, z, p.c, p.mate).start()

        p.around(near_row)
        p.around(far_row)

    def finish(self):
        p = self.place

        def from_mate(z):
            for y in range(2):
                for x in range(2):
                    self.arrive(x, y, z, 1 - p.c)

        each(p.depth, from_mate)

        def sent(kind, index, target):
            self.copy(kind, index, p.x, p.y, p.z, p.c, target).wait_send()

        each(4 * p.depth, lambda step: sent(0, step, p.mate))
        each(p.depth, lambda step: sent(1, step, p.mate))
        each(2 * p.depth, lambda step: sent(2, step, p.mate))

        def chained(z):
            @pl.when((z <= p.z) & (p.z + 1 < p.depth))
            def _():
                sent(3, z, p.mate)

            @pl.when((z >= p.z) & (p.z > 0))
            def _():
                sent(4, z, p.mate)

        each(p.depth, chained)
        self.kept().wait()


class Reducing:
    def __init__(self, place, turned, parts, total, bufs, sems):
        self.place, self.parts, self.total = place, parts, total
        self.own, self.core, self.send1, self.land1 = bufs[:4]
        self.send2, self.land2, self.send3, self.land3 = bufs[4:]
        self.own_sem, self.core_send, self.core_land = sems[:3]
        self.s1, self.l1, self.s2, self.l2, self.s3, self.l3 = sems[3:]
        self.turned = turned
        (x1, y1), (x2, y2) = place.axes(turned)
        self.first = place.at(x1, y1, place.z, place.c)
        self.second = place.at(x2, y2, place.z, place.c)
        self.mine = place.y + turned * (place.x - place.y)

    @staticmethod
    def scratch(depth, rows, tall):
        buffer = lambda *lead: pltpu.VMEM(lead + (rows, tall), LOW)
        sem = lambda *lead: pltpu.SemaphoreType.DMA(lead)
        bufs = [
            buffer(2, 2, depth), buffer(2, 2, depth), buffer(depth, 2), buffer(depth, 2),
            buffer(depth), buffer(depth), buffer(depth), buffer(depth),
        ]
        return bufs + [sem(2, 2, depth)] * 3 + [sem(depth)] * 6

    def spot(self, step):
        return lax.rem(self.place.z + 1 + step, self.place.depth)

    def whole(self, y, x, z):
        return remote(
            self.core.at[y, x, z], self.core.at[y, x, z], self.core_send.at[y, x, z],
            self.core_land.at[y, x, z], self.place.mate,
        )

    def own_whole(self, y, x, z):
        return pltpu.make_async_copy(
            self.own.at[y, x, z], self.own.at[y, x, z], self.own_sem.at[y, x, z]
        )

    def start(self, step):
        p = self.place
        z = self.spot(step)
        for y in range(2):
            for x in range(2):
                for ref, cols in self.parts:
                    remote(
                        ref.at[y, x, z * 2 + 1 - p.c], self.core.at[y, x, z, :, cols],
                        self.core_send.at[y, x, z], self.core_land.at[y, x, z], p.mate,
                    ).start()
                    pltpu.make_async_copy(
                        ref.at[y, x, z * 2 + p.c], self.own.at[y, x, z, :, cols],
                        self.own_sem.at[y, x, z],
                    ).start()

    def base(self, y, x, z):
        return self.own[y, x, z].astype(F32) + self.core[y, x, z].astype(F32)

    def copy1(self, z):
        return remote(
            self.send1.at[z], self.land1.at[z], self.s1.at[z], self.l1.at[z], self.first
        )

    def copy2(self, z):
        return remote(
            self.send2.at[z], self.land2.at[z], self.s2.at[z], self.l2.at[z], self.second
        )

    def copy3(self, z, lands_at):
        return remote(
            self.send3.at[z], self.land3.at[lands_at], self.s3.at[z], self.l3.at[lands_at],
            self.place.away(z),
        )

    def stage1(self, step):
        p, turned = self.place, self.turned
        z = self.spot(step)
        for y in range(2):
            for x in range(2):
                self.whole(y, x, z).wait_recv()
                self.own_whole(y, x, z).wait()
        for index in range(2):
            x = (1 - turned) * (1 - p.x) + turned * index
            y = turned * (1 - p.y) + (1 - turned) * index
            self.send1[z, index] = self.base(y, x, z).astype(LOW)
        self.copy1(z).start()

    def stage2(self, step):
        p, turned = self.place, self.turned
        z = self.spot(step)
        self.copy1(z).wait_recv()
        other = 1 - self.mine
        x = (1 - turned) * p.x + turned * other
        y = turned * p.y + (1 - turned) * other
        self.send2[z] = (self.base(y, x, z) + self.land1[z, other].astype(F32)).astype(LOW)
        self.copy2(z).start()

    def final(self, z):
        p = self.place
        self.copy2(z).wait_recv()
        return (
            self.base(p.y, p.x, z)
            + self.land1[z, self.mine].astype(F32)
            + self.land2[z].astype(F32)
        )

    def stage3(self, step):
        z = self.spot(step)
        self.send3[z] = self.final(z).astype(LOW)
        self.copy3(z, self.place.z).start()

    def turn(self, step):
        depth = self.place.depth

        @pl.when(step < depth)
        def _():
            self.stage1(step)

        @pl.when((step >= 1) & (step <= depth))
        def _():
            self.stage2(step - 1)

        @pl.when((step >= 2) & (step <= depth))
        def _():
            self.stage3(step - 2)

    def close(self):
        p = self.place
        self.total[...] = self.final(p.z)

        def add(step):
            z = lax.rem(p.z + step, p.depth)
            self.copy3(z, z).wait_recv()
            self.total[...] += self.land3[z].astype(F32)

        each(p.depth, add, 1)

    def finish(self):
        p = self.place

        def sent(z):
            for y in range(2):
                for x in range(2):
                    self.whole(y, x, z).wait_send()
            self.copy1(z).wait_send()
            self.copy2(z).wait_send()

        each(p.depth, sent)
        each(p.depth, lambda step: self.copy3(lax.rem(p.z + step, p.depth), p.z).wait_send(), 1)


CUTS = 4


class Chaining:
    def __init__(self, place, rounds, backward, fold, gain, out, bufs, sems):
        self.place, self.rounds = place, rounds
        self.fold, self.gain, self.out = fold, gain, out
        self.from_mate, self.from_chip, self.to_mate, self.to_chip = bufs
        self.mate_send, self.mate_land, self.chip_send, self.chip_land = sems
        first = 1 if backward else 0
        by = -1 if backward else 1
        self.order = place.depth - 1 - place.z if backward else place.z
        self.leads = place.c == first
        self.after = place.at(place.x, place.y, place.z + by, first)
        self.before = place.at(place.x, place.y, place.z - by, 1 - first)
        self.linked_before = self.leads & (self.order > 0)
        self.linked_after = jnp.logical_not(self.leads) & (self.order < place.depth - 1)
        self.width = fold.shape[1] // CUTS

    @staticmethod
    def scratch(rounds, states, wide):
        slots = lambda turns: pltpu.VMEM((turns, CUTS, states, wide // CUTS), LOW)
        marks = lambda turns: pltpu.SemaphoreType.DMA((turns, CUTS))
        return [
            slots(rounds + 1), slots(rounds), slots(rounds + 1), slots(rounds),
            marks(rounds + 1), marks(rounds + 1), marks(rounds), marks(rounds),
        ]

    def sometimes(self):
        return [(self.linked_before, self.before), (self.linked_after, self.after)]

    def mate_copy(self, turn, cut):
        return remote(
            self.to_mate.at[turn, cut], self.from_mate.at[turn, cut], self.mate_send.at[turn, cut],
            self.mate_land.at[turn, cut], self.place.mate,
        )

    def chip_copy(self, turn, cut):
        return remote(
            self.to_chip.at[turn, cut], self.from_chip.at[turn, cut], self.chip_send.at[turn, cut],
            self.chip_land.at[turn, cut], self.after,
        )

    def lanes(self, cut):
        return slice(cut * self.width, (cut + 1) * self.width)

    def joined(self, cut, arrived):
        at = self.lanes(cut)
        return (self.fold[:, at] + self.gain[0:1, at] * arrived.astype(F32)).astype(LOW)

    def open(self):
        @pl.when(self.leads)
        def _():
            for cut in range(CUTS):
                self.to_mate[0, cut] = self.fold[:, self.lanes(cut)].astype(LOW)
                self.mate_copy(0, cut).start()

        @pl.when(jnp.logical_not(self.leads))
        def _():
            self.pass_on(0)

    def pass_on(self, turn):
        for cut in range(CUTS):
            self.mate_copy(turn, cut).wait_recv()

            @pl.when(self.linked_after)
            def _():
                self.to_chip[turn, cut] = self.joined(cut, self.from_mate[turn, cut])
                self.chip_copy(turn, cut).start()

    def relay(self):
        @pl.when(self.linked_before)
        def _():
            for turn in range(self.rounds):
                for cut in range(CUTS):
                    self.chip_copy(turn, cut).wait_recv()
                    self.to_mate[turn + 1, cut] = self.joined(cut, self.from_chip[turn, cut])
                    self.mate_copy(turn + 1, cut).start()
            for cut in range(CUTS):
                self.out[:, self.lanes(cut)] = self.from_chip[self.rounds - 1, cut]

        @pl.when(self.leads & (self.order == 0))
        def _():
            for turn in range(self.rounds):
                for cut in range(CUTS):
                    self.to_mate[turn + 1, cut] = self.fold[:, self.lanes(cut)].astype(LOW)
                    self.mate_copy(turn + 1, cut).start()
            self.out[...] = jnp.zeros_like(self.out)

    def close(self):
        @pl.when(self.leads)
        def _():
            for turn in range(self.rounds + 1):
                for cut in range(CUTS):
                    self.mate_copy(turn, cut).wait_send()

        @pl.when(jnp.logical_not(self.leads))
        def _():
            for turn in range(1, self.rounds):
                self.pass_on(turn)
            for cut in range(CUTS):
                self.mate_copy(self.rounds, cut).wait_recv()
                self.out[:, self.lanes(cut)] = self.from_mate[self.rounds, cut]

        @pl.when(self.linked_after)
        def _():
            for turn in range(self.rounds):
                for cut in range(CUTS):
                    self.chip_copy(turn, cut).wait_send()


VMEM_SPEC = pl.BlockSpec(memory_space=pltpu.VMEM)
ANY_SPEC = pl.BlockSpec(memory_space=pl.ANY)


def pack_body(
    side_ref, entry, exits, state, steps, gain, inner_kernel, gate_gain, bias, decay, skip, docs,
    tail_tokens, packed, packed_exit, par, doc_col, doc_row, edge
):
    side = side_ref[0]
    rows = entry.shape[0]
    wide = entry.shape[2]

    def placed(value):
        filled = jnp.concatenate(
            [value, jnp.zeros((value.shape[0], LANES - value.shape[1]), F32)], axis=1
        )
        return jnp.where(side == 0, filled, pltpu.roll(filled, value.shape[1], 1))

    packed[:, :wide] = entry[:, 0].astype(LOW)
    packed[:, wide : 2 * wide] = entry[:, 1].astype(LOW)
    half = jnp.where(side == 0, state[:, :NSTATE], state[:, NSTATE:])
    packed[:, 2 * wide : 2 * wide + NSTATE] = half.astype(LOW)
    gain_row = jnp.concatenate([gain[...], jnp.zeros((1, LANES - rows), F32)], axis=1)
    gain_col = jnp.transpose(jnp.broadcast_to(gain_row, (LANES, LANES)))[:rows]
    lane = iota((rows, LANES), 1)
    small = jnp.where(lane == 24, gain_col, placed(steps[...]))
    packed[:, 2 * wide + NSTATE :] = small.astype(LOW)
    packed_exit[...] = exits[...].astype(LOW)
    par[0 : CONV + 1] = inner_kernel[...]
    par[CONV + 1 : CONV + 2] = gate_gain[...]
    par[CONV + 2 : CONV + 4] = jnp.zeros((2, wide), F32)
    for index, ref in enumerate((bias, decay, skip)):
        par[CONV + 2 : CONV + 3, index * LANES : (index + 1) * LANES] = placed(ref[...])
    own = jnp.where(side == 0, docs[0:1], docs[1:2]).astype(F32)
    doc_row[...] = jnp.broadcast_to(own, doc_row.shape)
    doc_col[...] = jnp.transpose(jnp.broadcast_to(own, (LANES, own.shape[1])))
    edge[...] = tail_tokens[0]


def pack(
    which, entry, exits, state, steps, gain, inner_kernel, gate_gain, bias, decay, skip, docs, tokens
):
    own_rows, _, wide = entry.shape
    rows, model = tokens.shape[1:]
    shape = jax.ShapeDtypeStruct
    arrays = (
        entry, exits, state, steps, gain[None], inner_kernel, gate_gain[None], bias[None],
        decay[None], skip[None], docs,
    )
    outs = (
        shape((own_rows, 2 * wide + WIDE), LOW),
        shape((own_rows, wide), LOW),
        shape((8, wide), F32),
        shape((rows, LANES), F32),
        shape((8, rows), F32),
        shape((HALO, model), LOW),
    )
    return pl.pallas_call(
        pack_body,
        out_shape=outs,
        grid_spec=pltpu.PrefetchScalarGridSpec(
            num_scalar_prefetch=1,
            grid=(1,),
            in_specs=[const(array.shape) for array in arrays]
            + [pl.BlockSpec((1, HALO, model), lambda s, w: (w[0], rows // HALO - 1, 0))],
            out_specs=[const(out.shape) for out in outs],
        ),
        compiler_params=params(),
        name="pack",
    )(which, *arrays, tokens)


def gather_body(
    depth, packed, par_own, edge_own, docs_own, cot, weights, par, heads, edge, docs, cot_t, docs_in,
    cot_in, side_send, side_land, local, *scratch
):
    place = Place(depth)
    count = 2 * depth
    onward = {"context": lax.rem(place.position + 1, count)}
    behind = {"context": lax.rem(place.position + count - 1, count)}
    x, y, z, c = place.x, place.y, place.z, place.c
    place.greet(
        [place.mate, place.x_peer, place.y_peer, onward, behind],
        [(z + 1 < depth, place.up()), (z > 0, place.down())],
    )
    gathering = Gathering(place, packed, weights, *scratch)
    sides = [
        remote(edge_own, edge, side_send.at[0], side_land.at[0], onward),
        remote(docs_own, docs_in, side_send.at[1], side_land.at[1], onward),
        remote(par_own, par.at[y], side_send.at[2], side_land.at[2], place.y_peer),
    ]
    for copy in sides:
        copy.start()
    gathering.own()
    cot_copy = pltpu.make_async_copy(cot.at[y], cot_in, local.at[1])
    cot_copy.start()
    par_keep = pltpu.make_async_copy(par_own, par.at[y], local.at[0])
    par_keep.start()
    cot_copy.wait()
    cot_t[...] = jnp.transpose(cot_in[...])
    gathering.near()
    gathering.across()
    for copy in sides:
        copy.wait()
    docs[...] = jnp.where(place.position == 0, -1.0, docs_in[...])
    par_keep.wait()
    both = par[0, CONV + 2 : CONV + 3] + par[1, CONV + 2 : CONV + 3]
    heads[...] = jnp.zeros_like(heads)
    for index in range(3):
        heads[index : index + 1] = both[:, index * LANES : (index + 1) * LANES]
    gathering.far()
    gathering.finish()


def gather(packed, par_own, edge_own, docs_own, cot):
    count = lax.axis_size("context")
    depth = count // 2
    rows, model = cot.shape[1:]
    shape = jax.ShapeDtypeStruct
    return pl.pallas_call(
        functools.partial(gather_body, depth),
        out_shape=(
            shape((2, 2, count) + packed.shape, LOW),
            shape((2,) + par_own.shape, F32),
            shape((8, LANES), F32),
            shape(edge_own.shape, LOW),
            shape(docs_own.shape, F32),
            shape((model, rows), LOW),
        ),
        in_specs=[VMEM_SPEC] * 4 + [ANY_SPEC],
        out_specs=[ANY_SPEC] + [VMEM_SPEC] * 5,
        scratch_shapes=[
            pltpu.VMEM(docs_own.shape, F32),
            pltpu.VMEM((rows, model), LOW),
            pltpu.SemaphoreType.DMA((3,)),
            pltpu.SemaphoreType.DMA((3,)),
            pltpu.SemaphoreType.DMA((2,)),
        ]
        + Gathering.scratch(depth),
        compiler_params=params(collective_id=0, has_side_effects=True),
        name="gather",
    )(packed, par_own, edge_own, docs_own, cot)


def chain_body(depth, rounds, fold, gain, packed, carry, weights, *scratch):
    place = Place(depth)
    chaining = Chaining(place, rounds, False, fold, gain, carry, scratch[:4], scratch[4:8])
    gathering = Gathering(place, packed, weights, *scratch[8:])
    place.greet(
        [place.mate, place.x_peer, place.y_peer],
        [(place.z + 1 < depth, place.up()), (place.z > 0, place.down())] + chaining.sometimes(),
    )
    chaining.open()
    gathering.own()
    gathering.near()
    chaining.relay()
    gathering.across()
    gathering.far()
    chaining.close()
    gathering.finish()


def chain(fold, gain, packed, rounds):
    count = lax.axis_size("context")
    depth = count // 2
    states, wide = fold.shape
    shape = jax.ShapeDtypeStruct
    return pl.pallas_call(
        functools.partial(chain_body, depth, rounds),
        out_shape=(shape(fold.shape, LOW), shape((2, 2, count) + packed.shape, LOW)),
        in_specs=[VMEM_SPEC] * 3,
        out_specs=[VMEM_SPEC, ANY_SPEC],
        scratch_shapes=Chaining.scratch(rounds, states, wide) + Gathering.scratch(depth),
        compiler_params=params(collective_id=1, has_side_effects=True),
        name="chain",
    )(fold, gain, packed)


def chain_back_body(depth, rounds, fold, gain, exits, carry, total, *scratch):
    place = Place(depth)
    chaining = Chaining(place, rounds, True, fold, gain, carry, scratch[:4], scratch[4:8])
    reducing = Reducing(
        place, place.c, [(exits, slice(0, exits.shape[-1]))], total, scratch[8:16], scratch[16:]
    )
    place.greet([place.mate, place.x_peer, place.y_peer], chaining.sometimes(), True)
    chaining.open()
    each(depth, reducing.start)
    for step in range(2):
        reducing.turn(step)
    chaining.relay()
    each(depth + 1, reducing.turn, 2)
    reducing.close()
    chaining.close()
    reducing.finish()


def chain_back(fold, gain, exits, rounds):
    count = lax.axis_size("context")
    depth = count // 2
    states, wide = fold.shape
    own_rows, tall = exits.shape[3:]
    shape = jax.ShapeDtypeStruct
    return pl.pallas_call(
        functools.partial(chain_back_body, depth, rounds),
        out_shape=(shape(fold.shape, LOW), shape((own_rows, tall), F32)),
        in_specs=[VMEM_SPEC] * 2 + [ANY_SPEC],
        out_specs=[VMEM_SPEC] * 2,
        scratch_shapes=Chaining.scratch(rounds, states, wide)
        + Reducing.scratch(depth, own_rows, tall),
        compiler_params=params(collective_id=2, has_side_effects=True),
        name="chain_back",
    )(fold, gain, exits)


def edges_body(depth, own, own_state, out, out_state, send, land):
    place = Place(depth)
    position, count = place.position, 2 * depth
    before, after = {"context": position - 1}, {"context": position + 1}
    place.greet([], [(position > 0, before), (position < count - 1, after)])
    copies = [
        remote(own, out, send.at[0], land.at[0], before),
        remote(own_state, out_state, send.at[1], land.at[1], before),
    ]

    @pl.when(position > 0)
    def _():
        for copy in copies:
            copy.start()

    @pl.when(position == count - 1)
    def _():
        out[...] = jnp.zeros_like(out)
        out_state[...] = jnp.zeros_like(out_state)

    @pl.when(position < count - 1)
    def _():
        for copy in copies:
            copy.wait_recv()

    @pl.when(position > 0)
    def _():
        for copy in copies:
            copy.wait_send()


def edges(own, own_state):
    return pl.pallas_call(
        functools.partial(edges_body, lax.axis_size("context") // 2),
        out_shape=(
            jax.ShapeDtypeStruct(own.shape, F32),
            jax.ShapeDtypeStruct(own_state.shape, F32),
        ),
        in_specs=[VMEM_SPEC] * 2,
        out_specs=[VMEM_SPEC] * 2,
        scratch_shapes=[pltpu.SemaphoreType.DMA((2,)), pltpu.SemaphoreType.DMA((2,))],
        compiler_params=params(collective_id=3, has_side_effects=True),
        name="edges",
    )(own, own_state)


def reduce_body(
    depth, gate, inner, small, token, taps, taps_state, gate_row, head_rows, skip_row, norm_row,
    total, state_out, vector_out, token_out, state_own, vec_send, vec_land, vs, vl, ts, tl, ss, sl,
    keep_sem, *scratch
):
    place = Place(depth)
    x, y, z, c = place.x, place.y, place.z, place.c
    wide = gate.shape[-1]
    parts = [
        (gate, slice(0, wide)),
        (inner, slice(wide, 2 * wide)),
        (small, slice(2 * wide, 2 * wide + WIDE)),
    ]
    reducing = Reducing(place, 0, parts, total, scratch[:8], scratch[8:])

    vec_send[0] = jnp.zeros(vec_send.shape[1:], F32)
    vec_send[0, : CONV + 1, : 2 * wide] = taps[: CONV + 1]
    vec_send[0, : CONV + 1, 2 * wide :] = taps_state[: CONV + 1]
    vec_send[0, 5:6, : 2 * wide] = gate_row[0:1]
    vec_send[0, 5:6, 2 * wide : 2 * wide + LANES] = head_rows[0:1]
    vec_send[0, 5:6, 2 * wide + LANES :] = skip_row[0:1]
    model = norm_row.shape[1]
    vec_send[0, 6:7, :model] = norm_row[0:1]
    vec_send[0, 6:7, model : model + LANES] = head_rows[1:2]

    place.greet([place.mate, place.x_peer, place.y_peer], (), True)
    vec_targets = [place.mate, place.x_peer, place.y_peer]

    def vec_copy(turn):
        return remote(
            vec_send.at[turn], vec_land.at[turn], vs.at[turn], vl.at[turn], vec_targets[turn]
        )

    def vec_far(away, lands_at):
        return remote(
            vec_send.at[3], vec_land.at[3 + lands_at], vs.at[3 + away], vl.at[3 + lands_at],
            place.away(away),
        )

    share = token.shape[0] // depth

    def token_copy(step):
        at = pl.ds(pl.multiple_of(step * share, share), share)
        return remote(token.at[at], token_out.at[y, at], ts.at[step], tl.at[step], place.y_peer)

    token_keep = pltpu.make_async_copy(token, token_out.at[y], keep_sem.at[0])

    vec_copy(0).start()
    each(depth, reducing.start)
    token_keep.start()

    def step_all(step):
        reducing.turn(step)

        @pl.when(step >= 1)
        def _():
            token_copy(step - 1).start()

        for turn in range(3):

            @pl.when(step == turn)
            def _():
                vec_copy(turn).wait_recv()
                vec_send[turn + 1] = vec_send[turn] + vec_land[turn]
                if turn < 2:
                    vec_copy(turn + 1).start()
                else:
                    each(depth, lambda s: vec_far(lax.rem(z + s, depth), z).start(), 1)
                    vec_land[3 + z] = vec_send[3]

    each(depth + 1, step_all)
    reducing.close()
    state_own[...] = total[:, 2 * wide : 2 * wide + NSTATE]
    state_copy = remote(state_own, state_out.at[y], ss.at[0], sl.at[0], place.y_peer)
    state_copy.start()
    state_out[y] = state_own[...]

    def vec_arrive(step):
        away = lax.rem(z + step, depth)
        vec_far(away, away).wait_recv()

    each(depth, vec_arrive, 1)
    vector_out[...] = vec_land[3]

    def vec_add(step):
        vector_out[...] += vec_land[3 + step]

    each(depth, vec_add, 1)
    for turn in range(3):
        vec_copy(turn).wait_send()
    each(depth, lambda s: vec_far(lax.rem(z + s, depth), z).wait_send(), 1)
    reducing.finish()
    each(depth, lambda step: token_copy(step).wait())
    state_copy.wait()
    token_keep.wait()


def reduce_all(gate, inner, small, token, taps, taps_state, gate_row, head_rows, skip_row, norm_row):
    count = lax.axis_size("context")
    depth = count // 2
    own_rows, wide = gate.shape[3:]
    tall = 2 * wide + WIDE
    shape = jax.ShapeDtypeStruct
    sem = lambda *lead: pltpu.SemaphoreType.DMA(lead)
    vector = (8, tall)
    return pl.pallas_call(
        functools.partial(reduce_body, depth),
        out_shape=(
            shape((own_rows, tall), F32),
            shape((2, own_rows, NSTATE), F32),
            shape(vector, F32),
            shape((2,) + token.shape, LOW),
        ),
        in_specs=[ANY_SPEC] * 3 + [VMEM_SPEC] * 7,
        out_specs=[VMEM_SPEC] * 3 + [ANY_SPEC],
        scratch_shapes=[
            pltpu.VMEM((own_rows, NSTATE), F32),
            pltpu.VMEM((4,) + vector, F32),
            pltpu.VMEM((3 + depth,) + vector, F32),
            sem(3 + depth),
            sem(3 + depth),
            sem(depth),
            sem(depth),
            sem(1),
            sem(1),
            sem(1),
        ]
        + Reducing.scratch(depth, own_rows, tall),
        compiler_params=params(collective_id=4, has_side_effects=True),
        name="reduce_all",
    )(gate, inner, small, token, taps, taps_state, gate_row, head_rows, skip_row, norm_row)


def finish_body(
    side_ref, mine, exits, state, vector, token, block_own, block_other, block_out, token_out,
    norm_out, entry_out, state_out, step_out, kernel_out, filter_out, bias_out, decay_out, skip_out,
    gate_out, exit_out
):
    side, spot = side_ref[0], side_ref[1]
    token_out[...] = token[...].astype(F32)
    first = side == 0
    block_out[0] = jnp.where(first, block_own[...], block_other[...])
    block_out[1] = jnp.where(first, block_other[...], block_own[...])

    @pl.when(pl.program_id(0) == 0)
    def _():
        own_rows, _, wide = entry_out.shape
        model = token.shape[2]
        entry_out[:, 0] = mine[:, :wide]
        entry_out[:, 1] = mine[:, wide : 2 * wide]
        exit_out[...] = exits[...]
        state_out[:, :NSTATE] = state[0]
        state_out[:, NSTATE:] = state[1]

        def twelve(value):
            return jnp.where(first, value, pltpu.roll(value, LANES - 12, 1))[:, :12]

        step_out[...] = twelve(mine[:, 2 * wide + NSTATE :])
        left, right = vector[:, :wide], vector[:, wide : 2 * wide]
        halves = jnp.where(first, left, right)
        kernel_out[...] = halves[: CONV + 1]
        gate_out[...] = halves[5:6]
        filter_out[...] = vector[: CONV + 1, 2 * wide :]
        bias_out[...] = twelve(vector[5:6, 2 * wide : 2 * wide + LANES])
        skip_out[...] = twelve(vector[5:6, 2 * wide + LANES :])
        decay_out[...] = twelve(vector[6:7, model : model + LANES])
        turned = pltpu.roll(vector[:, :model], lax.rem(model - spot * own_rows, model), 1)
        norm_out[...] = turned[6:7, :own_rows]


def finish(side, mine, exits, state, vector, token, block_own, block_other):
    own_rows, wide = exits.shape
    _, rows, model = token.shape
    share = rows // 4
    shape = jax.ShapeDtypeStruct
    outs = (
        (shape((2, rows, model), LOW), pl.BlockSpec((2, share, model), lambda s, w: (0, s, 0))),
        (shape((2, rows, model), F32), pl.BlockSpec((2, share, model), lambda s, w: (0, s, 0))),
        (shape((1, own_rows), F32), None),
        (shape((own_rows, 2, wide), F32), None),
        (shape((own_rows, WIDE), F32), None),
        (shape((own_rows, 12), F32), None),
        (shape((CONV + 1, wide), F32), None),
        (shape((CONV + 1, WIDE), F32), None),
        (shape((1, 12), F32), None),
        (shape((1, 12), F32), None),
        (shape((1, 12), F32), None),
        (shape((1, wide), F32), None),
        (shape((own_rows, wide), F32), None),
    )
    return pl.pallas_call(
        finish_body,
        out_shape=[out[0] for out in outs],
        grid_spec=pltpu.PrefetchScalarGridSpec(
            num_scalar_prefetch=1,
            grid=(4,),
            in_specs=[
                const(mine.shape),
                const(exits.shape),
                const(state.shape),
                const(vector.shape),
                pl.BlockSpec((2, share, model), lambda s, w: (0, s, 0)),
                pl.BlockSpec((share, model), lambda s, w: (s, 0)),
                pl.BlockSpec((share, model), lambda s, w: (s, 0)),
            ],
            out_specs=[out[1] if out[1] is not None else const(out[0].shape) for out in outs],
        ),
        compiler_params=params(),
        name="finish",
    )(side, mine, exits, state, vector, token, block_own, block_other)


def body(
    tokens, documents, norm_gain, entry_weight, state_weight, step_weight, inner_kernel,
    state_filter, step_bias, decay_log, skip_gain, gate_gain, exit_weight, cotangent,
):
    seqs, rows, model = tokens.shape
    count = lax.axis_size("context")
    position, side = lax.axis_index("context"), lax.axis_index("tensor")
    own_rows = norm_gain.shape[0]
    which = jnp.stack([side, lax.axis_index("dp") * count + position]).astype(jnp.int32)
    longest = rows * count // 4
    rounds = min(count // 2 - 1, -(-(longest - 1) // (2 * rows)))

    packed, packed_exit, par_own, doc_col, doc_row, edge_own = pack(
        which, entry_weight, exit_weight, state_weight, step_weight, norm_gain, inner_kernel,
        gate_gain, step_bias, decay_log, skip_gain, documents, tokens,
    )
    weights, par, par_heads, halo, halo_docs, cot_t = gather(
        packed, par_own, edge_own, doc_col[-HALO:], cotangent
    )
    weights = weights.reshape(2, model, -1)
    (
        hidden_t, cin, gate, pre, loc, fold, gain, cin_state, pre_state, bc, bct, score, mask, zst,
        dt, sp, cumt, fac, match,
    ) = front(which, tokens, halo, halo_docs, doc_col, doc_row, weights, par, par_heads, state_filter)
    carry, exit_weights = chain(fold, gain, packed_exit, rounds)
    exit_weights = exit_weights.reshape(2, model, -1)
    block_own, exit_part, dy, gpg, enter, gate_row, skip_row = middle(
        which, tokens, cotangent, cot_t, pre, gate, loc, carry, exit_weights, par, par_heads, bc,
        bct, score, mask, sp, cumt, fac,
    )
    cut = lambda v: v.reshape(2, 2, count, own_rows, v.shape[-1])
    adj, exit_mine = chain_back(enter, gain, cut(exit_part), rounds)
    block_sent, adj = lax.optimization_barrier((block_own, adj))
    block_other = lax.ppermute(block_sent, "tensor", [(0, 1), (1, 0)])
    cg, edge, taps, cg_state, edge_state, taps_state, srg, head_rows = scan_back(
        pre, dy, loc, carry, adj, cin, par, par_heads, state_filter, cin_state, pre_state, bc, bct,
        score, mask, sp, cumt, fac, match, zst, dt,
    )
    edge, edge_state = edges(edge, edge_state)
    gate_part, inner_part, small_part, token_own, norm_row = tail(
        which, tokens, cotangent, hidden_t, gpg, cg, edge, cg_state, edge_state, srg, weights
    )
    mine, state_both, vector, token_both = reduce_all(
        cut(gate_part), cut(inner_part), cut(small_part), token_own, taps, taps_state, gate_row,
        head_rows, skip_row, norm_row,
    )
    outs = finish(which, mine, exit_mine, state_both, vector, token_both, block_own, block_other)
    flat = (2, 8, 9, 10, 11)
    return tuple(out[0] if index in flat else out for index, out in enumerate(outs))


def solution(mesh):
    in_specs = (
        P("dp", "context", None),
        P("dp", "context"),
        P(("dp", "context")),
        P(("dp", "context"), None, "tensor"),
        P(("dp", "context"), None),
        P(("dp", "context"), "tensor"),
        P(None, "tensor"),
        P(),
        P("tensor"),
        P("tensor"),
        P("tensor"),
        P("tensor"),
        P(("dp", "context"), "tensor"),
        P("dp", "context", None),
    )
    out_specs = (
        P("dp", "context", None),
        P("dp", "context", None),
        P(("dp", "context")),
        P(("dp", "context"), None, "tensor"),
        P(("dp", "context"), None),
        P(("dp", "context"), "tensor"),
        P(None, "tensor"),
        P(),
        P("tensor"),
        P("tensor"),
        P("tensor"),
        P("tensor"),
        P(("dp", "context"), "tensor"),
    )
    return jax.shard_map(body, mesh=mesh, in_specs=in_specs, out_specs=out_specs, check_vma=False)
```

```python
import functools
import jax
import jax.numpy as jnp
from jax import lax
from jax.experimental import pallas as pl
from jax.experimental.pallas import tpu as pltpu
from jax.sharding import PartitionSpec as P

HEAD = 64
NSTATE = 128
CONV = 4
EPSILON = 1e-05
Q = 128
HALO = 16
EDGE = 8
GROUPS = 6
BLOCK_CUTS = 8
LANES = 128
WIDE = 256
LOG2E = 1.4426950408889634
FAR = -1e30
LOW = jnp.bfloat16
F32 = jnp.float32
VMEM_LIMIT = 60 * 1024 * 1024


def mm(a, b):
    return lax.dot_general(a, b, (((1,), (0,)), ((), ())), preferred_element_type=F32)


def mm_nt(a, b):
    return lax.dot_general(a, b, (((1,), (1,)), ((), ())), preferred_element_type=F32)


def mm_tn(a, b):
    return lax.dot_general(a, b, (((0,), (0,)), ((), ())), preferred_element_type=F32)


def mm_exact(a, b):
    return lax.dot_general(
        a, b, (((1,), (0,)), ((), ())), precision=lax.Precision.HIGHEST, preferred_element_type=F32
    )


def split3(v):
    high = v.astype(LOW).astype(F32)
    rest = v - high
    mid = rest.astype(LOW).astype(F32)
    low = rest - mid
    return (high + pltpu.roll(mid, 32, 1) + pltpu.roll(low, 64, 1)).astype(LOW)


def iota(shape, dim):
    return lax.broadcasted_iota(jnp.int32, shape, dim)


def spreader(first_head, width, count):
    k = iota((LANES, width * count), 0)
    lane = iota((LANES, width * count), 1)
    hit = ((k & 31) == first_head + lane // width) & (k < 96)
    return hit.astype(F32).astype(LOW)


def gatherer(first_head, width, count):
    lane = iota((width * count, LANES), 0)
    k = iota((width * count, LANES), 1)
    return (k == first_head + lane // width).astype(F32).astype(LOW)


def head_sums(v, collect):
    high = v.astype(LOW)
    rest = (v - high.astype(F32)).astype(LOW)
    return mm(high, collect) + mm(rest, collect)


def sigmoid(v):
    return 1.0 / (1.0 + jnp.exp(-v))


def twice(v):
    return jnp.concatenate([v, v], axis=1)


def conv_forward(cin, taps, masks):
    rows = cin.shape[0] - HALO
    out = taps[CONV : CONV + 1] + taps[CONV - 1 : CONV] * cin[HALO:]
    for back in range(1, CONV):
        part = cin[HALO - back : HALO - back + rows]
        out = out + taps[CONV - 1 - back : CONV - back] * (part * twice(masks[back - 1]))
    return out


def conv_backward(pg, cin, taps, masks):
    rows, width = pg.shape
    sums = [None] * (CONV + 1)
    sums[CONV] = jnp.sum(pg, axis=0, keepdims=True)
    sums[CONV - 1] = jnp.sum(pg * cin[HALO:], axis=0, keepdims=True)
    pad = jnp.zeros((HALO, width), F32)
    grad = jnp.concatenate([pad, pg * taps[CONV - 1 : CONV]], axis=0)
    for back in range(1, CONV):
        masked = pg * twice(masks[back - 1])
        part = cin[HALO - back : HALO - back + rows]
        sums[CONV - 1 - back] = jnp.sum(masked * part, axis=0, keepdims=True)
        padded = jnp.concatenate([pad, masked * taps[CONV - 1 - back : CONV - back], pad], axis=0)
        grad = grad + padded[back : back + rows + HALO]
    return sums, grad


def const(shape):
    zeros = (0,) * len(shape)
    return pl.BlockSpec(shape, lambda *_: zeros)


def params(**extra):
    return pltpu.CompilerParams(vmem_limit_bytes=VMEM_LIMIT, **extra)


VMEM_SPEC = pl.BlockSpec(memory_space=pltpu.VMEM)
ANY_SPEC = pl.BlockSpec(memory_space=pl.ANY)


def side():
    return lax.axis_index("tensor")


def remote(src, dst, send_sem, recv_sem, target):
    return pltpu.make_async_remote_copy(
        src_ref=src,
        dst_ref=dst,
        send_sem=send_sem,
        recv_sem=recv_sem,
        device_id=target,
        device_id_type=pl.DeviceIdType.MESH,
    )


def each(count, run, first=0):
    def one(step, carry):
        run(step)
        return carry

    lax.fori_loop(first, count, one, 0)


class Place:
    def __init__(self, depth):
        position = lax.axis_index("context")
        self.depth = depth
        self.position = position
        self.x, self.y = lax.axis_index("dp"), lax.axis_index("tensor")
        self.z, self.c = position // 2, position % 2
        self.mate = self.at(self.x, self.y, self.z, 1 - self.c)
        self.x_peer = self.at(1 - self.x, self.y, self.z, self.c)
        self.y_peer = self.at(self.x, 1 - self.y, self.z, self.c)

    def at(self, x, y, z, c):
        return {"dp": x, "context": z * 2 + c, "tensor": y}

    def up(self):
        return self.at(self.x, self.y, self.z + 1, self.c)

    def down(self):
        return self.at(self.x, self.y, self.z - 1, self.c)

    def away(self, z):
        return self.at(self.x, self.y, z, self.c)

    def axes(self, turned):
        x, y, z, c = self.x, self.y, self.z, self.c
        x1, y1 = x + (1 - turned) * (1 - 2 * x), y + turned * (1 - 2 * y)
        x2, y2 = x + turned * (1 - 2 * x), y + (1 - turned) * (1 - 2 * y)
        return (x1, y1), (x2, y2)

    def around(self, run, first=0, last=None):
        z, depth = self.z, self.depth
        if first == 0:
            run(z)

        def step(away):
            @pl.when(z - away >= 0)
            def _():
                run(z - away)

            @pl.when(z + away < depth)
            def _():
                run(z + away)

        each(depth if last is None else last, step, max(first, 1))

    def greet(self, always, sometimes=(), column=False):
        barrier = pltpu.get_barrier_semaphore()
        kind = pl.DeviceIdType.MESH
        total = len(always)
        for target in always:
            pl.semaphore_signal(barrier, inc=1, device_id=target, device_id_type=kind)
        for holds, target in sometimes:

            @pl.when(holds)
            def _():
                pl.semaphore_signal(barrier, inc=1, device_id=target, device_id_type=kind)

            total = total + holds.astype(jnp.int32)
        if column:
            for_all = lambda step: pl.semaphore_signal(
                barrier,
                inc=1,
                device_id=self.away(lax.rem(self.z + step, self.depth)),
                device_id_type=kind,
            )
            each(self.depth, for_all, 1)
            total = total + (self.depth - 1)
        pl.semaphore_wait(barrier, total)


class Gathering:
    def __init__(self, place, own, full, sends, lands, local):
        self.place, self.own_ref, self.full = place, own, full
        self.sends, self.lands, self.local = sends, lands, local
        (self.x1, self.y1), (self.x2, self.y2) = place.axes(place.c)
        self.first = place.at(self.x1, self.y1, place.z, place.c)
        self.second = place.at(self.x2, self.y2, place.z, place.c)

    @staticmethod
    def scratch(depth):
        sem = pltpu.SemaphoreType.DMA
        return [sem((5, 4 * depth)), sem((8 * depth,)), sem((1,))]

    def copy(self, kind, index, x, y, z, c, target, own=False):
        chunk = self.full.at[y, x, z * 2 + c]
        mark = ((y * 2 + x) * self.place.depth + z) * 2 + c
        return remote(
            self.own_ref if own else chunk, chunk, self.sends.at[kind, index], self.lands.at[mark],
            target,
        )

    def arrive(self, x, y, z, c):
        self.copy(0, 0, x, y, z, c, self.place.mate).wait_recv()

    def kept(self):
        p = self.place
        return pltpu.make_async_copy(
            self.own_ref, self.full.at[p.y, p.x, p.z * 2 + p.c], self.local.at[0]
        )

    def own(self):
        p = self.place
        mine = (p.x, p.y, p.z, p.c)

        @pl.when(p.z + 1 < p.depth)
        def _():
            self.copy(3, p.z, *mine, p.up(), True).start()

        @pl.when(p.z > 0)
        def _():
            self.copy(4, p.z, *mine, p.down(), True).start()

        self.copy(1, p.z, *mine, self.first, True).start()
        self.copy(2, p.z, *mine, self.second, True).start()
        self.copy(0, p.z, *mine, p.mate, True).start()
        self.kept().start()

    def near(self, first=1, last=None):
        p = self.place

        def run(z):
            chunk = (p.x, p.y, z, p.c)
            self.arrive(*chunk)

            @pl.when((z < p.z) & (p.z + 1 < p.depth))
            def _():
                self.copy(3, z, *chunk, p.up()).start()

            @pl.when((z > p.z) & (p.z > 0))
            def _():
                self.copy(4, z, *chunk, p.down()).start()

            self.copy(1, z, *chunk, self.first).start()
            self.copy(2, z, *chunk, self.second).start()
            self.copy(0, z, *chunk, p.mate).start()

        p.around(run, first, last)

    def across(self):
        p = self.place

        def run(z):
            chunk = (self.x1, self.y1, z, p.c)
            self.arrive(*chunk)
            self.copy(2, p.depth + z, *chunk, self.second).start()
            self.copy(0, p.depth + z, *chunk, p.mate).start()

        p.around(run)

    def far(self):
        p = self.place

        def near_row(z):
            self.arrive(self.x2, self.y2, z, p.c)
            self.copy(0, 2 * p.depth + z, self.x2, self.y2, z, p.c, p.mate).start()

        def far_row(z):
            self.arrive(1 - p.x, 1 - p.y, z, p.c)
            self.copy(0, 3 * p.depth + z, 1 - p.x, 1 - p.y, z, p.c, p.mate).start()

        p.around(near_row)
        p.around(far_row)

    def finish(self):
        p = self.place

        def from_mate(z):
            for y in range(2):
                for x in range(2):
                    self.arrive(x, y, z, 1 - p.c)

        each(p.depth, from_mate)

        def sent(kind, index, target):
            self.copy(kind, index, p.x, p.y, p.z, p.c, target).wait_send()

        each(4 * p.depth, lambda step: sent(0, step, p.mate))
        each(p.depth, lambda step: sent(1, step, p.mate))
        each(2 * p.depth, lambda step: sent(2, step, p.mate))

        def chained(z):
            @pl.when((z <= p.z) & (p.z + 1 < p.depth))
            def _():
                sent(3, z, p.mate)

            @pl.when((z >= p.z) & (p.z > 0))
            def _():
                sent(4, z, p.mate)

        each(p.depth, chained)
        self.kept().wait()


class Reducing:
    def __init__(self, place, turned, parts, total, bufs, sems):
        self.place, self.parts, self.total = place, parts, total
        self.own, self.core, self.send1, self.land1 = bufs[:4]
        self.send2, self.land2, self.send3, self.land3 = bufs[4:]
        self.own_sem, self.core_send, self.core_land = sems[:3]
        self.s1, self.l1, self.s2, self.l2, self.s3, self.l3 = sems[3:]
        self.turned = turned
        (x1, y1), (x2, y2) = place.axes(turned)
        self.first = place.at(x1, y1, place.z, place.c)
        self.second = place.at(x2, y2, place.z, place.c)
        self.mine = place.y + turned * (place.x - place.y)

    @staticmethod
    def scratch(depth, rows, tall):
        buffer = lambda *lead: pltpu.VMEM(lead + (rows, tall), LOW)
        sem = lambda *lead: pltpu.SemaphoreType.DMA(lead)
        bufs = [
            buffer(2, 2, depth), buffer(2, 2, depth), buffer(depth, 2), buffer(depth, 2),
            buffer(depth), buffer(depth), buffer(depth), buffer(depth),
        ]
        return bufs + [sem(2, 2, depth)] * 3 + [sem(depth)] * 6

    def spot(self, step):
        return lax.rem(self.place.z + 1 + step, self.place.depth)

    def whole(self, y, x, z):
        return remote(
            self.core.at[y, x, z], self.core.at[y, x, z], self.core_send.at[y, x, z],
            self.core_land.at[y, x, z], self.place.mate,
        )

    def own_whole(self, y, x, z):
        return pltpu.make_async_copy(
            self.own.at[y, x, z], self.own.at[y, x, z], self.own_sem.at[y, x, z]
        )

    def start(self, step):
        p = self.place
        z = self.spot(step)
        for y in range(2):
            for x in range(2):
                for ref, cols in self.parts:
                    remote(
                        ref.at[y, x, z * 2 + 1 - p.c], self.core.at[y, x, z, :, cols],
                        self.core_send.at[y, x, z], self.core_land.at[y, x, z], p.mate,
                    ).start()
                    pltpu.make_async_copy(
                        ref.at[y, x, z * 2 + p.c], self.own.at[y, x, z, :, cols],
                        self.own_sem.at[y, x, z],
                    ).start()

    def base(self, y, x, z):
        return self.own[y, x, z].astype(F32) + self.core[y, x, z].astype(F32)

    def copy1(self, z):
        return remote(
            self.send1.at[z], self.land1.at[z], self.s1.at[z], self.l1.at[z], self.first
        )

    def copy2(self, z):
        return remote(
            self.send2.at[z], self.land2.at[z], self.s2.at[z], self.l2.at[z], self.second
        )

    def copy3(self, z, lands_at):
        return remote(
            self.send3.at[z], self.land3.at[lands_at], self.s3.at[z], self.l3.at[lands_at],
            self.place.away(z),
        )

    def stage1(self, step):
        p, turned = self.place, self.turned
        z = self.spot(step)
        for y in range(2):
            for x in range(2):
                self.whole(y, x, z).wait_recv()
                self.own_whole(y, x, z).wait()
        for index in range(2):
            x = (1 - turned) * (1 - p.x) + turned * index
            y = turned * (1 - p.y) + (1 - turned) * index
            self.send1[z, index] = self.base(y, x, z).astype(LOW)
        self.copy1(z).start()

    def stage2(self, step):
        p, turned = self.place, self.turned
        z = self.spot(step)
        self.copy1(z).wait_recv()
        other = 1 - self.mine
        x = (1 - turned) * p.x + turned * other
        y = turned * p.y + (1 - turned) * other
        self.send2[z] = (self.base(y, x, z) + self.land1[z, other].astype(F32)).astype(LOW)
        self.copy2(z).start()

    def final(self, z):
        p = self.place
        self.copy2(z).wait_recv()
        return (
            self.base(p.y, p.x, z)
            + self.land1[z, self.mine].astype(F32)
            + self.land2[z].astype(F32)
        )

    def stage3(self, step):
        z = self.spot(step)
        self.send3[z] = self.final(z).astype(LOW)
        self.copy3(z, self.place.z).start()

    def turn(self, step):
        depth = self.place.depth

        @pl.when(step < depth)
        def _():
            self.stage1(step)

        @pl.when((step >= 1) & (step <= depth))
        def _():
            self.stage2(step - 1)

        @pl.when((step >= 2) & (step <= depth))
        def _():
            self.stage3(step - 2)

    def close(self):
        p = self.place
        self.total[...] = self.final(p.z)

        def add(step):
            z = lax.rem(p.z + step, p.depth)
            self.copy3(z, z).wait_recv()
            self.total[...] += self.land3[z].astype(F32)

        each(p.depth, add, 1)

    def finish(self):
        p = self.place

        def sent(z):
            for y in range(2):
                for x in range(2):
                    self.whole(y, x, z).wait_send()
            self.copy1(z).wait_send()
            self.copy2(z).wait_send()

        each(p.depth, sent)
        each(p.depth, lambda step: self.copy3(lax.rem(p.z + step, p.depth), p.z).wait_send(), 1)


class Chaining:
    def __init__(self, place, rounds, backward, fold, gain, bufs, sems):
        self.place, self.rounds = place, rounds
        self.fold, self.gain = fold, gain
        self.from_mate, self.from_chip, self.to_mate, self.to_chip = bufs
        self.mate_send, self.mate_land, self.chip_send, self.chip_land = sems
        first = 1 if backward else 0
        by = -1 if backward else 1
        self.order = place.depth - 1 - place.z if backward else place.z
        self.leads = place.c == first
        self.after = place.at(place.x, place.y, place.z + by, first)
        self.before = place.at(place.x, place.y, place.z - by, 1 - first)
        self.linked_before = self.leads & (self.order > 0)
        self.linked_after = jnp.logical_not(self.leads) & (self.order < place.depth - 1)

    @staticmethod
    def scratch(rounds):
        slots = lambda turns: pltpu.VMEM((turns, GROUPS, NSTATE, WIDE), LOW)
        marks = lambda turns: pltpu.SemaphoreType.DMA((turns, GROUPS))
        return [
            slots(rounds + 1), slots(rounds), slots(rounds + 1), slots(rounds),
            marks(rounds + 1), marks(rounds + 1), marks(rounds), marks(rounds),
        ]

    def sometimes(self):
        return [(self.linked_before, self.before), (self.linked_after, self.after)]

    def mate_copy(self, turn, cut):
        return remote(
            self.to_mate.at[turn, cut], self.from_mate.at[turn, cut], self.mate_send.at[turn, cut],
            self.mate_land.at[turn, cut], self.place.mate,
        )

    def chip_copy(self, turn, cut):
        return remote(
            self.to_chip.at[turn, cut], self.from_chip.at[turn, cut], self.chip_send.at[turn, cut],
            self.chip_land.at[turn, cut], self.after,
        )

    def joined(self, cut, arrived):
        return (self.fold[cut] + self.gain[cut, 0:1] * arrived.astype(F32)).astype(LOW)

    def open(self, cut):
        @pl.when(self.leads)
        def _():
            self.to_mate[0, cut] = self.fold[cut].astype(LOW)
            self.mate_copy(0, cut).start()

    def pass_on(self, turn, cut):
        @pl.when(jnp.logical_not(self.leads))
        def _():
            self.mate_copy(turn, cut).wait_recv()

        @pl.when(self.linked_after)
        def _():
            self.to_chip[turn, cut] = self.joined(cut, self.from_mate[turn, cut])
            self.chip_copy(turn, cut).start()

    def relay(self, turn, cut):
        @pl.when(self.linked_before)
        def _():
            self.chip_copy(turn, cut).wait_recv()
            self.to_mate[turn + 1, cut] = self.joined(cut, self.from_chip[turn, cut])
            self.mate_copy(turn + 1, cut).start()

        @pl.when(self.leads & (self.order == 0))
        def _():
            self.to_mate[turn + 1, cut] = self.fold[cut].astype(LOW)
            self.mate_copy(turn + 1, cut).start()

    def later(self):
        for turn in range(1, self.rounds):
            for cut in range(GROUPS):
                self.pass_on(turn, cut)
            for cut in range(GROUPS):
                self.relay(turn, cut)

    def arrive(self, put):
        last = self.rounds - 1

        @pl.when(self.linked_before)
        def _():
            for cut in range(GROUPS):
                put(cut, self.from_chip[last, cut])

        @pl.when(self.leads & (self.order == 0))
        def _():
            for cut in range(GROUPS):
                put(cut, jnp.zeros((NSTATE, WIDE), LOW))

        @pl.when(jnp.logical_not(self.leads))
        def _():
            for cut in range(GROUPS):
                self.mate_copy(self.rounds, cut).wait_recv()
                put(cut, self.from_mate[self.rounds, cut])

    def finish(self):
        @pl.when(self.leads)
        def _():
            for turn in range(self.rounds + 1):
                for cut in range(GROUPS):
                    self.mate_copy(turn, cut).wait_send()

        @pl.when(self.linked_after)
        def _():
            for turn in range(self.rounds):
                for cut in range(GROUPS):
                    self.chip_copy(turn, cut).wait_send()


def front_body(
    depth, rounds, tokens, halo, halo_docs, doc_col, doc_row, w_gate, w_inner, w_small, par, par_heads,
    state_filter, packed_exit, hidden_out, cin_out, gate_out, pre_out, loc_out, carry_out,
    exit_weights, cin_state_out, pre_state_out, bc_out, bct_out, score_out, mask_out, zst_out, dt_out, sp_out,
    cumt_out, fac_out, match_out, hidden, sp_tail, facs, folds, gains, *scratch
):
    step = pl.program_id(0)
    rows = tokens.shape[1]
    spans = rows // Q
    place = Place(depth)
    chaining = Chaining(place, rounds, False, folds, gains, scratch[:4], scratch[4:8])
    gathering = Gathering(place, packed_exit, exit_weights, *scratch[8:])

    @pl.when(step == 0)
    def _():
        place.greet(
            [place.mate, place.x_peer, place.y_peer],
            [(place.z + 1 < depth, place.up()), (place.z > 0, place.down())] + chaining.sometimes(),
        )
        gathering.own()

    for away in range(1, 4):

        @pl.when(step == away)
        def _():
            gathering.near(away, away + 1 if away < 3 else None)

    @pl.when(step == 4)
    def _():
        gathering.across()

    @pl.when(step == 5)
    def _():
        gathering.far()

    for cut in range(GROUPS - 1):

        @pl.when(step == cut + 1)
        def _():
            chaining.pass_on(0, cut)

    for cut in range(GROUPS - 3):

        @pl.when(step == cut + 3)
        def _():
            chaining.relay(0, cut)

    @pl.when(step == 0)
    def _():
        gain_t = jnp.transpose(w_small[0, :, LANES : 2 * LANES].astype(F32))
        gain = gain_t[24:25]
        for ref, first, count in ((halo, 0, HALO), (tokens, HALO, rows)):
            value = (ref[...] if ref is halo else ref[0]).astype(F32)
            scale = lax.rsqrt(jnp.mean(value * value, axis=1, keepdims=True) + EPSILON)
            hidden[first : first + count] = (value * scale * gain).astype(LOW)
        hidden_out[...] = jnp.transpose(hidden[HALO:])
        both = [mm(hidden[...], w_small[index]) for index in range(2)]
        cin = jnp.concatenate([both[0][:, :LANES], both[1][:, :LANES]], axis=1).astype(LOW)
        cin_state_out[...] = cin
        docs = jnp.concatenate([halo_docs[...], doc_col[...]], axis=0)
        masks = []
        for back in range(1, CONV):
            match = (docs[HALO - back : HALO - back + rows] == docs[HALO:]).astype(F32)
            match_out[back - 1] = match
            masks.append(match)
        pre = conv_forward(cin.astype(F32), state_filter[...], masks)
        pre_state_out[...] = pre
        mixed = (pre * sigmoid(pre)).astype(LOW)
        bc_out[...] = mixed
        turned = jnp.transpose(mixed.astype(F32)).astype(LOW)
        bct_out[...] = turned
        heads = par_heads[...]
        used = iota((rows, LANES), 1) < 24
        raw = both[0][HALO:, LANES:] + both[1][HALO:, LANES:]
        zst = jnp.where(used, raw, 0.0) + heads[0:1]
        zst_out[...] = zst
        dt = jnp.where(used, jnp.maximum(zst, 0.0) + jnp.log1p(jnp.exp(-jnp.abs(zst))), 0.0)
        dt_out[...] = dt
        decay = -dt * jnp.exp(heads[1:2])
        t_at, u_at = iota((Q, Q), 0), iota((Q, Q), 1)
        lower = (t_at >= u_at).astype(F32)
        fac_rows = []
        for index in range(spans):
            at = slice(index * Q, (index + 1) * Q)
            cum = mm_exact(lower, decay[at])
            final = cum[Q - 1 : Q]
            before = docs[HALO + index * Q - 1 : HALO + index * Q]
            here = doc_col[at]
            last = here[Q - 1 : Q]
            opened = (here == before).astype(F32)
            tail = (here == last).astype(F32) * jnp.exp(final - cum)
            fac_rows.append((last == before).astype(F32) * jnp.exp(final))
            cum2 = cum * LOG2E
            turned_cum = jnp.transpose(cum2)
            for group in range(6):
                cumt_out[group, 0:4, at] = turned_cum[4 * group : 4 * group + 4]
            sp_out[0, at] = split3(dt[at])
            sp_out[1, at] = split3(cum2)
            lanes_used = iota((Q, LANES), 1) < 24
            sp_out[2, at] = split3(jnp.where(lanes_used, opened * jnp.exp(cum), 0.0))
            sp_out[3, at] = split3(jnp.where(lanes_used, tail, 0.0))
            sp_tail[at] = split3(jnp.where(lanes_used, tail * dt[at], 0.0))
            same = (t_at >= u_at) & (here == doc_row[0:1, at])
            mask_out[at] = jnp.where(same, 0.0, FAR)
            score_out[at] = mm_nt(mixed[at, LANES:], mixed[at, :LANES])
        gain_total = fac_rows[0]
        for row in fac_rows[1:]:
            gain_total = gain_total * row
        rows8 = jnp.concatenate(
            fac_rows + [gain_total] + [jnp.zeros((1, LANES), F32)] * (7 - spans), axis=0
        )
        rows8 = jnp.where(iota((8, LANES), 1) < 24, rows8, 0.0)
        fac_out[...] = rows8
        facs[...] = split3(rows8)

    cin = mm(hidden[...], w_inner[0]).astype(LOW)
    cin_out[...] = cin
    gate_out[...] = mm(hidden[HALO:], w_gate[0])
    masks = [match_out[back] for back in range(CONV - 1)]
    pre = conv_forward(cin.astype(F32), par[0], masks)
    pre_out[...] = pre
    spread = spreader(4 * step, HEAD, 4)
    value = (pre * sigmoid(pre) * mm(sp_tail[...], spread)).astype(LOW)
    facx = mm(facs[...], spread)
    fold = jnp.zeros((NSTATE, WIDE), F32)
    for index in range(spans):
        at = slice(index * Q, (index + 1) * Q)
        loc = mm(bct_out[:NSTATE, at], value[at])
        loc_out[at] = loc
        fold = facx[index : index + 1] * fold + loc
    folds[step] = fold
    gains[step] = jnp.broadcast_to(facx[spans : spans + 1], (8, WIDE))
    for cut in range(GROUPS):

        @pl.when(step == cut)
        def _():
            chaining.open(cut)

    @pl.when(step == GROUPS - 1)
    def _():
        chaining.pass_on(0, GROUPS - 1)
        for cut in range(GROUPS - 3, GROUPS):
            chaining.relay(0, cut)
        chaining.later()

        def put(cut, value):
            carry_out[:, cut * WIDE : (cut + 1) * WIDE] = value

        chaining.arrive(put)
        gathering.finish()
        chaining.finish()


def front(
    tokens, halo, halo_docs, doc_col, doc_row, weights, par, par_heads, state_filter, packed_exit,
    rounds
):
    rows, model = tokens.shape[1:]
    count = lax.axis_size("context")
    depth = count // 2
    wide = 2 * 3 * WIDE
    ext = rows + HALO
    shape = jax.ShapeDtypeStruct
    outs = (
        (shape((model, rows), LOW), const((model, rows))),
        (shape((ext, wide), LOW), pl.BlockSpec((ext, WIDE), lambda s: (0, s))),
        (shape((rows, wide), F32), pl.BlockSpec((rows, WIDE), lambda s: (0, s))),
        (shape((rows, wide), F32), pl.BlockSpec((rows, WIDE), lambda s: (0, s))),
        (shape((rows, wide), F32), pl.BlockSpec((rows, WIDE), lambda s: (0, s))),
        (shape((NSTATE, wide), LOW), const((NSTATE, wide))),
        (shape((2, 2, count) + packed_exit.shape, LOW), ANY_SPEC),
        (shape((ext, WIDE), LOW), const((ext, WIDE))),
        (shape((rows, WIDE), F32), const((rows, WIDE))),
        (shape((rows, WIDE), LOW), const((rows, WIDE))),
        (shape((WIDE, rows), LOW), const((WIDE, rows))),
        (shape((rows, Q), F32), const((rows, Q))),
        (shape((rows, Q), F32), const((rows, Q))),
        (shape((rows, LANES), F32), const((rows, LANES))),
        (shape((rows, LANES), F32), const((rows, LANES))),
        (shape((4, rows, LANES), LOW), const((4, rows, LANES))),
        (shape((6, 8, rows), F32), const((6, 8, rows))),
        (shape((8, LANES), F32), const((8, LANES))),
        (shape((CONV - 1, rows, LANES), F32), const((CONV - 1, rows, LANES))),
    )
    return pl.pallas_call(
        functools.partial(front_body, depth, rounds),
        out_shape=[out[0] for out in outs],
        grid=(GROUPS,),
        in_specs=[
            pl.BlockSpec((1, rows, model), lambda s: (side(), 0, 0)),
            const((HALO, model)),
            const((HALO, LANES)),
            const((rows, LANES)),
            const((8, rows)),
            pl.BlockSpec((1, model, WIDE), lambda s: (s // 3, 0, s % 3)),
            pl.BlockSpec((1, model, WIDE), lambda s: (s // 3, 0, 3 + s % 3)),
            pl.BlockSpec((2, model, WIDE), lambda s: (0, 0, 6)),
            pl.BlockSpec((1, 8, WIDE), lambda s: (s // 3, 0, s % 3)),
            const((8, LANES)),
            const((CONV + 1, WIDE)),
            VMEM_SPEC,
        ],
        out_specs=[out[1] for out in outs],
        scratch_shapes=[
            pltpu.VMEM((ext, model), LOW),
            pltpu.VMEM((rows, LANES), LOW),
            pltpu.VMEM((8, LANES), LOW),
            pltpu.VMEM((GROUPS, NSTATE, WIDE), F32),
            pltpu.VMEM((GROUPS, 8, WIDE), F32),
        ]
        + Chaining.scratch(rounds)
        + Gathering.scratch(depth),
        compiler_params=params(collective_id=1, has_side_effects=True),
        name="front",
    )(
        tokens, halo, halo_docs, doc_col, doc_row, weights, weights, weights, par, par_heads,
        state_filter, packed_exit,
    )


def middle_body(
    tokens, cot, cot_t, hidden_t, pre_ref, gate_ref, loc_ref, carry_ref, w_exit, par, par_heads, bc,
    bct, score, mask, sp, cumt, fac, block_out, exit_out, gate_part_out, dy_out, gpg_out, enter_out, row_out,
    skip_out, outputs, gates, unit_grads, mixes, sums, total
):
    step = pl.program_id(0)
    rows = pre_ref.shape[0]
    spans = rows // Q
    wide = 6 * WIDE

    @pl.when(step == 0)
    def _():
        sums[...] = jnp.zeros_like(sums)
        total[...] = jnp.zeros_like(total)
        skip_out[...] = jnp.zeros_like(skip_out)

    @pl.when(step < 6)
    def _():
        group = step
        spread = spreader(4 * group, HEAD, 4)
        pre = pre_ref[...]
        mix = pre * sigmoid(pre)
        mixes[group] = mix
        value = mix * mm(sp[0], spread)
        growth = mm(sp[2], spread)
        facx = mm(split3(fac[...]), spread)
        cums = mm(sp[1], spreader(4 * group, LANES, 4))
        skipx = mm(split3(par_heads[...]), spread)[2:3]
        state = carry_ref[...].astype(F32)
        half = iota((Q, LANES), 1) < HEAD
        for index in range(spans):
            at = slice(index * Q, (index + 1) * Q)
            carried = mm(bc[at, LANES:], state.astype(LOW)) * growth[at]
            parts = []
            for pair in range(2):
                lanes = slice(pair * LANES, (pair + 1) * LANES)
                local = None
                for side in range(2):
                    head = 2 * pair + side
                    across = cumt[group, head : head + 1, at]
                    spread_at = cums[at, head * LANES : (head + 1) * LANES] - across + mask[at]
                    weight = (jnp.exp2(spread_at) * score[at]).astype(LOW)
                    keep = half if side == 0 else jnp.logical_not(half)
                    seen = jnp.where(keep, value[at, lanes], 0.0).astype(LOW)
                    part = mm(weight, seen)
                    local = part if local is None else local + part
                parts.append(local)
            out = jnp.concatenate(parts, axis=1) + carried + skipx * mix[at]
            outputs[group, at] = out
            state = facx[index : index + 1] * state + loc_ref[at]
        gate = gate_ref[...]
        gates[group] = gate
        gated = outputs[group] * (gate * sigmoid(gate))
        unit_grad = mm(cot[0], w_exit[0])
        unit_grads[group] = unit_grad
        square = gated * gated
        cross = unit_grad * par[0, 5:6] * gated
        sums[0] += square[:, :LANES] + square[:, LANES:]
        sums[1] += cross[:, :LANES] + cross[:, LANES:]

    @pl.when(step == 5)
    def _():
        square = jnp.sum(sums[0], axis=1, keepdims=True)
        cross = jnp.sum(sums[1], axis=1, keepdims=True)
        normal = lax.rsqrt(square / wide + EPSILON)
        sums[0] = jnp.broadcast_to(normal, (rows, LANES))
        sums[1] = jnp.broadcast_to(normal * normal * normal * cross / wide, (rows, LANES))

    @pl.when(step >= 6)
    def _():
        group = step - 6
        spread = spreader(4 * group, HEAD, 4)
        normal = twice(sums[0])
        pull = twice(sums[1])
        gain = par[0, 5:6]
        gate = gates[group]
        out = outputs[group]
        unit_grad = unit_grads[group]
        sigma = sigmoid(gate)
        act = gate * sigma
        gated = out * act
        scaled_in = gated * normal
        unit = (scaled_in * gain).astype(LOW)
        total[...] += mm_nt(unit, w_exit[0])
        exit_out[0] = mm(cot_t[...], unit).astype(LOW)
        gate_sum = jnp.sum(unit_grad * scaled_in, axis=0, keepdims=True)
        gated_grad = normal * (unit_grad * gain) - pull * gated
        dy = gated_grad * act
        dy_out[...] = dy
        gate_grad = (gated_grad * out * sigma * (1.0 + gate * (1.0 - sigma))).astype(LOW)
        gpg_out[...] = gate_grad
        gate_part_out[0] = mm(hidden_t[...], gate_grad).astype(LOW)
        skip_sum = jnp.sum(dy * mixes[group], axis=0, keepdims=True)
        row_out[...] = jnp.broadcast_to(gate_sum, (8, WIDE))
        skip_out[...] += head_sums(
            jnp.broadcast_to(skip_sum, (8, WIDE)), gatherer(4 * group, HEAD, 4)
        )
        facx = mm(split3(fac[...]), spread)
        pushed = (dy * mm(sp[2], spread)).astype(LOW)
        enter = jnp.zeros((NSTATE, WIDE), F32)
        for index in reversed(range(spans)):
            at = slice(index * Q, (index + 1) * Q)
            enter = facx[index : index + 1] * enter + mm(bct[NSTATE:, at], pushed[at])
        enter_out[...] = enter

    @pl.when(step == 11)
    def _():
        block_out[...] = (tokens[0].astype(F32) + total[...]).astype(LOW)


def middle(
    tokens, cot, cot_t, hidden_t, pre, gate, loc, carry, weights, par, par_heads, bc, bct, score, mask,
    sp, cumt, fac
):
    rows, model = tokens.shape[1:]
    wide = 6 * WIDE
    shape = jax.ShapeDtypeStruct

    def early(s):
        return jnp.minimum(s, 5)

    def late(s):
        return jnp.maximum(s - 6, 0)

    def group(s):
        return s % 6

    outs = (
        (shape((rows, model), LOW), const((rows, model))),
        (
            shape((2, model, 3 * WIDE), LOW),
            pl.BlockSpec((1, model, WIDE), lambda s: (late(s) // 3, 0, late(s) % 3)),
        ),
        (
            shape((2, model, 3 * WIDE), LOW),
            pl.BlockSpec((1, model, WIDE), lambda s: (late(s) // 3, 0, late(s) % 3)),
        ),
        (shape((rows, wide), F32), pl.BlockSpec((rows, WIDE), lambda s: (0, late(s)))),
        (shape((rows, wide), LOW), pl.BlockSpec((rows, WIDE), lambda s: (0, late(s)))),
        (shape((NSTATE, wide), F32), pl.BlockSpec((NSTATE, WIDE), lambda s: (0, late(s)))),
        (shape((8, wide), F32), pl.BlockSpec((8, WIDE), lambda s: (0, late(s)))),
        (shape((8, LANES), F32), const((8, LANES))),
    )
    return pl.pallas_call(
        middle_body,
        out_shape=[out[0] for out in outs],
        grid=(12,),
        in_specs=[
                pl.BlockSpec((1, rows, model), lambda s: (side(), 0, 0)),
                pl.BlockSpec((1, rows, model), lambda s: (side(), 0, 0)),
                const((model, rows)),
                const((model, rows)),
                pl.BlockSpec((rows, WIDE), lambda s: (0, early(s))),
                pl.BlockSpec((rows, WIDE), lambda s: (0, early(s))),
                pl.BlockSpec((rows, WIDE), lambda s: (0, early(s))),
                pl.BlockSpec((NSTATE, WIDE), lambda s: (0, early(s))),
                pl.BlockSpec((1, model, WIDE), lambda s: (group(s) // 3, 0, group(s) % 3)),
                pl.BlockSpec((1, 8, WIDE), lambda s: (group(s) // 3, 0, group(s) % 3)),
                const((8, LANES)),
                const((rows, WIDE)),
                const((WIDE, rows)),
                const((rows, Q)),
                const((rows, Q)),
                const((4, rows, LANES)),
                const((6, 8, rows)),
                const((8, LANES)),
        ],
        out_specs=[out[1] for out in outs],
        scratch_shapes=[
                pltpu.VMEM((6, rows, WIDE), F32),
                pltpu.VMEM((6, rows, WIDE), F32),
                pltpu.VMEM((6, rows, WIDE), F32),
                pltpu.VMEM((6, rows, WIDE), F32),
                pltpu.VMEM((2, rows, LANES), F32),
                pltpu.VMEM((rows, model), F32),
        ],
        compiler_params=params(),
        name="middle",
    )(
        tokens, cot, cot_t, hidden_t, pre, gate, loc, carry, weights, par, par_heads, bc, bct, score,
        mask, sp, cumt, fac,
    )


def scan_back_body(
    depth, rounds, pre_ref, dy_ref, loc_ref, carry_ref, enter, cin_ref, par, par_heads,
    state_filter, cin_state, pre_state, bc, bct, score, mask, sp, cumt, fac, match, zst, dt_ref,
    exits, gate_part, block_own, tokens, cot, hidden_t, gpg, w_gate, w_inner, w_small, tap_out,
    tap_state_out, small_out, mine, block_out, inner_part, small_part, token_out, norm_out, d_bc,
    d_score, d_cum, heads, local_value, enters, gains, adjoints, edge_own, edge_in, grads, total, es,
    el, bs, bl, block_keep, *scratch
):
    group = pl.program_id(0)
    blocks = BLOCK_CUTS
    rows = pre_ref.shape[0]
    spans = rows // Q
    place = Place(depth)
    wide = exits.shape[-1]
    chaining = Chaining(place, rounds, True, enters, gains, scratch[:4], scratch[4:8])
    reducing = Reducing(
        place, 0, [(exits, slice(0, wide)), (gate_part, slice(wide, 2 * wide))], mine,
        scratch[8:16], scratch[16:],
    )
    position = place.position
    has_before, has_after = position > 0, position < 2 * depth - 1
    before, after = {"context": position - 1}, {"context": position + 1}
    share = rows // blocks

    def block_copy(index):
        at = pl.ds(pl.multiple_of(index * share, share), share)
        return remote(
            block_own.at[at], block_out.at[place.y, at], bs.at[index], bl.at[index], place.y_peer
        )

    block_local = pltpu.make_async_copy(block_own, block_out.at[place.y], block_keep.at[0])

    def edge_copy(index):
        return remote(edge_own.at[index], edge_in.at[index], es.at[index], el.at[index], before)

    def edge_wait(index):
        @pl.when(has_after)
        def _():
            edge_copy(index).wait_recv()

    def joined(index):
        grad = grads[...]
        return jnp.concatenate(
            [grad[: rows - EDGE], grad[rows - EDGE :] + edge_in[index]], axis=0
        ).astype(LOW)

    @pl.when(group == 0)
    def _():
        d_bc[...] = jnp.zeros_like(d_bc)
        d_score[...] = jnp.zeros_like(d_score)
        d_cum[...] = jnp.zeros_like(d_cum)
        heads[...] = jnp.zeros_like(heads)
        grads[...] = jnp.zeros_like(grads)
        total[...] = jnp.zeros_like(total)
        edge_in[GROUPS + 1] = jnp.zeros((EDGE, WIDE), F32)

        @pl.when(jnp.logical_not(has_after))
        def _():
            edge_in[...] = jnp.zeros_like(edge_in)

        place.greet(
            [place.mate, place.x_peer, place.y_peer],
            chaining.sometimes() + [(has_before, before), (has_after, after)],
            True,
        )
        facs = split3(fac[...])
        for cut in range(GROUPS):
            enters[cut] = enter[:, cut * WIDE : (cut + 1) * WIDE]
            chaining.open(cut)
        for cut in range(GROUPS):
            rows8 = mm(facs, spreader(4 * cut, HEAD, 4))
            gains[cut] = jnp.broadcast_to(rows8[spans : spans + 1], (8, WIDE))
        each(depth, reducing.start)
        block_local.start()
        each(3, lambda index: block_copy(index).start())
        for cut in range(GROUPS):
            chaining.pass_on(0, cut)

    @pl.when(group < GROUPS)
    def _():
        spread = spreader(4 * group, HEAD, 4)
        collect = gatherer(4 * group, HEAD, 4)
        pre = pre_ref[...]
        sigma = sigmoid(pre)
        mix = pre * sigma
        dtx = mm(sp[0], spread)
        growth = mm(sp[2], spread)
        facx = mm(split3(fac[...]), spread)
        cums = mm(sp[1], spreader(4 * group, LANES, 4))
        half = iota((Q, LANES), 1) < HEAD
        ones = jnp.ones((8, Q), F32).astype(LOW)
        states = [carry_ref[...].astype(F32)]
        for index in range(spans - 1):
            at = slice(index * Q, (index + 1) * Q)
            states.append(facx[index : index + 1] * states[-1] + loc_ref[at])
        for index in range(spans):
            at = slice(index * Q, (index + 1) * Q)
            dy = dy_ref[at]
            value = mix[at] * dtx[at]
            parts = []
            sum_score = None
            for pair in range(2):
                lanes = slice(pair * LANES, (pair + 1) * LANES)
                value_low = value[:, lanes].astype(LOW)
                local = None
                for part_of in range(2):
                    head = 2 * pair + part_of
                    across = cumt[group, head : head + 1, at]
                    spread_at = cums[at, head * LANES : (head + 1) * LANES] - across + mask[at]
                    decay = jnp.exp2(spread_at)
                    keep = half if part_of == 0 else jnp.logical_not(half)
                    dy_low = jnp.where(keep, dy[:, lanes], 0.0).astype(LOW)
                    inner = decay * mm_nt(dy_low, value_low)
                    sum_score = inner if sum_score is None else sum_score + inner
                    moved = (inner * score[at]).astype(LOW)
                    turn = mm_nt(ones, moved) - mm(ones, moved)
                    d_cum[group, head : head + 1, at] = turn[0:1]
                    part = mm_tn((decay * score[at]).astype(LOW), dy_low)
                    local = part if local is None else local + part
                parts.append(local)
            d_score[at] += sum_score
            local_value[at] = jnp.concatenate(parts, axis=1)
            pushed = dy * growth[at]
            state_low = states[index].astype(LOW)
            carried = mm(bc[at, LANES:], state_low)
            d_bc[at, LANES:] += mm_nt(pushed.astype(LOW), state_low)
            heads[1, at] += head_sums(pushed * carried, collect)

    @pl.when(group == 0)
    def _():
        for cut in range(GROUPS):
            chaining.relay(0, cut)
        chaining.later()

        def put(cut, value):
            adjoints[cut] = value

        chaining.arrive(put)
        chaining.finish()

    for turn in range(5):

        @pl.when(group == turn)
        def _():
            each(turn + 1 if turn < 4 else depth + 1, reducing.turn, turn)
            block_copy(turn + 3).start()

    @pl.when(group == 5)
    def _():
        reducing.close()

    @pl.when((group > 0) & (group < GROUPS))
    def _():
        edge_wait(group - 1)

    @pl.when(group < GROUPS)
    def _():
        spread = spreader(4 * group, HEAD, 4)
        collect = gatherer(4 * group, HEAD, 4)
        pre = pre_ref[...]
        sigma = sigmoid(pre)
        mix = pre * sigma
        dtx = mm(sp[0], spread)
        growth = mm(sp[2], spread)
        facx = mm(split3(fac[...]), spread)
        states = [carry_ref[...].astype(F32)]
        for index in range(spans - 1):
            at = slice(index * Q, (index + 1) * Q)
            states.append(facx[index : index + 1] * states[-1] + loc_ref[at])
        arrived = jnp.where(group > 0, group - 1, GROUPS + 1)
        grad = joined(arrived)
        gate_grad = gpg[...]
        inner_part[0] = mm(hidden_t[...], grad).astype(LOW)
        total[...] += mm_nt(gate_grad, w_gate[0]) + mm_nt(grad, w_inner[0])
        tails = mm(sp[3], spread)
        skipx = mm(split3(par_heads[...]), spread)[2:3]
        adjoint = adjoints[group].astype(F32)
        masks = [match[back] for back in range(CONV - 1)]
        pgs = [None] * spans
        for index in reversed(range(spans)):
            at = slice(index * Q, (index + 1) * Q)
            dy = dy_ref[at]
            value = mix[at] * dtx[at]
            adj_low = adjoint.astype(LOW)
            reached = mm(bc[at, :LANES], adj_low) * tails[at]
            d_bc[at, :LANES] += mm_nt((value * tails[at]).astype(LOW), adj_low)
            heads[0, at] += head_sums(value * reached, collect)
            fac_part = jnp.sum(adjoint * states[index], axis=0, keepdims=True)
            heads[3, index * 8 : index * 8 + 8] += head_sums(
                jnp.broadcast_to(fac_part, (8, WIDE)), collect
            )
            pushed_low = (dy * growth[at]).astype(LOW)
            adjoint = facx[index : index + 1] * adjoint + mm(bct[NSTATE:, at], pushed_low)
            d_value = local_value[at] + reached
            heads[2, at] += head_sums(mix[at] * d_value, collect)
            d_mix = dtx[at] * d_value + skipx * dy
            s = sigma[at]
            pgs[index] = d_mix * s * (1.0 + pre[at] * (1.0 - s))
        pg = jnp.concatenate(pgs, axis=0)
        sums, grad = conv_backward(pg, cin_ref[...].astype(F32), par[0], masks)
        tap_out[...] = jnp.concatenate(sums + [jnp.zeros((3, WIDE), F32)], axis=0)
        grads[...] = grad[HALO:]
        edge_own[group] = grad[HALO - EDGE : HALO]

        @pl.when(has_before)
        def _():
            edge_copy(group).start()

    @pl.when(group == GROUPS)
    def _():
        masks = [match[back] for back in range(CONV - 1)]
        edge_wait(GROUPS - 1)
        grad = joined(GROUPS - 1)
        inner_part[0] = mm(hidden_t[...], grad).astype(LOW)
        total[...] += mm_nt(grad, w_inner[0])
        t_at, u_at = iota((Q, Q), 0), iota((Q, Q), 1)
        onward = (t_at <= u_at).astype(F32)
        earlier = (t_at > u_at).astype(F32)
        rate = jnp.exp(par_heads[1:2])
        raws = []
        bias_sum = jnp.zeros((1, LANES), F32)
        decay_sum = jnp.zeros((1, LANES), F32)
        used = iota((Q, LANES), 1) < 24
        for index in range(spans):
            at = slice(index * Q, (index + 1) * Q)
            pieces = [d_cum[piece, 0:4, at] for piece in range(6)]
            pieces.append(jnp.zeros((LANES - 24, Q), F32))
            cum_col = jnp.transpose(jnp.concatenate(pieces, axis=0))
            fac_row = fac[index : index + 1] * heads[3, index * 8 : index * 8 + 1]
            d_decay = (
                mm_exact(onward, cum_col + heads[1, at]) + mm_exact(earlier, heads[0, at]) + fac_row
            )
            dt = dt_ref[at]
            raw = (heads[2, at] - d_decay * rate) * sigmoid(zst[at])
            raw = jnp.where(used, raw, 0.0)
            raws.append(raw.astype(LOW))
            bias_sum += jnp.sum(raw, axis=0, keepdims=True)
            decay_sum -= jnp.sum(
                jnp.where(used, d_decay * dt * rate, 0.0), axis=0, keepdims=True
            )
            score_low = d_score[at].astype(LOW)
            d_bc[at, :LANES] += mm_tn(score_low, bc[at, LANES:])
            d_bc[at, LANES:] += mm(score_low, bc[at, :LANES])
        small_out[...] = jnp.concatenate(
            [bias_sum, decay_sum, jnp.zeros((6, LANES), F32)], axis=0
        )
        pre = pre_state[...]
        s = sigmoid(pre)
        pg = d_bc[...] * s * (1.0 + pre * (1.0 - s))
        sums, grad = conv_backward(pg, cin_state[...].astype(F32), state_filter[...], masks)
        tap_state_out[...] = jnp.concatenate(sums + [jnp.zeros((3, WIDE), F32)], axis=0)
        grads[...] = grad[HALO:]
        edge_own[GROUPS] = grad[HALO - EDGE : HALO]

        @pl.when(has_before)
        def _():
            edge_copy(GROUPS).start()

        steps = jnp.concatenate(raws, axis=0)
        turned = hidden_t[...]
        step_part = mm(turned, steps).astype(LOW)
        small_part[0, :, LANES:] = step_part
        small_part[1, :, LANES:] = step_part
        total[...] += mm_nt(steps, w_small[0, :, LANES:]) + mm_nt(steps, w_small[1, :, LANES:])
        edge_wait(GROUPS)
        state = joined(GROUPS)
        state_part = mm(turned, state).astype(LOW)
        small_part[0, :, :LANES] = state_part[:, :LANES]
        small_part[1, :, :LANES] = state_part[:, LANES:]
        value = tokens[0].astype(F32)
        scale = lax.rsqrt(jnp.mean(value * value, axis=1, keepdims=True) + EPSILON)
        hidden_grad = (
            total[...]
            + mm_nt(state[:, :LANES], w_small[0, :, :LANES])
            + mm_nt(state[:, LANES:], w_small[1, :, :LANES])
        )
        norm_sum = jnp.sum(hidden_grad * (value * scale), axis=0, keepdims=True)
        norm_out[...] = jnp.broadcast_to(norm_sum, norm_out.shape)
        gain = jnp.transpose(w_small[0, :, LANES : 2 * LANES].astype(F32))[24:25]
        normed = hidden_grad * gain
        pull = jnp.sum(normed * value, axis=1, keepdims=True) / value.shape[1]
        token_out[...] = (
            cot[0].astype(F32) + scale * normed - (scale * scale * scale) * value * pull
        ).astype(LOW)
        reducing.finish()
        each(blocks, lambda index: block_copy(index).wait())
        block_local.wait()

        @pl.when(has_before)
        def _():
            each(GROUPS + 1, lambda index: edge_copy(index).wait_send())


def scan_back(
    pre, dy, loc, carry, enter, cin, par, par_heads, state_filter, cin_state, pre_state, bc, bct,
    score, mask, sp, cumt, fac, match, zst, dt, exits, gate_part, block_own, tokens, cot, hidden_t,
    gpg, weights, rounds
):
    rows, wide = pre.shape
    ext = rows + HALO
    depth = lax.axis_size("context") // 2
    own_rows, half_wide = exits.shape[3:]
    shape = jax.ShapeDtypeStruct
    sem = lambda *lead: pltpu.SemaphoreType.DMA(lead)
    model = tokens.shape[2]
    now = lambda s: jnp.minimum(s, GROUPS - 1)
    lag = lambda s: jnp.maximum(s - 1, 0)
    column = lambda count: pl.BlockSpec((count, WIDE), lambda s: (0, now(s)))
    outs = (
        (shape((8, wide), F32), column(8)),
        (shape((8, WIDE), F32), const((8, WIDE))),
        (shape((8, LANES), F32), const((8, LANES))),
        (shape((own_rows, 2 * half_wide), F32), const((own_rows, 2 * half_wide))),
        (shape((2,) + block_own.shape, LOW), ANY_SPEC),
        (
            shape((2, model, 3 * WIDE), LOW),
            pl.BlockSpec((1, model, WIDE), lambda s: (lag(s) // 3, 0, lag(s) % 3)),
        ),
        (shape((2, model, WIDE), LOW), const((2, model, WIDE))),
        (shape((rows, model), LOW), const((rows, model))),
        (shape((8, model), F32), const((8, model))),
    )
    return pl.pallas_call(
        functools.partial(scan_back_body, depth, rounds),
        out_shape=[out[0] for out in outs],
        grid=(GROUPS + 1,),
        in_specs=[
            column(rows),
            column(rows),
            column(rows),
            column(NSTATE),
            const((NSTATE, wide)),
            column(ext),
            pl.BlockSpec((1, 8, WIDE), lambda s: (now(s) // 3, 0, now(s) % 3)),
            const((8, LANES)),
            const((CONV + 1, WIDE)),
            const((ext, WIDE)),
            const((rows, WIDE)),
            const((rows, WIDE)),
            const((WIDE, rows)),
            const((rows, Q)),
            const((rows, Q)),
            const((4, rows, LANES)),
            const((6, 8, rows)),
            const((8, LANES)),
            const((CONV - 1, rows, LANES)),
            const((rows, LANES)),
            const((rows, LANES)),
            ANY_SPEC,
            ANY_SPEC,
            VMEM_SPEC,
            pl.BlockSpec((1, rows, model), lambda s: (side(), 0, 0)),
            pl.BlockSpec((1, rows, model), lambda s: (side(), 0, 0)),
            const((model, rows)),
            column(rows),
            pl.BlockSpec((1, model, WIDE), lambda s: (now(s) // 3, 0, now(s) % 3)),
            pl.BlockSpec((1, model, WIDE), lambda s: (lag(s) // 3, 0, 3 + lag(s) % 3)),
            pl.BlockSpec((2, model, WIDE), lambda s: (0, 0, 6)),
        ],
        out_specs=[out[1] for out in outs],
        scratch_shapes=[
            pltpu.VMEM((rows, WIDE), F32),
            pltpu.VMEM((rows, Q), F32),
            pltpu.VMEM((6, 8, rows), F32),
            pltpu.VMEM((4, rows, LANES), F32),
            pltpu.VMEM((rows, WIDE), F32),
            pltpu.VMEM((GROUPS, NSTATE, WIDE), F32),
            pltpu.VMEM((GROUPS, 8, WIDE), F32),
            pltpu.VMEM((GROUPS, NSTATE, WIDE), LOW),
            pltpu.VMEM((GROUPS + 1, EDGE, WIDE), F32),
            pltpu.VMEM((GROUPS + 2, EDGE, WIDE), F32),
            pltpu.VMEM((rows, WIDE), F32),
            pltpu.VMEM((rows, model), F32),
            sem(GROUPS + 1),
            sem(GROUPS + 1),
            sem(BLOCK_CUTS),
            sem(BLOCK_CUTS),
            sem(1),
        ]
        + Chaining.scratch(rounds)
        + Reducing.scratch(depth, own_rows, 2 * half_wide),
        compiler_params=params(collective_id=2, has_side_effects=True),
        name="scan_back",
    )(
        pre, dy, loc, carry, enter, cin, par, par_heads, state_filter, cin_state, pre_state, bc,
        bct, score, mask, sp, cumt, fac, match, zst, dt, exits, gate_part, block_own, tokens, cot,
        hidden_t, gpg, weights, weights, weights,
    )


def pack_body(
    side_ref, entry, exits, state, steps, gain, inner_kernel, gate_gain, bias, decay, skip, docs,
    tail_tokens, packed, packed_exit, par, doc_col, doc_row, edge
):
    side = side_ref[0]
    rows = entry.shape[0]
    wide = entry.shape[2]

    def placed(value):
        filled = jnp.concatenate(
            [value, jnp.zeros((value.shape[0], LANES - value.shape[1]), F32)], axis=1
        )
        return jnp.where(side == 0, filled, pltpu.roll(filled, value.shape[1], 1))

    packed[:, :wide] = entry[:, 0].astype(LOW)
    packed[:, wide : 2 * wide] = entry[:, 1].astype(LOW)
    half = jnp.where(side == 0, state[:, :NSTATE], state[:, NSTATE:])
    packed[:, 2 * wide : 2 * wide + NSTATE] = half.astype(LOW)
    gain_row = jnp.concatenate([gain[...], jnp.zeros((1, LANES - rows), F32)], axis=1)
    gain_col = jnp.transpose(jnp.broadcast_to(gain_row, (LANES, LANES)))[:rows]
    lane = iota((rows, LANES), 1)
    small = jnp.where(lane == 24, gain_col, placed(steps[...]))
    packed[:, 2 * wide + NSTATE :] = small.astype(LOW)
    packed_exit[...] = exits[...].astype(LOW)
    par[0 : CONV + 1] = inner_kernel[...]
    par[CONV + 1 : CONV + 2] = gate_gain[...]
    par[CONV + 2 : CONV + 4] = jnp.zeros((2, wide), F32)
    for index, ref in enumerate((bias, decay, skip)):
        par[CONV + 2 : CONV + 3, index * LANES : (index + 1) * LANES] = placed(ref[...])
    own = jnp.where(side == 0, docs[0:1], docs[1:2]).astype(F32)
    doc_row[...] = jnp.broadcast_to(own, doc_row.shape)
    doc_col[...] = jnp.transpose(jnp.broadcast_to(own, (LANES, own.shape[1])))
    edge[...] = tail_tokens[0]


def pack(
    which, entry, exits, state, steps, gain, inner_kernel, gate_gain, bias, decay, skip, docs, tokens
):
    own_rows, _, wide = entry.shape
    rows, model = tokens.shape[1:]
    shape = jax.ShapeDtypeStruct
    arrays = (
        entry, exits, state, steps, gain[None], inner_kernel, gate_gain[None], bias[None],
        decay[None], skip[None], docs,
    )
    outs = (
        shape((own_rows, 2 * wide + WIDE), LOW),
        shape((own_rows, wide), LOW),
        shape((8, wide), F32),
        shape((rows, LANES), F32),
        shape((8, rows), F32),
        shape((HALO, model), LOW),
    )
    return pl.pallas_call(
        pack_body,
        out_shape=outs,
        grid_spec=pltpu.PrefetchScalarGridSpec(
            num_scalar_prefetch=1,
            grid=(1,),
            in_specs=[const(array.shape) for array in arrays]
            + [pl.BlockSpec((1, HALO, model), lambda s, w: (w[0], rows // HALO - 1, 0))],
            out_specs=[const(out.shape) for out in outs],
        ),
        compiler_params=params(),
        name="pack",
    )(which, *arrays, tokens)


def gather_body(
    depth, packed, par_own, edge_own, docs_own, cot, weights, par, heads, edge, docs, cot_t, docs_in,
    cot_in, side_send, side_land, local, *scratch
):
    place = Place(depth)
    count = 2 * depth
    onward = {"context": lax.rem(place.position + 1, count)}
    behind = {"context": lax.rem(place.position + count - 1, count)}
    x, y, z, c = place.x, place.y, place.z, place.c
    place.greet(
        [place.mate, place.x_peer, place.y_peer, onward, behind],
        [(z + 1 < depth, place.up()), (z > 0, place.down())],
    )
    gathering = Gathering(place, packed, weights, *scratch)
    sides = [
        remote(edge_own, edge, side_send.at[0], side_land.at[0], onward),
        remote(docs_own, docs_in, side_send.at[1], side_land.at[1], onward),
        remote(par_own, par.at[y], side_send.at[2], side_land.at[2], place.y_peer),
    ]
    for copy in sides:
        copy.start()
    gathering.own()
    cot_copy = pltpu.make_async_copy(cot.at[y], cot_in, local.at[1])
    cot_copy.start()
    par_keep = pltpu.make_async_copy(par_own, par.at[y], local.at[0])
    par_keep.start()
    cot_copy.wait()
    cot_t[...] = jnp.transpose(cot_in[...])
    gathering.near()
    gathering.across()
    for copy in sides:
        copy.wait()
    docs[...] = jnp.where(place.position == 0, -1.0, docs_in[...])
    par_keep.wait()
    both = par[0, CONV + 2 : CONV + 3] + par[1, CONV + 2 : CONV + 3]
    heads[...] = jnp.zeros_like(heads)
    for index in range(3):
        heads[index : index + 1] = both[:, index * LANES : (index + 1) * LANES]
    gathering.far()
    gathering.finish()


def gather(packed, par_own, edge_own, docs_own, cot):
    count = lax.axis_size("context")
    depth = count // 2
    rows, model = cot.shape[1:]
    shape = jax.ShapeDtypeStruct
    return pl.pallas_call(
        functools.partial(gather_body, depth),
        out_shape=(
            shape((2, 2, count) + packed.shape, LOW),
            shape((2,) + par_own.shape, F32),
            shape((8, LANES), F32),
            shape(edge_own.shape, LOW),
            shape(docs_own.shape, F32),
            shape((model, rows), LOW),
        ),
        in_specs=[VMEM_SPEC] * 4 + [ANY_SPEC],
        out_specs=[ANY_SPEC] + [VMEM_SPEC] * 5,
        scratch_shapes=[
            pltpu.VMEM(docs_own.shape, F32),
            pltpu.VMEM((rows, model), LOW),
            pltpu.SemaphoreType.DMA((3,)),
            pltpu.SemaphoreType.DMA((3,)),
            pltpu.SemaphoreType.DMA((2,)),
        ]
        + Gathering.scratch(depth),
        compiler_params=params(collective_id=0, has_side_effects=True),
        name="gather",
    )(packed, par_own, edge_own, docs_own, cot)


def reduce_body(
    depth, inner, small, token, taps, taps_state, gate_row, head_rows, skip_row, norm_row,
    total, state_out, vector_out, token_out, state_own, vec_send, vec_land, vs, vl, ts, tl, ss, sl,
    keep_sem, *scratch
):
    place = Place(depth)
    x, y, z, c = place.x, place.y, place.z, place.c
    wide = inner.shape[-1]
    parts = [(inner, slice(0, wide)), (small, slice(wide, wide + WIDE))]
    reducing = Reducing(place, 0, parts, total, scratch[:8], scratch[8:])

    vec_send[0] = jnp.zeros(vec_send.shape[1:], F32)
    vec_send[0, : CONV + 1, : 2 * wide] = taps[: CONV + 1]
    vec_send[0, : CONV + 1, 2 * wide :] = taps_state[: CONV + 1]
    vec_send[0, 5:6, : 2 * wide] = gate_row[0:1]
    vec_send[0, 5:6, 2 * wide : 2 * wide + LANES] = head_rows[0:1]
    vec_send[0, 5:6, 2 * wide + LANES :] = skip_row[0:1]
    model = norm_row.shape[1]
    vec_send[0, 6:7, :model] = norm_row[0:1]
    vec_send[0, 6:7, model : model + LANES] = head_rows[1:2]

    place.greet([place.mate, place.x_peer, place.y_peer], (), True)
    vec_targets = [place.mate, place.x_peer, place.y_peer]

    def vec_copy(turn):
        return remote(
            vec_send.at[turn], vec_land.at[turn], vs.at[turn], vl.at[turn], vec_targets[turn]
        )

    def vec_far(away, lands_at):
        return remote(
            vec_send.at[3], vec_land.at[3 + lands_at], vs.at[3 + away], vl.at[3 + lands_at],
            place.away(away),
        )

    share = token.shape[0] // depth

    def token_copy(step):
        at = pl.ds(pl.multiple_of(step * share, share), share)
        return remote(token.at[at], token_out.at[y, at], ts.at[step], tl.at[step], place.y_peer)

    token_keep = pltpu.make_async_copy(token, token_out.at[y], keep_sem.at[0])

    vec_copy(0).start()
    each(depth, reducing.start)
    token_keep.start()

    def step_all(step):
        reducing.turn(step)

        @pl.when(step >= 1)
        def _():
            token_copy(step - 1).start()

        for turn in range(3):

            @pl.when(step == turn)
            def _():
                vec_copy(turn).wait_recv()
                vec_send[turn + 1] = vec_send[turn] + vec_land[turn]
                if turn < 2:
                    vec_copy(turn + 1).start()
                else:
                    each(depth, lambda s: vec_far(lax.rem(z + s, depth), z).start(), 1)
                    vec_land[3 + z] = vec_send[3]

    each(depth + 1, step_all)
    reducing.close()
    state_own[...] = total[:, wide : wide + NSTATE]
    state_copy = remote(state_own, state_out.at[y], ss.at[0], sl.at[0], place.y_peer)
    state_copy.start()
    state_out[y] = state_own[...]

    def vec_arrive(step):
        away = lax.rem(z + step, depth)
        vec_far(away, away).wait_recv()

    each(depth, vec_arrive, 1)
    vector_out[...] = vec_land[3]

    def vec_add(step):
        vector_out[...] += vec_land[3 + step]

    each(depth, vec_add, 1)
    for turn in range(3):
        vec_copy(turn).wait_send()
    each(depth, lambda s: vec_far(lax.rem(z + s, depth), z).wait_send(), 1)
    reducing.finish()
    each(depth, lambda step: token_copy(step).wait())
    state_copy.wait()
    token_keep.wait()


def reduce_all(inner, small, token, taps, taps_state, gate_row, head_rows, skip_row, norm_row):
    count = lax.axis_size("context")
    depth = count // 2
    own_rows, wide = inner.shape[3:]
    tall = wide + WIDE
    shape = jax.ShapeDtypeStruct
    sem = lambda *lead: pltpu.SemaphoreType.DMA(lead)
    vector = (8, 2 * wide + WIDE)
    return pl.pallas_call(
        functools.partial(reduce_body, depth),
        out_shape=(
            shape((own_rows, tall), F32),
            shape((2, own_rows, NSTATE), F32),
            shape(vector, F32),
            shape((2,) + token.shape, LOW),
        ),
        in_specs=[ANY_SPEC] * 2 + [VMEM_SPEC] * 7,
        out_specs=[VMEM_SPEC] * 3 + [ANY_SPEC],
        scratch_shapes=[
            pltpu.VMEM((own_rows, NSTATE), F32),
            pltpu.VMEM((4,) + vector, F32),
            pltpu.VMEM((3 + depth,) + vector, F32),
            sem(3 + depth),
            sem(3 + depth),
            sem(depth),
            sem(depth),
            sem(1),
            sem(1),
            sem(1),
        ]
        + Reducing.scratch(depth, own_rows, tall),
        compiler_params=params(collective_id=4, has_side_effects=True),
        name="reduce_all",
    )(inner, small, token, taps, taps_state, gate_row, head_rows, skip_row, norm_row)


def finish_body(
    side_ref, mine, exits, state, vector, token, block, block_out, token_out,
    norm_out, entry_out, state_out, step_out, kernel_out, filter_out, bias_out, decay_out, skip_out,
    gate_out, exit_out
):
    side, spot = side_ref[0], side_ref[1]
    token_out[...] = token[...].astype(F32)
    first = side == 0
    block_out[...] = block[...]

    @pl.when(pl.program_id(0) == 0)
    def _():
        own_rows, _, wide = entry_out.shape
        model = token.shape[2]
        entry_out[:, 0] = exits[:, wide:]
        entry_out[:, 1] = mine[:, :wide]
        exit_out[...] = exits[:, :wide]
        state_out[:, :NSTATE] = state[0]
        state_out[:, NSTATE:] = state[1]

        def twelve(value):
            return jnp.where(first, value, pltpu.roll(value, LANES - 12, 1))[:, :12]

        step_out[...] = twelve(mine[:, wide + NSTATE :])
        left, right = vector[:, :wide], vector[:, wide : 2 * wide]
        halves = jnp.where(first, left, right)
        kernel_out[...] = halves[: CONV + 1]
        gate_out[...] = halves[5:6]
        filter_out[...] = vector[: CONV + 1, 2 * wide :]
        bias_out[...] = twelve(vector[5:6, 2 * wide : 2 * wide + LANES])
        skip_out[...] = twelve(vector[5:6, 2 * wide + LANES :])
        decay_out[...] = twelve(vector[6:7, model : model + LANES])
        turned = pltpu.roll(vector[:, :model], lax.rem(model - spot * own_rows, model), 1)
        norm_out[...] = turned[6:7, :own_rows]


def finish(side, mine, exits, state, vector, token, block):
    own_rows, wide = exits.shape[0], exits.shape[1] // 2
    _, rows, model = token.shape
    share = rows // 4
    shape = jax.ShapeDtypeStruct
    outs = (
        (shape((2, rows, model), LOW), pl.BlockSpec((2, share, model), lambda s, w: (0, s, 0))),
        (shape((2, rows, model), F32), pl.BlockSpec((2, share, model), lambda s, w: (0, s, 0))),
        (shape((1, own_rows), F32), None),
        (shape((own_rows, 2, wide), F32), None),
        (shape((own_rows, WIDE), F32), None),
        (shape((own_rows, 12), F32), None),
        (shape((CONV + 1, wide), F32), None),
        (shape((CONV + 1, WIDE), F32), None),
        (shape((1, 12), F32), None),
        (shape((1, 12), F32), None),
        (shape((1, 12), F32), None),
        (shape((1, wide), F32), None),
        (shape((own_rows, wide), F32), None),
    )
    return pl.pallas_call(
        finish_body,
        out_shape=[out[0] for out in outs],
        grid_spec=pltpu.PrefetchScalarGridSpec(
            num_scalar_prefetch=1,
            grid=(4,),
            in_specs=[
                const(mine.shape),
                const(exits.shape),
                const(state.shape),
                const(vector.shape),
                pl.BlockSpec((2, share, model), lambda s, w: (0, s, 0)),
                pl.BlockSpec((2, share, model), lambda s, w: (0, s, 0)),
            ],
            out_specs=[out[1] if out[1] is not None else const(out[0].shape) for out in outs],
        ),
        compiler_params=params(),
        name="finish",
    )(side, mine, exits, state, vector, token, block)


def body(
    tokens, documents, norm_gain, entry_weight, state_weight, step_weight, inner_kernel,
    state_filter, step_bias, decay_log, skip_gain, gate_gain, exit_weight, cotangent,
):
    seqs, rows, model = tokens.shape
    count = lax.axis_size("context")
    position, side = lax.axis_index("context"), lax.axis_index("tensor")
    own_rows = norm_gain.shape[0]
    which = jnp.stack([side, lax.axis_index("dp") * count + position]).astype(jnp.int32)
    longest = rows * count // 4
    rounds = min(count // 2 - 1, -(-(longest - 1) // (2 * rows)))

    packed, packed_exit, par_own, doc_col, doc_row, edge_own = pack(
        which, entry_weight, exit_weight, state_weight, step_weight, norm_gain, inner_kernel,
        gate_gain, step_bias, decay_log, skip_gain, documents, tokens,
    )
    weights, par, par_heads, halo, halo_docs, cot_t = gather(
        packed, par_own, edge_own, doc_col[-HALO:], cotangent
    )
    weights = weights.reshape(2, model, -1)
    (
        hidden_t, cin, gate, pre, loc, carry, exit_weights, cin_state, pre_state, bc, bct, score,
        mask, zst, dt, sp, cumt, fac, match,
    ) = front(
        tokens, halo, halo_docs, doc_col, doc_row, weights, par, par_heads, state_filter,
        packed_exit, rounds,
    )
    exit_weights = exit_weights.reshape(2, model, -1)
    block_own, exit_part, gate_part, dy, gpg, enter, gate_row, skip_row = middle(
        tokens, cotangent, cot_t, hidden_t, pre, gate, loc, carry, exit_weights, par, par_heads, bc,
        bct, score, mask, sp, cumt, fac,
    )
    cut = lambda v: v.reshape(2, 2, count, own_rows, v.shape[-1])
    (
        taps, taps_state, head_rows, exit_mine, block_both, inner_part, small_part, token_own,
        norm_row,
    ) = scan_back(
        pre, dy, loc, carry, enter, cin, par, par_heads, state_filter, cin_state, pre_state, bc, bct,
        score, mask, sp, cumt, fac, match, zst, dt, cut(exit_part), cut(gate_part), block_own,
        tokens, cotangent, hidden_t, gpg, weights, rounds,
    )
    mine, state_both, vector, token_both = reduce_all(
        cut(inner_part), cut(small_part), token_own, taps, taps_state, gate_row, head_rows, skip_row,
        norm_row,
    )
    outs = finish(which, mine, exit_mine, state_both, vector, token_both, block_both)
    flat = (2, 8, 9, 10, 11)
    return tuple(out[0] if index in flat else out for index, out in enumerate(outs))


def solution(mesh):
    in_specs = (
        P("dp", "context", None),
        P("dp", "context"),
        P(("dp", "context")),
        P(("dp", "context"), None, "tensor"),
        P(("dp", "context"), None),
        P(("dp", "context"), "tensor"),
        P(None, "tensor"),
        P(),
        P("tensor"),
        P("tensor"),
        P("tensor"),
        P("tensor"),
        P(("dp", "context"), "tensor"),
        P("dp", "context", None),
    )
    out_specs = (
        P("dp", "context", None),
        P("dp", "context", None),
        P(("dp", "context")),
        P(("dp", "context"), None, "tensor"),
        P(("dp", "context"), None),
        P(("dp", "context"), "tensor"),
        P(None, "tensor"),
        P(),
        P("tensor"),
        P("tensor"),
        P("tensor"),
        P("tensor"),
        P(("dp", "context"), "tensor"),
    )
    return jax.shard_map(body, mesh=mesh, in_specs=in_specs, out_specs=out_specs, check_vma=False)
```

```python
import functools
import jax
import jax.numpy as jnp
from jax import lax
from jax.experimental import pallas as pl
from jax.experimental.pallas import tpu as pltpu
from jax.sharding import PartitionSpec as P

HEAD = 64
NSTATE = 128
CONV = 4
EPSILON = 1e-05
Q = 128
HALO = 16
EDGE = 8
GROUPS = 6
BLOCK_CUTS = 8
ORDER = (0, 3, 1, 4, 2, 5)
LANES = 128
WIDE = 256
LOG2E = 1.4426950408889634
FAR = -1e30
LOW = jnp.bfloat16
F32 = jnp.float32
VMEM_LIMIT = 60 * 1024 * 1024


def mm(a, b):
    return lax.dot_general(a, b, (((1,), (0,)), ((), ())), preferred_element_type=F32)


def mm_nt(a, b):
    return lax.dot_general(a, b, (((1,), (1,)), ((), ())), preferred_element_type=F32)


def mm_tn(a, b):
    return lax.dot_general(a, b, (((0,), (0,)), ((), ())), preferred_element_type=F32)


def mm_exact(a, b):
    return lax.dot_general(
        a, b, (((1,), (0,)), ((), ())), precision=lax.Precision.HIGHEST, preferred_element_type=F32
    )


def split3(v):
    high = v.astype(LOW).astype(F32)
    rest = v - high
    mid = rest.astype(LOW).astype(F32)
    low = rest - mid
    return (high + pltpu.roll(mid, 32, 1) + pltpu.roll(low, 64, 1)).astype(LOW)


def iota(shape, dim):
    return lax.broadcasted_iota(jnp.int32, shape, dim)


def spreader(first_head, width, count):
    k = iota((LANES, width * count), 0)
    lane = iota((LANES, width * count), 1)
    hit = ((k & 31) == first_head + lane // width) & (k < 96)
    return hit.astype(F32).astype(LOW)


def gatherer(first_head, width, count):
    lane = iota((width * count, LANES), 0)
    k = iota((width * count, LANES), 1)
    return (k == first_head + lane // width).astype(F32).astype(LOW)


def head_sums(v, collect):
    high = v.astype(LOW)
    rest = (v - high.astype(F32)).astype(LOW)
    return mm(high, collect) + mm(rest, collect)


def sigmoid(v):
    return 1.0 / (1.0 + jnp.exp(-v))


def twice(v):
    return jnp.concatenate([v, v], axis=1)


def conv_forward(cin, taps, masks):
    rows = cin.shape[0] - HALO
    out = taps[CONV : CONV + 1] + taps[CONV - 1 : CONV] * cin[HALO:]
    for back in range(1, CONV):
        part = cin[HALO - back : HALO - back + rows]
        out = out + taps[CONV - 1 - back : CONV - back] * (part * twice(masks[back - 1]))
    return out


def conv_backward(pg, cin, taps, masks):
    rows, width = pg.shape
    sums = [None] * (CONV + 1)
    sums[CONV] = jnp.sum(pg, axis=0, keepdims=True)
    sums[CONV - 1] = jnp.sum(pg * cin[HALO:], axis=0, keepdims=True)
    pad = jnp.zeros((HALO, width), F32)
    grad = jnp.concatenate([pad, pg * taps[CONV - 1 : CONV]], axis=0)
    for back in range(1, CONV):
        masked = pg * twice(masks[back - 1])
        part = cin[HALO - back : HALO - back + rows]
        sums[CONV - 1 - back] = jnp.sum(masked * part, axis=0, keepdims=True)
        padded = jnp.concatenate([pad, masked * taps[CONV - 1 - back : CONV - back], pad], axis=0)
        grad = grad + padded[back : back + rows + HALO]
    return sums, grad


def const(shape):
    zeros = (0,) * len(shape)
    return pl.BlockSpec(shape, lambda *_: zeros)


def params(**extra):
    return pltpu.CompilerParams(vmem_limit_bytes=VMEM_LIMIT, **extra)


VMEM_SPEC = pl.BlockSpec(memory_space=pltpu.VMEM)
ANY_SPEC = pl.BlockSpec(memory_space=pl.ANY)


def side():
    return lax.axis_index("tensor")


def remote(src, dst, send_sem, recv_sem, target):
    return pltpu.make_async_remote_copy(
        src_ref=src,
        dst_ref=dst,
        send_sem=send_sem,
        recv_sem=recv_sem,
        device_id=target,
        device_id_type=pl.DeviceIdType.MESH,
    )


def each(count, run, first=0):
    def one(step, carry):
        run(step)
        return carry

    lax.fori_loop(first, count, one, 0)


class Place:
    def __init__(self, depth):
        position = lax.axis_index("context")
        self.depth = depth
        self.position = position
        self.x, self.y = lax.axis_index("dp"), lax.axis_index("tensor")
        self.z, self.c = position // 2, position % 2
        self.mate = self.at(self.x, self.y, self.z, 1 - self.c)
        self.x_peer = self.at(1 - self.x, self.y, self.z, self.c)
        self.y_peer = self.at(self.x, 1 - self.y, self.z, self.c)

    def at(self, x, y, z, c):
        return {"dp": x, "context": z * 2 + c, "tensor": y}

    def up(self):
        return self.at(self.x, self.y, self.z + 1, self.c)

    def down(self):
        return self.at(self.x, self.y, self.z - 1, self.c)

    def away(self, z):
        return self.at(self.x, self.y, z, self.c)

    def axes(self, turned):
        x, y, z, c = self.x, self.y, self.z, self.c
        x1, y1 = x + (1 - turned) * (1 - 2 * x), y + turned * (1 - 2 * y)
        x2, y2 = x + turned * (1 - 2 * x), y + (1 - turned) * (1 - 2 * y)
        return (x1, y1), (x2, y2)

    def around(self, run, first=0, last=None):
        z, depth = self.z, self.depth
        if first == 0:
            run(z)

        def step(away):
            @pl.when(z - away >= 0)
            def _():
                run(z - away)

            @pl.when(z + away < depth)
            def _():
                run(z + away)

        each(depth if last is None else last, step, max(first, 1))

    def greet(self, always, sometimes=(), column=False):
        barrier = pltpu.get_barrier_semaphore()
        kind = pl.DeviceIdType.MESH
        total = len(always)
        for target in always:
            pl.semaphore_signal(barrier, inc=1, device_id=target, device_id_type=kind)
        for holds, target in sometimes:

            @pl.when(holds)
            def _():
                pl.semaphore_signal(barrier, inc=1, device_id=target, device_id_type=kind)

            total = total + holds.astype(jnp.int32)
        if column:
            for_all = lambda step: pl.semaphore_signal(
                barrier,
                inc=1,
                device_id=self.away(lax.rem(self.z + step, self.depth)),
                device_id_type=kind,
            )
            each(self.depth, for_all, 1)
            total = total + (self.depth - 1)
        pl.semaphore_wait(barrier, total)


class Gathering:
    def __init__(self, place, own, full, sends, lands, local):
        self.place, self.own_ref, self.full = place, own, full
        self.sends, self.lands, self.local = sends, lands, local
        self.starts = [first * place.depth for first in (0, 4, 5, 7, 8)]
        (self.x1, self.y1), (self.x2, self.y2) = place.axes(place.c)
        self.first = place.at(self.x1, self.y1, place.z, place.c)
        self.second = place.at(self.x2, self.y2, place.z, place.c)

    @staticmethod
    def scratch(depth):
        sem = pltpu.SemaphoreType.DMA
        return [sem((9 * depth,)), sem((8 * depth,)), sem((1,))]

    def copy(self, kind, index, x, y, z, c, target, own=False):
        chunk = self.full.at[y, x, z * 2 + c]
        mark = ((y * 2 + x) * self.place.depth + z) * 2 + c
        return remote(
            self.own_ref if own else chunk, chunk, self.sends.at[self.starts[kind] + index],
            self.lands.at[mark], target,
        )

    def arrive(self, x, y, z, c):
        self.copy(0, 0, x, y, z, c, self.place.mate).wait_recv()

    def kept(self):
        p = self.place
        return pltpu.make_async_copy(
            self.own_ref, self.full.at[p.y, p.x, p.z * 2 + p.c], self.local.at[0]
        )

    def own(self):
        p = self.place
        mine = (p.x, p.y, p.z, p.c)

        @pl.when(p.z + 1 < p.depth)
        def _():
            self.copy(3, p.z, *mine, p.up(), True).start()

        @pl.when(p.z > 0)
        def _():
            self.copy(4, p.z, *mine, p.down(), True).start()

        self.copy(1, p.z, *mine, self.first, True).start()
        self.copy(2, p.z, *mine, self.second, True).start()
        self.copy(0, p.z, *mine, p.mate, True).start()
        self.kept().start()

    def near(self, first=1, last=None):
        p = self.place

        def run(z):
            chunk = (p.x, p.y, z, p.c)
            self.arrive(*chunk)

            @pl.when((z < p.z) & (p.z + 1 < p.depth))
            def _():
                self.copy(3, z, *chunk, p.up()).start()

            @pl.when((z > p.z) & (p.z > 0))
            def _():
                self.copy(4, z, *chunk, p.down()).start()

            self.copy(1, z, *chunk, self.first).start()
            self.copy(2, z, *chunk, self.second).start()
            self.copy(0, z, *chunk, p.mate).start()

        p.around(run, first, last)

    def across(self):
        p = self.place

        def run(z):
            chunk = (self.x1, self.y1, z, p.c)
            self.arrive(*chunk)
            self.copy(2, p.depth + z, *chunk, self.second).start()
            self.copy(0, p.depth + z, *chunk, p.mate).start()

        p.around(run)

    def far(self):
        p = self.place

        def near_row(z):
            self.arrive(self.x2, self.y2, z, p.c)
            self.copy(0, 2 * p.depth + z, self.x2, self.y2, z, p.c, p.mate).start()

        def far_row(z):
            self.arrive(1 - p.x, 1 - p.y, z, p.c)
            self.copy(0, 3 * p.depth + z, 1 - p.x, 1 - p.y, z, p.c, p.mate).start()

        p.around(near_row)
        p.around(far_row)

    def mates(self):
        p = self.place

        def from_mate(z):
            for y in range(2):
                for x in range(2):
                    self.arrive(x, y, z, 1 - p.c)

        each(p.depth, from_mate)
        self.kept().wait()

    def finish(self):
        p = self.place

        def sent(kind, index, target):
            self.copy(kind, index, p.x, p.y, p.z, p.c, target).wait_send()

        each(4 * p.depth, lambda step: sent(0, step, p.mate))
        each(p.depth, lambda step: sent(1, step, p.mate))
        each(2 * p.depth, lambda step: sent(2, step, p.mate))

        def chained(z):
            @pl.when((z <= p.z) & (p.z + 1 < p.depth))
            def _():
                sent(3, z, p.mate)

            @pl.when((z >= p.z) & (p.z > 0))
            def _():
                sent(4, z, p.mate)

        each(p.depth, chained)


class Reducing:
    def __init__(self, place, turned, parts, total, bufs, sems):
        self.place, self.parts, self.total = place, parts, total
        self.own, self.core, self.send1, self.land1 = bufs[:4]
        self.send2, self.land2, self.send3, self.land3 = bufs[4:]
        self.own_sem, self.core_send, self.core_land = sems[:3]
        self.s1, self.l1, self.s2, self.l2, self.s3, self.l3 = sems[3:]
        self.turned = turned
        (x1, y1), (x2, y2) = place.axes(turned)
        self.first = place.at(x1, y1, place.z, place.c)
        self.second = place.at(x2, y2, place.z, place.c)
        self.mine = place.y + turned * (place.x - place.y)

    @staticmethod
    def scratch(depth, rows, tall):
        buffer = lambda *lead: pltpu.VMEM(lead + (rows, tall), LOW)
        sem = lambda *lead: pltpu.SemaphoreType.DMA(lead)
        bufs = [
            buffer(2, 2, depth), buffer(2, 2, depth), buffer(depth, 2), buffer(depth, 2),
            buffer(depth), buffer(depth), buffer(depth), buffer(depth),
        ]
        return bufs + [sem(2, 2, depth)] * 3 + [sem(depth)] * 6

    def spot(self, step):
        return lax.rem(self.place.z + 1 + step, self.place.depth)

    def whole(self, y, x, z):
        return remote(
            self.core.at[y, x, z], self.core.at[y, x, z], self.core_send.at[y, x, z],
            self.core_land.at[y, x, z], self.place.mate,
        )

    def own_whole(self, y, x, z):
        return pltpu.make_async_copy(
            self.own.at[y, x, z], self.own.at[y, x, z], self.own_sem.at[y, x, z]
        )

    def start(self, step):
        p = self.place
        z = self.spot(step)
        for y in range(2):
            for x in range(2):
                for ref, cols in self.parts:
                    remote(
                        ref.at[y, x, z * 2 + 1 - p.c], self.core.at[y, x, z, :, cols],
                        self.core_send.at[y, x, z], self.core_land.at[y, x, z], p.mate,
                    ).start()
                    pltpu.make_async_copy(
                        ref.at[y, x, z * 2 + p.c], self.own.at[y, x, z, :, cols],
                        self.own_sem.at[y, x, z],
                    ).start()

    def base(self, y, x, z):
        return self.own[y, x, z].astype(F32) + self.core[y, x, z].astype(F32)

    def copy1(self, z):
        return remote(
            self.send1.at[z], self.land1.at[z], self.s1.at[z], self.l1.at[z], self.first
        )

    def copy2(self, z):
        return remote(
            self.send2.at[z], self.land2.at[z], self.s2.at[z], self.l2.at[z], self.second
        )

    def copy3(self, z, lands_at):
        return remote(
            self.send3.at[z], self.land3.at[lands_at], self.s3.at[z], self.l3.at[lands_at],
            self.place.away(z),
        )

    def stage1(self, step):
        p, turned = self.place, self.turned
        z = self.spot(step)
        for y in range(2):
            for x in range(2):
                self.whole(y, x, z).wait_recv()
                self.own_whole(y, x, z).wait()
        for index in range(2):
            x = (1 - turned) * (1 - p.x) + turned * index
            y = turned * (1 - p.y) + (1 - turned) * index
            self.send1[z, index] = self.base(y, x, z).astype(LOW)
        self.copy1(z).start()

    def stage2(self, step):
        p, turned = self.place, self.turned
        z = self.spot(step)
        self.copy1(z).wait_recv()
        other = 1 - self.mine
        x = (1 - turned) * p.x + turned * other
        y = turned * p.y + (1 - turned) * other
        self.send2[z] = (self.base(y, x, z) + self.land1[z, other].astype(F32)).astype(LOW)
        self.copy2(z).start()

    def final(self, z):
        p = self.place
        self.copy2(z).wait_recv()
        return (
            self.base(p.y, p.x, z)
            + self.land1[z, self.mine].astype(F32)
            + self.land2[z].astype(F32)
        )

    def stage3(self, step):
        z = self.spot(step)
        self.send3[z] = self.final(z).astype(LOW)
        self.copy3(z, self.place.z).start()

    def turn(self, step):
        depth = self.place.depth

        @pl.when(step < depth)
        def _():
            self.stage1(step)

        @pl.when((step >= 1) & (step <= depth))
        def _():
            self.stage2(step - 1)

        @pl.when((step >= 2) & (step <= depth))
        def _():
            self.stage3(step - 2)

    def close(self):
        p = self.place
        self.total[...] = self.final(p.z)

        def add(step):
            z = lax.rem(p.z + step, p.depth)
            self.copy3(z, z).wait_recv()
            self.total[...] += self.land3[z].astype(F32)

        each(p.depth, add, 1)

    def finish(self):
        p = self.place

        def sent(z):
            for y in range(2):
                for x in range(2):
                    self.whole(y, x, z).wait_send()
            self.copy1(z).wait_send()
            self.copy2(z).wait_send()

        each(p.depth, sent)
        each(p.depth, lambda step: self.copy3(lax.rem(p.z + step, p.depth), p.z).wait_send(), 1)


class Chaining:
    def __init__(self, place, rounds, backward, fold, gain, bufs, sems):
        self.place, self.rounds = place, rounds
        self.fold, self.gain = fold, gain
        self.from_mate, self.from_chip, self.to_mate, self.to_chip = bufs
        self.mate_send, self.mate_land, self.chip_send, self.chip_land = sems
        first = 1 if backward else 0
        by = -1 if backward else 1
        self.order = place.depth - 1 - place.z if backward else place.z
        self.leads = place.c == first
        self.after = place.at(place.x, place.y, place.z + by, first)
        self.before = place.at(place.x, place.y, place.z - by, 1 - first)
        self.linked_before = self.leads & (self.order > 0)
        self.linked_after = jnp.logical_not(self.leads) & (self.order < place.depth - 1)

    @staticmethod
    def scratch(rounds):
        slots = lambda turns: pltpu.VMEM((turns, GROUPS, NSTATE, WIDE), LOW)
        marks = lambda turns: pltpu.SemaphoreType.DMA((turns, GROUPS))
        return [
            slots(rounds + 1), slots(rounds), slots(rounds + 1), slots(rounds),
            marks(rounds + 1), marks(rounds + 1), marks(rounds), marks(rounds),
        ]

    def sometimes(self):
        return [(self.linked_before, self.before), (self.linked_after, self.after)]

    def mate_copy(self, turn, cut):
        return remote(
            self.to_mate.at[turn, cut], self.from_mate.at[turn, cut], self.mate_send.at[turn, cut],
            self.mate_land.at[turn, cut], self.place.mate,
        )

    def chip_copy(self, turn, cut):
        return remote(
            self.to_chip.at[turn, cut], self.from_chip.at[turn, cut], self.chip_send.at[turn, cut],
            self.chip_land.at[turn, cut], self.after,
        )

    def joined(self, cut, arrived):
        return (self.fold[cut] + self.gain[cut, 0:1] * arrived.astype(F32)).astype(LOW)

    def open(self, cut):
        @pl.when(self.leads)
        def _():
            self.to_mate[0, cut] = self.fold[cut].astype(LOW)
            self.mate_copy(0, cut).start()

    def pass_on(self, turn, cut):
        @pl.when(jnp.logical_not(self.leads))
        def _():
            self.mate_copy(turn, cut).wait_recv()

        @pl.when(self.linked_after)
        def _():
            self.to_chip[turn, cut] = self.joined(cut, self.from_mate[turn, cut])
            self.chip_copy(turn, cut).start()

    def relay(self, turn, cut):
        @pl.when(self.linked_before)
        def _():
            self.chip_copy(turn, cut).wait_recv()
            self.to_mate[turn + 1, cut] = self.joined(cut, self.from_chip[turn, cut])
            self.mate_copy(turn + 1, cut).start()

        @pl.when(self.leads & (self.order == 0))
        def _():
            self.to_mate[turn + 1, cut] = self.fold[cut].astype(LOW)
            self.mate_copy(turn + 1, cut).start()

    def later(self):
        for turn in range(1, self.rounds):
            for cut in range(GROUPS):
                self.pass_on(turn, cut)
            for cut in range(GROUPS):
                self.relay(turn, cut)

    def arrive(self, put):
        last = self.rounds - 1

        @pl.when(self.linked_before)
        def _():
            for cut in range(GROUPS):
                put(cut, self.from_chip[last, cut])

        @pl.when(self.leads & (self.order == 0))
        def _():
            for cut in range(GROUPS):
                put(cut, jnp.zeros((NSTATE, WIDE), LOW))

        @pl.when(jnp.logical_not(self.leads))
        def _():
            for cut in range(GROUPS):
                self.mate_copy(self.rounds, cut).wait_recv()
                put(cut, self.from_mate[self.rounds, cut])

    def finish(self):
        @pl.when(self.leads)
        def _():
            for turn in range(self.rounds + 1):
                for cut in range(GROUPS):
                    self.mate_copy(turn, cut).wait_send()

        @pl.when(self.linked_after)
        def _():
            for turn in range(self.rounds):
                for cut in range(GROUPS):
                    self.chip_copy(turn, cut).wait_send()


def turn_of(step):
    index = jnp.maximum(step - 1, 0)
    half, part = index % 2, index // 2
    return half * 3 + part, half, part


def entry_body(depth, rounds, fused, *refs):
    step = pl.program_id(0)
    tokens, doc_col, doc_row, state_filter = refs[:4]
    if fused:
        own_small, own_parts, own_exit, own_par, own_edge, own_docs, cot = refs[4:11]
    else:
        w_gate, w_inner, w_small, par, heads_ref, edge, halo_docs = refs[4:11]
    (
        hidden_out, cin_out, gate_out, pre_out, loc_out, carry_out, cin_state_out, pre_state_out,
        bc_out, bct_out, score_out, mask_out, zst_out, dt_out, sp_out, cumt_out, fac_out, match_out,
    ) = refs[11:29]
    refs = refs[29:]
    if fused:
        small_out, parts_out, exit_out, par, heads_ref, cot_t = refs[:6]
        refs = refs[6:]
    hidden, normed, sp_tail, facs, folds, gains = refs[:6]
    rows, model = tokens.shape[1:]
    spans = rows // Q
    place = Place(depth)
    chaining = Chaining(place, rounds, False, folds, gains, refs[6:10], refs[10:14])
    group, half, part = turn_of(step)
    x, y, z, c = place.x, place.y, place.z, place.c
    meets = [(z + 1 < depth, place.up()), (z > 0, place.down())]
    if fused:
        v_small, v_parts, edge, halo_docs, docs_in, cot_in, par_in = refs[14:21]
        side_send, side_land, local, out_sem = refs[21:25]
        marks = refs[25:]
        own = [own_small, own_parts.at[0], own_parts.at[1], own_parts.at[2], own_exit]
        full = [v_small, v_parts.at[0], v_parts.at[1], v_parts.at[2], exit_out]
        pieces = [
            Gathering(place, own[i], full[i], *marks[3 * i : 3 * i + 3]) for i in range(5)
        ]
        stores = [pltpu.make_async_copy(v_small, small_out, out_sem.at[0])]
        for index in range(3):
            stores.append(
                pltpu.make_async_copy(
                    v_parts.at[index], parts_out.at[index], out_sem.at[index + 1]
                )
            )

    def before_weights():
        for ref, first, count in ((edge, 0, HALO), (tokens, HALO, rows)):
            value = (ref[...] if ref is edge else ref[0]).astype(F32)
            scale = lax.rsqrt(jnp.mean(value * value, axis=1, keepdims=True) + EPSILON)
            normed[first : first + count] = value * scale
        docs = jnp.concatenate([halo_docs[...], doc_col[...]], axis=0)
        for back in range(1, CONV):
            match = (docs[HALO - back : HALO - back + rows] == docs[HALO:]).astype(F32)
            match_out[back - 1] = match
        t_at, u_at = iota((Q, Q), 0), iota((Q, Q), 1)
        for index in range(spans):
            at = slice(index * Q, (index + 1) * Q)
            same = (t_at >= u_at) & (doc_col[at] == doc_row[0:1, at])
            mask_out[at] = jnp.where(same, 0.0, FAR)

    def after_weights(small):
        gain = jnp.transpose(small[0][:, LANES:].astype(F32))[24:25]
        hidden[...] = (normed[...] * gain).astype(LOW)
        hidden_out[...] = jnp.transpose(hidden[HALO:])
        both = [mm(hidden[...], small[index]) for index in range(2)]
        cin = jnp.concatenate([both[0][:, :LANES], both[1][:, :LANES]], axis=1).astype(LOW)
        cin_state_out[...] = cin
        docs = jnp.concatenate([halo_docs[...], doc_col[...]], axis=0)
        masks = [match_out[back] for back in range(CONV - 1)]
        pre = conv_forward(cin.astype(F32), state_filter[...], masks)
        pre_state_out[...] = pre
        mixed = (pre * sigmoid(pre)).astype(LOW)
        bc_out[...] = mixed
        turned = jnp.transpose(mixed.astype(F32)).astype(LOW)
        bct_out[...] = turned
        heads = heads_ref[...]
        used = iota((rows, LANES), 1) < 24
        raw = both[0][HALO:, LANES:] + both[1][HALO:, LANES:]
        zst = jnp.where(used, raw, 0.0) + heads[0:1]
        zst_out[...] = zst
        dt = jnp.where(used, jnp.maximum(zst, 0.0) + jnp.log1p(jnp.exp(-jnp.abs(zst))), 0.0)
        dt_out[...] = dt
        decay = -dt * jnp.exp(heads[1:2])
        t_at, u_at = iota((Q, Q), 0), iota((Q, Q), 1)
        lower = (t_at >= u_at).astype(F32)
        fac_rows = []
        for index in range(spans):
            at = slice(index * Q, (index + 1) * Q)
            cum = mm_exact(lower, decay[at])
            final = cum[Q - 1 : Q]
            before = docs[HALO + index * Q - 1 : HALO + index * Q]
            here = doc_col[at]
            last = here[Q - 1 : Q]
            opened = (here == before).astype(F32)
            tail = (here == last).astype(F32) * jnp.exp(final - cum)
            fac_rows.append((last == before).astype(F32) * jnp.exp(final))
            cum2 = cum * LOG2E
            turned_cum = jnp.transpose(cum2)
            for group in range(6):
                cumt_out[group, 0:4, at] = turned_cum[4 * group : 4 * group + 4]
            sp_out[0, at] = split3(dt[at])
            sp_out[1, at] = split3(cum2)
            lanes_used = iota((Q, LANES), 1) < 24
            sp_out[2, at] = split3(jnp.where(lanes_used, opened * jnp.exp(cum), 0.0))
            sp_out[3, at] = split3(jnp.where(lanes_used, tail, 0.0))
            sp_tail[at] = split3(jnp.where(lanes_used, tail * dt[at], 0.0))
            score_out[at] = mm_nt(mixed[at, LANES:], mixed[at, :LANES])
        gain_total = fac_rows[0]
        for row in fac_rows[1:]:
            gain_total = gain_total * row
        rows8 = jnp.concatenate(
            fac_rows + [gain_total] + [jnp.zeros((1, LANES), F32)] * (7 - spans), axis=0
        )
        rows8 = jnp.where(iota((8, LANES), 1) < 24, rows8, 0.0)
        fac_out[...] = rows8
        facs[...] = split3(rows8)

    if fused:

        @pl.when(step == 0)
        def _():
            count = 2 * depth
            onward = {"context": lax.rem(place.position + 1, count)}
            behind = {"context": lax.rem(place.position + count - 1, count)}
            place.greet(
                [place.mate, place.x_peer, place.y_peer, onward, behind],
                meets + chaining.sometimes(),
            )
            sides = [
                remote(own_edge, edge, side_send.at[0], side_land.at[0], onward),
                remote(own_docs, docs_in, side_send.at[1], side_land.at[1], onward),
                remote(own_par, par_in.at[y], side_send.at[2], side_land.at[2], place.y_peer),
            ]
            for copy in sides:
                copy.start()
            for piece in pieces:
                piece.own()
            cot_copy = pltpu.make_async_copy(cot.at[y], cot_in, local.at[0])
            par_keep = pltpu.make_async_copy(own_par, par_in.at[y], local.at[1])
            cot_copy.start()
            par_keep.start()
            for copy in sides:
                copy.wait()
            par_keep.wait()
            pieces[0].near()
            pieces[1].near()
            halo_docs[...] = jnp.where(place.position == 0, -1.0, docs_in[...])
            par[...] = par_in[...]
            both = par[0, CONV + 2 : CONV + 3] + par[1, CONV + 2 : CONV + 3]
            heads_ref[...] = jnp.zeros_like(heads_ref)
            for index in range(3):
                heads_ref[index : index + 1] = both[:, index * LANES : (index + 1) * LANES]
            before_weights()
            pieces[0].across()
            pieces[2].near()
            pieces[1].across()
            pieces[0].far()
            cot_copy.wait()
            cot_t[...] = jnp.transpose(cot_in[...])
            pieces[0].mates()
            stores[0].start()
            after_weights([v_small[index].reshape(model, WIDE) for index in range(2)])

        @pl.when(step == 1)
        def _():
            pieces[3].near()
            pieces[2].across()
            pieces[1].far()
            pieces[1].mates()
            stores[1].start()

        @pl.when(step == 2)
        def _():
            pieces[4].near()

        @pl.when(step == 3)
        def _():
            pieces[3].across()
            pieces[2].far()
            pieces[2].mates()
            stores[2].start()

        @pl.when(step == 4)
        def _():
            pieces[4].across()

        @pl.when(step == 5)
        def _():
            pieces[3].far()
            pieces[3].mates()
            stores[3].start()

        @pl.when(step == 6)
        def _():
            pieces[4].far()

    else:

        @pl.when(step == 0)
        def _():
            place.greet([place.mate], chaining.sometimes())
            before_weights()
            after_weights([w_small[index] for index in range(2)])

    for cut in range(GROUPS - 1):

        @pl.when(step == cut + 2)
        def _():
            chaining.pass_on(0, cut)

    for cut in range(GROUPS - 3):

        @pl.when(step == cut + 4)
        def _():
            chaining.relay(0, cut)

    @pl.when(step > 0)
    def _():
        if fused:
            gate_low = v_parts[part, half, :, :, :, :WIDE].reshape(model, WIDE)
            inner_low = v_parts[part, half, :, :, :, WIDE:].reshape(model, WIDE)
        else:
            gate_low, inner_low = w_gate[0, 0], w_inner[0, 0]
        taps = par[half, :, pl.ds(pl.multiple_of(part * WIDE, WIDE), WIDE)]
        cin = mm(hidden[...], inner_low).astype(LOW)
        cin_out[...] = cin
        gate_out[...] = mm(hidden[HALO:], gate_low)
        masks = [match_out[back] for back in range(CONV - 1)]
        pre = conv_forward(cin.astype(F32), taps, masks)
        pre_out[...] = pre
        spread = spreader(4 * group, HEAD, 4)
        value = (pre * sigmoid(pre) * mm(sp_tail[...], spread)).astype(LOW)
        facx = mm(facs[...], spread)
        fold = jnp.zeros((NSTATE, WIDE), F32)
        for index in range(spans):
            at = slice(index * Q, (index + 1) * Q)
            loc = mm(bct_out[:NSTATE, at], value[at])
            loc_out[at] = loc
            fold = facx[index : index + 1] * fold + loc
        folds[step - 1] = fold
        gains[step - 1] = jnp.broadcast_to(facx[spans : spans + 1], (8, WIDE))

    for cut in range(GROUPS):

        @pl.when(step == cut + 1)
        def _():
            chaining.open(cut)

    @pl.when(step == GROUPS)
    def _():
        chaining.pass_on(0, GROUPS - 1)
        for cut in range(GROUPS - 3, GROUPS):
            chaining.relay(0, cut)
        chaining.later()

        def put(cut, value):
            at = ORDER[cut] * WIDE
            carry_out[:, at : at + WIDE] = value

        chaining.arrive(put)
        if fused:
            pieces[4].mates()
            for piece in pieces:
                piece.finish()
            for store in stores:
                store.wait()
        chaining.finish()


def entry(tokens, doc_col, doc_row, state_filter, packs, cot, rounds):
    own_small, own_parts, own_exit, own_par, own_edge, own_docs = packs
    rows, model = tokens.shape[1:]
    count = lax.axis_size("context")
    depth = count // 2
    wide = GROUPS * WIDE
    ext = rows + HALO
    fused = own_small.shape[0] % 16 == 0
    shape = jax.ShapeDtypeStruct
    sem = lambda *lead: pltpu.SemaphoreType.DMA(lead)
    column = lambda count: pl.BlockSpec((count, WIDE), lambda s: (0, turn_of(s)[0]))
    whole = lambda *dims, dtype=F32: (shape(dims, dtype), const(dims))
    outs = [
        whole(model, rows, dtype=LOW),
        (shape((ext, wide), LOW), column(ext)),
        (shape((rows, wide), F32), column(rows)),
        (shape((rows, wide), F32), column(rows)),
        (shape((rows, wide), F32), column(rows)),
        whole(NSTATE, wide, dtype=LOW),
        whole(ext, WIDE, dtype=LOW),
        whole(rows, WIDE),
        whole(rows, WIDE, dtype=LOW),
        whole(WIDE, rows, dtype=LOW),
        whole(rows, Q),
        whole(rows, Q),
        whole(rows, LANES),
        whole(rows, LANES),
        whole(4, rows, LANES, dtype=LOW),
        whole(6, 8, rows),
        whole(8, LANES),
        whole(CONV - 1, rows, LANES),
    ]
    scratch = [
        pltpu.VMEM((ext, model), LOW),
        pltpu.VMEM((ext, model), F32),
        pltpu.VMEM((rows, LANES), LOW),
        pltpu.VMEM((8, LANES), LOW),
        pltpu.VMEM((GROUPS, NSTATE, WIDE), F32),
        pltpu.VMEM((GROUPS, 8, WIDE), F32),
    ] + Chaining.scratch(rounds)
    in_specs = [
        pl.BlockSpec((1, rows, model), lambda s: (side(), 0, 0)),
        const((rows, LANES)),
        const((8, rows)),
        const((CONV + 1, WIDE)),
    ]
    args = [tokens, doc_col, doc_row, state_filter]
    full = lambda own: (2, 2, count) + own.shape[-2:]
    if fused:
        outs += [
            (shape(full(own_small), LOW), ANY_SPEC),
            (shape((3,) + full(own_parts), LOW), ANY_SPEC),
            (shape(full(own_exit), LOW), ANY_SPEC),
            (shape((2,) + own_par.shape, F32), VMEM_SPEC),
            (shape((8, LANES), F32), VMEM_SPEC),
            (shape((model, rows), LOW), VMEM_SPEC),
        ]
        scratch += [
            pltpu.VMEM(full(own_small), LOW),
            pltpu.VMEM((3,) + full(own_parts), LOW),
            pltpu.VMEM(own_edge.shape, LOW),
            pltpu.VMEM(own_docs.shape, F32),
            pltpu.VMEM(own_docs.shape, F32),
            pltpu.VMEM((rows, model), LOW),
            pltpu.VMEM((2,) + own_par.shape, F32),
            sem(3),
            sem(3),
            sem(2),
            sem(4),
        ] + Gathering.scratch(depth) * 5
        in_specs += [VMEM_SPEC] * 6 + [ANY_SPEC]
        args += [own_small, own_parts, own_exit, own_par, own_edge, own_docs, cot]
    else:
        small, parts, exits, par, heads, edge, docs, cot_t = gather(*packs, cot)
        weights = parts.reshape(3, 2, model, 2 * WIDE)
        block = lambda at: pl.BlockSpec(
            (1, 1, model, WIDE), lambda s: (turn_of(s)[2], turn_of(s)[1], 0, at)
        )
        in_specs += [block(0), block(1), const((2, model, WIDE))] + [VMEM_SPEC] * 4
        args += [weights, weights, small.reshape(2, model, WIDE), par, heads, edge, docs]
    results = pl.pallas_call(
        functools.partial(entry_body, depth, rounds, fused),
        out_shape=[out[0] for out in outs],
        grid=(GROUPS + 1,),
        in_specs=in_specs,
        out_specs=[out[1] for out in outs],
        scratch_shapes=scratch,
        compiler_params=params(collective_id=1, has_side_effects=True),
        name="entry",
    )(*args)
    if fused:
        small, parts, exits, par, heads, cot_t = results[18:]
    return tuple(results[:18]), (
        small.reshape(2, model, WIDE),
        parts.reshape(3, 2, model, 2 * WIDE),
        exits.reshape(2, model, -1),
        par,
        heads,
        cot_t,
    )


def middle_body(
    tokens, cot, cot_t, hidden_t, pre_ref, gate_ref, loc_ref, carry_ref, w_exit, par, par_heads, bc,
    bct, score, mask, sp, cumt, fac, block_out, exit_out, gate_part_out, dy_out, gpg_out, enter_out, row_out,
    skip_out, outputs, gates, unit_grads, mixes, sums, total
):
    step = pl.program_id(0)
    rows = pre_ref.shape[0]
    spans = rows // Q
    wide = 6 * WIDE

    @pl.when(step == 0)
    def _():
        sums[...] = jnp.zeros_like(sums)
        total[...] = jnp.zeros_like(total)
        skip_out[...] = jnp.zeros_like(skip_out)

    @pl.when(step < 6)
    def _():
        group = step
        spread = spreader(4 * group, HEAD, 4)
        pre = pre_ref[...]
        mix = pre * sigmoid(pre)
        mixes[group] = mix
        value = mix * mm(sp[0], spread)
        growth = mm(sp[2], spread)
        facx = mm(split3(fac[...]), spread)
        cums = mm(sp[1], spreader(4 * group, LANES, 4))
        skipx = mm(split3(par_heads[...]), spread)[2:3]
        state = carry_ref[...].astype(F32)
        half = iota((Q, LANES), 1) < HEAD
        for index in range(spans):
            at = slice(index * Q, (index + 1) * Q)
            carried = mm(bc[at, LANES:], state.astype(LOW)) * growth[at]
            parts = []
            for pair in range(2):
                lanes = slice(pair * LANES, (pair + 1) * LANES)
                local = None
                for side in range(2):
                    head = 2 * pair + side
                    across = cumt[group, head : head + 1, at]
                    spread_at = cums[at, head * LANES : (head + 1) * LANES] - across + mask[at]
                    weight = (jnp.exp2(spread_at) * score[at]).astype(LOW)
                    keep = half if side == 0 else jnp.logical_not(half)
                    seen = jnp.where(keep, value[at, lanes], 0.0).astype(LOW)
                    part = mm(weight, seen)
                    local = part if local is None else local + part
                parts.append(local)
            out = jnp.concatenate(parts, axis=1) + carried + skipx * mix[at]
            outputs[group, at] = out
            state = facx[index : index + 1] * state + loc_ref[at]
        gate = gate_ref[...]
        gates[group] = gate
        gated = outputs[group] * (gate * sigmoid(gate))
        unit_grad = mm(cot[0], w_exit[0])
        unit_grads[group] = unit_grad
        square = gated * gated
        cross = unit_grad * par[0, 5:6] * gated
        sums[0] += square[:, :LANES] + square[:, LANES:]
        sums[1] += cross[:, :LANES] + cross[:, LANES:]

    @pl.when(step == 5)
    def _():
        square = jnp.sum(sums[0], axis=1, keepdims=True)
        cross = jnp.sum(sums[1], axis=1, keepdims=True)
        normal = lax.rsqrt(square / wide + EPSILON)
        sums[0] = jnp.broadcast_to(normal, (rows, LANES))
        sums[1] = jnp.broadcast_to(normal * normal * normal * cross / wide, (rows, LANES))

    @pl.when(step >= 6)
    def _():
        group = step - 6
        spread = spreader(4 * group, HEAD, 4)
        normal = twice(sums[0])
        pull = twice(sums[1])
        gain = par[0, 5:6]
        gate = gates[group]
        out = outputs[group]
        unit_grad = unit_grads[group]
        sigma = sigmoid(gate)
        act = gate * sigma
        gated = out * act
        scaled_in = gated * normal
        unit = (scaled_in * gain).astype(LOW)
        total[...] += mm_nt(unit, w_exit[0])
        exit_out[0] = mm(cot_t[...], unit).astype(LOW)
        gate_sum = jnp.sum(unit_grad * scaled_in, axis=0, keepdims=True)
        gated_grad = normal * (unit_grad * gain) - pull * gated
        dy = gated_grad * act
        dy_out[...] = dy
        gate_grad = (gated_grad * out * sigma * (1.0 + gate * (1.0 - sigma))).astype(LOW)
        gpg_out[...] = gate_grad
        gate_part_out[0] = mm(hidden_t[...], gate_grad).astype(LOW)
        skip_sum = jnp.sum(dy * mixes[group], axis=0, keepdims=True)
        row_out[...] = jnp.broadcast_to(gate_sum, (8, WIDE))
        skip_out[...] += head_sums(
            jnp.broadcast_to(skip_sum, (8, WIDE)), gatherer(4 * group, HEAD, 4)
        )
        facx = mm(split3(fac[...]), spread)
        pushed = (dy * mm(sp[2], spread)).astype(LOW)
        enter = jnp.zeros((NSTATE, WIDE), F32)
        for index in reversed(range(spans)):
            at = slice(index * Q, (index + 1) * Q)
            enter = facx[index : index + 1] * enter + mm(bct[NSTATE:, at], pushed[at])
        enter_out[...] = enter

    @pl.when(step == 11)
    def _():
        block_out[...] = (tokens[0].astype(F32) + total[...]).astype(LOW)


def middle(
    tokens, cot, cot_t, hidden_t, pre, gate, loc, carry, weights, par, par_heads, bc, bct, score, mask,
    sp, cumt, fac
):
    rows, model = tokens.shape[1:]
    wide = 6 * WIDE
    shape = jax.ShapeDtypeStruct

    def early(s):
        return jnp.minimum(s, 5)

    def late(s):
        return jnp.maximum(s - 6, 0)

    def group(s):
        return s % 6

    outs = (
        (shape((rows, model), LOW), const((rows, model))),
        (
            shape((2, model, 3 * WIDE), LOW),
            pl.BlockSpec((1, model, WIDE), lambda s: (late(s) // 3, 0, late(s) % 3)),
        ),
        (
            shape((2, model, 3 * WIDE), LOW),
            pl.BlockSpec((1, model, WIDE), lambda s: (late(s) // 3, 0, late(s) % 3)),
        ),
        (shape((rows, wide), F32), pl.BlockSpec((rows, WIDE), lambda s: (0, late(s)))),
        (shape((rows, wide), LOW), pl.BlockSpec((rows, WIDE), lambda s: (0, late(s)))),
        (shape((NSTATE, wide), F32), pl.BlockSpec((NSTATE, WIDE), lambda s: (0, late(s)))),
        (shape((8, wide), F32), pl.BlockSpec((8, WIDE), lambda s: (0, late(s)))),
        (shape((8, LANES), F32), const((8, LANES))),
    )
    return pl.pallas_call(
        middle_body,
        out_shape=[out[0] for out in outs],
        grid=(12,),
        in_specs=[
                pl.BlockSpec((1, rows, model), lambda s: (side(), 0, 0)),
                pl.BlockSpec((1, rows, model), lambda s: (side(), 0, 0)),
                const((model, rows)),
                const((model, rows)),
                pl.BlockSpec((rows, WIDE), lambda s: (0, early(s))),
                pl.BlockSpec((rows, WIDE), lambda s: (0, early(s))),
                pl.BlockSpec((rows, WIDE), lambda s: (0, early(s))),
                pl.BlockSpec((NSTATE, WIDE), lambda s: (0, early(s))),
                pl.BlockSpec((1, model, WIDE), lambda s: (group(s) // 3, 0, group(s) % 3)),
                pl.BlockSpec((1, 8, WIDE), lambda s: (group(s) // 3, 0, group(s) % 3)),
                const((8, LANES)),
                const((rows, WIDE)),
                const((WIDE, rows)),
                const((rows, Q)),
                const((rows, Q)),
                const((4, rows, LANES)),
                const((6, 8, rows)),
                const((8, LANES)),
        ],
        out_specs=[out[1] for out in outs],
        scratch_shapes=[
                pltpu.VMEM((6, rows, WIDE), F32),
                pltpu.VMEM((6, rows, WIDE), F32),
                pltpu.VMEM((6, rows, WIDE), F32),
                pltpu.VMEM((6, rows, WIDE), F32),
                pltpu.VMEM((2, rows, LANES), F32),
                pltpu.VMEM((rows, model), F32),
        ],
        compiler_params=params(),
        name="middle",
    )(
        tokens, cot, cot_t, hidden_t, pre, gate, loc, carry, weights, par, par_heads, bc, bct, score,
        mask, sp, cumt, fac,
    )


def scan_back_body(
    depth, rounds, pre_ref, dy_ref, loc_ref, carry_ref, enter, cin_ref, par, par_heads,
    state_filter, cin_state, pre_state, bc, bct, score, mask, sp, cumt, fac, match, zst, dt_ref,
    exits, gate_part, block_own, tokens, cot, hidden_t, gpg, w_gate, w_inner, w_small, tap_out,
    tap_state_out, small_out, mine, block_out, inner_part, small_part, token_out, norm_out, d_bc,
    d_score, d_cum, heads, local_value, enters, gains, adjoints, edge_own, edge_in, grads, total, es,
    el, bs, bl, block_keep, *scratch
):
    group = pl.program_id(0)
    blocks = BLOCK_CUTS
    rows = pre_ref.shape[0]
    spans = rows // Q
    place = Place(depth)
    wide = exits.shape[-1]
    chaining = Chaining(place, rounds, True, enters, gains, scratch[:4], scratch[4:8])
    reducing = Reducing(
        place, 0, [(exits, slice(0, wide)), (gate_part, slice(wide, 2 * wide))], mine,
        scratch[8:16], scratch[16:],
    )
    position = place.position
    has_before, has_after = position > 0, position < 2 * depth - 1
    before, after = {"context": position - 1}, {"context": position + 1}
    share = rows // blocks

    def block_copy(index):
        at = pl.ds(pl.multiple_of(index * share, share), share)
        return remote(
            block_own.at[at], block_out.at[place.y, at], bs.at[index], bl.at[index], place.y_peer
        )

    block_local = pltpu.make_async_copy(block_own, block_out.at[place.y], block_keep.at[0])

    def edge_copy(index):
        return remote(edge_own.at[index], edge_in.at[index], es.at[index], el.at[index], before)

    def edge_wait(index):
        @pl.when(has_after)
        def _():
            edge_copy(index).wait_recv()

    def joined(index):
        grad = grads[...]
        return jnp.concatenate(
            [grad[: rows - EDGE], grad[rows - EDGE :] + edge_in[index]], axis=0
        ).astype(LOW)

    @pl.when(group == 0)
    def _():
        d_bc[...] = jnp.zeros_like(d_bc)
        d_score[...] = jnp.zeros_like(d_score)
        d_cum[...] = jnp.zeros_like(d_cum)
        heads[...] = jnp.zeros_like(heads)
        grads[...] = jnp.zeros_like(grads)
        total[...] = jnp.zeros_like(total)
        edge_in[GROUPS + 1] = jnp.zeros((EDGE, WIDE), F32)

        @pl.when(jnp.logical_not(has_after))
        def _():
            edge_in[...] = jnp.zeros_like(edge_in)

        place.greet(
            [place.mate, place.x_peer, place.y_peer],
            chaining.sometimes() + [(has_before, before), (has_after, after)],
            True,
        )
        facs = split3(fac[...])
        for cut in range(GROUPS):
            enters[cut] = enter[:, cut * WIDE : (cut + 1) * WIDE]
            chaining.open(cut)
        for cut in range(GROUPS):
            rows8 = mm(facs, spreader(4 * cut, HEAD, 4))
            gains[cut] = jnp.broadcast_to(rows8[spans : spans + 1], (8, WIDE))
        each(depth, reducing.start)
        block_local.start()
        each(3, lambda index: block_copy(index).start())
        for cut in range(GROUPS):
            chaining.pass_on(0, cut)

    @pl.when(group < GROUPS)
    def _():
        spread = spreader(4 * group, HEAD, 4)
        collect = gatherer(4 * group, HEAD, 4)
        pre = pre_ref[...]
        sigma = sigmoid(pre)
        mix = pre * sigma
        dtx = mm(sp[0], spread)
        growth = mm(sp[2], spread)
        facx = mm(split3(fac[...]), spread)
        cums = mm(sp[1], spreader(4 * group, LANES, 4))
        half = iota((Q, LANES), 1) < HEAD
        ones = jnp.ones((8, Q), F32).astype(LOW)
        states = [carry_ref[...].astype(F32)]
        for index in range(spans - 1):
            at = slice(index * Q, (index + 1) * Q)
            states.append(facx[index : index + 1] * states[-1] + loc_ref[at])
        for index in range(spans):
            at = slice(index * Q, (index + 1) * Q)
            dy = dy_ref[at]
            value = mix[at] * dtx[at]
            parts = []
            sum_score = None
            for pair in range(2):
                lanes = slice(pair * LANES, (pair + 1) * LANES)
                value_low = value[:, lanes].astype(LOW)
                local = None
                for part_of in range(2):
                    head = 2 * pair + part_of
                    across = cumt[group, head : head + 1, at]
                    spread_at = cums[at, head * LANES : (head + 1) * LANES] - across + mask[at]
                    decay = jnp.exp2(spread_at)
                    keep = half if part_of == 0 else jnp.logical_not(half)
                    dy_low = jnp.where(keep, dy[:, lanes], 0.0).astype(LOW)
                    inner = decay * mm_nt(dy_low, value_low)
                    sum_score = inner if sum_score is None else sum_score + inner
                    moved = (inner * score[at]).astype(LOW)
                    turn = mm_nt(ones, moved) - mm(ones, moved)
                    d_cum[group, head : head + 1, at] = turn[0:1]
                    part = mm_tn((decay * score[at]).astype(LOW), dy_low)
                    local = part if local is None else local + part
                parts.append(local)
            d_score[at] += sum_score
            local_value[at] = jnp.concatenate(parts, axis=1)
            pushed = dy * growth[at]
            state_low = states[index].astype(LOW)
            carried = mm(bc[at, LANES:], state_low)
            d_bc[at, LANES:] += mm_nt(pushed.astype(LOW), state_low)
            heads[1, at] += head_sums(pushed * carried, collect)

    @pl.when(group == 0)
    def _():
        for cut in range(GROUPS):
            chaining.relay(0, cut)
        chaining.later()

        def put(cut, value):
            adjoints[cut] = value

        chaining.arrive(put)
        chaining.finish()

    for turn in range(5):

        @pl.when(group == turn)
        def _():
            each(turn + 1 if turn < 4 else depth + 1, reducing.turn, turn)
            block_copy(turn + 3).start()

    @pl.when(group == 5)
    def _():
        reducing.close()

    @pl.when((group > 0) & (group < GROUPS))
    def _():
        edge_wait(group - 1)

    @pl.when(group < GROUPS)
    def _():
        spread = spreader(4 * group, HEAD, 4)
        collect = gatherer(4 * group, HEAD, 4)
        pre = pre_ref[...]
        sigma = sigmoid(pre)
        mix = pre * sigma
        dtx = mm(sp[0], spread)
        growth = mm(sp[2], spread)
        facx = mm(split3(fac[...]), spread)
        states = [carry_ref[...].astype(F32)]
        for index in range(spans - 1):
            at = slice(index * Q, (index + 1) * Q)
            states.append(facx[index : index + 1] * states[-1] + loc_ref[at])
        arrived = jnp.where(group > 0, group - 1, GROUPS + 1)
        grad = joined(arrived)
        gate_grad = gpg[...]
        inner_part[0] = mm(hidden_t[...], grad).astype(LOW)
        total[...] += mm_nt(gate_grad, w_gate[0, 0]) + mm_nt(grad, w_inner[0, 0])
        tails = mm(sp[3], spread)
        skipx = mm(split3(par_heads[...]), spread)[2:3]
        adjoint = adjoints[group].astype(F32)
        masks = [match[back] for back in range(CONV - 1)]
        pgs = [None] * spans
        for index in reversed(range(spans)):
            at = slice(index * Q, (index + 1) * Q)
            dy = dy_ref[at]
            value = mix[at] * dtx[at]
            adj_low = adjoint.astype(LOW)
            reached = mm(bc[at, :LANES], adj_low) * tails[at]
            d_bc[at, :LANES] += mm_nt((value * tails[at]).astype(LOW), adj_low)
            heads[0, at] += head_sums(value * reached, collect)
            fac_part = jnp.sum(adjoint * states[index], axis=0, keepdims=True)
            heads[3, index * 8 : index * 8 + 8] += head_sums(
                jnp.broadcast_to(fac_part, (8, WIDE)), collect
            )
            pushed_low = (dy * growth[at]).astype(LOW)
            adjoint = facx[index : index + 1] * adjoint + mm(bct[NSTATE:, at], pushed_low)
            d_value = local_value[at] + reached
            heads[2, at] += head_sums(mix[at] * d_value, collect)
            d_mix = dtx[at] * d_value + skipx * dy
            s = sigma[at]
            pgs[index] = d_mix * s * (1.0 + pre[at] * (1.0 - s))
        pg = jnp.concatenate(pgs, axis=0)
        sums, grad = conv_backward(pg, cin_ref[...].astype(F32), par[0], masks)
        tap_out[...] = jnp.concatenate(sums + [jnp.zeros((3, WIDE), F32)], axis=0)
        grads[...] = grad[HALO:]
        edge_own[group] = grad[HALO - EDGE : HALO]

        @pl.when(has_before)
        def _():
            edge_copy(group).start()

    @pl.when(group == GROUPS)
    def _():
        masks = [match[back] for back in range(CONV - 1)]
        edge_wait(GROUPS - 1)
        grad = joined(GROUPS - 1)
        inner_part[0] = mm(hidden_t[...], grad).astype(LOW)
        total[...] += mm_nt(grad, w_inner[0, 0])
        t_at, u_at = iota((Q, Q), 0), iota((Q, Q), 1)
        onward = (t_at <= u_at).astype(F32)
        earlier = (t_at > u_at).astype(F32)
        rate = jnp.exp(par_heads[1:2])
        raws = []
        bias_sum = jnp.zeros((1, LANES), F32)
        decay_sum = jnp.zeros((1, LANES), F32)
        used = iota((Q, LANES), 1) < 24
        for index in range(spans):
            at = slice(index * Q, (index + 1) * Q)
            pieces = [d_cum[piece, 0:4, at] for piece in range(6)]
            pieces.append(jnp.zeros((LANES - 24, Q), F32))
            cum_col = jnp.transpose(jnp.concatenate(pieces, axis=0))
            fac_row = fac[index : index + 1] * heads[3, index * 8 : index * 8 + 1]
            d_decay = (
                mm_exact(onward, cum_col + heads[1, at]) + mm_exact(earlier, heads[0, at]) + fac_row
            )
            dt = dt_ref[at]
            raw = (heads[2, at] - d_decay * rate) * sigmoid(zst[at])
            raw = jnp.where(used, raw, 0.0)
            raws.append(raw.astype(LOW))
            bias_sum += jnp.sum(raw, axis=0, keepdims=True)
            decay_sum -= jnp.sum(
                jnp.where(used, d_decay * dt * rate, 0.0), axis=0, keepdims=True
            )
            score_low = d_score[at].astype(LOW)
            d_bc[at, :LANES] += mm_tn(score_low, bc[at, LANES:])
            d_bc[at, LANES:] += mm(score_low, bc[at, :LANES])
        small_out[...] = jnp.concatenate(
            [bias_sum, decay_sum, jnp.zeros((6, LANES), F32)], axis=0
        )
        pre = pre_state[...]
        s = sigmoid(pre)
        pg = d_bc[...] * s * (1.0 + pre * (1.0 - s))
        sums, grad = conv_backward(pg, cin_state[...].astype(F32), state_filter[...], masks)
        tap_state_out[...] = jnp.concatenate(sums + [jnp.zeros((3, WIDE), F32)], axis=0)
        grads[...] = grad[HALO:]
        edge_own[GROUPS] = grad[HALO - EDGE : HALO]

        @pl.when(has_before)
        def _():
            edge_copy(GROUPS).start()

        steps = jnp.concatenate(raws, axis=0)
        turned = hidden_t[...]
        step_part = mm(turned, steps).astype(LOW)
        small_part[0, :, LANES:] = step_part
        small_part[1, :, LANES:] = step_part
        total[...] += mm_nt(steps, w_small[0, :, LANES:]) + mm_nt(steps, w_small[1, :, LANES:])
        edge_wait(GROUPS)
        state = joined(GROUPS)
        state_part = mm(turned, state).astype(LOW)
        small_part[0, :, :LANES] = state_part[:, :LANES]
        small_part[1, :, :LANES] = state_part[:, LANES:]
        value = tokens[0].astype(F32)
        scale = lax.rsqrt(jnp.mean(value * value, axis=1, keepdims=True) + EPSILON)
        hidden_grad = (
            total[...]
            + mm_nt(state[:, :LANES], w_small[0, :, :LANES])
            + mm_nt(state[:, LANES:], w_small[1, :, :LANES])
        )
        norm_sum = jnp.sum(hidden_grad * (value * scale), axis=0, keepdims=True)
        norm_out[...] = jnp.broadcast_to(norm_sum, norm_out.shape)
        gain = jnp.transpose(w_small[0, :, LANES : 2 * LANES].astype(F32))[24:25]
        normed = hidden_grad * gain
        pull = jnp.sum(normed * value, axis=1, keepdims=True) / value.shape[1]
        token_out[...] = (
            cot[0].astype(F32) + scale * normed - (scale * scale * scale) * value * pull
        ).astype(LOW)
        reducing.finish()
        each(blocks, lambda index: block_copy(index).wait())
        block_local.wait()

        @pl.when(has_before)
        def _():
            each(GROUPS + 1, lambda index: edge_copy(index).wait_send())


def scan_back(
    pre, dy, loc, carry, enter, cin, par, par_heads, state_filter, cin_state, pre_state, bc, bct,
    score, mask, sp, cumt, fac, match, zst, dt, exits, gate_part, block_own, tokens, cot, hidden_t,
    gpg, parts, small, rounds
):
    rows, wide = pre.shape
    ext = rows + HALO
    depth = lax.axis_size("context") // 2
    own_rows, half_wide = exits.shape[3:]
    shape = jax.ShapeDtypeStruct
    sem = lambda *lead: pltpu.SemaphoreType.DMA(lead)
    model = tokens.shape[2]
    now = lambda s: jnp.minimum(s, GROUPS - 1)
    lag = lambda s: jnp.maximum(s - 1, 0)
    column = lambda count: pl.BlockSpec((count, WIDE), lambda s: (0, now(s)))
    outs = (
        (shape((8, wide), F32), column(8)),
        (shape((8, WIDE), F32), const((8, WIDE))),
        (shape((8, LANES), F32), const((8, LANES))),
        (shape((own_rows, 2 * half_wide), F32), const((own_rows, 2 * half_wide))),
        (shape((2,) + block_own.shape, LOW), ANY_SPEC),
        (
            shape((2, model, 3 * WIDE), LOW),
            pl.BlockSpec((1, model, WIDE), lambda s: (lag(s) // 3, 0, lag(s) % 3)),
        ),
        (shape((2, model, WIDE), LOW), const((2, model, WIDE))),
        (shape((rows, model), LOW), const((rows, model))),
        (shape((8, model), F32), const((8, model))),
    )
    return pl.pallas_call(
        functools.partial(scan_back_body, depth, rounds),
        out_shape=[out[0] for out in outs],
        grid=(GROUPS + 1,),
        in_specs=[
            column(rows),
            column(rows),
            column(rows),
            column(NSTATE),
            const((NSTATE, wide)),
            column(ext),
            pl.BlockSpec((1, 8, WIDE), lambda s: (now(s) // 3, 0, now(s) % 3)),
            const((8, LANES)),
            const((CONV + 1, WIDE)),
            const((ext, WIDE)),
            const((rows, WIDE)),
            const((rows, WIDE)),
            const((WIDE, rows)),
            const((rows, Q)),
            const((rows, Q)),
            const((4, rows, LANES)),
            const((6, 8, rows)),
            const((8, LANES)),
            const((CONV - 1, rows, LANES)),
            const((rows, LANES)),
            const((rows, LANES)),
            ANY_SPEC,
            ANY_SPEC,
            VMEM_SPEC,
            pl.BlockSpec((1, rows, model), lambda s: (side(), 0, 0)),
            pl.BlockSpec((1, rows, model), lambda s: (side(), 0, 0)),
            const((model, rows)),
            column(rows),
            pl.BlockSpec((1, 1, model, WIDE), lambda s: (now(s) % 3, now(s) // 3, 0, 0)),
            pl.BlockSpec((1, 1, model, WIDE), lambda s: (lag(s) % 3, lag(s) // 3, 0, 1)),
            const((2, model, WIDE)),
        ],
        out_specs=[out[1] for out in outs],
        scratch_shapes=[
            pltpu.VMEM((rows, WIDE), F32),
            pltpu.VMEM((rows, Q), F32),
            pltpu.VMEM((6, 8, rows), F32),
            pltpu.VMEM((4, rows, LANES), F32),
            pltpu.VMEM((rows, WIDE), F32),
            pltpu.VMEM((GROUPS, NSTATE, WIDE), F32),
            pltpu.VMEM((GROUPS, 8, WIDE), F32),
            pltpu.VMEM((GROUPS, NSTATE, WIDE), LOW),
            pltpu.VMEM((GROUPS + 1, EDGE, WIDE), F32),
            pltpu.VMEM((GROUPS + 2, EDGE, WIDE), F32),
            pltpu.VMEM((rows, WIDE), F32),
            pltpu.VMEM((rows, model), F32),
            sem(GROUPS + 1),
            sem(GROUPS + 1),
            sem(BLOCK_CUTS),
            sem(BLOCK_CUTS),
            sem(1),
        ]
        + Chaining.scratch(rounds)
        + Reducing.scratch(depth, own_rows, 2 * half_wide),
        compiler_params=params(collective_id=2, has_side_effects=True),
        name="scan_back",
    )(
        pre, dy, loc, carry, enter, cin, par, par_heads, state_filter, cin_state, pre_state, bc,
        bct, score, mask, sp, cumt, fac, match, zst, dt, exits, gate_part, block_own, tokens, cot,
        hidden_t, gpg, parts, parts, small,
    )


def pack_body(
    side_ref, entry, exits, state, steps, gain, inner_kernel, gate_gain, bias, decay, skip, docs,
    tail_tokens, packed_small, packed_parts, packed_exit, par, doc_col, doc_row, edge, docs_own
):
    side = side_ref[0]
    rows = entry.shape[0]
    wide = entry.shape[2]

    def placed(value):
        filled = jnp.concatenate(
            [value, jnp.zeros((value.shape[0], LANES - value.shape[1]), F32)], axis=1
        )
        return jnp.where(side == 0, filled, pltpu.roll(filled, value.shape[1], 1))

    for part in range(3):
        at = slice(part * WIDE, (part + 1) * WIDE)
        packed_parts[part, :, :WIDE] = entry[:, 0, at].astype(LOW)
        packed_parts[part, :, WIDE:] = entry[:, 1, at].astype(LOW)
    half = jnp.where(side == 0, state[:, :NSTATE], state[:, NSTATE:])
    packed_small[:, :NSTATE] = half.astype(LOW)
    gain_row = jnp.concatenate([gain[...], jnp.zeros((1, LANES - rows), F32)], axis=1)
    gain_col = jnp.transpose(jnp.broadcast_to(gain_row, (LANES, LANES)))[:rows]
    lane = iota((rows, LANES), 1)
    small = jnp.where(lane == 24, gain_col, placed(steps[...]))
    packed_small[:, NSTATE:] = small.astype(LOW)
    packed_exit[...] = exits[...].astype(LOW)
    par[0 : CONV + 1] = inner_kernel[...]
    par[CONV + 1 : CONV + 2] = gate_gain[...]
    par[CONV + 2 : CONV + 4] = jnp.zeros((2, wide), F32)
    for index, ref in enumerate((bias, decay, skip)):
        par[CONV + 2 : CONV + 3, index * LANES : (index + 1) * LANES] = placed(ref[...])
    own = jnp.where(side == 0, docs[0:1], docs[1:2]).astype(F32)
    doc_row[...] = jnp.broadcast_to(own, doc_row.shape)
    doc_col[...] = jnp.transpose(jnp.broadcast_to(own, (LANES, own.shape[1])))
    docs_own[...] = doc_col[own.shape[1] - HALO :]
    edge[...] = tail_tokens[0]


def pack(
    which, entry, exits, state, steps, gain, inner_kernel, gate_gain, bias, decay, skip, docs, tokens
):
    own_rows, _, wide = entry.shape
    rows, model = tokens.shape[1:]
    shape = jax.ShapeDtypeStruct
    arrays = (
        entry, exits, state, steps, gain[None], inner_kernel, gate_gain[None], bias[None],
        decay[None], skip[None], docs,
    )
    outs = (
        shape((own_rows, WIDE), LOW),
        shape((3, own_rows, 2 * WIDE), LOW),
        shape((own_rows, wide), LOW),
        shape((8, wide), F32),
        shape((rows, LANES), F32),
        shape((8, rows), F32),
        shape((HALO, model), LOW),
        shape((HALO, LANES), F32),
    )
    return pl.pallas_call(
        pack_body,
        out_shape=outs,
        grid_spec=pltpu.PrefetchScalarGridSpec(
            num_scalar_prefetch=1,
            grid=(1,),
            in_specs=[const(array.shape) for array in arrays]
            + [pl.BlockSpec((1, HALO, model), lambda s, w: (w[0], rows // HALO - 1, 0))],
            out_specs=[const(out.shape) for out in outs],
        ),
        compiler_params=params(),
        name="pack",
    )(which, *arrays, tokens)


def gather_body(
    depth, own_small, own_parts, own_exit, par_own, edge_own, docs_own, cot, small, parts, exits, par,
    heads, edge, docs, cot_t, docs_in, cot_in, side_send, side_land, local, *marks
):
    place = Place(depth)
    count = 2 * depth
    onward = {"context": lax.rem(place.position + 1, count)}
    behind = {"context": lax.rem(place.position + count - 1, count)}
    y, z = place.y, place.z
    place.greet(
        [place.mate, place.x_peer, place.y_peer, onward, behind],
        [(z + 1 < depth, place.up()), (z > 0, place.down())],
    )
    own = [own_small, own_parts.at[0], own_parts.at[1], own_parts.at[2], own_exit]
    full = [small, parts.at[0], parts.at[1], parts.at[2], exits]
    pieces = [Gathering(place, own[i], full[i], *marks[3 * i : 3 * i + 3]) for i in range(5)]
    sides = [
        remote(edge_own, edge, side_send.at[0], side_land.at[0], onward),
        remote(docs_own, docs_in, side_send.at[1], side_land.at[1], onward),
        remote(par_own, par.at[y], side_send.at[2], side_land.at[2], place.y_peer),
    ]
    for copy in sides:
        copy.start()
    cot_copy = pltpu.make_async_copy(cot.at[y], cot_in, local.at[1])
    cot_copy.start()
    par_keep = pltpu.make_async_copy(par_own, par.at[y], local.at[0])
    par_keep.start()
    for piece in pieces:
        piece.own()
    cot_copy.wait()
    cot_t[...] = jnp.transpose(cot_in[...])
    for piece in pieces:
        piece.near()
        piece.across()
        piece.far()
    for copy in sides:
        copy.wait()
    docs[...] = jnp.where(place.position == 0, -1.0, docs_in[...])
    par_keep.wait()
    both = par[0, CONV + 2 : CONV + 3] + par[1, CONV + 2 : CONV + 3]
    heads[...] = jnp.zeros_like(heads)
    for index in range(3):
        heads[index : index + 1] = both[:, index * LANES : (index + 1) * LANES]
    for piece in pieces:
        piece.mates()
        piece.finish()


def gather(own_small, own_parts, own_exit, par_own, edge_own, docs_own, cot):
    count = lax.axis_size("context")
    depth = count // 2
    rows, model = cot.shape[1:]
    shape = jax.ShapeDtypeStruct
    full = lambda own: (2, 2, count) + own.shape[-2:]
    return pl.pallas_call(
        functools.partial(gather_body, depth),
        out_shape=(
            shape(full(own_small), LOW),
            shape((3,) + full(own_parts), LOW),
            shape(full(own_exit), LOW),
            shape((2,) + par_own.shape, F32),
            shape((8, LANES), F32),
            shape(edge_own.shape, LOW),
            shape(docs_own.shape, F32),
            shape((model, rows), LOW),
        ),
        in_specs=[VMEM_SPEC] * 6 + [ANY_SPEC],
        out_specs=[ANY_SPEC] * 3 + [VMEM_SPEC] * 5,
        scratch_shapes=[
            pltpu.VMEM(docs_own.shape, F32),
            pltpu.VMEM((rows, model), LOW),
            pltpu.SemaphoreType.DMA((3,)),
            pltpu.SemaphoreType.DMA((3,)),
            pltpu.SemaphoreType.DMA((2,)),
        ]
        + Gathering.scratch(depth) * 5,
        compiler_params=params(collective_id=0, has_side_effects=True),
        name="gather",
    )(own_small, own_parts, own_exit, par_own, edge_own, docs_own, cot)


def reduce_body(
    depth, inner, small, token, taps, taps_state, gate_row, head_rows, skip_row, norm_row,
    total, state_out, vector_out, token_out, state_own, vec_send, vec_land, vs, vl, ts, tl, ss, sl,
    keep_sem, *scratch
):
    place = Place(depth)
    x, y, z, c = place.x, place.y, place.z, place.c
    wide = inner.shape[-1]
    parts = [(inner, slice(0, wide)), (small, slice(wide, wide + WIDE))]
    reducing = Reducing(place, 0, parts, total, scratch[:8], scratch[8:])

    vec_send[0] = jnp.zeros(vec_send.shape[1:], F32)
    vec_send[0, : CONV + 1, : 2 * wide] = taps[: CONV + 1]
    vec_send[0, : CONV + 1, 2 * wide :] = taps_state[: CONV + 1]
    vec_send[0, 5:6, : 2 * wide] = gate_row[0:1]
    vec_send[0, 5:6, 2 * wide : 2 * wide + LANES] = head_rows[0:1]
    vec_send[0, 5:6, 2 * wide + LANES :] = skip_row[0:1]
    model = norm_row.shape[1]
    vec_send[0, 6:7, :model] = norm_row[0:1]
    vec_send[0, 6:7, model : model + LANES] = head_rows[1:2]

    place.greet([place.mate, place.x_peer, place.y_peer], (), True)
    vec_targets = [place.mate, place.x_peer, place.y_peer]

    def vec_copy(turn):
        return remote(
            vec_send.at[turn], vec_land.at[turn], vs.at[turn], vl.at[turn], vec_targets[turn]
        )

    def vec_far(away, lands_at):
        return remote(
            vec_send.at[3], vec_land.at[3 + lands_at], vs.at[3 + away], vl.at[3 + lands_at],
            place.away(away),
        )

    share = token.shape[0] // depth

    def token_copy(step):
        at = pl.ds(pl.multiple_of(step * share, share), share)
        return remote(token.at[at], token_out.at[y, at], ts.at[step], tl.at[step], place.y_peer)

    token_keep = pltpu.make_async_copy(token, token_out.at[y], keep_sem.at[0])

    vec_copy(0).start()
    each(depth, reducing.start)
    token_keep.start()

    def step_all(step):
        reducing.turn(step)

        @pl.when(step < depth)
        def _():
            token_copy(step).start()

        for turn in range(3):

            @pl.when(step == turn)
            def _():
                vec_copy(turn).wait_recv()
                vec_send[turn + 1] = vec_send[turn] + vec_land[turn]
                if turn < 2:
                    vec_copy(turn + 1).start()
                else:
                    each(depth, lambda s: vec_far(lax.rem(z + s, depth), z).start(), 1)
                    vec_land[3 + z] = vec_send[3]

    each(depth + 1, step_all)
    reducing.close()
    state_own[...] = total[:, wide : wide + NSTATE]
    state_copy = remote(state_own, state_out.at[y], ss.at[0], sl.at[0], place.y_peer)
    state_copy.start()
    state_out[y] = state_own[...]

    def vec_arrive(step):
        away = lax.rem(z + step, depth)
        vec_far(away, away).wait_recv()

    each(depth, vec_arrive, 1)
    vector_out[...] = vec_land[3]

    def vec_add(step):
        vector_out[...] += vec_land[3 + step]

    each(depth, vec_add, 1)
    for turn in range(3):
        vec_copy(turn).wait_send()
    each(depth, lambda s: vec_far(lax.rem(z + s, depth), z).wait_send(), 1)
    reducing.finish()
    each(depth, lambda step: token_copy(step).wait())
    state_copy.wait()
    token_keep.wait()


def reduce_all(inner, small, token, taps, taps_state, gate_row, head_rows, skip_row, norm_row):
    count = lax.axis_size("context")
    depth = count // 2
    own_rows, wide = inner.shape[3:]
    tall = wide + WIDE
    shape = jax.ShapeDtypeStruct
    sem = lambda *lead: pltpu.SemaphoreType.DMA(lead)
    vector = (8, 2 * wide + WIDE)
    return pl.pallas_call(
        functools.partial(reduce_body, depth),
        out_shape=(
            shape((own_rows, tall), F32),
            shape((2, own_rows, NSTATE), F32),
            shape(vector, F32),
            shape((2,) + token.shape, LOW),
        ),
        in_specs=[ANY_SPEC] * 2 + [VMEM_SPEC] * 7,
        out_specs=[VMEM_SPEC] * 3 + [ANY_SPEC],
        scratch_shapes=[
            pltpu.VMEM((own_rows, NSTATE), F32),
            pltpu.VMEM((4,) + vector, F32),
            pltpu.VMEM((3 + depth,) + vector, F32),
            sem(3 + depth),
            sem(3 + depth),
            sem(depth),
            sem(depth),
            sem(1),
            sem(1),
            sem(1),
        ]
        + Reducing.scratch(depth, own_rows, tall),
        compiler_params=params(collective_id=4, has_side_effects=True),
        name="reduce_all",
    )(inner, small, token, taps, taps_state, gate_row, head_rows, skip_row, norm_row)


def finish_body(
    side_ref, mine, exits, state, vector, token, block, block_out, token_out,
    norm_out, entry_out, state_out, step_out, kernel_out, filter_out, bias_out, decay_out, skip_out,
    gate_out, exit_out
):
    side, spot = side_ref[0], side_ref[1]
    token_out[...] = token[...].astype(F32)
    first = side == 0
    block_out[...] = block[...]

    @pl.when(pl.program_id(0) == 0)
    def _():
        own_rows, _, wide = entry_out.shape
        model = token.shape[2]
        entry_out[:, 0] = exits[:, wide:]
        entry_out[:, 1] = mine[:, :wide]
        exit_out[...] = exits[:, :wide]
        state_out[:, :NSTATE] = state[0]
        state_out[:, NSTATE:] = state[1]

        def twelve(value):
            return jnp.where(first, value, pltpu.roll(value, LANES - 12, 1))[:, :12]

        step_out[...] = twelve(mine[:, wide + NSTATE :])
        left, right = vector[:, :wide], vector[:, wide : 2 * wide]
        halves = jnp.where(first, left, right)
        kernel_out[...] = halves[: CONV + 1]
        gate_out[...] = halves[5:6]
        filter_out[...] = vector[: CONV + 1, 2 * wide :]
        bias_out[...] = twelve(vector[5:6, 2 * wide : 2 * wide + LANES])
        skip_out[...] = twelve(vector[5:6, 2 * wide + LANES :])
        decay_out[...] = twelve(vector[6:7, model : model + LANES])
        turned = pltpu.roll(vector[:, :model], lax.rem(model - spot * own_rows, model), 1)
        norm_out[...] = turned[6:7, :own_rows]


def finish(side, mine, exits, state, vector, token, block):
    own_rows, wide = exits.shape[0], exits.shape[1] // 2
    _, rows, model = token.shape
    share = rows // 4
    shape = jax.ShapeDtypeStruct
    outs = (
        (shape((2, rows, model), LOW), pl.BlockSpec((2, share, model), lambda s, w: (0, s, 0))),
        (shape((2, rows, model), F32), pl.BlockSpec((2, share, model), lambda s, w: (0, s, 0))),
        (shape((1, own_rows), F32), None),
        (shape((own_rows, 2, wide), F32), None),
        (shape((own_rows, WIDE), F32), None),
        (shape((own_rows, 12), F32), None),
        (shape((CONV + 1, wide), F32), None),
        (shape((CONV + 1, WIDE), F32), None),
        (shape((1, 12), F32), None),
        (shape((1, 12), F32), None),
        (shape((1, 12), F32), None),
        (shape((1, wide), F32), None),
        (shape((own_rows, wide), F32), None),
    )
    return pl.pallas_call(
        finish_body,
        out_shape=[out[0] for out in outs],
        grid_spec=pltpu.PrefetchScalarGridSpec(
            num_scalar_prefetch=1,
            grid=(4,),
            in_specs=[
                const(mine.shape),
                const(exits.shape),
                const(state.shape),
                const(vector.shape),
                pl.BlockSpec((2, share, model), lambda s, w: (0, s, 0)),
                pl.BlockSpec((2, share, model), lambda s, w: (0, s, 0)),
            ],
            out_specs=[out[1] if out[1] is not None else const(out[0].shape) for out in outs],
        ),
        compiler_params=params(),
        name="finish",
    )(side, mine, exits, state, vector, token, block)


def body(
    tokens, documents, norm_gain, entry_weight, state_weight, step_weight, inner_kernel,
    state_filter, step_bias, decay_log, skip_gain, gate_gain, exit_weight, cotangent,
):
    seqs, rows, model = tokens.shape
    count = lax.axis_size("context")
    position, side = lax.axis_index("context"), lax.axis_index("tensor")
    own_rows = norm_gain.shape[0]
    which = jnp.stack([side, lax.axis_index("dp") * count + position]).astype(jnp.int32)
    longest = rows * count // 4
    rounds = min(count // 2 - 1, -(-(longest - 1) // (2 * rows)))

    own_small, own_parts, own_exit, own_par, doc_col, doc_row, own_edge, own_docs = pack(
        which, entry_weight, exit_weight, state_weight, step_weight, norm_gain, inner_kernel,
        gate_gain, step_bias, decay_log, skip_gain, documents, tokens,
    )
    packs = (own_small, own_parts, own_exit, own_par, own_edge, own_docs)
    (
        hidden_t, cin, gate, pre, loc, carry, cin_state, pre_state, bc, bct, score, mask, zst, dt, sp,
        cumt, fac, match,
    ), (small, parts, exit_weights, par, par_heads, cot_t) = entry(
        tokens, doc_col, doc_row, state_filter, packs, cotangent, rounds
    )
    block_own, exit_part, gate_part, dy, gpg, enter, gate_row, skip_row = middle(
        tokens, cotangent, cot_t, hidden_t, pre, gate, loc, carry, exit_weights, par, par_heads, bc,
        bct, score, mask, sp, cumt, fac,
    )
    cut = lambda v: v.reshape(2, 2, count, own_rows, v.shape[-1])
    (
        taps, taps_state, head_rows, exit_mine, block_both, inner_part, small_part, token_own,
        norm_row,
    ) = scan_back(
        pre, dy, loc, carry, enter, cin, par, par_heads, state_filter, cin_state, pre_state, bc, bct,
        score, mask, sp, cumt, fac, match, zst, dt, cut(exit_part), cut(gate_part), block_own,
        tokens, cotangent, hidden_t, gpg, parts, small, rounds,
    )
    mine, state_both, vector, token_both = reduce_all(
        cut(inner_part), cut(small_part), token_own, taps, taps_state, gate_row, head_rows, skip_row,
        norm_row,
    )
    outs = finish(which, mine, exit_mine, state_both, vector, token_both, block_both)
    flat = (2, 8, 9, 10, 11)
    return tuple(out[0] if index in flat else out for index, out in enumerate(outs))


def solution(mesh):
    in_specs = (
        P("dp", "context", None),
        P("dp", "context"),
        P(("dp", "context")),
        P(("dp", "context"), None, "tensor"),
        P(("dp", "context"), None),
        P(("dp", "context"), "tensor"),
        P(None, "tensor"),
        P(),
        P("tensor"),
        P("tensor"),
        P("tensor"),
        P("tensor"),
        P(("dp", "context"), "tensor"),
        P("dp", "context", None),
    )
    out_specs = (
        P("dp", "context", None),
        P("dp", "context", None),
        P(("dp", "context")),
        P(("dp", "context"), None, "tensor"),
        P(("dp", "context"), None),
        P(("dp", "context"), "tensor"),
        P(None, "tensor"),
        P(),
        P("tensor"),
        P("tensor"),
        P("tensor"),
        P("tensor"),
        P(("dp", "context"), "tensor"),
    )
    return jax.shard_map(body, mesh=mesh, in_specs=in_specs, out_specs=out_specs, check_vma=False)
```

```python
import functools
import jax
import jax.numpy as jnp
from jax import lax
from jax.experimental import pallas as pl
from jax.experimental.pallas import tpu as pltpu
from jax.sharding import PartitionSpec as P

HEAD = 64
NSTATE = 128
CONV = 4
EPSILON = 1e-05
Q = 128
HALO = 16
EDGE = 8
GROUPS = 6
BLOCK_CUTS = 8
ORDER = (0, 3, 1, 4, 2, 5)
LANES = 128
WIDE = 256
LOG2E = 1.4426950408889634
FAR = -1e30
LOW = jnp.bfloat16
F32 = jnp.float32
VMEM_LIMIT = 60 * 1024 * 1024


def mm(a, b):
    return lax.dot_general(a, b, (((1,), (0,)), ((), ())), preferred_element_type=F32)


def mm_nt(a, b):
    return lax.dot_general(a, b, (((1,), (1,)), ((), ())), preferred_element_type=F32)


def mm_tn(a, b):
    return lax.dot_general(a, b, (((0,), (0,)), ((), ())), preferred_element_type=F32)


def mm_exact(a, b):
    return lax.dot_general(
        a, b, (((1,), (0,)), ((), ())), precision=lax.Precision.HIGHEST, preferred_element_type=F32
    )


def split3(v):
    high = v.astype(LOW).astype(F32)
    rest = v - high
    mid = rest.astype(LOW).astype(F32)
    low = rest - mid
    return (high + pltpu.roll(mid, 32, 1) + pltpu.roll(low, 64, 1)).astype(LOW)


def iota(shape, dim):
    return lax.broadcasted_iota(jnp.int32, shape, dim)


def spreader(first_head, width, count):
    k = iota((LANES, width * count), 0)
    lane = iota((LANES, width * count), 1)
    hit = ((k & 31) == first_head + lane // width) & (k < 96)
    return hit.astype(F32).astype(LOW)


def gatherer(first_head, width, count):
    lane = iota((width * count, LANES), 0)
    k = iota((width * count, LANES), 1)
    return (k == first_head + lane // width).astype(F32).astype(LOW)


def head_sums(v, collect):
    high = v.astype(LOW)
    rest = (v - high.astype(F32)).astype(LOW)
    return mm(high, collect) + mm(rest, collect)


def sigmoid(v):
    return 1.0 / (1.0 + jnp.exp(-v))


def twice(v):
    return jnp.concatenate([v, v], axis=1)


def conv_forward(cin, taps, masks):
    rows = cin.shape[0] - HALO
    out = taps[CONV : CONV + 1] + taps[CONV - 1 : CONV] * cin[HALO:]
    for back in range(1, CONV):
        part = cin[HALO - back : HALO - back + rows]
        out = out + taps[CONV - 1 - back : CONV - back] * (part * twice(masks[back - 1]))
    return out


def conv_backward(pg, cin, taps, masks):
    rows, width = pg.shape
    sums = [None] * (CONV + 1)
    sums[CONV] = jnp.sum(pg, axis=0, keepdims=True)
    sums[CONV - 1] = jnp.sum(pg * cin[HALO:], axis=0, keepdims=True)
    pad = jnp.zeros((HALO, width), F32)
    grad = jnp.concatenate([pad, pg * taps[CONV - 1 : CONV]], axis=0)
    for back in range(1, CONV):
        masked = pg * twice(masks[back - 1])
        part = cin[HALO - back : HALO - back + rows]
        sums[CONV - 1 - back] = jnp.sum(masked * part, axis=0, keepdims=True)
        padded = jnp.concatenate([pad, masked * taps[CONV - 1 - back : CONV - back], pad], axis=0)
        grad = grad + padded[back : back + rows + HALO]
    return sums, grad


def const(shape):
    zeros = (0,) * len(shape)
    return pl.BlockSpec(shape, lambda *_: zeros)


def params(**extra):
    return pltpu.CompilerParams(vmem_limit_bytes=VMEM_LIMIT, **extra)


VMEM_SPEC = pl.BlockSpec(memory_space=pltpu.VMEM)
ANY_SPEC = pl.BlockSpec(memory_space=pl.ANY)


def side():
    return lax.axis_index("tensor")


def remote(src, dst, send_sem, recv_sem, target):
    return pltpu.make_async_remote_copy(
        src_ref=src,
        dst_ref=dst,
        send_sem=send_sem,
        recv_sem=recv_sem,
        device_id=target,
        device_id_type=pl.DeviceIdType.MESH,
    )


def each(count, run, first=0):
    def one(step, carry):
        run(step)
        return carry

    lax.fori_loop(first, count, one, 0)


class Place:
    def __init__(self, depth):
        position = lax.axis_index("context")
        self.depth = depth
        self.position = position
        self.x, self.y = lax.axis_index("dp"), lax.axis_index("tensor")
        self.z, self.c = position // 2, position % 2
        self.mate = self.at(self.x, self.y, self.z, 1 - self.c)
        self.x_peer = self.at(1 - self.x, self.y, self.z, self.c)
        self.y_peer = self.at(self.x, 1 - self.y, self.z, self.c)

    def at(self, x, y, z, c):
        return {"dp": x, "context": z * 2 + c, "tensor": y}

    def away(self, z):
        return self.at(self.x, self.y, z, self.c)

    def axes(self, turned):
        x, y, z, c = self.x, self.y, self.z, self.c
        x1, y1 = x + (1 - turned) * (1 - 2 * x), y + turned * (1 - 2 * y)
        x2, y2 = x + turned * (1 - 2 * x), y + (1 - turned) * (1 - 2 * y)
        return (x1, y1), (x2, y2)

    def around(self, run, first=0, last=None):
        z, depth = self.z, self.depth
        if first == 0:
            run(z)

        def step(away):
            @pl.when(z - away >= 0)
            def _():
                run(z - away)

            @pl.when(z + away < depth)
            def _():
                run(z + away)

        each(depth if last is None else last, step, max(first, 1))

    def greet(self, always, sometimes=(), column=False):
        barrier = pltpu.get_barrier_semaphore()
        kind = pl.DeviceIdType.MESH
        total = len(always)
        for target in always:
            pl.semaphore_signal(barrier, inc=1, device_id=target, device_id_type=kind)
        for holds, target in sometimes:

            @pl.when(holds)
            def _():
                pl.semaphore_signal(barrier, inc=1, device_id=target, device_id_type=kind)

            total = total + holds.astype(jnp.int32)
        if column:
            for_all = lambda step: pl.semaphore_signal(
                barrier,
                inc=1,
                device_id=self.away(lax.rem(self.z + step, self.depth)),
                device_id_type=kind,
            )
            each(self.depth, for_all, 1)
            total = total + (self.depth - 1)
        pl.semaphore_wait(barrier, total)


class Gathering:
    def __init__(self, place, own, full, sends, lands, local):
        self.place, self.own_ref, self.full = place, own, full
        self.sends, self.lands, self.local = sends, lands, local
        self.starts = [first * place.depth for first in (0, 4, 5, 7)]
        (self.x1, self.y1), (self.x2, self.y2) = place.axes(place.c)
        self.first = place.at(self.x1, self.y1, place.z, place.c)
        self.second = place.at(self.x2, self.y2, place.z, place.c)

    @staticmethod
    def scratch(depth):
        sem = pltpu.SemaphoreType.DMA
        return [sem((8 * depth,)), sem((8 * depth,)), sem((1,))]

    def copy(self, kind, index, x, y, z, c, target, own=False):
        chunk = self.full.at[y, x, z * 2 + c]
        mark = ((y * 2 + x) * self.place.depth + z) * 2 + c
        return remote(
            self.own_ref if own else chunk, chunk, self.sends.at[self.starts[kind] + index],
            self.lands.at[mark], target,
        )

    def arrive(self, x, y, z, c):
        self.copy(0, 0, x, y, z, c, self.place.mate).wait_recv()

    def kept(self):
        p = self.place
        return pltpu.make_async_copy(
            self.own_ref, self.full.at[p.y, p.x, p.z * 2 + p.c], self.local.at[0]
        )

    def own(self):
        p = self.place
        mine = (p.x, p.y, p.z, p.c)

        def far_z(z):
            self.copy(3, z, *mine, p.away(z), True).start()

        p.around(far_z, 1)
        self.copy(1, p.z, *mine, self.first, True).start()
        self.copy(2, p.z, *mine, self.second, True).start()
        self.copy(0, p.z, *mine, p.mate, True).start()
        self.kept().start()

    def near(self, first=1, last=None):
        p = self.place

        def run(z):
            chunk = (p.x, p.y, z, p.c)
            self.arrive(*chunk)

            self.copy(1, z, *chunk, self.first).start()
            self.copy(2, z, *chunk, self.second).start()
            self.copy(0, z, *chunk, p.mate).start()

        p.around(run, first, last)

    def across(self):
        p = self.place

        def run(z):
            chunk = (self.x1, self.y1, z, p.c)
            self.arrive(*chunk)
            self.copy(2, p.depth + z, *chunk, self.second).start()
            self.copy(0, p.depth + z, *chunk, p.mate).start()

        p.around(run)

    def far(self):
        p = self.place

        def near_row(z):
            self.arrive(self.x2, self.y2, z, p.c)
            self.copy(0, 2 * p.depth + z, self.x2, self.y2, z, p.c, p.mate).start()

        def far_row(z):
            self.arrive(1 - p.x, 1 - p.y, z, p.c)
            self.copy(0, 3 * p.depth + z, 1 - p.x, 1 - p.y, z, p.c, p.mate).start()

        p.around(near_row)
        p.around(far_row)

    def mates(self):
        p = self.place

        def from_mate(z):
            for y in range(2):
                for x in range(2):
                    self.arrive(x, y, z, 1 - p.c)

        each(p.depth, from_mate)
        self.kept().wait()

    def finish(self):
        p = self.place

        def sent(kind, index, target):
            self.copy(kind, index, p.x, p.y, p.z, p.c, target).wait_send()

        each(4 * p.depth, lambda step: sent(0, step, p.mate))
        each(p.depth, lambda step: sent(1, step, p.mate))
        each(2 * p.depth, lambda step: sent(2, step, p.mate))

        p.around(lambda z: sent(3, z, p.mate), 1)


class Reducing:
    def __init__(self, place, turned, parts, total, bufs, sems):
        self.place, self.parts, self.total = place, parts, total
        self.own, self.core, self.send1, self.land1 = bufs[:4]
        self.send2, self.land2, self.send3, self.land3 = bufs[4:]
        self.own_sem, self.core_send, self.core_land = sems[:3]
        self.s1, self.l1, self.s2, self.l2, self.s3, self.l3 = sems[3:]
        self.turned = turned
        (x1, y1), (x2, y2) = place.axes(turned)
        self.first = place.at(x1, y1, place.z, place.c)
        self.second = place.at(x2, y2, place.z, place.c)
        self.mine = place.y + turned * (place.x - place.y)

    @staticmethod
    def scratch(depth, rows, tall):
        buffer = lambda *lead: pltpu.VMEM(lead + (rows, tall), LOW)
        sem = lambda *lead: pltpu.SemaphoreType.DMA(lead)
        bufs = [
            buffer(2, 2, depth), buffer(2, 2, depth), buffer(depth, 2), buffer(depth, 2),
            buffer(depth), buffer(depth), buffer(depth), buffer(depth),
        ]
        return bufs + [sem(2, 2, depth)] * 3 + [sem(depth)] * 6

    def spot(self, step):
        return lax.rem(self.place.z + 1 + step, self.place.depth)

    def whole(self, y, x, z):
        return remote(
            self.core.at[y, x, z], self.core.at[y, x, z], self.core_send.at[y, x, z],
            self.core_land.at[y, x, z], self.place.mate,
        )

    def own_whole(self, y, x, z):
        return pltpu.make_async_copy(
            self.own.at[y, x, z], self.own.at[y, x, z], self.own_sem.at[y, x, z]
        )

    def start(self, step):
        p = self.place
        z = self.spot(step)
        for y in range(2):
            for x in range(2):
                for ref, cols in self.parts:
                    remote(
                        ref.at[y, x, z * 2 + 1 - p.c], self.core.at[y, x, z, :, cols],
                        self.core_send.at[y, x, z], self.core_land.at[y, x, z], p.mate,
                    ).start()
                    pltpu.make_async_copy(
                        ref.at[y, x, z * 2 + p.c], self.own.at[y, x, z, :, cols],
                        self.own_sem.at[y, x, z],
                    ).start()

    def base(self, y, x, z):
        return self.own[y, x, z].astype(F32) + self.core[y, x, z].astype(F32)

    def copy1(self, z):
        return remote(
            self.send1.at[z], self.land1.at[z], self.s1.at[z], self.l1.at[z], self.first
        )

    def copy2(self, z):
        return remote(
            self.send2.at[z], self.land2.at[z], self.s2.at[z], self.l2.at[z], self.second
        )

    def copy3(self, z, lands_at):
        return remote(
            self.send3.at[z], self.land3.at[lands_at], self.s3.at[z], self.l3.at[lands_at],
            self.place.away(z),
        )

    def stage1(self, step):
        p, turned = self.place, self.turned
        z = self.spot(step)
        for y in range(2):
            for x in range(2):
                self.whole(y, x, z).wait_recv()
                self.own_whole(y, x, z).wait()
        for index in range(2):
            x = (1 - turned) * (1 - p.x) + turned * index
            y = turned * (1 - p.y) + (1 - turned) * index
            self.send1[z, index] = self.base(y, x, z).astype(LOW)
        self.copy1(z).start()

    def stage2(self, step):
        p, turned = self.place, self.turned
        z = self.spot(step)
        self.copy1(z).wait_recv()
        other = 1 - self.mine
        x = (1 - turned) * p.x + turned * other
        y = turned * p.y + (1 - turned) * other
        self.send2[z] = (self.base(y, x, z) + self.land1[z, other].astype(F32)).astype(LOW)
        self.copy2(z).start()

    def final(self, z):
        p = self.place
        self.copy2(z).wait_recv()
        return (
            self.base(p.y, p.x, z)
            + self.land1[z, self.mine].astype(F32)
            + self.land2[z].astype(F32)
        )

    def stage3(self, step):
        z = self.spot(step)
        self.send3[z] = self.final(z).astype(LOW)
        self.copy3(z, self.place.z).start()

    def turn(self, step):
        depth = self.place.depth

        @pl.when(step < depth)
        def _():
            self.stage1(step)

        @pl.when((step >= 1) & (step <= depth))
        def _():
            self.stage2(step - 1)

        @pl.when((step >= 2) & (step <= depth))
        def _():
            self.stage3(step - 2)

    def close(self):
        p = self.place
        self.total[...] = self.final(p.z)

        def add(step):
            z = lax.rem(p.z + step, p.depth)
            self.copy3(z, z).wait_recv()
            self.total[...] += self.land3[z].astype(F32)

        each(p.depth, add, 1)

    def finish(self):
        p = self.place

        def sent(z):
            for y in range(2):
                for x in range(2):
                    self.whole(y, x, z).wait_send()
            self.copy1(z).wait_send()
            self.copy2(z).wait_send()

        each(p.depth, sent)
        each(p.depth, lambda step: self.copy3(lax.rem(p.z + step, p.depth), p.z).wait_send(), 1)


class Chaining:
    def __init__(self, place, rounds, backward, fold, gain, bufs, sems):
        self.place, self.rounds = place, rounds
        self.fold, self.gain = fold, gain
        self.from_mate, self.from_chip, self.to_mate, self.to_chip = bufs
        self.mate_send, self.mate_land, self.chip_send, self.chip_land = sems
        first = 1 if backward else 0
        by = -1 if backward else 1
        self.order = place.depth - 1 - place.z if backward else place.z
        self.leads = place.c == first
        self.after = place.at(place.x, place.y, place.z + by, first)
        self.before = place.at(place.x, place.y, place.z - by, 1 - first)
        self.linked_before = self.leads & (self.order > 0)
        self.linked_after = jnp.logical_not(self.leads) & (self.order < place.depth - 1)

    @staticmethod
    def scratch(rounds):
        slots = lambda turns: pltpu.VMEM((turns, GROUPS, NSTATE, WIDE), LOW)
        marks = lambda turns: pltpu.SemaphoreType.DMA((turns, GROUPS))
        return [
            slots(rounds + 1), slots(rounds), slots(rounds + 1), slots(rounds),
            marks(rounds + 1), marks(rounds + 1), marks(rounds), marks(rounds),
        ]

    def sometimes(self):
        return [(self.linked_before, self.before), (self.linked_after, self.after)]

    def mate_copy(self, turn, cut):
        return remote(
            self.to_mate.at[turn, cut], self.from_mate.at[turn, cut], self.mate_send.at[turn, cut],
            self.mate_land.at[turn, cut], self.place.mate,
        )

    def chip_copy(self, turn, cut):
        return remote(
            self.to_chip.at[turn, cut], self.from_chip.at[turn, cut], self.chip_send.at[turn, cut],
            self.chip_land.at[turn, cut], self.after,
        )

    def joined(self, cut, arrived):
        return (self.fold[cut] + self.gain[cut, 0:1] * arrived.astype(F32)).astype(LOW)

    def open(self, cut):
        @pl.when(self.leads)
        def _():
            self.to_mate[0, cut] = self.fold[cut].astype(LOW)
            self.mate_copy(0, cut).start()

    def pass_on(self, turn, cut):
        @pl.when(jnp.logical_not(self.leads))
        def _():
            self.mate_copy(turn, cut).wait_recv()

        @pl.when(self.linked_after)
        def _():
            self.to_chip[turn, cut] = self.joined(cut, self.from_mate[turn, cut])
            self.chip_copy(turn, cut).start()

    def relay(self, turn, cut):
        @pl.when(self.linked_before)
        def _():
            self.chip_copy(turn, cut).wait_recv()
            self.to_mate[turn + 1, cut] = self.joined(cut, self.from_chip[turn, cut])
            self.mate_copy(turn + 1, cut).start()

        @pl.when(self.leads & (self.order == 0))
        def _():
            self.to_mate[turn + 1, cut] = self.fold[cut].astype(LOW)
            self.mate_copy(turn + 1, cut).start()

    def later(self):
        for turn in range(1, self.rounds):
            for cut in range(GROUPS):
                self.pass_on(turn, cut)
            for cut in range(GROUPS):
                self.relay(turn, cut)

    def arrive(self, put):
        last = self.rounds - 1

        @pl.when(self.linked_before)
        def _():
            for cut in range(GROUPS):
                put(cut, self.from_chip[last, cut])

        @pl.when(self.leads & (self.order == 0))
        def _():
            for cut in range(GROUPS):
                put(cut, jnp.zeros((NSTATE, WIDE), LOW))

        @pl.when(jnp.logical_not(self.leads))
        def _():
            for cut in range(GROUPS):
                self.mate_copy(self.rounds, cut).wait_recv()
                put(cut, self.from_mate[self.rounds, cut])

    def finish(self):
        @pl.when(self.leads)
        def _():
            for turn in range(self.rounds + 1):
                for cut in range(GROUPS):
                    self.mate_copy(turn, cut).wait_send()

        @pl.when(self.linked_after)
        def _():
            for turn in range(self.rounds):
                for cut in range(GROUPS):
                    self.chip_copy(turn, cut).wait_send()


def turn_of(step):
    index = jnp.maximum(step - 1, 0)
    half, part = index % 2, index // 2
    return half * 3 + part, half, part


def entry_body(depth, rounds, fused, *refs):
    step = pl.program_id(0)
    tokens, doc_col, doc_row, state_filter = refs[:4]
    if fused:
        own_small, own_parts, own_exit, own_par, own_edge, own_docs, cot = refs[4:11]
    else:
        w_gate, w_inner, w_small, par, heads_ref, edge, halo_docs = refs[4:11]
    (
        hidden_out, cin_out, gate_out, pre_out, loc_out, carry_out, cin_state_out, pre_state_out,
        bc_out, bct_out, score_out, mask_out, zst_out, dt_out, sp_out, cumt_out, fac_out, match_out,
    ) = refs[11:29]
    refs = refs[29:]
    if fused:
        small_out, parts_out, exit_out, par, heads_ref, cot_t = refs[:6]
        refs = refs[6:]
    hidden, normed, sp_tail, facs, folds, gains = refs[:6]
    rows, model = tokens.shape[1:]
    spans = rows // Q
    place = Place(depth)
    chaining = Chaining(place, rounds, False, folds, gains, refs[6:10], refs[10:14])
    group, half, part = turn_of(step)
    y = place.y
    if fused:
        v_small, v_parts, edge, halo_docs, docs_in, cot_in, par_in = refs[14:21]
        side_send, side_land, local, out_sem = refs[21:25]
        marks = refs[25:]
        own = [own_small, own_parts.at[0], own_parts.at[1], own_parts.at[2], own_exit]
        full = [v_small, v_parts.at[0], v_parts.at[1], v_parts.at[2], exit_out]
        pieces = [
            Gathering(place, own[i], full[i], *marks[3 * i : 3 * i + 3]) for i in range(5)
        ]
        stores = [pltpu.make_async_copy(v_small, small_out, out_sem.at[0])]
        for index in range(3):
            stores.append(
                pltpu.make_async_copy(
                    v_parts.at[index], parts_out.at[index], out_sem.at[index + 1]
                )
            )

    def before_weights():
        for ref, first, count in ((edge, 0, HALO), (tokens, HALO, rows)):
            value = (ref[...] if ref is edge else ref[0]).astype(F32)
            scale = lax.rsqrt(jnp.mean(value * value, axis=1, keepdims=True) + EPSILON)
            normed[first : first + count] = value * scale
        docs = jnp.concatenate([halo_docs[...], doc_col[...]], axis=0)
        for back in range(1, CONV):
            match = (docs[HALO - back : HALO - back + rows] == docs[HALO:]).astype(F32)
            match_out[back - 1] = match
        t_at, u_at = iota((Q, Q), 0), iota((Q, Q), 1)
        for index in range(spans):
            at = slice(index * Q, (index + 1) * Q)
            same = (t_at >= u_at) & (doc_col[at] == doc_row[0:1, at])
            mask_out[at] = jnp.where(same, 0.0, FAR)

    def after_weights(small):
        gain = jnp.transpose(small[0][:, LANES:].astype(F32))[24:25]
        hidden[...] = (normed[...] * gain).astype(LOW)
        hidden_out[...] = jnp.transpose(hidden[HALO:])
        both = [mm(hidden[...], small[index]) for index in range(2)]
        cin = jnp.concatenate([both[0][:, :LANES], both[1][:, :LANES]], axis=1).astype(LOW)
        cin_state_out[...] = cin
        docs = jnp.concatenate([halo_docs[...], doc_col[...]], axis=0)
        masks = [match_out[back] for back in range(CONV - 1)]
        pre = conv_forward(cin.astype(F32), state_filter[...], masks)
        pre_state_out[...] = pre
        mixed = (pre * sigmoid(pre)).astype(LOW)
        bc_out[...] = mixed
        turned = jnp.transpose(mixed.astype(F32)).astype(LOW)
        bct_out[...] = turned
        heads = heads_ref[...]
        used = iota((rows, LANES), 1) < 24
        raw = both[0][HALO:, LANES:] + both[1][HALO:, LANES:]
        zst = jnp.where(used, raw, 0.0) + heads[0:1]
        zst_out[...] = zst
        dt = jnp.where(used, jnp.maximum(zst, 0.0) + jnp.log1p(jnp.exp(-jnp.abs(zst))), 0.0)
        dt_out[...] = dt
        decay = -dt * jnp.exp(heads[1:2])
        t_at, u_at = iota((Q, Q), 0), iota((Q, Q), 1)
        lower = (t_at >= u_at).astype(F32)
        fac_rows = []
        for index in range(spans):
            at = slice(index * Q, (index + 1) * Q)
            cum = mm_exact(lower, decay[at])
            final = cum[Q - 1 : Q]
            before = docs[HALO + index * Q - 1 : HALO + index * Q]
            here = doc_col[at]
            last = here[Q - 1 : Q]
            opened = (here == before).astype(F32)
            tail = (here == last).astype(F32) * jnp.exp(final - cum)
            fac_rows.append((last == before).astype(F32) * jnp.exp(final))
            cum2 = cum * LOG2E
            turned_cum = jnp.transpose(cum2)
            for group in range(6):
                cumt_out[group, 0:4, at] = turned_cum[4 * group : 4 * group + 4]
            sp_out[0, at] = split3(dt[at])
            sp_out[1, at] = split3(cum2)
            lanes_used = iota((Q, LANES), 1) < 24
            sp_out[2, at] = split3(jnp.where(lanes_used, opened * jnp.exp(cum), 0.0))
            sp_out[3, at] = split3(jnp.where(lanes_used, tail, 0.0))
            sp_tail[at] = split3(jnp.where(lanes_used, tail * dt[at], 0.0))
            score_out[at] = mm_nt(mixed[at, LANES:], mixed[at, :LANES])
        gain_total = fac_rows[0]
        for row in fac_rows[1:]:
            gain_total = gain_total * row
        rows8 = jnp.concatenate(
            fac_rows + [gain_total] + [jnp.zeros((1, LANES), F32)] * (7 - spans), axis=0
        )
        rows8 = jnp.where(iota((8, LANES), 1) < 24, rows8, 0.0)
        fac_out[...] = rows8
        facs[...] = split3(rows8)

    if fused:

        @pl.when(step == 0)
        def _():
            count = 2 * depth
            onward = {"context": lax.rem(place.position + 1, count)}
            behind = {"context": lax.rem(place.position + count - 1, count)}
            place.greet(
                [place.mate, place.x_peer, place.y_peer, onward, behind], chaining.sometimes(), True
            )
            sides = [
                remote(own_edge, edge, side_send.at[0], side_land.at[0], onward),
                remote(own_docs, docs_in, side_send.at[1], side_land.at[1], onward),
                remote(own_par, par_in.at[y], side_send.at[2], side_land.at[2], place.y_peer),
            ]
            for copy in sides:
                copy.start()
            for piece in pieces:
                piece.own()
            cot_copy = pltpu.make_async_copy(cot.at[y], cot_in, local.at[0])
            par_keep = pltpu.make_async_copy(own_par, par_in.at[y], local.at[1])
            cot_copy.start()
            par_keep.start()
            for copy in sides:
                copy.wait()
            par_keep.wait()
            pieces[0].near()
            pieces[1].near()
            halo_docs[...] = jnp.where(place.position == 0, -1.0, docs_in[...])
            par[...] = par_in[...]
            both = par[0, CONV + 2 : CONV + 3] + par[1, CONV + 2 : CONV + 3]
            heads_ref[...] = jnp.zeros_like(heads_ref)
            for index in range(3):
                heads_ref[index : index + 1] = both[:, index * LANES : (index + 1) * LANES]
            before_weights()
            pieces[0].across()
            pieces[2].near()
            pieces[1].across()
            pieces[0].far()
            cot_copy.wait()
            cot_t[...] = jnp.transpose(cot_in[...])
            pieces[0].mates()
            stores[0].start()
            after_weights([v_small[index].reshape(model, WIDE) for index in range(2)])

        @pl.when(step == 1)
        def _():
            pieces[3].near()
            pieces[2].across()
            pieces[1].far()
            pieces[1].mates()
            stores[1].start()

        @pl.when(step == 2)
        def _():
            pieces[4].near()

        @pl.when(step == 3)
        def _():
            pieces[3].across()
            pieces[2].far()
            pieces[2].mates()
            stores[2].start()

        @pl.when(step == 4)
        def _():
            pieces[4].across()

        @pl.when(step == 5)
        def _():
            pieces[3].far()
            pieces[3].mates()
            stores[3].start()

        @pl.when(step == 6)
        def _():
            pieces[4].far()

    else:

        @pl.when(step == 0)
        def _():
            place.greet([place.mate], chaining.sometimes())
            before_weights()
            after_weights([w_small[index] for index in range(2)])

    for cut in range(GROUPS - 1):

        @pl.when(step == cut + 2)
        def _():
            chaining.pass_on(0, cut)

    for cut in range(GROUPS - 3):

        @pl.when(step == cut + 4)
        def _():
            chaining.relay(0, cut)

    @pl.when(step > 0)
    def _():
        if fused:
            gate_low = v_parts[part, half, :, :, :, :WIDE].reshape(model, WIDE)
            inner_low = v_parts[part, half, :, :, :, WIDE:].reshape(model, WIDE)
        else:
            gate_low, inner_low = w_gate[0, 0], w_inner[0, 0]
        taps = par[half, :, pl.ds(pl.multiple_of(part * WIDE, WIDE), WIDE)]
        cin = mm(hidden[...], inner_low).astype(LOW)
        cin_out[...] = cin
        gate_out[...] = mm(hidden[HALO:], gate_low)
        masks = [match_out[back] for back in range(CONV - 1)]
        pre = conv_forward(cin.astype(F32), taps, masks)
        pre_out[...] = pre
        spread = spreader(4 * group, HEAD, 4)
        value = (pre * sigmoid(pre) * mm(sp_tail[...], spread)).astype(LOW)
        facx = mm(facs[...], spread)
        fold = jnp.zeros((NSTATE, WIDE), F32)
        for index in range(spans):
            at = slice(index * Q, (index + 1) * Q)
            loc = mm(bct_out[:NSTATE, at], value[at])
            loc_out[at] = loc
            fold = facx[index : index + 1] * fold + loc
        folds[step - 1] = fold
        gains[step - 1] = jnp.broadcast_to(facx[spans : spans + 1], (8, WIDE))

    for cut in range(GROUPS):

        @pl.when(step == cut + 1)
        def _():
            chaining.open(cut)

    @pl.when(step == GROUPS)
    def _():
        chaining.pass_on(0, GROUPS - 1)
        for cut in range(GROUPS - 3, GROUPS):
            chaining.relay(0, cut)
        chaining.later()

        def put(cut, value):
            at = ORDER[cut] * WIDE
            carry_out[:, at : at + WIDE] = value

        chaining.arrive(put)
        if fused:
            pieces[4].mates()
            for piece in pieces:
                piece.finish()
            for store in stores:
                store.wait()
        chaining.finish()


def entry(tokens, doc_col, doc_row, state_filter, packs, cot, rounds):
    own_small, own_parts, own_exit, own_par, own_edge, own_docs = packs
    rows, model = tokens.shape[1:]
    count = lax.axis_size("context")
    depth = count // 2
    wide = GROUPS * WIDE
    ext = rows + HALO
    fused = own_small.shape[0] % 16 == 0
    shape = jax.ShapeDtypeStruct
    sem = lambda *lead: pltpu.SemaphoreType.DMA(lead)
    column = lambda count: pl.BlockSpec((count, WIDE), lambda s: (0, turn_of(s)[0]))
    whole = lambda *dims, dtype=F32: (shape(dims, dtype), const(dims))
    outs = [
        whole(model, rows, dtype=LOW),
        (shape((ext, wide), LOW), column(ext)),
        (shape((rows, wide), F32), column(rows)),
        (shape((rows, wide), F32), column(rows)),
        (shape((rows, wide), F32), column(rows)),
        whole(NSTATE, wide, dtype=LOW),
        whole(ext, WIDE, dtype=LOW),
        whole(rows, WIDE),
        whole(rows, WIDE, dtype=LOW),
        whole(WIDE, rows, dtype=LOW),
        whole(rows, Q),
        whole(rows, Q),
        whole(rows, LANES),
        whole(rows, LANES),
        whole(4, rows, LANES, dtype=LOW),
        whole(6, 8, rows),
        whole(8, LANES),
        whole(CONV - 1, rows, LANES),
    ]
    scratch = [
        pltpu.VMEM((ext, model), LOW),
        pltpu.VMEM((ext, model), F32),
        pltpu.VMEM((rows, LANES), LOW),
        pltpu.VMEM((8, LANES), LOW),
        pltpu.VMEM((GROUPS, NSTATE, WIDE), F32),
        pltpu.VMEM((GROUPS, 8, WIDE), F32),
    ] + Chaining.scratch(rounds)
    in_specs = [
        pl.BlockSpec((1, rows, model), lambda s: (side(), 0, 0)),
        const((rows, LANES)),
        const((8, rows)),
        const((CONV + 1, WIDE)),
    ]
    args = [tokens, doc_col, doc_row, state_filter]
    full = lambda own: (2, 2, count) + own.shape[-2:]
    if fused:
        outs += [
            (shape(full(own_small), LOW), ANY_SPEC),
            (shape((3,) + full(own_parts), LOW), ANY_SPEC),
            (shape(full(own_exit), LOW), ANY_SPEC),
            (shape((2,) + own_par.shape, F32), VMEM_SPEC),
            (shape((8, LANES), F32), VMEM_SPEC),
            (shape((model, rows), LOW), VMEM_SPEC),
        ]
        scratch += [
            pltpu.VMEM(full(own_small), LOW),
            pltpu.VMEM((3,) + full(own_parts), LOW),
            pltpu.VMEM(own_edge.shape, LOW),
            pltpu.VMEM(own_docs.shape, F32),
            pltpu.VMEM(own_docs.shape, F32),
            pltpu.VMEM((rows, model), LOW),
            pltpu.VMEM((2,) + own_par.shape, F32),
            sem(3),
            sem(3),
            sem(2),
            sem(4),
        ] + Gathering.scratch(depth) * 5
        in_specs += [VMEM_SPEC] * 6 + [ANY_SPEC]
        args += [own_small, own_parts, own_exit, own_par, own_edge, own_docs, cot]
    else:
        small, parts, exits, par, heads, edge, docs, cot_t = gather(*packs, cot)
        weights = parts.reshape(3, 2, model, 2 * WIDE)
        block = lambda at: pl.BlockSpec(
            (1, 1, model, WIDE), lambda s: (turn_of(s)[2], turn_of(s)[1], 0, at)
        )
        in_specs += [block(0), block(1), const((2, model, WIDE))] + [VMEM_SPEC] * 4
        args += [weights, weights, small.reshape(2, model, WIDE), par, heads, edge, docs]
    results = pl.pallas_call(
        functools.partial(entry_body, depth, rounds, fused),
        out_shape=[out[0] for out in outs],
        grid=(GROUPS + 1,),
        in_specs=in_specs,
        out_specs=[out[1] for out in outs],
        scratch_shapes=scratch,
        compiler_params=params(collective_id=1, has_side_effects=True),
        name="entry",
    )(*args)
    if fused:
        small, parts, exits, par, heads, cot_t = results[18:]
    return tuple(results[:18]), (
        small.reshape(2, model, WIDE),
        parts.reshape(3, 2, model, 2 * WIDE),
        exits.reshape(2, model, -1),
        par,
        heads,
        cot_t,
    )


def middle_body(
    tokens, cot, cot_t, hidden_t, pre_ref, gate_ref, loc_ref, carry_ref, w_exit, par, par_heads, bc,
    bct, score, mask, sp, cumt, fac, block_out, exit_out, gate_part_out, dy_out, gpg_out, enter_out, row_out,
    skip_out, outputs, gates, unit_grads, mixes, sums, total
):
    step = pl.program_id(0)
    rows = pre_ref.shape[0]
    spans = rows // Q
    wide = 6 * WIDE

    @pl.when(step == 0)
    def _():
        sums[...] = jnp.zeros_like(sums)
        total[...] = jnp.zeros_like(total)
        skip_out[...] = jnp.zeros_like(skip_out)

    @pl.when(step < 6)
    def _():
        group = step
        spread = spreader(4 * group, HEAD, 4)
        pre = pre_ref[...]
        mix = pre * sigmoid(pre)
        mixes[group] = mix
        value = mix * mm(sp[0], spread)
        growth = mm(sp[2], spread)
        facx = mm(split3(fac[...]), spread)
        cums = mm(sp[1], spreader(4 * group, LANES, 4))
        skipx = mm(split3(par_heads[...]), spread)[2:3]
        state = carry_ref[...].astype(F32)
        half = iota((Q, LANES), 1) < HEAD
        for index in range(spans):
            at = slice(index * Q, (index + 1) * Q)
            carried = mm(bc[at, LANES:], state.astype(LOW)) * growth[at]
            parts = []
            for pair in range(2):
                lanes = slice(pair * LANES, (pair + 1) * LANES)
                local = None
                for side in range(2):
                    head = 2 * pair + side
                    across = cumt[group, head : head + 1, at]
                    spread_at = cums[at, head * LANES : (head + 1) * LANES] - across + mask[at]
                    weight = (jnp.exp2(spread_at) * score[at]).astype(LOW)
                    keep = half if side == 0 else jnp.logical_not(half)
                    seen = jnp.where(keep, value[at, lanes], 0.0).astype(LOW)
                    part = mm(weight, seen)
                    local = part if local is None else local + part
                parts.append(local)
            out = jnp.concatenate(parts, axis=1) + carried + skipx * mix[at]
            outputs[group, at] = out
            state = facx[index : index + 1] * state + loc_ref[at]
        gate = gate_ref[...]
        gates[group] = gate
        gated = outputs[group] * (gate * sigmoid(gate))
        unit_grad = mm(cot[0], w_exit[0])
        unit_grads[group] = unit_grad
        square = gated * gated
        cross = unit_grad * par[0, 5:6] * gated
        sums[0] += square[:, :LANES] + square[:, LANES:]
        sums[1] += cross[:, :LANES] + cross[:, LANES:]

    @pl.when(step == 5)
    def _():
        square = jnp.sum(sums[0], axis=1, keepdims=True)
        cross = jnp.sum(sums[1], axis=1, keepdims=True)
        normal = lax.rsqrt(square / wide + EPSILON)
        sums[0] = jnp.broadcast_to(normal, (rows, LANES))
        sums[1] = jnp.broadcast_to(normal * normal * normal * cross / wide, (rows, LANES))

    @pl.when(step >= 6)
    def _():
        group = step - 6
        spread = spreader(4 * group, HEAD, 4)
        normal = twice(sums[0])
        pull = twice(sums[1])
        gain = par[0, 5:6]
        gate = gates[group]
        out = outputs[group]
        unit_grad = unit_grads[group]
        sigma = sigmoid(gate)
        act = gate * sigma
        gated = out * act
        scaled_in = gated * normal
        unit = (scaled_in * gain).astype(LOW)
        total[...] += mm_nt(unit, w_exit[0])
        exit_out[0] = mm(cot_t[...], unit).astype(LOW)
        gate_sum = jnp.sum(unit_grad * scaled_in, axis=0, keepdims=True)
        gated_grad = normal * (unit_grad * gain) - pull * gated
        dy = gated_grad * act
        dy_out[...] = dy
        gate_grad = (gated_grad * out * sigma * (1.0 + gate * (1.0 - sigma))).astype(LOW)
        gpg_out[...] = gate_grad
        gate_part_out[0] = mm(hidden_t[...], gate_grad).astype(LOW)
        skip_sum = jnp.sum(dy * mixes[group], axis=0, keepdims=True)
        row_out[...] = jnp.broadcast_to(gate_sum, (8, WIDE))
        skip_out[...] += head_sums(
            jnp.broadcast_to(skip_sum, (8, WIDE)), gatherer(4 * group, HEAD, 4)
        )
        facx = mm(split3(fac[...]), spread)
        pushed = (dy * mm(sp[2], spread)).astype(LOW)
        enter = jnp.zeros((NSTATE, WIDE), F32)
        for index in reversed(range(spans)):
            at = slice(index * Q, (index + 1) * Q)
            enter = facx[index : index + 1] * enter + mm(bct[NSTATE:, at], pushed[at])
        enter_out[...] = enter

    @pl.when(step == 11)
    def _():
        block_out[...] = (tokens[0].astype(F32) + total[...]).astype(LOW)


def middle(
    tokens, cot, cot_t, hidden_t, pre, gate, loc, carry, weights, par, par_heads, bc, bct, score, mask,
    sp, cumt, fac
):
    rows, model = tokens.shape[1:]
    wide = 6 * WIDE
    shape = jax.ShapeDtypeStruct

    def early(s):
        return jnp.minimum(s, 5)

    def late(s):
        return jnp.maximum(s - 6, 0)

    def group(s):
        return s % 6

    outs = (
        (shape((rows, model), LOW), const((rows, model))),
        (
            shape((2, model, 3 * WIDE), LOW),
            pl.BlockSpec((1, model, WIDE), lambda s: (late(s) // 3, 0, late(s) % 3)),
        ),
        (
            shape((2, model, 3 * WIDE), LOW),
            pl.BlockSpec((1, model, WIDE), lambda s: (late(s) // 3, 0, late(s) % 3)),
        ),
        (shape((rows, wide), F32), pl.BlockSpec((rows, WIDE), lambda s: (0, late(s)))),
        (shape((rows, wide), LOW), pl.BlockSpec((rows, WIDE), lambda s: (0, late(s)))),
        (shape((NSTATE, wide), F32), pl.BlockSpec((NSTATE, WIDE), lambda s: (0, late(s)))),
        (shape((8, wide), F32), pl.BlockSpec((8, WIDE), lambda s: (0, late(s)))),
        (shape((8, LANES), F32), const((8, LANES))),
    )
    return pl.pallas_call(
        middle_body,
        out_shape=[out[0] for out in outs],
        grid=(12,),
        in_specs=[
                pl.BlockSpec((1, rows, model), lambda s: (side(), 0, 0)),
                pl.BlockSpec((1, rows, model), lambda s: (side(), 0, 0)),
                const((model, rows)),
                const((model, rows)),
                pl.BlockSpec((rows, WIDE), lambda s: (0, early(s))),
                pl.BlockSpec((rows, WIDE), lambda s: (0, early(s))),
                pl.BlockSpec((rows, WIDE), lambda s: (0, early(s))),
                pl.BlockSpec((NSTATE, WIDE), lambda s: (0, early(s))),
                pl.BlockSpec((1, model, WIDE), lambda s: (group(s) // 3, 0, group(s) % 3)),
                pl.BlockSpec((1, 8, WIDE), lambda s: (group(s) // 3, 0, group(s) % 3)),
                const((8, LANES)),
                const((rows, WIDE)),
                const((WIDE, rows)),
                const((rows, Q)),
                const((rows, Q)),
                const((4, rows, LANES)),
                const((6, 8, rows)),
                const((8, LANES)),
        ],
        out_specs=[out[1] for out in outs],
        scratch_shapes=[
                pltpu.VMEM((6, rows, WIDE), F32),
                pltpu.VMEM((6, rows, WIDE), F32),
                pltpu.VMEM((6, rows, WIDE), F32),
                pltpu.VMEM((6, rows, WIDE), F32),
                pltpu.VMEM((2, rows, LANES), F32),
                pltpu.VMEM((rows, model), F32),
        ],
        compiler_params=params(),
        name="middle",
    )(
        tokens, cot, cot_t, hidden_t, pre, gate, loc, carry, weights, par, par_heads, bc, bct, score,
        mask, sp, cumt, fac,
    )


def scan_back_body(
    depth, rounds, pre_ref, dy_ref, loc_ref, carry_ref, enter, cin_ref, par, par_heads,
    state_filter, cin_state, pre_state, bc, bct, score, mask, sp, cumt, fac, match, zst, dt_ref,
    exits, gate_part, block_own, tokens, cot, hidden_t, gpg, w_gate, w_inner, w_small, tap_out,
    tap_state_out, small_out, mine, block_out, inner_part, small_part, token_out, norm_out, d_bc,
    d_score, d_cum, heads, local_value, enters, gains, adjoints, edge_own, edge_in, grads, total, es,
    el, bs, bl, block_keep, *scratch
):
    group = pl.program_id(0)
    blocks = BLOCK_CUTS
    rows = pre_ref.shape[0]
    spans = rows // Q
    place = Place(depth)
    wide = exits.shape[-1]
    chaining = Chaining(place, rounds, True, enters, gains, scratch[:4], scratch[4:8])
    reducing = Reducing(
        place, 0, [(exits, slice(0, wide)), (gate_part, slice(wide, 2 * wide))], mine,
        scratch[8:16], scratch[16:],
    )
    position = place.position
    has_before, has_after = position > 0, position < 2 * depth - 1
    before, after = {"context": position - 1}, {"context": position + 1}
    share = rows // blocks

    def block_copy(index):
        at = pl.ds(pl.multiple_of(index * share, share), share)
        return remote(
            block_own.at[at], block_out.at[place.y, at], bs.at[index], bl.at[index], place.y_peer
        )

    block_local = pltpu.make_async_copy(block_own, block_out.at[place.y], block_keep.at[0])

    def edge_copy(index):
        return remote(edge_own.at[index], edge_in.at[index], es.at[index], el.at[index], before)

    def edge_wait(index):
        @pl.when(has_after)
        def _():
            edge_copy(index).wait_recv()

    def joined(index):
        grad = grads[...]
        return jnp.concatenate(
            [grad[: rows - EDGE], grad[rows - EDGE :] + edge_in[index]], axis=0
        ).astype(LOW)

    @pl.when(group == 0)
    def _():
        d_bc[...] = jnp.zeros_like(d_bc)
        d_score[...] = jnp.zeros_like(d_score)
        d_cum[...] = jnp.zeros_like(d_cum)
        heads[...] = jnp.zeros_like(heads)
        grads[...] = jnp.zeros_like(grads)
        total[...] = jnp.zeros_like(total)
        edge_in[GROUPS + 1] = jnp.zeros((EDGE, WIDE), F32)

        @pl.when(jnp.logical_not(has_after))
        def _():
            edge_in[...] = jnp.zeros_like(edge_in)

        place.greet(
            [place.mate, place.x_peer, place.y_peer],
            chaining.sometimes() + [(has_before, before), (has_after, after)],
            True,
        )
        facs = split3(fac[...])
        for cut in range(GROUPS):
            enters[cut] = enter[:, cut * WIDE : (cut + 1) * WIDE]
            chaining.open(cut)
        for cut in range(GROUPS):
            rows8 = mm(facs, spreader(4 * cut, HEAD, 4))
            gains[cut] = jnp.broadcast_to(rows8[spans : spans + 1], (8, WIDE))
        each(depth, reducing.start)
        block_local.start()
        each(3, lambda index: block_copy(index).start())
        for cut in range(GROUPS):
            chaining.pass_on(0, cut)

    @pl.when(group < GROUPS)
    def _():
        spread = spreader(4 * group, HEAD, 4)
        collect = gatherer(4 * group, HEAD, 4)
        pre = pre_ref[...]
        sigma = sigmoid(pre)
        mix = pre * sigma
        dtx = mm(sp[0], spread)
        growth = mm(sp[2], spread)
        facx = mm(split3(fac[...]), spread)
        cums = mm(sp[1], spreader(4 * group, LANES, 4))
        half = iota((Q, LANES), 1) < HEAD
        ones = jnp.ones((8, Q), F32).astype(LOW)
        states = [carry_ref[...].astype(F32)]
        for index in range(spans - 1):
            at = slice(index * Q, (index + 1) * Q)
            states.append(facx[index : index + 1] * states[-1] + loc_ref[at])
        for index in range(spans):
            at = slice(index * Q, (index + 1) * Q)
            dy = dy_ref[at]
            value = mix[at] * dtx[at]
            parts = []
            sum_score = None
            for pair in range(2):
                lanes = slice(pair * LANES, (pair + 1) * LANES)
                value_low = value[:, lanes].astype(LOW)
                local = None
                for part_of in range(2):
                    head = 2 * pair + part_of
                    across = cumt[group, head : head + 1, at]
                    spread_at = cums[at, head * LANES : (head + 1) * LANES] - across + mask[at]
                    decay = jnp.exp2(spread_at)
                    keep = half if part_of == 0 else jnp.logical_not(half)
                    dy_low = jnp.where(keep, dy[:, lanes], 0.0).astype(LOW)
                    inner = decay * mm_nt(dy_low, value_low)
                    sum_score = inner if sum_score is None else sum_score + inner
                    moved = (inner * score[at]).astype(LOW)
                    turn = mm_nt(ones, moved) - mm(ones, moved)
                    d_cum[group, head : head + 1, at] = turn[0:1]
                    part = mm_tn((decay * score[at]).astype(LOW), dy_low)
                    local = part if local is None else local + part
                parts.append(local)
            d_score[at] += sum_score
            local_value[at] = jnp.concatenate(parts, axis=1)
            pushed = dy * growth[at]
            state_low = states[index].astype(LOW)
            carried = mm(bc[at, LANES:], state_low)
            d_bc[at, LANES:] += mm_nt(pushed.astype(LOW), state_low)
            heads[1, at] += head_sums(pushed * carried, collect)

    @pl.when(group == 0)
    def _():
        for cut in range(GROUPS):
            chaining.relay(0, cut)
        chaining.later()

        def put(cut, value):
            adjoints[cut] = value

        chaining.arrive(put)
        chaining.finish()

    for turn in range(5):

        @pl.when(group == turn)
        def _():
            each(turn + 1 if turn < 4 else depth + 1, reducing.turn, turn)
            block_copy(turn + 3).start()

    @pl.when(group == 5)
    def _():
        reducing.close()

    @pl.when((group > 0) & (group < GROUPS))
    def _():
        edge_wait(group - 1)

    @pl.when(group < GROUPS)
    def _():
        spread = spreader(4 * group, HEAD, 4)
        collect = gatherer(4 * group, HEAD, 4)
        pre = pre_ref[...]
        sigma = sigmoid(pre)
        mix = pre * sigma
        dtx = mm(sp[0], spread)
        growth = mm(sp[2], spread)
        facx = mm(split3(fac[...]), spread)
        states = [carry_ref[...].astype(F32)]
        for index in range(spans - 1):
            at = slice(index * Q, (index + 1) * Q)
            states.append(facx[index : index + 1] * states[-1] + loc_ref[at])
        arrived = jnp.where(group > 0, group - 1, GROUPS + 1)
        grad = joined(arrived)
        gate_grad = gpg[...]
        inner_part[0] = mm(hidden_t[...], grad).astype(LOW)
        total[...] += mm_nt(gate_grad, w_gate[0, 0]) + mm_nt(grad, w_inner[0, 0])
        tails = mm(sp[3], spread)
        skipx = mm(split3(par_heads[...]), spread)[2:3]
        adjoint = adjoints[group].astype(F32)
        masks = [match[back] for back in range(CONV - 1)]
        pgs = [None] * spans
        for index in reversed(range(spans)):
            at = slice(index * Q, (index + 1) * Q)
            dy = dy_ref[at]
            value = mix[at] * dtx[at]
            adj_low = adjoint.astype(LOW)
            reached = mm(bc[at, :LANES], adj_low) * tails[at]
            d_bc[at, :LANES] += mm_nt((value * tails[at]).astype(LOW), adj_low)
            heads[0, at] += head_sums(value * reached, collect)
            fac_part = jnp.sum(adjoint * states[index], axis=0, keepdims=True)
            heads[3, index * 8 : index * 8 + 8] += head_sums(
                jnp.broadcast_to(fac_part, (8, WIDE)), collect
            )
            pushed_low = (dy * growth[at]).astype(LOW)
            adjoint = facx[index : index + 1] * adjoint + mm(bct[NSTATE:, at], pushed_low)
            d_value = local_value[at] + reached
            heads[2, at] += head_sums(mix[at] * d_value, collect)
            d_mix = dtx[at] * d_value + skipx * dy
            s = sigma[at]
            pgs[index] = d_mix * s * (1.0 + pre[at] * (1.0 - s))
        pg = jnp.concatenate(pgs, axis=0)
        sums, grad = conv_backward(pg, cin_ref[...].astype(F32), par[0], masks)
        tap_out[...] = jnp.concatenate(sums + [jnp.zeros((3, WIDE), F32)], axis=0)
        grads[...] = grad[HALO:]
        edge_own[group] = grad[HALO - EDGE : HALO]

        @pl.when(has_before)
        def _():
            edge_copy(group).start()

    @pl.when(group == GROUPS)
    def _():
        masks = [match[back] for back in range(CONV - 1)]
        edge_wait(GROUPS - 1)
        grad = joined(GROUPS - 1)
        inner_part[0] = mm(hidden_t[...], grad).astype(LOW)
        total[...] += mm_nt(grad, w_inner[0, 0])
        t_at, u_at = iota((Q, Q), 0), iota((Q, Q), 1)
        onward = (t_at <= u_at).astype(F32)
        earlier = (t_at > u_at).astype(F32)
        rate = jnp.exp(par_heads[1:2])
        raws = []
        bias_sum = jnp.zeros((1, LANES), F32)
        decay_sum = jnp.zeros((1, LANES), F32)
        used = iota((Q, LANES), 1) < 24
        for index in range(spans):
            at = slice(index * Q, (index + 1) * Q)
            pieces = [d_cum[piece, 0:4, at] for piece in range(6)]
            pieces.append(jnp.zeros((LANES - 24, Q), F32))
            cum_col = jnp.transpose(jnp.concatenate(pieces, axis=0))
            fac_row = fac[index : index + 1] * heads[3, index * 8 : index * 8 + 1]
            d_decay = (
                mm_exact(onward, cum_col + heads[1, at]) + mm_exact(earlier, heads[0, at]) + fac_row
            )
            dt = dt_ref[at]
            raw = (heads[2, at] - d_decay * rate) * sigmoid(zst[at])
            raw = jnp.where(used, raw, 0.0)
            raws.append(raw.astype(LOW))
            bias_sum += jnp.sum(raw, axis=0, keepdims=True)
            decay_sum -= jnp.sum(
                jnp.where(used, d_decay * dt * rate, 0.0), axis=0, keepdims=True
            )
            score_low = d_score[at].astype(LOW)
            d_bc[at, :LANES] += mm_tn(score_low, bc[at, LANES:])
            d_bc[at, LANES:] += mm(score_low, bc[at, :LANES])
        small_out[...] = jnp.concatenate(
            [bias_sum, decay_sum, jnp.zeros((6, LANES), F32)], axis=0
        )
        pre = pre_state[...]
        s = sigmoid(pre)
        pg = d_bc[...] * s * (1.0 + pre * (1.0 - s))
        sums, grad = conv_backward(pg, cin_state[...].astype(F32), state_filter[...], masks)
        tap_state_out[...] = jnp.concatenate(sums + [jnp.zeros((3, WIDE), F32)], axis=0)
        grads[...] = grad[HALO:]
        edge_own[GROUPS] = grad[HALO - EDGE : HALO]

        @pl.when(has_before)
        def _():
            edge_copy(GROUPS).start()

        steps = jnp.concatenate(raws, axis=0)
        turned = hidden_t[...]
        step_part = mm(turned, steps).astype(LOW)
        small_part[0, :, LANES:] = step_part
        small_part[1, :, LANES:] = step_part
        total[...] += mm_nt(steps, w_small[0, :, LANES:]) + mm_nt(steps, w_small[1, :, LANES:])
        edge_wait(GROUPS)
        state = joined(GROUPS)
        state_part = mm(turned, state).astype(LOW)
        small_part[0, :, :LANES] = state_part[:, :LANES]
        small_part[1, :, :LANES] = state_part[:, LANES:]
        value = tokens[0].astype(F32)
        scale = lax.rsqrt(jnp.mean(value * value, axis=1, keepdims=True) + EPSILON)
        hidden_grad = (
            total[...]
            + mm_nt(state[:, :LANES], w_small[0, :, :LANES])
            + mm_nt(state[:, LANES:], w_small[1, :, :LANES])
        )
        norm_sum = jnp.sum(hidden_grad * (value * scale), axis=0, keepdims=True)
        norm_out[...] = jnp.broadcast_to(norm_sum, norm_out.shape)
        gain = jnp.transpose(w_small[0, :, LANES : 2 * LANES].astype(F32))[24:25]
        normed = hidden_grad * gain
        pull = jnp.sum(normed * value, axis=1, keepdims=True) / value.shape[1]
        token_out[...] = (
            cot[0].astype(F32) + scale * normed - (scale * scale * scale) * value * pull
        ).astype(LOW)
        reducing.finish()
        each(blocks, lambda index: block_copy(index).wait())
        block_local.wait()

        @pl.when(has_before)
        def _():
            each(GROUPS + 1, lambda index: edge_copy(index).wait_send())


def scan_back(
    pre, dy, loc, carry, enter, cin, par, par_heads, state_filter, cin_state, pre_state, bc, bct,
    score, mask, sp, cumt, fac, match, zst, dt, exits, gate_part, block_own, tokens, cot, hidden_t,
    gpg, parts, small, rounds
):
    rows, wide = pre.shape
    ext = rows + HALO
    depth = lax.axis_size("context") // 2
    own_rows, half_wide = exits.shape[3:]
    shape = jax.ShapeDtypeStruct
    sem = lambda *lead: pltpu.SemaphoreType.DMA(lead)
    model = tokens.shape[2]
    now = lambda s: jnp.minimum(s, GROUPS - 1)
    lag = lambda s: jnp.maximum(s - 1, 0)
    column = lambda count: pl.BlockSpec((count, WIDE), lambda s: (0, now(s)))
    outs = (
        (shape((8, wide), F32), column(8)),
        (shape((8, WIDE), F32), const((8, WIDE))),
        (shape((8, LANES), F32), const((8, LANES))),
        (shape((own_rows, 2 * half_wide), F32), const((own_rows, 2 * half_wide))),
        (shape((2,) + block_own.shape, LOW), ANY_SPEC),
        (
            shape((2, model, 3 * WIDE), LOW),
            pl.BlockSpec((1, model, WIDE), lambda s: (lag(s) // 3, 0, lag(s) % 3)),
        ),
        (shape((2, model, WIDE), LOW), const((2, model, WIDE))),
        (shape((rows, model), LOW), const((rows, model))),
        (shape((8, model), F32), const((8, model))),
    )
    return pl.pallas_call(
        functools.partial(scan_back_body, depth, rounds),
        out_shape=[out[0] for out in outs],
        grid=(GROUPS + 1,),
        in_specs=[
            column(rows),
            column(rows),
            column(rows),
            column(NSTATE),
            const((NSTATE, wide)),
            column(ext),
            pl.BlockSpec((1, 8, WIDE), lambda s: (now(s) // 3, 0, now(s) % 3)),
            const((8, LANES)),
            const((CONV + 1, WIDE)),
            const((ext, WIDE)),
            const((rows, WIDE)),
            const((rows, WIDE)),
            const((WIDE, rows)),
            const((rows, Q)),
            const((rows, Q)),
            const((4, rows, LANES)),
            const((6, 8, rows)),
            const((8, LANES)),
            const((CONV - 1, rows, LANES)),
            const((rows, LANES)),
            const((rows, LANES)),
            ANY_SPEC,
            ANY_SPEC,
            VMEM_SPEC,
            pl.BlockSpec((1, rows, model), lambda s: (side(), 0, 0)),
            pl.BlockSpec((1, rows, model), lambda s: (side(), 0, 0)),
            const((model, rows)),
            column(rows),
            pl.BlockSpec((1, 1, model, WIDE), lambda s: (now(s) % 3, now(s) // 3, 0, 0)),
            pl.BlockSpec((1, 1, model, WIDE), lambda s: (lag(s) % 3, lag(s) // 3, 0, 1)),
            const((2, model, WIDE)),
        ],
        out_specs=[out[1] for out in outs],
        scratch_shapes=[
            pltpu.VMEM((rows, WIDE), F32),
            pltpu.VMEM((rows, Q), F32),
            pltpu.VMEM((6, 8, rows), F32),
            pltpu.VMEM((4, rows, LANES), F32),
            pltpu.VMEM((rows, WIDE), F32),
            pltpu.VMEM((GROUPS, NSTATE, WIDE), F32),
            pltpu.VMEM((GROUPS, 8, WIDE), F32),
            pltpu.VMEM((GROUPS, NSTATE, WIDE), LOW),
            pltpu.VMEM((GROUPS + 1, EDGE, WIDE), F32),
            pltpu.VMEM((GROUPS + 2, EDGE, WIDE), F32),
            pltpu.VMEM((rows, WIDE), F32),
            pltpu.VMEM((rows, model), F32),
            sem(GROUPS + 1),
            sem(GROUPS + 1),
            sem(BLOCK_CUTS),
            sem(BLOCK_CUTS),
            sem(1),
        ]
        + Chaining.scratch(rounds)
        + Reducing.scratch(depth, own_rows, 2 * half_wide),
        compiler_params=params(collective_id=2, has_side_effects=True),
        name="scan_back",
    )(
        pre, dy, loc, carry, enter, cin, par, par_heads, state_filter, cin_state, pre_state, bc,
        bct, score, mask, sp, cumt, fac, match, zst, dt, exits, gate_part, block_own, tokens, cot,
        hidden_t, gpg, parts, parts, small,
    )


def pack_body(
    entry, exits, state, steps, gain, inner_kernel, gate_gain, bias, decay, skip, docs,
    tail_tokens, packed_small, packed_parts, packed_exit, par, doc_col, doc_row, edge, docs_own
):
    half_of = side()
    rows = entry.shape[0]
    wide = entry.shape[2]

    def placed(filled, used):
        return jnp.where(half_of == 0, filled, pltpu.roll(filled, used, 1))

    def widened(value):
        return jnp.concatenate(
            [value, jnp.zeros((value.shape[0], LANES - value.shape[1]), F32)], axis=1
        )

    for part in range(3):
        at = slice(part * WIDE, (part + 1) * WIDE)
        packed_parts[part, :, :WIDE] = entry[:, 0, at].astype(LOW)
        packed_parts[part, :, WIDE:] = entry[:, 1, at].astype(LOW)
    half = jnp.where(half_of == 0, state[:, :NSTATE], state[:, NSTATE:])
    packed_small[:, :NSTATE] = half.astype(LOW)
    gain_row = jnp.concatenate([gain[...], jnp.zeros((1, LANES - rows), F32)], axis=1)
    gain_col = jnp.transpose(jnp.broadcast_to(gain_row, (LANES, LANES)))[:rows]
    lane = iota((rows, LANES), 1)
    heads_here = steps.shape[0]
    step_rows = jnp.concatenate([steps[...], jnp.zeros((heads_here, LANES - rows), F32)], axis=1)
    step_rows = jnp.concatenate([step_rows, jnp.zeros((LANES - heads_here, LANES), F32)], axis=0)
    step_cols = jnp.transpose(step_rows)[:rows]
    small = jnp.where(lane == 24, gain_col, placed(step_cols, heads_here))
    packed_small[:, NSTATE:] = small.astype(LOW)
    packed_exit[...] = exits[...].astype(LOW)
    par[0 : CONV + 1] = inner_kernel[...]
    for index in range(wide // LANES):
        at = slice(index * LANES, (index + 1) * LANES)
        par[CONV + 1 : CONV + 2, at] = gate_gain[index : index + 1]
    par[CONV + 2 : CONV + 4] = jnp.zeros((2, wide), F32)
    for index, ref in enumerate((bias, decay, skip)):
        par[CONV + 2 : CONV + 3, index * LANES : (index + 1) * LANES] = placed(
            widened(ref[...]), ref.shape[1]
        )
    own = jnp.where(half_of == 0, docs[0:1], docs[1:2]).astype(F32)
    doc_row[...] = jnp.broadcast_to(own, doc_row.shape)
    doc_col[...] = jnp.transpose(jnp.broadcast_to(own, (LANES, own.shape[1])))
    docs_own[...] = doc_col[own.shape[1] - HALO :]
    edge[...] = tail_tokens[0]


def pack(
    entry, exits, state, steps, gain, inner_kernel, gate_gain, bias, decay, skip, docs, tokens
):
    own_rows, _, wide = entry.shape
    rows, model = tokens.shape[1:]
    shape = jax.ShapeDtypeStruct
    arrays = (
        entry, exits, state, steps.T, gain[None], inner_kernel, gate_gain.reshape(-1, LANES), bias[None],
        decay[None], skip[None], docs,
    )
    outs = (
        shape((own_rows, WIDE), LOW),
        shape((3, own_rows, 2 * WIDE), LOW),
        shape((own_rows, wide), LOW),
        shape((8, wide), F32),
        shape((rows, LANES), F32),
        shape((8, rows), F32),
        shape((HALO, model), LOW),
        shape((HALO, LANES), F32),
    )
    return pl.pallas_call(
        pack_body,
        out_shape=outs,
        grid=(1,),
        in_specs=[const(array.shape) for array in arrays]
        + [pl.BlockSpec((1, HALO, model), lambda s: (side(), rows // HALO - 1, 0))],
        out_specs=[const(out.shape) for out in outs],
        compiler_params=params(),
        name="pack",
    )(*arrays, tokens)


def gather_body(
    depth, own_small, own_parts, own_exit, par_own, edge_own, docs_own, cot, small, parts, exits, par,
    heads, edge, docs, cot_t, docs_in, cot_in, side_send, side_land, local, *marks
):
    place = Place(depth)
    count = 2 * depth
    onward = {"context": lax.rem(place.position + 1, count)}
    behind = {"context": lax.rem(place.position + count - 1, count)}
    y = place.y
    place.greet([place.mate, place.x_peer, place.y_peer, onward, behind], (), True)
    own = [own_small, own_parts.at[0], own_parts.at[1], own_parts.at[2], own_exit]
    full = [small, parts.at[0], parts.at[1], parts.at[2], exits]
    pieces = [Gathering(place, own[i], full[i], *marks[3 * i : 3 * i + 3]) for i in range(5)]
    sides = [
        remote(edge_own, edge, side_send.at[0], side_land.at[0], onward),
        remote(docs_own, docs_in, side_send.at[1], side_land.at[1], onward),
        remote(par_own, par.at[y], side_send.at[2], side_land.at[2], place.y_peer),
    ]
    for copy in sides:
        copy.start()
    cot_copy = pltpu.make_async_copy(cot.at[y], cot_in, local.at[1])
    cot_copy.start()
    par_keep = pltpu.make_async_copy(par_own, par.at[y], local.at[0])
    par_keep.start()
    for piece in pieces:
        piece.own()
    cot_copy.wait()
    cot_t[...] = jnp.transpose(cot_in[...])
    for piece in pieces:
        piece.near()
        piece.across()
        piece.far()
    for copy in sides:
        copy.wait()
    docs[...] = jnp.where(place.position == 0, -1.0, docs_in[...])
    par_keep.wait()
    both = par[0, CONV + 2 : CONV + 3] + par[1, CONV + 2 : CONV + 3]
    heads[...] = jnp.zeros_like(heads)
    for index in range(3):
        heads[index : index + 1] = both[:, index * LANES : (index + 1) * LANES]
    for piece in pieces:
        piece.mates()
        piece.finish()


def gather(own_small, own_parts, own_exit, par_own, edge_own, docs_own, cot):
    count = lax.axis_size("context")
    depth = count // 2
    rows, model = cot.shape[1:]
    shape = jax.ShapeDtypeStruct
    full = lambda own: (2, 2, count) + own.shape[-2:]
    return pl.pallas_call(
        functools.partial(gather_body, depth),
        out_shape=(
            shape(full(own_small), LOW),
            shape((3,) + full(own_parts), LOW),
            shape(full(own_exit), LOW),
            shape((2,) + par_own.shape, F32),
            shape((8, LANES), F32),
            shape(edge_own.shape, LOW),
            shape(docs_own.shape, F32),
            shape((model, rows), LOW),
        ),
        in_specs=[VMEM_SPEC] * 6 + [ANY_SPEC],
        out_specs=[ANY_SPEC] * 3 + [VMEM_SPEC] * 5,
        scratch_shapes=[
            pltpu.VMEM(docs_own.shape, F32),
            pltpu.VMEM((rows, model), LOW),
            pltpu.SemaphoreType.DMA((3,)),
            pltpu.SemaphoreType.DMA((3,)),
            pltpu.SemaphoreType.DMA((2,)),
        ]
        + Gathering.scratch(depth) * 5,
        compiler_params=params(collective_id=0, has_side_effects=True),
        name="gather",
    )(own_small, own_parts, own_exit, par_own, edge_own, docs_own, cot)


def reduce_body(
    depth, inner, small, token, taps, taps_state, gate_row, head_rows, skip_row, norm_row,
    total, state_out, vector_out, token_out, state_own, vec_send, vec_land, vs, vl, ts, tl, ss, sl,
    keep_sem, *scratch
):
    place = Place(depth)
    x, y, z, c = place.x, place.y, place.z, place.c
    wide = inner.shape[-1]
    parts = [(inner, slice(0, wide)), (small, slice(wide, wide + WIDE))]
    reducing = Reducing(place, 0, parts, total, scratch[:8], scratch[8:])

    vec_send[0] = jnp.zeros(vec_send.shape[1:], F32)
    vec_send[0, : CONV + 1, : 2 * wide] = taps[: CONV + 1]
    vec_send[0, : CONV + 1, 2 * wide :] = taps_state[: CONV + 1]
    vec_send[0, 5:6, : 2 * wide] = gate_row[0:1]
    vec_send[0, 5:6, 2 * wide : 2 * wide + LANES] = head_rows[0:1]
    vec_send[0, 5:6, 2 * wide + LANES :] = skip_row[0:1]
    model = norm_row.shape[1]
    vec_send[0, 6:7, :model] = norm_row[0:1]
    vec_send[0, 6:7, model : model + LANES] = head_rows[1:2]

    place.greet([place.mate, place.x_peer, place.y_peer], (), True)
    vec_targets = [place.mate, place.x_peer, place.y_peer]

    def vec_copy(turn):
        return remote(
            vec_send.at[turn], vec_land.at[turn], vs.at[turn], vl.at[turn], vec_targets[turn]
        )

    def vec_far(away, lands_at):
        return remote(
            vec_send.at[3], vec_land.at[3 + lands_at], vs.at[3 + away], vl.at[3 + lands_at],
            place.away(away),
        )

    share = token.shape[0] // depth

    def token_copy(step):
        at = pl.ds(pl.multiple_of(step * share, share), share)
        return remote(token.at[at], token_out.at[y, at], ts.at[step], tl.at[step], place.y_peer)

    token_keep = pltpu.make_async_copy(token, token_out.at[y], keep_sem.at[0])

    vec_copy(0).start()
    each(depth, reducing.start)
    token_keep.start()

    def step_all(step):
        reducing.turn(step)

        @pl.when(step < depth)
        def _():
            token_copy(step).start()

        for turn in range(3):

            @pl.when(step == turn)
            def _():
                vec_copy(turn).wait_recv()
                vec_send[turn + 1] = vec_send[turn] + vec_land[turn]
                if turn < 2:
                    vec_copy(turn + 1).start()
                else:
                    each(depth, lambda s: vec_far(lax.rem(z + s, depth), z).start(), 1)
                    vec_land[3 + z] = vec_send[3]

    each(depth + 1, step_all)
    reducing.close()
    state_own[...] = total[:, wide : wide + NSTATE]
    state_copy = remote(state_own, state_out.at[y], ss.at[0], sl.at[0], place.y_peer)
    state_copy.start()
    state_out[y] = state_own[...]

    def vec_arrive(step):
        away = lax.rem(z + step, depth)
        vec_far(away, away).wait_recv()

    each(depth, vec_arrive, 1)
    vector_out[...] = vec_land[3]

    def vec_add(step):
        vector_out[...] += vec_land[3 + step]

    each(depth, vec_add, 1)
    for turn in range(3):
        vec_copy(turn).wait_send()
    each(depth, lambda s: vec_far(lax.rem(z + s, depth), z).wait_send(), 1)
    reducing.finish()
    each(depth, lambda step: token_copy(step).wait())
    state_copy.wait()
    token_keep.wait()


def reduce_all(inner, small, token, taps, taps_state, gate_row, head_rows, skip_row, norm_row):
    count = lax.axis_size("context")
    depth = count // 2
    own_rows, wide = inner.shape[3:]
    tall = wide + WIDE
    shape = jax.ShapeDtypeStruct
    sem = lambda *lead: pltpu.SemaphoreType.DMA(lead)
    vector = (8, 2 * wide + WIDE)
    return pl.pallas_call(
        functools.partial(reduce_body, depth),
        out_shape=(
            shape((own_rows, tall), F32),
            shape((2, own_rows, NSTATE), F32),
            shape(vector, F32),
            shape((2,) + token.shape, LOW),
        ),
        in_specs=[ANY_SPEC] * 2 + [VMEM_SPEC] * 7,
        out_specs=[VMEM_SPEC] * 3 + [ANY_SPEC],
        scratch_shapes=[
            pltpu.VMEM((own_rows, NSTATE), F32),
            pltpu.VMEM((4,) + vector, F32),
            pltpu.VMEM((3 + depth,) + vector, F32),
            sem(3 + depth),
            sem(3 + depth),
            sem(depth),
            sem(depth),
            sem(1),
            sem(1),
            sem(1),
        ]
        + Reducing.scratch(depth, own_rows, tall),
        compiler_params=params(collective_id=4, has_side_effects=True),
        name="reduce_all",
    )(inner, small, token, taps, taps_state, gate_row, head_rows, skip_row, norm_row)


def finish_body(
    mine, exits, state, vector, token, block, block_out, token_out,
    norm_out, entry_out, state_out, step_out, kernel_out, filter_out, bias_out, decay_out, skip_out,
    gate_out, exit_out
):
    half_of = side()
    spot = lax.axis_index("dp") * lax.axis_size("context") + lax.axis_index("context")
    token_out[...] = token[...].astype(F32)
    first = half_of == 0
    block_out[...] = block[...]

    @pl.when(pl.program_id(0) == 0)
    def _():
        own_rows, _, wide = entry_out.shape
        model = token.shape[2]
        entry_out[:, 0] = exits[:, wide:]
        entry_out[:, 1] = mine[:, :wide]
        exit_out[...] = exits[:, :wide]
        state_out[:, :NSTATE] = state[0]
        state_out[:, NSTATE:] = state[1]

        def twelve(value):
            return jnp.where(first, value, pltpu.roll(value, LANES - 12, 1))[:, :12]

        steps = jnp.where(first, mine[:, wide + NSTATE :], pltpu.roll(mine[:, wide + NSTATE :], LANES - 12, 1))
        steps = jnp.concatenate([steps, jnp.zeros((LANES - own_rows, LANES), F32)], axis=0)
        step_out[...] = jnp.transpose(steps)[:12, :own_rows]
        left, right = vector[:, :wide], vector[:, wide : 2 * wide]
        halves = jnp.where(first, left, right)
        kernel_out[...] = halves[: CONV + 1]
        for index in range(wide // LANES):
            gate_out[index : index + 1] = halves[5:6, index * LANES : (index + 1) * LANES]
        filter_out[...] = vector[: CONV + 1, 2 * wide :]
        bias_out[...] = twelve(vector[5:6, 2 * wide : 2 * wide + LANES])
        skip_out[...] = twelve(vector[5:6, 2 * wide + LANES :])
        decay_out[...] = twelve(vector[6:7, model : model + LANES])
        turned = pltpu.roll(vector[:, :model], lax.rem(model - spot * own_rows, model), 1)
        norm_out[...] = turned[6:7, :own_rows]


def finish(mine, exits, state, vector, token, block):
    own_rows, wide = exits.shape[0], exits.shape[1] // 2
    _, rows, model = token.shape
    share = rows // 4
    shape = jax.ShapeDtypeStruct
    outs = (
        (shape((2, rows, model), LOW), pl.BlockSpec((2, share, model), lambda s: (0, s, 0))),
        (shape((2, rows, model), F32), pl.BlockSpec((2, share, model), lambda s: (0, s, 0))),
        (shape((1, own_rows), F32), None),
        (shape((own_rows, 2, wide), F32), None),
        (shape((own_rows, WIDE), F32), None),
        (shape((12, own_rows), F32), None),
        (shape((CONV + 1, wide), F32), None),
        (shape((CONV + 1, WIDE), F32), None),
        (shape((1, 12), F32), None),
        (shape((1, 12), F32), None),
        (shape((1, 12), F32), None),
        (shape((wide // LANES, LANES), F32), None),
        (shape((own_rows, wide), F32), None),
    )
    return pl.pallas_call(
        finish_body,
        out_shape=[out[0] for out in outs],
        grid=(4,),
        in_specs=[
            const(mine.shape),
            const(exits.shape),
            const(state.shape),
            const(vector.shape),
            pl.BlockSpec((2, share, model), lambda s: (0, s, 0)),
            pl.BlockSpec((2, share, model), lambda s: (0, s, 0)),
        ],
        out_specs=[out[1] if out[1] is not None else const(out[0].shape) for out in outs],
        compiler_params=params(),
        name="finish",
    )(mine, exits, state, vector, token, block)


def body(
    tokens, documents, norm_gain, entry_weight, state_weight, step_weight, inner_kernel,
    state_filter, step_bias, decay_log, skip_gain, gate_gain, exit_weight, cotangent,
):
    seqs, rows, model = tokens.shape
    count = lax.axis_size("context")
    own_rows = norm_gain.shape[0]
    longest = rows * count // 4
    rounds = min(count // 2 - 1, -(-(longest - 1) // (2 * rows)))

    own_small, own_parts, own_exit, own_par, doc_col, doc_row, own_edge, own_docs = pack(
        entry_weight, exit_weight, state_weight, step_weight, norm_gain, inner_kernel,
        gate_gain, step_bias, decay_log, skip_gain, documents, tokens,
    )
    packs = (own_small, own_parts, own_exit, own_par, own_edge, own_docs)
    (
        hidden_t, cin, gate, pre, loc, carry, cin_state, pre_state, bc, bct, score, mask, zst, dt, sp,
        cumt, fac, match,
    ), (small, parts, exit_weights, par, par_heads, cot_t) = entry(
        tokens, doc_col, doc_row, state_filter, packs, cotangent, rounds
    )
    block_own, exit_part, gate_part, dy, gpg, enter, gate_row, skip_row = middle(
        tokens, cotangent, cot_t, hidden_t, pre, gate, loc, carry, exit_weights, par, par_heads, bc,
        bct, score, mask, sp, cumt, fac,
    )
    cut = lambda v: v.reshape(2, 2, count, own_rows, v.shape[-1])
    (
        taps, taps_state, head_rows, exit_mine, block_both, inner_part, small_part, token_own,
        norm_row,
    ) = scan_back(
        pre, dy, loc, carry, enter, cin, par, par_heads, state_filter, cin_state, pre_state, bc, bct,
        score, mask, sp, cumt, fac, match, zst, dt, cut(exit_part), cut(gate_part), block_own,
        tokens, cotangent, hidden_t, gpg, parts, small, rounds,
    )
    mine, state_both, vector, token_both = reduce_all(
        cut(inner_part), cut(small_part), token_own, taps, taps_state, gate_row, head_rows, skip_row,
        norm_row,
    )
    outs = list(finish(mine, exit_mine, state_both, vector, token_both, block_both))
    for index in (2, 8, 9, 10):
        outs[index] = outs[index][0]
    outs[5] = outs[5].T
    outs[11] = outs[11].reshape(-1)
    return tuple(outs)


def solution(mesh):
    in_specs = (
        P("dp", "context", None),
        P("dp", "context"),
        P(("dp", "context")),
        P(("dp", "context"), None, "tensor"),
        P(("dp", "context"), None),
        P(("dp", "context"), "tensor"),
        P(None, "tensor"),
        P(),
        P("tensor"),
        P("tensor"),
        P("tensor"),
        P("tensor"),
        P(("dp", "context"), "tensor"),
        P("dp", "context", None),
    )
    out_specs = (
        P("dp", "context", None),
        P("dp", "context", None),
        P(("dp", "context")),
        P(("dp", "context"), None, "tensor"),
        P(("dp", "context"), None),
        P(("dp", "context"), "tensor"),
        P(None, "tensor"),
        P(),
        P("tensor"),
        P("tensor"),
        P("tensor"),
        P("tensor"),
        P(("dp", "context"), "tensor"),
    )
    return jax.shard_map(body, mesh=mesh, in_specs=in_specs, out_specs=out_specs, check_vma=False)
```

```python
import functools
import jax
import jax.numpy as jnp
from jax import lax
from jax.experimental import pallas as pl
from jax.experimental.pallas import tpu as pltpu
from jax.sharding import PartitionSpec as P

HEAD = 64
NSTATE = 128
CONV = 4
EPSILON = 1e-05
Q = 128
HALO = 16
EDGE = 8
GROUPS = 6
BLOCK_CUTS = 8
ORDER = (0, 3, 1, 4, 2, 5)
LANES = 128
WIDE = 256
LOG2E = 1.4426950408889634
FAR = -1e30
LOW = jnp.bfloat16
F32 = jnp.float32
VMEM_LIMIT = 60 * 1024 * 1024


def mm(a, b):
    return lax.dot_general(a, b, (((1,), (0,)), ((), ())), preferred_element_type=F32)


def mm_nt(a, b):
    return lax.dot_general(a, b, (((1,), (1,)), ((), ())), preferred_element_type=F32)


def mm_tn(a, b):
    return lax.dot_general(a, b, (((0,), (0,)), ((), ())), preferred_element_type=F32)


def mm_exact(a, b):
    return lax.dot_general(
        a, b, (((1,), (0,)), ((), ())), precision=lax.Precision.HIGHEST, preferred_element_type=F32
    )


def split3(v):
    high = v.astype(LOW).astype(F32)
    rest = v - high
    mid = rest.astype(LOW).astype(F32)
    low = rest - mid
    return (high + pltpu.roll(mid, 32, 1) + pltpu.roll(low, 64, 1)).astype(LOW)


def iota(shape, dim):
    return lax.broadcasted_iota(jnp.int32, shape, dim)


def spreader(first_head, width, count):
    k = iota((LANES, width * count), 0)
    lane = iota((LANES, width * count), 1)
    hit = ((k & 31) == first_head + lane // width) & (k < 96)
    return hit.astype(F32).astype(LOW)


def gatherer(first_head, width, count):
    lane = iota((width * count, LANES), 0)
    k = iota((width * count, LANES), 1)
    return (k == first_head + lane // width).astype(F32).astype(LOW)


def head_sums(v, collect):
    high = v.astype(LOW)
    rest = (v - high.astype(F32)).astype(LOW)
    return mm(high, collect) + mm(rest, collect)


def sigmoid(v):
    return 1.0 / (1.0 + jnp.exp(-v))


def twice(v):
    return jnp.concatenate([v, v], axis=1)


def conv_forward(cin, taps, masks):
    rows = cin.shape[0] - HALO
    out = taps[CONV : CONV + 1] + taps[CONV - 1 : CONV] * cin[HALO:]
    for back in range(1, CONV):
        part = cin[HALO - back : HALO - back + rows]
        out = out + taps[CONV - 1 - back : CONV - back] * (part * twice(masks[back - 1]))
    return out


def conv_backward(pg, cin, taps, masks):
    rows, width = pg.shape
    sums = [None] * (CONV + 1)
    sums[CONV] = jnp.sum(pg, axis=0, keepdims=True)
    sums[CONV - 1] = jnp.sum(pg * cin[HALO:], axis=0, keepdims=True)
    pad = jnp.zeros((HALO, width), F32)
    grad = jnp.concatenate([pad, pg * taps[CONV - 1 : CONV]], axis=0)
    for back in range(1, CONV):
        masked = pg * twice(masks[back - 1])
        part = cin[HALO - back : HALO - back + rows]
        sums[CONV - 1 - back] = jnp.sum(masked * part, axis=0, keepdims=True)
        padded = jnp.concatenate([pad, masked * taps[CONV - 1 - back : CONV - back], pad], axis=0)
        grad = grad + padded[back : back + rows + HALO]
    return sums, grad


def const(shape):
    zeros = (0,) * len(shape)
    return pl.BlockSpec(shape, lambda *_: zeros)


def params(**extra):
    return pltpu.CompilerParams(vmem_limit_bytes=VMEM_LIMIT, **extra)


VMEM_SPEC = pl.BlockSpec(memory_space=pltpu.VMEM)
ANY_SPEC = pl.BlockSpec(memory_space=pl.ANY)


def side():
    return lax.axis_index("tensor")


def remote(src, dst, send_sem, recv_sem, target):
    return pltpu.make_async_remote_copy(
        src_ref=src,
        dst_ref=dst,
        send_sem=send_sem,
        recv_sem=recv_sem,
        device_id=target,
        device_id_type=pl.DeviceIdType.MESH,
    )


def each(count, run, first=0):
    def one(step, carry):
        run(step)
        return carry

    lax.fori_loop(first, count, one, 0)


class Place:
    def __init__(self, depth):
        position = lax.axis_index("context")
        self.depth = depth
        self.position = position
        self.x, self.y = lax.axis_index("dp"), lax.axis_index("tensor")
        self.z, self.c = position // 2, position % 2
        self.mate = self.at(self.x, self.y, self.z, 1 - self.c)
        self.x_peer = self.at(1 - self.x, self.y, self.z, self.c)
        self.y_peer = self.at(self.x, 1 - self.y, self.z, self.c)

    def at(self, x, y, z, c):
        return {"dp": x, "context": z * 2 + c, "tensor": y}

    def away(self, z):
        return self.at(self.x, self.y, z, self.c)

    def axes(self, turned):
        x, y, z, c = self.x, self.y, self.z, self.c
        x1, y1 = x + (1 - turned) * (1 - 2 * x), y + turned * (1 - 2 * y)
        x2, y2 = x + turned * (1 - 2 * x), y + (1 - turned) * (1 - 2 * y)
        return (x1, y1), (x2, y2)

    def around(self, run, first=0, last=None):
        z, depth = self.z, self.depth
        if first == 0:
            run(z)

        def step(away):
            @pl.when(z - away >= 0)
            def _():
                run(z - away)

            @pl.when(z + away < depth)
            def _():
                run(z + away)

        each(depth if last is None else last, step, max(first, 1))

    def greet(self, always, sometimes=(), column=False):
        barrier = pltpu.get_barrier_semaphore()
        kind = pl.DeviceIdType.MESH
        total = len(always)
        for target in always:
            pl.semaphore_signal(barrier, inc=1, device_id=target, device_id_type=kind)
        for holds, target in sometimes:

            @pl.when(holds)
            def _():
                pl.semaphore_signal(barrier, inc=1, device_id=target, device_id_type=kind)

            total = total + holds.astype(jnp.int32)
        if column:
            for_all = lambda step: pl.semaphore_signal(
                barrier,
                inc=1,
                device_id=self.away(lax.rem(self.z + step, self.depth)),
                device_id_type=kind,
            )
            each(self.depth, for_all, 1)
            total = total + (self.depth - 1)
        pl.semaphore_wait(barrier, total)


class Gathering:
    def __init__(self, place, own, full, sends, lands, local):
        self.place, self.own_ref, self.full = place, own, full
        self.sends, self.lands, self.local = sends, lands, local
        self.starts = [first * place.depth for first in (0, 4, 5, 7)]
        (self.x1, self.y1), (self.x2, self.y2) = place.axes(place.c)
        self.first = place.at(self.x1, self.y1, place.z, place.c)
        self.second = place.at(self.x2, self.y2, place.z, place.c)

    @staticmethod
    def scratch(depth):
        sem = pltpu.SemaphoreType.DMA
        return [sem((8 * depth,)), sem((8 * depth,)), sem((1,))]

    def copy(self, kind, index, x, y, z, c, target, own=False):
        chunk = self.full.at[y, x, z * 2 + c]
        mark = ((y * 2 + x) * self.place.depth + z) * 2 + c
        return remote(
            self.own_ref if own else chunk, chunk, self.sends.at[self.starts[kind] + index],
            self.lands.at[mark], target,
        )

    def arrive(self, x, y, z, c):
        self.copy(0, 0, x, y, z, c, self.place.mate).wait_recv()

    def kept(self):
        p = self.place
        return pltpu.make_async_copy(
            self.own_ref, self.full.at[p.y, p.x, p.z * 2 + p.c], self.local.at[0]
        )

    def own(self):
        p = self.place
        mine = (p.x, p.y, p.z, p.c)

        def far_z(z):
            self.copy(3, z, *mine, p.away(z), True).start()

        p.around(far_z, 1)
        self.copy(1, p.z, *mine, self.first, True).start()
        self.copy(2, p.z, *mine, self.second, True).start()
        self.copy(0, p.z, *mine, p.mate, True).start()
        self.kept().start()

    def near(self, first=1, last=None):
        p = self.place

        def run(z):
            chunk = (p.x, p.y, z, p.c)
            self.arrive(*chunk)

            self.copy(1, z, *chunk, self.first).start()
            self.copy(2, z, *chunk, self.second).start()
            self.copy(0, z, *chunk, p.mate).start()

        p.around(run, first, last)

    def across(self):
        p = self.place

        def run(z):
            chunk = (self.x1, self.y1, z, p.c)
            self.arrive(*chunk)
            self.copy(2, p.depth + z, *chunk, self.second).start()
            self.copy(0, p.depth + z, *chunk, p.mate).start()

        p.around(run)

    def far(self):
        p = self.place

        def near_row(z):
            self.arrive(self.x2, self.y2, z, p.c)
            self.copy(0, 2 * p.depth + z, self.x2, self.y2, z, p.c, p.mate).start()

        def far_row(z):
            self.arrive(1 - p.x, 1 - p.y, z, p.c)
            self.copy(0, 3 * p.depth + z, 1 - p.x, 1 - p.y, z, p.c, p.mate).start()

        p.around(near_row)
        p.around(far_row)

    def mates(self):
        p = self.place

        def from_mate(z):
            for y in range(2):
                for x in range(2):
                    self.arrive(x, y, z, 1 - p.c)

        each(p.depth, from_mate)
        self.kept().wait()

    def finish(self):
        p = self.place

        def sent(kind, index, target):
            self.copy(kind, index, p.x, p.y, p.z, p.c, target).wait_send()

        each(4 * p.depth, lambda step: sent(0, step, p.mate))
        each(p.depth, lambda step: sent(1, step, p.mate))
        each(2 * p.depth, lambda step: sent(2, step, p.mate))

        p.around(lambda z: sent(3, z, p.mate), 1)


class Reducing:
    def __init__(self, place, turned, parts, total, bufs, sems):
        self.place, self.parts, self.total = place, parts, total
        self.own, self.core, self.send1, self.land1 = bufs[:4]
        self.send2, self.land2, self.send3, self.land3 = bufs[4:]
        self.own_sem, self.core_send, self.core_land = sems[:3]
        self.s1, self.l1, self.s2, self.l2, self.s3, self.l3 = sems[3:]
        self.turned = turned
        (x1, y1), (x2, y2) = place.axes(turned)
        self.first = place.at(x1, y1, place.z, place.c)
        self.second = place.at(x2, y2, place.z, place.c)
        self.mine = place.y + turned * (place.x - place.y)

    @staticmethod
    def scratch(depth, rows, tall):
        buffer = lambda *lead: pltpu.VMEM(lead + (rows, tall), LOW)
        sem = lambda *lead: pltpu.SemaphoreType.DMA(lead)
        bufs = [
            buffer(2, 2, depth), buffer(2, 2, depth), buffer(depth, 2), buffer(depth, 2),
            buffer(depth), buffer(depth), buffer(depth), buffer(depth),
        ]
        return bufs + [sem(2, 2, depth)] * 3 + [sem(depth)] * 6

    def spot(self, step):
        return lax.rem(self.place.z + 1 + step, self.place.depth)

    def whole(self, y, x, z):
        return remote(
            self.core.at[y, x, z], self.core.at[y, x, z], self.core_send.at[y, x, z],
            self.core_land.at[y, x, z], self.place.mate,
        )

    def own_whole(self, y, x, z):
        return pltpu.make_async_copy(
            self.own.at[y, x, z], self.own.at[y, x, z], self.own_sem.at[y, x, z]
        )

    def start(self, step):
        p = self.place
        z = self.spot(step)
        for y in range(2):
            for x in range(2):
                for ref, cols in self.parts:
                    remote(
                        ref.at[y, x, z * 2 + 1 - p.c], self.core.at[y, x, z, :, cols],
                        self.core_send.at[y, x, z], self.core_land.at[y, x, z], p.mate,
                    ).start()
                    pltpu.make_async_copy(
                        ref.at[y, x, z * 2 + p.c], self.own.at[y, x, z, :, cols],
                        self.own_sem.at[y, x, z],
                    ).start()

    def base(self, y, x, z):
        return self.own[y, x, z].astype(F32) + self.core[y, x, z].astype(F32)

    def copy1(self, z):
        return remote(
            self.send1.at[z], self.land1.at[z], self.s1.at[z], self.l1.at[z], self.first
        )

    def copy2(self, z):
        return remote(
            self.send2.at[z], self.land2.at[z], self.s2.at[z], self.l2.at[z], self.second
        )

    def copy3(self, z, lands_at):
        return remote(
            self.send3.at[z], self.land3.at[lands_at], self.s3.at[z], self.l3.at[lands_at],
            self.place.away(z),
        )

    def stage1(self, step):
        p, turned = self.place, self.turned
        z = self.spot(step)
        for y in range(2):
            for x in range(2):
                self.whole(y, x, z).wait_recv()
                self.own_whole(y, x, z).wait()
        for index in range(2):
            x = (1 - turned) * (1 - p.x) + turned * index
            y = turned * (1 - p.y) + (1 - turned) * index
            self.send1[z, index] = self.base(y, x, z).astype(LOW)
        self.copy1(z).start()

    def stage2(self, step):
        p, turned = self.place, self.turned
        z = self.spot(step)
        self.copy1(z).wait_recv()
        other = 1 - self.mine
        x = (1 - turned) * p.x + turned * other
        y = turned * p.y + (1 - turned) * other
        self.send2[z] = (self.base(y, x, z) + self.land1[z, other].astype(F32)).astype(LOW)
        self.copy2(z).start()

    def final(self, z):
        p = self.place
        self.copy2(z).wait_recv()
        return (
            self.base(p.y, p.x, z)
            + self.land1[z, self.mine].astype(F32)
            + self.land2[z].astype(F32)
        )

    def stage3(self, step):
        z = self.spot(step)
        self.send3[z] = self.final(z).astype(LOW)
        self.copy3(z, self.place.z).start()

    def turn(self, step):
        depth = self.place.depth

        @pl.when(step < depth)
        def _():
            self.stage1(step)

        @pl.when((step >= 1) & (step <= depth))
        def _():
            self.stage2(step - 1)

        @pl.when((step >= 2) & (step <= depth))
        def _():
            self.stage3(step - 2)

    def close(self):
        p = self.place
        self.total[...] = self.final(p.z)

        def add(step):
            z = lax.rem(p.z + step, p.depth)
            self.copy3(z, z).wait_recv()
            self.total[...] += self.land3[z].astype(F32)

        each(p.depth, add, 1)

    def finish(self):
        p = self.place

        def sent(z):
            for y in range(2):
                for x in range(2):
                    self.whole(y, x, z).wait_send()
            self.copy1(z).wait_send()
            self.copy2(z).wait_send()

        each(p.depth, sent)
        each(p.depth, lambda step: self.copy3(lax.rem(p.z + step, p.depth), p.z).wait_send(), 1)


class Chaining:
    def __init__(self, place, rounds, backward, fold, gain, bufs, sems):
        self.place, self.rounds = place, rounds
        self.fold, self.gain = fold, gain
        self.from_mate, self.from_chip, self.to_mate, self.to_chip = bufs
        self.mate_send, self.mate_land, self.chip_send, self.chip_land = sems
        first = 1 if backward else 0
        by = -1 if backward else 1
        self.order = place.depth - 1 - place.z if backward else place.z
        self.leads = place.c == first
        self.after = place.at(place.x, place.y, place.z + by, first)
        self.before = place.at(place.x, place.y, place.z - by, 1 - first)
        self.linked_before = self.leads & (self.order > 0)
        self.linked_after = jnp.logical_not(self.leads) & (self.order < place.depth - 1)

    @staticmethod
    def scratch(rounds):
        slots = lambda turns: pltpu.VMEM((turns, GROUPS, NSTATE, WIDE), LOW)
        marks = lambda turns: pltpu.SemaphoreType.DMA((turns, GROUPS))
        return [
            slots(rounds + 1), slots(rounds), slots(rounds + 1), slots(rounds),
            marks(rounds + 1), marks(rounds + 1), marks(rounds), marks(rounds),
        ]

    def sometimes(self):
        return [(self.linked_before, self.before), (self.linked_after, self.after)]

    def mate_copy(self, turn, cut):
        return remote(
            self.to_mate.at[turn, cut], self.from_mate.at[turn, cut], self.mate_send.at[turn, cut],
            self.mate_land.at[turn, cut], self.place.mate,
        )

    def chip_copy(self, turn, cut):
        return remote(
            self.to_chip.at[turn, cut], self.from_chip.at[turn, cut], self.chip_send.at[turn, cut],
            self.chip_land.at[turn, cut], self.after,
        )

    def joined(self, cut, arrived):
        return (self.fold[cut] + self.gain[cut, 0:1] * arrived.astype(F32)).astype(LOW)

    def open(self, cut):
        @pl.when(self.leads)
        def _():
            self.to_mate[0, cut] = self.fold[cut].astype(LOW)
            self.mate_copy(0, cut).start()

    def pass_on(self, turn, cut):
        @pl.when(jnp.logical_not(self.leads))
        def _():
            self.mate_copy(turn, cut).wait_recv()

        @pl.when(self.linked_after)
        def _():
            self.to_chip[turn, cut] = self.joined(cut, self.from_mate[turn, cut])
            self.chip_copy(turn, cut).start()

    def relay(self, turn, cut):
        @pl.when(self.linked_before)
        def _():
            self.chip_copy(turn, cut).wait_recv()
            self.to_mate[turn + 1, cut] = self.joined(cut, self.from_chip[turn, cut])
            self.mate_copy(turn + 1, cut).start()

        @pl.when(self.leads & (self.order == 0))
        def _():
            self.to_mate[turn + 1, cut] = self.fold[cut].astype(LOW)
            self.mate_copy(turn + 1, cut).start()

    def later(self):
        for turn in range(1, self.rounds):
            for cut in range(GROUPS):
                self.pass_on(turn, cut)
            for cut in range(GROUPS):
                self.relay(turn, cut)

    def arrive(self, put):
        last = self.rounds - 1

        @pl.when(self.linked_before)
        def _():
            for cut in range(GROUPS):
                put(cut, self.from_chip[last, cut])

        @pl.when(self.leads & (self.order == 0))
        def _():
            for cut in range(GROUPS):
                put(cut, jnp.zeros((NSTATE, WIDE), LOW))

        @pl.when(jnp.logical_not(self.leads))
        def _():
            for cut in range(GROUPS):
                self.mate_copy(self.rounds, cut).wait_recv()
                put(cut, self.from_mate[self.rounds, cut])

    def finish(self):
        @pl.when(self.leads)
        def _():
            for turn in range(self.rounds + 1):
                for cut in range(GROUPS):
                    self.mate_copy(turn, cut).wait_send()

        @pl.when(self.linked_after)
        def _():
            for turn in range(self.rounds):
                for cut in range(GROUPS):
                    self.chip_copy(turn, cut).wait_send()


class Closing:
    def __init__(self, place, token, token_out, refs):
        self.place, self.token, self.token_out = place, token, token_out
        self.state_own, self.state_in, self.send, self.land = refs[:4]
        self.vs, self.vl, self.ts, self.tl, self.ss, self.sl, self.keep_sem = refs[4:]
        self.targets = [place.mate, place.y_peer, place.x_peer]

    @staticmethod
    def scratch(depth, own_rows, vector):
        sem = lambda *lead: pltpu.SemaphoreType.DMA(lead)
        return [
            pltpu.VMEM((own_rows, NSTATE), F32),
            pltpu.VMEM((2, own_rows, NSTATE), F32),
            pltpu.VMEM((4,) + vector, F32),
            pltpu.VMEM((3 + depth,) + vector, F32),
            sem(3 + depth), sem(3 + depth), sem(depth), sem(depth), sem(1), sem(1), sem(1),
        ]

    def vec_copy(self, turn):
        return remote(
            self.send.at[turn], self.land.at[turn], self.vs.at[turn], self.vl.at[turn],
            self.targets[turn],
        )

    def vec_far(self, away, lands_at):
        return remote(
            self.send.at[3], self.land.at[3 + lands_at], self.vs.at[3 + away],
            self.vl.at[3 + lands_at], self.place.away(away),
        )

    def token_copy(self, step):
        p = self.place
        share = self.token.shape[0] // p.depth
        at = pl.ds(pl.multiple_of(step * share, share), share)
        return remote(
            self.token.at[at], self.token_out.at[p.y, at], self.ts.at[step], self.tl.at[step],
            p.y_peer,
        )

    def run(self, reducing, width, state_out, vector_out, first, pending=None):
        p = self.place
        depth, z = p.depth, p.z
        keep = pltpu.make_async_copy(self.token, self.token_out.at[p.y], self.keep_sem.at[0])
        keep.start()
        self.vec_copy(0).start()

        def step_all(step):
            if pending is not None:

                @pl.when(step + 3 <= depth)
                def _():
                    pending.turn(step + 3)

            reducing.turn(step)

            @pl.when(step < depth)
            def _():
                self.token_copy(step).start()

            for turn in range(3):

                @pl.when(step == turn)
                def _():
                    self.vec_copy(turn).wait_recv()
                    self.send[turn + 1] = self.send[turn] + self.land[turn]
                    if turn < 2:
                        self.vec_copy(turn + 1).start()
                    else:
                        each(depth, lambda s: self.vec_far(lax.rem(z + s, depth), z).start(), 1)
                        self.land[3 + z] = self.send[3]

        each(depth + 1, step_all)
        if pending is not None:
            pending.close()
        reducing.close()
        self.state_own[...] = reducing.total[:, first : first + width]
        state_copy = remote(
            self.state_own, self.state_in.at[p.y], self.ss.at[0], self.sl.at[0], p.y_peer
        )
        state_copy.start()
        self.state_in[p.y] = self.state_own[...]

        def vec_arrive(step):
            away = lax.rem(z + step, depth)
            self.vec_far(away, away).wait_recv()

        each(depth, vec_arrive, 1)
        vector_out[...] = self.land[3]

        def vec_add(step):
            vector_out[...] += self.land[3 + step]

        each(depth, vec_add, 1)
        for turn in range(3):
            self.vec_copy(turn).wait_send()
        each(depth, lambda s: self.vec_far(lax.rem(z + s, depth), z).wait_send(), 1)
        reducing.finish()
        each(depth, lambda step: self.token_copy(step).wait())
        state_copy.wait()
        state_out[...] = self.state_in[...]
        keep.wait()


def group_of(index):
    half, part = index % 2, index // 2
    return half * 3 + part, half, part


def turn_of(step):
    return group_of(jnp.maximum(step - 1, 0))


def entry_body(depth, rounds, fused, *refs):
    step = pl.program_id(0)
    tokens, doc_col, doc_row, state_filter = refs[:4]
    if fused:
        own_small, own_parts, own_exit, own_par, own_edge, own_docs, cot = refs[4:11]
    else:
        w_gate, w_inner, w_small, par, heads_ref, edge, halo_docs = refs[4:11]
    (
        hidden_out, cin_out, gate_out, pre_out, loc_out, carry_out, cin_state_out, pre_state_out,
        bc_out, bct_out, score_out, mask_out, zst_out, dt_out, sp_out, cumt_out, fac_out, match_out,
    ) = refs[11:29]
    refs = refs[29:]
    if fused:
        small_out, parts_out, exit_out, par, heads_ref, cot_t = refs[:6]
        refs = refs[6:]
    hidden, normed, sp_tail, facs, folds, gains = refs[:6]
    rows, model = tokens.shape[1:]
    spans = rows // Q
    place = Place(depth)
    chaining = Chaining(place, rounds, False, folds, gains, refs[6:10], refs[10:14])
    group, half, part = turn_of(step)
    y = place.y
    if fused:
        v_small, v_parts, edge, halo_docs, docs_in, cot_in, par_in = refs[14:21]
        side_send, side_land, local, out_sem = refs[21:25]
        marks = refs[25:]
        own = [own_small, own_parts.at[0], own_parts.at[1], own_parts.at[2], own_exit]
        full = [v_small, v_parts.at[0], v_parts.at[1], v_parts.at[2], exit_out]
        pieces = [
            Gathering(place, own[i], full[i], *marks[3 * i : 3 * i + 3]) for i in range(5)
        ]
        stores = [pltpu.make_async_copy(v_small, small_out, out_sem.at[0])]
        for index in range(3):
            stores.append(
                pltpu.make_async_copy(
                    v_parts.at[index], parts_out.at[index], out_sem.at[index + 1]
                )
            )

    def before_weights():
        for ref, first, count in ((edge, 0, HALO), (tokens, HALO, rows)):
            value = (ref[...] if ref is edge else ref[0]).astype(F32)
            scale = lax.rsqrt(jnp.mean(value * value, axis=1, keepdims=True) + EPSILON)
            normed[first : first + count] = value * scale
        docs = jnp.concatenate([halo_docs[...], doc_col[...]], axis=0)
        for back in range(1, CONV):
            match = (docs[HALO - back : HALO - back + rows] == docs[HALO:]).astype(F32)
            match_out[back - 1] = match
        t_at, u_at = iota((Q, Q), 0), iota((Q, Q), 1)
        for index in range(spans):
            at = slice(index * Q, (index + 1) * Q)
            same = (t_at >= u_at) & (doc_col[at] == doc_row[0:1, at])
            mask_out[at] = jnp.where(same, 0.0, FAR)

    def after_weights(small):
        gain = jnp.transpose(small[0][:, LANES:].astype(F32))[24:25]
        hidden[...] = (normed[...] * gain).astype(LOW)
        hidden_out[...] = jnp.transpose(hidden[HALO:])
        both = [mm(hidden[...], small[index]) for index in range(2)]
        cin = jnp.concatenate([both[0][:, :LANES], both[1][:, :LANES]], axis=1).astype(LOW)
        cin_state_out[...] = cin
        docs = jnp.concatenate([halo_docs[...], doc_col[...]], axis=0)
        masks = [match_out[back] for back in range(CONV - 1)]
        pre = conv_forward(cin.astype(F32), state_filter[...], masks)
        pre_state_out[...] = pre
        mixed = (pre * sigmoid(pre)).astype(LOW)
        bc_out[...] = mixed
        turned = jnp.transpose(mixed.astype(F32)).astype(LOW)
        bct_out[...] = turned
        heads = heads_ref[...]
        used = iota((rows, LANES), 1) < 24
        raw = both[0][HALO:, LANES:] + both[1][HALO:, LANES:]
        zst = jnp.where(used, raw, 0.0) + heads[0:1]
        zst_out[...] = zst
        dt = jnp.where(used, jnp.maximum(zst, 0.0) + jnp.log1p(jnp.exp(-jnp.abs(zst))), 0.0)
        dt_out[...] = dt
        decay = -dt * jnp.exp(heads[1:2])
        t_at, u_at = iota((Q, Q), 0), iota((Q, Q), 1)
        lower = (t_at >= u_at).astype(F32)
        fac_rows = []
        for index in range(spans):
            at = slice(index * Q, (index + 1) * Q)
            cum = mm_exact(lower, decay[at])
            final = cum[Q - 1 : Q]
            before = docs[HALO + index * Q - 1 : HALO + index * Q]
            here = doc_col[at]
            last = here[Q - 1 : Q]
            opened = (here == before).astype(F32)
            tail = (here == last).astype(F32) * jnp.exp(final - cum)
            fac_rows.append((last == before).astype(F32) * jnp.exp(final))
            cum2 = cum * LOG2E
            turned_cum = jnp.transpose(cum2)
            for group in range(6):
                cumt_out[group, 0:4, at] = turned_cum[4 * group : 4 * group + 4]
            sp_out[0, at] = split3(dt[at])
            sp_out[1, at] = split3(cum2)
            lanes_used = iota((Q, LANES), 1) < 24
            sp_out[2, at] = split3(jnp.where(lanes_used, opened * jnp.exp(cum), 0.0))
            sp_out[3, at] = split3(jnp.where(lanes_used, tail, 0.0))
            sp_tail[at] = split3(jnp.where(lanes_used, tail * dt[at], 0.0))
            score_out[at] = mm_nt(mixed[at, LANES:], mixed[at, :LANES])
        gain_total = fac_rows[0]
        for row in fac_rows[1:]:
            gain_total = gain_total * row
        rows8 = jnp.concatenate(
            fac_rows + [gain_total] + [jnp.zeros((1, LANES), F32)] * (7 - spans), axis=0
        )
        rows8 = jnp.where(iota((8, LANES), 1) < 24, rows8, 0.0)
        fac_out[...] = rows8
        facs[...] = split3(rows8)

    if fused:

        @pl.when(step == 0)
        def _():
            count = 2 * depth
            onward = {"context": lax.rem(place.position + 1, count)}
            behind = {"context": lax.rem(place.position + count - 1, count)}
            place.greet(
                [place.mate, place.x_peer, place.y_peer, onward, behind], chaining.sometimes(), True
            )
            sides = [
                remote(own_edge, edge, side_send.at[0], side_land.at[0], onward),
                remote(own_docs, docs_in, side_send.at[1], side_land.at[1], onward),
                remote(own_par, par_in.at[y], side_send.at[2], side_land.at[2], place.y_peer),
            ]
            for copy in sides:
                copy.start()
            for piece in pieces:
                piece.own()
            cot_copy = pltpu.make_async_copy(cot.at[y], cot_in, local.at[0])
            par_keep = pltpu.make_async_copy(own_par, par_in.at[y], local.at[1])
            cot_copy.start()
            par_keep.start()
            for copy in sides:
                copy.wait()
            par_keep.wait()
            pieces[0].near()
            pieces[1].near()
            halo_docs[...] = jnp.where(place.position == 0, -1.0, docs_in[...])
            par[...] = par_in[...]
            both = par[0, CONV + 2 : CONV + 3] + par[1, CONV + 2 : CONV + 3]
            heads_ref[...] = jnp.zeros_like(heads_ref)
            for index in range(3):
                heads_ref[index : index + 1] = both[:, index * LANES : (index + 1) * LANES]
            before_weights()
            pieces[0].across()
            pieces[2].near()
            pieces[1].across()
            pieces[0].far()
            cot_copy.wait()
            cot_t[...] = jnp.transpose(cot_in[...])
            pieces[0].mates()
            stores[0].start()
            after_weights([v_small[index].reshape(model, WIDE) for index in range(2)])

        @pl.when(step == 1)
        def _():
            pieces[3].near()
            pieces[2].across()
            pieces[1].far()
            pieces[1].mates()
            stores[1].start()

        @pl.when(step == 2)
        def _():
            pieces[4].near()

        @pl.when(step == 3)
        def _():
            pieces[3].across()
            pieces[2].far()
            pieces[2].mates()
            stores[2].start()

        @pl.when(step == 4)
        def _():
            pieces[4].across()

        @pl.when(step == 5)
        def _():
            pieces[3].far()
            pieces[3].mates()
            stores[3].start()

        @pl.when(step == 6)
        def _():
            pieces[4].far()

    else:

        @pl.when(step == 0)
        def _():
            place.greet([place.mate], chaining.sometimes())
            before_weights()
            after_weights([w_small[index] for index in range(2)])

    for cut in range(GROUPS - 1):

        @pl.when(step == cut + 2)
        def _():
            chaining.pass_on(0, cut)

    for cut in range(GROUPS - 3):

        @pl.when(step == cut + 4)
        def _():
            chaining.relay(0, cut)

    @pl.when(step > 0)
    def _():
        if fused:
            gate_low = v_parts[part, half, :, :, :, :WIDE].reshape(model, WIDE)
            inner_low = v_parts[part, half, :, :, :, WIDE:].reshape(model, WIDE)
        else:
            gate_low, inner_low = w_gate[0, 0], w_inner[0, 0]
        taps = par[half, :, pl.ds(pl.multiple_of(part * WIDE, WIDE), WIDE)]
        cin = mm(hidden[...], inner_low).astype(LOW)
        cin_out[...] = cin
        gate_out[...] = mm(hidden[HALO:], gate_low)
        masks = [match_out[back] for back in range(CONV - 1)]
        pre = conv_forward(cin.astype(F32), taps, masks)
        pre_out[...] = pre
        spread = spreader(4 * group, HEAD, 4)
        value = (pre * sigmoid(pre) * mm(sp_tail[...], spread)).astype(LOW)
        facx = mm(facs[...], spread)
        fold = jnp.zeros((NSTATE, WIDE), F32)
        for index in range(spans):
            at = slice(index * Q, (index + 1) * Q)
            loc = mm(bct_out[:NSTATE, at], value[at])
            loc_out[at] = loc
            fold = facx[index : index + 1] * fold + loc
        folds[step - 1] = fold
        gains[step - 1] = jnp.broadcast_to(facx[spans : spans + 1], (8, WIDE))

    for cut in range(GROUPS):

        @pl.when(step == cut + 1)
        def _():
            chaining.open(cut)

    @pl.when(step == GROUPS)
    def _():
        chaining.pass_on(0, GROUPS - 1)
        for cut in range(GROUPS - 3, GROUPS):
            chaining.relay(0, cut)
        chaining.later()

        def put(cut, value):
            at = ORDER[cut] * WIDE
            carry_out[:, at : at + WIDE] = value

        chaining.arrive(put)
        if fused:
            pieces[4].mates()
            for piece in pieces:
                piece.finish()
            for store in stores:
                store.wait()
        chaining.finish()


def entry(tokens, doc_col, doc_row, state_filter, packs, cot, rounds):
    own_small, own_parts, own_exit, own_par, own_edge, own_docs = packs
    rows, model = tokens.shape[1:]
    count = lax.axis_size("context")
    depth = count // 2
    wide = GROUPS * WIDE
    ext = rows + HALO
    fused = own_small.shape[0] % 16 == 0
    shape = jax.ShapeDtypeStruct
    sem = lambda *lead: pltpu.SemaphoreType.DMA(lead)
    column = lambda count: pl.BlockSpec((count, WIDE), lambda s: (0, turn_of(s)[0]))
    whole = lambda *dims, dtype=F32: (shape(dims, dtype), const(dims))
    outs = [
        whole(model, rows, dtype=LOW),
        (shape((ext, wide), LOW), column(ext)),
        (shape((rows, wide), F32), column(rows)),
        (shape((rows, wide), F32), column(rows)),
        (shape((rows, wide), F32), column(rows)),
        whole(NSTATE, wide, dtype=LOW),
        whole(ext, WIDE, dtype=LOW),
        whole(rows, WIDE),
        whole(rows, WIDE, dtype=LOW),
        whole(WIDE, rows, dtype=LOW),
        whole(rows, Q),
        whole(rows, Q),
        whole(rows, LANES),
        whole(rows, LANES),
        whole(4, rows, LANES, dtype=LOW),
        whole(6, 8, rows),
        whole(8, LANES),
        whole(CONV - 1, rows, LANES),
    ]
    scratch = [
        pltpu.VMEM((ext, model), LOW),
        pltpu.VMEM((ext, model), F32),
        pltpu.VMEM((rows, LANES), LOW),
        pltpu.VMEM((8, LANES), LOW),
        pltpu.VMEM((GROUPS, NSTATE, WIDE), F32),
        pltpu.VMEM((GROUPS, 8, WIDE), F32),
    ] + Chaining.scratch(rounds)
    in_specs = [
        pl.BlockSpec((1, rows, model), lambda s: (side(), 0, 0)),
        const((rows, LANES)),
        const((8, rows)),
        const((CONV + 1, WIDE)),
    ]
    args = [tokens, doc_col, doc_row, state_filter]
    full = lambda own: (2, 2, count) + own.shape[-2:]
    if fused:
        outs += [
            (shape(full(own_small), LOW), ANY_SPEC),
            (shape((3,) + full(own_parts), LOW), ANY_SPEC),
            (shape(full(own_exit), LOW), ANY_SPEC),
            (shape((2,) + own_par.shape, F32), VMEM_SPEC),
            (shape((8, LANES), F32), VMEM_SPEC),
            (shape((model, rows), LOW), VMEM_SPEC),
        ]
        scratch += [
            pltpu.VMEM(full(own_small), LOW),
            pltpu.VMEM((3,) + full(own_parts), LOW),
            pltpu.VMEM(own_edge.shape, LOW),
            pltpu.VMEM(own_docs.shape, F32),
            pltpu.VMEM(own_docs.shape, F32),
            pltpu.VMEM((rows, model), LOW),
            pltpu.VMEM((2,) + own_par.shape, F32),
            sem(3),
            sem(3),
            sem(2),
            sem(4),
        ] + Gathering.scratch(depth) * 5
        in_specs += [VMEM_SPEC] * 6 + [ANY_SPEC]
        args += [own_small, own_parts, own_exit, own_par, own_edge, own_docs, cot]
    else:
        small, parts, exits, par, heads, edge, docs, cot_t = gather(*packs, cot)
        weights = parts.reshape(3, 2, model, 2 * WIDE)
        block = lambda at: pl.BlockSpec(
            (1, 1, model, WIDE), lambda s: (turn_of(s)[2], turn_of(s)[1], 0, at)
        )
        in_specs += [block(0), block(1), const((2, model, WIDE))] + [VMEM_SPEC] * 4
        args += [weights, weights, small.reshape(2, model, WIDE), par, heads, edge, docs]
    results = pl.pallas_call(
        functools.partial(entry_body, depth, rounds, fused),
        out_shape=[out[0] for out in outs],
        grid=(GROUPS + 1,),
        in_specs=in_specs,
        out_specs=[out[1] for out in outs],
        scratch_shapes=scratch,
        compiler_params=params(collective_id=1, has_side_effects=True),
        name="entry",
    )(*args)
    if fused:
        small, parts, exits, par, heads, cot_t = results[18:]
    return tuple(results[:18]), (
        small.reshape(2, model, WIDE),
        parts.reshape(3, 2, model, 2 * WIDE),
        exits.reshape(2, model, -1),
        par,
        heads,
        cot_t,
    )


def middle_body(
    tokens, cot, cot_t, hidden_t, pre_ref, gate_ref, loc_ref, carry_ref, w_exit, par, par_heads, bc,
    bct, score, mask, sp, cumt, fac, block_out, exit_out, gate_part_out, dy_out, gpg_out, enter_out, row_out,
    skip_out, outputs, gates, unit_grads, mixes, sums, total
):
    step = pl.program_id(0)
    rows = pre_ref.shape[0]
    spans = rows // Q
    wide = 6 * WIDE

    @pl.when(step == 0)
    def _():
        sums[...] = jnp.zeros_like(sums)
        total[...] = jnp.zeros_like(total)
        skip_out[...] = jnp.zeros_like(skip_out)

    @pl.when(step < 6)
    def _():
        group = step
        spread = spreader(4 * group, HEAD, 4)
        pre = pre_ref[...]
        mix = pre * sigmoid(pre)
        mixes[group] = mix
        value = mix * mm(sp[0], spread)
        growth = mm(sp[2], spread)
        facx = mm(split3(fac[...]), spread)
        cums = mm(sp[1], spreader(4 * group, LANES, 4))
        skipx = mm(split3(par_heads[...]), spread)[2:3]
        state = carry_ref[...].astype(F32)
        half = iota((Q, LANES), 1) < HEAD
        for index in range(spans):
            at = slice(index * Q, (index + 1) * Q)
            carried = mm(bc[at, LANES:], state.astype(LOW)) * growth[at]
            parts = []
            for pair in range(2):
                lanes = slice(pair * LANES, (pair + 1) * LANES)
                local = None
                for side in range(2):
                    head = 2 * pair + side
                    across = cumt[group, head : head + 1, at]
                    spread_at = cums[at, head * LANES : (head + 1) * LANES] - across + mask[at]
                    weight = (jnp.exp2(spread_at) * score[at]).astype(LOW)
                    keep = half if side == 0 else jnp.logical_not(half)
                    seen = jnp.where(keep, value[at, lanes], 0.0).astype(LOW)
                    part = mm(weight, seen)
                    local = part if local is None else local + part
                parts.append(local)
            out = jnp.concatenate(parts, axis=1) + carried + skipx * mix[at]
            outputs[group, at] = out
            state = facx[index : index + 1] * state + loc_ref[at]
        gate = gate_ref[...]
        gates[group] = gate
        gated = outputs[group] * (gate * sigmoid(gate))
        unit_grad = mm(cot[0], w_exit[0])
        unit_grads[group] = unit_grad
        square = gated * gated
        cross = unit_grad * par[0, 5:6] * gated
        sums[0] += square[:, :LANES] + square[:, LANES:]
        sums[1] += cross[:, :LANES] + cross[:, LANES:]

    @pl.when(step == 5)
    def _():
        square = jnp.sum(sums[0], axis=1, keepdims=True)
        cross = jnp.sum(sums[1], axis=1, keepdims=True)
        normal = lax.rsqrt(square / wide + EPSILON)
        sums[0] = jnp.broadcast_to(normal, (rows, LANES))
        sums[1] = jnp.broadcast_to(normal * normal * normal * cross / wide, (rows, LANES))

    @pl.when(step >= 6)
    def _():
        group = step - 6
        spread = spreader(4 * group, HEAD, 4)
        normal = twice(sums[0])
        pull = twice(sums[1])
        gain = par[0, 5:6]
        gate = gates[group]
        out = outputs[group]
        unit_grad = unit_grads[group]
        sigma = sigmoid(gate)
        act = gate * sigma
        gated = out * act
        scaled_in = gated * normal
        unit = (scaled_in * gain).astype(LOW)
        total[...] += mm_nt(unit, w_exit[0])
        exit_out[0] = mm(cot_t[...], unit).astype(LOW)
        gate_sum = jnp.sum(unit_grad * scaled_in, axis=0, keepdims=True)
        gated_grad = normal * (unit_grad * gain) - pull * gated
        dy = gated_grad * act
        dy_out[...] = dy
        gate_grad = (gated_grad * out * sigma * (1.0 + gate * (1.0 - sigma))).astype(LOW)
        gpg_out[...] = gate_grad
        gate_part_out[0] = mm(hidden_t[...], gate_grad).astype(LOW)
        skip_sum = jnp.sum(dy * mixes[group], axis=0, keepdims=True)
        row_out[...] = jnp.broadcast_to(gate_sum, (8, WIDE))
        skip_out[...] += head_sums(
            jnp.broadcast_to(skip_sum, (8, WIDE)), gatherer(4 * group, HEAD, 4)
        )
        facx = mm(split3(fac[...]), spread)
        pushed = (dy * mm(sp[2], spread)).astype(LOW)
        enter = jnp.zeros((NSTATE, WIDE), F32)
        for index in reversed(range(spans)):
            at = slice(index * Q, (index + 1) * Q)
            enter = facx[index : index + 1] * enter + mm(bct[NSTATE:, at], pushed[at])
        enter_out[...] = enter

    @pl.when(step == 11)
    def _():
        block_out[...] = (tokens[0].astype(F32) + total[...]).astype(LOW)


def middle(
    tokens, cot, cot_t, hidden_t, pre, gate, loc, carry, weights, par, par_heads, bc, bct, score, mask,
    sp, cumt, fac
):
    rows, model = tokens.shape[1:]
    wide = 6 * WIDE
    shape = jax.ShapeDtypeStruct

    def early(s):
        return jnp.minimum(s, 5)

    def late(s):
        return jnp.maximum(s - 6, 0)

    def group(s):
        return s % 6

    outs = (
        (shape((rows, model), LOW), const((rows, model))),
        (
            shape((2, model, 3 * WIDE), LOW),
            pl.BlockSpec((1, model, WIDE), lambda s: (late(s) // 3, 0, late(s) % 3)),
        ),
        (
            shape((2, model, 3 * WIDE), LOW),
            pl.BlockSpec((1, model, WIDE), lambda s: (late(s) // 3, 0, late(s) % 3)),
        ),
        (shape((rows, wide), F32), pl.BlockSpec((rows, WIDE), lambda s: (0, late(s)))),
        (shape((rows, wide), LOW), pl.BlockSpec((rows, WIDE), lambda s: (0, late(s)))),
        (shape((NSTATE, wide), F32), pl.BlockSpec((NSTATE, WIDE), lambda s: (0, late(s)))),
        (shape((8, wide), F32), pl.BlockSpec((8, WIDE), lambda s: (0, late(s)))),
        (shape((8, LANES), F32), const((8, LANES))),
    )
    return pl.pallas_call(
        middle_body,
        out_shape=[out[0] for out in outs],
        grid=(12,),
        in_specs=[
                pl.BlockSpec((1, rows, model), lambda s: (side(), 0, 0)),
                pl.BlockSpec((1, rows, model), lambda s: (side(), 0, 0)),
                const((model, rows)),
                const((model, rows)),
                pl.BlockSpec((rows, WIDE), lambda s: (0, early(s))),
                pl.BlockSpec((rows, WIDE), lambda s: (0, early(s))),
                pl.BlockSpec((rows, WIDE), lambda s: (0, early(s))),
                pl.BlockSpec((NSTATE, WIDE), lambda s: (0, early(s))),
                pl.BlockSpec((1, model, WIDE), lambda s: (group(s) // 3, 0, group(s) % 3)),
                pl.BlockSpec((1, 8, WIDE), lambda s: (group(s) // 3, 0, group(s) % 3)),
                const((8, LANES)),
                const((rows, WIDE)),
                const((WIDE, rows)),
                const((rows, Q)),
                const((rows, Q)),
                const((4, rows, LANES)),
                const((6, 8, rows)),
                const((8, LANES)),
        ],
        out_specs=[out[1] for out in outs],
        scratch_shapes=[
                pltpu.VMEM((6, rows, WIDE), F32),
                pltpu.VMEM((6, rows, WIDE), F32),
                pltpu.VMEM((6, rows, WIDE), F32),
                pltpu.VMEM((6, rows, WIDE), F32),
                pltpu.VMEM((2, rows, LANES), F32),
                pltpu.VMEM((rows, model), F32),
        ],
        compiler_params=params(),
        name="middle",
    )(
        tokens, cot, cot_t, hidden_t, pre, gate, loc, carry, weights, par, par_heads, bc, bct, score,
        mask, sp, cumt, fac,
    )


def scan_back_body(depth, rounds, fused, *refs):
    (
        pre_ref, dy_ref, loc_ref, carry_ref, enter, cin_ref, par, par_heads, state_filter, cin_state,
        pre_state, bc, bct, score, mask, sp, cumt, fac, match, zst, dt_ref, exits, gate_part,
        block_own, tokens, cot, hidden_t, gpg, w_gate, w_inner, w_small, gate_row, skip_row,
    ) = refs[:33]
    mine, block_out = refs[33:35]
    if fused:
        mine2, mine3, state_out, vector_out, token_both = refs[35:40]
        refs = refs[40:]
    else:
        tap_out, tap_state_out, small_out, inner_part, small_part, token_out, norm_out = refs[35:42]
        refs = refs[42:]
    (
        d_bc, d_score, d_cum, heads, local_value, enters, gains, adjoints, edge_own, edge_in, grads,
        total, es, el, bs, bl, block_keep,
    ) = refs[:17]
    scratch = refs[17:42]
    step = pl.program_id(0)
    group, half_at, part_at = group_of(jnp.minimum(step, GROUPS - 1))
    last_group, last_half, last_part = group_of(jnp.maximum(step - 1, 0))
    blocks = BLOCK_CUTS
    rows = pre_ref.shape[0]
    spans = rows // Q
    place = Place(depth)
    wide = exits.shape[-1]
    chaining = Chaining(place, rounds, True, enters, gains, scratch[:4], scratch[4:8])
    reducing = Reducing(
        place, 0, [(exits, slice(0, wide)), (gate_part, slice(wide, 2 * wide))], mine,
        scratch[8:16], scratch[16:25],
    )
    if fused:
        inner_v, small_v, token_v, taps_v = refs[42:46]
        buffers = refs[46:]
        second = Reducing(
            place, 0, [(inner_v.at[0], slice(0, WIDE)), (inner_v.at[1], slice(WIDE, 2 * WIDE))],
            mine2, buffers[:8], buffers[8:17],
        )
        third = Reducing(
            place, 0, [(inner_v.at[2], slice(0, WIDE)), (small_v, slice(WIDE, 2 * WIDE))], mine3,
            buffers[17:25], buffers[25:34],
        )
        closing = Closing(place, token_v, token_both, buffers[34:])
    position = place.position
    has_before, has_after = position > 0, position < 2 * depth - 1
    before, after = {"context": position - 1}, {"context": position + 1}
    share = rows // blocks

    def block_copy(index):
        at = pl.ds(pl.multiple_of(index * share, share), share)
        return remote(
            block_own.at[at], block_out.at[place.y, at], bs.at[index], bl.at[index], place.y_peer
        )

    block_local = pltpu.make_async_copy(block_own, block_out.at[place.y], block_keep.at[0])

    def edge_copy(index):
        return remote(edge_own.at[index], edge_in.at[index], es.at[index], el.at[index], before)

    def edge_wait(index):
        @pl.when(has_after)
        def _():
            edge_copy(index).wait_recv()

    def put_inner(value):
        if fused:
            inner_v[last_part, last_half] = value.reshape(inner_v.shape[2:])
        else:
            inner_part[0] = value

    def joined(index):
        grad = grads[...]
        return jnp.concatenate(
            [grad[: rows - EDGE], grad[rows - EDGE :] + edge_in[index]], axis=0
        ).astype(LOW)

    @pl.when(step == 0)
    def _():
        d_bc[...] = jnp.zeros_like(d_bc)
        d_score[...] = jnp.zeros_like(d_score)
        d_cum[...] = jnp.zeros_like(d_cum)
        heads[...] = jnp.zeros_like(heads)
        grads[...] = jnp.zeros_like(grads)
        total[...] = jnp.zeros_like(total)
        edge_in[GROUPS + 1] = jnp.zeros((EDGE, WIDE), F32)

        @pl.when(jnp.logical_not(has_after))
        def _():
            edge_in[...] = jnp.zeros_like(edge_in)

        place.greet(
            [place.mate, place.x_peer, place.y_peer],
            chaining.sometimes() + [(has_before, before), (has_after, after)],
            True,
        )
        facs = split3(fac[...])
        for cut in range(GROUPS):
            enters[cut] = enter[:, cut * WIDE : (cut + 1) * WIDE]
            chaining.open(cut)
        for cut in range(GROUPS):
            rows8 = mm(facs, spreader(4 * cut, HEAD, 4))
            gains[cut] = jnp.broadcast_to(rows8[spans : spans + 1], (8, WIDE))
        each(depth, reducing.start)
        block_local.start()
        each(3, lambda index: block_copy(index).start())
        for cut in range(GROUPS):
            chaining.pass_on(0, cut)

    if fused:

        @pl.when(step == 5)
        def _():
            each(depth, second.start)

    @pl.when(step < GROUPS)
    def _():
        spread = spreader(4 * group, HEAD, 4)
        collect = gatherer(4 * group, HEAD, 4)
        pre = pre_ref[...]
        sigma = sigmoid(pre)
        mix = pre * sigma
        dtx = mm(sp[0], spread)
        growth = mm(sp[2], spread)
        facx = mm(split3(fac[...]), spread)
        cums = mm(sp[1], spreader(4 * group, LANES, 4))
        half = iota((Q, LANES), 1) < HEAD
        ones = jnp.ones((8, Q), F32).astype(LOW)
        states = [carry_ref[...].astype(F32)]
        for index in range(spans - 1):
            at = slice(index * Q, (index + 1) * Q)
            states.append(facx[index : index + 1] * states[-1] + loc_ref[at])
        for index in range(spans):
            at = slice(index * Q, (index + 1) * Q)
            dy = dy_ref[at]
            value = mix[at] * dtx[at]
            parts = []
            sum_score = None
            for pair in range(2):
                lanes = slice(pair * LANES, (pair + 1) * LANES)
                value_low = value[:, lanes].astype(LOW)
                local = None
                for part_of in range(2):
                    head = 2 * pair + part_of
                    across = cumt[group, head : head + 1, at]
                    spread_at = cums[at, head * LANES : (head + 1) * LANES] - across + mask[at]
                    decay = jnp.exp2(spread_at)
                    keep = half if part_of == 0 else jnp.logical_not(half)
                    dy_low = jnp.where(keep, dy[:, lanes], 0.0).astype(LOW)
                    inner = decay * mm_nt(dy_low, value_low)
                    sum_score = inner if sum_score is None else sum_score + inner
                    moved = (inner * score[at]).astype(LOW)
                    turn = mm_nt(ones, moved) - mm(ones, moved)
                    d_cum[group, head : head + 1, at] = turn[0:1]
                    part = mm_tn((decay * score[at]).astype(LOW), dy_low)
                    local = part if local is None else local + part
                parts.append(local)
            d_score[at] += sum_score
            local_value[at] = jnp.concatenate(parts, axis=1)
            pushed = dy * growth[at]
            state_low = states[index].astype(LOW)
            carried = mm(bc[at, LANES:], state_low)
            d_bc[at, LANES:] += mm_nt(pushed.astype(LOW), state_low)
            heads[1, at] += head_sums(pushed * carried, collect)

    @pl.when(step == 0)
    def _():
        for cut in range(GROUPS):
            chaining.relay(0, cut)
        chaining.later()

        def put(cut, value):
            adjoints[cut] = value

        chaining.arrive(put)
        chaining.finish()

    for turn in range(5):

        @pl.when(step == turn)
        def _():
            each(turn + 1 if turn < 4 else depth + 1, reducing.turn, turn)
            block_copy(turn + 3).start()

    @pl.when(step == 5)
    def _():
        reducing.close()
        if fused:
            second.turn(0)

    @pl.when((step > 0) & (step < GROUPS))
    def _():
        edge_wait(last_group)

    @pl.when(step < GROUPS)
    def _():
        spread = spreader(4 * group, HEAD, 4)
        collect = gatherer(4 * group, HEAD, 4)
        pre = pre_ref[...]
        sigma = sigmoid(pre)
        mix = pre * sigma
        dtx = mm(sp[0], spread)
        growth = mm(sp[2], spread)
        facx = mm(split3(fac[...]), spread)
        states = [carry_ref[...].astype(F32)]
        for index in range(spans - 1):
            at = slice(index * Q, (index + 1) * Q)
            states.append(facx[index : index + 1] * states[-1] + loc_ref[at])
        arrived = jnp.where(step > 0, last_group, GROUPS + 1)
        grad = joined(arrived)
        gate_grad = gpg[...]
        put_inner(mm(hidden_t[...], grad).astype(LOW))
        total[...] += mm_nt(gate_grad, w_gate[0, 0]) + mm_nt(grad, w_inner[0, 0])
        tails = mm(sp[3], spread)
        skipx = mm(split3(par_heads[...]), spread)[2:3]
        adjoint = adjoints[group].astype(F32)
        masks = [match[back] for back in range(CONV - 1)]
        pgs = [None] * spans
        for index in reversed(range(spans)):
            at = slice(index * Q, (index + 1) * Q)
            dy = dy_ref[at]
            value = mix[at] * dtx[at]
            adj_low = adjoint.astype(LOW)
            reached = mm(bc[at, :LANES], adj_low) * tails[at]
            d_bc[at, :LANES] += mm_nt((value * tails[at]).astype(LOW), adj_low)
            heads[0, at] += head_sums(value * reached, collect)
            fac_part = jnp.sum(adjoint * states[index], axis=0, keepdims=True)
            heads[3, index * 8 : index * 8 + 8] += head_sums(
                jnp.broadcast_to(fac_part, (8, WIDE)), collect
            )
            pushed_low = (dy * growth[at]).astype(LOW)
            adjoint = facx[index : index + 1] * adjoint + mm(bct[NSTATE:, at], pushed_low)
            d_value = local_value[at] + reached
            heads[2, at] += head_sums(mix[at] * d_value, collect)
            d_mix = dtx[at] * d_value + skipx * dy
            s = sigma[at]
            pgs[index] = d_mix * s * (1.0 + pre[at] * (1.0 - s))
        pg = jnp.concatenate(pgs, axis=0)
        sums, grad = conv_backward(pg, cin_ref[...].astype(F32), par[0], masks)
        taps8 = jnp.concatenate(sums + [jnp.zeros((3, WIDE), F32)], axis=0)
        if fused:
            taps_v[group] = taps8
        else:
            tap_out[...] = taps8
        grads[...] = grad[HALO:]
        edge_own[group] = grad[HALO - EDGE : HALO]

        @pl.when(has_before)
        def _():
            edge_copy(group).start()

    @pl.when(step == GROUPS)
    def _():
        if fused:
            second.turn(1)
        masks = [match[back] for back in range(CONV - 1)]
        edge_wait(GROUPS - 1)
        grad = joined(GROUPS - 1)
        put_inner(mm(hidden_t[...], grad).astype(LOW))
        total[...] += mm_nt(grad, w_inner[0, 0])
        t_at, u_at = iota((Q, Q), 0), iota((Q, Q), 1)
        onward = (t_at <= u_at).astype(F32)
        earlier = (t_at > u_at).astype(F32)
        rate = jnp.exp(par_heads[1:2])
        raws = []
        bias_sum = jnp.zeros((1, LANES), F32)
        decay_sum = jnp.zeros((1, LANES), F32)
        used = iota((Q, LANES), 1) < 24
        for index in range(spans):
            at = slice(index * Q, (index + 1) * Q)
            pieces = [d_cum[piece, 0:4, at] for piece in range(6)]
            pieces.append(jnp.zeros((LANES - 24, Q), F32))
            cum_col = jnp.transpose(jnp.concatenate(pieces, axis=0))
            fac_row = fac[index : index + 1] * heads[3, index * 8 : index * 8 + 1]
            d_decay = (
                mm_exact(onward, cum_col + heads[1, at]) + mm_exact(earlier, heads[0, at]) + fac_row
            )
            dt = dt_ref[at]
            raw = (heads[2, at] - d_decay * rate) * sigmoid(zst[at])
            raw = jnp.where(used, raw, 0.0)
            raws.append(raw.astype(LOW))
            bias_sum += jnp.sum(raw, axis=0, keepdims=True)
            decay_sum -= jnp.sum(
                jnp.where(used, d_decay * dt * rate, 0.0), axis=0, keepdims=True
            )
            score_low = d_score[at].astype(LOW)
            d_bc[at, :LANES] += mm_tn(score_low, bc[at, LANES:])
            d_bc[at, LANES:] += mm(score_low, bc[at, :LANES])
        if not fused:
            small_out[...] = jnp.concatenate(
                [bias_sum, decay_sum, jnp.zeros((6, LANES), F32)], axis=0
            )
        if fused:
            second.turn(2)
        pre = pre_state[...]
        s = sigmoid(pre)
        pg = d_bc[...] * s * (1.0 + pre * (1.0 - s))
        sums, grad = conv_backward(pg, cin_state[...].astype(F32), state_filter[...], masks)
        taps8 = jnp.concatenate(sums + [jnp.zeros((3, WIDE), F32)], axis=0)
        if fused:
            taps_v[GROUPS] = taps8
        else:
            tap_state_out[...] = taps8
        grads[...] = grad[HALO:]
        edge_own[GROUPS] = grad[HALO - EDGE : HALO]

        @pl.when(has_before)
        def _():
            edge_copy(GROUPS).start()

        steps = jnp.concatenate(raws, axis=0)
        turned = hidden_t[...]
        step_part = mm(turned, steps).astype(LOW)
        total[...] += mm_nt(steps, w_small[0, :, LANES:]) + mm_nt(steps, w_small[1, :, LANES:])
        edge_wait(GROUPS)
        state = joined(GROUPS)
        state_part = mm(turned, state).astype(LOW)
        for index in range(2):
            state_half = state_part[:, index * LANES : (index + 1) * LANES]
            value = jnp.concatenate([state_half, step_part], axis=1)
            if fused:
                small_v[index] = value.reshape(small_v.shape[1:])
            else:
                small_part[index] = value
        if fused:
            each(depth, third.start)
        value = tokens[0].astype(F32)
        scale = lax.rsqrt(jnp.mean(value * value, axis=1, keepdims=True) + EPSILON)
        hidden_grad = (
            total[...]
            + mm_nt(state[:, :LANES], w_small[0, :, :LANES])
            + mm_nt(state[:, LANES:], w_small[1, :, :LANES])
        )
        norm_sum = jnp.sum(hidden_grad * (value * scale), axis=0, keepdims=True)
        if not fused:
            norm_out[...] = jnp.broadcast_to(norm_sum, norm_out.shape)
        gain = jnp.transpose(w_small[0, :, LANES : 2 * LANES].astype(F32))[24:25]
        normed = hidden_grad * gain
        pull = jnp.sum(normed * value, axis=1, keepdims=True) / value.shape[1]
        token_low = (
            cot[0].astype(F32) + scale * normed - (scale * scale * scale) * value * pull
        ).astype(LOW)
        if fused:
            token_v[...] = token_low
            for index in range(GROUPS + 1):
                at = slice(index * WIDE, (index + 1) * WIDE)
                closing.send[0, : CONV + 1, at] = taps_v[index, : CONV + 1]
            high = GROUPS * WIDE
            closing.send[0, CONV + 1 :] = jnp.zeros((8 - CONV - 1, high + WIDE), F32)
            closing.send[0, 5:6, :high] = gate_row[0:1]
            closing.send[0, 5:6, high : high + LANES] = bias_sum
            closing.send[0, 5:6, high + LANES :] = skip_row[0:1]
            model = norm_sum.shape[1]
            closing.send[0, 6:7, :model] = norm_sum
            closing.send[0, 6:7, model : model + LANES] = decay_sum
            closing.run(third, NSTATE, state_out, vector_out, WIDE, second)
            second.finish()
        else:
            token_out[...] = token_low
        reducing.finish()
        each(blocks, lambda index: block_copy(index).wait())
        block_local.wait()

        @pl.when(has_before)
        def _():
            each(GROUPS + 1, lambda index: edge_copy(index).wait_send())


def scan_back(
    pre, dy, loc, carry, enter, cin, par, par_heads, state_filter, cin_state, pre_state, bc, bct,
    score, mask, sp, cumt, fac, match, zst, dt, exits, gate_part, block_own, tokens, cot, hidden_t,
    gpg, parts, small, gate_row, skip_row, rounds
):
    rows, wide = pre.shape
    ext = rows + HALO
    depth = lax.axis_size("context") // 2
    own_rows, half_wide = exits.shape[3:]
    shape = jax.ShapeDtypeStruct
    sem = lambda *lead: pltpu.SemaphoreType.DMA(lead)
    model = tokens.shape[2]
    count = 2 * depth
    fused = own_rows % 16 == 0
    now = lambda s: group_of(jnp.minimum(s, GROUPS - 1))
    lag = lambda s: group_of(jnp.maximum(s - 1, 0))
    column = lambda count: pl.BlockSpec((count, WIDE), lambda s: (0, now(s)[0]))
    whole = lambda *dims, dtype=F32: (shape(dims, dtype), const(dims))
    outs = [
        whole(own_rows, 2 * half_wide),
        (shape((2,) + block_own.shape, LOW), ANY_SPEC),
    ]
    if fused:
        outs += [
            whole(own_rows, 2 * WIDE),
            whole(own_rows, 2 * WIDE),
            whole(2, own_rows, NSTATE),
            whole(8, wide + WIDE),
            (shape((2, rows, model), LOW), ANY_SPEC),
        ]
        extra = (
            [
                pltpu.VMEM((3, 2, 2, count, own_rows, WIDE), LOW),
                pltpu.VMEM((2, 2, count, own_rows, WIDE), LOW),
                pltpu.VMEM((rows, model), LOW),
                pltpu.VMEM((GROUPS + 1, 8, WIDE), F32),
            ]
            + Reducing.scratch(depth, own_rows, 2 * WIDE) * 2
            + Closing.scratch(depth, own_rows, (8, wide + WIDE))
        )
    else:
        outs += [
            (shape((8, wide), F32), column(8)),
            whole(8, WIDE),
            whole(8, LANES),
            (
                shape((2, model, 3 * WIDE), LOW),
                pl.BlockSpec((1, model, WIDE), lambda s: (lag(s)[1], 0, lag(s)[2])),
            ),
            whole(2, model, WIDE, dtype=LOW),
            whole(rows, model, dtype=LOW),
            whole(8, model),
        ]
        extra = []
    return pl.pallas_call(
        functools.partial(scan_back_body, depth, rounds, fused),
        out_shape=[out[0] for out in outs],
        grid=(GROUPS + 1,),
        in_specs=[
            column(rows),
            column(rows),
            column(rows),
            column(NSTATE),
            const((NSTATE, wide)),
            column(ext),
            pl.BlockSpec((1, 8, WIDE), lambda s: (now(s)[1], 0, now(s)[2])),
            const((8, LANES)),
            const((CONV + 1, WIDE)),
            const((ext, WIDE)),
            const((rows, WIDE)),
            const((rows, WIDE)),
            const((WIDE, rows)),
            const((rows, Q)),
            const((rows, Q)),
            const((4, rows, LANES)),
            const((6, 8, rows)),
            const((8, LANES)),
            const((CONV - 1, rows, LANES)),
            const((rows, LANES)),
            const((rows, LANES)),
            ANY_SPEC,
            ANY_SPEC,
            VMEM_SPEC,
            pl.BlockSpec((1, rows, model), lambda s: (side(), 0, 0)),
            pl.BlockSpec((1, rows, model), lambda s: (side(), 0, 0)),
            const((model, rows)),
            column(rows),
            pl.BlockSpec((1, 1, model, WIDE), lambda s: (now(s)[2], now(s)[1], 0, 0)),
            pl.BlockSpec((1, 1, model, WIDE), lambda s: (lag(s)[2], lag(s)[1], 0, 1)),
            const((2, model, WIDE)),
            const((8, wide)),
            const((8, LANES)),
        ],
        out_specs=[out[1] for out in outs],
        scratch_shapes=[
            pltpu.VMEM((rows, WIDE), F32),
            pltpu.VMEM((rows, Q), F32),
            pltpu.VMEM((6, 8, rows), F32),
            pltpu.VMEM((4, rows, LANES), F32),
            pltpu.VMEM((rows, WIDE), F32),
            pltpu.VMEM((GROUPS, NSTATE, WIDE), F32),
            pltpu.VMEM((GROUPS, 8, WIDE), F32),
            pltpu.VMEM((GROUPS, NSTATE, WIDE), LOW),
            pltpu.VMEM((GROUPS + 1, EDGE, WIDE), F32),
            pltpu.VMEM((GROUPS + 2, EDGE, WIDE), F32),
            pltpu.VMEM((rows, WIDE), F32),
            pltpu.VMEM((rows, model), F32),
            sem(GROUPS + 1),
            sem(GROUPS + 1),
            sem(BLOCK_CUTS),
            sem(BLOCK_CUTS),
            sem(1),
        ]
        + Chaining.scratch(rounds)
        + Reducing.scratch(depth, own_rows, 2 * half_wide)
        + extra,
        compiler_params=params(collective_id=2, has_side_effects=True),
        name="scan_back",
    )(
        pre, dy, loc, carry, enter, cin, par, par_heads, state_filter, cin_state, pre_state, bc,
        bct, score, mask, sp, cumt, fac, match, zst, dt, exits, gate_part, block_own, tokens, cot,
        hidden_t, gpg, parts, parts, small, gate_row, skip_row,
    )


def pack_body(
    entry, exits, state, steps, gain, inner_kernel, gate_gain, bias, decay, skip, docs,
    tail_tokens, packed_small, packed_parts, packed_exit, par, doc_col, doc_row, edge, docs_own
):
    half_of = side()
    rows = entry.shape[0]
    wide = entry.shape[2]

    def placed(filled, used):
        return jnp.where(half_of == 0, filled, pltpu.roll(filled, used, 1))

    def widened(value):
        return jnp.concatenate(
            [value, jnp.zeros((value.shape[0], LANES - value.shape[1]), F32)], axis=1
        )

    for part in range(3):
        at = slice(part * WIDE, (part + 1) * WIDE)
        packed_parts[part, :, :WIDE] = entry[:, 0, at].astype(LOW)
        packed_parts[part, :, WIDE:] = entry[:, 1, at].astype(LOW)
    half = jnp.where(half_of == 0, state[:, :NSTATE], state[:, NSTATE:])
    packed_small[:, :NSTATE] = half.astype(LOW)
    gain_row = jnp.concatenate([gain[...], jnp.zeros((1, LANES - rows), F32)], axis=1)
    gain_col = jnp.transpose(jnp.broadcast_to(gain_row, (LANES, LANES)))[:rows]
    lane = iota((rows, LANES), 1)
    heads_here = steps.shape[0]
    step_rows = jnp.concatenate([steps[...], jnp.zeros((heads_here, LANES - rows), F32)], axis=1)
    step_rows = jnp.concatenate([step_rows, jnp.zeros((LANES - heads_here, LANES), F32)], axis=0)
    step_cols = jnp.transpose(step_rows)[:rows]
    small = jnp.where(lane == 24, gain_col, placed(step_cols, heads_here))
    packed_small[:, NSTATE:] = small.astype(LOW)
    packed_exit[...] = exits[...].astype(LOW)
    par[0 : CONV + 1] = inner_kernel[...]
    for index in range(wide // LANES):
        at = slice(index * LANES, (index + 1) * LANES)
        par[CONV + 1 : CONV + 2, at] = gate_gain[index : index + 1]
    par[CONV + 2 : CONV + 4] = jnp.zeros((2, wide), F32)
    for index, ref in enumerate((bias, decay, skip)):
        par[CONV + 2 : CONV + 3, index * LANES : (index + 1) * LANES] = placed(
            widened(ref[...]), ref.shape[1]
        )
    own = jnp.where(half_of == 0, docs[0:1], docs[1:2]).astype(F32)
    doc_row[...] = jnp.broadcast_to(own, doc_row.shape)
    doc_col[...] = jnp.transpose(jnp.broadcast_to(own, (LANES, own.shape[1])))
    docs_own[...] = doc_col[own.shape[1] - HALO :]
    edge[...] = tail_tokens[0]


def pack(
    entry, exits, state, steps, gain, inner_kernel, gate_gain, bias, decay, skip, docs, tokens
):
    own_rows, _, wide = entry.shape
    rows, model = tokens.shape[1:]
    shape = jax.ShapeDtypeStruct
    arrays = (
        entry, exits, state, steps.T, gain[None], inner_kernel, gate_gain.reshape(-1, LANES), bias[None],
        decay[None], skip[None], docs,
    )
    outs = (
        shape((own_rows, WIDE), LOW),
        shape((3, own_rows, 2 * WIDE), LOW),
        shape((own_rows, wide), LOW),
        shape((8, wide), F32),
        shape((rows, LANES), F32),
        shape((8, rows), F32),
        shape((HALO, model), LOW),
        shape((HALO, LANES), F32),
    )
    return pl.pallas_call(
        pack_body,
        out_shape=outs,
        grid=(1,),
        in_specs=[const(array.shape) for array in arrays]
        + [pl.BlockSpec((1, HALO, model), lambda s: (side(), rows // HALO - 1, 0))],
        out_specs=[const(out.shape) for out in outs],
        compiler_params=params(),
        name="pack",
    )(*arrays, tokens)


def gather_body(
    depth, own_small, own_parts, own_exit, par_own, edge_own, docs_own, cot, small, parts, exits, par,
    heads, edge, docs, cot_t, docs_in, cot_in, side_send, side_land, local, *marks
):
    place = Place(depth)
    count = 2 * depth
    onward = {"context": lax.rem(place.position + 1, count)}
    behind = {"context": lax.rem(place.position + count - 1, count)}
    y = place.y
    place.greet([place.mate, place.x_peer, place.y_peer, onward, behind], (), True)
    own = [own_small, own_parts.at[0], own_parts.at[1], own_parts.at[2], own_exit]
    full = [small, parts.at[0], parts.at[1], parts.at[2], exits]
    pieces = [Gathering(place, own[i], full[i], *marks[3 * i : 3 * i + 3]) for i in range(5)]
    sides = [
        remote(edge_own, edge, side_send.at[0], side_land.at[0], onward),
        remote(docs_own, docs_in, side_send.at[1], side_land.at[1], onward),
        remote(par_own, par.at[y], side_send.at[2], side_land.at[2], place.y_peer),
    ]
    for copy in sides:
        copy.start()
    cot_copy = pltpu.make_async_copy(cot.at[y], cot_in, local.at[1])
    cot_copy.start()
    par_keep = pltpu.make_async_copy(par_own, par.at[y], local.at[0])
    par_keep.start()
    for piece in pieces:
        piece.own()
    cot_copy.wait()
    cot_t[...] = jnp.transpose(cot_in[...])
    for piece in pieces:
        piece.near()
        piece.across()
        piece.far()
    for copy in sides:
        copy.wait()
    docs[...] = jnp.where(place.position == 0, -1.0, docs_in[...])
    par_keep.wait()
    both = par[0, CONV + 2 : CONV + 3] + par[1, CONV + 2 : CONV + 3]
    heads[...] = jnp.zeros_like(heads)
    for index in range(3):
        heads[index : index + 1] = both[:, index * LANES : (index + 1) * LANES]
    for piece in pieces:
        piece.mates()
        piece.finish()


def gather(own_small, own_parts, own_exit, par_own, edge_own, docs_own, cot):
    count = lax.axis_size("context")
    depth = count // 2
    rows, model = cot.shape[1:]
    shape = jax.ShapeDtypeStruct
    full = lambda own: (2, 2, count) + own.shape[-2:]
    return pl.pallas_call(
        functools.partial(gather_body, depth),
        out_shape=(
            shape(full(own_small), LOW),
            shape((3,) + full(own_parts), LOW),
            shape(full(own_exit), LOW),
            shape((2,) + par_own.shape, F32),
            shape((8, LANES), F32),
            shape(edge_own.shape, LOW),
            shape(docs_own.shape, F32),
            shape((model, rows), LOW),
        ),
        in_specs=[VMEM_SPEC] * 6 + [ANY_SPEC],
        out_specs=[ANY_SPEC] * 3 + [VMEM_SPEC] * 5,
        scratch_shapes=[
            pltpu.VMEM(docs_own.shape, F32),
            pltpu.VMEM((rows, model), LOW),
            pltpu.SemaphoreType.DMA((3,)),
            pltpu.SemaphoreType.DMA((3,)),
            pltpu.SemaphoreType.DMA((2,)),
        ]
        + Gathering.scratch(depth) * 5,
        compiler_params=params(collective_id=0, has_side_effects=True),
        name="gather",
    )(own_small, own_parts, own_exit, par_own, edge_own, docs_own, cot)


def reduce_body(
    depth, inner, small, token, taps, taps_state, gate_row, head_rows, skip_row, norm_row, mine,
    state_out, vector_out, token_out, *scratch
):
    place = Place(depth)
    wide = inner.shape[-1]
    parts = [(inner, slice(0, wide)), (small, slice(wide, wide + WIDE))]
    reducing = Reducing(place, 0, parts, mine, scratch[:8], scratch[8:17])
    closing = Closing(place, token, token_out, scratch[17:])
    vec = closing.send
    vec[0] = jnp.zeros(vec.shape[1:], F32)
    vec[0, : CONV + 1, : 2 * wide] = taps[: CONV + 1]
    vec[0, : CONV + 1, 2 * wide :] = taps_state[: CONV + 1]
    vec[0, 5:6, : 2 * wide] = gate_row[0:1]
    vec[0, 5:6, 2 * wide : 2 * wide + LANES] = head_rows[0:1]
    vec[0, 5:6, 2 * wide + LANES :] = skip_row[0:1]
    model = norm_row.shape[1]
    vec[0, 6:7, :model] = norm_row[0:1]
    vec[0, 6:7, model : model + LANES] = head_rows[1:2]
    place.greet([place.mate, place.x_peer, place.y_peer], (), True)
    each(depth, reducing.start)
    closing.run(reducing, NSTATE, state_out, vector_out, wide)


def reduce_all(inner, small, token, taps, taps_state, gate_row, head_rows, skip_row, norm_row):
    depth = lax.axis_size("context") // 2
    own_rows, wide = inner.shape[3:]
    tall = wide + WIDE
    shape = jax.ShapeDtypeStruct
    vector = (8, 2 * wide + WIDE)
    return pl.pallas_call(
        functools.partial(reduce_body, depth),
        out_shape=(
            shape((own_rows, tall), F32),
            shape((2, own_rows, NSTATE), F32),
            shape(vector, F32),
            shape((2,) + token.shape, LOW),
        ),
        in_specs=[ANY_SPEC] * 2 + [VMEM_SPEC] * 7,
        out_specs=[VMEM_SPEC] * 3 + [ANY_SPEC],
        scratch_shapes=Reducing.scratch(depth, own_rows, tall)
        + Closing.scratch(depth, own_rows, vector),
        compiler_params=params(collective_id=4, has_side_effects=True),
        name="reduce_all",
    )(inner, small, token, taps, taps_state, gate_row, head_rows, skip_row, norm_row)


def finish_body(
    mine, mine_last, exits, state, vector, token, block, block_out, token_out,
    norm_out, entry_out, state_out, step_out, kernel_out, filter_out, bias_out, decay_out, skip_out,
    gate_out, exit_out
):
    half_of = side()
    spot = lax.axis_index("dp") * lax.axis_size("context") + lax.axis_index("context")
    token_out[...] = token[...].astype(F32)
    first = half_of == 0
    block_out[...] = block[...]

    @pl.when(pl.program_id(0) == 0)
    def _():
        own_rows, _, wide = entry_out.shape
        model = token.shape[2]
        entry_out[:, 0] = exits[:, wide:]
        entry_out[:, 1, : 2 * WIDE] = mine[...]
        entry_out[:, 1, 2 * WIDE :] = mine_last[:, :WIDE]
        exit_out[...] = exits[:, :wide]
        state_out[:, :NSTATE] = state[0]
        state_out[:, NSTATE:] = state[1]

        def twelve(value):
            return jnp.where(first, value, pltpu.roll(value, LANES - 12, 1))[:, :12]

        steps = jnp.where(first, mine_last[:, WIDE + NSTATE :], pltpu.roll(mine_last[:, WIDE + NSTATE :], LANES - 12, 1))
        steps = jnp.concatenate([steps, jnp.zeros((LANES - own_rows, LANES), F32)], axis=0)
        step_out[...] = jnp.transpose(steps)[:12, :own_rows]
        left, right = vector[:, :wide], vector[:, wide : 2 * wide]
        halves = jnp.where(first, left, right)
        kernel_out[...] = halves[: CONV + 1]
        for index in range(wide // LANES):
            gate_out[index : index + 1] = halves[5:6, index * LANES : (index + 1) * LANES]
        filter_out[...] = vector[: CONV + 1, 2 * wide :]
        bias_out[...] = twelve(vector[5:6, 2 * wide : 2 * wide + LANES])
        skip_out[...] = twelve(vector[5:6, 2 * wide + LANES :])
        decay_out[...] = twelve(vector[6:7, model : model + LANES])
        turned = pltpu.roll(vector[:, :model], lax.rem(model - spot * own_rows, model), 1)
        norm_out[...] = turned[6:7, :own_rows]


def finish(mine, mine_last, exits, state, vector, token, block):
    own_rows, wide = exits.shape[0], exits.shape[1] // 2
    _, rows, model = token.shape
    share = rows // 4
    shape = jax.ShapeDtypeStruct
    outs = (
        (shape((2, rows, model), LOW), pl.BlockSpec((2, share, model), lambda s: (0, s, 0))),
        (shape((2, rows, model), F32), pl.BlockSpec((2, share, model), lambda s: (0, s, 0))),
        (shape((1, own_rows), F32), None),
        (shape((own_rows, 2, wide), F32), None),
        (shape((own_rows, WIDE), F32), None),
        (shape((12, own_rows), F32), None),
        (shape((CONV + 1, wide), F32), None),
        (shape((CONV + 1, WIDE), F32), None),
        (shape((1, 12), F32), None),
        (shape((1, 12), F32), None),
        (shape((1, 12), F32), None),
        (shape((wide // LANES, LANES), F32), None),
        (shape((own_rows, wide), F32), None),
    )
    return pl.pallas_call(
        finish_body,
        out_shape=[out[0] for out in outs],
        grid=(4,),
        in_specs=[
            const(mine.shape),
            const(mine_last.shape),
            const(exits.shape),
            const(state.shape),
            const(vector.shape),
            pl.BlockSpec((2, share, model), lambda s: (0, s, 0)),
            pl.BlockSpec((2, share, model), lambda s: (0, s, 0)),
        ],
        out_specs=[out[1] if out[1] is not None else const(out[0].shape) for out in outs],
        compiler_params=params(),
        name="finish",
    )(mine, mine_last, exits, state, vector, token, block)


def body(
    tokens, documents, norm_gain, entry_weight, state_weight, step_weight, inner_kernel,
    state_filter, step_bias, decay_log, skip_gain, gate_gain, exit_weight, cotangent,
):
    seqs, rows, model = tokens.shape
    count = lax.axis_size("context")
    own_rows = norm_gain.shape[0]
    longest = rows * count // 4
    rounds = min(count // 2 - 1, -(-(longest - 1) // (2 * rows)))

    own_small, own_parts, own_exit, own_par, doc_col, doc_row, own_edge, own_docs = pack(
        entry_weight, exit_weight, state_weight, step_weight, norm_gain, inner_kernel,
        gate_gain, step_bias, decay_log, skip_gain, documents, tokens,
    )
    packs = (own_small, own_parts, own_exit, own_par, own_edge, own_docs)
    (
        hidden_t, cin, gate, pre, loc, carry, cin_state, pre_state, bc, bct, score, mask, zst, dt, sp,
        cumt, fac, match,
    ), (small, parts, exit_weights, par, par_heads, cot_t) = entry(
        tokens, doc_col, doc_row, state_filter, packs, cotangent, rounds
    )
    block_own, exit_part, gate_part, dy, gpg, enter, gate_row, skip_row = middle(
        tokens, cotangent, cot_t, hidden_t, pre, gate, loc, carry, exit_weights, par, par_heads, bc,
        bct, score, mask, sp, cumt, fac,
    )
    cut = lambda v: v.reshape(2, 2, count, own_rows, v.shape[-1])
    exit_mine, block_both, *others = scan_back(
        pre, dy, loc, carry, enter, cin, par, par_heads, state_filter, cin_state, pre_state, bc, bct,
        score, mask, sp, cumt, fac, match, zst, dt, cut(exit_part), cut(gate_part), block_own,
        tokens, cotangent, hidden_t, gpg, parts, small, gate_row, skip_row, rounds,
    )
    if len(others) == 5:
        mine, mine_last, state_both, vector, token_both = others
    else:
        taps, taps_state, head_rows, inner_part, small_part, token_own, norm_row = others
        mine, state_both, vector, token_both = reduce_all(
            cut(inner_part), cut(small_part), token_own, taps, taps_state, gate_row, head_rows,
            skip_row, norm_row,
        )
        mine, mine_last = mine[:, : 2 * WIDE], mine[:, 2 * WIDE :]
    outs = list(finish(mine, mine_last, exit_mine, state_both, vector, token_both, block_both))
    for index in (2, 8, 9, 10):
        outs[index] = outs[index][0]
    outs[5] = outs[5].T
    outs[11] = outs[11].reshape(-1)
    return tuple(outs)


def solution(mesh):
    in_specs = (
        P("dp", "context", None),
        P("dp", "context"),
        P(("dp", "context")),
        P(("dp", "context"), None, "tensor"),
        P(("dp", "context"), None),
        P(("dp", "context"), "tensor"),
        P(None, "tensor"),
        P(),
        P("tensor"),
        P("tensor"),
        P("tensor"),
        P("tensor"),
        P(("dp", "context"), "tensor"),
        P("dp", "context", None),
    )
    out_specs = (
        P("dp", "context", None),
        P("dp", "context", None),
        P(("dp", "context")),
        P(("dp", "context"), None, "tensor"),
        P(("dp", "context"), None),
        P(("dp", "context"), "tensor"),
        P(None, "tensor"),
        P(),
        P("tensor"),
        P("tensor"),
        P("tensor"),
        P("tensor"),
        P(("dp", "context"), "tensor"),
    )
    return jax.shard_map(body, mesh=mesh, in_specs=in_specs, out_specs=out_specs, check_vma=False)
```

```python
import functools
import jax
import jax.numpy as jnp
from jax import lax
from jax.experimental import pallas as pl
from jax.experimental.pallas import tpu as pltpu
from jax.sharding import PartitionSpec as P

HEAD = 64
NSTATE = 128
CONV = 4
EPSILON = 1e-05
Q = 128
HALO = 16
EDGE = 8
GROUPS = 6
BLOCK_CUTS = 8
ORDER = (0, 3, 1, 4, 2, 5)
LANES = 128
WIDE = 256
LOG2E = 1.4426950408889634
FAR = -1e30
LOW = jnp.bfloat16
F32 = jnp.float32
VMEM_LIMIT = 60 * 1024 * 1024


def mm(a, b):
    return lax.dot_general(a, b, (((1,), (0,)), ((), ())), preferred_element_type=F32)


def mm_nt(a, b):
    return lax.dot_general(a, b, (((1,), (1,)), ((), ())), preferred_element_type=F32)


def mm_tn(a, b):
    return lax.dot_general(a, b, (((0,), (0,)), ((), ())), preferred_element_type=F32)


def mm_exact(a, b):
    return lax.dot_general(
        a, b, (((1,), (0,)), ((), ())), precision=lax.Precision.HIGHEST, preferred_element_type=F32
    )


def split3(v):
    high = v.astype(LOW).astype(F32)
    rest = v - high
    mid = rest.astype(LOW).astype(F32)
    low = rest - mid
    return (high + pltpu.roll(mid, 32, 1) + pltpu.roll(low, 64, 1)).astype(LOW)


def iota(shape, dim):
    return lax.broadcasted_iota(jnp.int32, shape, dim)


def spreader(first_head, width, count):
    k = iota((LANES, width * count), 0)
    lane = iota((LANES, width * count), 1)
    hit = ((k & 31) == first_head + lane // width) & (k < 96)
    return hit.astype(F32).astype(LOW)


def gatherer(first_head, width, count):
    lane = iota((width * count, LANES), 0)
    k = iota((width * count, LANES), 1)
    return (k == first_head + lane // width).astype(F32).astype(LOW)


def head_sums(v, collect):
    high = v.astype(LOW)
    rest = (v - high.astype(F32)).astype(LOW)
    return mm(high, collect) + mm(rest, collect)


def sigmoid(v):
    return 1.0 / (1.0 + jnp.exp(-v))


def twice(v):
    return jnp.concatenate([v, v], axis=1)


def conv_forward(cin, taps, masks):
    rows = cin.shape[0] - HALO
    out = taps[CONV : CONV + 1] + taps[CONV - 1 : CONV] * cin[HALO:]
    for back in range(1, CONV):
        part = cin[HALO - back : HALO - back + rows]
        out = out + taps[CONV - 1 - back : CONV - back] * (part * twice(masks[back - 1]))
    return out


def conv_backward(pg, cin, taps, masks):
    rows, width = pg.shape
    sums = [None] * (CONV + 1)
    sums[CONV] = jnp.sum(pg, axis=0, keepdims=True)
    sums[CONV - 1] = jnp.sum(pg * cin[HALO:], axis=0, keepdims=True)
    pad = jnp.zeros((HALO, width), F32)
    grad = jnp.concatenate([pad, pg * taps[CONV - 1 : CONV]], axis=0)
    for back in range(1, CONV):
        masked = pg * twice(masks[back - 1])
        part = cin[HALO - back : HALO - back + rows]
        sums[CONV - 1 - back] = jnp.sum(masked * part, axis=0, keepdims=True)
        padded = jnp.concatenate([pad, masked * taps[CONV - 1 - back : CONV - back], pad], axis=0)
        grad = grad + padded[back : back + rows + HALO]
    return sums, grad


def const(shape):
    zeros = (0,) * len(shape)
    return pl.BlockSpec(shape, lambda *_: zeros)


def params(**extra):
    return pltpu.CompilerParams(vmem_limit_bytes=VMEM_LIMIT, **extra)


VMEM_SPEC = pl.BlockSpec(memory_space=pltpu.VMEM)
ANY_SPEC = pl.BlockSpec(memory_space=pl.ANY)


def side():
    return lax.axis_index("tensor")


def remote(src, dst, send_sem, recv_sem, target):
    return pltpu.make_async_remote_copy(
        src_ref=src,
        dst_ref=dst,
        send_sem=send_sem,
        recv_sem=recv_sem,
        device_id=target,
        device_id_type=pl.DeviceIdType.MESH,
    )


def each(count, run, first=0):
    def one(step, carry):
        run(step)
        return carry

    lax.fori_loop(first, count, one, 0)


class Place:
    def __init__(self, depth):
        position = lax.axis_index("context")
        self.depth = depth
        self.position = position
        self.x, self.y = lax.axis_index("dp"), lax.axis_index("tensor")
        self.z, self.c = position // 2, position % 2
        self.mate = self.at(self.x, self.y, self.z, 1 - self.c)
        self.x_peer = self.at(1 - self.x, self.y, self.z, self.c)
        self.y_peer = self.at(self.x, 1 - self.y, self.z, self.c)

    def at(self, x, y, z, c):
        return {"dp": x, "context": z * 2 + c, "tensor": y}

    def away(self, z):
        return self.at(self.x, self.y, z, self.c)

    def axes(self, turned):
        x, y, z, c = self.x, self.y, self.z, self.c
        x1, y1 = x + (1 - turned) * (1 - 2 * x), y + turned * (1 - 2 * y)
        x2, y2 = x + turned * (1 - 2 * x), y + (1 - turned) * (1 - 2 * y)
        return (x1, y1), (x2, y2)

    def around(self, run, first=0, last=None):
        z, depth = self.z, self.depth
        if first == 0:
            run(z)

        def step(away):
            @pl.when(z - away >= 0)
            def _():
                run(z - away)

            @pl.when(z + away < depth)
            def _():
                run(z + away)

        each(depth if last is None else last, step, max(first, 1))

    def greet(self, always, sometimes=(), column=False):
        barrier = pltpu.get_barrier_semaphore()
        kind = pl.DeviceIdType.MESH
        total = len(always)
        for target in always:
            pl.semaphore_signal(barrier, inc=1, device_id=target, device_id_type=kind)
        for holds, target in sometimes:

            @pl.when(holds)
            def _():
                pl.semaphore_signal(barrier, inc=1, device_id=target, device_id_type=kind)

            total = total + holds.astype(jnp.int32)
        if column:
            for_all = lambda step: pl.semaphore_signal(
                barrier,
                inc=1,
                device_id=self.away(lax.rem(self.z + step, self.depth)),
                device_id_type=kind,
            )
            each(self.depth, for_all, 1)
            total = total + (self.depth - 1)
        pl.semaphore_wait(barrier, total)


class Gathering:
    def __init__(self, place, own, full, sends, lands, local):
        self.place, self.own_ref, self.full = place, own, full
        self.sends, self.lands, self.local = sends, lands, local
        self.starts = [first * place.depth for first in (0, 4, 5, 7)]
        (self.x1, self.y1), (self.x2, self.y2) = place.axes(place.c)
        self.first = place.at(self.x1, self.y1, place.z, place.c)
        self.second = place.at(self.x2, self.y2, place.z, place.c)

    @staticmethod
    def scratch(depth):
        sem = pltpu.SemaphoreType.DMA
        return [sem((8 * depth,)), sem((8 * depth,)), sem((1,))]

    def copy(self, kind, index, x, y, z, c, target, own=False):
        chunk = self.full.at[y, x, z * 2 + c]
        mark = ((y * 2 + x) * self.place.depth + z) * 2 + c
        return remote(
            self.own_ref if own else chunk, chunk, self.sends.at[self.starts[kind] + index],
            self.lands.at[mark], target,
        )

    def arrive(self, x, y, z, c):
        self.copy(0, 0, x, y, z, c, self.place.mate).wait_recv()

    def kept(self):
        p = self.place
        return pltpu.make_async_copy(
            self.own_ref, self.full.at[p.y, p.x, p.z * 2 + p.c], self.local.at[0]
        )

    def own(self):
        p = self.place
        mine = (p.x, p.y, p.z, p.c)

        def far_z(z):
            self.copy(3, z, *mine, p.away(z), True).start()

        p.around(far_z, 1)
        self.copy(1, p.z, *mine, self.first, True).start()
        self.copy(2, p.z, *mine, self.second, True).start()
        self.copy(0, p.z, *mine, p.mate, True).start()
        self.kept().start()

    def near(self, first=1, last=None):
        p = self.place

        def run(z):
            chunk = (p.x, p.y, z, p.c)
            self.arrive(*chunk)

            self.copy(1, z, *chunk, self.first).start()
            self.copy(2, z, *chunk, self.second).start()
            self.copy(0, z, *chunk, p.mate).start()

        p.around(run, first, last)

    def across(self):
        p = self.place

        def run(z):
            chunk = (self.x1, self.y1, z, p.c)
            self.arrive(*chunk)
            self.copy(2, p.depth + z, *chunk, self.second).start()
            self.copy(0, p.depth + z, *chunk, p.mate).start()

        p.around(run)

    def far(self):
        p = self.place

        def near_row(z):
            self.arrive(self.x2, self.y2, z, p.c)
            self.copy(0, 2 * p.depth + z, self.x2, self.y2, z, p.c, p.mate).start()

        def far_row(z):
            self.arrive(1 - p.x, 1 - p.y, z, p.c)
            self.copy(0, 3 * p.depth + z, 1 - p.x, 1 - p.y, z, p.c, p.mate).start()

        p.around(near_row)
        p.around(far_row)

    def mates(self):
        p = self.place

        def from_mate(z):
            for y in range(2):
                for x in range(2):
                    self.arrive(x, y, z, 1 - p.c)

        each(p.depth, from_mate)
        self.kept().wait()

    def finish(self):
        p = self.place

        def sent(kind, index, target):
            self.copy(kind, index, p.x, p.y, p.z, p.c, target).wait_send()

        each(4 * p.depth, lambda step: sent(0, step, p.mate))
        each(p.depth, lambda step: sent(1, step, p.mate))
        each(2 * p.depth, lambda step: sent(2, step, p.mate))

        p.around(lambda z: sent(3, z, p.mate), 1)


class Reducing:
    def __init__(self, place, turned, parts, total, bufs, sems):
        self.place, self.parts, self.total = place, parts, total
        self.own, self.core, self.send1, self.land1 = bufs[:4]
        self.send2, self.land2, self.send3, self.land3 = bufs[4:]
        self.own_sem, self.core_send, self.core_land = sems[:3]
        self.s1, self.l1, self.s2, self.l2, self.s3, self.l3 = sems[3:]
        self.turned = turned
        (x1, y1), (x2, y2) = place.axes(turned)
        self.first = place.at(x1, y1, place.z, place.c)
        self.second = place.at(x2, y2, place.z, place.c)
        self.mine = place.y + turned * (place.x - place.y)

    @staticmethod
    def scratch(depth, rows, tall):
        buffer = lambda *lead: pltpu.VMEM(lead + (rows, tall), LOW)
        sem = lambda *lead: pltpu.SemaphoreType.DMA(lead)
        bufs = [
            buffer(2, 2, depth), buffer(2, 2, depth), buffer(depth, 2), buffer(depth, 2),
            buffer(depth), buffer(depth), buffer(depth), buffer(depth),
        ]
        return bufs + [sem(2, 2, depth)] * 3 + [sem(depth)] * 6

    def spot(self, step):
        return lax.rem(self.place.z + 1 + step, self.place.depth)

    def whole(self, y, x, z):
        return remote(
            self.core.at[y, x, z], self.core.at[y, x, z], self.core_send.at[y, x, z],
            self.core_land.at[y, x, z], self.place.mate,
        )

    def own_whole(self, y, x, z):
        return pltpu.make_async_copy(
            self.own.at[y, x, z], self.own.at[y, x, z], self.own_sem.at[y, x, z]
        )

    def start(self, step):
        p = self.place
        z = self.spot(step)
        for y in range(2):
            for x in range(2):
                for ref, cols in self.parts:
                    remote(
                        ref.at[y, x, z * 2 + 1 - p.c], self.core.at[y, x, z, :, cols],
                        self.core_send.at[y, x, z], self.core_land.at[y, x, z], p.mate,
                    ).start()
                    pltpu.make_async_copy(
                        ref.at[y, x, z * 2 + p.c], self.own.at[y, x, z, :, cols],
                        self.own_sem.at[y, x, z],
                    ).start()

    def base(self, y, x, z):
        return self.own[y, x, z].astype(F32) + self.core[y, x, z].astype(F32)

    def copy1(self, z):
        return remote(
            self.send1.at[z], self.land1.at[z], self.s1.at[z], self.l1.at[z], self.first
        )

    def copy2(self, z):
        return remote(
            self.send2.at[z], self.land2.at[z], self.s2.at[z], self.l2.at[z], self.second
        )

    def copy3(self, z, lands_at):
        return remote(
            self.send3.at[z], self.land3.at[lands_at], self.s3.at[z], self.l3.at[lands_at],
            self.place.away(z),
        )

    def stage1(self, step):
        p, turned = self.place, self.turned
        z = self.spot(step)
        for y in range(2):
            for x in range(2):
                self.whole(y, x, z).wait_recv()
                self.own_whole(y, x, z).wait()
        for index in range(2):
            x = (1 - turned) * (1 - p.x) + turned * index
            y = turned * (1 - p.y) + (1 - turned) * index
            self.send1[z, index] = self.base(y, x, z).astype(LOW)
        self.copy1(z).start()

    def stage2(self, step):
        p, turned = self.place, self.turned
        z = self.spot(step)
        self.copy1(z).wait_recv()
        other = 1 - self.mine
        x = (1 - turned) * p.x + turned * other
        y = turned * p.y + (1 - turned) * other
        self.send2[z] = (self.base(y, x, z) + self.land1[z, other].astype(F32)).astype(LOW)
        self.copy2(z).start()

    def final(self, z):
        p = self.place
        self.copy2(z).wait_recv()
        return (
            self.base(p.y, p.x, z)
            + self.land1[z, self.mine].astype(F32)
            + self.land2[z].astype(F32)
        )

    def stage3(self, step):
        z = self.spot(step)
        self.send3[z] = self.final(z).astype(LOW)
        self.copy3(z, self.place.z).start()

    def turn(self, step):
        depth = self.place.depth

        @pl.when(step < depth)
        def _():
            self.stage1(step)

        @pl.when((step >= 1) & (step <= depth))
        def _():
            self.stage2(step - 1)

        @pl.when((step >= 2) & (step <= depth))
        def _():
            self.stage3(step - 2)

    def close(self):
        p = self.place
        self.total[...] = self.final(p.z)

        def add(step):
            z = lax.rem(p.z + step, p.depth)
            self.copy3(z, z).wait_recv()
            self.total[...] += self.land3[z].astype(F32)

        each(p.depth, add, 1)

    def finish(self):
        p = self.place

        def sent(z):
            for y in range(2):
                for x in range(2):
                    self.whole(y, x, z).wait_send()
            self.copy1(z).wait_send()
            self.copy2(z).wait_send()

        each(p.depth, sent)
        each(p.depth, lambda step: self.copy3(lax.rem(p.z + step, p.depth), p.z).wait_send(), 1)


class Chaining:
    def __init__(self, place, rounds, backward, fold, gain, bufs, sems):
        self.place, self.rounds = place, rounds
        self.fold, self.gain = fold, gain
        self.from_mate, self.from_chip, self.to_mate, self.to_chip = bufs
        self.mate_send, self.mate_land, self.chip_send, self.chip_land = sems
        first = 1 if backward else 0
        by = -1 if backward else 1
        self.order = place.depth - 1 - place.z if backward else place.z
        self.leads = place.c == first
        self.after = place.at(place.x, place.y, place.z + by, first)
        self.before = place.at(place.x, place.y, place.z - by, 1 - first)
        self.linked_before = self.leads & (self.order > 0)
        self.linked_after = jnp.logical_not(self.leads) & (self.order < place.depth - 1)

    @staticmethod
    def scratch(rounds):
        slots = lambda turns: pltpu.VMEM((turns, GROUPS, NSTATE, WIDE), LOW)
        marks = lambda turns: pltpu.SemaphoreType.DMA((turns, GROUPS))
        return [
            slots(rounds + 1), slots(rounds), slots(rounds + 1), slots(rounds),
            marks(rounds + 1), marks(rounds + 1), marks(rounds), marks(rounds),
        ]

    def sometimes(self):
        return [(self.linked_before, self.before), (self.linked_after, self.after)]

    def mate_copy(self, turn, cut):
        return remote(
            self.to_mate.at[turn, cut], self.from_mate.at[turn, cut], self.mate_send.at[turn, cut],
            self.mate_land.at[turn, cut], self.place.mate,
        )

    def chip_copy(self, turn, cut):
        return remote(
            self.to_chip.at[turn, cut], self.from_chip.at[turn, cut], self.chip_send.at[turn, cut],
            self.chip_land.at[turn, cut], self.after,
        )

    def joined(self, cut, arrived):
        return (self.fold[cut] + self.gain[cut, 0:1] * arrived.astype(F32)).astype(LOW)

    def open(self, cut):
        @pl.when(self.leads)
        def _():
            self.to_mate[0, cut] = self.fold[cut].astype(LOW)
            self.mate_copy(0, cut).start()

    def pass_on(self, turn, cut):
        @pl.when(jnp.logical_not(self.leads))
        def _():
            self.mate_copy(turn, cut).wait_recv()

        @pl.when(self.linked_after)
        def _():
            self.to_chip[turn, cut] = self.joined(cut, self.from_mate[turn, cut])
            self.chip_copy(turn, cut).start()

    def relay(self, turn, cut):
        @pl.when(self.linked_before)
        def _():
            self.chip_copy(turn, cut).wait_recv()
            self.to_mate[turn + 1, cut] = self.joined(cut, self.from_chip[turn, cut])
            self.mate_copy(turn + 1, cut).start()

        @pl.when(self.leads & (self.order == 0))
        def _():
            self.to_mate[turn + 1, cut] = self.fold[cut].astype(LOW)
            self.mate_copy(turn + 1, cut).start()

    def later(self):
        for turn in range(1, self.rounds):
            for cut in range(GROUPS):
                self.pass_on(turn, cut)
            for cut in range(GROUPS):
                self.relay(turn, cut)

    def arrive(self, put):
        last = self.rounds - 1

        @pl.when(self.linked_before)
        def _():
            for cut in range(GROUPS):
                put(cut, self.from_chip[last, cut])

        @pl.when(self.leads & (self.order == 0))
        def _():
            for cut in range(GROUPS):
                put(cut, jnp.zeros((NSTATE, WIDE), LOW))

        @pl.when(jnp.logical_not(self.leads))
        def _():
            for cut in range(GROUPS):
                self.mate_copy(self.rounds, cut).wait_recv()
                put(cut, self.from_mate[self.rounds, cut])

    def finish(self):
        @pl.when(self.leads)
        def _():
            for turn in range(self.rounds + 1):
                for cut in range(GROUPS):
                    self.mate_copy(turn, cut).wait_send()

        @pl.when(self.linked_after)
        def _():
            for turn in range(self.rounds):
                for cut in range(GROUPS):
                    self.chip_copy(turn, cut).wait_send()


class Closing:
    def __init__(self, place, token, token_out, refs):
        self.place, self.token, self.token_out = place, token, token_out
        self.state_own, self.state_in, self.send, self.land = refs[:4]
        self.vs, self.vl, self.ts, self.tl, self.ss, self.sl, self.keep_sem = refs[4:]
        self.targets = [place.mate, place.y_peer, place.x_peer]

    @staticmethod
    def scratch(depth, own_rows, vector):
        sem = lambda *lead: pltpu.SemaphoreType.DMA(lead)
        return [
            pltpu.VMEM((own_rows, NSTATE), F32),
            pltpu.VMEM((2, own_rows, NSTATE), F32),
            pltpu.VMEM((4,) + vector, F32),
            pltpu.VMEM((3 + depth,) + vector, F32),
            sem(3 + depth), sem(3 + depth), sem(depth), sem(depth), sem(1), sem(1), sem(1),
        ]

    def vec_copy(self, turn):
        return remote(
            self.send.at[turn], self.land.at[turn], self.vs.at[turn], self.vl.at[turn],
            self.targets[turn],
        )

    def vec_far(self, away, lands_at):
        return remote(
            self.send.at[3], self.land.at[3 + lands_at], self.vs.at[3 + away],
            self.vl.at[3 + lands_at], self.place.away(away),
        )

    def token_copy(self, step):
        p = self.place
        share = self.token.shape[0] // p.depth
        at = pl.ds(pl.multiple_of(step * share, share), share)
        return remote(
            self.token.at[at], self.token_out.at[p.y, at], self.ts.at[step], self.tl.at[step],
            p.y_peer,
        )

    def run(self, reducing, width, state_out, vector_out, first, pending=None):
        p = self.place
        depth, z = p.depth, p.z
        keep = pltpu.make_async_copy(self.token, self.token_out.at[p.y], self.keep_sem.at[0])
        keep.start()
        self.vec_copy(0).start()

        def step_all(step):
            if pending is not None:

                @pl.when(step + 3 <= depth)
                def _():
                    pending.turn(step + 3)

            reducing.turn(step)

            @pl.when(step < depth)
            def _():
                self.token_copy(step).start()

            for turn in range(3):

                @pl.when(step == turn)
                def _():
                    self.vec_copy(turn).wait_recv()
                    self.send[turn + 1] = self.send[turn] + self.land[turn]
                    if turn < 2:
                        self.vec_copy(turn + 1).start()
                    else:
                        each(depth, lambda s: self.vec_far(lax.rem(z + s, depth), z).start(), 1)
                        self.land[3 + z] = self.send[3]

        each(depth + 1, step_all)
        if pending is not None:
            pending.close()
        reducing.close()
        self.state_own[...] = reducing.total[:, first : first + width]
        state_copy = remote(
            self.state_own, self.state_in.at[p.y], self.ss.at[0], self.sl.at[0], p.y_peer
        )
        state_copy.start()
        self.state_in[p.y] = self.state_own[...]

        def vec_arrive(step):
            away = lax.rem(z + step, depth)
            self.vec_far(away, away).wait_recv()

        each(depth, vec_arrive, 1)
        vector_out[...] = self.land[3]

        def vec_add(step):
            vector_out[...] += self.land[3 + step]

        each(depth, vec_add, 1)
        for turn in range(3):
            self.vec_copy(turn).wait_send()
        each(depth, lambda s: self.vec_far(lax.rem(z + s, depth), z).wait_send(), 1)
        reducing.finish()
        each(depth, lambda step: self.token_copy(step).wait())
        state_copy.wait()
        state_out[...] = self.state_in[...]
        keep.wait()


def group_of(index):
    half, part = index % 2, index // 2
    return half * 3 + part, half, part


def turn_of(step):
    return group_of(jnp.maximum(step - 1, 0))


def entry_body(depth, rounds, fused, *refs):
    step = pl.program_id(0)
    tokens, doc_col, doc_row, state_filter = refs[:4]
    if fused:
        own_small, own_parts, own_exit, own_par, own_edge, own_docs, cot = refs[4:11]
    else:
        w_gate, w_inner, w_small, par, heads_ref, edge, halo_docs = refs[4:11]
    (
        hidden_out, cin_out, gate_out, pre_out, loc_out, carry_out, cin_state_out, pre_state_out,
        bc_out, bct_out, score_out, mask_out, zst_out, dt_out, sp_out, cumt_out, fac_out, match_out,
    ) = refs[11:29]
    refs = refs[29:]
    if fused:
        small_out, parts_out, exit_out, par, heads_ref, cot_t = refs[:6]
        refs = refs[6:]
    hidden, normed, sp_tail, facs, folds, gains = refs[:6]
    rows, model = tokens.shape[1:]
    spans = rows // Q
    place = Place(depth)
    chaining = Chaining(place, rounds, False, folds, gains, refs[6:10], refs[10:14])
    group, half, part = turn_of(step)
    y = place.y
    if fused:
        v_small, v_parts, edge, halo_docs, docs_in, cot_in, par_in = refs[14:21]
        side_send, side_land, local, out_sem = refs[21:25]
        marks = refs[25:]
        own = [own_small, own_parts.at[0], own_parts.at[1], own_parts.at[2], own_exit]
        full = [v_small, v_parts.at[0], v_parts.at[1], v_parts.at[2], exit_out]
        pieces = [
            Gathering(place, own[i], full[i], *marks[3 * i : 3 * i + 3]) for i in range(5)
        ]
        stores = [pltpu.make_async_copy(v_small, small_out, out_sem.at[0])]
        for index in range(3):
            stores.append(
                pltpu.make_async_copy(
                    v_parts.at[index], parts_out.at[index], out_sem.at[index + 1]
                )
            )

    def before_weights():
        for ref, first, count in ((edge, 0, HALO), (tokens, HALO, rows)):
            value = (ref[...] if ref is edge else ref[0]).astype(F32)
            scale = lax.rsqrt(jnp.mean(value * value, axis=1, keepdims=True) + EPSILON)
            normed[first : first + count] = value * scale
        docs = jnp.concatenate([halo_docs[...], doc_col[...]], axis=0)
        for back in range(1, CONV):
            match = (docs[HALO - back : HALO - back + rows] == docs[HALO:]).astype(F32)
            match_out[back - 1] = match
        t_at, u_at = iota((Q, Q), 0), iota((Q, Q), 1)
        for index in range(spans):
            at = slice(index * Q, (index + 1) * Q)
            same = (t_at >= u_at) & (doc_col[at] == doc_row[0:1, at])
            mask_out[at] = jnp.where(same, 0.0, FAR)

    def after_weights(small):
        gain = jnp.transpose(small[0][:, LANES:].astype(F32))[24:25]
        hidden[...] = (normed[...] * gain).astype(LOW)
        hidden_out[...] = jnp.transpose(hidden[HALO:])
        both = [mm(hidden[...], small[index]) for index in range(2)]
        cin = jnp.concatenate([both[0][:, :LANES], both[1][:, :LANES]], axis=1).astype(LOW)
        cin_state_out[...] = cin
        docs = jnp.concatenate([halo_docs[...], doc_col[...]], axis=0)
        masks = [match_out[back] for back in range(CONV - 1)]
        pre = conv_forward(cin.astype(F32), state_filter[...], masks)
        pre_state_out[...] = pre
        mixed = (pre * sigmoid(pre)).astype(LOW)
        bc_out[...] = mixed
        turned = jnp.transpose(mixed.astype(F32)).astype(LOW)
        bct_out[...] = turned
        heads = heads_ref[...]
        used = iota((rows, LANES), 1) < 24
        raw = both[0][HALO:, LANES:] + both[1][HALO:, LANES:]
        zst = jnp.where(used, raw, 0.0) + heads[0:1]
        zst_out[...] = zst
        dt = jnp.where(used, jnp.maximum(zst, 0.0) + jnp.log1p(jnp.exp(-jnp.abs(zst))), 0.0)
        dt_out[...] = dt
        decay = -dt * jnp.exp(heads[1:2])
        t_at, u_at = iota((Q, Q), 0), iota((Q, Q), 1)
        lower = (t_at >= u_at).astype(F32)
        fac_rows = []
        for index in range(spans):
            at = slice(index * Q, (index + 1) * Q)
            cum = mm_exact(lower, decay[at])
            final = cum[Q - 1 : Q]
            before = docs[HALO + index * Q - 1 : HALO + index * Q]
            here = doc_col[at]
            last = here[Q - 1 : Q]
            opened = (here == before).astype(F32)
            tail = (here == last).astype(F32) * jnp.exp(final - cum)
            fac_rows.append((last == before).astype(F32) * jnp.exp(final))
            cum2 = cum * LOG2E
            turned_cum = jnp.transpose(cum2)
            for group in range(6):
                cumt_out[group, 0:4, at] = turned_cum[4 * group : 4 * group + 4]
            sp_out[0, at] = split3(dt[at])
            sp_out[1, at] = split3(cum2)
            lanes_used = iota((Q, LANES), 1) < 24
            sp_out[2, at] = split3(jnp.where(lanes_used, opened * jnp.exp(cum), 0.0))
            sp_out[3, at] = split3(jnp.where(lanes_used, tail, 0.0))
            sp_tail[at] = split3(jnp.where(lanes_used, tail * dt[at], 0.0))
            score_out[at] = mm_nt(mixed[at, LANES:], mixed[at, :LANES])
        gain_total = fac_rows[0]
        for row in fac_rows[1:]:
            gain_total = gain_total * row
        rows8 = jnp.concatenate(
            fac_rows + [gain_total] + [jnp.zeros((1, LANES), F32)] * (7 - spans), axis=0
        )
        rows8 = jnp.where(iota((8, LANES), 1) < 24, rows8, 0.0)
        fac_out[...] = rows8
        facs[...] = split3(rows8)

    if fused:

        @pl.when(step == 0)
        def _():
            count = 2 * depth
            onward = {"context": lax.rem(place.position + 1, count)}
            behind = {"context": lax.rem(place.position + count - 1, count)}
            place.greet(
                [place.mate, place.x_peer, place.y_peer, onward, behind], chaining.sometimes(), True
            )
            sides = [
                remote(own_edge, edge, side_send.at[0], side_land.at[0], onward),
                remote(own_docs, docs_in, side_send.at[1], side_land.at[1], onward),
                remote(own_par, par_in.at[y], side_send.at[2], side_land.at[2], place.y_peer),
            ]
            for copy in sides:
                copy.start()
            for piece in pieces:
                piece.own()
            cot_copy = pltpu.make_async_copy(cot.at[y], cot_in, local.at[0])
            par_keep = pltpu.make_async_copy(own_par, par_in.at[y], local.at[1])
            cot_copy.start()
            par_keep.start()
            for copy in sides:
                copy.wait()
            par_keep.wait()
            pieces[0].near()
            pieces[1].near()
            halo_docs[...] = jnp.where(place.position == 0, -1.0, docs_in[...])
            par[...] = par_in[...]
            both = par[0, CONV + 2 : CONV + 3] + par[1, CONV + 2 : CONV + 3]
            heads_ref[...] = jnp.zeros_like(heads_ref)
            for index in range(3):
                heads_ref[index : index + 1] = both[:, index * LANES : (index + 1) * LANES]
            before_weights()
            pieces[0].across()
            pieces[2].near()
            pieces[1].across()
            pieces[0].far()
            cot_copy.wait()
            cot_t[...] = jnp.transpose(cot_in[...])
            pieces[0].mates()
            stores[0].start()
            after_weights([v_small[index].reshape(model, WIDE) for index in range(2)])

        @pl.when(step == 1)
        def _():
            pieces[3].near()
            pieces[2].across()
            pieces[1].far()
            pieces[1].mates()
            stores[1].start()

        @pl.when(step == 2)
        def _():
            pieces[4].near()

        @pl.when(step == 3)
        def _():
            pieces[3].across()
            pieces[2].far()
            pieces[2].mates()
            stores[2].start()

        @pl.when(step == 4)
        def _():
            pieces[4].across()

        @pl.when(step == 5)
        def _():
            pieces[3].far()
            pieces[3].mates()
            stores[3].start()

        @pl.when(step == 6)
        def _():
            pieces[4].far()

    else:

        @pl.when(step == 0)
        def _():
            place.greet([place.mate], chaining.sometimes())
            before_weights()
            after_weights([w_small[index] for index in range(2)])

    for cut in range(GROUPS - 1):

        @pl.when(step == cut + 2)
        def _():
            chaining.pass_on(0, cut)

    for cut in range(GROUPS - 3):

        @pl.when(step == cut + 4)
        def _():
            chaining.relay(0, cut)

    @pl.when(step > 0)
    def _():
        if fused:
            gate_low = v_parts[part, half, :, :, :, :WIDE].reshape(model, WIDE)
            inner_low = v_parts[part, half, :, :, :, WIDE:].reshape(model, WIDE)
        else:
            gate_low, inner_low = w_gate[0, 0], w_inner[0, 0]
        taps = par[half, :, pl.ds(pl.multiple_of(part * WIDE, WIDE), WIDE)]
        cin = mm(hidden[...], inner_low).astype(LOW)
        cin_out[...] = cin
        gate_out[...] = mm(hidden[HALO:], gate_low)
        masks = [match_out[back] for back in range(CONV - 1)]
        pre = conv_forward(cin.astype(F32), taps, masks)
        pre_out[...] = pre
        spread = spreader(4 * group, HEAD, 4)
        value = (pre * sigmoid(pre) * mm(sp_tail[...], spread)).astype(LOW)
        facx = mm(facs[...], spread)
        fold = jnp.zeros((NSTATE, WIDE), F32)
        for index in range(spans):
            at = slice(index * Q, (index + 1) * Q)
            loc = mm(bct_out[:NSTATE, at], value[at])
            loc_out[at] = loc
            fold = facx[index : index + 1] * fold + loc
        folds[step - 1] = fold
        gains[step - 1] = jnp.broadcast_to(facx[spans : spans + 1], (8, WIDE))

    for cut in range(GROUPS):

        @pl.when(step == cut + 1)
        def _():
            chaining.open(cut)

    @pl.when(step == GROUPS)
    def _():
        chaining.pass_on(0, GROUPS - 1)
        for cut in range(GROUPS - 3, GROUPS):
            chaining.relay(0, cut)
        chaining.later()

        def put(cut, value):
            at = ORDER[cut] * WIDE
            carry_out[:, at : at + WIDE] = value

        chaining.arrive(put)
        if fused:
            pieces[4].mates()
            for piece in pieces:
                piece.finish()
            for store in stores:
                store.wait()
        chaining.finish()


def entry(tokens, doc_col, doc_row, state_filter, packs, cot, rounds):
    own_small, own_parts, own_exit, own_par, own_edge, own_docs = packs
    rows, model = tokens.shape[1:]
    count = lax.axis_size("context")
    depth = count // 2
    wide = GROUPS * WIDE
    ext = rows + HALO
    fused = own_small.shape[0] % 16 == 0
    shape = jax.ShapeDtypeStruct
    sem = lambda *lead: pltpu.SemaphoreType.DMA(lead)
    column = lambda count: pl.BlockSpec((count, WIDE), lambda s: (0, turn_of(s)[0]))
    whole = lambda *dims, dtype=F32: (shape(dims, dtype), const(dims))
    outs = [
        whole(model, rows, dtype=LOW),
        (shape((ext, wide), LOW), column(ext)),
        (shape((rows, wide), F32), column(rows)),
        (shape((rows, wide), F32), column(rows)),
        (shape((rows, wide), F32), column(rows)),
        whole(NSTATE, wide, dtype=LOW),
        whole(ext, WIDE, dtype=LOW),
        whole(rows, WIDE),
        whole(rows, WIDE, dtype=LOW),
        whole(WIDE, rows, dtype=LOW),
        whole(rows, Q),
        whole(rows, Q),
        whole(rows, LANES),
        whole(rows, LANES),
        whole(4, rows, LANES, dtype=LOW),
        whole(6, 8, rows),
        whole(8, LANES),
        whole(CONV - 1, rows, LANES),
    ]
    scratch = [
        pltpu.VMEM((ext, model), LOW),
        pltpu.VMEM((ext, model), F32),
        pltpu.VMEM((rows, LANES), LOW),
        pltpu.VMEM((8, LANES), LOW),
        pltpu.VMEM((GROUPS, NSTATE, WIDE), F32),
        pltpu.VMEM((GROUPS, 8, WIDE), F32),
    ] + Chaining.scratch(rounds)
    in_specs = [
        pl.BlockSpec((1, rows, model), lambda s: (side(), 0, 0)),
        const((rows, LANES)),
        const((8, rows)),
        const((CONV + 1, WIDE)),
    ]
    args = [tokens, doc_col, doc_row, state_filter]
    full = lambda own: (2, 2, count) + own.shape[-2:]
    if fused:
        outs += [
            (shape(full(own_small), LOW), ANY_SPEC),
            (shape((3,) + full(own_parts), LOW), ANY_SPEC),
            (shape(full(own_exit), LOW), ANY_SPEC),
            (shape((2,) + own_par.shape, F32), VMEM_SPEC),
            (shape((8, LANES), F32), VMEM_SPEC),
            (shape((model, rows), LOW), VMEM_SPEC),
        ]
        scratch += [
            pltpu.VMEM(full(own_small), LOW),
            pltpu.VMEM((3,) + full(own_parts), LOW),
            pltpu.VMEM(own_edge.shape, LOW),
            pltpu.VMEM(own_docs.shape, F32),
            pltpu.VMEM(own_docs.shape, F32),
            pltpu.VMEM((rows, model), LOW),
            pltpu.VMEM((2,) + own_par.shape, F32),
            sem(3),
            sem(3),
            sem(2),
            sem(4),
        ] + Gathering.scratch(depth) * 5
        in_specs += [VMEM_SPEC] * 6 + [ANY_SPEC]
        args += [own_small, own_parts, own_exit, own_par, own_edge, own_docs, cot]
    else:
        small, parts, exits, par, heads, edge, docs, cot_t = gather(*packs, cot)
        weights = parts.reshape(3, 2, model, 2 * WIDE)
        block = lambda at: pl.BlockSpec(
            (1, 1, model, WIDE), lambda s: (turn_of(s)[2], turn_of(s)[1], 0, at)
        )
        in_specs += [block(0), block(1), const((2, model, WIDE))] + [VMEM_SPEC] * 4
        args += [weights, weights, small.reshape(2, model, WIDE), par, heads, edge, docs]
    results = pl.pallas_call(
        functools.partial(entry_body, depth, rounds, fused),
        out_shape=[out[0] for out in outs],
        grid=(GROUPS + 1,),
        in_specs=in_specs,
        out_specs=[out[1] for out in outs],
        scratch_shapes=scratch,
        compiler_params=params(collective_id=1, has_side_effects=True),
        name="entry",
    )(*args)
    if fused:
        small, parts, exits, par, heads, cot_t = results[18:]
    return tuple(results[:18]), (
        small.reshape(2, model, WIDE),
        parts.reshape(3, 2, model, 2 * WIDE),
        exits.reshape(2, model, -1),
        par,
        heads,
        cot_t,
    )


def middle_body(
    tokens_far, cot, cot_t_far, hidden_far, pre_ref, gate_ref, loc_ref, carry_ref, w_exit, par, par_heads, bc,
    bct, score, mask, sp, cumt, fac, block_out, exit_out, gate_part_out, dy_out, gpg_out, enter_out, row_out,
    skip_out, outputs, gates, unit_grads, mixes, sums, total,
    tokens, cot_t, hidden_t, late_sem
):
    step = pl.program_id(0)
    rows = pre_ref.shape[0]
    spans = rows // Q
    wide = 6 * WIDE

    late = [
        pltpu.make_async_copy(src, dst, late_sem.at[index])
        for index, (src, dst) in enumerate(
            ((cot_t_far, cot_t), (hidden_far, hidden_t), (tokens_far.at[side()], tokens))
        )
    ]

    @pl.when(step == 0)
    def _():
        for copy in late:
            copy.start()
        sums[...] = jnp.zeros_like(sums)
        total[...] = jnp.zeros_like(total)
        skip_out[...] = jnp.zeros_like(skip_out)

    @pl.when(step < 6)
    def _():
        group = step
        spread = spreader(4 * group, HEAD, 4)
        pre = pre_ref[...]
        mix = pre * sigmoid(pre)
        mixes[group] = mix
        value = mix * mm(sp[0], spread)
        growth = mm(sp[2], spread)
        facx = mm(split3(fac[...]), spread)
        cums = mm(sp[1], spreader(4 * group, LANES, 4))
        skipx = mm(split3(par_heads[...]), spread)[2:3]
        state = carry_ref[...].astype(F32)
        half = iota((Q, LANES), 1) < HEAD
        for index in range(spans):
            at = slice(index * Q, (index + 1) * Q)
            carried = mm(bc[at, LANES:], state.astype(LOW)) * growth[at]
            parts = []
            for pair in range(2):
                lanes = slice(pair * LANES, (pair + 1) * LANES)
                weights, seen = [], []
                for head in (2 * pair, 2 * pair + 1):
                    across = cumt[group, head : head + 1, at]
                    spread_at = cums[at, head * LANES : (head + 1) * LANES] - across + mask[at]
                    weights.append((jnp.exp2(spread_at) * score[at]).astype(LOW))
                    keep = half if head % 2 == 0 else jnp.logical_not(half)
                    seen.append(jnp.where(keep, value[at, lanes], 0.0).astype(LOW))
                local = mm(jnp.concatenate(weights, axis=1), jnp.concatenate(seen, axis=0))
                parts.append(local)
            out = jnp.concatenate(parts, axis=1) + carried + skipx * mix[at]
            outputs[group, at] = out
            state = facx[index : index + 1] * state + loc_ref[at]
        gate = gate_ref[...]
        gates[group] = gate
        gated = outputs[group] * (gate * sigmoid(gate))
        unit_grad = mm(cot[0], w_exit[0])
        unit_grads[group] = unit_grad
        square = gated * gated
        cross = unit_grad * par[0, 5:6] * gated
        sums[0] += square[:, :LANES] + square[:, LANES:]
        sums[1] += cross[:, :LANES] + cross[:, LANES:]

    @pl.when(step == 5)
    def _():
        for copy in late:
            copy.wait()
        square = jnp.sum(sums[0], axis=1, keepdims=True)
        cross = jnp.sum(sums[1], axis=1, keepdims=True)
        normal = lax.rsqrt(square / wide + EPSILON)
        sums[0] = jnp.broadcast_to(normal, (rows, LANES))
        sums[1] = jnp.broadcast_to(normal * normal * normal * cross / wide, (rows, LANES))

    @pl.when(step >= 6)
    def _():
        group = step - 6
        spread = spreader(4 * group, HEAD, 4)
        normal = twice(sums[0])
        pull = twice(sums[1])
        gain = par[0, 5:6]
        gate = gates[group]
        out = outputs[group]
        unit_grad = unit_grads[group]
        sigma = sigmoid(gate)
        act = gate * sigma
        gated = out * act
        scaled_in = gated * normal
        unit = (scaled_in * gain).astype(LOW)
        total[...] += mm_nt(unit, w_exit[0])
        exit_out[0] = mm(cot_t[...], unit).astype(LOW)
        gate_sum = jnp.sum(unit_grad * scaled_in, axis=0, keepdims=True)
        gated_grad = normal * (unit_grad * gain) - pull * gated
        dy = gated_grad * act
        dy_out[...] = dy
        gate_grad = (gated_grad * out * sigma * (1.0 + gate * (1.0 - sigma))).astype(LOW)
        gpg_out[...] = gate_grad
        gate_part_out[0] = mm(hidden_t[...], gate_grad).astype(LOW)
        skip_sum = jnp.sum(dy * mixes[group], axis=0, keepdims=True)
        row_out[...] = jnp.broadcast_to(gate_sum, (8, WIDE))
        skip_out[...] += head_sums(
            jnp.broadcast_to(skip_sum, (8, WIDE)), gatherer(4 * group, HEAD, 4)
        )
        facx = mm(split3(fac[...]), spread)
        pushed = (dy * mm(sp[2], spread)).astype(LOW)
        enter = jnp.zeros((NSTATE, WIDE), F32)
        for index in reversed(range(spans)):
            at = slice(index * Q, (index + 1) * Q)
            enter = facx[index : index + 1] * enter + mm(bct[NSTATE:, at], pushed[at])
        enter_out[...] = enter

    @pl.when(step == 11)
    def _():
        block_out[...] = (tokens[...].astype(F32) + total[...]).astype(LOW)


def middle(
    tokens, cot, cot_t, hidden_t, pre, gate, loc, carry, weights, par, par_heads, bc, bct, score, mask,
    sp, cumt, fac
):
    rows, model = tokens.shape[1:]
    wide = 6 * WIDE
    shape = jax.ShapeDtypeStruct

    def early(s):
        return jnp.minimum(s, 5)

    def late(s):
        return jnp.maximum(s - 6, 0)

    def group(s):
        return s % 6

    outs = (
        (shape((rows, model), LOW), const((rows, model))),
        (
            shape((2, model, 3 * WIDE), LOW),
            pl.BlockSpec((1, model, WIDE), lambda s: (late(s) // 3, 0, late(s) % 3)),
        ),
        (
            shape((2, model, 3 * WIDE), LOW),
            pl.BlockSpec((1, model, WIDE), lambda s: (late(s) // 3, 0, late(s) % 3)),
        ),
        (shape((rows, wide), F32), pl.BlockSpec((rows, WIDE), lambda s: (0, late(s)))),
        (shape((rows, wide), LOW), pl.BlockSpec((rows, WIDE), lambda s: (0, late(s)))),
        (shape((NSTATE, wide), F32), pl.BlockSpec((NSTATE, WIDE), lambda s: (0, late(s)))),
        (shape((8, wide), F32), pl.BlockSpec((8, WIDE), lambda s: (0, late(s)))),
        (shape((8, LANES), F32), const((8, LANES))),
    )
    return pl.pallas_call(
        middle_body,
        out_shape=[out[0] for out in outs],
        grid=(12,),
        in_specs=[
                ANY_SPEC,
                pl.BlockSpec((1, rows, model), lambda s: (side(), 0, 0)),
                ANY_SPEC,
                ANY_SPEC,
                pl.BlockSpec((rows, WIDE), lambda s: (0, early(s))),
                pl.BlockSpec((rows, WIDE), lambda s: (0, early(s))),
                pl.BlockSpec((rows, WIDE), lambda s: (0, early(s))),
                pl.BlockSpec((NSTATE, WIDE), lambda s: (0, early(s))),
                pl.BlockSpec((1, model, WIDE), lambda s: (group(s) // 3, 0, group(s) % 3)),
                pl.BlockSpec((1, 8, WIDE), lambda s: (group(s) // 3, 0, group(s) % 3)),
                const((8, LANES)),
                const((rows, WIDE)),
                const((WIDE, rows)),
                const((rows, Q)),
                const((rows, Q)),
                const((4, rows, LANES)),
                const((6, 8, rows)),
                const((8, LANES)),
        ],
        out_specs=[out[1] for out in outs],
        scratch_shapes=[
                pltpu.VMEM((6, rows, WIDE), F32),
                pltpu.VMEM((6, rows, WIDE), F32),
                pltpu.VMEM((6, rows, WIDE), F32),
                pltpu.VMEM((6, rows, WIDE), F32),
                pltpu.VMEM((2, rows, LANES), F32),
                pltpu.VMEM((rows, model), F32),
                pltpu.VMEM((rows, model), LOW),
                pltpu.VMEM((model, rows), LOW),
                pltpu.VMEM((model, rows), LOW),
                pltpu.SemaphoreType.DMA((3,)),
        ],
        compiler_params=params(),
        name="middle",
    )(
        tokens, cot, cot_t, hidden_t, pre, gate, loc, carry, weights, par, par_heads, bc, bct, score,
        mask, sp, cumt, fac,
    )


def scan_back_body(depth, rounds, fused, *refs):
    (
        pre_ref, dy_ref, loc_ref, carry_ref, enter, cin_ref, par, par_heads, state_filter, cin_far,
        pre_far, bc, bct, score, mask, sp, cumt, fac, match_far, zst_far, dt_far, exits, gate_part,
        block_far, tokens_far, cot_far, hidden_far, gpg, w_gate, w_inner, small_far, gate_row,
        skip_row,
    ) = refs[:33]
    mine, block_out = refs[33:35]
    if fused:
        mine2, mine3, state_out, vector_out, token_both = refs[35:40]
        refs = refs[40:]
    else:
        tap_out, tap_state_out, small_out, inner_part, small_part, token_out, norm_out = refs[35:42]
        refs = refs[42:]
    block_own, hidden_t, match, tokens, cot, w_small, pre_state, cin_state, zst, dt_ref = refs[:10]
    late_sem = refs[10]
    refs = refs[11:]
    late = [
        pltpu.make_async_copy(src, dst, late_sem.at[index])
        for index, (src, dst) in enumerate(
            (
                (block_far, block_own), (hidden_far, hidden_t), (match_far, match),
                (tokens_far.at[side()], tokens), (cot_far.at[side()], cot), (small_far, w_small),
                (pre_far, pre_state), (cin_far, cin_state), (zst_far, zst), (dt_far, dt_ref),
            )
        )
    ]
    (
        d_bc, d_score, d_cum, heads, local_value, enters, gains, adjoints, edge_own, edge_in, grads,
        total, es, el, bs, bl, block_keep,
    ) = refs[:17]
    scratch = refs[17:42]
    step = pl.program_id(0)
    group, half_at, part_at = group_of(jnp.minimum(step, GROUPS - 1))
    last_group, last_half, last_part = group_of(jnp.maximum(step - 1, 0))
    blocks = BLOCK_CUTS
    rows = pre_ref.shape[0]
    spans = rows // Q
    place = Place(depth)
    wide = exits.shape[-1]
    chaining = Chaining(place, rounds, True, enters, gains, scratch[:4], scratch[4:8])
    reducing = Reducing(
        place, 0, [(exits, slice(0, wide)), (gate_part, slice(wide, 2 * wide))], mine,
        scratch[8:16], scratch[16:25],
    )
    if fused:
        inner_v, small_v, token_v, taps_v = refs[42:46]
        buffers = refs[46:]
        second = Reducing(
            place, 0, [(inner_v.at[0], slice(0, WIDE)), (inner_v.at[1], slice(WIDE, 2 * WIDE))],
            mine2, buffers[:8], buffers[8:17],
        )
        third = Reducing(
            place, 0, [(inner_v.at[2], slice(0, WIDE)), (small_v, slice(WIDE, 2 * WIDE))], mine3,
            buffers[17:25], buffers[25:34],
        )
        closing = Closing(place, token_v, token_both, buffers[34:])
    position = place.position
    has_before, has_after = position > 0, position < 2 * depth - 1
    before, after = {"context": position - 1}, {"context": position + 1}
    share = rows // blocks

    def block_copy(index):
        at = pl.ds(pl.multiple_of(index * share, share), share)
        return remote(
            block_own.at[at], block_out.at[place.y, at], bs.at[index], bl.at[index], place.y_peer
        )

    block_local = pltpu.make_async_copy(block_own, block_out.at[place.y], block_keep.at[0])

    def edge_copy(index):
        return remote(edge_own.at[index], edge_in.at[index], es.at[index], el.at[index], before)

    def edge_wait(index):
        @pl.when(has_after)
        def _():
            edge_copy(index).wait_recv()

    def put_inner(value):
        if fused:
            inner_v[last_part, last_half] = value.reshape(inner_v.shape[2:])
        else:
            inner_part[0] = value

    def joined(index):
        grad = grads[...]
        return jnp.concatenate(
            [grad[: rows - EDGE], grad[rows - EDGE :] + edge_in[index]], axis=0
        ).astype(LOW)

    @pl.when(step == 0)
    def _():
        for copy in late:
            copy.start()
        d_bc[...] = jnp.zeros_like(d_bc)
        d_score[...] = jnp.zeros_like(d_score)
        d_cum[...] = jnp.zeros_like(d_cum)
        heads[...] = jnp.zeros_like(heads)
        grads[...] = jnp.zeros_like(grads)
        total[...] = jnp.zeros_like(total)
        edge_in[GROUPS + 1] = jnp.zeros((EDGE, WIDE), F32)

        @pl.when(jnp.logical_not(has_after))
        def _():
            edge_in[...] = jnp.zeros_like(edge_in)

        place.greet(
            [place.mate, place.x_peer, place.y_peer],
            chaining.sometimes() + [(has_before, before), (has_after, after)],
            True,
        )
        facs = split3(fac[...])
        for cut in range(GROUPS):
            enters[cut] = enter[:, cut * WIDE : (cut + 1) * WIDE]
            chaining.open(cut)
        for cut in range(GROUPS):
            rows8 = mm(facs, spreader(4 * cut, HEAD, 4))
            gains[cut] = jnp.broadcast_to(rows8[spans : spans + 1], (8, WIDE))
        each(depth, reducing.start)
        late[0].wait()
        block_local.start()
        each(3, lambda index: block_copy(index).start())
        for cut in range(GROUPS):
            chaining.pass_on(0, cut)

    if fused:

        @pl.when(step == 5)
        def _():
            each(depth, second.start)

    @pl.when(step < GROUPS)
    def _():
        spread = spreader(4 * group, HEAD, 4)
        collect = gatherer(4 * group, HEAD, 4)
        pre = pre_ref[...]
        sigma = sigmoid(pre)
        mix = pre * sigma
        dtx = mm(sp[0], spread)
        growth = mm(sp[2], spread)
        facx = mm(split3(fac[...]), spread)
        cums = mm(sp[1], spreader(4 * group, LANES, 4))
        ones = jnp.ones((8, Q), F32).astype(LOW)
        states = [carry_ref[...].astype(F32)]
        for index in range(spans - 1):
            at = slice(index * Q, (index + 1) * Q)
            states.append(facx[index : index + 1] * states[-1] + loc_ref[at])
        for index in range(spans):
            at = slice(index * Q, (index + 1) * Q)
            dy = dy_ref[at]
            value = mix[at] * dtx[at]
            value_low = value.astype(LOW)
            lane = iota((Q, WIDE), 1) // HEAD
            dy_heads = [jnp.where(lane == head, dy, 0.0).astype(LOW) for head in range(4)]
            d_weight = mm_nt(jnp.concatenate(dy_heads, axis=0), value_low)
            parts = []
            sum_score = None
            row_sums = None
            for pair in range(2):
                lanes = slice(pair * LANES, (pair + 1) * LANES)
                moved, weights = [], []
                for head in (2 * pair, 2 * pair + 1):
                    across = cumt[group, head : head + 1, at]
                    spread_at = cums[at, head * LANES : (head + 1) * LANES] - across + mask[at]
                    decay = jnp.exp2(spread_at)
                    inner = decay * d_weight[head * Q : (head + 1) * Q]
                    sum_score = inner if sum_score is None else sum_score + inner
                    moved.append((inner * score[at]).astype(LOW))
                    weights.append((decay * score[at]).astype(LOW))
                both = jnp.concatenate(moved, axis=1)
                column_sums = mm(ones, both)
                for index_in in range(2):
                    head = 2 * pair + index_in
                    d_cum[group, head : head + 1, at] = -column_sums[
                        0:1, index_in * Q : (index_in + 1) * Q
                    ]
                part = mm(both, gatherer(4 * group + 2 * pair, LANES, 2))
                row_sums = part if row_sums is None else row_sums + part
                pushed_heads = [dy_heads[2 * pair][:, lanes], dy_heads[2 * pair + 1][:, lanes]]
                parts.append(
                    mm_tn(jnp.concatenate(weights, axis=0), jnp.concatenate(pushed_heads, axis=0))
                )
            d_score[at] += sum_score
            local_value[at] = jnp.concatenate(parts, axis=1)
            pushed = dy * growth[at]
            state_low = states[index].astype(LOW)
            carried = mm(bc[at, LANES:], state_low)
            d_bc[at, LANES:] += mm_nt(pushed.astype(LOW), state_low)
            heads[1, at] += head_sums(pushed * carried, collect) + row_sums

    @pl.when(step == 0)
    def _():
        for cut in range(GROUPS):
            chaining.relay(0, cut)
        chaining.later()

        def put(cut, value):
            adjoints[cut] = value

        chaining.arrive(put)
        chaining.finish()
        late[1].wait()
        late[2].wait()

    for turn in range(5):

        @pl.when(step == turn)
        def _():
            each(turn + 1 if turn < 4 else depth + 1, reducing.turn, turn)
            block_copy(turn + 3).start()

    @pl.when(step == 5)
    def _():
        reducing.close()
        if fused:
            second.turn(0)

    @pl.when((step > 0) & (step < GROUPS))
    def _():
        edge_wait(last_group)

    @pl.when(step < GROUPS)
    def _():
        spread = spreader(4 * group, HEAD, 4)
        collect = gatherer(4 * group, HEAD, 4)
        pre = pre_ref[...]
        sigma = sigmoid(pre)
        mix = pre * sigma
        dtx = mm(sp[0], spread)
        growth = mm(sp[2], spread)
        facx = mm(split3(fac[...]), spread)
        states = [carry_ref[...].astype(F32)]
        for index in range(spans - 1):
            at = slice(index * Q, (index + 1) * Q)
            states.append(facx[index : index + 1] * states[-1] + loc_ref[at])
        arrived = jnp.where(step > 0, last_group, GROUPS + 1)
        grad = joined(arrived)
        gate_grad = gpg[...]
        put_inner(mm(hidden_t[...], grad).astype(LOW))
        total[...] += mm_nt(gate_grad, w_gate[0, 0]) + mm_nt(grad, w_inner[0, 0])
        tails = mm(sp[3], spread)
        skipx = mm(split3(par_heads[...]), spread)[2:3]
        adjoint = adjoints[group].astype(F32)
        masks = [match[back] for back in range(CONV - 1)]
        pgs = [None] * spans
        for index in reversed(range(spans)):
            at = slice(index * Q, (index + 1) * Q)
            dy = dy_ref[at]
            value = mix[at] * dtx[at]
            adj_low = adjoint.astype(LOW)
            reached = mm(bc[at, :LANES], adj_low) * tails[at]
            d_bc[at, :LANES] += mm_nt((value * tails[at]).astype(LOW), adj_low)
            heads[0, at] += head_sums(value * reached, collect)
            fac_part = jnp.sum(adjoint * states[index], axis=0, keepdims=True)
            heads[3, index * 8 : index * 8 + 8] += head_sums(
                jnp.broadcast_to(fac_part, (8, WIDE)), collect
            )
            pushed_low = (dy * growth[at]).astype(LOW)
            adjoint = facx[index : index + 1] * adjoint + mm(bct[NSTATE:, at], pushed_low)
            d_value = local_value[at] + reached
            heads[2, at] += head_sums(mix[at] * d_value, collect)
            d_mix = dtx[at] * d_value + skipx * dy
            s = sigma[at]
            pgs[index] = d_mix * s * (1.0 + pre[at] * (1.0 - s))
        pg = jnp.concatenate(pgs, axis=0)
        sums, grad = conv_backward(pg, cin_ref[...].astype(F32), par[0], masks)
        taps8 = jnp.concatenate(sums + [jnp.zeros((3, WIDE), F32)], axis=0)
        if fused:
            taps_v[group] = taps8
        else:
            tap_out[...] = taps8
        grads[...] = grad[HALO:]
        edge_own[group] = grad[HALO - EDGE : HALO]

        @pl.when(has_before)
        def _():
            edge_copy(group).start()

    @pl.when(step == GROUPS)
    def _():
        for copy in late[3:]:
            copy.wait()
        if fused:
            second.turn(1)
        masks = [match[back] for back in range(CONV - 1)]
        edge_wait(GROUPS - 1)
        grad = joined(GROUPS - 1)
        put_inner(mm(hidden_t[...], grad).astype(LOW))
        total[...] += mm_nt(grad, w_inner[0, 0])
        t_at, u_at = iota((Q, Q), 0), iota((Q, Q), 1)
        onward = (t_at <= u_at).astype(F32)
        earlier = (t_at > u_at).astype(F32)
        rate = jnp.exp(par_heads[1:2])
        raws = []
        bias_sum = jnp.zeros((1, LANES), F32)
        decay_sum = jnp.zeros((1, LANES), F32)
        used = iota((Q, LANES), 1) < 24
        for index in range(spans):
            at = slice(index * Q, (index + 1) * Q)
            pieces = [d_cum[piece, 0:4, at] for piece in range(6)]
            pieces.append(jnp.zeros((LANES - 24, Q), F32))
            cum_col = jnp.transpose(jnp.concatenate(pieces, axis=0))
            fac_row = fac[index : index + 1] * heads[3, index * 8 : index * 8 + 1]
            d_decay = (
                mm_exact(onward, cum_col + heads[1, at]) + mm_exact(earlier, heads[0, at]) + fac_row
            )
            dt = dt_ref[at]
            raw = (heads[2, at] - d_decay * rate) * sigmoid(zst[at])
            raw = jnp.where(used, raw, 0.0)
            raws.append(raw.astype(LOW))
            bias_sum += jnp.sum(raw, axis=0, keepdims=True)
            decay_sum -= jnp.sum(
                jnp.where(used, d_decay * dt * rate, 0.0), axis=0, keepdims=True
            )
            score_low = d_score[at].astype(LOW)
            d_bc[at, :LANES] += mm_tn(score_low, bc[at, LANES:])
            d_bc[at, LANES:] += mm(score_low, bc[at, :LANES])
        if not fused:
            small_out[...] = jnp.concatenate(
                [bias_sum, decay_sum, jnp.zeros((6, LANES), F32)], axis=0
            )
        if fused:
            second.turn(2)
        pre = pre_state[...]
        s = sigmoid(pre)
        pg = d_bc[...] * s * (1.0 + pre * (1.0 - s))
        sums, grad = conv_backward(pg, cin_state[...].astype(F32), state_filter[...], masks)
        taps8 = jnp.concatenate(sums + [jnp.zeros((3, WIDE), F32)], axis=0)
        if fused:
            taps_v[GROUPS] = taps8
        else:
            tap_state_out[...] = taps8
        grads[...] = grad[HALO:]
        edge_own[GROUPS] = grad[HALO - EDGE : HALO]

        @pl.when(has_before)
        def _():
            edge_copy(GROUPS).start()

        steps = jnp.concatenate(raws, axis=0)
        turned = hidden_t[...]
        step_part = mm(turned, steps).astype(LOW)
        total[...] += mm_nt(steps, w_small[0, :, LANES:]) + mm_nt(steps, w_small[1, :, LANES:])
        edge_wait(GROUPS)
        state = joined(GROUPS)
        state_part = mm(turned, state).astype(LOW)
        for index in range(2):
            state_half = state_part[:, index * LANES : (index + 1) * LANES]
            value = jnp.concatenate([state_half, step_part], axis=1)
            if fused:
                small_v[index] = value.reshape(small_v.shape[1:])
            else:
                small_part[index] = value
        if fused:
            each(depth, third.start)
        value = tokens[...].astype(F32)
        scale = lax.rsqrt(jnp.mean(value * value, axis=1, keepdims=True) + EPSILON)
        hidden_grad = (
            total[...]
            + mm_nt(state[:, :LANES], w_small[0, :, :LANES])
            + mm_nt(state[:, LANES:], w_small[1, :, :LANES])
        )
        norm_sum = jnp.sum(hidden_grad * (value * scale), axis=0, keepdims=True)
        if not fused:
            norm_out[...] = jnp.broadcast_to(norm_sum, norm_out.shape)
        gain = jnp.transpose(w_small[0, :, LANES : 2 * LANES].astype(F32))[24:25]
        normed = hidden_grad * gain
        pull = jnp.sum(normed * value, axis=1, keepdims=True) / value.shape[1]
        token_low = (
            cot[...].astype(F32) + scale * normed - (scale * scale * scale) * value * pull
        ).astype(LOW)
        if fused:
            token_v[...] = token_low
            for index in range(GROUPS + 1):
                at = slice(index * WIDE, (index + 1) * WIDE)
                closing.send[0, : CONV + 1, at] = taps_v[index, : CONV + 1]
            high = GROUPS * WIDE
            closing.send[0, CONV + 1 :] = jnp.zeros((8 - CONV - 1, high + WIDE), F32)
            closing.send[0, 5:6, :high] = gate_row[0:1]
            closing.send[0, 5:6, high : high + LANES] = bias_sum
            closing.send[0, 5:6, high + LANES :] = skip_row[0:1]
            model = norm_sum.shape[1]
            closing.send[0, 6:7, :model] = norm_sum
            closing.send[0, 6:7, model : model + LANES] = decay_sum
            closing.run(third, NSTATE, state_out, vector_out, WIDE, second)
            second.finish()
        else:
            token_out[...] = token_low
        reducing.finish()
        each(blocks, lambda index: block_copy(index).wait())
        block_local.wait()

        @pl.when(has_before)
        def _():
            each(GROUPS + 1, lambda index: edge_copy(index).wait_send())


def scan_back(
    pre, dy, loc, carry, enter, cin, par, par_heads, state_filter, cin_state, pre_state, bc, bct,
    score, mask, sp, cumt, fac, match, zst, dt, exits, gate_part, block_own, tokens, cot, hidden_t,
    gpg, parts, small, gate_row, skip_row, rounds
):
    rows, wide = pre.shape
    ext = rows + HALO
    depth = lax.axis_size("context") // 2
    own_rows, half_wide = exits.shape[3:]
    shape = jax.ShapeDtypeStruct
    sem = lambda *lead: pltpu.SemaphoreType.DMA(lead)
    model = tokens.shape[2]
    count = 2 * depth
    fused = own_rows % 16 == 0
    now = lambda s: group_of(jnp.minimum(s, GROUPS - 1))
    lag = lambda s: group_of(jnp.maximum(s - 1, 0))
    column = lambda count: pl.BlockSpec((count, WIDE), lambda s: (0, now(s)[0]))
    whole = lambda *dims, dtype=F32: (shape(dims, dtype), const(dims))
    outs = [
        whole(own_rows, 2 * half_wide),
        (shape((2,) + block_own.shape, LOW), ANY_SPEC),
    ]
    if fused:
        outs += [
            whole(own_rows, 2 * WIDE),
            whole(own_rows, 2 * WIDE),
            whole(2, own_rows, NSTATE),
            whole(8, wide + WIDE),
            (shape((2, rows, model), LOW), ANY_SPEC),
        ]
        extra = (
            [
                pltpu.VMEM((3, 2, 2, count, own_rows, WIDE), LOW),
                pltpu.VMEM((2, 2, count, own_rows, WIDE), LOW),
                pltpu.VMEM((rows, model), LOW),
                pltpu.VMEM((GROUPS + 1, 8, WIDE), F32),
            ]
            + Reducing.scratch(depth, own_rows, 2 * WIDE) * 2
            + Closing.scratch(depth, own_rows, (8, wide + WIDE))
        )
    else:
        outs += [
            (shape((8, wide), F32), column(8)),
            whole(8, WIDE),
            whole(8, LANES),
            (
                shape((2, model, 3 * WIDE), LOW),
                pl.BlockSpec((1, model, WIDE), lambda s: (lag(s)[1], 0, lag(s)[2])),
            ),
            whole(2, model, WIDE, dtype=LOW),
            whole(rows, model, dtype=LOW),
            whole(8, model),
        ]
        extra = []
    return pl.pallas_call(
        functools.partial(scan_back_body, depth, rounds, fused),
        out_shape=[out[0] for out in outs],
        grid=(GROUPS + 1,),
        in_specs=[
            column(rows),
            column(rows),
            column(rows),
            column(NSTATE),
            const((NSTATE, wide)),
            column(ext),
            pl.BlockSpec((1, 8, WIDE), lambda s: (now(s)[1], 0, now(s)[2])),
            const((8, LANES)),
            const((CONV + 1, WIDE)),
            ANY_SPEC,
            ANY_SPEC,
            const((rows, WIDE)),
            const((WIDE, rows)),
            const((rows, Q)),
            const((rows, Q)),
            const((4, rows, LANES)),
            const((6, 8, rows)),
            const((8, LANES)),
            ANY_SPEC,
            ANY_SPEC,
            ANY_SPEC,
            ANY_SPEC,
            ANY_SPEC,
            ANY_SPEC,
            ANY_SPEC,
            ANY_SPEC,
            ANY_SPEC,
            column(rows),
            pl.BlockSpec((1, 1, model, WIDE), lambda s: (now(s)[2], now(s)[1], 0, 0)),
            pl.BlockSpec((1, 1, model, WIDE), lambda s: (lag(s)[2], lag(s)[1], 0, 1)),
            ANY_SPEC,
            const((8, wide)),
            const((8, LANES)),
        ],
        out_specs=[out[1] for out in outs],
        scratch_shapes=[
            pltpu.VMEM((rows, model), LOW),
            pltpu.VMEM((model, rows), LOW),
            pltpu.VMEM((CONV - 1, rows, LANES), F32),
            pltpu.VMEM((rows, model), LOW),
            pltpu.VMEM((rows, model), LOW),
            pltpu.VMEM((2, model, WIDE), LOW),
            pltpu.VMEM((rows, WIDE), F32),
            pltpu.VMEM((ext, WIDE), LOW),
            pltpu.VMEM((rows, LANES), F32),
            pltpu.VMEM((rows, LANES), F32),
            sem(10),
            pltpu.VMEM((rows, WIDE), F32),
            pltpu.VMEM((rows, Q), F32),
            pltpu.VMEM((6, 8, rows), F32),
            pltpu.VMEM((4, rows, LANES), F32),
            pltpu.VMEM((rows, WIDE), F32),
            pltpu.VMEM((GROUPS, NSTATE, WIDE), F32),
            pltpu.VMEM((GROUPS, 8, WIDE), F32),
            pltpu.VMEM((GROUPS, NSTATE, WIDE), LOW),
            pltpu.VMEM((GROUPS + 1, EDGE, WIDE), F32),
            pltpu.VMEM((GROUPS + 2, EDGE, WIDE), F32),
            pltpu.VMEM((rows, WIDE), F32),
            pltpu.VMEM((rows, model), F32),
            sem(GROUPS + 1),
            sem(GROUPS + 1),
            sem(BLOCK_CUTS),
            sem(BLOCK_CUTS),
            sem(1),
        ]
        + Chaining.scratch(rounds)
        + Reducing.scratch(depth, own_rows, 2 * half_wide)
        + extra,
        compiler_params=params(collective_id=2, has_side_effects=True),
        name="scan_back",
    )(
        pre, dy, loc, carry, enter, cin, par, par_heads, state_filter, cin_state, pre_state, bc,
        bct, score, mask, sp, cumt, fac, match, zst, dt, exits, gate_part, block_own, tokens, cot,
        hidden_t, gpg, parts, parts, small, gate_row, skip_row,
    )


def pack_body(
    entry, exits, state, steps, gain, inner_kernel, gate_gain, bias, decay, skip, docs,
    tail_tokens, packed_small, packed_parts, packed_exit, par, doc_col, doc_row, edge, docs_own
):
    half_of = side()
    rows = entry.shape[0]
    wide = entry.shape[2]

    def placed(filled, used):
        return jnp.where(half_of == 0, filled, pltpu.roll(filled, used, 1))

    def widened(value):
        return jnp.concatenate(
            [value, jnp.zeros((value.shape[0], LANES - value.shape[1]), F32)], axis=1
        )

    for part in range(3):
        at = slice(part * WIDE, (part + 1) * WIDE)
        packed_parts[part, :, :WIDE] = entry[:, 0, at].astype(LOW)
        packed_parts[part, :, WIDE:] = entry[:, 1, at].astype(LOW)
    half = jnp.where(half_of == 0, state[:, :NSTATE], state[:, NSTATE:])
    packed_small[:, :NSTATE] = half.astype(LOW)
    gain_row = jnp.concatenate([gain[...], jnp.zeros((1, LANES - rows), F32)], axis=1)
    gain_col = jnp.transpose(jnp.broadcast_to(gain_row, (LANES, LANES)))[:rows]
    lane = iota((rows, LANES), 1)
    heads_here = steps.shape[0]
    step_rows = jnp.concatenate([steps[...], jnp.zeros((heads_here, LANES - rows), F32)], axis=1)
    step_rows = jnp.concatenate([step_rows, jnp.zeros((LANES - heads_here, LANES), F32)], axis=0)
    step_cols = jnp.transpose(step_rows)[:rows]
    small = jnp.where(lane == 24, gain_col, placed(step_cols, heads_here))
    packed_small[:, NSTATE:] = small.astype(LOW)
    packed_exit[...] = exits[...].astype(LOW)
    par[0 : CONV + 1] = inner_kernel[...]
    for index in range(wide // LANES):
        at = slice(index * LANES, (index + 1) * LANES)
        par[CONV + 1 : CONV + 2, at] = gate_gain[index : index + 1]
    par[CONV + 2 : CONV + 4] = jnp.zeros((2, wide), F32)
    for index, ref in enumerate((bias, decay, skip)):
        par[CONV + 2 : CONV + 3, index * LANES : (index + 1) * LANES] = placed(
            widened(ref[...]), ref.shape[1]
        )
    own = jnp.where(half_of == 0, docs[0:1], docs[1:2]).astype(F32)
    doc_row[...] = jnp.broadcast_to(own, doc_row.shape)
    doc_col[...] = jnp.transpose(jnp.broadcast_to(own, (LANES, own.shape[1])))
    docs_own[...] = doc_col[own.shape[1] - HALO :]
    edge[...] = tail_tokens[0]


def pack(
    entry, exits, state, steps, gain, inner_kernel, gate_gain, bias, decay, skip, docs, tokens
):
    own_rows, _, wide = entry.shape
    rows, model = tokens.shape[1:]
    shape = jax.ShapeDtypeStruct
    arrays = (
        entry, exits, state, steps.T, gain[None], inner_kernel, gate_gain.reshape(-1, LANES), bias[None],
        decay[None], skip[None], docs,
    )
    outs = (
        shape((own_rows, WIDE), LOW),
        shape((3, own_rows, 2 * WIDE), LOW),
        shape((own_rows, wide), LOW),
        shape((8, wide), F32),
        shape((rows, LANES), F32),
        shape((8, rows), F32),
        shape((HALO, model), LOW),
        shape((HALO, LANES), F32),
    )
    return pl.pallas_call(
        pack_body,
        out_shape=outs,
        grid=(1,),
        in_specs=[const(array.shape) for array in arrays]
        + [pl.BlockSpec((1, HALO, model), lambda s: (side(), rows // HALO - 1, 0))],
        out_specs=[const(out.shape) for out in outs],
        compiler_params=params(),
        name="pack",
    )(*arrays, tokens)


def gather_body(
    depth, own_small, own_parts, own_exit, par_own, edge_own, docs_own, cot, small, parts, exits, par,
    heads, edge, docs, cot_t, docs_in, cot_in, side_send, side_land, local, *marks
):
    place = Place(depth)
    count = 2 * depth
    onward = {"context": lax.rem(place.position + 1, count)}
    behind = {"context": lax.rem(place.position + count - 1, count)}
    y = place.y
    place.greet([place.mate, place.x_peer, place.y_peer, onward, behind], (), True)
    own = [own_small, own_parts.at[0], own_parts.at[1], own_parts.at[2], own_exit]
    full = [small, parts.at[0], parts.at[1], parts.at[2], exits]
    pieces = [Gathering(place, own[i], full[i], *marks[3 * i : 3 * i + 3]) for i in range(5)]
    sides = [
        remote(edge_own, edge, side_send.at[0], side_land.at[0], onward),
        remote(docs_own, docs_in, side_send.at[1], side_land.at[1], onward),
        remote(par_own, par.at[y], side_send.at[2], side_land.at[2], place.y_peer),
    ]
    for copy in sides:
        copy.start()
    cot_copy = pltpu.make_async_copy(cot.at[y], cot_in, local.at[1])
    cot_copy.start()
    par_keep = pltpu.make_async_copy(par_own, par.at[y], local.at[0])
    par_keep.start()
    for piece in pieces:
        piece.own()
    cot_copy.wait()
    cot_t[...] = jnp.transpose(cot_in[...])
    for piece in pieces:
        piece.near()
        piece.across()
        piece.far()
    for copy in sides:
        copy.wait()
    docs[...] = jnp.where(place.position == 0, -1.0, docs_in[...])
    par_keep.wait()
    both = par[0, CONV + 2 : CONV + 3] + par[1, CONV + 2 : CONV + 3]
    heads[...] = jnp.zeros_like(heads)
    for index in range(3):
        heads[index : index + 1] = both[:, index * LANES : (index + 1) * LANES]
    for piece in pieces:
        piece.mates()
        piece.finish()


def gather(own_small, own_parts, own_exit, par_own, edge_own, docs_own, cot):
    count = lax.axis_size("context")
    depth = count // 2
    rows, model = cot.shape[1:]
    shape = jax.ShapeDtypeStruct
    full = lambda own: (2, 2, count) + own.shape[-2:]
    return pl.pallas_call(
        functools.partial(gather_body, depth),
        out_shape=(
            shape(full(own_small), LOW),
            shape((3,) + full(own_parts), LOW),
            shape(full(own_exit), LOW),
            shape((2,) + par_own.shape, F32),
            shape((8, LANES), F32),
            shape(edge_own.shape, LOW),
            shape(docs_own.shape, F32),
            shape((model, rows), LOW),
        ),
        in_specs=[VMEM_SPEC] * 6 + [ANY_SPEC],
        out_specs=[ANY_SPEC] * 3 + [VMEM_SPEC] * 5,
        scratch_shapes=[
            pltpu.VMEM(docs_own.shape, F32),
            pltpu.VMEM((rows, model), LOW),
            pltpu.SemaphoreType.DMA((3,)),
            pltpu.SemaphoreType.DMA((3,)),
            pltpu.SemaphoreType.DMA((2,)),
        ]
        + Gathering.scratch(depth) * 5,
        compiler_params=params(collective_id=0, has_side_effects=True),
        name="gather",
    )(own_small, own_parts, own_exit, par_own, edge_own, docs_own, cot)


def reduce_body(
    depth, inner, small, token, taps, taps_state, gate_row, head_rows, skip_row, norm_row, mine,
    state_out, vector_out, token_out, *scratch
):
    place = Place(depth)
    wide = inner.shape[-1]
    parts = [(inner, slice(0, wide)), (small, slice(wide, wide + WIDE))]
    reducing = Reducing(place, 0, parts, mine, scratch[:8], scratch[8:17])
    closing = Closing(place, token, token_out, scratch[17:])
    vec = closing.send
    vec[0] = jnp.zeros(vec.shape[1:], F32)
    vec[0, : CONV + 1, : 2 * wide] = taps[: CONV + 1]
    vec[0, : CONV + 1, 2 * wide :] = taps_state[: CONV + 1]
    vec[0, 5:6, : 2 * wide] = gate_row[0:1]
    vec[0, 5:6, 2 * wide : 2 * wide + LANES] = head_rows[0:1]
    vec[0, 5:6, 2 * wide + LANES :] = skip_row[0:1]
    model = norm_row.shape[1]
    vec[0, 6:7, :model] = norm_row[0:1]
    vec[0, 6:7, model : model + LANES] = head_rows[1:2]
    place.greet([place.mate, place.x_peer, place.y_peer], (), True)
    each(depth, reducing.start)
    closing.run(reducing, NSTATE, state_out, vector_out, wide)


def reduce_all(inner, small, token, taps, taps_state, gate_row, head_rows, skip_row, norm_row):
    depth = lax.axis_size("context") // 2
    own_rows, wide = inner.shape[3:]
    tall = wide + WIDE
    shape = jax.ShapeDtypeStruct
    vector = (8, 2 * wide + WIDE)
    return pl.pallas_call(
        functools.partial(reduce_body, depth),
        out_shape=(
            shape((own_rows, tall), F32),
            shape((2, own_rows, NSTATE), F32),
            shape(vector, F32),
            shape((2,) + token.shape, LOW),
        ),
        in_specs=[ANY_SPEC] * 2 + [VMEM_SPEC] * 7,
        out_specs=[VMEM_SPEC] * 3 + [ANY_SPEC],
        scratch_shapes=Reducing.scratch(depth, own_rows, tall)
        + Closing.scratch(depth, own_rows, vector),
        compiler_params=params(collective_id=4, has_side_effects=True),
        name="reduce_all",
    )(inner, small, token, taps, taps_state, gate_row, head_rows, skip_row, norm_row)


def finish_body(
    mine, mine_last, exits, state, vector, token, block, block_out, token_out,
    norm_out, entry_out, state_out, step_out, kernel_out, filter_out, bias_out, decay_out, skip_out,
    gate_out, exit_out
):
    half_of = side()
    spot = lax.axis_index("dp") * lax.axis_size("context") + lax.axis_index("context")
    token_out[...] = token[...].astype(F32)
    first = half_of == 0
    block_out[...] = block[...]

    @pl.when(pl.program_id(0) == 0)
    def _():
        own_rows, _, wide = entry_out.shape
        model = token.shape[2]
        entry_out[:, 0] = exits[:, wide:]
        entry_out[:, 1, : 2 * WIDE] = mine[...]
        entry_out[:, 1, 2 * WIDE :] = mine_last[:, :WIDE]
        exit_out[...] = exits[:, :wide]
        state_out[:, :NSTATE] = state[0]
        state_out[:, NSTATE:] = state[1]

        def twelve(value):
            return jnp.where(first, value, pltpu.roll(value, LANES - 12, 1))[:, :12]

        steps = jnp.where(first, mine_last[:, WIDE + NSTATE :], pltpu.roll(mine_last[:, WIDE + NSTATE :], LANES - 12, 1))
        steps = jnp.concatenate([steps, jnp.zeros((LANES - own_rows, LANES), F32)], axis=0)
        step_out[...] = jnp.transpose(steps)[:12, :own_rows]
        left, right = vector[:, :wide], vector[:, wide : 2 * wide]
        halves = jnp.where(first, left, right)
        kernel_out[...] = halves[: CONV + 1]
        for index in range(wide // LANES):
            gate_out[index : index + 1] = halves[5:6, index * LANES : (index + 1) * LANES]
        filter_out[...] = vector[: CONV + 1, 2 * wide :]
        bias_out[...] = twelve(vector[5:6, 2 * wide : 2 * wide + LANES])
        skip_out[...] = twelve(vector[5:6, 2 * wide + LANES :])
        decay_out[...] = twelve(vector[6:7, model : model + LANES])
        turned = pltpu.roll(vector[:, :model], lax.rem(model - spot * own_rows, model), 1)
        norm_out[...] = turned[6:7, :own_rows]


def finish(mine, mine_last, exits, state, vector, token, block):
    own_rows, wide = exits.shape[0], exits.shape[1] // 2
    _, rows, model = token.shape
    share = rows // 4
    shape = jax.ShapeDtypeStruct
    outs = (
        (shape((2, rows, model), LOW), pl.BlockSpec((2, share, model), lambda s: (0, s, 0))),
        (shape((2, rows, model), F32), pl.BlockSpec((2, share, model), lambda s: (0, s, 0))),
        (shape((1, own_rows), F32), None),
        (shape((own_rows, 2, wide), F32), None),
        (shape((own_rows, WIDE), F32), None),
        (shape((12, own_rows), F32), None),
        (shape((CONV + 1, wide), F32), None),
        (shape((CONV + 1, WIDE), F32), None),
        (shape((1, 12), F32), None),
        (shape((1, 12), F32), None),
        (shape((1, 12), F32), None),
        (shape((wide // LANES, LANES), F32), None),
        (shape((own_rows, wide), F32), None),
    )
    return pl.pallas_call(
        finish_body,
        out_shape=[out[0] for out in outs],
        grid=(4,),
        in_specs=[
            const(mine.shape),
            const(mine_last.shape),
            const(exits.shape),
            const(state.shape),
            const(vector.shape),
            pl.BlockSpec((2, share, model), lambda s: (0, s, 0)),
            pl.BlockSpec((2, share, model), lambda s: (0, s, 0)),
        ],
        out_specs=[out[1] if out[1] is not None else const(out[0].shape) for out in outs],
        compiler_params=params(),
        name="finish",
    )(mine, mine_last, exits, state, vector, token, block)


def body(
    tokens, documents, norm_gain, entry_weight, state_weight, step_weight, inner_kernel,
    state_filter, step_bias, decay_log, skip_gain, gate_gain, exit_weight, cotangent,
):
    seqs, rows, model = tokens.shape
    count = lax.axis_size("context")
    own_rows = norm_gain.shape[0]
    longest = rows * count // 4
    rounds = min(count // 2 - 1, -(-(longest - 1) // (2 * rows)))

    own_small, own_parts, own_exit, own_par, doc_col, doc_row, own_edge, own_docs = pack(
        entry_weight, exit_weight, state_weight, step_weight, norm_gain, inner_kernel,
        gate_gain, step_bias, decay_log, skip_gain, documents, tokens,
    )
    packs = (own_small, own_parts, own_exit, own_par, own_edge, own_docs)
    (
        hidden_t, cin, gate, pre, loc, carry, cin_state, pre_state, bc, bct, score, mask, zst, dt, sp,
        cumt, fac, match,
    ), (small, parts, exit_weights, par, par_heads, cot_t) = entry(
        tokens, doc_col, doc_row, state_filter, packs, cotangent, rounds
    )
    block_own, exit_part, gate_part, dy, gpg, enter, gate_row, skip_row = middle(
        tokens, cotangent, cot_t, hidden_t, pre, gate, loc, carry, exit_weights, par, par_heads, bc,
        bct, score, mask, sp, cumt, fac,
    )
    cut = lambda v: v.reshape(2, 2, count, own_rows, v.shape[-1])
    exit_mine, block_both, *others = scan_back(
        pre, dy, loc, carry, enter, cin, par, par_heads, state_filter, cin_state, pre_state, bc, bct,
        score, mask, sp, cumt, fac, match, zst, dt, cut(exit_part), cut(gate_part), block_own,
        tokens, cotangent, hidden_t, gpg, parts, small, gate_row, skip_row, rounds,
    )
    if len(others) == 5:
        mine, mine_last, state_both, vector, token_both = others
    else:
        taps, taps_state, head_rows, inner_part, small_part, token_own, norm_row = others
        mine, state_both, vector, token_both = reduce_all(
            cut(inner_part), cut(small_part), token_own, taps, taps_state, gate_row, head_rows,
            skip_row, norm_row,
        )
        mine, mine_last = mine[:, : 2 * WIDE], mine[:, 2 * WIDE :]
    outs = list(finish(mine, mine_last, exit_mine, state_both, vector, token_both, block_both))
    for index in (2, 8, 9, 10):
        outs[index] = outs[index][0]
    outs[5] = outs[5].T
    outs[11] = outs[11].reshape(-1)
    return tuple(outs)


def solution(mesh):
    in_specs = (
        P("dp", "context", None),
        P("dp", "context"),
        P(("dp", "context")),
        P(("dp", "context"), None, "tensor"),
        P(("dp", "context"), None),
        P(("dp", "context"), "tensor"),
        P(None, "tensor"),
        P(),
        P("tensor"),
        P("tensor"),
        P("tensor"),
        P("tensor"),
        P(("dp", "context"), "tensor"),
        P("dp", "context", None),
    )
    out_specs = (
        P("dp", "context", None),
        P("dp", "context", None),
        P(("dp", "context")),
        P(("dp", "context"), None, "tensor"),
        P(("dp", "context"), None),
        P(("dp", "context"), "tensor"),
        P(None, "tensor"),
        P(),
        P("tensor"),
        P("tensor"),
        P("tensor"),
        P("tensor"),
        P(("dp", "context"), "tensor"),
    )
    return jax.shard_map(body, mesh=mesh, in_specs=in_specs, out_specs=out_specs, check_vma=False)
```

```python
import functools
import jax
import jax.numpy as jnp
from jax import lax
from jax.experimental import pallas as pl
from jax.experimental.pallas import tpu as pltpu
from jax.sharding import PartitionSpec as P

HEAD = 64
NSTATE = 128
CONV = 4
EPSILON = 1e-05
Q = 128
HALO = 16
EDGE = 8
GROUPS = 6
BLOCK_CUTS = 8
ORDER = (0, 3, 1, 4, 2, 5)
LANES = 128
WIDE = 256
LOG2E = 1.4426950408889634
FAR = -1e30
LOW = jnp.bfloat16
F32 = jnp.float32
VMEM_LIMIT = 60 * 1024 * 1024


def mm(a, b):
    return lax.dot_general(a, b, (((1,), (0,)), ((), ())), preferred_element_type=F32)


def mm_nt(a, b):
    return lax.dot_general(a, b, (((1,), (1,)), ((), ())), preferred_element_type=F32)


def mm_tn(a, b):
    return lax.dot_general(a, b, (((0,), (0,)), ((), ())), preferred_element_type=F32)


def mm_exact(a, b):
    return lax.dot_general(
        a, b, (((1,), (0,)), ((), ())), precision=lax.Precision.HIGHEST, preferred_element_type=F32
    )


def split3(v):
    high = v.astype(LOW).astype(F32)
    rest = v - high
    mid = rest.astype(LOW).astype(F32)
    low = rest - mid
    return (high + pltpu.roll(mid, 32, 1) + pltpu.roll(low, 64, 1)).astype(LOW)


def iota(shape, dim):
    return lax.broadcasted_iota(jnp.int32, shape, dim)


def spreader(first_head, width, count):
    k = iota((LANES, width * count), 0)
    lane = iota((LANES, width * count), 1)
    hit = ((k & 31) == first_head + lane // width) & (k < 96)
    return hit.astype(F32).astype(LOW)


def gatherer(first_head, width, count):
    lane = iota((width * count, LANES), 0)
    k = iota((width * count, LANES), 1)
    return (k == first_head + lane // width).astype(F32).astype(LOW)


def head_sums(v, collect):
    high = v.astype(LOW)
    rest = (v - high.astype(F32)).astype(LOW)
    return mm(high, collect) + mm(rest, collect)


def sigmoid(v):
    return 1.0 / (1.0 + jnp.exp(-v))


def twice(v):
    return jnp.concatenate([v, v], axis=1)


def conv_forward(cin, taps, masks):
    rows = cin.shape[0] - HALO
    out = taps[CONV : CONV + 1] + taps[CONV - 1 : CONV] * cin[HALO:]
    for back in range(1, CONV):
        part = cin[HALO - back : HALO - back + rows]
        out = out + taps[CONV - 1 - back : CONV - back] * (part * twice(masks[back - 1]))
    return out


def conv_backward(pg, cin, taps, masks):
    rows, width = pg.shape
    sums = [None] * (CONV + 1)
    sums[CONV] = jnp.sum(pg, axis=0, keepdims=True)
    sums[CONV - 1] = jnp.sum(pg * cin[HALO:], axis=0, keepdims=True)
    pad = jnp.zeros((HALO, width), F32)
    grad = jnp.concatenate([pad, pg * taps[CONV - 1 : CONV]], axis=0)
    for back in range(1, CONV):
        masked = pg * twice(masks[back - 1])
        part = cin[HALO - back : HALO - back + rows]
        sums[CONV - 1 - back] = jnp.sum(masked * part, axis=0, keepdims=True)
        padded = jnp.concatenate([pad, masked * taps[CONV - 1 - back : CONV - back], pad], axis=0)
        grad = grad + padded[back : back + rows + HALO]
    return sums, grad


def const(shape):
    zeros = (0,) * len(shape)
    return pl.BlockSpec(shape, lambda *_: zeros)


def fixed(shape):
    zeros = (0,) * len(shape)
    return pl.BlockSpec(shape, lambda *_: zeros, pipeline_mode=pl.Buffered(1))


def params(**extra):
    return pltpu.CompilerParams(vmem_limit_bytes=VMEM_LIMIT, **extra)


VMEM_SPEC = pl.BlockSpec(memory_space=pltpu.VMEM)
ANY_SPEC = pl.BlockSpec(memory_space=pl.ANY)


def side():
    return lax.axis_index("tensor")


def remote(src, dst, send_sem, recv_sem, target):
    return pltpu.make_async_remote_copy(
        src_ref=src,
        dst_ref=dst,
        send_sem=send_sem,
        recv_sem=recv_sem,
        device_id=target,
        device_id_type=pl.DeviceIdType.MESH,
    )


def each(count, run, first=0):
    def one(step, carry):
        run(step)
        return carry

    lax.fori_loop(first, count, one, 0)


class Place:
    def __init__(self, depth):
        position = lax.axis_index("context")
        self.depth = depth
        self.position = position
        self.x, self.y = lax.axis_index("dp"), lax.axis_index("tensor")
        self.z, self.c = position // 2, position % 2
        self.mate = self.at(self.x, self.y, self.z, 1 - self.c)
        self.x_peer = self.at(1 - self.x, self.y, self.z, self.c)
        self.y_peer = self.at(self.x, 1 - self.y, self.z, self.c)

    def at(self, x, y, z, c):
        return {"dp": x, "context": z * 2 + c, "tensor": y}

    def away(self, z):
        return self.at(self.x, self.y, z, self.c)

    def axes(self, turned):
        x, y, z, c = self.x, self.y, self.z, self.c
        x1, y1 = x + (1 - turned) * (1 - 2 * x), y + turned * (1 - 2 * y)
        x2, y2 = x + turned * (1 - 2 * x), y + (1 - turned) * (1 - 2 * y)
        return (x1, y1), (x2, y2)

    def around(self, run, first=0, last=None):
        z, depth = self.z, self.depth
        if first == 0:
            run(z)

        def step(away):
            @pl.when(z - away >= 0)
            def _():
                run(z - away)

            @pl.when(z + away < depth)
            def _():
                run(z + away)

        each(depth if last is None else last, step, max(first, 1))

    def greet(self, always, sometimes=(), column=False):
        barrier = pltpu.get_barrier_semaphore()
        kind = pl.DeviceIdType.MESH
        total = len(always)
        for target in always:
            pl.semaphore_signal(barrier, inc=1, device_id=target, device_id_type=kind)
        for holds, target in sometimes:

            @pl.when(holds)
            def _():
                pl.semaphore_signal(barrier, inc=1, device_id=target, device_id_type=kind)

            total = total + holds.astype(jnp.int32)
        if column:
            for_all = lambda step: pl.semaphore_signal(
                barrier,
                inc=1,
                device_id=self.away(lax.rem(self.z + step, self.depth)),
                device_id_type=kind,
            )
            each(self.depth, for_all, 1)
            total = total + (self.depth - 1)
        pl.semaphore_wait(barrier, total)


class Gathering:
    def __init__(self, place, own, full, sends, lands, local):
        self.place, self.own_ref, self.full = place, own, full
        self.sends, self.lands, self.local = sends, lands, local
        self.starts = [first * place.depth for first in (0, 4, 5, 7)]
        (self.x1, self.y1), (self.x2, self.y2) = place.axes(place.c)
        self.first = place.at(self.x1, self.y1, place.z, place.c)
        self.second = place.at(self.x2, self.y2, place.z, place.c)

    @staticmethod
    def scratch(depth):
        sem = pltpu.SemaphoreType.DMA
        return [sem((8 * depth,)), sem((8 * depth,)), sem((1,))]

    def copy(self, kind, index, x, y, z, c, target, own=False):
        chunk = self.full.at[y, x, z * 2 + c]
        mark = ((y * 2 + x) * self.place.depth + z) * 2 + c
        return remote(
            self.own_ref if own else chunk, chunk, self.sends.at[self.starts[kind] + index],
            self.lands.at[mark], target,
        )

    def arrive(self, x, y, z, c):
        self.copy(0, 0, x, y, z, c, self.place.mate).wait_recv()

    def kept(self):
        p = self.place
        return pltpu.make_async_copy(
            self.own_ref, self.full.at[p.y, p.x, p.z * 2 + p.c], self.local.at[0]
        )

    def own(self):
        p = self.place
        mine = (p.x, p.y, p.z, p.c)

        def far_z(z):
            self.copy(3, z, *mine, p.away(z), True).start()

        p.around(far_z, 1)
        self.copy(1, p.z, *mine, self.first, True).start()
        self.copy(2, p.z, *mine, self.second, True).start()
        self.copy(0, p.z, *mine, p.mate, True).start()
        self.kept().start()

    def near(self, first=1, last=None):
        p = self.place

        def run(z):
            chunk = (p.x, p.y, z, p.c)
            self.arrive(*chunk)

            self.copy(1, z, *chunk, self.first).start()
            self.copy(2, z, *chunk, self.second).start()
            self.copy(0, z, *chunk, p.mate).start()

        p.around(run, first, last)

    def across(self):
        p = self.place

        def run(z):
            chunk = (self.x1, self.y1, z, p.c)
            self.arrive(*chunk)
            self.copy(2, p.depth + z, *chunk, self.second).start()
            self.copy(0, p.depth + z, *chunk, p.mate).start()

        p.around(run)

    def far(self):
        p = self.place

        def near_row(z):
            self.arrive(self.x2, self.y2, z, p.c)
            self.copy(0, 2 * p.depth + z, self.x2, self.y2, z, p.c, p.mate).start()

        def far_row(z):
            self.arrive(1 - p.x, 1 - p.y, z, p.c)
            self.copy(0, 3 * p.depth + z, 1 - p.x, 1 - p.y, z, p.c, p.mate).start()

        p.around(near_row)
        p.around(far_row)

    def mates(self):
        p = self.place

        def from_mate(z):
            for y in range(2):
                for x in range(2):
                    self.arrive(x, y, z, 1 - p.c)

        each(p.depth, from_mate)
        self.kept().wait()

    def finish(self):
        p = self.place

        def sent(kind, index, target):
            self.copy(kind, index, p.x, p.y, p.z, p.c, target).wait_send()

        each(4 * p.depth, lambda step: sent(0, step, p.mate))
        each(p.depth, lambda step: sent(1, step, p.mate))
        each(2 * p.depth, lambda step: sent(2, step, p.mate))

        p.around(lambda z: sent(3, z, p.mate), 1)


class Reducing:
    def __init__(self, place, turned, parts, total, bufs, sems):
        self.place, self.parts, self.total = place, parts, total
        self.own, self.core, self.send1, self.land1 = bufs[:4]
        self.send2, self.land2, self.send3, self.land3 = bufs[4:]
        self.own_sem, self.core_send, self.core_land = sems[:3]
        self.s1, self.l1, self.s2, self.l2, self.s3, self.l3 = sems[3:]
        self.turned = turned
        (x1, y1), (x2, y2) = place.axes(turned)
        self.first = place.at(x1, y1, place.z, place.c)
        self.second = place.at(x2, y2, place.z, place.c)
        self.mine = place.y + turned * (place.x - place.y)

    @staticmethod
    def scratch(depth, rows, tall):
        buffer = lambda *lead: pltpu.VMEM(lead + (rows, tall), LOW)
        sem = lambda *lead: pltpu.SemaphoreType.DMA(lead)
        bufs = [
            buffer(2, 2, depth), buffer(2, 2, depth), buffer(depth, 2), buffer(depth, 2),
            buffer(depth), buffer(depth), buffer(depth), buffer(depth),
        ]
        return bufs + [sem(2, 2, depth)] * 3 + [sem(depth)] * 6

    def spot(self, step):
        return lax.rem(self.place.z + 1 + step, self.place.depth)

    def whole(self, y, x, z):
        return remote(
            self.core.at[y, x, z], self.core.at[y, x, z], self.core_send.at[y, x, z],
            self.core_land.at[y, x, z], self.place.mate,
        )

    def own_whole(self, y, x, z):
        return pltpu.make_async_copy(
            self.own.at[y, x, z], self.own.at[y, x, z], self.own_sem.at[y, x, z]
        )

    def start(self, step):
        p = self.place
        z = self.spot(step)
        for y in range(2):
            for x in range(2):
                for ref, cols in self.parts:
                    remote(
                        ref.at[y, x, z * 2 + 1 - p.c], self.core.at[y, x, z, :, cols],
                        self.core_send.at[y, x, z], self.core_land.at[y, x, z], p.mate,
                    ).start()
                    pltpu.make_async_copy(
                        ref.at[y, x, z * 2 + p.c], self.own.at[y, x, z, :, cols],
                        self.own_sem.at[y, x, z],
                    ).start()

    def base(self, y, x, z):
        return self.own[y, x, z].astype(F32) + self.core[y, x, z].astype(F32)

    def copy1(self, z):
        return remote(
            self.send1.at[z], self.land1.at[z], self.s1.at[z], self.l1.at[z], self.first
        )

    def copy2(self, z):
        return remote(
            self.send2.at[z], self.land2.at[z], self.s2.at[z], self.l2.at[z], self.second
        )

    def copy3(self, z, lands_at):
        return remote(
            self.send3.at[z], self.land3.at[lands_at], self.s3.at[z], self.l3.at[lands_at],
            self.place.away(z),
        )

    def stage1(self, step):
        p, turned = self.place, self.turned
        z = self.spot(step)
        for y in range(2):
            for x in range(2):
                self.whole(y, x, z).wait_recv()
                self.own_whole(y, x, z).wait()
        for index in range(2):
            x = (1 - turned) * (1 - p.x) + turned * index
            y = turned * (1 - p.y) + (1 - turned) * index
            self.send1[z, index] = self.base(y, x, z).astype(LOW)
        self.copy1(z).start()

    def stage2(self, step):
        p, turned = self.place, self.turned
        z = self.spot(step)
        self.copy1(z).wait_recv()
        other = 1 - self.mine
        x = (1 - turned) * p.x + turned * other
        y = turned * p.y + (1 - turned) * other
        self.send2[z] = (self.base(y, x, z) + self.land1[z, other].astype(F32)).astype(LOW)
        self.copy2(z).start()

    def final(self, z):
        p = self.place
        self.copy2(z).wait_recv()
        return (
            self.base(p.y, p.x, z)
            + self.land1[z, self.mine].astype(F32)
            + self.land2[z].astype(F32)
        )

    def stage3(self, step):
        z = self.spot(step)
        self.send3[z] = self.final(z).astype(LOW)
        self.copy3(z, self.place.z).start()

    def turn(self, step):
        depth = self.place.depth

        @pl.when(step < depth)
        def _():
            self.stage1(step)

        @pl.when((step >= 1) & (step <= depth))
        def _():
            self.stage2(step - 1)

        @pl.when((step >= 2) & (step <= depth))
        def _():
            self.stage3(step - 2)

    def close(self):
        p = self.place
        self.total[...] = self.final(p.z)

        def add(step):
            z = lax.rem(p.z + step, p.depth)
            self.copy3(z, z).wait_recv()
            self.total[...] += self.land3[z].astype(F32)

        each(p.depth, add, 1)

    def finish(self):
        p = self.place

        def sent(z):
            for y in range(2):
                for x in range(2):
                    self.whole(y, x, z).wait_send()
            self.copy1(z).wait_send()
            self.copy2(z).wait_send()

        each(p.depth, sent)
        each(p.depth, lambda step: self.copy3(lax.rem(p.z + step, p.depth), p.z).wait_send(), 1)


class Chaining:
    def __init__(self, place, rounds, backward, fold, gain, bufs, sems):
        self.place, self.rounds = place, rounds
        self.fold, self.gain = fold, gain
        self.from_mate, self.from_chip, self.to_mate, self.to_chip = bufs
        self.mate_send, self.mate_land, self.chip_send, self.chip_land = sems
        first = 1 if backward else 0
        by = -1 if backward else 1
        self.order = place.depth - 1 - place.z if backward else place.z
        self.leads = place.c == first
        self.after = place.at(place.x, place.y, place.z + by, first)
        self.before = place.at(place.x, place.y, place.z - by, 1 - first)
        self.linked_before = self.leads & (self.order > 0)
        self.linked_after = jnp.logical_not(self.leads) & (self.order < place.depth - 1)

    @staticmethod
    def scratch(rounds):
        slots = lambda turns: pltpu.VMEM((turns, GROUPS, NSTATE, WIDE), LOW)
        marks = lambda turns: pltpu.SemaphoreType.DMA((turns, GROUPS))
        return [
            slots(rounds + 1), slots(rounds), slots(rounds + 1), slots(rounds),
            marks(rounds + 1), marks(rounds + 1), marks(rounds), marks(rounds),
        ]

    def sometimes(self):
        return [(self.linked_before, self.before), (self.linked_after, self.after)]

    def mate_copy(self, turn, cut):
        return remote(
            self.to_mate.at[turn, cut], self.from_mate.at[turn, cut], self.mate_send.at[turn, cut],
            self.mate_land.at[turn, cut], self.place.mate,
        )

    def chip_copy(self, turn, cut):
        return remote(
            self.to_chip.at[turn, cut], self.from_chip.at[turn, cut], self.chip_send.at[turn, cut],
            self.chip_land.at[turn, cut], self.after,
        )

    def joined(self, cut, arrived):
        return (self.fold[cut] + self.gain[cut, 0:1] * arrived.astype(F32)).astype(LOW)

    def open(self, cut):
        @pl.when(self.leads)
        def _():
            self.to_mate[0, cut] = self.fold[cut].astype(LOW)
            self.mate_copy(0, cut).start()

    def pass_on(self, turn, cut):
        @pl.when(jnp.logical_not(self.leads))
        def _():
            self.mate_copy(turn, cut).wait_recv()

        @pl.when(self.linked_after)
        def _():
            self.to_chip[turn, cut] = self.joined(cut, self.from_mate[turn, cut])
            self.chip_copy(turn, cut).start()

    def relay(self, turn, cut):
        @pl.when(self.linked_before)
        def _():
            self.chip_copy(turn, cut).wait_recv()
            self.to_mate[turn + 1, cut] = self.joined(cut, self.from_chip[turn, cut])
            self.mate_copy(turn + 1, cut).start()

        @pl.when(self.leads & (self.order == 0))
        def _():
            self.to_mate[turn + 1, cut] = self.fold[cut].astype(LOW)
            self.mate_copy(turn + 1, cut).start()

    def later(self):
        for turn in range(1, self.rounds):
            for cut in range(GROUPS):
                self.pass_on(turn, cut)
            for cut in range(GROUPS):
                self.relay(turn, cut)

    def arrive(self, put):
        last = self.rounds - 1

        @pl.when(self.linked_before)
        def _():
            for cut in range(GROUPS):
                put(cut, self.from_chip[last, cut])

        @pl.when(self.leads & (self.order == 0))
        def _():
            for cut in range(GROUPS):
                put(cut, jnp.zeros((NSTATE, WIDE), LOW))

        @pl.when(jnp.logical_not(self.leads))
        def _():
            for cut in range(GROUPS):
                self.mate_copy(self.rounds, cut).wait_recv()
                put(cut, self.from_mate[self.rounds, cut])

    def finish(self):
        @pl.when(self.leads)
        def _():
            for turn in range(self.rounds + 1):
                for cut in range(GROUPS):
                    self.mate_copy(turn, cut).wait_send()

        @pl.when(self.linked_after)
        def _():
            for turn in range(self.rounds):
                for cut in range(GROUPS):
                    self.chip_copy(turn, cut).wait_send()


class Closing:
    def __init__(self, place, token, token_out, refs):
        self.place, self.token, self.token_out = place, token, token_out
        self.state_own, self.state_in, self.send, self.land = refs[:4]
        self.vs, self.vl, self.ts, self.tl, self.ss, self.sl, self.keep_sem = refs[4:]
        self.targets = [place.mate, place.y_peer, place.x_peer]

    @staticmethod
    def scratch(depth, own_rows, vector):
        sem = lambda *lead: pltpu.SemaphoreType.DMA(lead)
        return [
            pltpu.VMEM((own_rows, NSTATE), F32),
            pltpu.VMEM((2, own_rows, NSTATE), F32),
            pltpu.VMEM((4,) + vector, F32),
            pltpu.VMEM((3 + depth,) + vector, F32),
            sem(3 + depth), sem(3 + depth), sem(depth), sem(depth), sem(1), sem(1), sem(1),
        ]

    def vec_copy(self, turn):
        return remote(
            self.send.at[turn], self.land.at[turn], self.vs.at[turn], self.vl.at[turn],
            self.targets[turn],
        )

    def vec_far(self, away, lands_at):
        return remote(
            self.send.at[3], self.land.at[3 + lands_at], self.vs.at[3 + away],
            self.vl.at[3 + lands_at], self.place.away(away),
        )

    def token_copy(self, step):
        p = self.place
        share = self.token.shape[0] // p.depth
        at = pl.ds(pl.multiple_of(step * share, share), share)
        return remote(
            self.token.at[at], self.token_out.at[p.y, at], self.ts.at[step], self.tl.at[step],
            p.y_peer,
        )

    def run(self, reducing, width, state_out, vector_out, first, pending=None):
        p = self.place
        depth, z = p.depth, p.z
        keep = pltpu.make_async_copy(self.token, self.token_out.at[p.y], self.keep_sem.at[0])
        keep.start()
        self.vec_copy(0).start()

        def step_all(step):
            if pending is not None:

                @pl.when(step + 3 <= depth)
                def _():
                    pending.turn(step + 3)

            reducing.turn(step)

            @pl.when(step < depth)
            def _():
                self.token_copy(step).start()

            for turn in range(3):

                @pl.when(step == turn)
                def _():
                    self.vec_copy(turn).wait_recv()
                    self.send[turn + 1] = self.send[turn] + self.land[turn]
                    if turn < 2:
                        self.vec_copy(turn + 1).start()
                    else:
                        each(depth, lambda s: self.vec_far(lax.rem(z + s, depth), z).start(), 1)
                        self.land[3 + z] = self.send[3]

        each(depth + 1, step_all)
        if pending is not None:
            pending.close()
        reducing.close()
        self.state_own[...] = reducing.total[:, first : first + width]
        state_copy = remote(
            self.state_own, self.state_in.at[p.y], self.ss.at[0], self.sl.at[0], p.y_peer
        )
        state_copy.start()
        self.state_in[p.y] = self.state_own[...]

        def vec_arrive(step):
            away = lax.rem(z + step, depth)
            self.vec_far(away, away).wait_recv()

        each(depth, vec_arrive, 1)
        vector_out[...] = self.land[3]

        def vec_add(step):
            vector_out[...] += self.land[3 + step]

        each(depth, vec_add, 1)
        for turn in range(3):
            self.vec_copy(turn).wait_send()
        each(depth, lambda s: self.vec_far(lax.rem(z + s, depth), z).wait_send(), 1)
        reducing.finish()
        each(depth, lambda step: self.token_copy(step).wait())
        state_copy.wait()
        state_out[...] = self.state_in[...]
        keep.wait()


def group_of(index):
    half, part = index % 2, index // 2
    return half * 3 + part, half, part


def turn_of(step):
    return group_of(jnp.maximum(step - 1, 0))


def entry_body(depth, rounds, fused, *refs):
    step = pl.program_id(0)
    tokens, doc_col, doc_row, state_filter = refs[:4]
    if fused:
        own_small, own_parts, own_exit, own_par, own_edge, own_docs, cot = refs[4:11]
    else:
        w_gate, w_inner, w_small, par, heads_ref, edge, halo_docs = refs[4:11]
    (
        hidden_out, cin_out, gate_out, pre_out, loc_out, carry_out, cin_state_out, pre_state_out,
        bc_out, bct_out, score_out, mask_out, zst_out, dt_out, sp_out, cumt_out, fac_out, match_out,
        local_out,
    ) = refs[11:30]
    refs = refs[30:]
    if fused:
        small_out, parts_out, exit_out, par, heads_ref, cot_t = refs[:6]
        refs = refs[6:]
    hidden, normed, sp_tail, facs, folds, gains = refs[:6]
    rows, model = tokens.shape[1:]
    spans = rows // Q
    place = Place(depth)
    chaining = Chaining(place, rounds, False, folds, gains, refs[6:10], refs[10:14])
    group, half, part = turn_of(step)
    y = place.y
    if fused:
        v_small, v_parts, edge, halo_docs, docs_in, cot_in, par_in = refs[14:21]
        side_send, side_land, local, out_sem = refs[21:25]
        marks = refs[25:]
        own = [own_small, own_parts.at[0], own_parts.at[1], own_parts.at[2], own_exit]
        full = [v_small, v_parts.at[0], v_parts.at[1], v_parts.at[2], exit_out]
        pieces = [
            Gathering(place, own[i], full[i], *marks[3 * i : 3 * i + 3]) for i in range(5)
        ]
        stores = [pltpu.make_async_copy(v_small, small_out, out_sem.at[0])]
        for index in range(3):
            stores.append(
                pltpu.make_async_copy(
                    v_parts.at[index], parts_out.at[index], out_sem.at[index + 1]
                )
            )

    def before_weights():
        for ref, first, count in ((edge, 0, HALO), (tokens, HALO, rows)):
            value = (ref[...] if ref is edge else ref[0]).astype(F32)
            scale = lax.rsqrt(jnp.mean(value * value, axis=1, keepdims=True) + EPSILON)
            normed[first : first + count] = value * scale
        docs = jnp.concatenate([halo_docs[...], doc_col[...]], axis=0)
        for back in range(1, CONV):
            match = (docs[HALO - back : HALO - back + rows] == docs[HALO:]).astype(F32)
            match_out[back - 1] = match
        t_at, u_at = iota((Q, Q), 0), iota((Q, Q), 1)
        for index in range(spans):
            at = slice(index * Q, (index + 1) * Q)
            same = (t_at >= u_at) & (doc_col[at] == doc_row[0:1, at])
            mask_out[at] = jnp.where(same, 0.0, FAR)

    def after_weights(small):
        gain = jnp.transpose(small[0][:, LANES:].astype(F32))[24:25]
        hidden[...] = (normed[...] * gain).astype(LOW)
        hidden_out[...] = jnp.transpose(hidden[HALO:])
        both = [mm(hidden[...], small[index]) for index in range(2)]
        cin = jnp.concatenate([both[0][:, :LANES], both[1][:, :LANES]], axis=1).astype(LOW)
        cin_state_out[...] = cin
        docs = jnp.concatenate([halo_docs[...], doc_col[...]], axis=0)
        masks = [match_out[back] for back in range(CONV - 1)]
        pre = conv_forward(cin.astype(F32), state_filter[...], masks)
        pre_state_out[...] = pre
        mixed = (pre * sigmoid(pre)).astype(LOW)
        bc_out[...] = mixed
        turned = jnp.transpose(mixed.astype(F32)).astype(LOW)
        bct_out[...] = turned
        heads = heads_ref[...]
        used = iota((rows, LANES), 1) < 24
        raw = both[0][HALO:, LANES:] + both[1][HALO:, LANES:]
        zst = jnp.where(used, raw, 0.0) + heads[0:1]
        zst_out[...] = zst
        dt = jnp.where(used, jnp.maximum(zst, 0.0) + jnp.log1p(jnp.exp(-jnp.abs(zst))), 0.0)
        dt_out[...] = dt
        decay = -dt * jnp.exp(heads[1:2])
        t_at, u_at = iota((Q, Q), 0), iota((Q, Q), 1)
        lower = (t_at >= u_at).astype(F32)
        fac_rows = []
        for index in range(spans):
            at = slice(index * Q, (index + 1) * Q)
            cum = mm_exact(lower, decay[at])
            final = cum[Q - 1 : Q]
            before = docs[HALO + index * Q - 1 : HALO + index * Q]
            here = doc_col[at]
            last = here[Q - 1 : Q]
            opened = (here == before).astype(F32)
            tail = (here == last).astype(F32) * jnp.exp(final - cum)
            fac_rows.append((last == before).astype(F32) * jnp.exp(final))
            cum2 = cum * LOG2E
            turned_cum = jnp.transpose(cum2)
            for group in range(6):
                cumt_out[group, 0:4, at] = turned_cum[4 * group : 4 * group + 4]
            sp_out[0, at] = split3(dt[at])
            sp_out[1, at] = split3(cum2)
            lanes_used = iota((Q, LANES), 1) < 24
            sp_out[2, at] = split3(jnp.where(lanes_used, opened * jnp.exp(cum), 0.0))
            sp_out[3, at] = split3(jnp.where(lanes_used, tail, 0.0))
            sp_tail[at] = split3(jnp.where(lanes_used, tail * dt[at], 0.0))
            score_out[at] = mm_nt(mixed[at, LANES:], mixed[at, :LANES])
        gain_total = fac_rows[0]
        for row in fac_rows[1:]:
            gain_total = gain_total * row
        rows8 = jnp.concatenate(
            fac_rows + [gain_total] + [jnp.zeros((1, LANES), F32)] * (7 - spans), axis=0
        )
        rows8 = jnp.where(iota((8, LANES), 1) < 24, rows8, 0.0)
        fac_out[...] = rows8
        facs[...] = split3(rows8)

    if fused:

        @pl.when(step == 0)
        def _():
            count = 2 * depth
            onward = {"context": lax.rem(place.position + 1, count)}
            behind = {"context": lax.rem(place.position + count - 1, count)}
            place.greet(
                [place.mate, place.x_peer, place.y_peer, onward, behind], chaining.sometimes(), True
            )
            sides = [
                remote(own_edge, edge, side_send.at[0], side_land.at[0], onward),
                remote(own_docs, docs_in, side_send.at[1], side_land.at[1], onward),
                remote(own_par, par_in.at[y], side_send.at[2], side_land.at[2], place.y_peer),
            ]
            for copy in sides:
                copy.start()
            for piece in pieces:
                piece.own()
            cot_copy = pltpu.make_async_copy(cot.at[y], cot_in, local.at[0])
            par_keep = pltpu.make_async_copy(own_par, par_in.at[y], local.at[1])
            cot_copy.start()
            par_keep.start()
            for copy in sides:
                copy.wait()
            par_keep.wait()
            pieces[0].near()
            pieces[1].near()
            halo_docs[...] = jnp.where(place.position == 0, -1.0, docs_in[...])
            par[...] = par_in[...]
            both = par[0, CONV + 2 : CONV + 3] + par[1, CONV + 2 : CONV + 3]
            heads_ref[...] = jnp.zeros_like(heads_ref)
            for index in range(3):
                heads_ref[index : index + 1] = both[:, index * LANES : (index + 1) * LANES]
            before_weights()
            pieces[0].across()
            pieces[2].near()
            pieces[1].across()
            pieces[0].far()
            cot_copy.wait()
            cot_t[...] = jnp.transpose(cot_in[...])
            pieces[0].mates()
            stores[0].start()
            after_weights([v_small[index].reshape(model, WIDE) for index in range(2)])

        @pl.when(step == 1)
        def _():
            pieces[3].near()
            pieces[2].across()
            pieces[1].far()
            pieces[1].mates()
            stores[1].start()

        @pl.when(step == 2)
        def _():
            pieces[4].near()

        @pl.when(step == 3)
        def _():
            pieces[3].across()
            pieces[2].far()
            pieces[2].mates()
            stores[2].start()

        @pl.when(step == 4)
        def _():
            pieces[4].across()

        @pl.when(step == 5)
        def _():
            pieces[3].far()
            pieces[3].mates()
            stores[3].start()

        @pl.when(step == 6)
        def _():
            pieces[4].far()

    else:

        @pl.when(step == 0)
        def _():
            place.greet([place.mate], chaining.sometimes())
            before_weights()
            after_weights([w_small[index] for index in range(2)])

    for cut in range(GROUPS - 1):

        @pl.when(step == cut + 2)
        def _():
            chaining.pass_on(0, cut)

    for cut in range(GROUPS - 3):

        @pl.when(step == cut + 4)
        def _():
            chaining.relay(0, cut)

    @pl.when(step > 0)
    def _():
        if fused:
            gate_low = v_parts[part, half, :, :, :, :WIDE].reshape(model, WIDE)
            inner_low = v_parts[part, half, :, :, :, WIDE:].reshape(model, WIDE)
        else:
            gate_low, inner_low = w_gate[0, 0], w_inner[0, 0]
        taps = par[half, :, pl.ds(pl.multiple_of(part * WIDE, WIDE), WIDE)]
        cin = mm(hidden[...], inner_low).astype(LOW)
        cin_out[...] = cin
        gate_out[...] = mm(hidden[HALO:], gate_low)
        masks = [match_out[back] for back in range(CONV - 1)]
        pre = conv_forward(cin.astype(F32), taps, masks)
        pre_out[...] = pre
        spread = spreader(4 * group, HEAD, 4)
        mix = pre * sigmoid(pre)
        value = (mix * mm(sp_tail[...], spread)).astype(LOW)
        facx = mm(facs[...], spread)
        cums = mm(sp_out[1], spreader(4 * group, LANES, 4))
        skipx = mm(split3(heads_ref[...]), spread)[2:3]
        stepped = mix * mm(sp_out[0], spread)
        first_half = iota((Q, LANES), 1) < HEAD
        fold = jnp.zeros((NSTATE, WIDE), F32)
        for index in range(spans):
            at = slice(index * Q, (index + 1) * Q)
            loc = mm(bct_out[:NSTATE, at], value[at])
            loc_out[at] = loc
            fold = facx[index : index + 1] * fold + loc
            parts = []
            for pair in range(2):
                lanes = slice(pair * LANES, (pair + 1) * LANES)
                weights, seen = [], []
                for head in (2 * pair, 2 * pair + 1):
                    across = cumt_out[group, head : head + 1, at]
                    spread_at = cums[at, head * LANES : (head + 1) * LANES] - across + mask_out[at]
                    weights.append((jnp.exp2(spread_at) * score_out[at]).astype(LOW))
                    keep = first_half if head % 2 == 0 else jnp.logical_not(first_half)
                    seen.append(jnp.where(keep, stepped[at, lanes], 0.0).astype(LOW))
                parts.append(mm(jnp.concatenate(weights, axis=1), jnp.concatenate(seen, axis=0)))
            local_out[at] = jnp.concatenate(parts, axis=1) + skipx * mix[at]
        folds[step - 1] = fold
        gains[step - 1] = jnp.broadcast_to(facx[spans : spans + 1], (8, WIDE))

    for cut in range(GROUPS):

        @pl.when(step == cut + 1)
        def _():
            chaining.open(cut)

    @pl.when(step == GROUPS)
    def _():
        chaining.pass_on(0, GROUPS - 1)
        for cut in range(GROUPS - 3, GROUPS):
            chaining.relay(0, cut)
        chaining.later()

        def put(cut, value):
            at = ORDER[cut] * WIDE
            carry_out[:, at : at + WIDE] = value

        chaining.arrive(put)
        if fused:
            pieces[4].mates()
            for piece in pieces:
                piece.finish()
            for store in stores:
                store.wait()
        chaining.finish()


def entry(tokens, doc_col, doc_row, state_filter, packs, cot, rounds):
    own_small, own_parts, own_exit, own_par, own_edge, own_docs = packs
    rows, model = tokens.shape[1:]
    count = lax.axis_size("context")
    depth = count // 2
    wide = GROUPS * WIDE
    ext = rows + HALO
    fused = own_small.shape[0] % 16 == 0
    shape = jax.ShapeDtypeStruct
    sem = lambda *lead: pltpu.SemaphoreType.DMA(lead)
    column = lambda count: pl.BlockSpec((count, WIDE), lambda s: (0, turn_of(s)[0]))
    whole = lambda *dims, dtype=F32: (shape(dims, dtype), const(dims))
    outs = [
        whole(model, rows, dtype=LOW),
        (shape((ext, wide), LOW), column(ext)),
        (shape((rows, wide), F32), column(rows)),
        (shape((rows, wide), F32), column(rows)),
        (shape((rows, wide), F32), column(rows)),
        whole(NSTATE, wide, dtype=LOW),
        whole(ext, WIDE, dtype=LOW),
        whole(rows, WIDE),
        whole(rows, WIDE, dtype=LOW),
        whole(WIDE, rows, dtype=LOW),
        whole(rows, Q),
        whole(rows, Q),
        whole(rows, LANES),
        whole(rows, LANES),
        whole(4, rows, LANES, dtype=LOW),
        whole(6, 8, rows),
        whole(8, LANES),
        whole(CONV - 1, rows, LANES),
        (shape((rows, wide), F32), column(rows)),
    ]
    scratch = [
        pltpu.VMEM((ext, model), LOW),
        pltpu.VMEM((ext, model), F32),
        pltpu.VMEM((rows, LANES), LOW),
        pltpu.VMEM((8, LANES), LOW),
        pltpu.VMEM((GROUPS, NSTATE, WIDE), F32),
        pltpu.VMEM((GROUPS, 8, WIDE), F32),
    ] + Chaining.scratch(rounds)
    in_specs = [
        pl.BlockSpec((1, rows, model), lambda s: (side(), 0, 0)),
        fixed((rows, LANES)),
        fixed((8, rows)),
        fixed((CONV + 1, WIDE)),
    ]
    args = [tokens, doc_col, doc_row, state_filter]
    full = lambda own: (2, 2, count) + own.shape[-2:]
    if fused:
        outs += [
            (shape(full(own_small), LOW), ANY_SPEC),
            (shape((3,) + full(own_parts), LOW), ANY_SPEC),
            (shape(full(own_exit), LOW), ANY_SPEC),
            (shape((2,) + own_par.shape, F32), VMEM_SPEC),
            (shape((8, LANES), F32), VMEM_SPEC),
            (shape((model, rows), LOW), VMEM_SPEC),
        ]
        scratch += [
            pltpu.VMEM(full(own_small), LOW),
            pltpu.VMEM((3,) + full(own_parts), LOW),
            pltpu.VMEM(own_edge.shape, LOW),
            pltpu.VMEM(own_docs.shape, F32),
            pltpu.VMEM(own_docs.shape, F32),
            pltpu.VMEM((rows, model), LOW),
            pltpu.VMEM((2,) + own_par.shape, F32),
            sem(3),
            sem(3),
            sem(2),
            sem(4),
        ] + Gathering.scratch(depth) * 5
        in_specs += [VMEM_SPEC] * 6 + [ANY_SPEC]
        args += [own_small, own_parts, own_exit, own_par, own_edge, own_docs, cot]
    else:
        small, parts, exits, par, heads, edge, docs, cot_t = gather(*packs, cot)
        weights = parts.reshape(3, 2, model, 2 * WIDE)
        block = lambda at: pl.BlockSpec(
            (1, 1, model, WIDE), lambda s: (turn_of(s)[2], turn_of(s)[1], 0, at)
        )
        in_specs += [block(0), block(1), fixed((2, model, WIDE))] + [VMEM_SPEC] * 4
        args += [weights, weights, small.reshape(2, model, WIDE), par, heads, edge, docs]
    results = pl.pallas_call(
        functools.partial(entry_body, depth, rounds, fused),
        out_shape=[out[0] for out in outs],
        grid=(GROUPS + 1,),
        in_specs=in_specs,
        out_specs=[out[1] for out in outs],
        scratch_shapes=scratch,
        compiler_params=params(collective_id=1, has_side_effects=True),
        name="entry",
    )(*args)
    if fused:
        small, parts, exits, par, heads, cot_t = results[19:]
    return tuple(results[:19]), (
        small.reshape(2, model, WIDE),
        parts.reshape(3, 2, model, 2 * WIDE),
        exits.reshape(2, model, -1),
        par,
        heads,
        cot_t,
    )


def middle_body(
    tokens_far, cot, cot_t_far, hidden_far, pre_ref, gate_ref, loc_ref, local_ref, carry_ref, w_exit,
    par, bc, bct, sp, fac, block_out, exit_out, gate_part_out, dy_out, gpg_out, enter_out, row_out,
    skip_out, outputs, gates, unit_grads, mixes, sums, total,
    tokens, cot_t, hidden_t, late_sem
):
    step = pl.program_id(0)
    rows = pre_ref.shape[0]
    spans = rows // Q
    wide = 6 * WIDE

    late = [
        pltpu.make_async_copy(src, dst, late_sem.at[index])
        for index, (src, dst) in enumerate(
            ((cot_t_far, cot_t), (hidden_far, hidden_t), (tokens_far.at[side()], tokens))
        )
    ]

    @pl.when(step == 0)
    def _():
        for copy in late:
            copy.start()
        sums[...] = jnp.zeros_like(sums)
        total[...] = jnp.zeros_like(total)
        skip_out[...] = jnp.zeros_like(skip_out)

    @pl.when(step < 6)
    def _():
        group = step
        spread = spreader(4 * group, HEAD, 4)
        pre = pre_ref[...]
        mix = pre * sigmoid(pre)
        mixes[group] = mix
        growth = mm(sp[2], spread)
        facx = mm(split3(fac[...]), spread)
        state = carry_ref[...].astype(F32)
        for index in range(spans):
            at = slice(index * Q, (index + 1) * Q)
            carried = mm(bc[at, LANES:], state.astype(LOW)) * growth[at]
            out = local_ref[at] + carried
            outputs[group, at] = out
            state = facx[index : index + 1] * state + loc_ref[at]
        gate = gate_ref[...]
        gates[group] = gate
        gated = outputs[group] * (gate * sigmoid(gate))
        unit_grad = mm(cot[0], w_exit[0])
        unit_grads[group] = unit_grad
        square = gated * gated
        cross = unit_grad * par[0, 5:6] * gated
        sums[0] += square[:, :LANES] + square[:, LANES:]
        sums[1] += cross[:, :LANES] + cross[:, LANES:]

    @pl.when(step == 5)
    def _():
        for copy in late:
            copy.wait()
        square = jnp.sum(sums[0], axis=1, keepdims=True)
        cross = jnp.sum(sums[1], axis=1, keepdims=True)
        normal = lax.rsqrt(square / wide + EPSILON)
        sums[0] = jnp.broadcast_to(normal, (rows, LANES))
        sums[1] = jnp.broadcast_to(normal * normal * normal * cross / wide, (rows, LANES))

    @pl.when(step >= 6)
    def _():
        group = step - 6
        spread = spreader(4 * group, HEAD, 4)
        normal = twice(sums[0])
        pull = twice(sums[1])
        gain = par[0, 5:6]
        gate = gates[group]
        out = outputs[group]
        unit_grad = unit_grads[group]
        sigma = sigmoid(gate)
        act = gate * sigma
        gated = out * act
        scaled_in = gated * normal
        unit = (scaled_in * gain).astype(LOW)
        total[...] += mm_nt(unit, w_exit[0])
        exit_out[0] = mm(cot_t[...], unit).astype(LOW)
        gate_sum = jnp.sum(unit_grad * scaled_in, axis=0, keepdims=True)
        gated_grad = normal * (unit_grad * gain) - pull * gated
        dy = gated_grad * act
        dy_out[...] = dy
        gate_grad = (gated_grad * out * sigma * (1.0 + gate * (1.0 - sigma))).astype(LOW)
        gpg_out[...] = gate_grad
        gate_part_out[0] = mm(hidden_t[...], gate_grad).astype(LOW)
        skip_sum = jnp.sum(dy * mixes[group], axis=0, keepdims=True)
        row_out[...] = jnp.broadcast_to(gate_sum, (8, WIDE))
        skip_out[...] += head_sums(
            jnp.broadcast_to(skip_sum, (8, WIDE)), gatherer(4 * group, HEAD, 4)
        )
        facx = mm(split3(fac[...]), spread)
        pushed = (dy * mm(sp[2], spread)).astype(LOW)
        enter = jnp.zeros((NSTATE, WIDE), F32)
        for index in reversed(range(spans)):
            at = slice(index * Q, (index + 1) * Q)
            enter = facx[index : index + 1] * enter + mm(bct[NSTATE:, at], pushed[at])
        enter_out[...] = enter

    @pl.when(step == 11)
    def _():
        block_out[...] = (tokens[...].astype(F32) + total[...]).astype(LOW)


def middle(
    tokens, cot, cot_t, hidden_t, pre, gate, loc, local, carry, weights, par, bc, bct, sp, fac
):
    rows, model = tokens.shape[1:]
    wide = 6 * WIDE
    shape = jax.ShapeDtypeStruct

    def early(s):
        return jnp.minimum(s, 5)

    def late(s):
        return jnp.maximum(s - 6, 0)

    def group(s):
        return s % 6

    outs = (
        (shape((rows, model), LOW), const((rows, model))),
        (
            shape((2, model, 3 * WIDE), LOW),
            pl.BlockSpec((1, model, WIDE), lambda s: (late(s) // 3, 0, late(s) % 3)),
        ),
        (
            shape((2, model, 3 * WIDE), LOW),
            pl.BlockSpec((1, model, WIDE), lambda s: (late(s) // 3, 0, late(s) % 3)),
        ),
        (shape((rows, wide), F32), pl.BlockSpec((rows, WIDE), lambda s: (0, late(s)))),
        (shape((rows, wide), LOW), pl.BlockSpec((rows, WIDE), lambda s: (0, late(s)))),
        (shape((NSTATE, wide), F32), pl.BlockSpec((NSTATE, WIDE), lambda s: (0, late(s)))),
        (shape((8, wide), F32), pl.BlockSpec((8, WIDE), lambda s: (0, late(s)))),
        (shape((8, LANES), F32), const((8, LANES))),
    )
    return pl.pallas_call(
        middle_body,
        out_shape=[out[0] for out in outs],
        grid=(12,),
        in_specs=[
                ANY_SPEC,
                pl.BlockSpec((1, rows, model), lambda s: (side(), 0, 0)),
                ANY_SPEC,
                ANY_SPEC,
                pl.BlockSpec((rows, WIDE), lambda s: (0, early(s))),
                pl.BlockSpec((rows, WIDE), lambda s: (0, early(s))),
                pl.BlockSpec((rows, WIDE), lambda s: (0, early(s))),
                pl.BlockSpec((rows, WIDE), lambda s: (0, early(s))),
                pl.BlockSpec((NSTATE, WIDE), lambda s: (0, early(s))),
                pl.BlockSpec((1, model, WIDE), lambda s: (group(s) // 3, 0, group(s) % 3)),
                pl.BlockSpec((1, 8, WIDE), lambda s: (group(s) // 3, 0, group(s) % 3)),
                fixed((rows, WIDE)),
                fixed((WIDE, rows)),
                fixed((4, rows, LANES)),
                fixed((8, LANES)),
        ],
        out_specs=[out[1] for out in outs],
        scratch_shapes=[
                pltpu.VMEM((6, rows, WIDE), F32),
                pltpu.VMEM((6, rows, WIDE), F32),
                pltpu.VMEM((6, rows, WIDE), F32),
                pltpu.VMEM((6, rows, WIDE), F32),
                pltpu.VMEM((2, rows, LANES), F32),
                pltpu.VMEM((rows, model), F32),
                pltpu.VMEM((rows, model), LOW),
                pltpu.VMEM((model, rows), LOW),
                pltpu.VMEM((model, rows), LOW),
                pltpu.SemaphoreType.DMA((3,)),
        ],
        compiler_params=params(),
        name="middle",
    )(tokens, cot, cot_t, hidden_t, pre, gate, loc, local, carry, weights, par, bc, bct, sp, fac)


def scan_back_body(depth, rounds, fused, *refs):
    (
        pre_ref, dy_ref, loc_ref, carry_ref, enter, cin_ref, par, par_heads, state_filter, cin_far,
        pre_far, bc, bct, score, mask, sp, cumt, fac, match_far, zst_far, dt_far, exits, gate_part,
        block_far, tokens_far, cot_far, hidden_far, gpg, w_gate, w_inner, small_far, gate_row,
        skip_row,
    ) = refs[:33]
    mine, block_out = refs[33:35]
    if fused:
        mine2, mine3, state_out, vector_out, token_both = refs[35:40]
        refs = refs[40:]
    else:
        tap_out, tap_state_out, small_out, inner_part, small_part, token_out, norm_out = refs[35:42]
        refs = refs[42:]
    block_own, hidden_t, match, tokens, cot, w_small, pre_state, cin_state, zst, dt_ref = refs[:10]
    late_sem = refs[10]
    refs = refs[11:]
    late = [
        pltpu.make_async_copy(src, dst, late_sem.at[index])
        for index, (src, dst) in enumerate(
            (
                (block_far, block_own), (hidden_far, hidden_t), (match_far, match),
                (tokens_far.at[side()], tokens), (cot_far.at[side()], cot), (small_far, w_small),
                (pre_far, pre_state), (cin_far, cin_state), (zst_far, zst), (dt_far, dt_ref),
            )
        )
    ]
    (
        d_bc, d_score, d_cum, heads, local_value, enters, gains, adjoints, edge_own, edge_in, grads,
        total, es, el, bs, bl, block_keep,
    ) = refs[:17]
    scratch = refs[17:42]
    step = pl.program_id(0)
    group, half_at, part_at = group_of(jnp.minimum(step, GROUPS - 1))
    last_group, last_half, last_part = group_of(jnp.maximum(step - 1, 0))
    blocks = BLOCK_CUTS
    rows = pre_ref.shape[0]
    spans = rows // Q
    place = Place(depth)
    wide = exits.shape[-1]
    chaining = Chaining(place, rounds, True, enters, gains, scratch[:4], scratch[4:8])
    reducing = Reducing(
        place, 0, [(exits, slice(0, wide)), (gate_part, slice(wide, 2 * wide))], mine,
        scratch[8:16], scratch[16:25],
    )
    if fused:
        inner_v, small_v, token_v, taps_v = refs[42:46]
        buffers = refs[46:]
        second = Reducing(
            place, 0, [(inner_v.at[0], slice(0, WIDE)), (inner_v.at[1], slice(WIDE, 2 * WIDE))],
            mine2, buffers[:8], buffers[8:17],
        )
        third = Reducing(
            place, 0, [(inner_v.at[2], slice(0, WIDE)), (small_v, slice(WIDE, 2 * WIDE))], mine3,
            buffers[17:25], buffers[25:34],
        )
        closing = Closing(place, token_v, token_both, buffers[34:])
    position = place.position
    has_before, has_after = position > 0, position < 2 * depth - 1
    before, after = {"context": position - 1}, {"context": position + 1}
    share = rows // blocks

    def block_copy(index):
        at = pl.ds(pl.multiple_of(index * share, share), share)
        return remote(
            block_own.at[at], block_out.at[place.y, at], bs.at[index], bl.at[index], place.y_peer
        )

    block_local = pltpu.make_async_copy(block_own, block_out.at[place.y], block_keep.at[0])

    def edge_copy(index):
        return remote(edge_own.at[index], edge_in.at[index], es.at[index], el.at[index], before)

    def edge_wait(index):
        @pl.when(has_after)
        def _():
            edge_copy(index).wait_recv()

    def put_inner(value):
        if fused:
            inner_v[last_part, last_half] = value.reshape(inner_v.shape[2:])
        else:
            inner_part[0] = value

    def joined(index):
        grad = grads[...]
        return jnp.concatenate(
            [grad[: rows - EDGE], grad[rows - EDGE :] + edge_in[index]], axis=0
        ).astype(LOW)

    @pl.when(step == 0)
    def _():
        for copy in late:
            copy.start()
        d_bc[...] = jnp.zeros_like(d_bc)
        d_score[...] = jnp.zeros_like(d_score)
        d_cum[...] = jnp.zeros_like(d_cum)
        heads[...] = jnp.zeros_like(heads)
        grads[...] = jnp.zeros_like(grads)
        total[...] = jnp.zeros_like(total)
        edge_in[GROUPS + 1] = jnp.zeros((EDGE, WIDE), F32)

        @pl.when(jnp.logical_not(has_after))
        def _():
            edge_in[...] = jnp.zeros_like(edge_in)

        place.greet(
            [place.mate, place.x_peer, place.y_peer],
            chaining.sometimes() + [(has_before, before), (has_after, after)],
            True,
        )
        facs = split3(fac[...])
        for cut in range(GROUPS):
            enters[cut] = enter[:, cut * WIDE : (cut + 1) * WIDE]
            chaining.open(cut)
        for cut in range(GROUPS):
            rows8 = mm(facs, spreader(4 * cut, HEAD, 4))
            gains[cut] = jnp.broadcast_to(rows8[spans : spans + 1], (8, WIDE))
        each(depth, reducing.start)
        late[0].wait()
        block_local.start()
        each(3, lambda index: block_copy(index).start())
        for cut in range(GROUPS):
            chaining.pass_on(0, cut)

    if fused:

        @pl.when(step == 5)
        def _():
            each(depth, second.start)

    @pl.when(step < GROUPS)
    def _():
        spread = spreader(4 * group, HEAD, 4)
        collect = gatherer(4 * group, HEAD, 4)
        pre = pre_ref[...]
        sigma = sigmoid(pre)
        mix = pre * sigma
        dtx = mm(sp[0], spread)
        growth = mm(sp[2], spread)
        facx = mm(split3(fac[...]), spread)
        cums = mm(sp[1], spreader(4 * group, LANES, 4))
        ones = jnp.ones((8, Q), F32).astype(LOW)
        states = [carry_ref[...].astype(F32)]
        for index in range(spans - 1):
            at = slice(index * Q, (index + 1) * Q)
            states.append(facx[index : index + 1] * states[-1] + loc_ref[at])
        for index in range(spans):
            at = slice(index * Q, (index + 1) * Q)
            dy = dy_ref[at]
            value = mix[at] * dtx[at]
            value_low = value.astype(LOW)
            lane = iota((Q, WIDE), 1) // HEAD
            dy_heads = [jnp.where(lane == head, dy, 0.0).astype(LOW) for head in range(4)]
            d_weight = mm_nt(jnp.concatenate(dy_heads, axis=0), value_low)
            parts = []
            sum_score = None
            row_sums = None
            for pair in range(2):
                lanes = slice(pair * LANES, (pair + 1) * LANES)
                moved, weights = [], []
                for head in (2 * pair, 2 * pair + 1):
                    across = cumt[group, head : head + 1, at]
                    spread_at = cums[at, head * LANES : (head + 1) * LANES] - across + mask[at]
                    decay = jnp.exp2(spread_at)
                    inner = decay * d_weight[head * Q : (head + 1) * Q]
                    sum_score = inner if sum_score is None else sum_score + inner
                    moved.append((inner * score[at]).astype(LOW))
                    weights.append((decay * score[at]).astype(LOW))
                both = jnp.concatenate(moved, axis=1)
                column_sums = mm(ones, both)
                for index_in in range(2):
                    head = 2 * pair + index_in
                    d_cum[group, head : head + 1, at] = -column_sums[
                        0:1, index_in * Q : (index_in + 1) * Q
                    ]
                part = mm(both, gatherer(4 * group + 2 * pair, LANES, 2))
                row_sums = part if row_sums is None else row_sums + part
                pushed_heads = [dy_heads[2 * pair][:, lanes], dy_heads[2 * pair + 1][:, lanes]]
                parts.append(
                    mm_tn(jnp.concatenate(weights, axis=0), jnp.concatenate(pushed_heads, axis=0))
                )
            d_score[at] += sum_score
            local_value[at] = jnp.concatenate(parts, axis=1)
            pushed = dy * growth[at]
            state_low = states[index].astype(LOW)
            carried = mm(bc[at, LANES:], state_low)
            d_bc[at, LANES:] += mm_nt(pushed.astype(LOW), state_low)
            heads[1, at] += head_sums(pushed * carried, collect) + row_sums

    @pl.when(step == 0)
    def _():
        for cut in range(GROUPS):
            chaining.relay(0, cut)
        chaining.later()

        def put(cut, value):
            adjoints[cut] = value

        chaining.arrive(put)
        chaining.finish()
        late[1].wait()
        late[2].wait()

    for turn in range(5):

        @pl.when(step == turn)
        def _():
            each(turn + 1 if turn < 4 else depth + 1, reducing.turn, turn)
            block_copy(turn + 3).start()

    @pl.when(step == 5)
    def _():
        reducing.close()
        if fused:
            second.turn(0)

    @pl.when((step > 0) & (step < GROUPS))
    def _():
        edge_wait(last_group)

    @pl.when(step < GROUPS)
    def _():
        spread = spreader(4 * group, HEAD, 4)
        collect = gatherer(4 * group, HEAD, 4)
        pre = pre_ref[...]
        sigma = sigmoid(pre)
        mix = pre * sigma
        dtx = mm(sp[0], spread)
        growth = mm(sp[2], spread)
        facx = mm(split3(fac[...]), spread)
        states = [carry_ref[...].astype(F32)]
        for index in range(spans - 1):
            at = slice(index * Q, (index + 1) * Q)
            states.append(facx[index : index + 1] * states[-1] + loc_ref[at])
        arrived = jnp.where(step > 0, last_group, GROUPS + 1)
        grad = joined(arrived)
        gate_grad = gpg[...]
        put_inner(mm(hidden_t[...], grad).astype(LOW))
        total[...] += mm_nt(gate_grad, w_gate[0, 0]) + mm_nt(grad, w_inner[0, 0])
        tails = mm(sp[3], spread)
        skipx = mm(split3(par_heads[...]), spread)[2:3]
        adjoint = adjoints[group].astype(F32)
        masks = [match[back] for back in range(CONV - 1)]
        pgs = [None] * spans
        for index in reversed(range(spans)):
            at = slice(index * Q, (index + 1) * Q)
            dy = dy_ref[at]
            value = mix[at] * dtx[at]
            adj_low = adjoint.astype(LOW)
            reached = mm(bc[at, :LANES], adj_low) * tails[at]
            d_bc[at, :LANES] += mm_nt((value * tails[at]).astype(LOW), adj_low)
            heads[0, at] += head_sums(value * reached, collect)
            fac_part = jnp.sum(adjoint * states[index], axis=0, keepdims=True)
            heads[3, index * 8 : index * 8 + 8] += head_sums(
                jnp.broadcast_to(fac_part, (8, WIDE)), collect
            )
            pushed_low = (dy * growth[at]).astype(LOW)
            adjoint = facx[index : index + 1] * adjoint + mm(bct[NSTATE:, at], pushed_low)
            d_value = local_value[at] + reached
            heads[2, at] += head_sums(mix[at] * d_value, collect)
            d_mix = dtx[at] * d_value + skipx * dy
            s = sigma[at]
            pgs[index] = d_mix * s * (1.0 + pre[at] * (1.0 - s))
        pg = jnp.concatenate(pgs, axis=0)
        sums, grad = conv_backward(pg, cin_ref[...].astype(F32), par[0], masks)
        taps8 = jnp.concatenate(sums + [jnp.zeros((3, WIDE), F32)], axis=0)
        if fused:
            taps_v[group] = taps8
        else:
            tap_out[...] = taps8
        grads[...] = grad[HALO:]
        edge_own[group] = grad[HALO - EDGE : HALO]

        @pl.when(has_before)
        def _():
            edge_copy(group).start()

    @pl.when(step == GROUPS)
    def _():
        for copy in late[3:]:
            copy.wait()
        if fused:
            second.turn(1)
        masks = [match[back] for back in range(CONV - 1)]
        edge_wait(GROUPS - 1)
        grad = joined(GROUPS - 1)
        put_inner(mm(hidden_t[...], grad).astype(LOW))
        total[...] += mm_nt(grad, w_inner[0, 0])
        t_at, u_at = iota((Q, Q), 0), iota((Q, Q), 1)
        onward = (t_at <= u_at).astype(F32)
        earlier = (t_at > u_at).astype(F32)
        rate = jnp.exp(par_heads[1:2])
        raws = []
        bias_sum = jnp.zeros((1, LANES), F32)
        decay_sum = jnp.zeros((1, LANES), F32)
        used = iota((Q, LANES), 1) < 24
        for index in range(spans):
            at = slice(index * Q, (index + 1) * Q)
            pieces = [d_cum[piece, 0:4, at] for piece in range(6)]
            pieces.append(jnp.zeros((LANES - 24, Q), F32))
            cum_col = jnp.transpose(jnp.concatenate(pieces, axis=0))
            fac_row = fac[index : index + 1] * heads[3, index * 8 : index * 8 + 1]
            d_decay = (
                mm_exact(onward, cum_col + heads[1, at]) + mm_exact(earlier, heads[0, at]) + fac_row
            )
            dt = dt_ref[at]
            raw = (heads[2, at] - d_decay * rate) * sigmoid(zst[at])
            raw = jnp.where(used, raw, 0.0)
            raws.append(raw.astype(LOW))
            bias_sum += jnp.sum(raw, axis=0, keepdims=True)
            decay_sum -= jnp.sum(
                jnp.where(used, d_decay * dt * rate, 0.0), axis=0, keepdims=True
            )
            score_low = d_score[at].astype(LOW)
            d_bc[at, :LANES] += mm_tn(score_low, bc[at, LANES:])
            d_bc[at, LANES:] += mm(score_low, bc[at, :LANES])
        if not fused:
            small_out[...] = jnp.concatenate(
                [bias_sum, decay_sum, jnp.zeros((6, LANES), F32)], axis=0
            )
        if fused:
            second.turn(2)
        pre = pre_state[...]
        s = sigmoid(pre)
        pg = d_bc[...] * s * (1.0 + pre * (1.0 - s))
        sums, grad = conv_backward(pg, cin_state[...].astype(F32), state_filter[...], masks)
        taps8 = jnp.concatenate(sums + [jnp.zeros((3, WIDE), F32)], axis=0)
        if fused:
            taps_v[GROUPS] = taps8
        else:
            tap_state_out[...] = taps8
        grads[...] = grad[HALO:]
        edge_own[GROUPS] = grad[HALO - EDGE : HALO]

        @pl.when(has_before)
        def _():
            edge_copy(GROUPS).start()

        steps = jnp.concatenate(raws, axis=0)
        turned = hidden_t[...]
        step_part = mm(turned, steps).astype(LOW)
        total[...] += mm_nt(steps, w_small[0, :, LANES:]) + mm_nt(steps, w_small[1, :, LANES:])
        edge_wait(GROUPS)
        state = joined(GROUPS)
        state_part = mm(turned, state).astype(LOW)
        for index in range(2):
            state_half = state_part[:, index * LANES : (index + 1) * LANES]
            value = jnp.concatenate([state_half, step_part], axis=1)
            if fused:
                small_v[index] = value.reshape(small_v.shape[1:])
            else:
                small_part[index] = value
        if fused:
            each(depth, third.start)
        value = tokens[...].astype(F32)
        scale = lax.rsqrt(jnp.mean(value * value, axis=1, keepdims=True) + EPSILON)
        hidden_grad = (
            total[...]
            + mm_nt(state[:, :LANES], w_small[0, :, :LANES])
            + mm_nt(state[:, LANES:], w_small[1, :, :LANES])
        )
        norm_sum = jnp.sum(hidden_grad * (value * scale), axis=0, keepdims=True)
        if not fused:
            norm_out[...] = jnp.broadcast_to(norm_sum, norm_out.shape)
        gain = jnp.transpose(w_small[0, :, LANES : 2 * LANES].astype(F32))[24:25]
        normed = hidden_grad * gain
        pull = jnp.sum(normed * value, axis=1, keepdims=True) / value.shape[1]
        token_low = (
            cot[...].astype(F32) + scale * normed - (scale * scale * scale) * value * pull
        ).astype(LOW)
        if fused:
            token_v[...] = token_low
            for index in range(GROUPS + 1):
                at = slice(index * WIDE, (index + 1) * WIDE)
                closing.send[0, : CONV + 1, at] = taps_v[index, : CONV + 1]
            high = GROUPS * WIDE
            closing.send[0, CONV + 1 :] = jnp.zeros((8 - CONV - 1, high + WIDE), F32)
            closing.send[0, 5:6, :high] = gate_row[0:1]
            closing.send[0, 5:6, high : high + LANES] = bias_sum
            closing.send[0, 5:6, high + LANES :] = skip_row[0:1]
            model = norm_sum.shape[1]
            closing.send[0, 6:7, :model] = norm_sum
            closing.send[0, 6:7, model : model + LANES] = decay_sum
            closing.run(third, NSTATE, state_out, vector_out, WIDE, second)
            second.finish()
        else:
            token_out[...] = token_low
        reducing.finish()
        each(blocks, lambda index: block_copy(index).wait())
        block_local.wait()

        @pl.when(has_before)
        def _():
            each(GROUPS + 1, lambda index: edge_copy(index).wait_send())


def scan_back(
    pre, dy, loc, carry, enter, cin, par, par_heads, state_filter, cin_state, pre_state, bc, bct,
    score, mask, sp, cumt, fac, match, zst, dt, exits, gate_part, block_own, tokens, cot, hidden_t,
    gpg, parts, small, gate_row, skip_row, rounds
):
    rows, wide = pre.shape
    ext = rows + HALO
    depth = lax.axis_size("context") // 2
    own_rows, half_wide = exits.shape[3:]
    shape = jax.ShapeDtypeStruct
    sem = lambda *lead: pltpu.SemaphoreType.DMA(lead)
    model = tokens.shape[2]
    count = 2 * depth
    fused = own_rows % 16 == 0
    now = lambda s: group_of(jnp.minimum(s, GROUPS - 1))
    lag = lambda s: group_of(jnp.maximum(s - 1, 0))
    column = lambda count: pl.BlockSpec((count, WIDE), lambda s: (0, now(s)[0]))
    whole = lambda *dims, dtype=F32: (shape(dims, dtype), const(dims))
    outs = [
        whole(own_rows, 2 * half_wide),
        (shape((2,) + block_own.shape, LOW), ANY_SPEC),
    ]
    if fused:
        outs += [
            whole(own_rows, 2 * WIDE),
            whole(own_rows, 2 * WIDE),
            whole(2, own_rows, NSTATE),
            whole(8, wide + WIDE),
            (shape((2, rows, model), LOW), ANY_SPEC),
        ]
        extra = (
            [
                pltpu.VMEM((3, 2, 2, count, own_rows, WIDE), LOW),
                pltpu.VMEM((2, 2, count, own_rows, WIDE), LOW),
                pltpu.VMEM((rows, model), LOW),
                pltpu.VMEM((GROUPS + 1, 8, WIDE), F32),
            ]
            + Reducing.scratch(depth, own_rows, 2 * WIDE) * 2
            + Closing.scratch(depth, own_rows, (8, wide + WIDE))
        )
    else:
        outs += [
            (shape((8, wide), F32), column(8)),
            whole(8, WIDE),
            whole(8, LANES),
            (
                shape((2, model, 3 * WIDE), LOW),
                pl.BlockSpec((1, model, WIDE), lambda s: (lag(s)[1], 0, lag(s)[2])),
            ),
            whole(2, model, WIDE, dtype=LOW),
            whole(rows, model, dtype=LOW),
            whole(8, model),
        ]
        extra = []
    return pl.pallas_call(
        functools.partial(scan_back_body, depth, rounds, fused),
        out_shape=[out[0] for out in outs],
        grid=(GROUPS + 1,),
        in_specs=[
            column(rows),
            column(rows),
            column(rows),
            column(NSTATE),
            fixed((NSTATE, wide)),
            column(ext),
            pl.BlockSpec((1, 8, WIDE), lambda s: (now(s)[1], 0, now(s)[2])),
            fixed((8, LANES)),
            fixed((CONV + 1, WIDE)),
            ANY_SPEC,
            ANY_SPEC,
            fixed((rows, WIDE)),
            fixed((WIDE, rows)),
            fixed((rows, Q)),
            fixed((rows, Q)),
            fixed((4, rows, LANES)),
            fixed((6, 8, rows)),
            fixed((8, LANES)),
            ANY_SPEC,
            ANY_SPEC,
            ANY_SPEC,
            ANY_SPEC,
            ANY_SPEC,
            ANY_SPEC,
            ANY_SPEC,
            ANY_SPEC,
            ANY_SPEC,
            column(rows),
            pl.BlockSpec((1, 1, model, WIDE), lambda s: (now(s)[2], now(s)[1], 0, 0)),
            pl.BlockSpec((1, 1, model, WIDE), lambda s: (lag(s)[2], lag(s)[1], 0, 1)),
            ANY_SPEC,
            fixed((8, wide)),
            fixed((8, LANES)),
        ],
        out_specs=[out[1] for out in outs],
        scratch_shapes=[
            pltpu.VMEM((rows, model), LOW),
            pltpu.VMEM((model, rows), LOW),
            pltpu.VMEM((CONV - 1, rows, LANES), F32),
            pltpu.VMEM((rows, model), LOW),
            pltpu.VMEM((rows, model), LOW),
            pltpu.VMEM((2, model, WIDE), LOW),
            pltpu.VMEM((rows, WIDE), F32),
            pltpu.VMEM((ext, WIDE), LOW),
            pltpu.VMEM((rows, LANES), F32),
            pltpu.VMEM((rows, LANES), F32),
            sem(10),
            pltpu.VMEM((rows, WIDE), F32),
            pltpu.VMEM((rows, Q), F32),
            pltpu.VMEM((6, 8, rows), F32),
            pltpu.VMEM((4, rows, LANES), F32),
            pltpu.VMEM((rows, WIDE), F32),
            pltpu.VMEM((GROUPS, NSTATE, WIDE), F32),
            pltpu.VMEM((GROUPS, 8, WIDE), F32),
            pltpu.VMEM((GROUPS, NSTATE, WIDE), LOW),
            pltpu.VMEM((GROUPS + 1, EDGE, WIDE), F32),
            pltpu.VMEM((GROUPS + 2, EDGE, WIDE), F32),
            pltpu.VMEM((rows, WIDE), F32),
            pltpu.VMEM((rows, model), F32),
            sem(GROUPS + 1),
            sem(GROUPS + 1),
            sem(BLOCK_CUTS),
            sem(BLOCK_CUTS),
            sem(1),
        ]
        + Chaining.scratch(rounds)
        + Reducing.scratch(depth, own_rows, 2 * half_wide)
        + extra,
        compiler_params=params(collective_id=2, has_side_effects=True),
        name="scan_back",
    )(
        pre, dy, loc, carry, enter, cin, par, par_heads, state_filter, cin_state, pre_state, bc,
        bct, score, mask, sp, cumt, fac, match, zst, dt, exits, gate_part, block_own, tokens, cot,
        hidden_t, gpg, parts, parts, small, gate_row, skip_row,
    )


def pack_body(
    entry, exits, state, steps, gain, inner_kernel, gate_gain, bias, decay, skip, docs,
    tail_tokens, packed_small, packed_parts, packed_exit, par, doc_col, doc_row, edge, docs_own
):
    half_of = side()
    rows = entry.shape[0]
    wide = entry.shape[2]

    def placed(filled, used):
        return jnp.where(half_of == 0, filled, pltpu.roll(filled, used, 1))

    def widened(value):
        return jnp.concatenate(
            [value, jnp.zeros((value.shape[0], LANES - value.shape[1]), F32)], axis=1
        )

    for part in range(3):
        at = slice(part * WIDE, (part + 1) * WIDE)
        packed_parts[part, :, :WIDE] = entry[:, 0, at].astype(LOW)
        packed_parts[part, :, WIDE:] = entry[:, 1, at].astype(LOW)
    half = jnp.where(half_of == 0, state[:, :NSTATE], state[:, NSTATE:])
    packed_small[:, :NSTATE] = half.astype(LOW)
    gain_row = jnp.concatenate([gain[...], jnp.zeros((1, LANES - rows), F32)], axis=1)
    gain_col = jnp.transpose(jnp.broadcast_to(gain_row, (LANES, LANES)))[:rows]
    lane = iota((rows, LANES), 1)
    heads_here = steps.shape[0]
    step_rows = jnp.concatenate([steps[...], jnp.zeros((heads_here, LANES - rows), F32)], axis=1)
    step_rows = jnp.concatenate([step_rows, jnp.zeros((LANES - heads_here, LANES), F32)], axis=0)
    step_cols = jnp.transpose(step_rows)[:rows]
    small = jnp.where(lane == 24, gain_col, placed(step_cols, heads_here))
    packed_small[:, NSTATE:] = small.astype(LOW)
    packed_exit[...] = exits[...].astype(LOW)
    par[0 : CONV + 1] = inner_kernel[...]
    for index in range(wide // LANES):
        at = slice(index * LANES, (index + 1) * LANES)
        par[CONV + 1 : CONV + 2, at] = gate_gain[index : index + 1]
    par[CONV + 2 : CONV + 4] = jnp.zeros((2, wide), F32)
    for index, ref in enumerate((bias, decay, skip)):
        par[CONV + 2 : CONV + 3, index * LANES : (index + 1) * LANES] = placed(
            widened(ref[...]), ref.shape[1]
        )
    own = jnp.where(half_of == 0, docs[0:1], docs[1:2]).astype(F32)
    doc_row[...] = jnp.broadcast_to(own, doc_row.shape)
    doc_col[...] = jnp.transpose(jnp.broadcast_to(own, (LANES, own.shape[1])))
    docs_own[...] = doc_col[own.shape[1] - HALO :]
    edge[...] = tail_tokens[0]


def pack(
    entry, exits, state, steps, gain, inner_kernel, gate_gain, bias, decay, skip, docs, tokens
):
    own_rows, _, wide = entry.shape
    rows, model = tokens.shape[1:]
    shape = jax.ShapeDtypeStruct
    arrays = (
        entry, exits, state, steps.T, gain[None], inner_kernel, gate_gain.reshape(-1, LANES), bias[None],
        decay[None], skip[None], docs,
    )
    outs = (
        shape((own_rows, WIDE), LOW),
        shape((3, own_rows, 2 * WIDE), LOW),
        shape((own_rows, wide), LOW),
        shape((8, wide), F32),
        shape((rows, LANES), F32),
        shape((8, rows), F32),
        shape((HALO, model), LOW),
        shape((HALO, LANES), F32),
    )
    return pl.pallas_call(
        pack_body,
        out_shape=outs,
        grid=(1,),
        in_specs=[fixed(array.shape) for array in arrays]
        + [pl.BlockSpec((1, HALO, model), lambda s: (side(), rows // HALO - 1, 0))],
        out_specs=[const(out.shape) for out in outs],
        compiler_params=params(),
        name="pack",
    )(*arrays, tokens)


def gather_body(
    depth, own_small, own_parts, own_exit, par_own, edge_own, docs_own, cot, small, parts, exits, par,
    heads, edge, docs, cot_t, docs_in, cot_in, side_send, side_land, local, *marks
):
    place = Place(depth)
    count = 2 * depth
    onward = {"context": lax.rem(place.position + 1, count)}
    behind = {"context": lax.rem(place.position + count - 1, count)}
    y = place.y
    place.greet([place.mate, place.x_peer, place.y_peer, onward, behind], (), True)
    own = [own_small, own_parts.at[0], own_parts.at[1], own_parts.at[2], own_exit]
    full = [small, parts.at[0], parts.at[1], parts.at[2], exits]
    pieces = [Gathering(place, own[i], full[i], *marks[3 * i : 3 * i + 3]) for i in range(5)]
    sides = [
        remote(edge_own, edge, side_send.at[0], side_land.at[0], onward),
        remote(docs_own, docs_in, side_send.at[1], side_land.at[1], onward),
        remote(par_own, par.at[y], side_send.at[2], side_land.at[2], place.y_peer),
    ]
    for copy in sides:
        copy.start()
    cot_copy = pltpu.make_async_copy(cot.at[y], cot_in, local.at[1])
    cot_copy.start()
    par_keep = pltpu.make_async_copy(par_own, par.at[y], local.at[0])
    par_keep.start()
    for piece in pieces:
        piece.own()
    cot_copy.wait()
    cot_t[...] = jnp.transpose(cot_in[...])
    for piece in pieces:
        piece.near()
        piece.across()
        piece.far()
    for copy in sides:
        copy.wait()
    docs[...] = jnp.where(place.position == 0, -1.0, docs_in[...])
    par_keep.wait()
    both = par[0, CONV + 2 : CONV + 3] + par[1, CONV + 2 : CONV + 3]
    heads[...] = jnp.zeros_like(heads)
    for index in range(3):
        heads[index : index + 1] = both[:, index * LANES : (index + 1) * LANES]
    for piece in pieces:
        piece.mates()
        piece.finish()


def gather(own_small, own_parts, own_exit, par_own, edge_own, docs_own, cot):
    count = lax.axis_size("context")
    depth = count // 2
    rows, model = cot.shape[1:]
    shape = jax.ShapeDtypeStruct
    full = lambda own: (2, 2, count) + own.shape[-2:]
    return pl.pallas_call(
        functools.partial(gather_body, depth),
        out_shape=(
            shape(full(own_small), LOW),
            shape((3,) + full(own_parts), LOW),
            shape(full(own_exit), LOW),
            shape((2,) + par_own.shape, F32),
            shape((8, LANES), F32),
            shape(edge_own.shape, LOW),
            shape(docs_own.shape, F32),
            shape((model, rows), LOW),
        ),
        in_specs=[VMEM_SPEC] * 6 + [ANY_SPEC],
        out_specs=[ANY_SPEC] * 3 + [VMEM_SPEC] * 5,
        scratch_shapes=[
            pltpu.VMEM(docs_own.shape, F32),
            pltpu.VMEM((rows, model), LOW),
            pltpu.SemaphoreType.DMA((3,)),
            pltpu.SemaphoreType.DMA((3,)),
            pltpu.SemaphoreType.DMA((2,)),
        ]
        + Gathering.scratch(depth) * 5,
        compiler_params=params(collective_id=0, has_side_effects=True),
        name="gather",
    )(own_small, own_parts, own_exit, par_own, edge_own, docs_own, cot)


def reduce_body(
    depth, inner, small, token, taps, taps_state, gate_row, head_rows, skip_row, norm_row, mine,
    state_out, vector_out, token_out, *scratch
):
    place = Place(depth)
    wide = inner.shape[-1]
    parts = [(inner, slice(0, wide)), (small, slice(wide, wide + WIDE))]
    reducing = Reducing(place, 0, parts, mine, scratch[:8], scratch[8:17])
    closing = Closing(place, token, token_out, scratch[17:])
    vec = closing.send
    vec[0] = jnp.zeros(vec.shape[1:], F32)
    vec[0, : CONV + 1, : 2 * wide] = taps[: CONV + 1]
    vec[0, : CONV + 1, 2 * wide :] = taps_state[: CONV + 1]
    vec[0, 5:6, : 2 * wide] = gate_row[0:1]
    vec[0, 5:6, 2 * wide : 2 * wide + LANES] = head_rows[0:1]
    vec[0, 5:6, 2 * wide + LANES :] = skip_row[0:1]
    model = norm_row.shape[1]
    vec[0, 6:7, :model] = norm_row[0:1]
    vec[0, 6:7, model : model + LANES] = head_rows[1:2]
    place.greet([place.mate, place.x_peer, place.y_peer], (), True)
    each(depth, reducing.start)
    closing.run(reducing, NSTATE, state_out, vector_out, wide)


def reduce_all(inner, small, token, taps, taps_state, gate_row, head_rows, skip_row, norm_row):
    depth = lax.axis_size("context") // 2
    own_rows, wide = inner.shape[3:]
    tall = wide + WIDE
    shape = jax.ShapeDtypeStruct
    vector = (8, 2 * wide + WIDE)
    return pl.pallas_call(
        functools.partial(reduce_body, depth),
        out_shape=(
            shape((own_rows, tall), F32),
            shape((2, own_rows, NSTATE), F32),
            shape(vector, F32),
            shape((2,) + token.shape, LOW),
        ),
        in_specs=[ANY_SPEC] * 2 + [VMEM_SPEC] * 7,
        out_specs=[VMEM_SPEC] * 3 + [ANY_SPEC],
        scratch_shapes=Reducing.scratch(depth, own_rows, tall)
        + Closing.scratch(depth, own_rows, vector),
        compiler_params=params(collective_id=4, has_side_effects=True),
        name="reduce_all",
    )(inner, small, token, taps, taps_state, gate_row, head_rows, skip_row, norm_row)


def finish_body(
    mine, mine_last, exits, state, vector, token, block, block_out, token_out,
    norm_out, entry_out, state_out, step_out, kernel_out, filter_out, bias_out, decay_out, skip_out,
    gate_out, exit_out
):
    half_of = side()
    spot = lax.axis_index("dp") * lax.axis_size("context") + lax.axis_index("context")
    token_out[...] = token[...].astype(F32)
    first = half_of == 0
    block_out[...] = block[...]

    @pl.when(pl.program_id(0) == 0)
    def _():
        own_rows, _, wide = entry_out.shape
        model = token.shape[2]
        entry_out[:, 0] = exits[:, wide:]
        entry_out[:, 1, : 2 * WIDE] = mine[...]
        entry_out[:, 1, 2 * WIDE :] = mine_last[:, :WIDE]
        exit_out[...] = exits[:, :wide]
        state_out[:, :NSTATE] = state[0]
        state_out[:, NSTATE:] = state[1]

        def twelve(value):
            return jnp.where(first, value, pltpu.roll(value, LANES - 12, 1))[:, :12]

        steps = jnp.where(first, mine_last[:, WIDE + NSTATE :], pltpu.roll(mine_last[:, WIDE + NSTATE :], LANES - 12, 1))
        steps = jnp.concatenate([steps, jnp.zeros((LANES - own_rows, LANES), F32)], axis=0)
        step_out[...] = jnp.transpose(steps)[:12, :own_rows]
        left, right = vector[:, :wide], vector[:, wide : 2 * wide]
        halves = jnp.where(first, left, right)
        kernel_out[...] = halves[: CONV + 1]
        for index in range(wide // LANES):
            gate_out[index : index + 1] = halves[5:6, index * LANES : (index + 1) * LANES]
        filter_out[...] = vector[: CONV + 1, 2 * wide :]
        bias_out[...] = twelve(vector[5:6, 2 * wide : 2 * wide + LANES])
        skip_out[...] = twelve(vector[5:6, 2 * wide + LANES :])
        decay_out[...] = twelve(vector[6:7, model : model + LANES])
        turned = pltpu.roll(vector[:, :model], lax.rem(model - spot * own_rows, model), 1)
        norm_out[...] = turned[6:7, :own_rows]


def finish(mine, mine_last, exits, state, vector, token, block):
    own_rows, wide = exits.shape[0], exits.shape[1] // 2
    _, rows, model = token.shape
    share = rows // 2
    shape = jax.ShapeDtypeStruct
    outs = (
        (shape((2, rows, model), LOW), pl.BlockSpec((2, share, model), lambda s: (0, s, 0))),
        (shape((2, rows, model), F32), pl.BlockSpec((2, share, model), lambda s: (0, s, 0))),
        (shape((1, own_rows), F32), None),
        (shape((own_rows, 2, wide), F32), None),
        (shape((own_rows, WIDE), F32), None),
        (shape((12, own_rows), F32), None),
        (shape((CONV + 1, wide), F32), None),
        (shape((CONV + 1, WIDE), F32), None),
        (shape((1, 12), F32), None),
        (shape((1, 12), F32), None),
        (shape((1, 12), F32), None),
        (shape((wide // LANES, LANES), F32), None),
        (shape((own_rows, wide), F32), None),
    )
    return pl.pallas_call(
        finish_body,
        out_shape=[out[0] for out in outs],
        grid=(2,),
        in_specs=[
            fixed(mine.shape),
            fixed(mine_last.shape),
            fixed(exits.shape),
            fixed(state.shape),
            fixed(vector.shape),
            pl.BlockSpec((2, share, model), lambda s: (0, s, 0)),
            pl.BlockSpec((2, share, model), lambda s: (0, s, 0)),
        ],
        out_specs=[out[1] if out[1] is not None else const(out[0].shape) for out in outs],
        compiler_params=params(),
        name="finish",
    )(mine, mine_last, exits, state, vector, token, block)


def body(
    tokens, documents, norm_gain, entry_weight, state_weight, step_weight, inner_kernel,
    state_filter, step_bias, decay_log, skip_gain, gate_gain, exit_weight, cotangent,
):
    seqs, rows, model = tokens.shape
    count = lax.axis_size("context")
    own_rows = norm_gain.shape[0]
    longest = rows * count // 4
    rounds = min(count // 2 - 1, -(-(longest - 1) // (2 * rows)))

    own_small, own_parts, own_exit, own_par, doc_col, doc_row, own_edge, own_docs = pack(
        entry_weight, exit_weight, state_weight, step_weight, norm_gain, inner_kernel,
        gate_gain, step_bias, decay_log, skip_gain, documents, tokens,
    )
    packs = (own_small, own_parts, own_exit, own_par, own_edge, own_docs)
    (
        hidden_t, cin, gate, pre, loc, carry, cin_state, pre_state, bc, bct, score, mask, zst, dt, sp,
        cumt, fac, match, local,
    ), (small, parts, exit_weights, par, par_heads, cot_t) = entry(
        tokens, doc_col, doc_row, state_filter, packs, cotangent, rounds
    )
    block_own, exit_part, gate_part, dy, gpg, enter, gate_row, skip_row = middle(
        tokens, cotangent, cot_t, hidden_t, pre, gate, loc, local, carry, exit_weights, par, bc, bct,
        sp, fac,
    )
    cut = lambda v: v.reshape(2, 2, count, own_rows, v.shape[-1])
    exit_mine, block_both, *others = scan_back(
        pre, dy, loc, carry, enter, cin, par, par_heads, state_filter, cin_state, pre_state, bc, bct,
        score, mask, sp, cumt, fac, match, zst, dt, cut(exit_part), cut(gate_part), block_own,
        tokens, cotangent, hidden_t, gpg, parts, small, gate_row, skip_row, rounds,
    )
    if len(others) == 5:
        mine, mine_last, state_both, vector, token_both = others
    else:
        taps, taps_state, head_rows, inner_part, small_part, token_own, norm_row = others
        mine, state_both, vector, token_both = reduce_all(
            cut(inner_part), cut(small_part), token_own, taps, taps_state, gate_row, head_rows,
            skip_row, norm_row,
        )
        mine, mine_last = mine[:, : 2 * WIDE], mine[:, 2 * WIDE :]
    outs = list(finish(mine, mine_last, exit_mine, state_both, vector, token_both, block_both))
    for index in (2, 8, 9, 10):
        outs[index] = outs[index][0]
    outs[5] = outs[5].T
    outs[11] = outs[11].reshape(-1)
    return tuple(outs)


def solution(mesh):
    in_specs = (
        P("dp", "context", None),
        P("dp", "context"),
        P(("dp", "context")),
        P(("dp", "context"), None, "tensor"),
        P(("dp", "context"), None),
        P(("dp", "context"), "tensor"),
        P(None, "tensor"),
        P(),
        P("tensor"),
        P("tensor"),
        P("tensor"),
        P("tensor"),
        P(("dp", "context"), "tensor"),
        P("dp", "context", None),
    )
    out_specs = (
        P("dp", "context", None),
        P("dp", "context", None),
        P(("dp", "context")),
        P(("dp", "context"), None, "tensor"),
        P(("dp", "context"), None),
        P(("dp", "context"), "tensor"),
        P(None, "tensor"),
        P(),
        P("tensor"),
        P("tensor"),
        P("tensor"),
        P("tensor"),
        P(("dp", "context"), "tensor"),
    )
    return jax.shard_map(body, mesh=mesh, in_specs=in_specs, out_specs=out_specs, check_vma=False)
```

```python
import functools
import jax
import jax.numpy as jnp
from jax import lax
from jax.experimental import pallas as pl
from jax.experimental.pallas import tpu as pltpu
from jax.sharding import PartitionSpec as P

HEAD = 64
NSTATE = 128
CONV = 4
EPSILON = 1e-05
Q = 128
HALO = 16
EDGE = 8
GROUPS = 6
BLOCK_CUTS = 8
ORDER = (0, 3, 1, 4, 2, 5)
LANES = 128
WIDE = 256
LOG2E = 1.4426950408889634
FAR = -1e30
LOW = jnp.bfloat16
F32 = jnp.float32
VMEM_LIMIT = 60 * 1024 * 1024


def mm(a, b):
    return lax.dot_general(a, b, (((1,), (0,)), ((), ())), preferred_element_type=F32)


def mm_nt(a, b):
    return lax.dot_general(a, b, (((1,), (1,)), ((), ())), preferred_element_type=F32)


def mm_tn(a, b):
    return lax.dot_general(a, b, (((0,), (0,)), ((), ())), preferred_element_type=F32)


def mm_exact(a, b):
    return lax.dot_general(
        a, b, (((1,), (0,)), ((), ())), precision=lax.Precision.HIGHEST, preferred_element_type=F32
    )


def split3(v):
    high = v.astype(LOW).astype(F32)
    rest = v - high
    mid = rest.astype(LOW).astype(F32)
    low = rest - mid
    return (high + pltpu.roll(mid, 32, 1) + pltpu.roll(low, 64, 1)).astype(LOW)


def iota(shape, dim):
    return lax.broadcasted_iota(jnp.int32, shape, dim)


def spreader(first_head, width, count):
    k = iota((LANES, width * count), 0)
    lane = iota((LANES, width * count), 1)
    hit = ((k & 31) == first_head + lane // width) & (k < 96)
    return hit.astype(F32).astype(LOW)


def gatherer(first_head, width, count):
    lane = iota((width * count, LANES), 0)
    k = iota((width * count, LANES), 1)
    return (k == first_head + lane // width).astype(F32).astype(LOW)


def head_sums(v, collect):
    high = v.astype(LOW)
    rest = (v - high.astype(F32)).astype(LOW)
    return mm(high, collect) + mm(rest, collect)


def sigmoid(v):
    return 1.0 / (1.0 + jnp.exp(-v))


def twice(v):
    return jnp.concatenate([v, v], axis=1)


def conv_forward(cin, taps, masks):
    rows = cin.shape[0] - HALO
    out = taps[CONV : CONV + 1] + taps[CONV - 1 : CONV] * cin[HALO:]
    for back in range(1, CONV):
        part = cin[HALO - back : HALO - back + rows]
        out = out + taps[CONV - 1 - back : CONV - back] * (part * twice(masks[back - 1]))
    return out


def conv_backward(pg, cin, taps, masks):
    rows, width = pg.shape
    sums = [None] * (CONV + 1)
    sums[CONV] = jnp.sum(pg, axis=0, keepdims=True)
    sums[CONV - 1] = jnp.sum(pg * cin[HALO:], axis=0, keepdims=True)
    pad = jnp.zeros((HALO, width), F32)
    grad = jnp.concatenate([pad, pg * taps[CONV - 1 : CONV]], axis=0)
    for back in range(1, CONV):
        masked = pg * twice(masks[back - 1])
        part = cin[HALO - back : HALO - back + rows]
        sums[CONV - 1 - back] = jnp.sum(masked * part, axis=0, keepdims=True)
        padded = jnp.concatenate([pad, masked * taps[CONV - 1 - back : CONV - back], pad], axis=0)
        grad = grad + padded[back : back + rows + HALO]
    return sums, grad


def const(shape):
    zeros = (0,) * len(shape)
    return pl.BlockSpec(shape, lambda *_: zeros)


def fixed(shape):
    zeros = (0,) * len(shape)
    return pl.BlockSpec(shape, lambda *_: zeros, pipeline_mode=pl.Buffered(1))


def params(**extra):
    return pltpu.CompilerParams(vmem_limit_bytes=VMEM_LIMIT, **extra)


VMEM_SPEC = pl.BlockSpec(memory_space=pltpu.VMEM)
ANY_SPEC = pl.BlockSpec(memory_space=pl.ANY)


def side():
    return lax.axis_index("tensor")


def remote(src, dst, send_sem, recv_sem, target):
    return pltpu.make_async_remote_copy(
        src_ref=src,
        dst_ref=dst,
        send_sem=send_sem,
        recv_sem=recv_sem,
        device_id=target,
        device_id_type=pl.DeviceIdType.MESH,
    )


def each(count, run, first=0):
    def one(step, carry):
        run(step)
        return carry

    lax.fori_loop(first, count, one, 0)


class Place:
    def __init__(self, depth):
        position = lax.axis_index("context")
        self.depth = depth
        self.position = position
        self.x, self.y = lax.axis_index("dp"), lax.axis_index("tensor")
        self.z, self.c = position // 2, position % 2
        self.mate = self.at(self.x, self.y, self.z, 1 - self.c)
        self.x_peer = self.at(1 - self.x, self.y, self.z, self.c)
        self.y_peer = self.at(self.x, 1 - self.y, self.z, self.c)

    def at(self, x, y, z, c):
        return {"dp": x, "context": z * 2 + c, "tensor": y}

    def away(self, z):
        return self.at(self.x, self.y, z, self.c)

    def axes(self, turned):
        x, y, z, c = self.x, self.y, self.z, self.c
        x1, y1 = x + (1 - turned) * (1 - 2 * x), y + turned * (1 - 2 * y)
        x2, y2 = x + turned * (1 - 2 * x), y + (1 - turned) * (1 - 2 * y)
        return (x1, y1), (x2, y2)

    def around(self, run, first=0, last=None):
        z, depth = self.z, self.depth
        if first == 0:
            run(z)

        def step(away):
            @pl.when(z - away >= 0)
            def _():
                run(z - away)

            @pl.when(z + away < depth)
            def _():
                run(z + away)

        each(depth if last is None else last, step, max(first, 1))

    def greet(self, always, sometimes=(), column=False):
        barrier = pltpu.get_barrier_semaphore()
        kind = pl.DeviceIdType.MESH
        total = len(always)
        for target in always:
            pl.semaphore_signal(barrier, inc=1, device_id=target, device_id_type=kind)
        for holds, target in sometimes:

            @pl.when(holds)
            def _():
                pl.semaphore_signal(barrier, inc=1, device_id=target, device_id_type=kind)

            total = total + holds.astype(jnp.int32)
        if column:
            for_all = lambda step: pl.semaphore_signal(
                barrier,
                inc=1,
                device_id=self.away(lax.rem(self.z + step, self.depth)),
                device_id_type=kind,
            )
            each(self.depth, for_all, 1)
            total = total + (self.depth - 1)
        pl.semaphore_wait(barrier, total)


class Gathering:
    def __init__(self, place, own, full, sends, lands, local):
        self.place, self.own_ref, self.full = place, own, full
        self.sends, self.lands, self.local = sends, lands, local
        self.starts = [first * place.depth for first in (0, 4, 5, 7)]
        (self.x1, self.y1), (self.x2, self.y2) = place.axes(place.c)
        self.first = place.at(self.x1, self.y1, place.z, place.c)
        self.second = place.at(self.x2, self.y2, place.z, place.c)

    @staticmethod
    def scratch(depth):
        sem = pltpu.SemaphoreType.DMA
        return [sem((8 * depth,)), sem((8 * depth,)), sem((1,))]

    def copy(self, kind, index, x, y, z, c, target, own=False):
        chunk = self.full.at[y, x, z * 2 + c]
        mark = ((y * 2 + x) * self.place.depth + z) * 2 + c
        return remote(
            self.own_ref if own else chunk, chunk, self.sends.at[self.starts[kind] + index],
            self.lands.at[mark], target,
        )

    def arrive(self, x, y, z, c):
        self.copy(0, 0, x, y, z, c, self.place.mate).wait_recv()

    def kept(self):
        p = self.place
        return pltpu.make_async_copy(
            self.own_ref, self.full.at[p.y, p.x, p.z * 2 + p.c], self.local.at[0]
        )

    def own(self):
        p = self.place
        mine = (p.x, p.y, p.z, p.c)

        def far_z(z):
            self.copy(3, z, *mine, p.away(z), True).start()

        p.around(far_z, 1)
        self.copy(1, p.z, *mine, self.first, True).start()
        self.copy(2, p.z, *mine, self.second, True).start()
        self.copy(0, p.z, *mine, p.mate, True).start()
        self.kept().start()

    def near(self, first=1, last=None):
        p = self.place

        def run(z):
            chunk = (p.x, p.y, z, p.c)
            self.arrive(*chunk)

            self.copy(1, z, *chunk, self.first).start()
            self.copy(2, z, *chunk, self.second).start()
            self.copy(0, z, *chunk, p.mate).start()

        p.around(run, first, last)

    def across(self):
        p = self.place

        def run(z):
            chunk = (self.x1, self.y1, z, p.c)
            self.arrive(*chunk)
            self.copy(2, p.depth + z, *chunk, self.second).start()
            self.copy(0, p.depth + z, *chunk, p.mate).start()

        p.around(run)

    def far(self):
        p = self.place

        def near_row(z):
            self.arrive(self.x2, self.y2, z, p.c)
            self.copy(0, 2 * p.depth + z, self.x2, self.y2, z, p.c, p.mate).start()

        def far_row(z):
            self.arrive(1 - p.x, 1 - p.y, z, p.c)
            self.copy(0, 3 * p.depth + z, 1 - p.x, 1 - p.y, z, p.c, p.mate).start()

        p.around(near_row)
        p.around(far_row)

    def mates(self):
        p = self.place

        def from_mate(z):
            for y in range(2):
                for x in range(2):
                    self.arrive(x, y, z, 1 - p.c)

        each(p.depth, from_mate)
        self.kept().wait()

    def finish(self):
        p = self.place

        def sent(kind, index, target):
            self.copy(kind, index, p.x, p.y, p.z, p.c, target).wait_send()

        each(4 * p.depth, lambda step: sent(0, step, p.mate))
        each(p.depth, lambda step: sent(1, step, p.mate))
        each(2 * p.depth, lambda step: sent(2, step, p.mate))

        p.around(lambda z: sent(3, z, p.mate), 1)


class Reducing:
    def __init__(self, place, turned, parts, total, bufs, sems):
        self.place, self.parts, self.total = place, parts, total
        self.own, self.core, self.send1, self.land1 = bufs[:4]
        self.send2, self.land2, self.send3, self.land3 = bufs[4:]
        self.own_sem, self.core_send, self.core_land = sems[:3]
        self.s1, self.l1, self.s2, self.l2, self.s3, self.l3 = sems[3:]
        self.turned = turned
        (x1, y1), (x2, y2) = place.axes(turned)
        self.first = place.at(x1, y1, place.z, place.c)
        self.second = place.at(x2, y2, place.z, place.c)
        self.mine = place.y + turned * (place.x - place.y)

    @staticmethod
    def scratch(depth, rows, tall):
        buffer = lambda *lead: pltpu.VMEM(lead + (rows, tall), LOW)
        sem = lambda *lead: pltpu.SemaphoreType.DMA(lead)
        bufs = [
            buffer(2, 2, depth), buffer(2, 2, depth), buffer(depth, 2), buffer(depth, 2),
            buffer(depth), buffer(depth), buffer(depth), buffer(depth),
        ]
        return bufs + [sem(2, 2, depth)] * 3 + [sem(depth)] * 6

    def spot(self, step):
        return lax.rem(self.place.z + 1 + step, self.place.depth)

    def whole(self, y, x, z):
        return remote(
            self.core.at[y, x, z], self.core.at[y, x, z], self.core_send.at[y, x, z],
            self.core_land.at[y, x, z], self.place.mate,
        )

    def own_whole(self, y, x, z):
        return pltpu.make_async_copy(
            self.own.at[y, x, z], self.own.at[y, x, z], self.own_sem.at[y, x, z]
        )

    def start(self, step):
        p = self.place
        z = self.spot(step)
        for y in range(2):
            for x in range(2):
                for ref, cols in self.parts:
                    remote(
                        ref.at[y, x, z * 2 + 1 - p.c], self.core.at[y, x, z, :, cols],
                        self.core_send.at[y, x, z], self.core_land.at[y, x, z], p.mate,
                    ).start()
                    pltpu.make_async_copy(
                        ref.at[y, x, z * 2 + p.c], self.own.at[y, x, z, :, cols],
                        self.own_sem.at[y, x, z],
                    ).start()

    def base(self, y, x, z):
        return self.own[y, x, z].astype(F32) + self.core[y, x, z].astype(F32)

    def copy1(self, z):
        return remote(
            self.send1.at[z], self.land1.at[z], self.s1.at[z], self.l1.at[z], self.first
        )

    def copy2(self, z):
        return remote(
            self.send2.at[z], self.land2.at[z], self.s2.at[z], self.l2.at[z], self.second
        )

    def copy3(self, z, lands_at):
        return remote(
            self.send3.at[z], self.land3.at[lands_at], self.s3.at[z], self.l3.at[lands_at],
            self.place.away(z),
        )

    def stage1(self, step):
        p, turned = self.place, self.turned
        z = self.spot(step)
        for y in range(2):
            for x in range(2):
                self.whole(y, x, z).wait_recv()
                self.own_whole(y, x, z).wait()
        for index in range(2):
            x = (1 - turned) * (1 - p.x) + turned * index
            y = turned * (1 - p.y) + (1 - turned) * index
            self.send1[z, index] = self.base(y, x, z).astype(LOW)
        self.copy1(z).start()

    def stage2(self, step):
        p, turned = self.place, self.turned
        z = self.spot(step)
        self.copy1(z).wait_recv()
        other = 1 - self.mine
        x = (1 - turned) * p.x + turned * other
        y = turned * p.y + (1 - turned) * other
        self.send2[z] = (self.base(y, x, z) + self.land1[z, other].astype(F32)).astype(LOW)
        self.copy2(z).start()

    def final(self, z):
        p = self.place
        self.copy2(z).wait_recv()
        return (
            self.base(p.y, p.x, z)
            + self.land1[z, self.mine].astype(F32)
            + self.land2[z].astype(F32)
        )

    def stage3(self, step):
        z = self.spot(step)
        self.send3[z] = self.final(z).astype(LOW)
        self.copy3(z, self.place.z).start()

    def turn(self, step):
        depth = self.place.depth

        @pl.when(step < depth)
        def _():
            self.stage1(step)

        @pl.when((step >= 1) & (step <= depth))
        def _():
            self.stage2(step - 1)

        @pl.when((step >= 2) & (step <= depth))
        def _():
            self.stage3(step - 2)

    def close(self):
        p = self.place
        self.total[...] = self.final(p.z)

        def add(step):
            z = lax.rem(p.z + step, p.depth)
            self.copy3(z, z).wait_recv()
            self.total[...] += self.land3[z].astype(F32)

        each(p.depth, add, 1)

    def finish(self):
        p = self.place

        def sent(z):
            for y in range(2):
                for x in range(2):
                    self.whole(y, x, z).wait_send()
            self.copy1(z).wait_send()
            self.copy2(z).wait_send()

        each(p.depth, sent)
        each(p.depth, lambda step: self.copy3(lax.rem(p.z + step, p.depth), p.z).wait_send(), 1)


class Chaining:
    def __init__(self, place, rounds, backward, fold, gain, bufs, sems):
        self.place, self.rounds = place, rounds
        self.fold, self.gain = fold, gain
        self.from_mate, self.from_chip, self.to_mate, self.to_chip = bufs
        self.mate_send, self.mate_land, self.chip_send, self.chip_land = sems
        first = 1 if backward else 0
        by = -1 if backward else 1
        self.order = place.depth - 1 - place.z if backward else place.z
        self.leads = place.c == first
        self.after = place.at(place.x, place.y, place.z + by, first)
        self.before = place.at(place.x, place.y, place.z - by, 1 - first)
        self.linked_before = self.leads & (self.order > 0)
        self.linked_after = jnp.logical_not(self.leads) & (self.order < place.depth - 1)

    @staticmethod
    def scratch(rounds):
        slots = lambda turns: pltpu.VMEM((turns, GROUPS, NSTATE, WIDE), LOW)
        marks = lambda turns: pltpu.SemaphoreType.DMA((turns, GROUPS))
        return [
            slots(rounds + 1), slots(rounds), slots(rounds + 1), slots(rounds),
            marks(rounds + 1), marks(rounds + 1), marks(rounds), marks(rounds),
        ]

    def sometimes(self):
        return [(self.linked_before, self.before), (self.linked_after, self.after)]

    def mate_copy(self, turn, cut):
        return remote(
            self.to_mate.at[turn, cut], self.from_mate.at[turn, cut], self.mate_send.at[turn, cut],
            self.mate_land.at[turn, cut], self.place.mate,
        )

    def chip_copy(self, turn, cut):
        return remote(
            self.to_chip.at[turn, cut], self.from_chip.at[turn, cut], self.chip_send.at[turn, cut],
            self.chip_land.at[turn, cut], self.after,
        )

    def joined(self, cut, arrived):
        return (self.fold[cut] + self.gain[cut, 0:1] * arrived.astype(F32)).astype(LOW)

    def open(self, cut):
        @pl.when(self.leads)
        def _():
            self.to_mate[0, cut] = self.fold[cut].astype(LOW)
            self.mate_copy(0, cut).start()

    def pass_on(self, turn, cut):
        @pl.when(jnp.logical_not(self.leads))
        def _():
            self.mate_copy(turn, cut).wait_recv()

        @pl.when(self.linked_after)
        def _():
            self.to_chip[turn, cut] = self.joined(cut, self.from_mate[turn, cut])
            self.chip_copy(turn, cut).start()

    def relay(self, turn, cut):
        @pl.when(self.linked_before)
        def _():
            self.chip_copy(turn, cut).wait_recv()
            self.to_mate[turn + 1, cut] = self.joined(cut, self.from_chip[turn, cut])
            self.mate_copy(turn + 1, cut).start()

        @pl.when(self.leads & (self.order == 0))
        def _():
            self.to_mate[turn + 1, cut] = self.fold[cut].astype(LOW)
            self.mate_copy(turn + 1, cut).start()

    def later(self):
        for turn in range(1, self.rounds):
            for cut in range(GROUPS):
                self.pass_on(turn, cut)
            for cut in range(GROUPS):
                self.relay(turn, cut)

    def arrive(self, put):
        last = self.rounds - 1

        @pl.when(self.linked_before)
        def _():
            for cut in range(GROUPS):
                put(cut, self.from_chip[last, cut])

        @pl.when(self.leads & (self.order == 0))
        def _():
            for cut in range(GROUPS):
                put(cut, jnp.zeros((NSTATE, WIDE), LOW))

        @pl.when(jnp.logical_not(self.leads))
        def _():
            for cut in range(GROUPS):
                self.mate_copy(self.rounds, cut).wait_recv()
                put(cut, self.from_mate[self.rounds, cut])

    def finish(self):
        @pl.when(self.leads)
        def _():
            for turn in range(self.rounds + 1):
                for cut in range(GROUPS):
                    self.mate_copy(turn, cut).wait_send()

        @pl.when(self.linked_after)
        def _():
            for turn in range(self.rounds):
                for cut in range(GROUPS):
                    self.chip_copy(turn, cut).wait_send()


class Closing:
    def __init__(self, place, token, token_out, refs):
        self.place, self.token, self.token_out = place, token, token_out
        self.state_own, self.state_in, self.send, self.land = refs[:4]
        self.vs, self.vl, self.ts, self.tl, self.ss, self.sl, self.keep_sem = refs[4:]
        self.targets = [place.mate, place.y_peer, place.x_peer]

    @staticmethod
    def scratch(depth, own_rows, vector):
        sem = lambda *lead: pltpu.SemaphoreType.DMA(lead)
        return [
            pltpu.VMEM((own_rows, NSTATE), F32),
            pltpu.VMEM((2, own_rows, NSTATE), F32),
            pltpu.VMEM((4,) + vector, F32),
            pltpu.VMEM((3 + depth,) + vector, F32),
            sem(3 + depth), sem(3 + depth), sem(depth), sem(depth), sem(1), sem(1), sem(1),
        ]

    def vec_copy(self, turn):
        return remote(
            self.send.at[turn], self.land.at[turn], self.vs.at[turn], self.vl.at[turn],
            self.targets[turn],
        )

    def vec_far(self, away, lands_at):
        return remote(
            self.send.at[3], self.land.at[3 + lands_at], self.vs.at[3 + away],
            self.vl.at[3 + lands_at], self.place.away(away),
        )

    def token_copy(self, step):
        p = self.place
        share = self.token.shape[0] // p.depth
        at = pl.ds(pl.multiple_of(step * share, share), share)
        return remote(
            self.token.at[at], self.token_out.at[p.y, at], self.ts.at[step], self.tl.at[step],
            p.y_peer,
        )

    def run(self, reducing, width, state_out, vector_out, first, pending=None):
        p = self.place
        depth, z = p.depth, p.z
        keep = pltpu.make_async_copy(self.token, self.token_out.at[p.y], self.keep_sem.at[0])
        keep.start()
        self.vec_copy(0).start()

        def step_all(step):
            if pending is not None:

                @pl.when(step + 3 <= depth)
                def _():
                    pending.turn(step + 3)

            reducing.turn(step)

            @pl.when(step < depth)
            def _():
                self.token_copy(step).start()

            for turn in range(3):

                @pl.when(step == turn)
                def _():
                    self.vec_copy(turn).wait_recv()
                    self.send[turn + 1] = self.send[turn] + self.land[turn]
                    if turn < 2:
                        self.vec_copy(turn + 1).start()
                    else:
                        each(depth, lambda s: self.vec_far(lax.rem(z + s, depth), z).start(), 1)
                        self.land[3 + z] = self.send[3]

        each(depth + 1, step_all)
        if pending is not None:
            pending.close()
        reducing.close()
        self.state_own[...] = reducing.total[:, first : first + width]
        state_copy = remote(
            self.state_own, self.state_in.at[p.y], self.ss.at[0], self.sl.at[0], p.y_peer
        )
        state_copy.start()
        self.state_in[p.y] = self.state_own[...]

        def vec_arrive(step):
            away = lax.rem(z + step, depth)
            self.vec_far(away, away).wait_recv()

        each(depth, vec_arrive, 1)
        vector_out[...] = self.land[3]

        def vec_add(step):
            vector_out[...] += self.land[3 + step]

        each(depth, vec_add, 1)
        for turn in range(3):
            self.vec_copy(turn).wait_send()
        each(depth, lambda s: self.vec_far(lax.rem(z + s, depth), z).wait_send(), 1)
        reducing.finish()
        each(depth, lambda step: self.token_copy(step).wait())
        state_copy.wait()
        state_out[...] = self.state_in[...]
        keep.wait()


def group_of(index):
    half, part = index % 2, index // 2
    return half * 3 + part, half, part


def turn_of(step):
    return group_of(jnp.maximum(step - 1, 0))


def entry_body(depth, rounds, fused, *refs):
    step = pl.program_id(0)
    tokens, state_filter = refs[:2]
    if fused:
        raw, cot = refs[2:13], refs[13]
        refs = refs[14:]
    else:
        doc_col, doc_row, w_gate, w_inner, w_small, par, heads_ref, edge, halo_docs = refs[2:11]
        refs = refs[11:]
    (
        hidden_out, cin_out, gate_out, pre_out, loc_out, carry_out, cin_state_out, pre_state_out,
        bc_out, bct_out, score_out, mask_out, zst_out, dt_out, sp_out, cumt_out, fac_out, match_out,
        local_out,
    ) = refs[:19]
    refs = refs[19:]
    if fused:
        small_out, parts_out, exit_out, par, heads_ref, cot_t = refs[:6]
        refs = refs[6:]
    hidden, normed, sp_tail, facs, folds, gains = refs[:6]
    rows, model = tokens.shape[1:]
    spans = rows // Q
    place = Place(depth)
    chaining = Chaining(place, rounds, False, folds, gains, refs[6:10], refs[10:14])
    group, half, part = turn_of(step)
    y = place.y
    if fused:
        v_small, v_parts, edge, halo_docs, docs_in, cot_in, par_in = refs[14:21]
        side_send, side_land, local, out_sem = refs[21:25]
        packed = refs[25:33]
        own_small, own_parts, own_exit, own_par, doc_col, doc_row, own_edge, own_docs = packed
        marks = refs[33:]
        own = [own_small, own_parts.at[0], own_parts.at[1], own_parts.at[2], own_exit]
        full = [v_small, v_parts.at[0], v_parts.at[1], v_parts.at[2], exit_out]
        pieces = [
            Gathering(place, own[i], full[i], *marks[3 * i : 3 * i + 3]) for i in range(5)
        ]
        stores = [pltpu.make_async_copy(v_small, small_out, out_sem.at[0])]
        for index in range(3):
            stores.append(
                pltpu.make_async_copy(
                    v_parts.at[index], parts_out.at[index], out_sem.at[index + 1]
                )
            )

    def before_weights():
        for ref, first, count in ((edge, 0, HALO), (tokens, HALO, rows)):
            value = (ref[...] if ref is edge else ref[0]).astype(F32)
            scale = lax.rsqrt(jnp.mean(value * value, axis=1, keepdims=True) + EPSILON)
            normed[first : first + count] = value * scale
        docs = jnp.concatenate([halo_docs[...], doc_col[...]], axis=0)
        for back in range(1, CONV):
            match = (docs[HALO - back : HALO - back + rows] == docs[HALO:]).astype(F32)
            match_out[back - 1] = match
        t_at, u_at = iota((Q, Q), 0), iota((Q, Q), 1)
        for index in range(spans):
            at = slice(index * Q, (index + 1) * Q)
            same = (t_at >= u_at) & (doc_col[at] == doc_row[0:1, at])
            mask_out[at] = jnp.where(same, 0.0, FAR)

    def after_weights(small):
        gain = jnp.transpose(small[0][:, LANES:].astype(F32))[24:25]
        hidden[...] = (normed[...] * gain).astype(LOW)
        hidden_out[...] = jnp.transpose(hidden[HALO:])
        both = [mm(hidden[...], small[index]) for index in range(2)]
        cin = jnp.concatenate([both[0][:, :LANES], both[1][:, :LANES]], axis=1).astype(LOW)
        cin_state_out[...] = cin
        docs = jnp.concatenate([halo_docs[...], doc_col[...]], axis=0)
        masks = [match_out[back] for back in range(CONV - 1)]
        pre = conv_forward(cin.astype(F32), state_filter[...], masks)
        pre_state_out[...] = pre
        mixed = (pre * sigmoid(pre)).astype(LOW)
        bc_out[...] = mixed
        turned = jnp.transpose(mixed.astype(F32)).astype(LOW)
        bct_out[...] = turned
        heads = heads_ref[...]
        used = iota((rows, LANES), 1) < 24
        raw = both[0][HALO:, LANES:] + both[1][HALO:, LANES:]
        zst = jnp.where(used, raw, 0.0) + heads[0:1]
        zst_out[...] = zst
        dt = jnp.where(used, jnp.maximum(zst, 0.0) + jnp.log1p(jnp.exp(-jnp.abs(zst))), 0.0)
        dt_out[...] = dt
        decay = -dt * jnp.exp(heads[1:2])
        t_at, u_at = iota((Q, Q), 0), iota((Q, Q), 1)
        lower = (t_at >= u_at).astype(F32)
        fac_rows = []
        for index in range(spans):
            at = slice(index * Q, (index + 1) * Q)
            cum = mm_exact(lower, decay[at])
            final = cum[Q - 1 : Q]
            before = docs[HALO + index * Q - 1 : HALO + index * Q]
            here = doc_col[at]
            last = here[Q - 1 : Q]
            opened = (here == before).astype(F32)
            tail = (here == last).astype(F32) * jnp.exp(final - cum)
            fac_rows.append((last == before).astype(F32) * jnp.exp(final))
            cum2 = cum * LOG2E
            turned_cum = jnp.transpose(cum2)
            for group in range(6):
                cumt_out[group, 0:4, at] = turned_cum[4 * group : 4 * group + 4]
            sp_out[0, at] = split3(dt[at])
            sp_out[1, at] = split3(cum2)
            lanes_used = iota((Q, LANES), 1) < 24
            sp_out[2, at] = split3(jnp.where(lanes_used, opened * jnp.exp(cum), 0.0))
            sp_out[3, at] = split3(jnp.where(lanes_used, tail, 0.0))
            sp_tail[at] = split3(jnp.where(lanes_used, tail * dt[at], 0.0))
            score_out[at] = mm_nt(mixed[at, LANES:], mixed[at, :LANES])
        gain_total = fac_rows[0]
        for row in fac_rows[1:]:
            gain_total = gain_total * row
        rows8 = jnp.concatenate(
            fac_rows + [gain_total] + [jnp.zeros((1, LANES), F32)] * (7 - spans), axis=0
        )
        rows8 = jnp.where(iota((8, LANES), 1) < 24, rows8, 0.0)
        fac_out[...] = rows8
        facs[...] = split3(rows8)

    if fused:

        @pl.when(step == 0)
        def _():
            count = 2 * depth
            onward = {"context": lax.rem(place.position + 1, count)}
            behind = {"context": lax.rem(place.position + count - 1, count)}
            pack_body(*raw, tokens.at[:, rows - HALO :], *packed)
            place.greet(
                [place.mate, place.x_peer, place.y_peer, onward, behind], chaining.sometimes(), True
            )
            sides = [
                remote(own_edge, edge, side_send.at[0], side_land.at[0], onward),
                remote(own_docs, docs_in, side_send.at[1], side_land.at[1], onward),
                remote(own_par, par_in.at[y], side_send.at[2], side_land.at[2], place.y_peer),
            ]
            for copy in sides:
                copy.start()
            for piece in pieces:
                piece.own()
            cot_copy = pltpu.make_async_copy(cot.at[y], cot_in, local.at[0])
            par_keep = pltpu.make_async_copy(own_par, par_in.at[y], local.at[1])
            cot_copy.start()
            par_keep.start()
            for copy in sides:
                copy.wait()
            par_keep.wait()
            pieces[0].near()
            pieces[1].near()
            halo_docs[...] = jnp.where(place.position == 0, -1.0, docs_in[...])
            par[...] = par_in[...]
            both = par[0, CONV + 2 : CONV + 3] + par[1, CONV + 2 : CONV + 3]
            heads_ref[...] = jnp.zeros_like(heads_ref)
            for index in range(3):
                heads_ref[index : index + 1] = both[:, index * LANES : (index + 1) * LANES]
            before_weights()
            pieces[0].across()
            pieces[2].near()
            pieces[1].across()
            pieces[0].far()
            cot_copy.wait()
            cot_t[...] = jnp.transpose(cot_in[...])
            pieces[0].mates()
            stores[0].start()
            after_weights([v_small[index].reshape(model, WIDE) for index in range(2)])

        @pl.when(step == 1)
        def _():
            pieces[3].near()
            pieces[2].across()
            pieces[1].far()
            pieces[1].mates()
            stores[1].start()

        @pl.when(step == 2)
        def _():
            pieces[4].near()

        @pl.when(step == 3)
        def _():
            pieces[3].across()
            pieces[2].far()
            pieces[2].mates()
            stores[2].start()

        @pl.when(step == 4)
        def _():
            pieces[4].across()

        @pl.when(step == 5)
        def _():
            pieces[3].far()
            pieces[3].mates()
            stores[3].start()

        @pl.when(step == 6)
        def _():
            pieces[4].far()

    else:

        @pl.when(step == 0)
        def _():
            place.greet([place.mate], chaining.sometimes())
            before_weights()
            after_weights([w_small[index] for index in range(2)])

    for cut in range(GROUPS - 1):

        @pl.when(step == cut + 2)
        def _():
            chaining.pass_on(0, cut)

    for cut in range(GROUPS - 3):

        @pl.when(step == cut + 4)
        def _():
            chaining.relay(0, cut)

    @pl.when(step > 0)
    def _():
        if fused:
            gate_low = v_parts[part, half, :, :, :, :WIDE].reshape(model, WIDE)
            inner_low = v_parts[part, half, :, :, :, WIDE:].reshape(model, WIDE)
        else:
            gate_low, inner_low = w_gate[0, 0], w_inner[0, 0]
        taps = par[half, :, pl.ds(pl.multiple_of(part * WIDE, WIDE), WIDE)]
        cin = mm(hidden[...], inner_low).astype(LOW)
        cin_out[...] = cin
        gate_out[...] = mm(hidden[HALO:], gate_low)
        masks = [match_out[back] for back in range(CONV - 1)]
        pre = conv_forward(cin.astype(F32), taps, masks)
        pre_out[...] = pre
        spread = spreader(4 * group, HEAD, 4)
        mix = pre * sigmoid(pre)
        value = (mix * mm(sp_tail[...], spread)).astype(LOW)
        facx = mm(facs[...], spread)
        cums = mm(sp_out[1], spreader(4 * group, LANES, 4))
        skipx = mm(split3(heads_ref[...]), spread)[2:3]
        stepped = mix * mm(sp_out[0], spread)
        first_half = iota((Q, LANES), 1) < HEAD
        fold = jnp.zeros((NSTATE, WIDE), F32)
        for index in range(spans):
            at = slice(index * Q, (index + 1) * Q)
            loc = mm(bct_out[:NSTATE, at], value[at])
            loc_out[at] = loc
            fold = facx[index : index + 1] * fold + loc
            parts = []
            for pair in range(2):
                lanes = slice(pair * LANES, (pair + 1) * LANES)
                weights, seen = [], []
                for head in (2 * pair, 2 * pair + 1):
                    across = cumt_out[group, head : head + 1, at]
                    spread_at = cums[at, head * LANES : (head + 1) * LANES] - across + mask_out[at]
                    weights.append((jnp.exp2(spread_at) * score_out[at]).astype(LOW))
                    keep = first_half if head % 2 == 0 else jnp.logical_not(first_half)
                    seen.append(jnp.where(keep, stepped[at, lanes], 0.0).astype(LOW))
                parts.append(mm(jnp.concatenate(weights, axis=1), jnp.concatenate(seen, axis=0)))
            local_out[at] = jnp.concatenate(parts, axis=1) + skipx * mix[at]
        folds[step - 1] = fold
        gains[step - 1] = jnp.broadcast_to(facx[spans : spans + 1], (8, WIDE))

    for cut in range(GROUPS):

        @pl.when(step == cut + 1)
        def _():
            chaining.open(cut)

    @pl.when(step == GROUPS)
    def _():
        chaining.pass_on(0, GROUPS - 1)
        for cut in range(GROUPS - 3, GROUPS):
            chaining.relay(0, cut)
        chaining.later()

        def put(cut, value):
            at = ORDER[cut] * WIDE
            carry_out[:, at : at + WIDE] = value

        chaining.arrive(put)
        if fused:
            pieces[4].mates()
            for piece in pieces:
                piece.finish()
            for store in stores:
                store.wait()
        chaining.finish()


def entry(tokens, raw, state_filter, cot, rounds):
    rows, model = tokens.shape[1:]
    own_small, own_parts, own_exit, own_par, doc_col, doc_row, own_edge, own_docs = pack_shapes(
        raw[0].shape[0], raw[0].shape[2], rows, model
    )
    count = lax.axis_size("context")
    depth = count // 2
    wide = GROUPS * WIDE
    ext = rows + HALO
    fused = own_small.shape[0] % 16 == 0
    shape = jax.ShapeDtypeStruct
    sem = lambda *lead: pltpu.SemaphoreType.DMA(lead)
    column = lambda count: pl.BlockSpec((count, WIDE), lambda s: (0, turn_of(s)[0]))
    whole = lambda *dims, dtype=F32: (shape(dims, dtype), const(dims))
    outs = [
        whole(model, rows, dtype=LOW),
        (shape((ext, wide), LOW), column(ext)),
        (shape((rows, wide), F32), column(rows)),
        (shape((rows, wide), F32), column(rows)),
        (shape((rows, wide), F32), column(rows)),
        whole(NSTATE, wide, dtype=LOW),
        whole(ext, WIDE, dtype=LOW),
        whole(rows, WIDE),
        whole(rows, WIDE, dtype=LOW),
        whole(WIDE, rows, dtype=LOW),
        whole(rows, Q),
        whole(rows, Q),
        whole(rows, LANES),
        whole(rows, LANES),
        whole(4, rows, LANES, dtype=LOW),
        whole(6, 8, rows),
        whole(8, LANES),
        whole(CONV - 1, rows, LANES),
        (shape((rows, wide), F32), column(rows)),
    ]
    scratch = [
        pltpu.VMEM((ext, model), LOW),
        pltpu.VMEM((ext, model), F32),
        pltpu.VMEM((rows, LANES), LOW),
        pltpu.VMEM((8, LANES), LOW),
        pltpu.VMEM((GROUPS, NSTATE, WIDE), F32),
        pltpu.VMEM((GROUPS, 8, WIDE), F32),
    ] + Chaining.scratch(rounds)
    in_specs = [
        pl.BlockSpec((1, rows, model), lambda s: (side(), 0, 0)),
        fixed((CONV + 1, WIDE)),
    ]
    args = [tokens, state_filter]
    full = lambda own: (2, 2, count) + own.shape[-2:]
    if fused:
        outs += [
            (shape(full(own_small), LOW), ANY_SPEC),
            (shape((3,) + full(own_parts), LOW), ANY_SPEC),
            (shape(full(own_exit), LOW), ANY_SPEC),
            (shape((2,) + own_par.shape, F32), VMEM_SPEC),
            (shape((8, LANES), F32), VMEM_SPEC),
            (shape((model, rows), LOW), VMEM_SPEC),
        ]
        scratch += [
            pltpu.VMEM(full(own_small), LOW),
            pltpu.VMEM((3,) + full(own_parts), LOW),
            pltpu.VMEM(own_edge.shape, LOW),
            pltpu.VMEM(own_docs.shape, F32),
            pltpu.VMEM(own_docs.shape, F32),
            pltpu.VMEM((rows, model), LOW),
            pltpu.VMEM((2,) + own_par.shape, F32),
            sem(3),
            sem(3),
            sem(2),
            sem(4),
        ]
        own = (own_small, own_parts, own_exit, own_par, doc_col, doc_row, own_edge, own_docs)
        scratch += [pltpu.VMEM(one.shape, one.dtype) for one in own] + Gathering.scratch(depth) * 5
        in_specs += [fixed(one.shape) for one in raw] + [ANY_SPEC]
        args += [*raw, cot]
    else:
        *packs, doc_col, doc_row, edge, docs = pack(raw, tokens)
        small, parts, exits, par, heads, edge, docs, cot_t = gather(*packs, edge, docs, cot)
        in_specs += [fixed((rows, LANES)), fixed((8, rows))]
        args += [doc_col, doc_row]
        weights = parts.reshape(3, 2, model, 2 * WIDE)
        block = lambda at: pl.BlockSpec(
            (1, 1, model, WIDE), lambda s: (turn_of(s)[2], turn_of(s)[1], 0, at)
        )
        in_specs += [block(0), block(1), fixed((2, model, WIDE))] + [VMEM_SPEC] * 4
        args += [weights, weights, small.reshape(2, model, WIDE), par, heads, edge, docs]
    results = pl.pallas_call(
        functools.partial(entry_body, depth, rounds, fused),
        out_shape=[out[0] for out in outs],
        grid=(GROUPS + 1,),
        in_specs=in_specs,
        out_specs=[out[1] for out in outs],
        scratch_shapes=scratch,
        compiler_params=params(collective_id=1, has_side_effects=True),
        name="entry",
    )(*args)
    if fused:
        small, parts, exits, par, heads, cot_t = results[19:]
    return tuple(results[:19]), (
        small.reshape(2, model, WIDE),
        parts.reshape(3, 2, model, 2 * WIDE),
        exits.reshape(2, model, -1),
        par,
        heads,
        cot_t,
    )


def middle_body(
    tokens_far, cot, cot_t_far, hidden_far, pre_ref, gate_ref, loc_ref, local_ref, carry_ref, w_exit,
    par, bc, bct, sp, fac, block_out, exit_out, gate_part_out, dy_out, gpg_out, enter_out, row_out,
    skip_out, outputs, gates, unit_grads, mixes, sums, total,
    tokens, cot_t, hidden_t, late_sem
):
    step = pl.program_id(0)
    rows = pre_ref.shape[0]
    spans = rows // Q
    wide = 6 * WIDE

    late = [
        pltpu.make_async_copy(src, dst, late_sem.at[index])
        for index, (src, dst) in enumerate(
            ((cot_t_far, cot_t), (hidden_far, hidden_t), (tokens_far.at[side()], tokens))
        )
    ]

    @pl.when(step == 0)
    def _():
        for copy in late:
            copy.start()
        sums[...] = jnp.zeros_like(sums)
        total[...] = jnp.zeros_like(total)
        skip_out[...] = jnp.zeros_like(skip_out)

    @pl.when(step < 6)
    def _():
        group = step
        spread = spreader(4 * group, HEAD, 4)
        pre = pre_ref[...]
        mix = pre * sigmoid(pre)
        mixes[group] = mix
        growth = mm(sp[2], spread)
        facx = mm(split3(fac[...]), spread)
        state = carry_ref[...].astype(F32)
        for index in range(spans):
            at = slice(index * Q, (index + 1) * Q)
            carried = mm(bc[at, LANES:], state.astype(LOW)) * growth[at]
            out = local_ref[at] + carried
            outputs[group, at] = out
            state = facx[index : index + 1] * state + loc_ref[at]
        gate = gate_ref[...]
        gates[group] = gate
        gated = outputs[group] * (gate * sigmoid(gate))
        unit_grad = mm(cot[0], w_exit[0])
        unit_grads[group] = unit_grad
        square = gated * gated
        cross = unit_grad * par[0, 5:6] * gated
        sums[0] += square[:, :LANES] + square[:, LANES:]
        sums[1] += cross[:, :LANES] + cross[:, LANES:]

    @pl.when(step == 5)
    def _():
        for copy in late:
            copy.wait()
        square = jnp.sum(sums[0], axis=1, keepdims=True)
        cross = jnp.sum(sums[1], axis=1, keepdims=True)
        normal = lax.rsqrt(square / wide + EPSILON)
        sums[0] = jnp.broadcast_to(normal, (rows, LANES))
        sums[1] = jnp.broadcast_to(normal * normal * normal * cross / wide, (rows, LANES))

    @pl.when(step >= 6)
    def _():
        group = step - 6
        spread = spreader(4 * group, HEAD, 4)
        normal = twice(sums[0])
        pull = twice(sums[1])
        gain = par[0, 5:6]
        gate = gates[group]
        out = outputs[group]
        unit_grad = unit_grads[group]
        sigma = sigmoid(gate)
        act = gate * sigma
        gated = out * act
        scaled_in = gated * normal
        unit = (scaled_in * gain).astype(LOW)
        total[...] += mm_nt(unit, w_exit[0])
        exit_out[0] = mm(cot_t[...], unit).astype(LOW)
        gate_sum = jnp.sum(unit_grad * scaled_in, axis=0, keepdims=True)
        gated_grad = normal * (unit_grad * gain) - pull * gated
        dy = gated_grad * act
        dy_out[...] = dy
        gate_grad = (gated_grad * out * sigma * (1.0 + gate * (1.0 - sigma))).astype(LOW)
        gpg_out[...] = gate_grad
        gate_part_out[0] = mm(hidden_t[...], gate_grad).astype(LOW)
        skip_sum = jnp.sum(dy * mixes[group], axis=0, keepdims=True)
        row_out[...] = jnp.broadcast_to(gate_sum, (8, WIDE))
        skip_out[...] += head_sums(
            jnp.broadcast_to(skip_sum, (8, WIDE)), gatherer(4 * group, HEAD, 4)
        )
        facx = mm(split3(fac[...]), spread)
        pushed = (dy * mm(sp[2], spread)).astype(LOW)
        enter = jnp.zeros((NSTATE, WIDE), F32)
        for index in reversed(range(spans)):
            at = slice(index * Q, (index + 1) * Q)
            enter = facx[index : index + 1] * enter + mm(bct[NSTATE:, at], pushed[at])
        enter_out[...] = enter

    @pl.when(step == 11)
    def _():
        block_out[...] = (tokens[...].astype(F32) + total[...]).astype(LOW)


def middle(
    tokens, cot, cot_t, hidden_t, pre, gate, loc, local, carry, weights, par, bc, bct, sp, fac
):
    rows, model = tokens.shape[1:]
    wide = 6 * WIDE
    shape = jax.ShapeDtypeStruct

    def early(s):
        return jnp.minimum(s, 5)

    def late(s):
        return jnp.maximum(s - 6, 0)

    def group(s):
        return s % 6

    outs = (
        (shape((rows, model), LOW), const((rows, model))),
        (
            shape((2, model, 3 * WIDE), LOW),
            pl.BlockSpec((1, model, WIDE), lambda s: (late(s) // 3, 0, late(s) % 3)),
        ),
        (
            shape((2, model, 3 * WIDE), LOW),
            pl.BlockSpec((1, model, WIDE), lambda s: (late(s) // 3, 0, late(s) % 3)),
        ),
        (shape((rows, wide), F32), pl.BlockSpec((rows, WIDE), lambda s: (0, late(s)))),
        (shape((rows, wide), LOW), pl.BlockSpec((rows, WIDE), lambda s: (0, late(s)))),
        (shape((NSTATE, wide), F32), pl.BlockSpec((NSTATE, WIDE), lambda s: (0, late(s)))),
        (shape((8, wide), F32), pl.BlockSpec((8, WIDE), lambda s: (0, late(s)))),
        (shape((8, LANES), F32), const((8, LANES))),
    )
    return pl.pallas_call(
        middle_body,
        out_shape=[out[0] for out in outs],
        grid=(12,),
        in_specs=[
                ANY_SPEC,
                pl.BlockSpec((1, rows, model), lambda s: (side(), 0, 0)),
                ANY_SPEC,
                ANY_SPEC,
                pl.BlockSpec((rows, WIDE), lambda s: (0, early(s))),
                pl.BlockSpec((rows, WIDE), lambda s: (0, early(s))),
                pl.BlockSpec((rows, WIDE), lambda s: (0, early(s))),
                pl.BlockSpec((rows, WIDE), lambda s: (0, early(s))),
                pl.BlockSpec((NSTATE, WIDE), lambda s: (0, early(s))),
                pl.BlockSpec((1, model, WIDE), lambda s: (group(s) // 3, 0, group(s) % 3)),
                pl.BlockSpec((1, 8, WIDE), lambda s: (group(s) // 3, 0, group(s) % 3)),
                fixed((rows, WIDE)),
                fixed((WIDE, rows)),
                fixed((4, rows, LANES)),
                fixed((8, LANES)),
        ],
        out_specs=[out[1] for out in outs],
        scratch_shapes=[
                pltpu.VMEM((6, rows, WIDE), F32),
                pltpu.VMEM((6, rows, WIDE), F32),
                pltpu.VMEM((6, rows, WIDE), F32),
                pltpu.VMEM((6, rows, WIDE), F32),
                pltpu.VMEM((2, rows, LANES), F32),
                pltpu.VMEM((rows, model), F32),
                pltpu.VMEM((rows, model), LOW),
                pltpu.VMEM((model, rows), LOW),
                pltpu.VMEM((model, rows), LOW),
                pltpu.SemaphoreType.DMA((3,)),
        ],
        compiler_params=params(),
        name="middle",
    )(tokens, cot, cot_t, hidden_t, pre, gate, loc, local, carry, weights, par, bc, bct, sp, fac)


def scan_back_body(depth, rounds, fused, *refs):
    (
        pre_ref, dy_ref, loc_ref, carry_ref, enter, cin_ref, par, par_heads, state_filter, cin_far,
        pre_far, bc, bct, score, mask, sp, cumt, fac, match_far, zst_far, dt_far, exits, gate_part,
        block_far, tokens_far, cot_far, hidden_far, gpg, w_gate, w_inner, small_far, gate_row,
        skip_row,
    ) = refs[:33]
    mine, block_out = refs[33:35]
    if fused:
        mine2, mine3, state_out, vector_out, token_both = refs[35:40]
        refs = refs[40:]
    else:
        tap_out, tap_state_out, small_out, inner_part, small_part, token_out, norm_out = refs[35:42]
        refs = refs[42:]
    block_own, hidden_t, match, tokens, cot, w_small, pre_state, cin_state, zst, dt_ref = refs[:10]
    late_sem = refs[10]
    refs = refs[11:]
    late = [
        pltpu.make_async_copy(src, dst, late_sem.at[index])
        for index, (src, dst) in enumerate(
            (
                (block_far, block_own), (hidden_far, hidden_t), (match_far, match),
                (tokens_far.at[side()], tokens), (cot_far.at[side()], cot), (small_far, w_small),
                (pre_far, pre_state), (cin_far, cin_state), (zst_far, zst), (dt_far, dt_ref),
            )
        )
    ]
    (
        d_bc, d_score, d_cum, heads, local_value, enters, gains, adjoints, edge_own, edge_in, grads,
        total, es, el, bs, bl, block_keep,
    ) = refs[:17]
    scratch = refs[17:42]
    step = pl.program_id(0)
    group, half_at, part_at = group_of(jnp.minimum(step, GROUPS - 1))
    last_group, last_half, last_part = group_of(jnp.maximum(step - 1, 0))
    blocks = BLOCK_CUTS
    rows = pre_ref.shape[0]
    spans = rows // Q
    place = Place(depth)
    wide = exits.shape[-1]
    chaining = Chaining(place, rounds, True, enters, gains, scratch[:4], scratch[4:8])
    reducing = Reducing(
        place, 0, [(exits, slice(0, wide)), (gate_part, slice(wide, 2 * wide))], mine,
        scratch[8:16], scratch[16:25],
    )
    if fused:
        inner_v, small_v, token_v, taps_v = refs[42:46]
        buffers = refs[46:]
        second = Reducing(
            place, 0, [(inner_v.at[0], slice(0, WIDE)), (inner_v.at[1], slice(WIDE, 2 * WIDE))],
            mine2, buffers[:8], buffers[8:17],
        )
        third = Reducing(
            place, 0, [(inner_v.at[2], slice(0, WIDE)), (small_v, slice(WIDE, 2 * WIDE))], mine3,
            buffers[17:25], buffers[25:34],
        )
        closing = Closing(place, token_v, token_both, buffers[34:])
    position = place.position
    has_before, has_after = position > 0, position < 2 * depth - 1
    before, after = {"context": position - 1}, {"context": position + 1}
    share = rows // blocks

    def block_copy(index):
        at = pl.ds(pl.multiple_of(index * share, share), share)
        return remote(
            block_own.at[at], block_out.at[place.y, at], bs.at[index], bl.at[index], place.y_peer
        )

    block_local = pltpu.make_async_copy(block_own, block_out.at[place.y], block_keep.at[0])

    def edge_copy(index):
        return remote(edge_own.at[index], edge_in.at[index], es.at[index], el.at[index], before)

    def edge_wait(index):
        @pl.when(has_after)
        def _():
            edge_copy(index).wait_recv()

    def put_inner(value):
        if fused:
            inner_v[last_part, last_half] = value.reshape(inner_v.shape[2:])
        else:
            inner_part[0] = value

    def joined(index):
        grad = grads[...]
        return jnp.concatenate(
            [grad[: rows - EDGE], grad[rows - EDGE :] + edge_in[index]], axis=0
        ).astype(LOW)

    @pl.when(step == 0)
    def _():
        for copy in late:
            copy.start()
        d_bc[...] = jnp.zeros_like(d_bc)
        d_score[...] = jnp.zeros_like(d_score)
        d_cum[...] = jnp.zeros_like(d_cum)
        heads[...] = jnp.zeros_like(heads)
        grads[...] = jnp.zeros_like(grads)
        total[...] = jnp.zeros_like(total)
        edge_in[GROUPS + 1] = jnp.zeros((EDGE, WIDE), F32)

        @pl.when(jnp.logical_not(has_after))
        def _():
            edge_in[...] = jnp.zeros_like(edge_in)

        place.greet(
            [place.mate, place.x_peer, place.y_peer],
            chaining.sometimes() + [(has_before, before), (has_after, after)],
            True,
        )
        facs = split3(fac[...])
        for cut in range(GROUPS):
            enters[cut] = enter[:, cut * WIDE : (cut + 1) * WIDE]
            chaining.open(cut)
        for cut in range(GROUPS):
            rows8 = mm(facs, spreader(4 * cut, HEAD, 4))
            gains[cut] = jnp.broadcast_to(rows8[spans : spans + 1], (8, WIDE))
        each(depth, reducing.start)
        late[0].wait()
        block_local.start()
        each(3, lambda index: block_copy(index).start())
        for cut in range(GROUPS):
            chaining.pass_on(0, cut)

    if fused:

        @pl.when(step == 5)
        def _():
            each(depth, second.start)

    @pl.when(step < GROUPS)
    def _():
        spread = spreader(4 * group, HEAD, 4)
        collect = gatherer(4 * group, HEAD, 4)
        pre = pre_ref[...]
        sigma = sigmoid(pre)
        mix = pre * sigma
        dtx = mm(sp[0], spread)
        growth = mm(sp[2], spread)
        facx = mm(split3(fac[...]), spread)
        cums = mm(sp[1], spreader(4 * group, LANES, 4))
        ones = jnp.ones((8, Q), F32).astype(LOW)
        states = [carry_ref[...].astype(F32)]
        for index in range(spans - 1):
            at = slice(index * Q, (index + 1) * Q)
            states.append(facx[index : index + 1] * states[-1] + loc_ref[at])
        for index in range(spans):
            at = slice(index * Q, (index + 1) * Q)
            dy = dy_ref[at]
            value = mix[at] * dtx[at]
            value_low = value.astype(LOW)
            lane = iota((Q, WIDE), 1) // HEAD
            dy_heads = [jnp.where(lane == head, dy, 0.0).astype(LOW) for head in range(4)]
            d_weight = mm_nt(jnp.concatenate(dy_heads, axis=0), value_low)
            parts = []
            sum_score = None
            row_sums = None
            for pair in range(2):
                lanes = slice(pair * LANES, (pair + 1) * LANES)
                moved, weights = [], []
                for head in (2 * pair, 2 * pair + 1):
                    across = cumt[group, head : head + 1, at]
                    spread_at = cums[at, head * LANES : (head + 1) * LANES] - across + mask[at]
                    decay = jnp.exp2(spread_at)
                    inner = decay * d_weight[head * Q : (head + 1) * Q]
                    sum_score = inner if sum_score is None else sum_score + inner
                    moved.append((inner * score[at]).astype(LOW))
                    weights.append((decay * score[at]).astype(LOW))
                both = jnp.concatenate(moved, axis=1)
                column_sums = mm(ones, both)
                for index_in in range(2):
                    head = 2 * pair + index_in
                    d_cum[group, head : head + 1, at] = -column_sums[
                        0:1, index_in * Q : (index_in + 1) * Q
                    ]
                part = mm(both, gatherer(4 * group + 2 * pair, LANES, 2))
                row_sums = part if row_sums is None else row_sums + part
                pushed_heads = [dy_heads[2 * pair][:, lanes], dy_heads[2 * pair + 1][:, lanes]]
                parts.append(
                    mm_tn(jnp.concatenate(weights, axis=0), jnp.concatenate(pushed_heads, axis=0))
                )
            d_score[at] += sum_score
            local_value[at] = jnp.concatenate(parts, axis=1)
            pushed = dy * growth[at]
            state_low = states[index].astype(LOW)
            carried = mm(bc[at, LANES:], state_low)
            d_bc[at, LANES:] += mm_nt(pushed.astype(LOW), state_low)
            heads[1, at] += head_sums(pushed * carried, collect) + row_sums

    @pl.when(step == 0)
    def _():
        for cut in range(GROUPS):
            chaining.relay(0, cut)
        chaining.later()

        def put(cut, value):
            adjoints[cut] = value

        chaining.arrive(put)
        chaining.finish()
        late[1].wait()
        late[2].wait()

    for turn in range(5):

        @pl.when(step == turn)
        def _():
            each(turn + 1 if turn < 4 else depth + 1, reducing.turn, turn)
            block_copy(turn + 3).start()

    @pl.when(step == 5)
    def _():
        reducing.close()
        if fused:
            second.turn(0)

    @pl.when((step > 0) & (step < GROUPS))
    def _():
        edge_wait(last_group)

    @pl.when(step < GROUPS)
    def _():
        spread = spreader(4 * group, HEAD, 4)
        collect = gatherer(4 * group, HEAD, 4)
        pre = pre_ref[...]
        sigma = sigmoid(pre)
        mix = pre * sigma
        dtx = mm(sp[0], spread)
        growth = mm(sp[2], spread)
        facx = mm(split3(fac[...]), spread)
        states = [carry_ref[...].astype(F32)]
        for index in range(spans - 1):
            at = slice(index * Q, (index + 1) * Q)
            states.append(facx[index : index + 1] * states[-1] + loc_ref[at])
        arrived = jnp.where(step > 0, last_group, GROUPS + 1)
        grad = joined(arrived)
        gate_grad = gpg[...]
        put_inner(mm(hidden_t[...], grad).astype(LOW))
        total[...] += mm_nt(gate_grad, w_gate[0, 0]) + mm_nt(grad, w_inner[0, 0])
        tails = mm(sp[3], spread)
        skipx = mm(split3(par_heads[...]), spread)[2:3]
        adjoint = adjoints[group].astype(F32)
        masks = [match[back] for back in range(CONV - 1)]
        pgs = [None] * spans
        for index in reversed(range(spans)):
            at = slice(index * Q, (index + 1) * Q)
            dy = dy_ref[at]
            value = mix[at] * dtx[at]
            adj_low = adjoint.astype(LOW)
            reached = mm(bc[at, :LANES], adj_low) * tails[at]
            d_bc[at, :LANES] += mm_nt((value * tails[at]).astype(LOW), adj_low)
            heads[0, at] += head_sums(value * reached, collect)
            fac_part = jnp.sum(adjoint * states[index], axis=0, keepdims=True)
            heads[3, index * 8 : index * 8 + 8] += head_sums(
                jnp.broadcast_to(fac_part, (8, WIDE)), collect
            )
            pushed_low = (dy * growth[at]).astype(LOW)
            adjoint = facx[index : index + 1] * adjoint + mm(bct[NSTATE:, at], pushed_low)
            d_value = local_value[at] + reached
            heads[2, at] += head_sums(mix[at] * d_value, collect)
            d_mix = dtx[at] * d_value + skipx * dy
            s = sigma[at]
            pgs[index] = d_mix * s * (1.0 + pre[at] * (1.0 - s))
        pg = jnp.concatenate(pgs, axis=0)
        sums, grad = conv_backward(pg, cin_ref[...].astype(F32), par[0], masks)
        taps8 = jnp.concatenate(sums + [jnp.zeros((3, WIDE), F32)], axis=0)
        if fused:
            taps_v[group] = taps8
        else:
            tap_out[...] = taps8
        grads[...] = grad[HALO:]
        edge_own[group] = grad[HALO - EDGE : HALO]

        @pl.when(has_before)
        def _():
            edge_copy(group).start()

    @pl.when(step == GROUPS)
    def _():
        for copy in late[3:]:
            copy.wait()
        if fused:
            second.turn(1)
        masks = [match[back] for back in range(CONV - 1)]
        edge_wait(GROUPS - 1)
        grad = joined(GROUPS - 1)
        put_inner(mm(hidden_t[...], grad).astype(LOW))
        total[...] += mm_nt(grad, w_inner[0, 0])
        t_at, u_at = iota((Q, Q), 0), iota((Q, Q), 1)
        onward = (t_at <= u_at).astype(F32)
        earlier = (t_at > u_at).astype(F32)
        rate = jnp.exp(par_heads[1:2])
        raws = []
        bias_sum = jnp.zeros((1, LANES), F32)
        decay_sum = jnp.zeros((1, LANES), F32)
        used = iota((Q, LANES), 1) < 24
        for index in range(spans):
            at = slice(index * Q, (index + 1) * Q)
            pieces = [d_cum[piece, 0:4, at] for piece in range(6)]
            pieces.append(jnp.zeros((LANES - 24, Q), F32))
            cum_col = jnp.transpose(jnp.concatenate(pieces, axis=0))
            fac_row = fac[index : index + 1] * heads[3, index * 8 : index * 8 + 1]
            d_decay = (
                mm_exact(onward, cum_col + heads[1, at]) + mm_exact(earlier, heads[0, at]) + fac_row
            )
            dt = dt_ref[at]
            raw = (heads[2, at] - d_decay * rate) * sigmoid(zst[at])
            raw = jnp.where(used, raw, 0.0)
            raws.append(raw.astype(LOW))
            bias_sum += jnp.sum(raw, axis=0, keepdims=True)
            decay_sum -= jnp.sum(
                jnp.where(used, d_decay * dt * rate, 0.0), axis=0, keepdims=True
            )
            score_low = d_score[at].astype(LOW)
            d_bc[at, :LANES] += mm_tn(score_low, bc[at, LANES:])
            d_bc[at, LANES:] += mm(score_low, bc[at, :LANES])
        if not fused:
            small_out[...] = jnp.concatenate(
                [bias_sum, decay_sum, jnp.zeros((6, LANES), F32)], axis=0
            )
        if fused:
            second.turn(2)
        pre = pre_state[...]
        s = sigmoid(pre)
        pg = d_bc[...] * s * (1.0 + pre * (1.0 - s))
        sums, grad = conv_backward(pg, cin_state[...].astype(F32), state_filter[...], masks)
        taps8 = jnp.concatenate(sums + [jnp.zeros((3, WIDE), F32)], axis=0)
        if fused:
            taps_v[GROUPS] = taps8
        else:
            tap_state_out[...] = taps8
        grads[...] = grad[HALO:]
        edge_own[GROUPS] = grad[HALO - EDGE : HALO]

        @pl.when(has_before)
        def _():
            edge_copy(GROUPS).start()

        steps = jnp.concatenate(raws, axis=0)
        turned = hidden_t[...]
        step_part = mm(turned, steps).astype(LOW)
        total[...] += mm_nt(steps, w_small[0, :, LANES:]) + mm_nt(steps, w_small[1, :, LANES:])
        edge_wait(GROUPS)
        state = joined(GROUPS)
        state_part = mm(turned, state).astype(LOW)
        for index in range(2):
            state_half = state_part[:, index * LANES : (index + 1) * LANES]
            value = jnp.concatenate([state_half, step_part], axis=1)
            if fused:
                small_v[index] = value.reshape(small_v.shape[1:])
            else:
                small_part[index] = value
        if fused:
            each(depth, third.start)
        value = tokens[...].astype(F32)
        scale = lax.rsqrt(jnp.mean(value * value, axis=1, keepdims=True) + EPSILON)
        hidden_grad = (
            total[...]
            + mm_nt(state[:, :LANES], w_small[0, :, :LANES])
            + mm_nt(state[:, LANES:], w_small[1, :, :LANES])
        )
        norm_sum = jnp.sum(hidden_grad * (value * scale), axis=0, keepdims=True)
        if not fused:
            norm_out[...] = jnp.broadcast_to(norm_sum, norm_out.shape)
        gain = jnp.transpose(w_small[0, :, LANES : 2 * LANES].astype(F32))[24:25]
        normed = hidden_grad * gain
        pull = jnp.sum(normed * value, axis=1, keepdims=True) / value.shape[1]
        token_low = (
            cot[...].astype(F32) + scale * normed - (scale * scale * scale) * value * pull
        ).astype(LOW)
        if fused:
            token_v[...] = token_low
            for index in range(GROUPS + 1):
                at = slice(index * WIDE, (index + 1) * WIDE)
                closing.send[0, : CONV + 1, at] = taps_v[index, : CONV + 1]
            high = GROUPS * WIDE
            closing.send[0, CONV + 1 :] = jnp.zeros((8 - CONV - 1, high + WIDE), F32)
            closing.send[0, 5:6, :high] = gate_row[0:1]
            closing.send[0, 5:6, high : high + LANES] = bias_sum
            closing.send[0, 5:6, high + LANES :] = skip_row[0:1]
            model = norm_sum.shape[1]
            closing.send[0, 6:7, :model] = norm_sum
            closing.send[0, 6:7, model : model + LANES] = decay_sum
            closing.run(third, NSTATE, state_out, vector_out, WIDE, second)
            second.finish()
        else:
            token_out[...] = token_low
        reducing.finish()
        each(blocks, lambda index: block_copy(index).wait())
        block_local.wait()

        @pl.when(has_before)
        def _():
            each(GROUPS + 1, lambda index: edge_copy(index).wait_send())


def scan_back(
    pre, dy, loc, carry, enter, cin, par, par_heads, state_filter, cin_state, pre_state, bc, bct,
    score, mask, sp, cumt, fac, match, zst, dt, exits, gate_part, block_own, tokens, cot, hidden_t,
    gpg, parts, small, gate_row, skip_row, rounds
):
    rows, wide = pre.shape
    ext = rows + HALO
    depth = lax.axis_size("context") // 2
    own_rows, half_wide = exits.shape[3:]
    shape = jax.ShapeDtypeStruct
    sem = lambda *lead: pltpu.SemaphoreType.DMA(lead)
    model = tokens.shape[2]
    count = 2 * depth
    fused = own_rows % 16 == 0
    now = lambda s: group_of(jnp.minimum(s, GROUPS - 1))
    lag = lambda s: group_of(jnp.maximum(s - 1, 0))
    column = lambda count: pl.BlockSpec((count, WIDE), lambda s: (0, now(s)[0]))
    whole = lambda *dims, dtype=F32: (shape(dims, dtype), const(dims))
    outs = [
        whole(own_rows, 2 * half_wide),
        (shape((2,) + block_own.shape, LOW), ANY_SPEC),
    ]
    if fused:
        outs += [
            whole(own_rows, 2 * WIDE),
            whole(own_rows, 2 * WIDE),
            whole(2, own_rows, NSTATE),
            whole(8, wide + WIDE),
            (shape((2, rows, model), LOW), ANY_SPEC),
        ]
        extra = (
            [
                pltpu.VMEM((3, 2, 2, count, own_rows, WIDE), LOW),
                pltpu.VMEM((2, 2, count, own_rows, WIDE), LOW),
                pltpu.VMEM((rows, model), LOW),
                pltpu.VMEM((GROUPS + 1, 8, WIDE), F32),
            ]
            + Reducing.scratch(depth, own_rows, 2 * WIDE) * 2
            + Closing.scratch(depth, own_rows, (8, wide + WIDE))
        )
    else:
        outs += [
            (shape((8, wide), F32), column(8)),
            whole(8, WIDE),
            whole(8, LANES),
            (
                shape((2, model, 3 * WIDE), LOW),
                pl.BlockSpec((1, model, WIDE), lambda s: (lag(s)[1], 0, lag(s)[2])),
            ),
            whole(2, model, WIDE, dtype=LOW),
            whole(rows, model, dtype=LOW),
            whole(8, model),
        ]
        extra = []
    return pl.pallas_call(
        functools.partial(scan_back_body, depth, rounds, fused),
        out_shape=[out[0] for out in outs],
        grid=(GROUPS + 1,),
        in_specs=[
            column(rows),
            column(rows),
            column(rows),
            column(NSTATE),
            fixed((NSTATE, wide)),
            column(ext),
            pl.BlockSpec((1, 8, WIDE), lambda s: (now(s)[1], 0, now(s)[2])),
            fixed((8, LANES)),
            fixed((CONV + 1, WIDE)),
            ANY_SPEC,
            ANY_SPEC,
            fixed((rows, WIDE)),
            fixed((WIDE, rows)),
            fixed((rows, Q)),
            fixed((rows, Q)),
            fixed((4, rows, LANES)),
            fixed((6, 8, rows)),
            fixed((8, LANES)),
            ANY_SPEC,
            ANY_SPEC,
            ANY_SPEC,
            ANY_SPEC,
            ANY_SPEC,
            ANY_SPEC,
            ANY_SPEC,
            ANY_SPEC,
            ANY_SPEC,
            column(rows),
            pl.BlockSpec((1, 1, model, WIDE), lambda s: (now(s)[2], now(s)[1], 0, 0)),
            pl.BlockSpec((1, 1, model, WIDE), lambda s: (lag(s)[2], lag(s)[1], 0, 1)),
            ANY_SPEC,
            fixed((8, wide)),
            fixed((8, LANES)),
        ],
        out_specs=[out[1] for out in outs],
        scratch_shapes=[
            pltpu.VMEM((rows, model), LOW),
            pltpu.VMEM((model, rows), LOW),
            pltpu.VMEM((CONV - 1, rows, LANES), F32),
            pltpu.VMEM((rows, model), LOW),
            pltpu.VMEM((rows, model), LOW),
            pltpu.VMEM((2, model, WIDE), LOW),
            pltpu.VMEM((rows, WIDE), F32),
            pltpu.VMEM((ext, WIDE), LOW),
            pltpu.VMEM((rows, LANES), F32),
            pltpu.VMEM((rows, LANES), F32),
            sem(10),
            pltpu.VMEM((rows, WIDE), F32),
            pltpu.VMEM((rows, Q), F32),
            pltpu.VMEM((6, 8, rows), F32),
            pltpu.VMEM((4, rows, LANES), F32),
            pltpu.VMEM((rows, WIDE), F32),
            pltpu.VMEM((GROUPS, NSTATE, WIDE), F32),
            pltpu.VMEM((GROUPS, 8, WIDE), F32),
            pltpu.VMEM((GROUPS, NSTATE, WIDE), LOW),
            pltpu.VMEM((GROUPS + 1, EDGE, WIDE), F32),
            pltpu.VMEM((GROUPS + 2, EDGE, WIDE), F32),
            pltpu.VMEM((rows, WIDE), F32),
            pltpu.VMEM((rows, model), F32),
            sem(GROUPS + 1),
            sem(GROUPS + 1),
            sem(BLOCK_CUTS),
            sem(BLOCK_CUTS),
            sem(1),
        ]
        + Chaining.scratch(rounds)
        + Reducing.scratch(depth, own_rows, 2 * half_wide)
        + extra,
        compiler_params=params(collective_id=2, has_side_effects=True),
        name="scan_back",
    )(
        pre, dy, loc, carry, enter, cin, par, par_heads, state_filter, cin_state, pre_state, bc,
        bct, score, mask, sp, cumt, fac, match, zst, dt, exits, gate_part, block_own, tokens, cot,
        hidden_t, gpg, parts, parts, small, gate_row, skip_row,
    )


def pack_body(
    entry, exits, state, steps, gain, inner_kernel, gate_gain, bias, decay, skip, docs,
    tail_tokens, packed_small, packed_parts, packed_exit, par, doc_col, doc_row, edge, docs_own
):
    half_of = side()
    rows = entry.shape[0]
    wide = entry.shape[2]

    def placed(filled, used):
        return jnp.where(half_of == 0, filled, pltpu.roll(filled, used, 1))

    def widened(value):
        return jnp.concatenate(
            [value, jnp.zeros((value.shape[0], LANES - value.shape[1]), F32)], axis=1
        )

    for part in range(3):
        at = slice(part * WIDE, (part + 1) * WIDE)
        packed_parts[part, :, :WIDE] = entry[:, 0, at].astype(LOW)
        packed_parts[part, :, WIDE:] = entry[:, 1, at].astype(LOW)
    half = jnp.where(half_of == 0, state[:, :NSTATE], state[:, NSTATE:])
    packed_small[:, :NSTATE] = half.astype(LOW)
    gain_row = jnp.concatenate([gain[...], jnp.zeros((1, LANES - rows), F32)], axis=1)
    gain_col = jnp.transpose(jnp.broadcast_to(gain_row, (LANES, LANES)))[:rows]
    lane = iota((rows, LANES), 1)
    heads_here = steps.shape[0]
    step_rows = jnp.concatenate([steps[...], jnp.zeros((heads_here, LANES - rows), F32)], axis=1)
    step_rows = jnp.concatenate([step_rows, jnp.zeros((LANES - heads_here, LANES), F32)], axis=0)
    step_cols = jnp.transpose(step_rows)[:rows]
    small = jnp.where(lane == 24, gain_col, placed(step_cols, heads_here))
    packed_small[:, NSTATE:] = small.astype(LOW)
    packed_exit[...] = exits[...].astype(LOW)
    par[0 : CONV + 1] = inner_kernel[...]
    for index in range(wide // LANES):
        at = slice(index * LANES, (index + 1) * LANES)
        par[CONV + 1 : CONV + 2, at] = gate_gain[index : index + 1]
    par[CONV + 2 : CONV + 4] = jnp.zeros((2, wide), F32)
    for index, ref in enumerate((bias, decay, skip)):
        par[CONV + 2 : CONV + 3, index * LANES : (index + 1) * LANES] = placed(
            widened(ref[...]), ref.shape[1]
        )
    own = jnp.where(half_of == 0, docs[0:1], docs[1:2]).astype(F32)
    doc_row[...] = jnp.broadcast_to(own, doc_row.shape)
    doc_col[...] = jnp.transpose(jnp.broadcast_to(own, (LANES, own.shape[1])))
    docs_own[...] = doc_col[own.shape[1] - HALO :]
    edge[...] = tail_tokens[0]


def pack_shapes(own_rows, wide, rows, model):
    shape = jax.ShapeDtypeStruct
    return (
        shape((own_rows, WIDE), LOW),
        shape((3, own_rows, 2 * WIDE), LOW),
        shape((own_rows, wide), LOW),
        shape((8, wide), F32),
        shape((rows, LANES), F32),
        shape((8, rows), F32),
        shape((HALO, model), LOW),
        shape((HALO, LANES), F32),
    )


def pack(arrays, tokens):
    own_rows, _, wide = arrays[0].shape
    rows, model = tokens.shape[1:]
    outs = pack_shapes(own_rows, wide, rows, model)
    return pl.pallas_call(
        pack_body,
        out_shape=outs,
        grid=(1,),
        in_specs=[fixed(array.shape) for array in arrays]
        + [pl.BlockSpec((1, HALO, model), lambda s: (side(), rows // HALO - 1, 0))],
        out_specs=[const(out.shape) for out in outs],
        compiler_params=params(),
        name="pack",
    )(*arrays, tokens)


def gather_body(
    depth, own_small, own_parts, own_exit, par_own, edge_own, docs_own, cot, small, parts, exits, par,
    heads, edge, docs, cot_t, docs_in, cot_in, side_send, side_land, local, *marks
):
    place = Place(depth)
    count = 2 * depth
    onward = {"context": lax.rem(place.position + 1, count)}
    behind = {"context": lax.rem(place.position + count - 1, count)}
    y = place.y
    place.greet([place.mate, place.x_peer, place.y_peer, onward, behind], (), True)
    own = [own_small, own_parts.at[0], own_parts.at[1], own_parts.at[2], own_exit]
    full = [small, parts.at[0], parts.at[1], parts.at[2], exits]
    pieces = [Gathering(place, own[i], full[i], *marks[3 * i : 3 * i + 3]) for i in range(5)]
    sides = [
        remote(edge_own, edge, side_send.at[0], side_land.at[0], onward),
        remote(docs_own, docs_in, side_send.at[1], side_land.at[1], onward),
        remote(par_own, par.at[y], side_send.at[2], side_land.at[2], place.y_peer),
    ]
    for copy in sides:
        copy.start()
    cot_copy = pltpu.make_async_copy(cot.at[y], cot_in, local.at[1])
    cot_copy.start()
    par_keep = pltpu.make_async_copy(par_own, par.at[y], local.at[0])
    par_keep.start()
    for piece in pieces:
        piece.own()
    cot_copy.wait()
    cot_t[...] = jnp.transpose(cot_in[...])
    for piece in pieces:
        piece.near()
        piece.across()
        piece.far()
    for copy in sides:
        copy.wait()
    docs[...] = jnp.where(place.position == 0, -1.0, docs_in[...])
    par_keep.wait()
    both = par[0, CONV + 2 : CONV + 3] + par[1, CONV + 2 : CONV + 3]
    heads[...] = jnp.zeros_like(heads)
    for index in range(3):
        heads[index : index + 1] = both[:, index * LANES : (index + 1) * LANES]
    for piece in pieces:
        piece.mates()
        piece.finish()


def gather(own_small, own_parts, own_exit, par_own, edge_own, docs_own, cot):
    count = lax.axis_size("context")
    depth = count // 2
    rows, model = cot.shape[1:]
    shape = jax.ShapeDtypeStruct
    full = lambda own: (2, 2, count) + own.shape[-2:]
    return pl.pallas_call(
        functools.partial(gather_body, depth),
        out_shape=(
            shape(full(own_small), LOW),
            shape((3,) + full(own_parts), LOW),
            shape(full(own_exit), LOW),
            shape((2,) + par_own.shape, F32),
            shape((8, LANES), F32),
            shape(edge_own.shape, LOW),
            shape(docs_own.shape, F32),
            shape((model, rows), LOW),
        ),
        in_specs=[VMEM_SPEC] * 6 + [ANY_SPEC],
        out_specs=[ANY_SPEC] * 3 + [VMEM_SPEC] * 5,
        scratch_shapes=[
            pltpu.VMEM(docs_own.shape, F32),
            pltpu.VMEM((rows, model), LOW),
            pltpu.SemaphoreType.DMA((3,)),
            pltpu.SemaphoreType.DMA((3,)),
            pltpu.SemaphoreType.DMA((2,)),
        ]
        + Gathering.scratch(depth) * 5,
        compiler_params=params(collective_id=0, has_side_effects=True),
        name="gather",
    )(own_small, own_parts, own_exit, par_own, edge_own, docs_own, cot)


def reduce_body(
    depth, inner, small, token, taps, taps_state, gate_row, head_rows, skip_row, norm_row, mine,
    state_out, vector_out, token_out, *scratch
):
    place = Place(depth)
    wide = inner.shape[-1]
    parts = [(inner, slice(0, wide)), (small, slice(wide, wide + WIDE))]
    reducing = Reducing(place, 0, parts, mine, scratch[:8], scratch[8:17])
    closing = Closing(place, token, token_out, scratch[17:])
    vec = closing.send
    vec[0] = jnp.zeros(vec.shape[1:], F32)
    vec[0, : CONV + 1, : 2 * wide] = taps[: CONV + 1]
    vec[0, : CONV + 1, 2 * wide :] = taps_state[: CONV + 1]
    vec[0, 5:6, : 2 * wide] = gate_row[0:1]
    vec[0, 5:6, 2 * wide : 2 * wide + LANES] = head_rows[0:1]
    vec[0, 5:6, 2 * wide + LANES :] = skip_row[0:1]
    model = norm_row.shape[1]
    vec[0, 6:7, :model] = norm_row[0:1]
    vec[0, 6:7, model : model + LANES] = head_rows[1:2]
    place.greet([place.mate, place.x_peer, place.y_peer], (), True)
    each(depth, reducing.start)
    closing.run(reducing, NSTATE, state_out, vector_out, wide)


def reduce_all(inner, small, token, taps, taps_state, gate_row, head_rows, skip_row, norm_row):
    depth = lax.axis_size("context") // 2
    own_rows, wide = inner.shape[3:]
    tall = wide + WIDE
    shape = jax.ShapeDtypeStruct
    vector = (8, 2 * wide + WIDE)
    return pl.pallas_call(
        functools.partial(reduce_body, depth),
        out_shape=(
            shape((own_rows, tall), F32),
            shape((2, own_rows, NSTATE), F32),
            shape(vector, F32),
            shape((2,) + token.shape, LOW),
        ),
        in_specs=[ANY_SPEC] * 2 + [VMEM_SPEC] * 7,
        out_specs=[VMEM_SPEC] * 3 + [ANY_SPEC],
        scratch_shapes=Reducing.scratch(depth, own_rows, tall)
        + Closing.scratch(depth, own_rows, vector),
        compiler_params=params(collective_id=4, has_side_effects=True),
        name="reduce_all",
    )(inner, small, token, taps, taps_state, gate_row, head_rows, skip_row, norm_row)


def finish_body(
    mine, mine_last, exits, state, vector, token, block, block_out, token_out,
    norm_out, entry_out, state_out, step_out, kernel_out, filter_out, bias_out, decay_out, skip_out,
    gate_out, exit_out
):
    half_of = side()
    spot = lax.axis_index("dp") * lax.axis_size("context") + lax.axis_index("context")
    token_out[...] = token[...].astype(F32)
    first = half_of == 0
    block_out[...] = block[...]

    @pl.when(pl.program_id(0) == 0)
    def _():
        own_rows, _, wide = entry_out.shape
        model = token.shape[2]
        entry_out[:, 0] = exits[:, wide:]
        entry_out[:, 1, : 2 * WIDE] = mine[...]
        entry_out[:, 1, 2 * WIDE :] = mine_last[:, :WIDE]
        exit_out[...] = exits[:, :wide]
        state_out[:, :NSTATE] = state[0]
        state_out[:, NSTATE:] = state[1]

        def twelve(value):
            return jnp.where(first, value, pltpu.roll(value, LANES - 12, 1))[:, :12]

        steps = jnp.where(first, mine_last[:, WIDE + NSTATE :], pltpu.roll(mine_last[:, WIDE + NSTATE :], LANES - 12, 1))
        steps = jnp.concatenate([steps, jnp.zeros((LANES - own_rows, LANES), F32)], axis=0)
        step_out[...] = jnp.transpose(steps)[:12, :own_rows]
        left, right = vector[:, :wide], vector[:, wide : 2 * wide]
        halves = jnp.where(first, left, right)
        kernel_out[...] = halves[: CONV + 1]
        for index in range(wide // LANES):
            gate_out[index : index + 1] = halves[5:6, index * LANES : (index + 1) * LANES]
        filter_out[...] = vector[: CONV + 1, 2 * wide :]
        bias_out[...] = twelve(vector[5:6, 2 * wide : 2 * wide + LANES])
        skip_out[...] = twelve(vector[5:6, 2 * wide + LANES :])
        decay_out[...] = twelve(vector[6:7, model : model + LANES])
        turned = pltpu.roll(vector[:, :model], lax.rem(model - spot * own_rows, model), 1)
        norm_out[...] = turned[6:7, :own_rows]


def finish(mine, mine_last, exits, state, vector, token, block):
    own_rows, wide = exits.shape[0], exits.shape[1] // 2
    _, rows, model = token.shape
    share = rows // 2
    shape = jax.ShapeDtypeStruct
    outs = (
        (shape((2, rows, model), LOW), pl.BlockSpec((2, share, model), lambda s: (0, s, 0))),
        (shape((2, rows, model), F32), pl.BlockSpec((2, share, model), lambda s: (0, s, 0))),
        (shape((1, own_rows), F32), None),
        (shape((own_rows, 2, wide), F32), None),
        (shape((own_rows, WIDE), F32), None),
        (shape((12, own_rows), F32), None),
        (shape((CONV + 1, wide), F32), None),
        (shape((CONV + 1, WIDE), F32), None),
        (shape((1, 12), F32), None),
        (shape((1, 12), F32), None),
        (shape((1, 12), F32), None),
        (shape((wide // LANES, LANES), F32), None),
        (shape((own_rows, wide), F32), None),
    )
    return pl.pallas_call(
        finish_body,
        out_shape=[out[0] for out in outs],
        grid=(2,),
        in_specs=[
            fixed(mine.shape),
            fixed(mine_last.shape),
            fixed(exits.shape),
            fixed(state.shape),
            fixed(vector.shape),
            pl.BlockSpec((2, share, model), lambda s: (0, s, 0)),
            pl.BlockSpec((2, share, model), lambda s: (0, s, 0)),
        ],
        out_specs=[out[1] if out[1] is not None else const(out[0].shape) for out in outs],
        compiler_params=params(),
        name="finish",
    )(mine, mine_last, exits, state, vector, token, block)


def body(
    tokens, documents, norm_gain, entry_weight, state_weight, step_weight, inner_kernel,
    state_filter, step_bias, decay_log, skip_gain, gate_gain, exit_weight, cotangent,
):
    seqs, rows, model = tokens.shape
    count = lax.axis_size("context")
    own_rows = norm_gain.shape[0]
    longest = rows * count // 4
    rounds = min(count // 2 - 1, -(-(longest - 1) // (2 * rows)))

    raw = (
        entry_weight, exit_weight, state_weight, step_weight.T, norm_gain[None], inner_kernel,
        gate_gain.reshape(-1, LANES), step_bias[None], decay_log[None], skip_gain[None], documents,
    )
    (
        hidden_t, cin, gate, pre, loc, carry, cin_state, pre_state, bc, bct, score, mask, zst, dt, sp,
        cumt, fac, match, local,
    ), (small, parts, exit_weights, par, par_heads, cot_t) = entry(
        tokens, raw, state_filter, cotangent, rounds
    )
    block_own, exit_part, gate_part, dy, gpg, enter, gate_row, skip_row = middle(
        tokens, cotangent, cot_t, hidden_t, pre, gate, loc, local, carry, exit_weights, par, bc, bct,
        sp, fac,
    )
    cut = lambda v: v.reshape(2, 2, count, own_rows, v.shape[-1])
    exit_mine, block_both, *others = scan_back(
        pre, dy, loc, carry, enter, cin, par, par_heads, state_filter, cin_state, pre_state, bc, bct,
        score, mask, sp, cumt, fac, match, zst, dt, cut(exit_part), cut(gate_part), block_own,
        tokens, cotangent, hidden_t, gpg, parts, small, gate_row, skip_row, rounds,
    )
    if len(others) == 5:
        mine, mine_last, state_both, vector, token_both = others
    else:
        taps, taps_state, head_rows, inner_part, small_part, token_own, norm_row = others
        mine, state_both, vector, token_both = reduce_all(
            cut(inner_part), cut(small_part), token_own, taps, taps_state, gate_row, head_rows,
            skip_row, norm_row,
        )
        mine, mine_last = mine[:, : 2 * WIDE], mine[:, 2 * WIDE :]
    outs = list(finish(mine, mine_last, exit_mine, state_both, vector, token_both, block_both))
    for index in (2, 8, 9, 10):
        outs[index] = outs[index][0]
    outs[5] = outs[5].T
    outs[11] = outs[11].reshape(-1)
    return tuple(outs)


def solution(mesh):
    in_specs = (
        P("dp", "context", None),
        P("dp", "context"),
        P(("dp", "context")),
        P(("dp", "context"), None, "tensor"),
        P(("dp", "context"), None),
        P(("dp", "context"), "tensor"),
        P(None, "tensor"),
        P(),
        P("tensor"),
        P("tensor"),
        P("tensor"),
        P("tensor"),
        P(("dp", "context"), "tensor"),
        P("dp", "context", None),
    )
    out_specs = (
        P("dp", "context", None),
        P("dp", "context", None),
        P(("dp", "context")),
        P(("dp", "context"), None, "tensor"),
        P(("dp", "context"), None),
        P(("dp", "context"), "tensor"),
        P(None, "tensor"),
        P(),
        P("tensor"),
        P("tensor"),
        P("tensor"),
        P("tensor"),
        P(("dp", "context"), "tensor"),
    )
    return jax.shard_map(body, mesh=mesh, in_specs=in_specs, out_specs=out_specs, check_vma=False)
```

```python
import functools
import jax
import jax.numpy as jnp
from jax import lax
from jax.experimental import pallas as pl
from jax.experimental.pallas import tpu as pltpu
from jax.sharding import PartitionSpec as P

HEAD = 64
NSTATE = 128
CONV = 4
EPSILON = 1e-05
Q = 128
HALO = 16
EDGE = 8
GROUPS = 6
BLOCK_CUTS = 8
ORDER = (0, 3, 1, 4, 2, 5)
LANES = 128
WIDE = 256
LOG2E = 1.4426950408889634
FAR = -1e30
LOW = jnp.bfloat16
F32 = jnp.float32
VMEM_LIMIT = 60 * 1024 * 1024


def mm(a, b):
    return lax.dot_general(a, b, (((1,), (0,)), ((), ())), preferred_element_type=F32)


def mm_nt(a, b):
    return lax.dot_general(a, b, (((1,), (1,)), ((), ())), preferred_element_type=F32)


def mm_tn(a, b):
    return lax.dot_general(a, b, (((0,), (0,)), ((), ())), preferred_element_type=F32)


def mm_exact(a, b):
    return lax.dot_general(
        a, b, (((1,), (0,)), ((), ())), precision=lax.Precision.HIGHEST, preferred_element_type=F32
    )


def split3(v):
    high = v.astype(LOW).astype(F32)
    rest = v - high
    mid = rest.astype(LOW).astype(F32)
    low = rest - mid
    return (high + pltpu.roll(mid, 32, 1) + pltpu.roll(low, 64, 1)).astype(LOW)


def iota(shape, dim):
    return lax.broadcasted_iota(jnp.int32, shape, dim)


def spreader(first_head, width, count):
    k = iota((LANES, width * count), 0)
    lane = iota((LANES, width * count), 1)
    hit = ((k & 31) == first_head + lane // width) & (k < 96)
    return hit.astype(F32).astype(LOW)


def gatherer(first_head, width, count):
    lane = iota((width * count, LANES), 0)
    k = iota((width * count, LANES), 1)
    return (k == first_head + lane // width).astype(F32).astype(LOW)


def head_sums(v, collect):
    high = v.astype(LOW)
    rest = (v - high.astype(F32)).astype(LOW)
    return mm(high, collect) + mm(rest, collect)


def sigmoid(v):
    return 1.0 / (1.0 + jnp.exp(-v))


def twice(v):
    return jnp.concatenate([v, v], axis=1)


def conv_forward(cin, taps, masks):
    rows = cin.shape[0] - HALO
    out = taps[CONV : CONV + 1] + taps[CONV - 1 : CONV] * cin[HALO:]
    for back in range(1, CONV):
        part = cin[HALO - back : HALO - back + rows]
        out = out + taps[CONV - 1 - back : CONV - back] * (part * twice(masks[back - 1]))
    return out


def conv_backward(pg, cin, taps, masks):
    rows, width = pg.shape
    sums = [None] * (CONV + 1)
    sums[CONV] = jnp.sum(pg, axis=0, keepdims=True)
    sums[CONV - 1] = jnp.sum(pg * cin[HALO:], axis=0, keepdims=True)
    pad = jnp.zeros((HALO, width), F32)
    grad = jnp.concatenate([pad, pg * taps[CONV - 1 : CONV]], axis=0)
    for back in range(1, CONV):
        padded = jnp.concatenate([pad, pg * twice(masks[back - 1]), pad], axis=0)
        moved = padded[back : back + rows + HALO]
        sums[CONV - 1 - back] = jnp.sum(moved * cin, axis=0, keepdims=True)
        grad = grad + moved * taps[CONV - 1 - back : CONV - back]
    return sums, grad


def const(shape):
    zeros = (0,) * len(shape)
    return pl.BlockSpec(shape, lambda *_: zeros)


def fixed(shape):
    zeros = (0,) * len(shape)
    return pl.BlockSpec(shape, lambda *_: zeros, pipeline_mode=pl.Buffered(1))


def params(**extra):
    return pltpu.CompilerParams(vmem_limit_bytes=VMEM_LIMIT, **extra)


VMEM_SPEC = pl.BlockSpec(memory_space=pltpu.VMEM)
ANY_SPEC = pl.BlockSpec(memory_space=pl.ANY)


def side():
    return lax.axis_index("tensor")


def remote(src, dst, send_sem, recv_sem, target):
    return pltpu.make_async_remote_copy(
        src_ref=src,
        dst_ref=dst,
        send_sem=send_sem,
        recv_sem=recv_sem,
        device_id=target,
        device_id_type=pl.DeviceIdType.MESH,
    )


def each(count, run, first=0):
    def one(step, carry):
        run(step)
        return carry

    lax.fori_loop(first, count, one, 0)


class Place:
    def __init__(self, depth):
        position = lax.axis_index("context")
        self.depth = depth
        self.position = position
        self.x, self.y = lax.axis_index("dp"), lax.axis_index("tensor")
        self.z, self.c = position // 2, position % 2
        self.mate = self.at(self.x, self.y, self.z, 1 - self.c)
        self.x_peer = self.at(1 - self.x, self.y, self.z, self.c)
        self.y_peer = self.at(self.x, 1 - self.y, self.z, self.c)

    def at(self, x, y, z, c):
        return {"dp": x, "context": z * 2 + c, "tensor": y}

    def away(self, z):
        return self.at(self.x, self.y, z, self.c)

    def axes(self, turned):
        x, y, z, c = self.x, self.y, self.z, self.c
        x1, y1 = x + (1 - turned) * (1 - 2 * x), y + turned * (1 - 2 * y)
        x2, y2 = x + turned * (1 - 2 * x), y + (1 - turned) * (1 - 2 * y)
        return (x1, y1), (x2, y2)

    def around(self, run, first=0, last=None):
        z, depth = self.z, self.depth
        if first == 0:
            run(z)

        def step(away):
            @pl.when(z - away >= 0)
            def _():
                run(z - away)

            @pl.when(z + away < depth)
            def _():
                run(z + away)

        each(depth if last is None else last, step, max(first, 1))

    def greet(self, always, sometimes=(), column=False):
        barrier = pltpu.get_barrier_semaphore()
        kind = pl.DeviceIdType.MESH
        total = len(always)
        for target in always:
            pl.semaphore_signal(barrier, inc=1, device_id=target, device_id_type=kind)
        for holds, target in sometimes:

            @pl.when(holds)
            def _():
                pl.semaphore_signal(barrier, inc=1, device_id=target, device_id_type=kind)

            total = total + holds.astype(jnp.int32)
        if column:
            for_all = lambda step: pl.semaphore_signal(
                barrier,
                inc=1,
                device_id=self.away(lax.rem(self.z + step, self.depth)),
                device_id_type=kind,
            )
            each(self.depth, for_all, 1)
            total = total + (self.depth - 1)
        pl.semaphore_wait(barrier, total)


class Gathering:
    def __init__(self, place, own, full, sends, lands, local):
        self.place, self.own_ref, self.full = place, own, full
        self.sends, self.lands, self.local = sends, lands, local
        self.starts = [first * place.depth for first in (0, 4, 5, 7)]
        (self.x1, self.y1), (self.x2, self.y2) = place.axes(place.c)
        self.first = place.at(self.x1, self.y1, place.z, place.c)
        self.second = place.at(self.x2, self.y2, place.z, place.c)

    @staticmethod
    def scratch(depth):
        sem = pltpu.SemaphoreType.DMA
        return [sem((8 * depth,)), sem((8 * depth,)), sem((1,))]

    def copy(self, kind, index, x, y, z, c, target, own=False):
        chunk = self.full.at[y, x, z * 2 + c]
        mark = ((y * 2 + x) * self.place.depth + z) * 2 + c
        return remote(
            self.own_ref if own else chunk, chunk, self.sends.at[self.starts[kind] + index],
            self.lands.at[mark], target,
        )

    def arrive(self, x, y, z, c):
        self.copy(0, 0, x, y, z, c, self.place.mate).wait_recv()

    def kept(self):
        p = self.place
        return pltpu.make_async_copy(
            self.own_ref, self.full.at[p.y, p.x, p.z * 2 + p.c], self.local.at[0]
        )

    def own(self):
        p = self.place
        mine = (p.x, p.y, p.z, p.c)

        def far_z(z):
            self.copy(3, z, *mine, p.away(z), True).start()

        p.around(far_z, 1)
        self.copy(1, p.z, *mine, self.first, True).start()
        self.copy(2, p.z, *mine, self.second, True).start()
        self.copy(0, p.z, *mine, p.mate, True).start()
        self.kept().start()

    def near(self, first=1, last=None):
        p = self.place

        def run(z):
            chunk = (p.x, p.y, z, p.c)
            self.arrive(*chunk)

            self.copy(1, z, *chunk, self.first).start()
            self.copy(2, z, *chunk, self.second).start()
            self.copy(0, z, *chunk, p.mate).start()

        p.around(run, first, last)

    def across(self):
        p = self.place

        def run(z):
            chunk = (self.x1, self.y1, z, p.c)
            self.arrive(*chunk)
            self.copy(2, p.depth + z, *chunk, self.second).start()
            self.copy(0, p.depth + z, *chunk, p.mate).start()

        p.around(run)

    def far(self):
        p = self.place

        def near_row(z):
            self.arrive(self.x2, self.y2, z, p.c)
            self.copy(0, 2 * p.depth + z, self.x2, self.y2, z, p.c, p.mate).start()

        def far_row(z):
            self.arrive(1 - p.x, 1 - p.y, z, p.c)
            self.copy(0, 3 * p.depth + z, 1 - p.x, 1 - p.y, z, p.c, p.mate).start()

        p.around(near_row)
        p.around(far_row)

    def mates(self):
        p = self.place

        def from_mate(z):
            for y in range(2):
                for x in range(2):
                    self.arrive(x, y, z, 1 - p.c)

        each(p.depth, from_mate)
        self.kept().wait()

    def finish(self):
        p = self.place

        def sent(kind, index, target):
            self.copy(kind, index, p.x, p.y, p.z, p.c, target).wait_send()

        each(4 * p.depth, lambda step: sent(0, step, p.mate))
        each(p.depth, lambda step: sent(1, step, p.mate))
        each(2 * p.depth, lambda step: sent(2, step, p.mate))

        p.around(lambda z: sent(3, z, p.mate), 1)


class Reducing:
    def __init__(self, place, turned, parts, total, bufs, sems):
        self.place, self.parts, self.total = place, parts, total
        self.own, self.core, self.send1, self.land1 = bufs[:4]
        self.send2, self.land2, self.send3, self.land3 = bufs[4:]
        self.own_sem, self.core_send, self.core_land = sems[:3]
        self.s1, self.l1, self.s2, self.l2, self.s3, self.l3 = sems[3:]
        self.turned = turned
        (x1, y1), (x2, y2) = place.axes(turned)
        self.first = place.at(x1, y1, place.z, place.c)
        self.second = place.at(x2, y2, place.z, place.c)
        self.mine = place.y + turned * (place.x - place.y)

    @staticmethod
    def scratch(depth, rows, tall):
        buffer = lambda *lead: pltpu.VMEM(lead + (rows, tall), LOW)
        sem = lambda *lead: pltpu.SemaphoreType.DMA(lead)
        bufs = [
            buffer(2, 2, depth), buffer(2, 2, depth), buffer(depth, 2), buffer(depth, 2),
            buffer(depth), buffer(depth), buffer(depth), buffer(depth),
        ]
        return bufs + [sem(2, 2, depth)] * 3 + [sem(depth)] * 6

    def spot(self, step):
        return lax.rem(self.place.z + 1 + step, self.place.depth)

    def whole(self, y, x, z):
        return remote(
            self.core.at[y, x, z], self.core.at[y, x, z], self.core_send.at[y, x, z],
            self.core_land.at[y, x, z], self.place.mate,
        )

    def own_whole(self, y, x, z):
        return pltpu.make_async_copy(
            self.own.at[y, x, z], self.own.at[y, x, z], self.own_sem.at[y, x, z]
        )

    def start(self, step):
        p = self.place
        z = self.spot(step)
        for y in range(2):
            for x in range(2):
                for ref, cols in self.parts:
                    remote(
                        ref.at[y, x, z * 2 + 1 - p.c], self.core.at[y, x, z, :, cols],
                        self.core_send.at[y, x, z], self.core_land.at[y, x, z], p.mate,
                    ).start()
                    pltpu.make_async_copy(
                        ref.at[y, x, z * 2 + p.c], self.own.at[y, x, z, :, cols],
                        self.own_sem.at[y, x, z],
                    ).start()

    def base(self, y, x, z):
        return self.own[y, x, z].astype(F32) + self.core[y, x, z].astype(F32)

    def copy1(self, z):
        return remote(
            self.send1.at[z], self.land1.at[z], self.s1.at[z], self.l1.at[z], self.first
        )

    def copy2(self, z):
        return remote(
            self.send2.at[z], self.land2.at[z], self.s2.at[z], self.l2.at[z], self.second
        )

    def copy3(self, z, lands_at):
        return remote(
            self.send3.at[z], self.land3.at[lands_at], self.s3.at[z], self.l3.at[lands_at],
            self.place.away(z),
        )

    def stage1(self, step):
        p, turned = self.place, self.turned
        z = self.spot(step)
        for y in range(2):
            for x in range(2):
                self.whole(y, x, z).wait_recv()
                self.own_whole(y, x, z).wait()
        for index in range(2):
            x = (1 - turned) * (1 - p.x) + turned * index
            y = turned * (1 - p.y) + (1 - turned) * index
            self.send1[z, index] = self.base(y, x, z).astype(LOW)
        self.copy1(z).start()

    def stage2(self, step):
        p, turned = self.place, self.turned
        z = self.spot(step)
        self.copy1(z).wait_recv()
        other = 1 - self.mine
        x = (1 - turned) * p.x + turned * other
        y = turned * p.y + (1 - turned) * other
        self.send2[z] = (self.base(y, x, z) + self.land1[z, other].astype(F32)).astype(LOW)
        self.copy2(z).start()

    def final(self, z):
        p = self.place
        self.copy2(z).wait_recv()
        return (
            self.base(p.y, p.x, z)
            + self.land1[z, self.mine].astype(F32)
            + self.land2[z].astype(F32)
        )

    def stage3(self, step):
        z = self.spot(step)
        self.send3[z] = self.final(z).astype(LOW)
        self.copy3(z, self.place.z).start()

    def turn(self, step):
        depth = self.place.depth

        @pl.when(step < depth)
        def _():
            self.stage1(step)

        @pl.when((step >= 1) & (step <= depth))
        def _():
            self.stage2(step - 1)

        @pl.when((step >= 2) & (step <= depth))
        def _():
            self.stage3(step - 2)

    def close(self):
        p = self.place
        self.total[...] = self.final(p.z)

        def add(step):
            z = lax.rem(p.z + step, p.depth)
            self.copy3(z, z).wait_recv()
            self.total[...] += self.land3[z].astype(F32)

        each(p.depth, add, 1)

    def finish(self):
        p = self.place

        def sent(z):
            for y in range(2):
                for x in range(2):
                    self.whole(y, x, z).wait_send()
            self.copy1(z).wait_send()
            self.copy2(z).wait_send()

        each(p.depth, sent)
        each(p.depth, lambda step: self.copy3(lax.rem(p.z + step, p.depth), p.z).wait_send(), 1)


class Chaining:
    def __init__(self, place, rounds, backward, fold, gain, bufs, sems):
        self.place, self.rounds = place, rounds
        self.fold, self.gain = fold, gain
        self.from_mate, self.from_chip, self.to_mate, self.to_chip = bufs
        self.mate_send, self.mate_land, self.chip_send, self.chip_land = sems
        first = 1 if backward else 0
        by = -1 if backward else 1
        self.order = place.depth - 1 - place.z if backward else place.z
        self.leads = place.c == first
        self.after = place.at(place.x, place.y, place.z + by, first)
        self.before = place.at(place.x, place.y, place.z - by, 1 - first)
        self.linked_before = self.leads & (self.order > 0)
        self.linked_after = jnp.logical_not(self.leads) & (self.order < place.depth - 1)

    @staticmethod
    def scratch(rounds):
        slots = lambda turns: pltpu.VMEM((turns, GROUPS, NSTATE, WIDE), LOW)
        marks = lambda turns: pltpu.SemaphoreType.DMA((turns, GROUPS))
        return [
            slots(rounds + 1), slots(rounds), slots(rounds + 1), slots(rounds),
            marks(rounds + 1), marks(rounds + 1), marks(rounds), marks(rounds),
        ]

    def sometimes(self):
        return [(self.linked_before, self.before), (self.linked_after, self.after)]

    def mate_copy(self, turn, cut):
        return remote(
            self.to_mate.at[turn, cut], self.from_mate.at[turn, cut], self.mate_send.at[turn, cut],
            self.mate_land.at[turn, cut], self.place.mate,
        )

    def chip_copy(self, turn, cut):
        return remote(
            self.to_chip.at[turn, cut], self.from_chip.at[turn, cut], self.chip_send.at[turn, cut],
            self.chip_land.at[turn, cut], self.after,
        )

    def joined(self, cut, arrived):
        return (self.fold[cut] + self.gain[cut, 0:1] * arrived.astype(F32)).astype(LOW)

    def open(self, cut):
        @pl.when(self.leads)
        def _():
            self.to_mate[0, cut] = self.fold[cut].astype(LOW)
            self.mate_copy(0, cut).start()

    def pass_on(self, turn, cut):
        @pl.when(jnp.logical_not(self.leads))
        def _():
            self.mate_copy(turn, cut).wait_recv()

        @pl.when(self.linked_after)
        def _():
            self.to_chip[turn, cut] = self.joined(cut, self.from_mate[turn, cut])
            self.chip_copy(turn, cut).start()

    def relay(self, turn, cut):
        @pl.when(self.linked_before)
        def _():
            self.chip_copy(turn, cut).wait_recv()
            self.to_mate[turn + 1, cut] = self.joined(cut, self.from_chip[turn, cut])
            self.mate_copy(turn + 1, cut).start()

        @pl.when(self.leads & (self.order == 0))
        def _():
            self.to_mate[turn + 1, cut] = self.fold[cut].astype(LOW)
            self.mate_copy(turn + 1, cut).start()

    def later(self):
        for turn in range(1, self.rounds):
            for cut in range(GROUPS):
                self.pass_on(turn, cut)
            for cut in range(GROUPS):
                self.relay(turn, cut)

    def arrive(self, put):
        last = self.rounds - 1

        @pl.when(self.linked_before)
        def _():
            for cut in range(GROUPS):
                put(cut, self.from_chip[last, cut])

        @pl.when(self.leads & (self.order == 0))
        def _():
            for cut in range(GROUPS):
                put(cut, jnp.zeros((NSTATE, WIDE), LOW))

        @pl.when(jnp.logical_not(self.leads))
        def _():
            for cut in range(GROUPS):
                self.mate_copy(self.rounds, cut).wait_recv()
                put(cut, self.from_mate[self.rounds, cut])

    def finish(self):
        @pl.when(self.leads)
        def _():
            for turn in range(self.rounds + 1):
                for cut in range(GROUPS):
                    self.mate_copy(turn, cut).wait_send()

        @pl.when(self.linked_after)
        def _():
            for turn in range(self.rounds):
                for cut in range(GROUPS):
                    self.chip_copy(turn, cut).wait_send()


class Closing:
    def __init__(self, place, token, token_out, refs):
        self.place, self.token, self.token_out = place, token, token_out
        self.state_own, self.state_in, self.send, self.land = refs[:4]
        self.vs, self.vl, self.ts, self.tl, self.ss, self.sl, self.keep_sem = refs[4:]
        self.targets = [place.mate, place.y_peer, place.x_peer]

    @staticmethod
    def scratch(depth, own_rows, vector):
        sem = lambda *lead: pltpu.SemaphoreType.DMA(lead)
        return [
            pltpu.VMEM((own_rows, NSTATE), F32),
            pltpu.VMEM((2, own_rows, NSTATE), F32),
            pltpu.VMEM((4,) + vector, F32),
            pltpu.VMEM((3 + depth,) + vector, F32),
            sem(3 + depth), sem(3 + depth), sem(depth), sem(depth), sem(1), sem(1), sem(1),
        ]

    def vec_copy(self, turn):
        return remote(
            self.send.at[turn], self.land.at[turn], self.vs.at[turn], self.vl.at[turn],
            self.targets[turn],
        )

    def vec_far(self, away, lands_at):
        return remote(
            self.send.at[3], self.land.at[3 + lands_at], self.vs.at[3 + away],
            self.vl.at[3 + lands_at], self.place.away(away),
        )

    def token_copy(self, step):
        p = self.place
        share = self.token.shape[0] // p.depth
        at = pl.ds(pl.multiple_of(step * share, share), share)
        return remote(
            self.token.at[at], self.token_out.at[p.y, at], self.ts.at[step], self.tl.at[step],
            p.y_peer,
        )

    def run(self, reducing, width, state_out, vector_out, first, pending=None):
        p = self.place
        depth, z = p.depth, p.z
        keep = pltpu.make_async_copy(self.token, self.token_out.at[p.y], self.keep_sem.at[0])
        keep.start()
        self.vec_copy(0).start()

        def step_all(step):
            if pending is not None:

                @pl.when(step + 3 <= depth)
                def _():
                    pending.turn(step + 3)

            reducing.turn(step)

            @pl.when(step < depth)
            def _():
                self.token_copy(step).start()

            for turn in range(3):

                @pl.when(step == turn)
                def _():
                    self.vec_copy(turn).wait_recv()
                    self.send[turn + 1] = self.send[turn] + self.land[turn]
                    if turn < 2:
                        self.vec_copy(turn + 1).start()
                    else:
                        each(depth, lambda s: self.vec_far(lax.rem(z + s, depth), z).start(), 1)
                        self.land[3 + z] = self.send[3]

        each(depth + 1, step_all)
        if pending is not None:
            pending.close()
        reducing.close()
        self.state_own[...] = reducing.total[:, first : first + width]
        state_copy = remote(
            self.state_own, self.state_in.at[p.y], self.ss.at[0], self.sl.at[0], p.y_peer
        )
        state_copy.start()
        self.state_in[p.y] = self.state_own[...]

        def vec_arrive(step):
            away = lax.rem(z + step, depth)
            self.vec_far(away, away).wait_recv()

        each(depth, vec_arrive, 1)
        vector_out[...] = self.land[3]

        def vec_add(step):
            vector_out[...] += self.land[3 + step]

        each(depth, vec_add, 1)
        for turn in range(3):
            self.vec_copy(turn).wait_send()
        each(depth, lambda s: self.vec_far(lax.rem(z + s, depth), z).wait_send(), 1)
        reducing.finish()
        each(depth, lambda step: self.token_copy(step).wait())
        state_copy.wait()
        state_out[...] = self.state_in[...]
        keep.wait()


def group_of(index):
    half, part = index % 2, index // 2
    return half * 3 + part, half, part


def turn_of(step):
    return group_of(jnp.maximum(step - 1, 0))


def entry_body(depth, rounds, fused, *refs):
    step = pl.program_id(0)
    tokens, state_filter = refs[:2]
    if fused:
        raw, cot = refs[2:13], refs[13]
        refs = refs[14:]
    else:
        doc_col, doc_row, w_gate, w_inner, w_small, par, heads_ref, edge, halo_docs = refs[2:11]
        refs = refs[11:]
    (
        hidden_out, cin_out, gate_out, pre_out, loc_out, carry_out, cin_state_out, pre_state_out,
        bc_out, bct_out, score_out, mask_out, zst_out, dt_out, sp_out, cumt_out, fac_out, match_out,
        local_out,
    ) = refs[:19]
    refs = refs[19:]
    if fused:
        small_out, parts_out, exit_out, par, heads_ref, cot_t = refs[:6]
        refs = refs[6:]
    hidden, normed, sp_tail, facs, folds, gains = refs[:6]
    rows, model = tokens.shape[1:]
    spans = rows // Q
    place = Place(depth)
    chaining = Chaining(place, rounds, False, folds, gains, refs[6:10], refs[10:14])
    group, half, part = turn_of(step)
    y = place.y
    if fused:
        v_small, v_parts, edge, halo_docs, docs_in, cot_in, par_in = refs[14:21]
        side_send, side_land, local, out_sem = refs[21:25]
        packed = refs[25:33]
        own_small, own_parts, own_exit, own_par, doc_col, doc_row, own_edge, own_docs = packed
        marks = refs[33:]
        own = [own_small, own_parts.at[0], own_parts.at[1], own_parts.at[2], own_exit]
        full = [v_small, v_parts.at[0], v_parts.at[1], v_parts.at[2], exit_out]
        pieces = [
            Gathering(place, own[i], full[i], *marks[3 * i : 3 * i + 3]) for i in range(5)
        ]
        stores = [pltpu.make_async_copy(v_small, small_out, out_sem.at[0])]
        for index in range(3):
            stores.append(
                pltpu.make_async_copy(
                    v_parts.at[index], parts_out.at[index], out_sem.at[index + 1]
                )
            )

    def before_weights():
        for ref, first, count in ((edge, 0, HALO), (tokens, HALO, rows)):
            value = (ref[...] if ref is edge else ref[0]).astype(F32)
            scale = lax.rsqrt(jnp.mean(value * value, axis=1, keepdims=True) + EPSILON)
            normed[first : first + count] = value * scale
        docs = jnp.concatenate([halo_docs[...], doc_col[...]], axis=0)
        for back in range(1, CONV):
            match = (docs[HALO - back : HALO - back + rows] == docs[HALO:]).astype(F32)
            match_out[back - 1] = match
        t_at, u_at = iota((Q, Q), 0), iota((Q, Q), 1)
        for index in range(spans):
            at = slice(index * Q, (index + 1) * Q)
            same = (t_at >= u_at) & (doc_col[at] == doc_row[0:1, at])
            mask_out[at] = jnp.where(same, 0.0, FAR)

    def after_weights(small):
        gain = jnp.transpose(small[0][:, LANES:].astype(F32))[24:25]
        hidden[...] = (normed[...] * gain).astype(LOW)
        hidden_out[...] = jnp.transpose(hidden[HALO:])
        both = [mm(hidden[...], small[index]) for index in range(2)]
        cin = jnp.concatenate([both[0][:, :LANES], both[1][:, :LANES]], axis=1).astype(LOW)
        cin_state_out[...] = cin
        docs = jnp.concatenate([halo_docs[...], doc_col[...]], axis=0)
        masks = [match_out[back] for back in range(CONV - 1)]
        pre = conv_forward(cin.astype(F32), state_filter[...], masks)
        pre_state_out[...] = pre
        mixed = (pre * sigmoid(pre)).astype(LOW)
        bc_out[...] = mixed
        turned = jnp.transpose(mixed.astype(F32)).astype(LOW)
        bct_out[...] = turned
        heads = heads_ref[...]
        used = iota((rows, LANES), 1) < 24
        raw = both[0][HALO:, LANES:] + both[1][HALO:, LANES:]
        zst = jnp.where(used, raw, 0.0) + heads[0:1]
        zst_out[...] = zst
        dt = jnp.where(used, jnp.maximum(zst, 0.0) + jnp.log1p(jnp.exp(-jnp.abs(zst))), 0.0)
        dt_out[...] = dt
        decay = -dt * jnp.exp(heads[1:2])
        t_at, u_at = iota((Q, Q), 0), iota((Q, Q), 1)
        lower = (t_at >= u_at).astype(F32)
        fac_rows = []
        for index in range(spans):
            at = slice(index * Q, (index + 1) * Q)
            cum = mm_exact(lower, decay[at])
            final = cum[Q - 1 : Q]
            before = docs[HALO + index * Q - 1 : HALO + index * Q]
            here = doc_col[at]
            last = here[Q - 1 : Q]
            opened = (here == before).astype(F32)
            tail = (here == last).astype(F32) * jnp.exp(final - cum)
            fac_rows.append((last == before).astype(F32) * jnp.exp(final))
            cum2 = cum * LOG2E
            turned_cum = jnp.transpose(cum2)
            for group in range(6):
                cumt_out[group, 0:4, at] = turned_cum[4 * group : 4 * group + 4]
            sp_out[0, at] = split3(dt[at])
            sp_out[1, at] = split3(cum2)
            lanes_used = iota((Q, LANES), 1) < 24
            sp_out[2, at] = split3(jnp.where(lanes_used, opened * jnp.exp(cum), 0.0))
            sp_out[3, at] = split3(jnp.where(lanes_used, tail, 0.0))
            sp_tail[at] = split3(jnp.where(lanes_used, tail * dt[at], 0.0))
            score_out[at] = mm_nt(mixed[at, LANES:], mixed[at, :LANES])
        gain_total = fac_rows[0]
        for row in fac_rows[1:]:
            gain_total = gain_total * row
        rows8 = jnp.concatenate(
            fac_rows + [gain_total] + [jnp.zeros((1, LANES), F32)] * (7 - spans), axis=0
        )
        rows8 = jnp.where(iota((8, LANES), 1) < 24, rows8, 0.0)
        fac_out[...] = rows8
        facs[...] = split3(rows8)

    if fused:

        @pl.when(step == 0)
        def _():
            count = 2 * depth
            onward = {"context": lax.rem(place.position + 1, count)}
            behind = {"context": lax.rem(place.position + count - 1, count)}
            pack_body(*raw, tokens.at[:, rows - HALO :], *packed)
            place.greet(
                [place.mate, place.x_peer, place.y_peer, onward, behind], chaining.sometimes(), True
            )
            sides = [
                remote(own_edge, edge, side_send.at[0], side_land.at[0], onward),
                remote(own_docs, docs_in, side_send.at[1], side_land.at[1], onward),
                remote(own_par, par_in.at[y], side_send.at[2], side_land.at[2], place.y_peer),
            ]
            for copy in sides:
                copy.start()
            for piece in pieces:
                piece.own()
            cot_copy = pltpu.make_async_copy(cot.at[y], cot_in, local.at[0])
            par_keep = pltpu.make_async_copy(own_par, par_in.at[y], local.at[1])
            cot_copy.start()
            par_keep.start()
            for copy in sides:
                copy.wait()
            par_keep.wait()
            pieces[0].near()
            pieces[1].near()
            halo_docs[...] = jnp.where(place.position == 0, -1.0, docs_in[...])
            par[...] = par_in[...]
            both = par[0, CONV + 2 : CONV + 3] + par[1, CONV + 2 : CONV + 3]
            heads_ref[...] = jnp.zeros_like(heads_ref)
            for index in range(3):
                heads_ref[index : index + 1] = both[:, index * LANES : (index + 1) * LANES]
            before_weights()
            pieces[0].across()
            pieces[2].near()
            pieces[1].across()
            pieces[0].far()
            cot_copy.wait()
            cot_t[...] = jnp.transpose(cot_in[...])
            pieces[0].mates()
            stores[0].start()
            after_weights([v_small[index].reshape(model, WIDE) for index in range(2)])

        @pl.when(step == 1)
        def _():
            pieces[3].near()
            pieces[2].across()
            pieces[1].far()
            pieces[1].mates()
            stores[1].start()

        @pl.when(step == 2)
        def _():
            pieces[4].near()

        @pl.when(step == 3)
        def _():
            pieces[3].across()
            pieces[2].far()
            pieces[2].mates()
            stores[2].start()

        @pl.when(step == 4)
        def _():
            pieces[4].across()

        @pl.when(step == 5)
        def _():
            pieces[3].far()
            pieces[3].mates()
            stores[3].start()

        @pl.when(step == 6)
        def _():
            pieces[4].far()

    else:

        @pl.when(step == 0)
        def _():
            place.greet([place.mate], chaining.sometimes())
            before_weights()
            after_weights([w_small[index] for index in range(2)])

    for cut in range(GROUPS - 1):

        @pl.when(step == cut + 2)
        def _():
            chaining.pass_on(0, cut)

    for cut in range(GROUPS - 3):

        @pl.when(step == cut + 4)
        def _():
            chaining.relay(0, cut)

    @pl.when(step > 0)
    def _():
        if fused:
            gate_low = v_parts[part, half, :, :, :, :WIDE].reshape(model, WIDE)
            inner_low = v_parts[part, half, :, :, :, WIDE:].reshape(model, WIDE)
        else:
            gate_low, inner_low = w_gate[0, 0], w_inner[0, 0]
        taps = par[half, :, pl.ds(pl.multiple_of(part * WIDE, WIDE), WIDE)]
        cin = mm(hidden[...], inner_low).astype(LOW)
        cin_out[...] = cin
        gate_out[...] = mm(hidden[HALO:], gate_low)
        masks = [match_out[back] for back in range(CONV - 1)]
        pre = conv_forward(cin.astype(F32), taps, masks)
        pre_out[...] = pre
        spread = spreader(4 * group, HEAD, 4)
        mix = pre * sigmoid(pre)
        value = (mix * mm(sp_tail[...], spread)).astype(LOW)
        facx = mm(facs[...], spread)
        cums = mm(sp_out[1], spreader(4 * group, LANES, 4))
        skipx = mm(split3(heads_ref[...]), spread)[2:3]
        stepped = mix * mm(sp_out[0], spread)
        first_half = iota((Q, LANES), 1) < HEAD
        fold = jnp.zeros((NSTATE, WIDE), F32)
        for index in range(spans):
            at = slice(index * Q, (index + 1) * Q)
            loc = mm(bct_out[:NSTATE, at], value[at])
            loc_out[at] = loc
            fold = facx[index : index + 1] * fold + loc
            parts = []
            for pair in range(2):
                lanes = slice(pair * LANES, (pair + 1) * LANES)
                weights, seen = [], []
                for head in (2 * pair, 2 * pair + 1):
                    across = cumt_out[group, head : head + 1, at]
                    spread_at = cums[at, head * LANES : (head + 1) * LANES] - across + mask_out[at]
                    weights.append((jnp.exp2(spread_at) * score_out[at]).astype(LOW))
                    keep = first_half if head % 2 == 0 else jnp.logical_not(first_half)
                    seen.append(jnp.where(keep, stepped[at, lanes], 0.0).astype(LOW))
                parts.append(mm(jnp.concatenate(weights, axis=1), jnp.concatenate(seen, axis=0)))
            local_out[at] = jnp.concatenate(parts, axis=1) + skipx * mix[at]
        folds[step - 1] = fold
        gains[step - 1] = jnp.broadcast_to(facx[spans : spans + 1], (8, WIDE))

    for cut in range(GROUPS):

        @pl.when(step == cut + 1)
        def _():
            chaining.open(cut)

    @pl.when(step == GROUPS)
    def _():
        chaining.pass_on(0, GROUPS - 1)
        for cut in range(GROUPS - 3, GROUPS):
            chaining.relay(0, cut)
        chaining.later()

        def put(cut, value):
            at = ORDER[cut] * WIDE
            carry_out[:, at : at + WIDE] = value

        chaining.arrive(put)
        if fused:
            pieces[4].mates()
            for piece in pieces:
                piece.finish()
            for store in stores:
                store.wait()
        chaining.finish()


def entry(tokens, raw, state_filter, cot, rounds):
    rows, model = tokens.shape[1:]
    own_small, own_parts, own_exit, own_par, doc_col, doc_row, own_edge, own_docs = pack_shapes(
        raw[0].shape[0], raw[0].shape[2], rows, model
    )
    count = lax.axis_size("context")
    depth = count // 2
    wide = GROUPS * WIDE
    ext = rows + HALO
    fused = own_small.shape[0] % 16 == 0
    shape = jax.ShapeDtypeStruct
    sem = lambda *lead: pltpu.SemaphoreType.DMA(lead)
    column = lambda count: pl.BlockSpec((count, WIDE), lambda s: (0, turn_of(s)[0]))
    whole = lambda *dims, dtype=F32: (shape(dims, dtype), const(dims))
    outs = [
        whole(model, rows, dtype=LOW),
        (shape((ext, wide), LOW), column(ext)),
        (shape((rows, wide), F32), column(rows)),
        (shape((rows, wide), F32), column(rows)),
        (shape((rows, wide), F32), column(rows)),
        whole(NSTATE, wide, dtype=LOW),
        whole(ext, WIDE, dtype=LOW),
        whole(rows, WIDE),
        whole(rows, WIDE, dtype=LOW),
        whole(WIDE, rows, dtype=LOW),
        whole(rows, Q),
        whole(rows, Q),
        whole(rows, LANES),
        whole(rows, LANES),
        whole(4, rows, LANES, dtype=LOW),
        whole(6, 8, rows),
        whole(8, LANES),
        whole(CONV - 1, rows, LANES),
        (shape((rows, wide), F32), column(rows)),
    ]
    scratch = [
        pltpu.VMEM((ext, model), LOW),
        pltpu.VMEM((ext, model), F32),
        pltpu.VMEM((rows, LANES), LOW),
        pltpu.VMEM((8, LANES), LOW),
        pltpu.VMEM((GROUPS, NSTATE, WIDE), F32),
        pltpu.VMEM((GROUPS, 8, WIDE), F32),
    ] + Chaining.scratch(rounds)
    in_specs = [
        pl.BlockSpec((1, rows, model), lambda s: (side(), 0, 0)),
        fixed((CONV + 1, WIDE)),
    ]
    args = [tokens, state_filter]
    full = lambda own: (2, 2, count) + own.shape[-2:]
    if fused:
        outs += [
            (shape(full(own_small), LOW), ANY_SPEC),
            (shape((3,) + full(own_parts), LOW), ANY_SPEC),
            (shape(full(own_exit), LOW), ANY_SPEC),
            (shape((2,) + own_par.shape, F32), VMEM_SPEC),
            (shape((8, LANES), F32), VMEM_SPEC),
            (shape((model, rows), LOW), VMEM_SPEC),
        ]
        scratch += [
            pltpu.VMEM(full(own_small), LOW),
            pltpu.VMEM((3,) + full(own_parts), LOW),
            pltpu.VMEM(own_edge.shape, LOW),
            pltpu.VMEM(own_docs.shape, F32),
            pltpu.VMEM(own_docs.shape, F32),
            pltpu.VMEM((rows, model), LOW),
            pltpu.VMEM((2,) + own_par.shape, F32),
            sem(3),
            sem(3),
            sem(2),
            sem(4),
        ]
        own = (own_small, own_parts, own_exit, own_par, doc_col, doc_row, own_edge, own_docs)
        scratch += [pltpu.VMEM(one.shape, one.dtype) for one in own] + Gathering.scratch(depth) * 5
        in_specs += [fixed(one.shape) for one in raw] + [ANY_SPEC]
        args += [*raw, cot]
    else:
        *packs, doc_col, doc_row, edge, docs = pack(raw, tokens)
        small, parts, exits, par, heads, edge, docs, cot_t = gather(*packs, edge, docs, cot)
        in_specs += [fixed((rows, LANES)), fixed((8, rows))]
        args += [doc_col, doc_row]
        weights = parts.reshape(3, 2, model, 2 * WIDE)
        block = lambda at: pl.BlockSpec(
            (1, 1, model, WIDE), lambda s: (turn_of(s)[2], turn_of(s)[1], 0, at)
        )
        in_specs += [block(0), block(1), fixed((2, model, WIDE))] + [VMEM_SPEC] * 4
        args += [weights, weights, small.reshape(2, model, WIDE), par, heads, edge, docs]
    results = pl.pallas_call(
        functools.partial(entry_body, depth, rounds, fused),
        out_shape=[out[0] for out in outs],
        grid=(GROUPS + 1,),
        in_specs=in_specs,
        out_specs=[out[1] for out in outs],
        scratch_shapes=scratch,
        compiler_params=params(collective_id=1, has_side_effects=True),
        name="entry",
    )(*args)
    if fused:
        small, parts, exits, par, heads, cot_t = results[19:]
    return tuple(results[:19]), (
        small.reshape(2, model, WIDE),
        parts.reshape(3, 2, model, 2 * WIDE),
        exits.reshape(2, model, -1),
        par,
        heads,
        cot_t,
    )


def middle_body(
    tokens_far, cot, cot_t_far, hidden_far, pre_ref, gate_ref, loc_ref, local_ref, carry_ref, w_exit,
    par, bc, bct, sp, fac, block_out, exit_out, gate_part_out, dy_out, gpg_out, enter_out, row_out,
    skip_out, outputs, gates, unit_grads, mixes, sums, total,
    tokens, cot_t, hidden_t, late_sem
):
    step = pl.program_id(0)
    rows = pre_ref.shape[0]
    spans = rows // Q
    wide = 6 * WIDE

    late = [
        pltpu.make_async_copy(src, dst, late_sem.at[index])
        for index, (src, dst) in enumerate(
            ((cot_t_far, cot_t), (hidden_far, hidden_t), (tokens_far.at[side()], tokens))
        )
    ]

    @pl.when(step == 0)
    def _():
        for copy in late:
            copy.start()
        sums[...] = jnp.zeros_like(sums)
        total[...] = jnp.zeros_like(total)
        skip_out[...] = jnp.zeros_like(skip_out)

    @pl.when(step < 6)
    def _():
        group = step
        spread = spreader(4 * group, HEAD, 4)
        pre = pre_ref[...]
        mix = pre * sigmoid(pre)
        mixes[group] = mix
        growth = mm(sp[2], spread)
        facx = mm(split3(fac[...]), spread)
        state = carry_ref[...].astype(F32)
        for index in range(spans):
            at = slice(index * Q, (index + 1) * Q)
            carried = mm(bc[at, LANES:], state.astype(LOW)) * growth[at]
            out = local_ref[at] + carried
            outputs[group, at] = out
            state = facx[index : index + 1] * state + loc_ref[at]
        gate = gate_ref[...]
        gates[group] = gate
        gated = outputs[group] * (gate * sigmoid(gate))
        unit_grad = mm(cot[0], w_exit[0])
        unit_grads[group] = unit_grad
        square = gated * gated
        cross = unit_grad * par[0, 5:6] * gated
        sums[0] += square[:, :LANES] + square[:, LANES:]
        sums[1] += cross[:, :LANES] + cross[:, LANES:]

    @pl.when(step == 5)
    def _():
        for copy in late:
            copy.wait()
        square = jnp.sum(sums[0], axis=1, keepdims=True)
        cross = jnp.sum(sums[1], axis=1, keepdims=True)
        normal = lax.rsqrt(square / wide + EPSILON)
        sums[0] = jnp.broadcast_to(normal, (rows, LANES))
        sums[1] = jnp.broadcast_to(normal * normal * normal * cross / wide, (rows, LANES))

    @pl.when(step >= 6)
    def _():
        group = step - 6
        spread = spreader(4 * group, HEAD, 4)
        normal = twice(sums[0])
        pull = twice(sums[1])
        gain = par[0, 5:6]
        gate = gates[group]
        out = outputs[group]
        unit_grad = unit_grads[group]
        sigma = sigmoid(gate)
        act = gate * sigma
        gated = out * act
        scaled_in = gated * normal
        unit = (scaled_in * gain).astype(LOW)
        total[...] += mm_nt(unit, w_exit[0])
        exit_out[0] = mm(cot_t[...], unit).astype(LOW)
        gate_sum = jnp.sum(unit_grad * scaled_in, axis=0, keepdims=True)
        gated_grad = normal * (unit_grad * gain) - pull * gated
        dy = gated_grad * act
        dy_out[...] = dy
        gate_grad = (gated_grad * out * sigma * (1.0 + gate * (1.0 - sigma))).astype(LOW)
        gpg_out[...] = gate_grad
        gate_part_out[0] = mm(hidden_t[...], gate_grad).astype(LOW)
        skip_sum = jnp.sum(dy * mixes[group], axis=0, keepdims=True)
        row_out[...] = jnp.broadcast_to(gate_sum, (8, WIDE))
        skip_out[...] += head_sums(
            jnp.broadcast_to(skip_sum, (8, WIDE)), gatherer(4 * group, HEAD, 4)
        )
        facx = mm(split3(fac[...]), spread)
        pushed = (dy * mm(sp[2], spread)).astype(LOW)
        enter = jnp.zeros((NSTATE, WIDE), F32)
        for index in reversed(range(spans)):
            at = slice(index * Q, (index + 1) * Q)
            enter = facx[index : index + 1] * enter + mm(bct[NSTATE:, at], pushed[at])
        enter_out[...] = enter

    @pl.when(step == 11)
    def _():
        block_out[...] = (tokens[...].astype(F32) + total[...]).astype(LOW)


def middle(
    tokens, cot, cot_t, hidden_t, pre, gate, loc, local, carry, weights, par, bc, bct, sp, fac
):
    rows, model = tokens.shape[1:]
    wide = 6 * WIDE
    shape = jax.ShapeDtypeStruct

    def early(s):
        return jnp.minimum(s, 5)

    def late(s):
        return jnp.maximum(s - 6, 0)

    def group(s):
        return s % 6

    outs = (
        (shape((rows, model), LOW), const((rows, model))),
        (
            shape((2, model, 3 * WIDE), LOW),
            pl.BlockSpec((1, model, WIDE), lambda s: (late(s) // 3, 0, late(s) % 3)),
        ),
        (
            shape((2, model, 3 * WIDE), LOW),
            pl.BlockSpec((1, model, WIDE), lambda s: (late(s) // 3, 0, late(s) % 3)),
        ),
        (shape((rows, wide), F32), pl.BlockSpec((rows, WIDE), lambda s: (0, late(s)))),
        (shape((rows, wide), LOW), pl.BlockSpec((rows, WIDE), lambda s: (0, late(s)))),
        (shape((NSTATE, wide), F32), pl.BlockSpec((NSTATE, WIDE), lambda s: (0, late(s)))),
        (shape((8, wide), F32), pl.BlockSpec((8, WIDE), lambda s: (0, late(s)))),
        (shape((8, LANES), F32), const((8, LANES))),
    )
    return pl.pallas_call(
        middle_body,
        out_shape=[out[0] for out in outs],
        grid=(12,),
        in_specs=[
                ANY_SPEC,
                pl.BlockSpec((1, rows, model), lambda s: (side(), 0, 0)),
                ANY_SPEC,
                ANY_SPEC,
                pl.BlockSpec((rows, WIDE), lambda s: (0, early(s))),
                pl.BlockSpec((rows, WIDE), lambda s: (0, early(s))),
                pl.BlockSpec((rows, WIDE), lambda s: (0, early(s))),
                pl.BlockSpec((rows, WIDE), lambda s: (0, early(s))),
                pl.BlockSpec((NSTATE, WIDE), lambda s: (0, early(s))),
                pl.BlockSpec((1, model, WIDE), lambda s: (group(s) // 3, 0, group(s) % 3)),
                pl.BlockSpec((1, 8, WIDE), lambda s: (group(s) // 3, 0, group(s) % 3)),
                fixed((rows, WIDE)),
                fixed((WIDE, rows)),
                fixed((4, rows, LANES)),
                fixed((8, LANES)),
        ],
        out_specs=[out[1] for out in outs],
        scratch_shapes=[
                pltpu.VMEM((6, rows, WIDE), F32),
                pltpu.VMEM((6, rows, WIDE), F32),
                pltpu.VMEM((6, rows, WIDE), F32),
                pltpu.VMEM((6, rows, WIDE), F32),
                pltpu.VMEM((2, rows, LANES), F32),
                pltpu.VMEM((rows, model), F32),
                pltpu.VMEM((rows, model), LOW),
                pltpu.VMEM((model, rows), LOW),
                pltpu.VMEM((model, rows), LOW),
                pltpu.SemaphoreType.DMA((3,)),
        ],
        compiler_params=params(),
        name="middle",
    )(tokens, cot, cot_t, hidden_t, pre, gate, loc, local, carry, weights, par, bc, bct, sp, fac)


def scan_back_body(depth, rounds, fused, *refs):
    (
        pre_ref, dy_ref, loc_ref, carry_ref, enter, cin_ref, par, par_heads, state_filter, cin_far,
        pre_far, bc, bct, score, mask, sp, cumt, fac, match_far, zst_far, dt_far, exits, gate_part,
        block_far, tokens_far, cot_far, hidden_far, gpg, w_gate, w_inner, small_far, gate_row,
        skip_row,
    ) = refs[:33]
    mine, block_out = refs[33:35]
    if fused:
        mine2, mine3, state_out, vector_out, token_both = refs[35:40]
        refs = refs[40:]
    else:
        tap_out, tap_state_out, small_out, inner_part, small_part, token_out, norm_out = refs[35:42]
        refs = refs[42:]
    block_own, hidden_t, match, tokens, cot, w_small, pre_state, cin_state, zst, dt_ref = refs[:10]
    late_sem = refs[10]
    refs = refs[11:]
    late = [
        pltpu.make_async_copy(src, dst, late_sem.at[index])
        for index, (src, dst) in enumerate(
            (
                (block_far, block_own), (hidden_far, hidden_t), (match_far, match),
                (tokens_far.at[side()], tokens), (cot_far.at[side()], cot), (small_far, w_small),
                (pre_far, pre_state), (cin_far, cin_state), (zst_far, zst), (dt_far, dt_ref),
            )
        )
    ]
    (
        d_bc, d_score, d_cum, heads, local_value, enters, gains, adjoints, edge_own, edge_in, grads,
        total, es, el, bs, bl, block_keep,
    ) = refs[:17]
    scratch = refs[17:42]
    step = pl.program_id(0)
    group, half_at, part_at = group_of(jnp.minimum(step, GROUPS - 1))
    last_group, last_half, last_part = group_of(jnp.maximum(step - 1, 0))
    blocks = BLOCK_CUTS
    rows = pre_ref.shape[0]
    spans = rows // Q
    place = Place(depth)
    wide = exits.shape[-1]
    chaining = Chaining(place, rounds, True, enters, gains, scratch[:4], scratch[4:8])
    reducing = Reducing(
        place, 0, [(exits, slice(0, wide)), (gate_part, slice(wide, 2 * wide))], mine,
        scratch[8:16], scratch[16:25],
    )
    if fused:
        inner_v, small_v, token_v, taps_v = refs[42:46]
        buffers = refs[46:]
        second = Reducing(
            place, 0, [(inner_v.at[0], slice(0, WIDE)), (inner_v.at[1], slice(WIDE, 2 * WIDE))],
            mine2, buffers[:8], buffers[8:17],
        )
        third = Reducing(
            place, 0, [(inner_v.at[2], slice(0, WIDE)), (small_v, slice(WIDE, 2 * WIDE))], mine3,
            buffers[17:25], buffers[25:34],
        )
        closing = Closing(place, token_v, token_both, buffers[34:])
    position = place.position
    has_before, has_after = position > 0, position < 2 * depth - 1
    before, after = {"context": position - 1}, {"context": position + 1}
    share = rows // blocks

    def block_copy(index):
        at = pl.ds(pl.multiple_of(index * share, share), share)
        return remote(
            block_own.at[at], block_out.at[place.y, at], bs.at[index], bl.at[index], place.y_peer
        )

    block_local = pltpu.make_async_copy(block_own, block_out.at[place.y], block_keep.at[0])

    def edge_copy(index):
        return remote(edge_own.at[index], edge_in.at[index], es.at[index], el.at[index], before)

    def edge_wait(index):
        @pl.when(has_after)
        def _():
            edge_copy(index).wait_recv()

    def put_inner(value):
        if fused:
            inner_v[last_part, last_half] = value.reshape(inner_v.shape[2:])
        else:
            inner_part[0] = value

    def joined(index):
        grad = grads[...]
        return jnp.concatenate(
            [grad[: rows - EDGE], grad[rows - EDGE :] + edge_in[index]], axis=0
        ).astype(LOW)

    @pl.when(step == 0)
    def _():
        for copy in late:
            copy.start()
        d_bc[...] = jnp.zeros_like(d_bc)
        d_score[...] = jnp.zeros_like(d_score)
        d_cum[...] = jnp.zeros_like(d_cum)
        heads[...] = jnp.zeros_like(heads)
        grads[...] = jnp.zeros_like(grads)
        total[...] = jnp.zeros_like(total)
        edge_in[GROUPS + 1] = jnp.zeros((EDGE, WIDE), F32)

        @pl.when(jnp.logical_not(has_after))
        def _():
            edge_in[...] = jnp.zeros_like(edge_in)

        place.greet(
            [place.mate, place.x_peer, place.y_peer],
            chaining.sometimes() + [(has_before, before), (has_after, after)],
            True,
        )
        facs = split3(fac[...])
        for cut in range(GROUPS):
            enters[cut] = enter[:, cut * WIDE : (cut + 1) * WIDE]
            chaining.open(cut)
        for cut in range(GROUPS):
            rows8 = mm(facs, spreader(4 * cut, HEAD, 4))
            gains[cut] = jnp.broadcast_to(rows8[spans : spans + 1], (8, WIDE))
        each(depth, reducing.start)
        late[0].wait()
        block_local.start()
        each(3, lambda index: block_copy(index).start())
        for cut in range(GROUPS):
            chaining.pass_on(0, cut)

    if fused:

        @pl.when(step == 5)
        def _():
            each(depth, second.start)

    @pl.when(step < GROUPS)
    def _():
        spread = spreader(4 * group, HEAD, 4)
        collect = gatherer(4 * group, HEAD, 4)
        pre = pre_ref[...]
        sigma = sigmoid(pre)
        mix = pre * sigma
        dtx = mm(sp[0], spread)
        growth = mm(sp[2], spread)
        facx = mm(split3(fac[...]), spread)
        cums = mm(sp[1], spreader(4 * group, LANES, 4))
        ones = jnp.ones((8, Q), F32).astype(LOW)
        states = [carry_ref[...].astype(F32)]
        for index in range(spans - 1):
            at = slice(index * Q, (index + 1) * Q)
            states.append(facx[index : index + 1] * states[-1] + loc_ref[at])
        for index in range(spans):
            at = slice(index * Q, (index + 1) * Q)
            dy = dy_ref[at]
            value = mix[at] * dtx[at]
            value_low = value.astype(LOW)
            lane = iota((Q, WIDE), 1) // HEAD
            dy_heads = [jnp.where(lane == head, dy, 0.0).astype(LOW) for head in range(4)]
            d_weight = mm_nt(jnp.concatenate(dy_heads, axis=0), value_low)
            parts = []
            sum_score = None
            row_sums = None
            for pair in range(2):
                lanes = slice(pair * LANES, (pair + 1) * LANES)
                moved, weights = [], []
                for head in (2 * pair, 2 * pair + 1):
                    across = cumt[group, head : head + 1, at]
                    spread_at = cums[at, head * LANES : (head + 1) * LANES] - across + mask[at]
                    decay = jnp.exp2(spread_at)
                    inner = decay * d_weight[head * Q : (head + 1) * Q]
                    sum_score = inner if sum_score is None else sum_score + inner
                    moved.append((inner * score[at]).astype(LOW))
                    weights.append((decay * score[at]).astype(LOW))
                both = jnp.concatenate(moved, axis=1)
                column_sums = mm(ones, both)
                for index_in in range(2):
                    head = 2 * pair + index_in
                    d_cum[group, head : head + 1, at] = -column_sums[
                        0:1, index_in * Q : (index_in + 1) * Q
                    ]
                part = mm(both, gatherer(4 * group + 2 * pair, LANES, 2))
                row_sums = part if row_sums is None else row_sums + part
                pushed_heads = [dy_heads[2 * pair][:, lanes], dy_heads[2 * pair + 1][:, lanes]]
                parts.append(
                    mm_tn(jnp.concatenate(weights, axis=0), jnp.concatenate(pushed_heads, axis=0))
                )
            d_score[at] += sum_score
            local_value[at] = jnp.concatenate(parts, axis=1)
            pushed = dy * growth[at]
            state_low = states[index].astype(LOW)
            carried = mm(bc[at, LANES:], state_low)
            d_bc[at, LANES:] += mm_nt(pushed.astype(LOW), state_low)
            heads[1, at] += head_sums(pushed * carried, collect) + row_sums

    @pl.when(step == 0)
    def _():
        for cut in range(GROUPS):
            chaining.relay(0, cut)
        chaining.later()

        def put(cut, value):
            adjoints[cut] = value

        chaining.arrive(put)
        chaining.finish()
        late[1].wait()
        late[2].wait()

    for turn in range(5):

        @pl.when(step == turn)
        def _():
            each(turn + 1 if turn < 4 else depth + 1, reducing.turn, turn)
            block_copy(turn + 3).start()

    @pl.when(step == 5)
    def _():
        reducing.close()
        if fused:
            second.turn(0)

    @pl.when((step > 0) & (step < GROUPS))
    def _():
        edge_wait(last_group)

    @pl.when(step < GROUPS)
    def _():
        spread = spreader(4 * group, HEAD, 4)
        collect = gatherer(4 * group, HEAD, 4)
        pre = pre_ref[...]
        sigma = sigmoid(pre)
        mix = pre * sigma
        dtx = mm(sp[0], spread)
        growth = mm(sp[2], spread)
        facx = mm(split3(fac[...]), spread)
        states = [carry_ref[...].astype(F32)]
        for index in range(spans - 1):
            at = slice(index * Q, (index + 1) * Q)
            states.append(facx[index : index + 1] * states[-1] + loc_ref[at])
        arrived = jnp.where(step > 0, last_group, GROUPS + 1)
        grad = joined(arrived)
        gate_grad = gpg[...]
        put_inner(mm(hidden_t[...], grad).astype(LOW))
        total[...] += mm_nt(gate_grad, w_gate[0, 0]) + mm_nt(grad, w_inner[0, 0])
        tails = mm(sp[3], spread)
        skipx = mm(split3(par_heads[...]), spread)[2:3]
        adjoint = adjoints[group].astype(F32)
        masks = [match[back] for back in range(CONV - 1)]
        pgs = [None] * spans
        for index in reversed(range(spans)):
            at = slice(index * Q, (index + 1) * Q)
            dy = dy_ref[at]
            value = mix[at] * dtx[at]
            adj_low = adjoint.astype(LOW)
            reached = mm(bc[at, :LANES], adj_low) * tails[at]
            d_bc[at, :LANES] += mm_nt((value * tails[at]).astype(LOW), adj_low)
            heads[0, at] += head_sums(value * reached, collect)
            fac_part = jnp.sum(adjoint * states[index], axis=0, keepdims=True)
            heads[3, index * 8 : index * 8 + 8] += head_sums(
                jnp.broadcast_to(fac_part, (8, WIDE)), collect
            )
            pushed_low = (dy * growth[at]).astype(LOW)
            adjoint = facx[index : index + 1] * adjoint + mm(bct[NSTATE:, at], pushed_low)
            d_value = local_value[at] + reached
            heads[2, at] += head_sums(mix[at] * d_value, collect)
            d_mix = dtx[at] * d_value + skipx * dy
            s = sigma[at]
            pgs[index] = d_mix * s * (1.0 + pre[at] * (1.0 - s))
        pg = jnp.concatenate(pgs, axis=0)
        sums, grad = conv_backward(pg, cin_ref[...].astype(F32), par[0], masks)
        taps8 = jnp.concatenate(sums + [jnp.zeros((3, WIDE), F32)], axis=0)
        if fused:
            taps_v[group] = taps8
        else:
            tap_out[...] = taps8
        grads[...] = grad[HALO:]
        edge_own[group] = grad[HALO - EDGE : HALO]

        @pl.when(has_before)
        def _():
            edge_copy(group).start()

    @pl.when(step == GROUPS)
    def _():
        for copy in late[3:]:
            copy.wait()
        if fused:
            second.turn(1)
        masks = [match[back] for back in range(CONV - 1)]
        edge_wait(GROUPS - 1)
        grad = joined(GROUPS - 1)
        put_inner(mm(hidden_t[...], grad).astype(LOW))
        total[...] += mm_nt(grad, w_inner[0, 0])
        t_at, u_at = iota((Q, Q), 0), iota((Q, Q), 1)
        onward = (t_at <= u_at).astype(F32)
        earlier = (t_at > u_at).astype(F32)
        rate = jnp.exp(par_heads[1:2])
        raws = []
        bias_sum = jnp.zeros((1, LANES), F32)
        decay_sum = jnp.zeros((1, LANES), F32)
        used = iota((Q, LANES), 1) < 24
        for index in range(spans):
            at = slice(index * Q, (index + 1) * Q)
            pieces = [d_cum[piece, 0:4, at] for piece in range(6)]
            pieces.append(jnp.zeros((LANES - 24, Q), F32))
            cum_col = jnp.transpose(jnp.concatenate(pieces, axis=0))
            fac_row = fac[index : index + 1] * heads[3, index * 8 : index * 8 + 1]
            d_decay = (
                mm_exact(onward, cum_col + heads[1, at]) + mm_exact(earlier, heads[0, at]) + fac_row
            )
            dt = dt_ref[at]
            raw = (heads[2, at] - d_decay * rate) * sigmoid(zst[at])
            raw = jnp.where(used, raw, 0.0)
            raws.append(raw.astype(LOW))
            bias_sum += jnp.sum(raw, axis=0, keepdims=True)
            decay_sum -= jnp.sum(
                jnp.where(used, d_decay * dt * rate, 0.0), axis=0, keepdims=True
            )
            score_low = d_score[at].astype(LOW)
            d_bc[at, :LANES] += mm_tn(score_low, bc[at, LANES:])
            d_bc[at, LANES:] += mm(score_low, bc[at, :LANES])
        if not fused:
            small_out[...] = jnp.concatenate(
                [bias_sum, decay_sum, jnp.zeros((6, LANES), F32)], axis=0
            )
        if fused:
            second.turn(2)
        pre = pre_state[...]
        s = sigmoid(pre)
        pg = d_bc[...] * s * (1.0 + pre * (1.0 - s))
        sums, grad = conv_backward(pg, cin_state[...].astype(F32), state_filter[...], masks)
        taps8 = jnp.concatenate(sums + [jnp.zeros((3, WIDE), F32)], axis=0)
        if fused:
            taps_v[GROUPS] = taps8
        else:
            tap_state_out[...] = taps8
        grads[...] = grad[HALO:]
        edge_own[GROUPS] = grad[HALO - EDGE : HALO]

        @pl.when(has_before)
        def _():
            edge_copy(GROUPS).start()

        steps = jnp.concatenate(raws, axis=0)
        turned = hidden_t[...]
        step_part = mm(turned, steps).astype(LOW)
        total[...] += mm_nt(steps, w_small[0, :, LANES:]) + mm_nt(steps, w_small[1, :, LANES:])
        edge_wait(GROUPS)
        state = joined(GROUPS)
        state_part = mm(turned, state).astype(LOW)
        for index in range(2):
            state_half = state_part[:, index * LANES : (index + 1) * LANES]
            value = jnp.concatenate([state_half, step_part], axis=1)
            if fused:
                small_v[index] = value.reshape(small_v.shape[1:])
            else:
                small_part[index] = value
        if fused:
            each(depth, third.start)
        value = tokens[...].astype(F32)
        scale = lax.rsqrt(jnp.mean(value * value, axis=1, keepdims=True) + EPSILON)
        hidden_grad = (
            total[...]
            + mm_nt(state[:, :LANES], w_small[0, :, :LANES])
            + mm_nt(state[:, LANES:], w_small[1, :, :LANES])
        )
        norm_sum = jnp.sum(hidden_grad * (value * scale), axis=0, keepdims=True)
        if not fused:
            norm_out[...] = jnp.broadcast_to(norm_sum, norm_out.shape)
        gain = jnp.transpose(w_small[0, :, LANES : 2 * LANES].astype(F32))[24:25]
        normed = hidden_grad * gain
        pull = jnp.sum(normed * value, axis=1, keepdims=True) / value.shape[1]
        token_low = (
            cot[...].astype(F32) + scale * normed - (scale * scale * scale) * value * pull
        ).astype(LOW)
        if fused:
            token_v[...] = token_low
            for index in range(GROUPS + 1):
                at = slice(index * WIDE, (index + 1) * WIDE)
                closing.send[0, : CONV + 1, at] = taps_v[index, : CONV + 1]
            high = GROUPS * WIDE
            closing.send[0, CONV + 1 :] = jnp.zeros((8 - CONV - 1, high + WIDE), F32)
            closing.send[0, 5:6, :high] = gate_row[0:1]
            closing.send[0, 5:6, high : high + LANES] = bias_sum
            closing.send[0, 5:6, high + LANES :] = skip_row[0:1]
            model = norm_sum.shape[1]
            closing.send[0, 6:7, :model] = norm_sum
            closing.send[0, 6:7, model : model + LANES] = decay_sum
            closing.run(third, NSTATE, state_out, vector_out, WIDE, second)
            second.finish()
        else:
            token_out[...] = token_low
        reducing.finish()
        each(blocks, lambda index: block_copy(index).wait())
        block_local.wait()

        @pl.when(has_before)
        def _():
            each(GROUPS + 1, lambda index: edge_copy(index).wait_send())


def scan_back(
    pre, dy, loc, carry, enter, cin, par, par_heads, state_filter, cin_state, pre_state, bc, bct,
    score, mask, sp, cumt, fac, match, zst, dt, exits, gate_part, block_own, tokens, cot, hidden_t,
    gpg, parts, small, gate_row, skip_row, rounds
):
    rows, wide = pre.shape
    ext = rows + HALO
    depth = lax.axis_size("context") // 2
    own_rows, half_wide = exits.shape[3:]
    shape = jax.ShapeDtypeStruct
    sem = lambda *lead: pltpu.SemaphoreType.DMA(lead)
    model = tokens.shape[2]
    count = 2 * depth
    fused = own_rows % 16 == 0
    now = lambda s: group_of(jnp.minimum(s, GROUPS - 1))
    lag = lambda s: group_of(jnp.maximum(s - 1, 0))
    column = lambda count: pl.BlockSpec((count, WIDE), lambda s: (0, now(s)[0]))
    whole = lambda *dims, dtype=F32: (shape(dims, dtype), const(dims))
    outs = [
        whole(own_rows, 2 * half_wide),
        (shape((2,) + block_own.shape, LOW), ANY_SPEC),
    ]
    if fused:
        outs += [
            whole(own_rows, 2 * WIDE),
            whole(own_rows, 2 * WIDE),
            whole(2, own_rows, NSTATE),
            whole(8, wide + WIDE),
            (shape((2, rows, model), LOW), ANY_SPEC),
        ]
        extra = (
            [
                pltpu.VMEM((3, 2, 2, count, own_rows, WIDE), LOW),
                pltpu.VMEM((2, 2, count, own_rows, WIDE), LOW),
                pltpu.VMEM((rows, model), LOW),
                pltpu.VMEM((GROUPS + 1, 8, WIDE), F32),
            ]
            + Reducing.scratch(depth, own_rows, 2 * WIDE) * 2
            + Closing.scratch(depth, own_rows, (8, wide + WIDE))
        )
    else:
        outs += [
            (shape((8, wide), F32), column(8)),
            whole(8, WIDE),
            whole(8, LANES),
            (
                shape((2, model, 3 * WIDE), LOW),
                pl.BlockSpec((1, model, WIDE), lambda s: (lag(s)[1], 0, lag(s)[2])),
            ),
            whole(2, model, WIDE, dtype=LOW),
            whole(rows, model, dtype=LOW),
            whole(8, model),
        ]
        extra = []
    return pl.pallas_call(
        functools.partial(scan_back_body, depth, rounds, fused),
        out_shape=[out[0] for out in outs],
        grid=(GROUPS + 1,),
        in_specs=[
            column(rows),
            column(rows),
            column(rows),
            column(NSTATE),
            fixed((NSTATE, wide)),
            column(ext),
            pl.BlockSpec((1, 8, WIDE), lambda s: (now(s)[1], 0, now(s)[2])),
            fixed((8, LANES)),
            fixed((CONV + 1, WIDE)),
            ANY_SPEC,
            ANY_SPEC,
            fixed((rows, WIDE)),
            fixed((WIDE, rows)),
            fixed((rows, Q)),
            fixed((rows, Q)),
            fixed((4, rows, LANES)),
            fixed((6, 8, rows)),
            fixed((8, LANES)),
            ANY_SPEC,
            ANY_SPEC,
            ANY_SPEC,
            ANY_SPEC,
            ANY_SPEC,
            ANY_SPEC,
            ANY_SPEC,
            ANY_SPEC,
            ANY_SPEC,
            column(rows),
            pl.BlockSpec((1, 1, model, WIDE), lambda s: (now(s)[2], now(s)[1], 0, 0)),
            pl.BlockSpec((1, 1, model, WIDE), lambda s: (lag(s)[2], lag(s)[1], 0, 1)),
            ANY_SPEC,
            fixed((8, wide)),
            fixed((8, LANES)),
        ],
        out_specs=[out[1] for out in outs],
        scratch_shapes=[
            pltpu.VMEM((rows, model), LOW),
            pltpu.VMEM((model, rows), LOW),
            pltpu.VMEM((CONV - 1, rows, LANES), F32),
            pltpu.VMEM((rows, model), LOW),
            pltpu.VMEM((rows, model), LOW),
            pltpu.VMEM((2, model, WIDE), LOW),
            pltpu.VMEM((rows, WIDE), F32),
            pltpu.VMEM((ext, WIDE), LOW),
            pltpu.VMEM((rows, LANES), F32),
            pltpu.VMEM((rows, LANES), F32),
            sem(10),
            pltpu.VMEM((rows, WIDE), F32),
            pltpu.VMEM((rows, Q), F32),
            pltpu.VMEM((6, 8, rows), F32),
            pltpu.VMEM((4, rows, LANES), F32),
            pltpu.VMEM((rows, WIDE), F32),
            pltpu.VMEM((GROUPS, NSTATE, WIDE), F32),
            pltpu.VMEM((GROUPS, 8, WIDE), F32),
            pltpu.VMEM((GROUPS, NSTATE, WIDE), LOW),
            pltpu.VMEM((GROUPS + 1, EDGE, WIDE), F32),
            pltpu.VMEM((GROUPS + 2, EDGE, WIDE), F32),
            pltpu.VMEM((rows, WIDE), F32),
            pltpu.VMEM((rows, model), F32),
            sem(GROUPS + 1),
            sem(GROUPS + 1),
            sem(BLOCK_CUTS),
            sem(BLOCK_CUTS),
            sem(1),
        ]
        + Chaining.scratch(rounds)
        + Reducing.scratch(depth, own_rows, 2 * half_wide)
        + extra,
        compiler_params=params(collective_id=2, has_side_effects=True),
        name="scan_back",
    )(
        pre, dy, loc, carry, enter, cin, par, par_heads, state_filter, cin_state, pre_state, bc,
        bct, score, mask, sp, cumt, fac, match, zst, dt, exits, gate_part, block_own, tokens, cot,
        hidden_t, gpg, parts, parts, small, gate_row, skip_row,
    )


def pack_body(
    entry, exits, state, steps, gain, inner_kernel, gate_gain, bias, decay, skip, docs,
    tail_tokens, packed_small, packed_parts, packed_exit, par, doc_col, doc_row, edge, docs_own
):
    half_of = side()
    rows = entry.shape[0]
    wide = entry.shape[2]

    def placed(filled, used):
        return jnp.where(half_of == 0, filled, pltpu.roll(filled, used, 1))

    def widened(value):
        return jnp.concatenate(
            [value, jnp.zeros((value.shape[0], LANES - value.shape[1]), F32)], axis=1
        )

    for part in range(3):
        at = slice(part * WIDE, (part + 1) * WIDE)
        packed_parts[part, :, :WIDE] = entry[:, 0, at].astype(LOW)
        packed_parts[part, :, WIDE:] = entry[:, 1, at].astype(LOW)
    half = jnp.where(half_of == 0, state[:, :NSTATE], state[:, NSTATE:])
    packed_small[:, :NSTATE] = half.astype(LOW)
    gain_row = jnp.concatenate([gain[...], jnp.zeros((1, LANES - rows), F32)], axis=1)
    gain_col = jnp.transpose(jnp.broadcast_to(gain_row, (LANES, LANES)))[:rows]
    lane = iota((rows, LANES), 1)
    heads_here = steps.shape[0]
    step_rows = jnp.concatenate([steps[...], jnp.zeros((heads_here, LANES - rows), F32)], axis=1)
    step_rows = jnp.concatenate([step_rows, jnp.zeros((LANES - heads_here, LANES), F32)], axis=0)
    step_cols = jnp.transpose(step_rows)[:rows]
    small = jnp.where(lane == 24, gain_col, placed(step_cols, heads_here))
    packed_small[:, NSTATE:] = small.astype(LOW)
    packed_exit[...] = exits[...].astype(LOW)
    par[0 : CONV + 1] = inner_kernel[...]
    for index in range(wide // LANES):
        at = slice(index * LANES, (index + 1) * LANES)
        par[CONV + 1 : CONV + 2, at] = gate_gain[index : index + 1]
    par[CONV + 2 : CONV + 4] = jnp.zeros((2, wide), F32)
    for index, ref in enumerate((bias, decay, skip)):
        par[CONV + 2 : CONV + 3, index * LANES : (index + 1) * LANES] = placed(
            widened(ref[...]), ref.shape[1]
        )
    own = jnp.where(half_of == 0, docs[0:1], docs[1:2]).astype(F32)
    doc_row[...] = jnp.broadcast_to(own, doc_row.shape)
    doc_col[...] = jnp.transpose(jnp.broadcast_to(own, (LANES, own.shape[1])))
    docs_own[...] = doc_col[own.shape[1] - HALO :]
    edge[...] = tail_tokens[0]


def pack_shapes(own_rows, wide, rows, model):
    shape = jax.ShapeDtypeStruct
    return (
        shape((own_rows, WIDE), LOW),
        shape((3, own_rows, 2 * WIDE), LOW),
        shape((own_rows, wide), LOW),
        shape((8, wide), F32),
        shape((rows, LANES), F32),
        shape((8, rows), F32),
        shape((HALO, model), LOW),
        shape((HALO, LANES), F32),
    )


def pack(arrays, tokens):
    own_rows, _, wide = arrays[0].shape
    rows, model = tokens.shape[1:]
    outs = pack_shapes(own_rows, wide, rows, model)
    return pl.pallas_call(
        pack_body,
        out_shape=outs,
        grid=(1,),
        in_specs=[fixed(array.shape) for array in arrays]
        + [pl.BlockSpec((1, HALO, model), lambda s: (side(), rows // HALO - 1, 0))],
        out_specs=[const(out.shape) for out in outs],
        compiler_params=params(),
        name="pack",
    )(*arrays, tokens)


def gather_body(
    depth, own_small, own_parts, own_exit, par_own, edge_own, docs_own, cot, small, parts, exits, par,
    heads, edge, docs, cot_t, docs_in, cot_in, side_send, side_land, local, *marks
):
    place = Place(depth)
    count = 2 * depth
    onward = {"context": lax.rem(place.position + 1, count)}
    behind = {"context": lax.rem(place.position + count - 1, count)}
    y = place.y
    place.greet([place.mate, place.x_peer, place.y_peer, onward, behind], (), True)
    own = [own_small, own_parts.at[0], own_parts.at[1], own_parts.at[2], own_exit]
    full = [small, parts.at[0], parts.at[1], parts.at[2], exits]
    pieces = [Gathering(place, own[i], full[i], *marks[3 * i : 3 * i + 3]) for i in range(5)]
    sides = [
        remote(edge_own, edge, side_send.at[0], side_land.at[0], onward),
        remote(docs_own, docs_in, side_send.at[1], side_land.at[1], onward),
        remote(par_own, par.at[y], side_send.at[2], side_land.at[2], place.y_peer),
    ]
    for copy in sides:
        copy.start()
    cot_copy = pltpu.make_async_copy(cot.at[y], cot_in, local.at[1])
    cot_copy.start()
    par_keep = pltpu.make_async_copy(par_own, par.at[y], local.at[0])
    par_keep.start()
    for piece in pieces:
        piece.own()
    cot_copy.wait()
    cot_t[...] = jnp.transpose(cot_in[...])
    for piece in pieces:
        piece.near()
        piece.across()
        piece.far()
    for copy in sides:
        copy.wait()
    docs[...] = jnp.where(place.position == 0, -1.0, docs_in[...])
    par_keep.wait()
    both = par[0, CONV + 2 : CONV + 3] + par[1, CONV + 2 : CONV + 3]
    heads[...] = jnp.zeros_like(heads)
    for index in range(3):
        heads[index : index + 1] = both[:, index * LANES : (index + 1) * LANES]
    for piece in pieces:
        piece.mates()
        piece.finish()


def gather(own_small, own_parts, own_exit, par_own, edge_own, docs_own, cot):
    count = lax.axis_size("context")
    depth = count // 2
    rows, model = cot.shape[1:]
    shape = jax.ShapeDtypeStruct
    full = lambda own: (2, 2, count) + own.shape[-2:]
    return pl.pallas_call(
        functools.partial(gather_body, depth),
        out_shape=(
            shape(full(own_small), LOW),
            shape((3,) + full(own_parts), LOW),
            shape(full(own_exit), LOW),
            shape((2,) + par_own.shape, F32),
            shape((8, LANES), F32),
            shape(edge_own.shape, LOW),
            shape(docs_own.shape, F32),
            shape((model, rows), LOW),
        ),
        in_specs=[VMEM_SPEC] * 6 + [ANY_SPEC],
        out_specs=[ANY_SPEC] * 3 + [VMEM_SPEC] * 5,
        scratch_shapes=[
            pltpu.VMEM(docs_own.shape, F32),
            pltpu.VMEM((rows, model), LOW),
            pltpu.SemaphoreType.DMA((3,)),
            pltpu.SemaphoreType.DMA((3,)),
            pltpu.SemaphoreType.DMA((2,)),
        ]
        + Gathering.scratch(depth) * 5,
        compiler_params=params(collective_id=0, has_side_effects=True),
        name="gather",
    )(own_small, own_parts, own_exit, par_own, edge_own, docs_own, cot)


def reduce_body(
    depth, inner, small, token, taps, taps_state, gate_row, head_rows, skip_row, norm_row, mine,
    state_out, vector_out, token_out, *scratch
):
    place = Place(depth)
    wide = inner.shape[-1]
    parts = [(inner, slice(0, wide)), (small, slice(wide, wide + WIDE))]
    reducing = Reducing(place, 0, parts, mine, scratch[:8], scratch[8:17])
    closing = Closing(place, token, token_out, scratch[17:])
    vec = closing.send
    vec[0] = jnp.zeros(vec.shape[1:], F32)
    vec[0, : CONV + 1, : 2 * wide] = taps[: CONV + 1]
    vec[0, : CONV + 1, 2 * wide :] = taps_state[: CONV + 1]
    vec[0, 5:6, : 2 * wide] = gate_row[0:1]
    vec[0, 5:6, 2 * wide : 2 * wide + LANES] = head_rows[0:1]
    vec[0, 5:6, 2 * wide + LANES :] = skip_row[0:1]
    model = norm_row.shape[1]
    vec[0, 6:7, :model] = norm_row[0:1]
    vec[0, 6:7, model : model + LANES] = head_rows[1:2]
    place.greet([place.mate, place.x_peer, place.y_peer], (), True)
    each(depth, reducing.start)
    closing.run(reducing, NSTATE, state_out, vector_out, wide)


def reduce_all(inner, small, token, taps, taps_state, gate_row, head_rows, skip_row, norm_row):
    depth = lax.axis_size("context") // 2
    own_rows, wide = inner.shape[3:]
    tall = wide + WIDE
    shape = jax.ShapeDtypeStruct
    vector = (8, 2 * wide + WIDE)
    return pl.pallas_call(
        functools.partial(reduce_body, depth),
        out_shape=(
            shape((own_rows, tall), F32),
            shape((2, own_rows, NSTATE), F32),
            shape(vector, F32),
            shape((2,) + token.shape, LOW),
        ),
        in_specs=[ANY_SPEC] * 2 + [VMEM_SPEC] * 7,
        out_specs=[VMEM_SPEC] * 3 + [ANY_SPEC],
        scratch_shapes=Reducing.scratch(depth, own_rows, tall)
        + Closing.scratch(depth, own_rows, vector),
        compiler_params=params(collective_id=4, has_side_effects=True),
        name="reduce_all",
    )(inner, small, token, taps, taps_state, gate_row, head_rows, skip_row, norm_row)


def finish_body(
    mine, mine_last, exits, state, vector, token, block, block_out, token_out,
    norm_out, entry_out, state_out, step_out, kernel_out, filter_out, bias_out, decay_out, skip_out,
    gate_out, exit_out
):
    half_of = side()
    spot = lax.axis_index("dp") * lax.axis_size("context") + lax.axis_index("context")
    token_out[...] = token[...].astype(F32)
    first = half_of == 0
    block_out[...] = block[...]

    @pl.when(pl.program_id(0) == 0)
    def _():
        own_rows, _, wide = entry_out.shape
        model = token.shape[2]
        entry_out[:, 0] = exits[:, wide:]
        entry_out[:, 1, : 2 * WIDE] = mine[...]
        entry_out[:, 1, 2 * WIDE :] = mine_last[:, :WIDE]
        exit_out[...] = exits[:, :wide]
        state_out[:, :NSTATE] = state[0]
        state_out[:, NSTATE:] = state[1]

        def twelve(value):
            return jnp.where(first, value, pltpu.roll(value, LANES - 12, 1))[:, :12]

        steps = jnp.where(first, mine_last[:, WIDE + NSTATE :], pltpu.roll(mine_last[:, WIDE + NSTATE :], LANES - 12, 1))
        steps = jnp.concatenate([steps, jnp.zeros((LANES - own_rows, LANES), F32)], axis=0)
        step_out[...] = jnp.transpose(steps)[:12, :own_rows]
        left, right = vector[:, :wide], vector[:, wide : 2 * wide]
        halves = jnp.where(first, left, right)
        kernel_out[...] = halves[: CONV + 1]
        for index in range(wide // LANES):
            gate_out[index : index + 1] = halves[5:6, index * LANES : (index + 1) * LANES]
        filter_out[...] = vector[: CONV + 1, 2 * wide :]
        bias_out[...] = twelve(vector[5:6, 2 * wide : 2 * wide + LANES])
        skip_out[...] = twelve(vector[5:6, 2 * wide + LANES :])
        decay_out[...] = twelve(vector[6:7, model : model + LANES])
        turned = pltpu.roll(vector[:, :model], lax.rem(model - spot * own_rows, model), 1)
        norm_out[...] = turned[6:7, :own_rows]


def finish(mine, mine_last, exits, state, vector, token, block):
    own_rows, wide = exits.shape[0], exits.shape[1] // 2
    _, rows, model = token.shape
    share = rows // 2
    shape = jax.ShapeDtypeStruct
    outs = (
        (shape((2, rows, model), LOW), pl.BlockSpec((2, share, model), lambda s: (0, s, 0))),
        (shape((2, rows, model), F32), pl.BlockSpec((2, share, model), lambda s: (0, s, 0))),
        (shape((1, own_rows), F32), None),
        (shape((own_rows, 2, wide), F32), None),
        (shape((own_rows, WIDE), F32), None),
        (shape((12, own_rows), F32), None),
        (shape((CONV + 1, wide), F32), None),
        (shape((CONV + 1, WIDE), F32), None),
        (shape((1, 12), F32), None),
        (shape((1, 12), F32), None),
        (shape((1, 12), F32), None),
        (shape((wide // LANES, LANES), F32), None),
        (shape((own_rows, wide), F32), None),
    )
    return pl.pallas_call(
        finish_body,
        out_shape=[out[0] for out in outs],
        grid=(2,),
        in_specs=[
            fixed(mine.shape),
            fixed(mine_last.shape),
            fixed(exits.shape),
            fixed(state.shape),
            fixed(vector.shape),
            pl.BlockSpec((2, share, model), lambda s: (0, s, 0)),
            pl.BlockSpec((2, share, model), lambda s: (0, s, 0)),
        ],
        out_specs=[out[1] if out[1] is not None else const(out[0].shape) for out in outs],
        compiler_params=params(),
        name="finish",
    )(mine, mine_last, exits, state, vector, token, block)


def body(
    tokens, documents, norm_gain, entry_weight, state_weight, step_weight, inner_kernel,
    state_filter, step_bias, decay_log, skip_gain, gate_gain, exit_weight, cotangent,
):
    seqs, rows, model = tokens.shape
    count = lax.axis_size("context")
    own_rows = norm_gain.shape[0]
    longest = rows * count // 4
    rounds = min(count // 2 - 1, -(-(longest - 1) // (2 * rows)))

    raw = (
        entry_weight, exit_weight, state_weight, step_weight.T, norm_gain[None], inner_kernel,
        gate_gain.reshape(-1, LANES), step_bias[None], decay_log[None], skip_gain[None], documents,
    )
    (
        hidden_t, cin, gate, pre, loc, carry, cin_state, pre_state, bc, bct, score, mask, zst, dt, sp,
        cumt, fac, match, local,
    ), (small, parts, exit_weights, par, par_heads, cot_t) = entry(
        tokens, raw, state_filter, cotangent, rounds
    )
    block_own, exit_part, gate_part, dy, gpg, enter, gate_row, skip_row = middle(
        tokens, cotangent, cot_t, hidden_t, pre, gate, loc, local, carry, exit_weights, par, bc, bct,
        sp, fac,
    )
    cut = lambda v: v.reshape(2, 2, count, own_rows, v.shape[-1])
    exit_mine, block_both, *others = scan_back(
        pre, dy, loc, carry, enter, cin, par, par_heads, state_filter, cin_state, pre_state, bc, bct,
        score, mask, sp, cumt, fac, match, zst, dt, cut(exit_part), cut(gate_part), block_own,
        tokens, cotangent, hidden_t, gpg, parts, small, gate_row, skip_row, rounds,
    )
    if len(others) == 5:
        mine, mine_last, state_both, vector, token_both = others
    else:
        taps, taps_state, head_rows, inner_part, small_part, token_own, norm_row = others
        mine, state_both, vector, token_both = reduce_all(
            cut(inner_part), cut(small_part), token_own, taps, taps_state, gate_row, head_rows,
            skip_row, norm_row,
        )
        mine, mine_last = mine[:, : 2 * WIDE], mine[:, 2 * WIDE :]
    outs = list(finish(mine, mine_last, exit_mine, state_both, vector, token_both, block_both))
    for index in (2, 8, 9, 10):
        outs[index] = outs[index][0]
    outs[5] = outs[5].T
    outs[11] = outs[11].reshape(-1)
    return tuple(outs)


def solution(mesh):
    in_specs = (
        P("dp", "context", None),
        P("dp", "context"),
        P(("dp", "context")),
        P(("dp", "context"), None, "tensor"),
        P(("dp", "context"), None),
        P(("dp", "context"), "tensor"),
        P(None, "tensor"),
        P(),
        P("tensor"),
        P("tensor"),
        P("tensor"),
        P("tensor"),
        P(("dp", "context"), "tensor"),
        P("dp", "context", None),
    )
    out_specs = (
        P("dp", "context", None),
        P("dp", "context", None),
        P(("dp", "context")),
        P(("dp", "context"), None, "tensor"),
        P(("dp", "context"), None),
        P(("dp", "context"), "tensor"),
        P(None, "tensor"),
        P(),
        P("tensor"),
        P("tensor"),
        P("tensor"),
        P("tensor"),
        P(("dp", "context"), "tensor"),
    )
    return jax.shard_map(body, mesh=mesh, in_specs=in_specs, out_specs=out_specs, check_vma=False)
```
